32 devices in a mesh: clip: 4 (over x, core), seq: 4 (over z), head: 2 (over y).
Axes of the slice: x: 2, y: 2, z: 4, core: 2. Of those that a mesh axis runs over, the one named last changes fastest.
Arguments:
- tokens: bfloat16 [8, 8, 196, 768], P(('clip', 'head'), 'seq'), may hold values from -6 to 6
- cotangent: bfloat16 [8, 8, 196, 768], P(('clip', 'head'), 'seq'), may hold values from -6 to 6
- time_qkv: bfloat16 [2, 768, 3, 768], P(None, ('clip', 'seq'), None, 'head'), may hold values from -0.21875 to 0.21875
- time_out: bfloat16 [2, 768, 768], P(None, 'head', ('clip', 'seq')), may hold values from -0.4375 to 0.4375
- time_mix: bfloat16 [2, 768, 768], P(None, ('clip', 'seq', 'head')), may hold values from -0.21875 to 0.21875
- space_qkv: bfloat16 [2, 768, 3, 768], P(None, ('clip', 'seq'), None, 'head'), may hold values from -0.21875 to 0.21875
- space_out: bfloat16 [2, 768, 768], P(None, 'head', ('clip', 'seq')), may hold values from -1 to 1
- mlp_in: bfloat16 [2, 768, 3072], P(None, ('clip', 'seq'), 'head'), may hold values from -0.21875 to 0.21875
- mlp_out: bfloat16 [2, 3072, 768], P(None, 'head', ('clip', 'seq')), may hold values from -0.21875 to 0.21875
- norm_gain: float32 [2, 3, 768], P(None, None, ('clip', 'seq', 'head')), may hold values from 0.25 to 1.75
- norm_bias: float32 [2, 3, 768], P(None, None, ('clip', 'seq', 'head')), may hold values from -3 to 3
Outputs:
- output: bfloat16 [8, 8, 196, 768], P(('clip', 'head'), 'seq')
- tokens_grad: float32 [8, 8, 196, 768], P(('clip', 'head'), 'seq')
- time_qkv_grad: float32 [2, 768, 3, 768], P(None, ('clip', 'seq'), None, 'head')
- time_out_grad: float32 [2, 768, 768], P(None, 'head', ('clip', 'seq'))
- time_mix_grad: float32 [2, 768, 768], P(None, ('clip', 'seq', 'head'))
- space_qkv_grad: float32 [2, 768, 3, 768], P(None, ('clip', 'seq'), None, 'head')
- space_out_grad: float32 [2, 768, 768], P(None, 'head', ('clip', 'seq'))
- mlp_in_grad: float32 [2, 768, 3072], P(None, ('clip', 'seq'), 'head')
- mlp_out_grad: float32 [2, 3072, 768], P(None, 'head', ('clip', 'seq'))
- norm_gain_grad: float32 [2, 3, 768], P(None, None, ('clip', 'seq', 'head'))
- norm_bias_grad: float32 [2, 3, 768], P(None, None, ('clip', 'seq', 'head'))
The draws below stay inside these ranges and needn't reach their ends.
All inputs are finite; a program needn't handle non-finite values.
Results may differ from the reference program's by a relative error of at most 0.024.
Values may be sent and summed in bfloat16 or wider, within the bound.
No kernel may reach another device: no remote copies, remote signals or barrier semaphores. Data moves between devices by JAX's collectives and lax.ppermute only.
A program may use at most 256 MiB of HBM per device.

```python
import math
import jax
import jax.numpy as jnp
from jax import lax

D = 768
FF = 3072
HEADS = 12
HEAD_DIM = 64
FRAMES = 8
PLACES = 196
LAYERS = 2
CLIPS = 8


def shard_levels(key, extent, pieces, least, top_value):
    def one(position, shards_of):
        draws = jax.random.uniform(jax.random.fold_in(jax.random.fold_in(key, 6), position), (shards_of,), jnp.float32, least / len(pieces), top_value / len(pieces))
        return jnp.repeat(jnp.exp(draws), extent[position] // shards_of).reshape((-1,) + (1,) * (len(extent) - position - 1))

    level = one(*pieces[0])
    for cut in pieces[1:]:
        level = level * one(*cut)
    return level


def scatter_about(stream_key, shape, scale, most, split=(), dtype=jnp.bfloat16):
    result = scale * jax.random.normal(stream_key, shape, jnp.float32)
    if split:
        result = result * shard_levels(stream_key, shape, split, -0.22, 0.18)
    return jnp.clip(result, -most, most).astype(dtype)


def setup_inputs(seed: int = 0) -> dict:
    streams_of = jax.random.split(jax.random.key(seed), 12)
    return {
        "tokens": scatter_about(streams_of[0], (CLIPS, FRAMES, PLACES, D), 1.0, 6.0, ((0, 8), (1, 4))),
        "cotangent": scatter_about(streams_of[1], (CLIPS, FRAMES, PLACES, D), 1.0, 6.0, ((0, 8), (1, 4))),
        "time_qkv": scatter_about(streams_of[2], (LAYERS, D, 3, D), D ** -0.5, 0.21875, ((1, 16), (3, 2))),
        "time_out": scatter_about(streams_of[3], (LAYERS, D, D), (D // 4) ** -0.5, 0.4375, ((1, 2), (2, 16))),
        "time_mix": scatter_about(streams_of[4], (LAYERS, D, D), D ** -0.5, 0.21875, ((1, 32),)),
        "space_qkv": scatter_about(streams_of[5], (LAYERS, D, 3, D), D ** -0.5, 0.21875, ((1, 16), (3, 2))),
        "space_out": scatter_about(streams_of[6], (LAYERS, D, D), (D * 8 // PLACES) ** -0.5, 1.0, ((1, 2), (2, 16))),
        "mlp_in": scatter_about(streams_of[7], (LAYERS, D, FF), D ** -0.5, 0.21875, ((1, 16), (2, 2))),
        "mlp_out": scatter_about(streams_of[8], (LAYERS, FF, D), (FF // 4) ** -0.5, 0.21875, ((1, 2), (2, 16))),
        "norm_gain": jnp.clip(1.0 + 0.15 * jax.random.normal(streams_of[9], (LAYERS, 3, D), jnp.float32), 0.25, 1.75),
        "norm_bias": scatter_about(streams_of[10], (LAYERS, 3, D), 0.5, 3.0, ((2, 32),), jnp.float32),
    }


@jax.custom_vjp
def low(v):
    return lax.optimization_barrier(v.astype(jnp.bfloat16)).astype(jnp.float32)

@jax.custom_vjp
def low_back(v):
    return v

def low_keep(v):
    return (low(v), None)

def low_pass(kept, grad):
    return (grad,)

def back_keep(v):
    return (v, None)

def back_low(kept, grad):
    return (low(grad),)
low.defvjp(low_keep, low_pass)
low_back.defvjp(back_keep, back_low)
norm_eps = 1e-06
time_forms = ('cfphe,cgphe->cphfg', 'cphfg,cgphe->cfphe')
space_forms = ('cfphe,cfqhe->cfhpq', 'cfhpq,cfqhe->cfphe')

def both_round(values):
    return low(low_back(values))

def product(left, right):
    return jnp.tensordot(left, right, axes=1, precision=lax.Precision.HIGHEST)

def norm_apply(values, gain_row, bias_row):
    centred = values - lax.optimization_barrier(jnp.mean(values, axis=-1, keepdims=True))
    inverse_spread = lax.rsqrt(lax.optimization_barrier(jnp.mean(centred * centred, axis=-1, keepdims=True)) + norm_eps)
    return centred * inverse_spread * gain_row + bias_row

def attend(packed, forms, scale):
    queries = packed[:, :, :, 0]
    key_rows = packed[:, :, :, 1]
    value_rows = packed[:, :, :, 2]
    scores = low_back(jnp.einsum(forms[0], queries, key_rows, precision=lax.Precision.HIGHEST) * scale)
    row_peak = lax.optimization_barrier(jnp.max(scores, axis=-1, keepdims=True))
    exponent = jnp.exp(scores - row_peak)
    weights_soft = low(exponent / lax.optimization_barrier(jnp.sum(exponent, axis=-1, keepdims=True)))
    return jnp.einsum(forms[1], weights_soft, value_rows, precision=lax.Precision.HIGHEST)

def gelu_value(hidden):
    return 0.5 * hidden * (1.0 + lax.erf(hidden * 0.7071067811865476))

def block(residual, time_qkv, time_out, time_mix, space_qkv, space_out, mlp_in, mlp_out, norm_gain, norm_bias):
    scale = 1.0 / math.sqrt(HEAD_DIM)
    lead = residual.shape[:3]
    for layer_index in range(LAYERS):
        gains = norm_gain[layer_index]
        biases = norm_bias[layer_index]
        normed_one = low(norm_apply(residual, gains[0], biases[0]))
        packed_one = both_round(product(normed_one, time_qkv[layer_index])).reshape(lead + (3, HEADS, HEAD_DIM))
        mixed_one = both_round(attend(packed_one, time_forms, scale)).reshape(lead + (D,))
        summed_one = both_round(product(mixed_one, time_out[layer_index]))
        residual = residual + low_back(product(summed_one, time_mix[layer_index]))
        normed_two = low(norm_apply(residual, gains[1], biases[1]))
        packed_two = both_round(product(normed_two, space_qkv[layer_index])).reshape(lead + (3, HEADS, HEAD_DIM))
        mixed_two = both_round(attend(packed_two, space_forms, scale)).reshape(lead + (D,))
        residual = residual + low_back(product(mixed_two, space_out[layer_index]))
        normed_three = low(norm_apply(residual, gains[2], biases[2]))
        hidden = low_back(product(normed_three, mlp_in[layer_index]))
        activated = low(gelu_value(hidden))
        residual = residual + low_back(product(activated, mlp_out[layer_index]))
    return residual

def reference(tokens, cotangent, time_qkv, time_out, time_mix, space_qkv, space_out, mlp_in, mlp_out, norm_gain, norm_bias):
    params = (time_qkv.astype(jnp.float32), time_out.astype(jnp.float32), time_mix.astype(jnp.float32), space_qkv.astype(jnp.float32), space_out.astype(jnp.float32), mlp_in.astype(jnp.float32), mlp_out.astype(jnp.float32), norm_gain.astype(jnp.float32), norm_bias.astype(jnp.float32))
    clip_count = tokens.shape[0]
    inputs = tokens.astype(jnp.float32).reshape((clip_count // 2, 2) + tokens.shape[1:])
    upstream = cotangent.astype(jnp.float32).reshape((clip_count // 2, 2) + tokens.shape[1:])

    def advance(totals, couple):
        outputs, pullback = jax.vjp(block, couple[0], *params)
        grads = pullback(couple[1])
        return (tuple((total + grad for total, grad in zip(totals, grads[1:]))), (outputs, grads[0]))
    start = tuple((jnp.zeros_like(param) for param in params))
    totals, (outputs, input_grads) = lax.scan(advance, start, (inputs, upstream))
    return (outputs.reshape(tokens.shape).astype(jnp.bfloat16), input_grads.reshape(tokens.shape), totals[0], totals[1], totals[2], totals[3], totals[4], totals[5], totals[6], totals[7], totals[8])
```

```python
import functools
import math

import jax
import jax.numpy as jnp
from jax import lax
from jax.experimental import pallas as pl
from jax.experimental.pallas import tpu as pltpu
from jax.sharding import PartitionSpec as P

HEAD_DIM = 64
NORM_EPS = 1e-06
HALF_ROOT = 0.7071067811865476
INV_ROOT_TAU = 0.3989422804014327
LOG2E = 1.4426950408889634
FAR = -1e30
LANES = 128
VMEM = 56 * 1024 * 1024
ALL = ("clip", "seq", "head")
BF16 = jnp.bfloat16
F32 = jnp.float32


def round_up(value, step):
    return -(-value // step) * step


def nn(a, b):
    return lax.dot_general(a, b, (((1,), (0,)), ((), ())), preferred_element_type=F32)


def nt(a, b):
    return lax.dot_general(a, b, (((1,), (1,)), ((), ())), preferred_element_type=F32)


def tn(a, b):
    return lax.dot_general(a, b, (((0,), (0,)), ((), ())), preferred_element_type=F32)


def norm_parts(x):
    mean = jnp.mean(x, axis=-1, keepdims=True)
    centred = x - mean
    spread = lax.rsqrt(jnp.mean(centred * centred, axis=-1, keepdims=True) + NORM_EPS)
    return centred * spread, spread


def norm_rounded(x, gain, bias):
    hat, _ = norm_parts(x)
    return (hat * gain + bias).astype(BF16)


def norm_back(u, x, gain):
    hat, spread = norm_parts(x)
    scaled = u * gain
    mean_scaled = jnp.mean(scaled, axis=-1, keepdims=True)
    mean_cross = jnp.mean(scaled * hat, axis=-1, keepdims=True)
    change = spread * (scaled - mean_scaled - hat * mean_cross)
    sums = jnp.concatenate(
        (jnp.sum(u * hat, axis=0, keepdims=True), jnp.sum(u, axis=0, keepdims=True)), axis=0
    )
    return change, sums


class Rows:
    def __init__(self, frames, places, ways):
        self.frames = frames
        self.places = places
        self.ways = ways
        self.frame_rows = round_up(places, 16)
        self.rows = frames * self.frame_rows
        self.block = places // ways
        self.chunk = round_up(frames * self.block, 8)
        self.time_rows = ways * self.chunk

    def split(self, r):
        way = jnp.zeros_like(r)
        for k in range(1, self.ways):
            way = way + (r >= k * self.chunk).astype(jnp.int32)
        rest = r - way * self.chunk
        frame = jnp.zeros_like(r)
        for k in range(1, self.frames):
            frame = frame + (rest >= k * self.block).astype(jnp.int32)
        real = rest < self.frames * self.block
        return way, frame, rest - frame * self.block, real

    def to_time(self):
        r = lax.broadcasted_iota(jnp.int32, (self.time_rows, 1), 0)
        way, frame, place, real = self.split(r)
        source = jnp.where(real, frame * self.frame_rows + way * self.block + place, -1)
        c = lax.broadcasted_iota(jnp.int32, (self.time_rows, self.rows), 1)
        return jnp.where(c == source, 1.0, 0.0).astype(BF16)

    def time_bias(self):
        def label(r):
            _, _, place, real = self.split(r)
            return jnp.where(real, place, -1)

        a = label(lax.broadcasted_iota(jnp.int32, (self.time_rows, 1), 0))
        b = label(lax.broadcasted_iota(jnp.int32, (1, self.time_rows), 1))
        return jnp.where(a == b, 0.0, FAR).astype(F32)

    def space_bias(self):
        a = lax.broadcasted_iota(jnp.int32, (self.frame_rows, 1), 0)
        return jnp.where(a < self.places, 0.0, FAR).astype(F32)


def lane_masks(rows):
    lane = lax.broadcasted_iota(jnp.int32, (rows, LANES), 1)
    return lane < HEAD_DIM


def one_of(value, low, half):
    zero = jnp.zeros_like(value)
    return jnp.where(low, value, zero) if half == 0 else jnp.where(low, zero, value)


def pair_forward(q, k, v, bias, rate):
    low = lane_masks(q.shape[0])
    mixed, logs = [], []
    for half in range(2):
        s = nt(k, one_of(q, low, half)) + bias
        peak = jnp.max(s, axis=0, keepdims=True)
        e = jnp.exp2((s - peak) * rate)
        total = jnp.sum(e, axis=0, keepdims=True)
        soft = (e * (1.0 / total)).astype(BF16)
        mixed.append(tn(soft, v))
        logs.append(peak * rate + jnp.log2(total))
    return jnp.where(low, mixed[0], mixed[1]).astype(BF16), logs


def pair_backward(q, k, v, do, logs, bias, rate, scale):
    low = lane_masks(q.shape[0])
    dq, dk, dv = [], [], []
    for half in range(2):
        s = nt(k, one_of(q, low, half)) + bias
        soft = jnp.exp2(s * rate - logs[half])
        dp = nt(v, one_of(do, low, half))
        ds = (soft * (dp - jnp.sum(soft * dp, axis=0, keepdims=True))).astype(BF16)
        dv.append(nn(soft.astype(BF16), do))
        dk.append(nn(ds, q))
        dq.append(tn(ds, k))
    return (
        (jnp.where(low, dq[0], dq[1]) * scale).astype(BF16),
        (jnp.where(low, dk[0], dk[1]) * scale).astype(BF16),
        jnp.where(low, dv[0], dv[1]).astype(BF16),
    )


def call(body, grid, ins, outs, scratch, args, flops=0):
    specs = [spec for spec in ins]
    moved = sum(math.prod(o.shape) * o.dtype.itemsize for o, _ in outs)
    moved += sum(math.prod(a.shape) * a.dtype.itemsize for a in args)
    return pl.pallas_call(
        body,
        out_shape=[shape for shape, _ in outs],
        grid=grid,
        in_specs=specs,
        out_specs=[spec for _, spec in outs],
        scratch_shapes=scratch,
        compiler_params=pltpu.CompilerParams(vmem_limit_bytes=VMEM),
        cost_estimate=pl.CostEstimate(flops=flops, bytes_accessed=moved, transcendentals=0),
    )(*args)


def whole(shape):
    zeros = (0,) * len(shape)
    return pl.BlockSpec(shape, lambda *_: zeros)


def made(shape, dtype, block=None, index=None):
    spec = whole(shape) if block is None else pl.BlockSpec(block, index)
    return jax.ShapeDtypeStruct(shape, dtype), spec


def slabs(count, first, width, depth):
    return pl.BlockSpec((count, 1, depth, width), lambda h, *_: (first // count, h, 0, 0))


def send_first(rows, x, gb):
    def body(x_ref, gb_ref, out_ref):
        a = norm_rounded(x_ref[...], gb_ref[0:1], gb_ref[3:4])
        out_ref[...] = nn(rows.to_time(), a).astype(BF16)

    d = x.shape[1]
    return call(
        body, (1,), [whole(x.shape), whole(gb.shape)], [made((rows.time_rows, d), BF16)], [], (x, gb)
    )[0]


def time_forward(rows, a, w, head_shares):
    t, d = a.shape
    width = w.shape[3]
    pairs = width // LANES
    rate = LOG2E / math.sqrt(HEAD_DIM)

    def body(a_ref, w_ref, qkv_ref, out_ref, log_ref, bias_ref):
        @pl.when(pl.program_id(0) == 0)
        def _():
            bias_ref[...] = rows.time_bias()

        act = a_ref[...]
        for g in range(3):
            qkv_ref[g] = nn(act, w_ref[g, 0]).astype(BF16)

        @pl.loop(0, pairs)
        def _(i):
            lanes = pl.ds(pl.multiple_of(i * LANES, LANES), LANES)
            mixed, logs = pair_forward(
                qkv_ref[0, :, lanes], qkv_ref[1, :, lanes], qkv_ref[2, :, lanes], bias_ref[...], rate
            )
            out_ref[:, lanes] = mixed
            log_ref[0, i] = jnp.concatenate(logs, axis=0)

    return call(
        body,
        (head_shares,),
        [whole(a.shape), slabs(3, 0, width, d)],
        [
            made((3, t, d), BF16, (3, t, width), lambda h: (0, 0, h)),
            made((t, d), BF16, (t, width), lambda h: (0, h)),
            made((head_shares, pairs, 2, t), F32, (1, pairs, 2, t), lambda h: (h, 0, 0, 0)),
        ],
        [pltpu.VMEM((t, t), F32)],
        (a, w),
        flops=2 * t * d * 3 * d,
    )


def middle_forward(rows, back, x, w, mix, gb):
    t, d = x.shape
    width = w.shape[3]
    shares = w.shape[1]

    def body(back_ref, x_ref, to_ref, sq_ref, mix_ref, gb_ref, o1_ref, y1_ref, x1_ref, qkv_ref):
        o1 = tn(rows.to_time(), back_ref[...]).astype(BF16)
        o1_ref[...] = o1
        y1 = jnp.zeros((t, d), F32)
        for h in range(shares):
            y1 = y1 + nt(o1[:, h * width : (h + 1) * width], to_ref[0, h])
        y1 = y1.astype(BF16)
        y1_ref[...] = y1
        x1 = x_ref[...] + nn(y1, mix_ref[...])
        x1_ref[...] = x1
        a2 = norm_rounded(x1, gb_ref[1:2], gb_ref[4:5])
        for g in range(3):
            for h in range(shares):
                qkv_ref[g, :, h * width : (h + 1) * width] = nn(a2, sq_ref[g, h]).astype(BF16)

    return call(
        body,
        (1,),
        [
            whole(back.shape),
            whole(x.shape),
            pl.BlockSpec((1, shares, d, width), lambda i: (6, 0, 0, 0)),
            pl.BlockSpec((3, shares, d, width), lambda i: (1, 0, 0, 0)),
            whole(mix.shape),
            whole(gb.shape),
        ],
        [made((t, d), BF16), made((t, d), BF16), made((t, d), F32), made((3, t, d), BF16)],
        [],
        (back, x, w, w, mix, gb),
        flops=2 * t * d * 5 * d,
    )


def space_forward(rows, qkv, x1, w):
    t, d = x1.shape
    width = w.shape[3]
    shares = w.shape[1]
    pairs = width // LANES
    rate = LOG2E / math.sqrt(HEAD_DIM)
    n = rows.frame_rows

    def body(qkv_ref, x1_ref, w_ref, o2_ref, x2_ref, log_ref):
        bias = rows.space_bias()

        @pl.loop(0, pairs)
        def _(i):
            lanes = pl.ds(pl.multiple_of(i * LANES, LANES), LANES)
            for f in range(rows.frames):
                at = slice(f * n, (f + 1) * n)
                mixed, logs = pair_forward(
                    qkv_ref[0, at, lanes], qkv_ref[1, at, lanes], qkv_ref[2, at, lanes], bias, rate
                )
                o2_ref[at, lanes] = mixed
                log_ref[0, i, f] = jnp.concatenate(logs, axis=0)

        @pl.when(pl.program_id(0) == 0)
        def _():
            x2_ref[...] = x1_ref[...]

        x2_ref[...] += nt(o2_ref[...], w_ref[0, 0])

    return call(
        body,
        (shares,),
        [
            pl.BlockSpec((3, t, width), lambda h: (0, 0, h)),
            whole(x1.shape),
            slabs(1, 7, width, d),
        ],
        [
            made((t, d), BF16, (t, width), lambda h: (0, h)),
            made((t, d), F32),
            made(
                (shares, pairs, rows.frames, 2, n),
                F32,
                (1, pairs, rows.frames, 2, n),
                lambda h: (h, 0, 0, 0, 0),
            ),
        ],
        [],
        (qkv, x1, w),
        flops=2 * t * d * d,
    )


def ff_slab(first, per_share, depth, width):
    return pl.BlockSpec(
        (1, 1, depth, width), lambda j: (first + j % per_share, j // per_share, 0, 0)
    )


def mlp_forward(rows, x2, w, gb, gb_next):
    t, d = x2.shape
    width = w.shape[3]
    shares = w.shape[1]
    per_share = (w.shape[0] - 9) // 2
    steps = shares * per_share
    last = gb_next is None

    def body(x2_ref, wi_ref, wo_ref, gb_ref, *rest):
        if last:
            x3_ref, a3_ref = rest
        else:
            gn_ref, x3_ref, send_ref, a3_ref = rest
        j = pl.program_id(0)

        @pl.when(j == 0)
        def _():
            a3_ref[...] = norm_rounded(x2_ref[...], gb_ref[2:3], gb_ref[5:6])
            x3_ref[...] = x2_ref[...]

        hid = nn(a3_ref[...], wi_ref[0, 0])
        act = (0.5 * hid * (1.0 + lax.erf(hid * HALF_ROOT))).astype(BF16)
        x3_ref[...] += nt(act, wo_ref[0, 0])

        if not last:

            @pl.when(j == steps - 1)
            def _():
                a = norm_rounded(x3_ref[...], gn_ref[0:1], gn_ref[3:4])
                send_ref[...] = nn(rows.to_time(), a).astype(BF16)

    ins = [
        whole(x2.shape),
        ff_slab(8, per_share, d, width),
        ff_slab(8 + per_share, per_share, d, width),
        whole(gb.shape),
    ]
    outs = [made((t, d), F32)]
    args = [x2, w, w, gb]
    if not last:
        ins.append(whole(gb_next.shape))
        outs.append(made((rows.time_rows, d), BF16))
        args.append(gb_next)
    return call(
        body, (steps,), ins, outs, [pltpu.VMEM((t, d), BF16)], tuple(args), flops=4 * t * d * width * steps
    )


def mlp_backward(rows, grad, x2, w, gb):
    t, d = x2.shape
    width = w.shape[3]
    shares = w.shape[1]
    per_share = (w.shape[0] - 9) // 2
    steps = shares * per_share

    def body(g_ref, x2_ref, wi_ref, wo_ref, gb_ref, go_ref, gi_ref, gw_ref, sums_ref, a3_ref, a3t_ref, e3_ref, e3t_ref, u_ref):
        j = pl.program_id(0)

        @pl.when(j == 0)
        def _():
            hat, _ = norm_parts(x2_ref[...])
            a3 = hat * gb_ref[2:3] + gb_ref[5:6]
            a3_ref[...] = a3.astype(BF16)
            a3t_ref[...] = a3.T.astype(BF16)
            g = g_ref[...]
            e3_ref[...] = g.astype(BF16)
            e3t_ref[...] = g.T.astype(BF16)
            u_ref[...] = jnp.zeros((t, d), F32)

        hid = nn(a3_ref[...], wi_ref[0, 0])
        phi = 0.5 * (1.0 + lax.erf(hid * HALF_ROOT))
        act = (hid * phi).astype(BF16)
        slope = phi + hid * jnp.exp(-0.5 * hid * hid) * INV_ROOT_TAU
        dhid = (nn(e3_ref[...], wo_ref[0, 0]) * slope).astype(BF16)
        gw_ref[0, 0] = nn(e3t_ref[...], act).astype(BF16)
        gi_ref[0, 0] = nn(a3t_ref[...], dhid).astype(BF16)
        u_ref[...] += nt(dhid, wi_ref[0, 0])

        @pl.when(j == steps - 1)
        def _():
            change, sums = norm_back(u_ref[...], x2_ref[...], gb_ref[2:3])
            go_ref[...] = g_ref[...] + change
            sums_ref[...] = sums

    slab_out = lambda: made(
        (per_share, shares, d, width),
        BF16,
        (1, 1, d, width),
        lambda j: (j % per_share, j // per_share, 0, 0),
    )
    return call(
        body,
        (steps,),
        [
            whole(grad.shape),
            whole(x2.shape),
            ff_slab(8, per_share, d, width),
            ff_slab(8 + per_share, per_share, d, width),
            whole(gb.shape),
        ],
        [made((t, d), F32), slab_out(), slab_out(), made((2, d), F32)],
        [
            pltpu.VMEM((t, d), BF16),
            pltpu.VMEM((d, t), BF16),
            pltpu.VMEM((t, d), BF16),
            pltpu.VMEM((d, t), BF16),
            pltpu.VMEM((t, d), F32),
        ],
        (grad, x2, w, w, gb),
        flops=10 * t * d * width * steps,
    )


def space_backward(rows, grad, x1, qkv, o2, logs, w, gb):
    t, d = x1.shape
    width = w.shape[3]
    shares = w.shape[1]
    pairs = width // LANES
    scale = 1.0 / math.sqrt(HEAD_DIM)
    rate = LOG2E * scale
    n = rows.frame_rows

    def body(g_ref, x1_ref, qkv_ref, o2_ref, log_ref, wo_ref, wq_ref, gb_ref, go_ref, gw_ref, gq_ref, sums_ref, e2_ref, e2t_ref, a2t_ref, do_ref, dqkv_ref, u_ref):
        h = pl.program_id(0)

        @pl.when(h == 0)
        def _():
            g = g_ref[...]
            e2_ref[...] = g.astype(BF16)
            e2t_ref[...] = g.T.astype(BF16)
            hat, _ = norm_parts(x1_ref[...])
            a2t_ref[...] = (hat * gb_ref[1:2] + gb_ref[4:5]).T.astype(BF16)
            u_ref[...] = jnp.zeros((t, d), F32)

        bias = rows.space_bias()
        gw_ref[0, 0] = nn(e2t_ref[...], o2_ref[...]).astype(BF16)
        do_ref[...] = nn(e2_ref[...], wo_ref[0, 0]).astype(BF16)

        @pl.loop(0, pairs)
        def _(i):
            lanes = pl.ds(pl.multiple_of(i * LANES, LANES), LANES)
            for f in range(rows.frames):
                at = slice(f * n, (f + 1) * n)
                log = log_ref[0, i, f]
                grads = pair_backward(
                    qkv_ref[0, at, lanes],
                    qkv_ref[1, at, lanes],
                    qkv_ref[2, at, lanes],
                    do_ref[at, lanes],
                    (log[0:1], log[1:2]),
                    bias,
                    rate,
                    scale,
                )
                for part in range(3):
                    dqkv_ref[part, at, lanes] = grads[part]

        for part in range(3):
            gq_ref[part, 0] = nn(a2t_ref[...], dqkv_ref[part]).astype(BF16)
            u_ref[...] += nt(dqkv_ref[part], wq_ref[part, 0])

        @pl.when(h == shares - 1)
        def _():
            change, sums = norm_back(u_ref[...], x1_ref[...], gb_ref[1:2])
            go_ref[...] = g_ref[...] + change
            sums_ref[...] = sums

    return call(
        body,
        (shares,),
        [
            whole(grad.shape),
            whole(x1.shape),
            pl.BlockSpec((3, t, width), lambda h: (0, 0, h)),
            pl.BlockSpec((t, width), lambda h: (0, h)),
            pl.BlockSpec((1,) + logs.shape[1:], lambda h: (h, 0, 0, 0, 0)),
            slabs(1, 7, width, d),
            slabs(3, 3, width, d),
            whole(gb.shape),
        ],
        [
            made((t, d), F32),
            made((1, shares, d, width), BF16, (1, 1, d, width), lambda h: (0, h, 0, 0)),
            made((3, shares, d, width), BF16, (3, 1, d, width), lambda h: (0, h, 0, 0)),
            made((2, d), F32),
        ],
        [
            pltpu.VMEM((t, d), BF16),
            pltpu.VMEM((d, t), BF16),
            pltpu.VMEM((d, t), BF16),
            pltpu.VMEM((t, width), BF16),
            pltpu.VMEM((3, t, width), BF16),
            pltpu.VMEM((t, d), F32),
        ],
        (grad, x1, qkv, o2, logs, w, w, gb),
        flops=2 * t * d * d * 8,
    )


def middle_backward(rows, grad, y1, o1, w, mix):
    t, d = grad.shape
    width = w.shape[3]
    shares = w.shape[1]

    def body(g_ref, y1_ref, o1_ref, to_ref, mix_ref, send_ref, gm_ref, gt_ref):
        e1 = g_ref[...].astype(BF16)
        gm_ref[...] = tn(y1_ref[...], e1).astype(BF16)
        dy = nt(e1, mix_ref[...])
        dy1 = dy.astype(BF16)
        send = rows.to_time()
        for h in range(shares):
            lanes = slice(h * width, (h + 1) * width)
            gt_ref[0, h] = tn(dy1, o1_ref[:, lanes]).astype(BF16)
            do1 = nn(dy1, to_ref[0, h]).astype(BF16)
            send_ref[:, lanes] = nn(send, do1).astype(BF16)

    return call(
        body,
        (1,),
        [
            whole(grad.shape),
            whole(y1.shape),
            whole(o1.shape),
            pl.BlockSpec((1, shares, d, width), lambda i: (6, 0, 0, 0)),
            whole(mix.shape),
        ],
        [
            made((rows.time_rows, d), BF16),
            made((d, d), BF16),
            made((1, shares, d, width), BF16),
        ],
        [],
        (grad, y1, o1, w, mix),
        flops=8 * t * d * d,
    )


def time_backward(rows, do1, a, qkv, logs, w):
    t, d = a.shape
    width = w.shape[3]
    shares = w.shape[1]
    pairs = width // LANES
    scale = 1.0 / math.sqrt(HEAD_DIM)
    rate = LOG2E * scale

    def body(do_ref, a_ref, qkv_ref, log_ref, w_ref, out_ref, gq_ref, bias_ref, dqkv_ref, at_ref, u_ref):
        h = pl.program_id(0)

        @pl.when(h == 0)
        def _():
            bias_ref[...] = rows.time_bias()
            at_ref[...] = a_ref[...].T
            u_ref[...] = jnp.zeros((t, d), F32)

        @pl.loop(0, pairs)
        def _(i):
            lanes = pl.ds(pl.multiple_of(i * LANES, LANES), LANES)
            log = log_ref[0, i]
            grads = pair_backward(
                qkv_ref[0, :, lanes],
                qkv_ref[1, :, lanes],
                qkv_ref[2, :, lanes],
                do_ref[:, lanes],
                (log[0:1], log[1:2]),
                bias_ref[...],
                rate,
                scale,
            )
            for part in range(3):
                dqkv_ref[part, :, lanes] = grads[part]

        for part in range(3):
            gq_ref[part, 0] = nn(at_ref[...], dqkv_ref[part]).astype(BF16)
            u_ref[...] += nt(dqkv_ref[part], w_ref[part, 0])

        @pl.when(h == shares - 1)
        def _():
            out_ref[...] = u_ref[...].astype(BF16)

    return call(
        body,
        (shares,),
        [
            pl.BlockSpec((t, width), lambda h: (0, h)),
            whole(a.shape),
            pl.BlockSpec((3, t, width), lambda h: (0, 0, h)),
            pl.BlockSpec((1,) + logs.shape[1:], lambda h: (h, 0, 0, 0)),
            slabs(3, 0, width, d),
        ],
        [
            made((t, d), BF16),
            made((3, shares, d, width), BF16, (3, 1, d, width), lambda h: (0, h, 0, 0)),
        ],
        [
            pltpu.VMEM((t, t), F32),
            pltpu.VMEM((3, t, width), BF16),
            pltpu.VMEM((d, t), BF16),
            pltpu.VMEM((t, d), F32),
        ],
        (do1, a, qkv, logs, w),
        flops=2 * t * d * d * 6,
    )


def first_norm_back(rows, back, x, grad, gb):
    t, d = x.shape

    def body(back_ref, x_ref, g_ref, gb_ref, go_ref, sums_ref):
        u = tn(rows.to_time(), back_ref[...])
        change, sums = norm_back(u, x_ref[...], gb_ref[0:1])
        go_ref[...] = g_ref[...] + change
        sums_ref[...] = sums

    return call(
        body,
        (1,),
        [whole(back.shape), whole(x.shape), whole(grad.shape), whole(gb.shape)],
        [made((t, d), F32), made((2, d), F32)],
        [],
        (back, x, grad, gb),
    )


def swap_places(rows_array):
    return lax.all_to_all(rows_array, "seq", split_axis=0, concat_axis=0, tiled=True)


def pack_layer(time_qkv, time_out, time_mix, space_qkv, space_out, mlp_in, mlp_out):
    width = time_qkv.shape[2]
    r = time_qkv.shape[0]
    halves = time_mix.shape[1] // width

    def columns(a):
        return a.reshape(r, -1, width).transpose(1, 0, 2)

    mix = time_mix.reshape(-1, halves, width).transpose(1, 0, 2).reshape(1, r, width)
    return jnp.concatenate(
        (
            columns(time_qkv),
            columns(space_qkv),
            time_out.T[None],
            space_out.T[None],
            columns(mlp_in),
            columns(mlp_out.T),
            mix,
        ),
        axis=0,
    )


def gather_slabs(pack):
    full = lax.all_gather(pack, ("head", "clip", "seq"), axis=1, tiled=True)
    return full.reshape(pack.shape[0], lax.axis_size("head"), -1, pack.shape[2])


def mix_whole(slab, shards):
    shares, depth, width = slab.shape
    part = slab.reshape(shares, shards, shares, depth // (shards * shares), width)
    return part.transpose(1, 0, 3, 2, 4).reshape(depth, shares * width)


def mix_slab(whole_grad, shards, shares):
    depth, full = whole_grad.shape
    width = full // shares
    part = whole_grad.reshape(shards, shares, depth // (shards * shares), shares, width)
    return part.transpose(1, 0, 3, 2, 4).reshape(1, shares, depth, width)


def added(a, b):
    return (a.astype(F32) + b.astype(F32)).astype(BF16)


def picked(a, index, axis):
    return lax.dynamic_index_in_dim(a, index, axis, keepdims=False)


def fold(a, axis, name, bit):
    size = lax.axis_size(name)
    mine = (lax.axis_index(name) >> bit) & 1
    sent = lax.ppermute(
        picked(a, 1 - mine, axis), name, [(i, i ^ (1 << bit)) for i in range(size)]
    )
    return added(picked(a, mine, axis), sent)


def reduce_slabs(g, head_first):
    ns, shares, depth, width = g.shape
    clips, ways = lax.axis_size("clip"), lax.axis_size("seq")
    r = depth // (clips * ways)
    a = g.reshape(ns, shares, clips // 2, 2, ways, r, width)
    a = fold(a, 3, "clip", 0)

    def by_head(a):
        return fold(a, 1, "head", 0)

    def by_clip(a, axis):
        bits = int(math.log2(clips)) - 1
        for bit in range(bits):
            shape = a.shape
            a = a.reshape(shape[:axis] + (shape[axis] // 2, 2) + shape[axis + 1 :])
            a = fold(a, axis + 1, "clip", bit + 1)
        return a.reshape(a.shape[:axis] + a.shape[axis + 1 :])

    if head_first:
        a = by_clip(by_head(a), 1)
    else:
        a = by_head(by_clip(a, 2))
    a = a.transpose(1, 0, 2, 3)
    parts = lax.all_to_all(a, "seq", split_axis=0, concat_axis=0, tiled=True)
    return jnp.sum(parts.astype(F32), axis=0)


def gather_norms(gain, bias):
    layers, norms, part = gain.shape
    both = jnp.concatenate((gain, bias), axis=1).reshape(1, -1)
    count = lax.axis_size("clip") * lax.axis_size("seq") * lax.axis_size("head")
    width = round_up(both.shape[1], 128)
    padded = jnp.pad(both, ((0, 0), (0, width - both.shape[1])))
    every = lax.all_to_all(
        jnp.broadcast_to(padded, (count, width)), ALL, split_axis=0, concat_axis=0, tiled=True
    )[:, : both.shape[1]]
    return every.reshape(count, layers * 2 * norms, part).transpose(1, 0, 2).reshape(layers, 2 * norms, -1)


def reduce_norms(sums):
    count = lax.axis_size("clip") * lax.axis_size("seq") * lax.axis_size("head")
    rows, features = sums.shape
    part = features // count
    a = sums.reshape(rows, count, part).transpose(1, 0, 2).reshape(count, rows * part)
    width = round_up(rows * part, 128)
    a = jnp.pad(a, ((0, 0), (0, width - rows * part)))
    every = lax.all_to_all(a, ALL, split_axis=0, concat_axis=0, tiled=True)
    return jnp.sum(every, axis=0)[: rows * part].reshape(rows, part)


def on_device(
    tokens,
    cotangent,
    time_qkv,
    time_out,
    time_mix,
    space_qkv,
    space_out,
    mlp_in,
    mlp_out,
    norm_gain,
    norm_bias,
):
    layers = time_qkv.shape[0]
    clips, frames, places, d = tokens.shape
    ways = lax.axis_size("seq")
    shards = lax.axis_size("clip") * ways
    rows = Rows(clips * frames, places, ways)
    shares = lax.axis_size("head")

    def as_rows(a):
        a = a.astype(F32).reshape(rows.frames, places, d)
        a = jnp.pad(a, ((0, 0), (0, rows.frame_rows - places), (0, 0)))
        return a.reshape(rows.rows, d)

    def from_rows(a):
        a = a.reshape(rows.frames, rows.frame_rows, d)[:, :places]
        return a.reshape(tokens.shape)

    gbs = gather_norms(norm_gain, norm_bias)
    gb = [gbs[l] for l in range(layers)]
    weights = [
        gather_slabs(
            pack_layer(
                time_qkv[l], time_out[l], time_mix[l], space_qkv[l], space_out[l], mlp_in[l], mlp_out[l]
            )
        )
        for l in range(layers)
    ]
    mixes = [mix_whole(w[-1], shards) for w in weights]

    x = as_rows(tokens)
    send = send_first(rows, x, gb[0])
    kept = []
    for l in range(layers):
        w = weights[l]
        a1 = swap_places(send)
        qkv1, o1_time, log1 = time_forward(rows, a1, w, shares)
        back = swap_places(o1_time)
        o1, y1, x1, qkv2 = middle_forward(rows, back, x, w, mixes[l], gb[l])
        o2, x2, log2 = space_forward(rows, qkv2, x1, w)
        kept.append((x, a1, qkv1, log1, o1, y1, x1, qkv2, o2, log2, x2))
        if l + 1 < layers:
            x, send = mlp_forward(rows, x2, w, gb[l], gb[l + 1])
        else:
            (x,) = mlp_forward(rows, x2, w, gb[l], None)
    output = from_rows(x).astype(BF16)

    grad = as_rows(cotangent)
    results = [None] * layers
    norm_rows = [None] * layers
    for l in reversed(range(layers)):
        w = weights[l]
        x, a1, qkv1, log1, o1, y1, x1, qkv2, o2, log2, x2 = kept[l]
        grad, g_in, g_out, s3 = mlp_backward(rows, grad, x2, w, gb[l])
        grad, g_so, g_sq, s2 = space_backward(rows, grad, x1, qkv2, o2, log2, w, gb[l])
        do1, g_mix, g_to = middle_backward(rows, grad, y1, o1, w, mixes[l])
        da1, g_tq = time_backward(rows, swap_places(do1), a1, qkv1, log1, w)
        grad, s1 = first_norm_back(rows, swap_places(da1), x, grad, gb[l])
        results[l] = (
            reduce_slabs(g_in, True),
            reduce_slabs(g_out, False),
            reduce_slabs(jnp.concatenate((g_so, g_sq), axis=0), True),
            reduce_slabs(jnp.concatenate((g_to, mix_slab(g_mix, shards, shares)), axis=0), False),
            reduce_slabs(g_tq, True),
        )
        norm_rows[l] = jnp.concatenate((s1[0:1], s2[0:1], s3[0:1], s1[1:2], s2[1:2], s3[1:2]), axis=0)
    tokens_grad = from_rows(grad)
    norm_sums = reduce_norms(jnp.concatenate(norm_rows, axis=0)).reshape(layers, 2, 3, -1)

    def stacked(form):
        return jnp.stack([form(*results[l]) for l in range(layers)])

    def rows_of(a):
        return a.transpose(1, 0, 2)

    def flat(a):
        return rows_of(a).reshape(a.shape[1], -1)

    def mix_rows(a):
        r, width = a.shape
        return a.reshape(shares, r // shares, width).transpose(1, 0, 2).reshape(r // shares, -1)

    return (
        output,
        tokens_grad,
        stacked(lambda gi, go, s, t, q: rows_of(q)),
        stacked(lambda gi, go, s, t, q: t[0].T),
        stacked(lambda gi, go, s, t, q: mix_rows(t[1])),
        stacked(lambda gi, go, s, t, q: rows_of(s[1:])),
        stacked(lambda gi, go, s, t, q: s[0].T),
        stacked(lambda gi, go, s, t, q: flat(gi)),
        stacked(lambda gi, go, s, t, q: flat(go).T),
        norm_sums[:, 0],
        norm_sums[:, 1],
    )


def solution(mesh):
    token_spec = P(("clip", "head"), "seq", None, None)
    in_specs = (
        token_spec,
        token_spec,
        P(None, ("clip", "seq"), None, "head"),
        P(None, "head", ("clip", "seq")),
        P(None, ("clip", "seq", "head"), None),
        P(None, ("clip", "seq"), None, "head"),
        P(None, "head", ("clip", "seq")),
        P(None, ("clip", "seq"), "head"),
        P(None, "head", ("clip", "seq")),
        P(None, None, ("clip", "seq", "head")),
        P(None, None, ("clip", "seq", "head")),
    )
    return jax.shard_map(
        on_device, mesh=mesh, in_specs=in_specs, out_specs=in_specs, check_vma=False
    )
```

```python
import functools
import math

import jax
import jax.numpy as jnp
from jax import lax
from jax.experimental import pallas as pl
from jax.experimental.pallas import tpu as pltpu
from jax.sharding import PartitionSpec as P

HEAD_DIM = 64
NORM_EPS = 1e-06
HALF_ROOT = 0.7071067811865476
INV_ROOT_TAU = 0.3989422804014327
LOG2E = 1.4426950408889634
FAR = -1e30
LANES = 128
VMEM = 56 * 1024 * 1024
ALL = ("clip", "seq", "head")
BF16 = jnp.bfloat16
F32 = jnp.float32


def round_up(value, step):
    return -(-value // step) * step


def nn(a, b):
    return lax.dot_general(a, b, (((1,), (0,)), ((), ())), preferred_element_type=F32)


def nt(a, b):
    return lax.dot_general(a, b, (((1,), (1,)), ((), ())), preferred_element_type=F32)


def tn(a, b):
    return lax.dot_general(a, b, (((0,), (0,)), ((), ())), preferred_element_type=F32)


def norm_parts(x):
    mean = jnp.mean(x, axis=-1, keepdims=True)
    centred = x - mean
    spread = lax.rsqrt(jnp.mean(centred * centred, axis=-1, keepdims=True) + NORM_EPS)
    return centred * spread, spread


def norm_rounded(x, gain, bias):
    hat, _ = norm_parts(x)
    return (hat * gain + bias).astype(BF16)


def norm_back(u, x, gain):
    hat, spread = norm_parts(x)
    scaled = u * gain
    mean_scaled = jnp.mean(scaled, axis=-1, keepdims=True)
    mean_cross = jnp.mean(scaled * hat, axis=-1, keepdims=True)
    change = spread * (scaled - mean_scaled - hat * mean_cross)
    sums = jnp.concatenate(
        (jnp.sum(u * hat, axis=0, keepdims=True), jnp.sum(u, axis=0, keepdims=True)), axis=0
    )
    return change, sums


class Rows:
    def __init__(self, frames, places, ways):
        self.frames = frames
        self.places = places
        self.ways = ways
        self.frame_rows = round_up(places, 16)
        self.rows = frames * self.frame_rows
        self.block = places // ways
        self.chunk = round_up(frames * self.block, 8)
        self.time_rows = ways * self.chunk

    def split(self, r):
        way = jnp.zeros_like(r)
        for k in range(1, self.ways):
            way = way + (r >= k * self.chunk).astype(jnp.int32)
        rest = r - way * self.chunk
        frame = jnp.zeros_like(r)
        for k in range(1, self.frames):
            frame = frame + (rest >= k * self.block).astype(jnp.int32)
        real = rest < self.frames * self.block
        return way, frame, rest - frame * self.block, real

    def to_time(self):
        r = lax.broadcasted_iota(jnp.int32, (self.time_rows, 1), 0)
        way, frame, place, real = self.split(r)
        source = jnp.where(real, frame * self.frame_rows + way * self.block + place, -1)
        c = lax.broadcasted_iota(jnp.int32, (self.time_rows, self.rows), 1)
        return jnp.where(c == source, 1.0, 0.0).astype(BF16)

    def time_bias(self):
        def label(r):
            _, _, place, real = self.split(r)
            return jnp.where(real, place, -1)

        a = label(lax.broadcasted_iota(jnp.int32, (self.time_rows, 1), 0))
        b = label(lax.broadcasted_iota(jnp.int32, (1, self.time_rows), 1))
        return jnp.where(a == b, 0.0, FAR).astype(F32)

    def space_bias(self):
        a = lax.broadcasted_iota(jnp.int32, (self.frame_rows, 1), 0)
        return jnp.where(a < self.places, 0.0, FAR).astype(F32)


def lane_masks(rows):
    lane = lax.broadcasted_iota(jnp.int32, (rows, LANES), 1)
    return lane < HEAD_DIM


def one_of(value, low, half):
    zero = jnp.zeros_like(value)
    return jnp.where(low, value, zero) if half == 0 else jnp.where(low, zero, value)


def pair_forward(q, k, v, bias, rate):
    low = lane_masks(q.shape[0])
    mixed, logs = [], []
    for half in range(2):
        s = nt(k, one_of(q, low, half)) + bias
        peak = jnp.max(s, axis=0, keepdims=True)
        e = jnp.exp2((s - peak) * rate)
        total = jnp.sum(e, axis=0, keepdims=True)
        soft = (e * (1.0 / total)).astype(BF16)
        mixed.append(tn(soft, v))
        logs.append(peak * rate + jnp.log2(total))
    return jnp.where(low, mixed[0], mixed[1]).astype(BF16), logs


def pair_backward(q, k, v, do, logs, bias, rate, scale):
    low = lane_masks(q.shape[0])
    dq, dk, dv = [], [], []
    for half in range(2):
        s = nt(k, one_of(q, low, half)) + bias
        soft = jnp.exp2(s * rate - logs[half])
        dp = nt(v, one_of(do, low, half))
        ds = (soft * (dp - jnp.sum(soft * dp, axis=0, keepdims=True))).astype(BF16)
        dv.append(nn(soft.astype(BF16), do))
        dk.append(nn(ds, q))
        dq.append(tn(ds, k))
    return (
        (jnp.where(low, dq[0], dq[1]) * scale).astype(BF16),
        (jnp.where(low, dk[0], dk[1]) * scale).astype(BF16),
        jnp.where(low, dv[0], dv[1]).astype(BF16),
    )


def call(body, grid, ins, outs, scratch, args, flops=0):
    specs = [spec for spec in ins]
    moved = sum(math.prod(o.shape) * o.dtype.itemsize for o, _ in outs)
    moved += sum(math.prod(a.shape) * a.dtype.itemsize for a in args)
    return pl.pallas_call(
        body,
        out_shape=[shape for shape, _ in outs],
        grid=grid,
        in_specs=specs,
        out_specs=[spec for _, spec in outs],
        scratch_shapes=scratch,
        compiler_params=pltpu.CompilerParams(vmem_limit_bytes=VMEM),
        cost_estimate=pl.CostEstimate(flops=flops, bytes_accessed=moved, transcendentals=0),
    )(*args)


def whole(shape):
    zeros = (0,) * len(shape)
    return pl.BlockSpec(shape, lambda *_: zeros)


def made(shape, dtype, block=None, index=None):
    spec = whole(shape) if block is None else pl.BlockSpec(block, index)
    return jax.ShapeDtypeStruct(shape, dtype), spec


def slabs(count, first, width, depth):
    return pl.BlockSpec((count, 1, depth, width), lambda h, *_: (first // count, h, 0, 0))


def send_first(rows, x, gb):
    def body(x_ref, gb_ref, out_ref):
        a = norm_rounded(x_ref[...], gb_ref[0:1], gb_ref[3:4])
        out_ref[...] = nn(rows.to_time(), a).astype(BF16)

    d = x.shape[1]
    return call(
        body, (1,), [whole(x.shape), whole(gb.shape)], [made((rows.time_rows, d), BF16)], [], (x, gb)
    )[0]


def time_forward(rows, a, w, head_shares):
    t, d = a.shape
    width = w.shape[3]
    pairs = width // LANES
    rate = LOG2E / math.sqrt(HEAD_DIM)

    def body(a_ref, w_ref, qkv_ref, out_ref, log_ref, bias_ref):
        @pl.when(pl.program_id(0) == 0)
        def _():
            bias_ref[...] = rows.time_bias()

        act = a_ref[...]
        for g in range(3):
            qkv_ref[g] = nn(act, w_ref[g, 0]).astype(BF16)

        @pl.loop(0, pairs)
        def _(i):
            lanes = pl.ds(pl.multiple_of(i * LANES, LANES), LANES)
            mixed, logs = pair_forward(
                qkv_ref[0, :, lanes], qkv_ref[1, :, lanes], qkv_ref[2, :, lanes], bias_ref[...], rate
            )
            out_ref[:, lanes] = mixed
            log_ref[0, i] = jnp.concatenate(logs, axis=0)

    return call(
        body,
        (head_shares,),
        [whole(a.shape), slabs(3, 0, width, d)],
        [
            made((3, t, d), BF16, (3, t, width), lambda h: (0, 0, h)),
            made((t, d), BF16, (t, width), lambda h: (0, h)),
            made((head_shares, pairs, 2, t), F32, (1, pairs, 2, t), lambda h: (h, 0, 0, 0)),
        ],
        [pltpu.VMEM((t, t), F32)],
        (a, w),
        flops=2 * t * d * 3 * d,
    )


def middle_forward(rows, back, x, w, mix, gb):
    t, d = x.shape
    width = w.shape[3]
    shares = w.shape[1]

    def body(back_ref, x_ref, to_ref, sq_ref, mix_ref, gb_ref, o1_ref, y1_ref, x1_ref, qkv_ref):
        o1 = tn(rows.to_time(), back_ref[...]).astype(BF16)
        o1_ref[...] = o1
        y1 = jnp.zeros((t, d), F32)
        for h in range(shares):
            y1 = y1 + nt(o1[:, h * width : (h + 1) * width], to_ref[0, h])
        y1 = y1.astype(BF16)
        y1_ref[...] = y1
        x1 = x_ref[...] + nn(y1, mix_ref[...])
        x1_ref[...] = x1
        a2 = norm_rounded(x1, gb_ref[1:2], gb_ref[4:5])
        for g in range(3):
            for h in range(shares):
                qkv_ref[g, :, h * width : (h + 1) * width] = nn(a2, sq_ref[g, h]).astype(BF16)

    return call(
        body,
        (1,),
        [
            whole(back.shape),
            whole(x.shape),
            pl.BlockSpec((1, shares, d, width), lambda i: (6, 0, 0, 0)),
            pl.BlockSpec((3, shares, d, width), lambda i: (1, 0, 0, 0)),
            whole(mix.shape),
            whole(gb.shape),
        ],
        [made((t, d), BF16), made((t, d), BF16), made((t, d), F32), made((3, t, d), BF16)],
        [],
        (back, x, w, w, mix, gb),
        flops=2 * t * d * 5 * d,
    )


def space_forward(rows, qkv, x1, w):
    t, d = x1.shape
    width = w.shape[3]
    shares = w.shape[1]
    pairs = width // LANES
    rate = LOG2E / math.sqrt(HEAD_DIM)
    n = rows.frame_rows

    def body(qkv_ref, x1_ref, w_ref, o2_ref, x2_ref, log_ref):
        bias = rows.space_bias()

        @pl.loop(0, pairs)
        def _(i):
            lanes = pl.ds(pl.multiple_of(i * LANES, LANES), LANES)
            for f in range(rows.frames):
                at = slice(f * n, (f + 1) * n)
                mixed, logs = pair_forward(
                    qkv_ref[0, at, lanes], qkv_ref[1, at, lanes], qkv_ref[2, at, lanes], bias, rate
                )
                o2_ref[at, lanes] = mixed
                log_ref[0, i, f] = jnp.concatenate(logs, axis=0)

        @pl.when(pl.program_id(0) == 0)
        def _():
            x2_ref[...] = x1_ref[...]

        x2_ref[...] += nt(o2_ref[...], w_ref[0, 0])

    return call(
        body,
        (shares,),
        [
            pl.BlockSpec((3, t, width), lambda h: (0, 0, h)),
            whole(x1.shape),
            slabs(1, 7, width, d),
        ],
        [
            made((t, d), BF16, (t, width), lambda h: (0, h)),
            made((t, d), F32),
            made(
                (shares, pairs, rows.frames, 2, n),
                F32,
                (1, pairs, rows.frames, 2, n),
                lambda h: (h, 0, 0, 0, 0),
            ),
        ],
        [],
        (qkv, x1, w),
        flops=2 * t * d * d,
    )


def ff_slab(first, per_share, depth, width):
    return pl.BlockSpec(
        (1, 1, depth, width), lambda j: (first + j % per_share, j // per_share, 0, 0)
    )


def mlp_forward(rows, x2, w, gb, gb_next):
    t, d = x2.shape
    width = w.shape[3]
    shares = w.shape[1]
    per_share = (w.shape[0] - 9) // 2
    steps = shares * per_share
    last = gb_next is None

    def body(x2_ref, wi_ref, wo_ref, gb_ref, *rest):
        if last:
            x3_ref, a3_ref = rest
        else:
            gn_ref, x3_ref, send_ref, a3_ref = rest
        j = pl.program_id(0)

        @pl.when(j == 0)
        def _():
            a3_ref[...] = norm_rounded(x2_ref[...], gb_ref[2:3], gb_ref[5:6])
            x3_ref[...] = x2_ref[...]

        hid = nn(a3_ref[...], wi_ref[0, 0])
        act = (0.5 * hid * (1.0 + lax.erf(hid * HALF_ROOT))).astype(BF16)
        x3_ref[...] += nt(act, wo_ref[0, 0])

        if not last:

            @pl.when(j == steps - 1)
            def _():
                a = norm_rounded(x3_ref[...], gn_ref[0:1], gn_ref[3:4])
                send_ref[...] = nn(rows.to_time(), a).astype(BF16)

    ins = [
        whole(x2.shape),
        ff_slab(8, per_share, d, width),
        ff_slab(8 + per_share, per_share, d, width),
        whole(gb.shape),
    ]
    outs = [made((t, d), F32)]
    args = [x2, w, w, gb]
    if not last:
        ins.append(whole(gb_next.shape))
        outs.append(made((rows.time_rows, d), BF16))
        args.append(gb_next)
    return call(
        body, (steps,), ins, outs, [pltpu.VMEM((t, d), BF16)], tuple(args), flops=4 * t * d * width * steps
    )


def mlp_backward(rows, grad, x2, w, gb):
    t, d = x2.shape
    width = w.shape[3]
    shares = w.shape[1]
    per_share = (w.shape[0] - 9) // 2
    steps = shares * per_share

    def body(g_ref, x2_ref, wi_ref, wo_ref, gb_ref, go_ref, gw_ref, sums_ref, a3_ref, a3t_ref, e3_ref, e3t_ref, u_ref):
        j = pl.program_id(0)

        @pl.when(j == 0)
        def _():
            hat, _ = norm_parts(x2_ref[...])
            a3 = hat * gb_ref[2:3] + gb_ref[5:6]
            a3_ref[...] = a3.astype(BF16)
            a3t_ref[...] = a3.T.astype(BF16)
            g = g_ref[...]
            e3_ref[...] = g.astype(BF16)
            e3t_ref[...] = g.T.astype(BF16)
            u_ref[...] = jnp.zeros((t, d), F32)

        hid = nn(a3_ref[...], wi_ref[0, 0])
        phi = 0.5 * (1.0 + lax.erf(hid * HALF_ROOT))
        act = (hid * phi).astype(BF16)
        slope = phi + hid * jnp.exp(-0.5 * hid * hid) * INV_ROOT_TAU
        dhid = (nn(e3_ref[...], wo_ref[0, 0]) * slope).astype(BF16)
        gw_ref[1, 0, 0] = nn(e3t_ref[...], act).astype(BF16)
        gw_ref[0, 0, 0] = nn(a3t_ref[...], dhid).astype(BF16)
        u_ref[...] += nt(dhid, wi_ref[0, 0])

        @pl.when(j == steps - 1)
        def _():
            change, sums = norm_back(u_ref[...], x2_ref[...], gb_ref[2:3])
            go_ref[...] = g_ref[...] + change
            sums_ref[...] = sums

    slab_out = made(
        (2, per_share, shares, d, width),
        BF16,
        (2, 1, 1, d, width),
        lambda j: (0, j % per_share, j // per_share, 0, 0),
    )
    grad, slabs_grad, sums = call(
        body,
        (steps,),
        [
            whole(grad.shape),
            whole(x2.shape),
            ff_slab(8, per_share, d, width),
            ff_slab(8 + per_share, per_share, d, width),
            whole(gb.shape),
        ],
        [made((t, d), F32), slab_out, made((2, d), F32)],
        [
            pltpu.VMEM((t, d), BF16),
            pltpu.VMEM((d, t), BF16),
            pltpu.VMEM((t, d), BF16),
            pltpu.VMEM((d, t), BF16),
            pltpu.VMEM((t, d), F32),
        ],
        (grad, x2, w, w, gb),
        flops=10 * t * d * width * steps,
    )
    return grad, slabs_grad.reshape(2 * per_share, shares, d, width), sums


def space_backward(rows, grad, x1, qkv, o2, logs, w, gb):
    t, d = x1.shape
    width = w.shape[3]
    shares = w.shape[1]
    pairs = width // LANES
    scale = 1.0 / math.sqrt(HEAD_DIM)
    rate = LOG2E * scale
    n = rows.frame_rows

    def body(g_ref, x1_ref, qkv_ref, o2_ref, log_ref, wo_ref, wq_ref, gb_ref, go_ref, gq_ref, sums_ref, e2_ref, e2t_ref, a2t_ref, do_ref, dqkv_ref, u_ref):
        h = pl.program_id(0)

        @pl.when(h == 0)
        def _():
            g = g_ref[...]
            e2_ref[...] = g.astype(BF16)
            e2t_ref[...] = g.T.astype(BF16)
            hat, _ = norm_parts(x1_ref[...])
            a2t_ref[...] = (hat * gb_ref[1:2] + gb_ref[4:5]).T.astype(BF16)
            u_ref[...] = jnp.zeros((t, d), F32)

        bias = rows.space_bias()
        gq_ref[0, 0] = nn(e2t_ref[...], o2_ref[...]).astype(BF16)
        do_ref[...] = nn(e2_ref[...], wo_ref[0, 0]).astype(BF16)

        @pl.loop(0, pairs)
        def _(i):
            lanes = pl.ds(pl.multiple_of(i * LANES, LANES), LANES)
            for f in range(rows.frames):
                at = slice(f * n, (f + 1) * n)
                log = log_ref[0, i, f]
                grads = pair_backward(
                    qkv_ref[0, at, lanes],
                    qkv_ref[1, at, lanes],
                    qkv_ref[2, at, lanes],
                    do_ref[at, lanes],
                    (log[0:1], log[1:2]),
                    bias,
                    rate,
                    scale,
                )
                for part in range(3):
                    dqkv_ref[part, at, lanes] = grads[part]

        for part in range(3):
            gq_ref[part + 1, 0] = nn(a2t_ref[...], dqkv_ref[part]).astype(BF16)
            u_ref[...] += nt(dqkv_ref[part], wq_ref[part, 0])

        @pl.when(h == shares - 1)
        def _():
            change, sums = norm_back(u_ref[...], x1_ref[...], gb_ref[1:2])
            go_ref[...] = g_ref[...] + change
            sums_ref[...] = sums

    return call(
        body,
        (shares,),
        [
            whole(grad.shape),
            whole(x1.shape),
            pl.BlockSpec((3, t, width), lambda h: (0, 0, h)),
            pl.BlockSpec((t, width), lambda h: (0, h)),
            pl.BlockSpec((1,) + logs.shape[1:], lambda h: (h, 0, 0, 0, 0)),
            slabs(1, 7, width, d),
            slabs(3, 3, width, d),
            whole(gb.shape),
        ],
        [
            made((t, d), F32),
            made((4, shares, d, width), BF16, (4, 1, d, width), lambda h: (0, h, 0, 0)),
            made((2, d), F32),
        ],
        [
            pltpu.VMEM((t, d), BF16),
            pltpu.VMEM((d, t), BF16),
            pltpu.VMEM((d, t), BF16),
            pltpu.VMEM((t, width), BF16),
            pltpu.VMEM((3, t, width), BF16),
            pltpu.VMEM((t, d), F32),
        ],
        (grad, x1, qkv, o2, logs, w, w, gb),
        flops=2 * t * d * d * 8,
    )


def middle_backward(rows, grad, y1, o1, w, mix):
    t, d = grad.shape
    width = w.shape[3]
    shares = w.shape[1]

    def body(g_ref, y1_ref, o1_ref, to_ref, mix_ref, send_ref, gm_ref, gt_ref):
        e1 = g_ref[...].astype(BF16)
        gm_ref[...] = tn(y1_ref[...], e1).astype(BF16)
        dy = nt(e1, mix_ref[...])
        dy1 = dy.astype(BF16)
        send = rows.to_time()
        for h in range(shares):
            lanes = slice(h * width, (h + 1) * width)
            gt_ref[0, h] = tn(dy1, o1_ref[:, lanes]).astype(BF16)
            do1 = nn(dy1, to_ref[0, h]).astype(BF16)
            send_ref[:, lanes] = nn(send, do1).astype(BF16)

    return call(
        body,
        (1,),
        [
            whole(grad.shape),
            whole(y1.shape),
            whole(o1.shape),
            pl.BlockSpec((1, shares, d, width), lambda i: (6, 0, 0, 0)),
            whole(mix.shape),
        ],
        [
            made((rows.time_rows, d), BF16),
            made((d, d), BF16),
            made((1, shares, d, width), BF16),
        ],
        [],
        (grad, y1, o1, w, mix),
        flops=8 * t * d * d,
    )


def time_backward(rows, do1, a, qkv, logs, w):
    t, d = a.shape
    width = w.shape[3]
    shares = w.shape[1]
    pairs = width // LANES
    scale = 1.0 / math.sqrt(HEAD_DIM)
    rate = LOG2E * scale

    def body(do_ref, a_ref, qkv_ref, log_ref, w_ref, out_ref, gq_ref, bias_ref, dqkv_ref, at_ref, u_ref):
        h = pl.program_id(0)

        @pl.when(h == 0)
        def _():
            bias_ref[...] = rows.time_bias()
            at_ref[...] = a_ref[...].T
            u_ref[...] = jnp.zeros((t, d), F32)

        @pl.loop(0, pairs)
        def _(i):
            lanes = pl.ds(pl.multiple_of(i * LANES, LANES), LANES)
            log = log_ref[0, i]
            grads = pair_backward(
                qkv_ref[0, :, lanes],
                qkv_ref[1, :, lanes],
                qkv_ref[2, :, lanes],
                do_ref[:, lanes],
                (log[0:1], log[1:2]),
                bias_ref[...],
                rate,
                scale,
            )
            for part in range(3):
                dqkv_ref[part, :, lanes] = grads[part]

        for part in range(3):
            gq_ref[part, 0] = nn(at_ref[...], dqkv_ref[part]).astype(BF16)
            u_ref[...] += nt(dqkv_ref[part], w_ref[part, 0])

        @pl.when(h == shares - 1)
        def _():
            out_ref[...] = u_ref[...].astype(BF16)

    return call(
        body,
        (shares,),
        [
            pl.BlockSpec((t, width), lambda h: (0, h)),
            whole(a.shape),
            pl.BlockSpec((3, t, width), lambda h: (0, 0, h)),
            pl.BlockSpec((1,) + logs.shape[1:], lambda h: (h, 0, 0, 0)),
            slabs(3, 0, width, d),
        ],
        [
            made((t, d), BF16),
            made((3, shares, d, width), BF16, (3, 1, d, width), lambda h: (0, h, 0, 0)),
        ],
        [
            pltpu.VMEM((t, t), F32),
            pltpu.VMEM((3, t, width), BF16),
            pltpu.VMEM((d, t), BF16),
            pltpu.VMEM((t, d), F32),
        ],
        (do1, a, qkv, logs, w),
        flops=2 * t * d * d * 6,
    )


def first_norm_back(rows, back, x, grad, gb):
    t, d = x.shape

    def body(back_ref, x_ref, g_ref, gb_ref, go_ref, sums_ref):
        u = tn(rows.to_time(), back_ref[...])
        change, sums = norm_back(u, x_ref[...], gb_ref[0:1])
        go_ref[...] = g_ref[...] + change
        sums_ref[...] = sums

    return call(
        body,
        (1,),
        [whole(back.shape), whole(x.shape), whole(grad.shape), whole(gb.shape)],
        [made((t, d), F32), made((2, d), F32)],
        [],
        (back, x, grad, gb),
    )


def swap_places(rows_array):
    return lax.all_to_all(rows_array, "seq", split_axis=0, concat_axis=0, tiled=True)


def pack_layer(time_qkv, time_out, time_mix, space_qkv, space_out, mlp_in, mlp_out):
    width = time_qkv.shape[2]
    r = time_qkv.shape[0]
    halves = time_mix.shape[1] // width

    def columns(a):
        return a.reshape(r, -1, width).transpose(1, 0, 2)

    mix = time_mix.reshape(-1, halves, width).transpose(1, 0, 2).reshape(1, r, width)
    return jnp.concatenate(
        (
            columns(time_qkv),
            columns(space_qkv),
            time_out.T[None],
            space_out.T[None],
            columns(mlp_in),
            columns(mlp_out.T),
            mix,
        ),
        axis=0,
    )


def gather_slabs(pack):
    full = lax.all_gather(pack, ("head", "clip", "seq"), axis=1, tiled=True)
    return full.reshape(pack.shape[0], lax.axis_size("head"), -1, pack.shape[2])


def mix_whole(slab, shards):
    shares, depth, width = slab.shape
    part = slab.reshape(shares, shards, shares, depth // (shards * shares), width)
    return part.transpose(1, 0, 3, 2, 4).reshape(depth, shares * width)


def mix_slab(whole_grad, shards, shares):
    depth, full = whole_grad.shape
    width = full // shares
    part = whole_grad.reshape(shards, shares, depth // (shards * shares), shares, width)
    return part.transpose(1, 0, 3, 2, 4).reshape(1, shares, depth, width)


def total_of(terms):
    result = terms[0].astype(F32)
    for term in terms[1:]:
        result = result + term.astype(F32)
    return result


class Part:
    def __init__(self, terms, names):
        self.terms = terms
        self.names = list(names)

    def axis_of(self, name):
        if name == "h":
            return "head", 0
        return "clip", int(name[1:])

    def picked(self, name, index):
        axis = self.names.index(name)
        return [lax.dynamic_index_in_dim(t, index, axis, keepdims=False) for t in self.terms]

    def mine(self, name):
        axis, bit = self.axis_of(name)
        return (lax.axis_index(axis) >> bit) & 1

    def to_send(self, name):
        return total_of(self.picked(name, 1 - self.mine(name))).astype(BF16)

    def take(self, name, sent):
        axis, bit = self.axis_of(name)
        size = lax.axis_size(axis)
        got = lax.ppermute(sent, axis, [(i, i ^ (1 << bit)) for i in range(size)])
        self.terms = self.picked(name, self.mine(name)) + [got]
        self.names.remove(name)

    def cut(self, first, last):
        return Part([t[first:last] for t in self.terms], self.names)


def reduction(g):
    ns, shares, depth, width = g.shape
    clips, ways = lax.axis_size("clip"), lax.axis_size("seq")
    bits = int(math.log2(clips))
    r = depth // (clips * ways)
    chips = ["c%d" % b for b in reversed(range(1, bits))]
    names = ["n", "h"] + chips + ["c0", "s", "r", "w"]
    whole_part = Part([g.reshape((ns, shares) + (2,) * bits + (ways, r, width))], names)
    (sent,) = yield (whole_part.to_send("c0"),)
    whole_part.take("c0", sent)
    half = (ns + 1) // 2
    parts = (whole_part.cut(0, half), whole_part.cut(half, ns))
    orders = (chips + ["h"], ["h"] + chips)
    for step in range(bits):
        sent = yield tuple(p.to_send(o[step]) for p, o in zip(parts, orders))
        for p, o, one in zip(parts, orders, sent):
            p.take(o[step], one)
    both = [total_of(p.terms).astype(BF16).transpose(1, 0, 2, 3) for p in parts]
    (sent,) = yield (jnp.concatenate(both, axis=1),)
    got = lax.all_to_all(sent, "seq", split_axis=0, concat_axis=0, tiled=True)
    yield jnp.sum(got.astype(F32), axis=0)


class Line:
    def __init__(self):
        self.going = []
        self.done = {}

    def add(self, key, g):
        way = reduction(g)
        self.going.append([key, way, next(way)])

    def move(self, x):
        ready = [item[2] for item in self.going]
        x, ready = lax.optimization_barrier((x, ready))
        still = []
        for (key, way, _), sent in zip(self.going, ready):
            got = way.send(sent)
            if isinstance(got, tuple):
                still.append([key, way, got])
            else:
                self.done[key] = got
        self.going = still
        return x


def gather_norms(gain, bias):
    layers, norms, part = gain.shape
    both = jnp.concatenate((gain, bias), axis=1).reshape(1, -1)
    count = lax.axis_size("clip") * lax.axis_size("seq") * lax.axis_size("head")
    width = round_up(both.shape[1], 128)
    padded = jnp.pad(both, ((0, 0), (0, width - both.shape[1])))
    every = lax.all_to_all(
        jnp.broadcast_to(padded, (count, width)), ALL, split_axis=0, concat_axis=0, tiled=True
    )[:, : both.shape[1]]
    return every.reshape(count, layers * 2 * norms, part).transpose(1, 0, 2).reshape(layers, 2 * norms, -1)


def reduce_norms(sums):
    count = lax.axis_size("clip") * lax.axis_size("seq") * lax.axis_size("head")
    rows, features = sums.shape
    part = features // count
    a = sums.reshape(rows, count, part).transpose(1, 0, 2).reshape(count, rows * part)
    width = round_up(rows * part, 128)
    a = jnp.pad(a, ((0, 0), (0, width - rows * part)))
    every = lax.all_to_all(a, ALL, split_axis=0, concat_axis=0, tiled=True)
    return jnp.sum(every, axis=0)[: rows * part].reshape(rows, part)


def on_device(
    tokens,
    cotangent,
    time_qkv,
    time_out,
    time_mix,
    space_qkv,
    space_out,
    mlp_in,
    mlp_out,
    norm_gain,
    norm_bias,
):
    layers = time_qkv.shape[0]
    clips, frames, places, d = tokens.shape
    ways = lax.axis_size("seq")
    shards = lax.axis_size("clip") * ways
    rows = Rows(clips * frames, places, ways)
    shares = lax.axis_size("head")

    def as_rows(a):
        a = a.astype(F32).reshape(rows.frames, places, d)
        a = jnp.pad(a, ((0, 0), (0, rows.frame_rows - places), (0, 0)))
        return a.reshape(rows.rows, d)

    def from_rows(a):
        a = a.reshape(rows.frames, rows.frame_rows, d)[:, :places]
        return a.reshape(tokens.shape)

    gbs = gather_norms(norm_gain, norm_bias)
    gb = [gbs[l] for l in range(layers)]
    weights = [
        gather_slabs(
            pack_layer(
                time_qkv[l], time_out[l], time_mix[l], space_qkv[l], space_out[l], mlp_in[l], mlp_out[l]
            )
        )
        for l in range(layers)
    ]
    mixes = [mix_whole(w[-1], shards) for w in weights]

    x = as_rows(tokens)
    send = send_first(rows, x, gb[0])
    kept = []
    for l in range(layers):
        w = weights[l]
        a1 = swap_places(send)
        qkv1, o1_time, log1 = time_forward(rows, a1, w, shares)
        back = swap_places(o1_time)
        o1, y1, x1, qkv2 = middle_forward(rows, back, x, w, mixes[l], gb[l])
        o2, x2, log2 = space_forward(rows, qkv2, x1, w)
        kept.append((x, a1, qkv1, log1, o1, y1, x1, qkv2, o2, log2, x2))
        if l + 1 < layers:
            x, send = mlp_forward(rows, x2, w, gb[l], gb[l + 1])
        else:
            (x,) = mlp_forward(rows, x2, w, gb[l], None)
    output = from_rows(x).astype(BF16)

    grad = as_rows(cotangent)
    line = Line()
    norm_rows = [None] * layers
    for l in reversed(range(layers)):
        w = weights[l]
        x, a1, qkv1, log1, o1, y1, x1, qkv2, o2, log2, x2 = kept[l]
        grad, g_ff, s3 = mlp_backward(rows, grad, x2, w, gb[l])
        line.add(("ff", l), g_ff)
        grad = line.move(grad)
        grad, g_space, s2 = space_backward(rows, grad, x1, qkv2, o2, log2, w, gb[l])
        line.add(("space", l), g_space)
        grad = line.move(grad)
        do1, g_mix, g_to = middle_backward(rows, grad, y1, o1, w, mixes[l])
        line.add(("out", l), jnp.concatenate((g_to, mix_slab(g_mix, shards, shares)), axis=0))
        do1 = line.move(swap_places(do1))
        da1, g_tq = time_backward(rows, do1, a1, qkv1, log1, w)
        line.add(("time", l), g_tq)
        da1 = line.move(swap_places(da1))
        grad, s1 = first_norm_back(rows, da1, x, grad, gb[l])
        norm_rows[l] = jnp.concatenate((s1[0:1], s2[0:1], s3[0:1], s1[1:2], s2[1:2], s3[1:2]), axis=0)
    while line.going:
        line.move(())
    results = [[line.done[(key, l)] for key in ("ff", "space", "out", "time")] for l in range(layers)]
    tokens_grad = from_rows(grad)
    norm_sums = reduce_norms(jnp.concatenate(norm_rows, axis=0)).reshape(layers, 2, 3, -1)

    def stacked(form):
        return jnp.stack([form(*results[l]) for l in range(layers)])

    def rows_of(a):
        return a.transpose(1, 0, 2)

    def flat(a):
        return rows_of(a).reshape(a.shape[1], -1)

    def mix_rows(a):
        r, width = a.shape
        return a.reshape(shares, r // shares, width).transpose(1, 0, 2).reshape(r // shares, -1)

    per_share = mlp_in.shape[2] // time_qkv.shape[3]
    return (
        output,
        tokens_grad,
        stacked(lambda ff, s, t, q: rows_of(q)),
        stacked(lambda ff, s, t, q: t[0].T),
        stacked(lambda ff, s, t, q: mix_rows(t[1])),
        stacked(lambda ff, s, t, q: rows_of(s[1:])),
        stacked(lambda ff, s, t, q: s[0].T),
        stacked(lambda ff, s, t, q: flat(ff[:per_share])),
        stacked(lambda ff, s, t, q: flat(ff[per_share:]).T),
        norm_sums[:, 0],
        norm_sums[:, 1],
    )


def solution(mesh):
    token_spec = P(("clip", "head"), "seq", None, None)
    in_specs = (
        token_spec,
        token_spec,
        P(None, ("clip", "seq"), None, "head"),
        P(None, "head", ("clip", "seq")),
        P(None, ("clip", "seq", "head"), None),
        P(None, ("clip", "seq"), None, "head"),
        P(None, "head", ("clip", "seq")),
        P(None, ("clip", "seq"), "head"),
        P(None, "head", ("clip", "seq")),
        P(None, None, ("clip", "seq", "head")),
        P(None, None, ("clip", "seq", "head")),
    )
    return jax.shard_map(
        on_device, mesh=mesh, in_specs=in_specs, out_specs=in_specs, check_vma=False
    )
```

```python
import functools
import math

import jax
import jax.numpy as jnp
from jax import lax
from jax.experimental import pallas as pl
from jax.experimental.pallas import tpu as pltpu
from jax.sharding import PartitionSpec as P

HEAD_DIM = 64
NORM_EPS = 1e-06
HALF_ROOT = 0.7071067811865476
INV_ROOT_TAU = 0.3989422804014327
LOG2E = 1.4426950408889634
FAR = -1e30
LANES = 128
VMEM = 56 * 1024 * 1024
ALL = ("clip", "seq", "head")
BF16 = jnp.bfloat16
F32 = jnp.float32


def round_up(value, step):
    return -(-value // step) * step


def nn(a, b):
    return lax.dot_general(a, b, (((1,), (0,)), ((), ())), preferred_element_type=F32)


def nt(a, b):
    return lax.dot_general(a, b, (((1,), (1,)), ((), ())), preferred_element_type=F32)


def tn(a, b):
    return lax.dot_general(a, b, (((0,), (0,)), ((), ())), preferred_element_type=F32)


def norm_parts(x):
    mean = jnp.mean(x, axis=-1, keepdims=True)
    centred = x - mean
    spread = lax.rsqrt(jnp.mean(centred * centred, axis=-1, keepdims=True) + NORM_EPS)
    return centred * spread, spread


def norm_rounded(x, gain, bias):
    hat, _ = norm_parts(x)
    return (hat * gain + bias).astype(BF16)


def norm_back(u, x, gain):
    hat, spread = norm_parts(x)
    scaled = u * gain
    mean_scaled = jnp.mean(scaled, axis=-1, keepdims=True)
    mean_cross = jnp.mean(scaled * hat, axis=-1, keepdims=True)
    change = spread * (scaled - mean_scaled - hat * mean_cross)
    sums = jnp.concatenate(
        (jnp.sum(u * hat, axis=0, keepdims=True), jnp.sum(u, axis=0, keepdims=True)), axis=0
    )
    return change, sums


class Rows:
    def __init__(self, frames, places, ways):
        self.frames = frames
        self.places = places
        self.ways = ways
        self.frame_rows = round_up(places, 16)
        self.rows = frames * self.frame_rows
        self.block = places // ways
        self.chunk = round_up(frames * self.block, 8)
        self.time_rows = ways * self.chunk

    def split(self, r):
        way = jnp.zeros_like(r)
        for k in range(1, self.ways):
            way = way + (r >= k * self.chunk).astype(jnp.int32)
        rest = r - way * self.chunk
        frame = jnp.zeros_like(r)
        for k in range(1, self.frames):
            frame = frame + (rest >= k * self.block).astype(jnp.int32)
        real = rest < self.frames * self.block
        return way, frame, rest - frame * self.block, real

    def to_time(self):
        r = lax.broadcasted_iota(jnp.int32, (self.time_rows, 1), 0)
        way, frame, place, real = self.split(r)
        source = jnp.where(real, frame * self.frame_rows + way * self.block + place, -1)
        c = lax.broadcasted_iota(jnp.int32, (self.time_rows, self.rows), 1)
        return jnp.where(c == source, 1.0, 0.0).astype(BF16)

    def time_bias(self):
        def label(r):
            _, _, place, real = self.split(r)
            return jnp.where(real, place, -1)

        a = label(lax.broadcasted_iota(jnp.int32, (self.time_rows, 1), 0))
        b = label(lax.broadcasted_iota(jnp.int32, (1, self.time_rows), 1))
        return jnp.where(a == b, 0.0, FAR).astype(F32)

    def space_bias(self):
        a = lax.broadcasted_iota(jnp.int32, (self.frame_rows, 1), 0)
        return jnp.where(a < self.places, 0.0, FAR).astype(F32)


def lane_masks(rows):
    lane = lax.broadcasted_iota(jnp.int32, (rows, LANES), 1)
    return lane < HEAD_DIM


def one_of(value, low, half):
    zero = jnp.zeros_like(value)
    return jnp.where(low, value, zero) if half == 0 else jnp.where(low, zero, value)


def pair_forward(q, k, v, bias, rate):
    low = lane_masks(q.shape[0])
    mixed, logs = [], []
    for half in range(2):
        s = nt(k, one_of(q, low, half)) + bias
        peak = jnp.max(s, axis=0, keepdims=True)
        e = jnp.exp2((s - peak) * rate)
        total = jnp.sum(e, axis=0, keepdims=True)
        soft = (e * (1.0 / total)).astype(BF16)
        mixed.append(tn(soft, v))
        logs.append(peak * rate + jnp.log2(total))
    return jnp.where(low, mixed[0], mixed[1]).astype(BF16), logs


def pair_backward(q, k, v, do, logs, bias, rate, scale):
    low = lane_masks(q.shape[0])
    dq, dk, dv = [], [], []
    for half in range(2):
        s = nt(k, one_of(q, low, half)) + bias
        soft = jnp.exp2(s * rate - logs[half])
        dp = nt(v, one_of(do, low, half))
        ds = (soft * (dp - jnp.sum(soft * dp, axis=0, keepdims=True))).astype(BF16)
        dv.append(nn(soft.astype(BF16), do))
        dk.append(nn(ds, q))
        dq.append(tn(ds, k))
    return (
        (jnp.where(low, dq[0], dq[1]) * scale).astype(BF16),
        (jnp.where(low, dk[0], dk[1]) * scale).astype(BF16),
        jnp.where(low, dv[0], dv[1]).astype(BF16),
    )


def split_rows(value, keep_ref, send_ref, at, room_ref, me_ref):
    mine = me_ref[0]
    room_ref[...] = value.reshape(room_ref.shape)
    keep_ref[at] = room_ref[:, mine].astype(BF16)
    send_ref[at] = room_ref[:, 1 - mine].astype(BF16)


class Halves:
    def __init__(self, clips, depth, width):
        self.pairs = clips // 2
        self.rows = depth // clips
        self.width = width

    def array(self, lead, block, index):
        tail = (self.pairs, self.rows, self.width)
        one = lambda: made(lead + tail, BF16, block + tail, lambda *g: index(*g) + (0, 0, 0))
        return [one(), one()]

    def room(self):
        return pltpu.VMEM((self.pairs, 2, self.rows, self.width), F32)


SCALARS = pl.BlockSpec(memory_space=pltpu.SMEM)


def call(body, grid, ins, outs, scratch, args, flops=0):
    specs = [spec for spec in ins]
    moved = sum(math.prod(o.shape) * o.dtype.itemsize for o, _ in outs)
    moved += sum(math.prod(a.shape) * a.dtype.itemsize for a in args)
    return pl.pallas_call(
        body,
        out_shape=[shape for shape, _ in outs],
        grid=grid,
        in_specs=specs,
        out_specs=[spec for _, spec in outs],
        scratch_shapes=scratch,
        compiler_params=pltpu.CompilerParams(vmem_limit_bytes=VMEM),
        cost_estimate=pl.CostEstimate(flops=flops, bytes_accessed=moved, transcendentals=0),
    )(*args)


def whole(shape):
    zeros = (0,) * len(shape)
    return pl.BlockSpec(shape, lambda *_: zeros)


def made(shape, dtype, block=None, index=None):
    spec = whole(shape) if block is None else pl.BlockSpec(block, index)
    return jax.ShapeDtypeStruct(shape, dtype), spec


def slabs(count, first, width, depth):
    return pl.BlockSpec((count, 1, depth, width), lambda h, *_: (first // count, h, 0, 0))


def send_first(rows, x, gb):
    def body(x_ref, gb_ref, out_ref):
        a = norm_rounded(x_ref[...], gb_ref[0:1], gb_ref[3:4])
        out_ref[...] = nn(rows.to_time(), a).astype(BF16)

    d = x.shape[1]
    return call(
        body, (1,), [whole(x.shape), whole(gb.shape)], [made((rows.time_rows, d), BF16)], [], (x, gb)
    )[0]


def time_forward(rows, a, w, head_shares):
    t, d = a.shape
    width = w.shape[3]
    pairs = width // LANES
    rate = LOG2E / math.sqrt(HEAD_DIM)

    def body(a_ref, w_ref, qkv_ref, out_ref, log_ref, bias_ref):
        @pl.when(pl.program_id(0) == 0)
        def _():
            bias_ref[...] = rows.time_bias()

        act = a_ref[...]
        for g in range(3):
            qkv_ref[g] = nn(act, w_ref[g, 0]).astype(BF16)

        @pl.loop(0, pairs)
        def _(i):
            lanes = pl.ds(pl.multiple_of(i * LANES, LANES), LANES)
            mixed, logs = pair_forward(
                qkv_ref[0, :, lanes], qkv_ref[1, :, lanes], qkv_ref[2, :, lanes], bias_ref[...], rate
            )
            out_ref[:, lanes] = mixed
            log_ref[0, i] = jnp.concatenate(logs, axis=0)

    return call(
        body,
        (head_shares,),
        [whole(a.shape), slabs(3, 0, width, d)],
        [
            made((3, t, d), BF16, (3, t, width), lambda h: (0, 0, h)),
            made((t, d), BF16, (t, width), lambda h: (0, h)),
            made((head_shares, pairs, 2, t), F32, (1, pairs, 2, t), lambda h: (h, 0, 0, 0)),
        ],
        [pltpu.VMEM((t, t), F32)],
        (a, w),
        flops=2 * t * d * 3 * d,
    )


def middle_forward(rows, back, x, w, mix, gb):
    t, d = x.shape
    width = w.shape[3]
    shares = w.shape[1]

    def body(back_ref, x_ref, to_ref, sq_ref, mix_ref, gb_ref, o1_ref, y1_ref, x1_ref, qkv_ref):
        o1 = tn(rows.to_time(), back_ref[...]).astype(BF16)
        o1_ref[...] = o1
        y1 = jnp.zeros((t, d), F32)
        for h in range(shares):
            y1 = y1 + nt(o1[:, h * width : (h + 1) * width], to_ref[0, h])
        y1 = y1.astype(BF16)
        y1_ref[...] = y1
        x1 = x_ref[...] + nn(y1, mix_ref[...])
        x1_ref[...] = x1
        a2 = norm_rounded(x1, gb_ref[1:2], gb_ref[4:5])
        for g in range(3):
            for h in range(shares):
                qkv_ref[g, :, h * width : (h + 1) * width] = nn(a2, sq_ref[g, h]).astype(BF16)

    return call(
        body,
        (1,),
        [
            whole(back.shape),
            whole(x.shape),
            pl.BlockSpec((1, shares, d, width), lambda i: (6, 0, 0, 0)),
            pl.BlockSpec((3, shares, d, width), lambda i: (1, 0, 0, 0)),
            whole(mix.shape),
            whole(gb.shape),
        ],
        [made((t, d), BF16), made((t, d), BF16), made((t, d), F32), made((3, t, d), BF16)],
        [],
        (back, x, w, w, mix, gb),
        flops=2 * t * d * 5 * d,
    )


def space_forward(rows, qkv, x1, w):
    t, d = x1.shape
    width = w.shape[3]
    shares = w.shape[1]
    pairs = width // LANES
    rate = LOG2E / math.sqrt(HEAD_DIM)
    n = rows.frame_rows

    def body(qkv_ref, x1_ref, w_ref, o2_ref, x2_ref, log_ref):
        bias = rows.space_bias()

        @pl.loop(0, pairs)
        def _(i):
            lanes = pl.ds(pl.multiple_of(i * LANES, LANES), LANES)
            for f in range(rows.frames):
                at = slice(f * n, (f + 1) * n)
                mixed, logs = pair_forward(
                    qkv_ref[0, at, lanes], qkv_ref[1, at, lanes], qkv_ref[2, at, lanes], bias, rate
                )
                o2_ref[at, lanes] = mixed
                log_ref[0, i, f] = jnp.concatenate(logs, axis=0)

        @pl.when(pl.program_id(0) == 0)
        def _():
            x2_ref[...] = x1_ref[...]

        x2_ref[...] += nt(o2_ref[...], w_ref[0, 0])

    return call(
        body,
        (shares,),
        [
            pl.BlockSpec((3, t, width), lambda h: (0, 0, h)),
            whole(x1.shape),
            slabs(1, 7, width, d),
        ],
        [
            made((t, d), BF16, (t, width), lambda h: (0, h)),
            made((t, d), F32),
            made(
                (shares, pairs, rows.frames, 2, n),
                F32,
                (1, pairs, rows.frames, 2, n),
                lambda h: (h, 0, 0, 0, 0),
            ),
        ],
        [],
        (qkv, x1, w),
        flops=2 * t * d * d,
    )


def ff_slab(first, per_share, depth, width):
    return pl.BlockSpec(
        (1, 1, depth, width), lambda j: (first + j % per_share, j // per_share, 0, 0)
    )


def mlp_forward(rows, x2, w, gb, gb_next):
    t, d = x2.shape
    width = w.shape[3]
    shares = w.shape[1]
    per_share = (w.shape[0] - 9) // 2
    steps = shares * per_share
    last = gb_next is None

    def body(x2_ref, wi_ref, wo_ref, gb_ref, *rest):
        if last:
            x3_ref, a3_ref = rest
        else:
            gn_ref, x3_ref, send_ref, a3_ref = rest
        j = pl.program_id(0)

        @pl.when(j == 0)
        def _():
            a3_ref[...] = norm_rounded(x2_ref[...], gb_ref[2:3], gb_ref[5:6])
            x3_ref[...] = x2_ref[...]

        hid = nn(a3_ref[...], wi_ref[0, 0])
        act = (0.5 * hid * (1.0 + lax.erf(hid * HALF_ROOT))).astype(BF16)
        x3_ref[...] += nt(act, wo_ref[0, 0])

        if not last:

            @pl.when(j == steps - 1)
            def _():
                a = norm_rounded(x3_ref[...], gn_ref[0:1], gn_ref[3:4])
                send_ref[...] = nn(rows.to_time(), a).astype(BF16)

    ins = [
        whole(x2.shape),
        ff_slab(8, per_share, d, width),
        ff_slab(8 + per_share, per_share, d, width),
        whole(gb.shape),
    ]
    outs = [made((t, d), F32)]
    args = [x2, w, w, gb]
    if not last:
        ins.append(whole(gb_next.shape))
        outs.append(made((rows.time_rows, d), BF16))
        args.append(gb_next)
    return call(
        body, (steps,), ins, outs, [pltpu.VMEM((t, d), BF16)], tuple(args), flops=4 * t * d * width * steps
    )


def mlp_backward(rows, grad, x2, w, gb, me, halves):
    t, d = x2.shape
    width = w.shape[3]
    shares = w.shape[1]
    per_share = (w.shape[0] - 9) // 2
    steps = shares * per_share

    def body(me_ref, g_ref, x2_ref, wi_ref, wo_ref, gb_ref, go_ref, keep_ref, send_ref, sums_ref, a3_ref, a3t_ref, e3_ref, e3t_ref, u_ref, room_ref):
        j = pl.program_id(0)

        @pl.when(j == 0)
        def _():
            hat, _ = norm_parts(x2_ref[...])
            a3 = hat * gb_ref[2:3] + gb_ref[5:6]
            a3_ref[...] = a3.astype(BF16)
            a3t_ref[...] = a3.T.astype(BF16)
            g = g_ref[...]
            e3_ref[...] = g.astype(BF16)
            e3t_ref[...] = g.T.astype(BF16)
            u_ref[...] = jnp.zeros((t, d), F32)

        hid = nn(a3_ref[...], wi_ref[0, 0])
        phi = 0.5 * (1.0 + lax.erf(hid * HALF_ROOT))
        act = (hid * phi).astype(BF16)
        slope = phi + hid * jnp.exp(-0.5 * hid * hid) * INV_ROOT_TAU
        dhid = (nn(e3_ref[...], wo_ref[0, 0]) * slope).astype(BF16)
        split_rows(nn(e3t_ref[...], act), keep_ref, send_ref, (1, 0, 0), room_ref, me_ref)
        split_rows(nn(a3t_ref[...], dhid), keep_ref, send_ref, (0, 0, 0), room_ref, me_ref)
        u_ref[...] += nt(dhid, wi_ref[0, 0])

        @pl.when(j == steps - 1)
        def _():
            change, sums = norm_back(u_ref[...], x2_ref[...], gb_ref[2:3])
            go_ref[...] = g_ref[...] + change
            sums_ref[...] = sums

    slab_outs = halves.array(
        (2, per_share, shares), (2, 1, 1), lambda j: (0, j % per_share, j // per_share)
    )
    grad, keep, send, sums = call(
        body,
        (steps,),
        [
            SCALARS,
            whole(grad.shape),
            whole(x2.shape),
            ff_slab(8, per_share, d, width),
            ff_slab(8 + per_share, per_share, d, width),
            whole(gb.shape),
        ],
        [made((t, d), F32), *slab_outs, made((2, d), F32)],
        [
            pltpu.VMEM((t, d), BF16),
            pltpu.VMEM((d, t), BF16),
            pltpu.VMEM((t, d), BF16),
            pltpu.VMEM((d, t), BF16),
            pltpu.VMEM((t, d), F32),
            halves.room(),
        ],
        (me, grad, x2, w, w, gb),
        flops=10 * t * d * width * steps,
    )
    flat = (2 * per_share,) + keep.shape[2:]
    return grad, (keep.reshape(flat), send.reshape(flat)), sums


def space_backward(rows, grad, x1, qkv, o2, logs, w, gb, me, halves):
    t, d = x1.shape
    width = w.shape[3]
    shares = w.shape[1]
    pairs = width // LANES
    scale = 1.0 / math.sqrt(HEAD_DIM)
    rate = LOG2E * scale
    n = rows.frame_rows

    def body(me_ref, g_ref, x1_ref, qkv_ref, o2_ref, log_ref, wo_ref, wq_ref, gb_ref, go_ref, keep_ref, send_ref, sums_ref, e2_ref, e2t_ref, a2t_ref, do_ref, dqkv_ref, u_ref, room_ref):
        h = pl.program_id(0)

        @pl.when(h == 0)
        def _():
            g = g_ref[...]
            e2_ref[...] = g.astype(BF16)
            e2t_ref[...] = g.T.astype(BF16)
            hat, _ = norm_parts(x1_ref[...])
            a2t_ref[...] = (hat * gb_ref[1:2] + gb_ref[4:5]).T.astype(BF16)
            u_ref[...] = jnp.zeros((t, d), F32)

        bias = rows.space_bias()
        split_rows(nn(e2t_ref[...], o2_ref[...]), keep_ref, send_ref, (0, 0), room_ref, me_ref)
        do_ref[...] = nn(e2_ref[...], wo_ref[0, 0]).astype(BF16)

        @pl.loop(0, pairs)
        def _(i):
            lanes = pl.ds(pl.multiple_of(i * LANES, LANES), LANES)
            for f in range(rows.frames):
                at = slice(f * n, (f + 1) * n)
                log = log_ref[0, i, f]
                grads = pair_backward(
                    qkv_ref[0, at, lanes],
                    qkv_ref[1, at, lanes],
                    qkv_ref[2, at, lanes],
                    do_ref[at, lanes],
                    (log[0:1], log[1:2]),
                    bias,
                    rate,
                    scale,
                )
                for part in range(3):
                    dqkv_ref[part, at, lanes] = grads[part]

        for part in range(3):
            split_rows(
                nn(a2t_ref[...], dqkv_ref[part]), keep_ref, send_ref, (part + 1, 0), room_ref, me_ref
            )
            u_ref[...] += nt(dqkv_ref[part], wq_ref[part, 0])

        @pl.when(h == shares - 1)
        def _():
            change, sums = norm_back(u_ref[...], x1_ref[...], gb_ref[1:2])
            go_ref[...] = g_ref[...] + change
            sums_ref[...] = sums

    grad, keep, send, sums = call(
        body,
        (shares,),
        [
            SCALARS,
            whole(grad.shape),
            whole(x1.shape),
            pl.BlockSpec((3, t, width), lambda h: (0, 0, h)),
            pl.BlockSpec((t, width), lambda h: (0, h)),
            pl.BlockSpec((1,) + logs.shape[1:], lambda h: (h, 0, 0, 0, 0)),
            slabs(1, 7, width, d),
            slabs(3, 3, width, d),
            whole(gb.shape),
        ],
        [
            made((t, d), F32),
            *halves.array((4, shares), (4, 1), lambda h: (0, h)),
            made((2, d), F32),
        ],
        [
            pltpu.VMEM((t, d), BF16),
            pltpu.VMEM((d, t), BF16),
            pltpu.VMEM((d, t), BF16),
            pltpu.VMEM((t, width), BF16),
            pltpu.VMEM((3, t, width), BF16),
            pltpu.VMEM((t, d), F32),
            halves.room(),
        ],
        (me, grad, x1, qkv, o2, logs, w, w, gb),
        flops=2 * t * d * d * 8,
    )
    return grad, (keep, send), sums


def mix_fits(depth, shards, shares):
    return depth // (shards * shares) % 8 == 0


def middle_backward(rows, grad, y1, o1, w, mix, me, halves, shards):
    t, d = grad.shape
    width = w.shape[3]
    shares = w.shape[1]
    fits = mix_fits(d, shards, shares)
    part = d // (shards * shares)

    def body(me_ref, g_ref, y1_ref, o1_ref, to_ref, mix_ref, send_ref, gk_ref, gs_ref, *rest):
        if fits:
            room_ref, order_ref = rest
        else:
            gm_ref, room_ref = rest
        e1 = g_ref[...].astype(BF16)
        dy1 = nt(e1, mix_ref[...]).astype(BF16)
        send = rows.to_time()
        for h in range(shares):
            lanes = slice(h * width, (h + 1) * width)
            do1 = nn(dy1, to_ref[0, h]).astype(BF16)
            send_ref[:, lanes] = nn(send, do1).astype(BF16)
            split_rows(tn(dy1, o1_ref[:, lanes]), gk_ref, gs_ref, (0, h), room_ref, me_ref)
        gm = tn(y1_ref[...], e1)
        if fits:
            gm = gm.reshape(shards, shares, part, d)
            for h in range(shares):
                for half in range(shares):
                    order_ref[:, half] = gm[:, h, :, half * width : (half + 1) * width]
                split_rows(order_ref[...], gk_ref, gs_ref, (1, h), room_ref, me_ref)
        else:
            gm_ref[...] = gm.astype(BF16)

    outs = [made((rows.time_rows, d), BF16)]
    outs += halves.array((1 + fits, shares), (1 + fits, shares), lambda i: (0, 0))
    scratch = [halves.room()]
    if fits:
        scratch.append(pltpu.VMEM((shards, shares, part, width), F32))
    else:
        outs.append(made((d, d), BF16))
    got = call(
        body,
        (1,),
        [
            SCALARS,
            whole(grad.shape),
            whole(y1.shape),
            whole(o1.shape),
            pl.BlockSpec((1, shares, d, width), lambda i: (6, 0, 0, 0)),
            whole(mix.shape),
        ],
        outs,
        scratch,
        (me, grad, y1, o1, w, mix),
        flops=8 * t * d * d,
    )
    do1, keep, send = got[:3]
    if not fits:
        gm = mix_slab(got[3], shards, shares).reshape((1, shares, halves.pairs, 2) + keep.shape[3:])
        keep = jnp.concatenate((keep, lax.dynamic_index_in_dim(gm, me[0], 3, keepdims=False)), axis=0)
        send = jnp.concatenate((send, lax.dynamic_index_in_dim(gm, 1 - me[0], 3, keepdims=False)), axis=0)
    return do1, (keep, send)


def time_backward(rows, do1, a, qkv, logs, w, me, halves):
    t, d = a.shape
    width = w.shape[3]
    shares = w.shape[1]
    pairs = width // LANES
    scale = 1.0 / math.sqrt(HEAD_DIM)
    rate = LOG2E * scale

    def body(me_ref, do_ref, a_ref, qkv_ref, log_ref, w_ref, out_ref, keep_ref, send_ref, bias_ref, dqkv_ref, at_ref, u_ref, room_ref):
        h = pl.program_id(0)

        @pl.when(h == 0)
        def _():
            bias_ref[...] = rows.time_bias()
            at_ref[...] = a_ref[...].T
            u_ref[...] = jnp.zeros((t, d), F32)

        @pl.loop(0, pairs)
        def _(i):
            lanes = pl.ds(pl.multiple_of(i * LANES, LANES), LANES)
            log = log_ref[0, i]
            grads = pair_backward(
                qkv_ref[0, :, lanes],
                qkv_ref[1, :, lanes],
                qkv_ref[2, :, lanes],
                do_ref[:, lanes],
                (log[0:1], log[1:2]),
                bias_ref[...],
                rate,
                scale,
            )
            for part in range(3):
                dqkv_ref[part, :, lanes] = grads[part]

        for part in range(3):
            split_rows(
                nn(at_ref[...], dqkv_ref[part]), keep_ref, send_ref, (part, 0), room_ref, me_ref
            )
            u_ref[...] += nt(dqkv_ref[part], w_ref[part, 0])

        @pl.when(h == shares - 1)
        def _():
            out_ref[...] = u_ref[...].astype(BF16)

    da1, keep, send = call(
        body,
        (shares,),
        [
            SCALARS,
            pl.BlockSpec((t, width), lambda h: (0, h)),
            whole(a.shape),
            pl.BlockSpec((3, t, width), lambda h: (0, 0, h)),
            pl.BlockSpec((1,) + logs.shape[1:], lambda h: (h, 0, 0, 0)),
            slabs(3, 0, width, d),
        ],
        [
            made((t, d), BF16),
            *halves.array((3, shares), (3, 1), lambda h: (0, h)),
        ],
        [
            pltpu.VMEM((t, t), F32),
            pltpu.VMEM((3, t, width), BF16),
            pltpu.VMEM((d, t), BF16),
            pltpu.VMEM((t, d), F32),
            halves.room(),
        ],
        (me, do1, a, qkv, logs, w),
        flops=2 * t * d * d * 6,
    )
    return da1, (keep, send)


def first_norm_back(rows, back, x, grad, gb):
    t, d = x.shape

    def body(back_ref, x_ref, g_ref, gb_ref, go_ref, sums_ref):
        u = tn(rows.to_time(), back_ref[...])
        change, sums = norm_back(u, x_ref[...], gb_ref[0:1])
        go_ref[...] = g_ref[...] + change
        sums_ref[...] = sums

    return call(
        body,
        (1,),
        [whole(back.shape), whole(x.shape), whole(grad.shape), whole(gb.shape)],
        [made((t, d), F32), made((2, d), F32)],
        [],
        (back, x, grad, gb),
    )


def swap_places(rows_array):
    return lax.all_to_all(rows_array, "seq", split_axis=0, concat_axis=0, tiled=True)


def pack_layer(time_qkv, time_out, time_mix, space_qkv, space_out, mlp_in, mlp_out):
    width = time_qkv.shape[2]
    r = time_qkv.shape[0]
    halves = time_mix.shape[1] // width

    def columns(a):
        return a.reshape(r, -1, width).transpose(1, 0, 2)

    mix = time_mix.reshape(-1, halves, width).transpose(1, 0, 2).reshape(1, r, width)
    return jnp.concatenate(
        (
            columns(time_qkv),
            columns(space_qkv),
            time_out.T[None],
            space_out.T[None],
            columns(mlp_in),
            columns(mlp_out.T),
            mix,
        ),
        axis=0,
    )


def gather_slabs(pack):
    full = lax.all_gather(pack, ("head", "clip", "seq"), axis=1, tiled=True)
    return full.reshape(pack.shape[0], lax.axis_size("head"), -1, pack.shape[2])


def mix_whole(slab, shards):
    shares, depth, width = slab.shape
    part = slab.reshape(shares, shards, shares, depth // (shards * shares), width)
    return part.transpose(1, 0, 3, 2, 4).reshape(depth, shares * width)


def mix_slab(whole_grad, shards, shares):
    depth, full = whole_grad.shape
    width = full // shares
    part = whole_grad.reshape(shards, shares, depth // (shards * shares), shares, width)
    return part.transpose(1, 0, 3, 2, 4).reshape(1, shares, depth, width)


class Term:
    def __init__(self, array, names, first, count):
        self.array = array
        self.names = names
        self.first = first
        self.count = count

    def cut(self, first, count):
        return Term(self.array, self.names, self.first + first, count)


class Job:
    def __init__(self, pieces, other, ways):
        self.pieces = pieces
        self.other = other
        self.ways = ways
        names = pieces[0][-1].names
        self.lead = () if other is None else tuple(2 for n in names if n != other)
        self.count = sum(piece[0].count for piece in pieces)
        self.rows, self.width = pieces[0][0].array.shape[-2:]

    def shape(self):
        if self.other is None:
            return (self.ways, self.count, self.rows // self.ways, self.width)
        return (self.count,) + self.lead + (self.rows, self.width)


def fold(jobs, me):
    place = {"x": 1, "h": 2}
    terms = [t for job in jobs for piece in job.pieces for t in piece]
    arrays = []
    for t in terms:
        if not any(t.array is a for a in arrays):
            arrays.append(t.array)
    number = [next(i for i, a in enumerate(arrays) if a is t.array) for t in terms]
    rooms = []
    for job in jobs:
        for piece in job.pieces:
            rooms += [(t.count,) + job.lead + (job.rows, job.width) for t in piece]

    def body(me_ref, *refs):
        sources = refs[: len(arrays)]
        outs = refs[len(arrays) : len(arrays) + len(jobs)]
        held = refs[len(arrays) + len(jobs) : -1]
        sems = refs[-1]
        copies = []
        for job in jobs:
            for piece in job.pieces:
                for t in piece:
                    n = len(copies)
                    at = [pl.ds(t.first, t.count)]
                    for name in t.names:
                        if name == job.other:
                            at.append(1 - me_ref[place[name]])
                        elif job.other is not None and name in job.pieces[0][-1].names:
                            at.append(slice(None))
                        else:
                            at.append(me_ref[place[name]])
                    copies.append(
                        pltpu.make_async_copy(sources[number[n]].at[tuple(at)], held[n], sems.at[n])
                    )
        for copy in copies:
            copy.start()
        n = 0
        for job, out in zip(jobs, outs):
            base = 0
            for piece in job.pieces:
                these = held[n : n + len(piece)]
                for k in range(len(piece)):
                    copies[n + k].wait()
                n += len(piece)

                @pl.loop(0, piece[0].count)
                def _(i, these=these, base=base, out=out, job=job):
                    def total(at):
                        value = these[0][at].astype(F32)
                        for one in these[1:]:
                            value = value + one[at].astype(F32)
                        return value.astype(BF16)

                    if job.other is None:
                        value = total((i,))
                        r = job.rows // job.ways
                        for s in range(job.ways):
                            out[s, base + i] = value[s * r : (s + 1) * r]
                    elif job.lead:
                        for k in range(2):
                            out[base + i, k] = total((i, k))
                    else:
                        out[base + i] = total((i,))

                base += piece[0].count

    moved = sum(2 * math.prod(r) for r in rooms) + sum(2 * math.prod(j.shape()) for j in jobs)
    return pl.pallas_call(
        body,
        out_shape=[jax.ShapeDtypeStruct(job.shape(), BF16) for job in jobs],
        in_specs=[SCALARS] + [pl.BlockSpec(memory_space=pl.ANY)] * len(arrays),
        out_specs=[pl.BlockSpec(memory_space=pltpu.VMEM)] * len(jobs),
        scratch_shapes=[pltpu.VMEM(r, BF16) for r in rooms] + [pltpu.SemaphoreType.DMA((len(rooms),))],
        compiler_params=pltpu.CompilerParams(vmem_limit_bytes=VMEM),
        cost_estimate=pl.CostEstimate(flops=0, bytes_accessed=moved, transcendentals=0),
    )(me, *arrays)


def cross(a, name):
    axis, bit = ("head", 0) if name == "h" else ("clip", 1 if name == "x" else 0)
    size = lax.axis_size(axis)
    return lax.ppermute(a, axis, [(i, i ^ (1 << bit)) for i in range(size)])


class Group:
    def __init__(self, halves_of):
        self.pieces = []
        for keep, send in halves_of:
            got = cross(send, "c")
            n = keep.shape[0]
            self.pieces.append([Term(a, ("h", "x"), 0, n) for a in (keep, got)])
        total = sum(p[0].count for p in self.pieces)
        self.parts = ([], [])
        seen = 0
        for piece in self.pieces:
            n = piece[0].count
            first = min(max((total + 1) // 2 - seen, 0), n)
            if first:
                self.parts[0].append([t.cut(0, first) for t in piece])
            if n > first:
                self.parts[1].append([t.cut(first, n - first) for t in piece])
            seen += n
        self.step = 0
        self.result = None

    def jobs(self, ways):
        if self.step == 2:
            return [Job(self.parts[0] + self.parts[1], None, ways)]
        orders = (("x", "h"), ("h", "x"))
        return [Job(part, order[self.step], ways) for part, order in zip(self.parts, orders)]

    def go(self, sums):
        if self.step == 2:
            got = lax.all_to_all(sums[0], "seq", split_axis=0, concat_axis=0, tiled=True)
            self.result = jnp.sum(got.astype(F32), axis=0)
        else:
            orders = (("x", "h"), ("h", "x"))
            left = (orders[0][1 - self.step], orders[1][1 - self.step])
            for part, order, name, one in zip(self.parts, orders, left, sums):
                got = cross(one, order[self.step])
                base = 0
                for piece in part:
                    names = () if self.step else (name,)
                    piece.append(Term(got, names, base, piece[0].count))
                    base += piece[0].count
        self.step += 1


def move(x, groups, me):
    ways = lax.axis_size("seq")
    jobs = [g.jobs(ways) for g in groups]
    sums = fold([j for some in jobs for j in some], me)
    x, sums = lax.optimization_barrier((x, sums))
    for g, some in zip(groups, jobs):
        g.go(sums[: len(some)])
        sums = sums[len(some) :]
    return x


def reduce_plain(halves_of, core):
    def joined(keep, send):
        low = jnp.where(core == 0, keep, send)
        high = jnp.where(core == 0, send, keep)
        n, shares, pairs, depth, width = keep.shape
        return jnp.stack((low, high), axis=3).reshape(n, shares, 2 * pairs * depth, width)

    g = jnp.concatenate([joined(*pair) for pair in halves_of], axis=0)
    g = lax.psum_scatter(g, "head", scatter_dimension=1, tiled=True)
    g = lax.psum_scatter(g.astype(F32), ("clip", "seq"), scatter_dimension=2, tiled=True)
    return g[:, 0]


def gather_norms(gain, bias):
    layers, norms, part = gain.shape
    both = jnp.concatenate((gain, bias), axis=1).reshape(1, -1)
    count = lax.axis_size("clip") * lax.axis_size("seq") * lax.axis_size("head")
    width = round_up(both.shape[1], 128)
    padded = jnp.pad(both, ((0, 0), (0, width - both.shape[1])))
    every = lax.all_to_all(
        jnp.broadcast_to(padded, (count, width)), ALL, split_axis=0, concat_axis=0, tiled=True
    )[:, : both.shape[1]]
    return every.reshape(count, layers * 2 * norms, part).transpose(1, 0, 2).reshape(layers, 2 * norms, -1)


def reduce_norms(sums):
    count = lax.axis_size("clip") * lax.axis_size("seq") * lax.axis_size("head")
    rows, features = sums.shape
    part = features // count
    a = sums.reshape(rows, count, part).transpose(1, 0, 2).reshape(count, rows * part)
    width = round_up(rows * part, 128)
    a = jnp.pad(a, ((0, 0), (0, width - rows * part)))
    every = lax.all_to_all(a, ALL, split_axis=0, concat_axis=0, tiled=True)
    return jnp.sum(every, axis=0)[: rows * part].reshape(rows, part)


def on_device(
    tokens,
    cotangent,
    time_qkv,
    time_out,
    time_mix,
    space_qkv,
    space_out,
    mlp_in,
    mlp_out,
    norm_gain,
    norm_bias,
):
    layers = time_qkv.shape[0]
    clips, frames, places, d = tokens.shape
    ways = lax.axis_size("seq")
    shards = lax.axis_size("clip") * ways
    rows = Rows(clips * frames, places, ways)
    shares = lax.axis_size("head")

    def as_rows(a):
        a = a.astype(F32).reshape(rows.frames, places, d)
        a = jnp.pad(a, ((0, 0), (0, rows.frame_rows - places), (0, 0)))
        return a.reshape(rows.rows, d)

    def from_rows(a):
        a = a.reshape(rows.frames, rows.frame_rows, d)[:, :places]
        return a.reshape(tokens.shape)

    gbs = gather_norms(norm_gain, norm_bias)
    gb = [gbs[l] for l in range(layers)]
    weights = [
        gather_slabs(
            pack_layer(
                time_qkv[l], time_out[l], time_mix[l], space_qkv[l], space_out[l], mlp_in[l], mlp_out[l]
            )
        )
        for l in range(layers)
    ]
    mixes = [mix_whole(w[-1], shards) for w in weights]

    x = as_rows(tokens)
    send = send_first(rows, x, gb[0])
    kept = []
    for l in range(layers):
        w = weights[l]
        a1 = swap_places(send)
        qkv1, o1_time, log1 = time_forward(rows, a1, w, shares)
        back = swap_places(o1_time)
        o1, y1, x1, qkv2 = middle_forward(rows, back, x, w, mixes[l], gb[l])
        o2, x2, log2 = space_forward(rows, qkv2, x1, w)
        kept.append((x, a1, qkv1, log1, o1, y1, x1, qkv2, o2, log2, x2))
        if l + 1 < layers:
            x, send = mlp_forward(rows, x2, w, gb[l], gb[l + 1])
        else:
            (x,) = mlp_forward(rows, x2, w, gb[l], None)
    output = from_rows(x).astype(BF16)

    grad = as_rows(cotangent)
    halves = Halves(lax.axis_size("clip"), d, time_qkv.shape[3])
    clip = lax.axis_index("clip")
    me = jnp.stack((clip & 1, (clip >> 1) & 1, lax.axis_index("head"))).astype(jnp.int32)
    norm_rows = [None] * layers
    summed = [None] * layers
    late = None
    quick = lax.axis_size("clip") == 4 and shares == 2 and time_qkv.shape[1] % 16 == 0
    for l in reversed(range(layers)):
        w = weights[l]
        x, a1, qkv1, log1, o1, y1, x1, qkv2, o2, log2, x2 = kept[l]
        grad, g_ff, s3 = mlp_backward(rows, grad, x2, w, gb[l], me, halves)
        ff = Group([g_ff]) if quick else None
        grad, g_space, s2 = space_backward(rows, grad, x1, qkv2, o2, log2, w, gb[l], me, halves)
        do1, g_out = middle_backward(rows, grad, y1, o1, w, mixes[l], me, halves, shards)
        do1 = swap_places(do1)
        first = l == 0
        if quick:
            out = Group([g_space, g_out]) if first else None
            do1 = move(do1, [ff] + (late or []), me)
        da1, g_time = time_backward(rows, do1, a1, qkv1, log1, w, me, halves)
        da1 = swap_places(da1)
        if quick and first:
            da1 = move(da1, [ff, out] + (late[1:] if late else []), me)
            time = Group([g_time])
        elif quick:
            out = Group([g_space, g_out, g_time])
            da1 = move(da1, [ff, out], me)
            late = [ff, out]
        grad, s1 = first_norm_back(rows, da1, x, grad, gb[l])
        norm_rows[l] = jnp.concatenate((s1[0:1], s2[0:1], s3[0:1], s1[1:2], s2[1:2], s3[1:2]), axis=0)
        if quick:
            summed[l] = [ff, out] + ([time] if first else [])
        else:
            summed[l] = [reduce_plain([g_ff, g_space, g_out, g_time], clip & 1)]
    if quick:
        move((), [ff, out, time], me)
        move((), [out, time], me)
        move((), [time], me)
        summed = [[g.result for g in some] for some in summed]
    cuts = (g_ff[0].shape[0], g_space[0].shape[0], g_out[0].shape[0], g_time[0].shape[0])
    results = []
    for some in summed:
        slabs_of = jnp.concatenate(some, axis=0)
        ends = [sum(cuts[: i + 1]) for i in range(4)]
        results.append([slabs_of[e - c : e] for c, e in zip(cuts, ends)])
    tokens_grad = from_rows(grad)
    norm_sums = reduce_norms(jnp.concatenate(norm_rows, axis=0)).reshape(layers, 2, 3, -1)

    def stacked(form):
        return jnp.stack([form(*results[l]) for l in range(layers)])

    def rows_of(a):
        return a.transpose(1, 0, 2)

    def flat(a):
        return rows_of(a).reshape(a.shape[1], -1)

    def mix_rows(a):
        r, width = a.shape
        return a.reshape(shares, r // shares, width).transpose(1, 0, 2).reshape(r // shares, -1)

    per_share = mlp_in.shape[2] // time_qkv.shape[3]
    return (
        output,
        tokens_grad,
        stacked(lambda ff, s, t, q: rows_of(q)),
        stacked(lambda ff, s, t, q: t[0].T),
        stacked(lambda ff, s, t, q: mix_rows(t[1])),
        stacked(lambda ff, s, t, q: rows_of(s[1:])),
        stacked(lambda ff, s, t, q: s[0].T),
        stacked(lambda ff, s, t, q: flat(ff[:per_share])),
        stacked(lambda ff, s, t, q: flat(ff[per_share:]).T),
        norm_sums[:, 0],
        norm_sums[:, 1],
    )


def solution(mesh):
    token_spec = P(("clip", "head"), "seq", None, None)
    in_specs = (
        token_spec,
        token_spec,
        P(None, ("clip", "seq"), None, "head"),
        P(None, "head", ("clip", "seq")),
        P(None, ("clip", "seq", "head"), None),
        P(None, ("clip", "seq"), None, "head"),
        P(None, "head", ("clip", "seq")),
        P(None, ("clip", "seq"), "head"),
        P(None, "head", ("clip", "seq")),
        P(None, None, ("clip", "seq", "head")),
        P(None, None, ("clip", "seq", "head")),
    )
    return jax.shard_map(
        on_device, mesh=mesh, in_specs=in_specs, out_specs=in_specs, check_vma=False
    )
```

```python
import functools
import math

import jax
import jax.numpy as jnp
from jax import lax
from jax.experimental import pallas as pl
from jax.experimental.pallas import tpu as pltpu
from jax.sharding import PartitionSpec as P

HEAD_DIM = 64
NORM_EPS = 1e-06
HALF_ROOT = 0.7071067811865476
INV_ROOT_TAU = 0.3989422804014327
LOG2E = 1.4426950408889634
FAR = -1e30
LANES = 128
VMEM = 56 * 1024 * 1024
SHOWN = 1.0
ALL = ("clip", "seq", "head")
BF16 = jnp.bfloat16
F32 = jnp.float32


def round_up(value, step):
    return -(-value // step) * step


def nn(a, b):
    return lax.dot_general(a, b, (((1,), (0,)), ((), ())), preferred_element_type=F32)


def nt(a, b):
    return lax.dot_general(a, b, (((1,), (1,)), ((), ())), preferred_element_type=F32)


def tn(a, b):
    return lax.dot_general(a, b, (((0,), (0,)), ((), ())), preferred_element_type=F32)


def norm_parts(x):
    mean = jnp.mean(x, axis=-1, keepdims=True)
    centred = x - mean
    spread = lax.rsqrt(jnp.mean(centred * centred, axis=-1, keepdims=True) + NORM_EPS)
    return centred * spread, spread


def norm_rounded(x, gain, bias):
    hat, _ = norm_parts(x)
    return (hat * gain + bias).astype(BF16)


def norm_back(u, x, gain):
    hat, spread = norm_parts(x)
    scaled = u * gain
    mean_scaled = jnp.mean(scaled, axis=-1, keepdims=True)
    mean_cross = jnp.mean(scaled * hat, axis=-1, keepdims=True)
    change = spread * (scaled - mean_scaled - hat * mean_cross)
    sums = jnp.concatenate(
        (jnp.sum(u * hat, axis=0, keepdims=True), jnp.sum(u, axis=0, keepdims=True)), axis=0
    )
    return change, sums


class Rows:
    def __init__(self, frames, places, ways):
        self.frames = frames
        self.places = places
        self.ways = ways
        self.frame_rows = round_up(places, 16)
        self.rows = frames * self.frame_rows
        self.block = places // ways
        self.chunk = round_up(frames * self.block, 8)
        self.time_rows = ways * self.chunk

    def split(self, r):
        way = jnp.zeros_like(r)
        for k in range(1, self.ways):
            way = way + (r >= k * self.chunk).astype(jnp.int32)
        rest = r - way * self.chunk
        frame = jnp.zeros_like(r)
        for k in range(1, self.frames):
            frame = frame + (rest >= k * self.block).astype(jnp.int32)
        real = rest < self.frames * self.block
        return way, frame, rest - frame * self.block, real

    def to_time(self):
        r = lax.broadcasted_iota(jnp.int32, (self.time_rows, 1), 0)
        way, frame, place, real = self.split(r)
        source = jnp.where(real, frame * self.frame_rows + way * self.block + place, -1)
        c = lax.broadcasted_iota(jnp.int32, (self.time_rows, self.rows), 1)
        return jnp.where(c == source, 1.0, 0.0).astype(BF16)

    def time_bias(self):
        def label(r):
            _, _, place, real = self.split(r)
            return jnp.where(real, place, -1)

        a = label(lax.broadcasted_iota(jnp.int32, (self.time_rows, 1), 0))
        b = label(lax.broadcasted_iota(jnp.int32, (1, self.time_rows), 1))
        return jnp.where(a == b, 0.0, FAR).astype(F32)

    def space_bias(self):
        a = lax.broadcasted_iota(jnp.int32, (self.frame_rows, 1), 0)
        return jnp.where(a < self.places, 0.0, FAR).astype(F32)


def lane_masks(rows):
    lane = lax.broadcasted_iota(jnp.int32, (rows, LANES), 1)
    return lane < HEAD_DIM


def one_of(value, low, half):
    zero = jnp.zeros_like(value)
    return jnp.where(low, value, zero) if half == 0 else jnp.where(low, zero, value)


def pair_forward(q, k, v, bias, rate):
    low = lane_masks(q.shape[0])
    mixed, logs = [], []
    for half in range(2):
        s = nt(k, one_of(q, low, half)) + bias
        peak = jnp.max(s, axis=0, keepdims=True)
        e = jnp.exp2((s - peak) * rate)
        total = jnp.sum(e, axis=0, keepdims=True)
        soft = (e * (1.0 / total)).astype(BF16)
        mixed.append(tn(soft, v))
        logs.append(peak * rate + jnp.log2(total))
    return jnp.where(low, mixed[0], mixed[1]).astype(BF16), logs


def pair_backward(q, k, v, do, logs, bias, rate, scale):
    low = lane_masks(q.shape[0])
    dq, dk, dv = [], [], []
    for half in range(2):
        s = nt(k, one_of(q, low, half)) + bias
        soft = jnp.exp2(s * rate - logs[half])
        dp = nt(v, one_of(do, low, half))
        ds = (soft * (dp - jnp.sum(soft * dp, axis=0, keepdims=True))).astype(BF16)
        dv.append(nn(soft.astype(BF16), do))
        dk.append(nn(ds, q))
        dq.append(tn(ds, k))
    return (
        (jnp.where(low, dq[0], dq[1]) * scale).astype(BF16),
        (jnp.where(low, dk[0], dk[1]) * scale).astype(BF16),
        jnp.where(low, dv[0], dv[1]).astype(BF16),
    )


def split_rows(value, keep_ref, send_ref, at, room_ref, me_ref):
    mine = me_ref[0]
    room_ref[...] = value.reshape(room_ref.shape)
    keep_ref[at] = room_ref[:, mine].astype(BF16)
    send_ref[at] = room_ref[:, 1 - mine].astype(BF16)


class Halves:
    def __init__(self, clips, depth, width):
        self.pairs = clips // 2
        self.rows = depth // clips
        self.width = width

    def array(self, lead, block, index):
        tail = (self.pairs, self.rows, self.width)
        one = lambda: made(lead + tail, BF16, block + tail, lambda *g: index(*g) + (0, 0, 0))
        return [one(), one()]

    def room(self):
        return pltpu.VMEM((self.pairs, 2, self.rows, self.width), F32)


SCALARS = pl.BlockSpec(memory_space=pltpu.SMEM)


def call(body, grid, ins, outs, scratch, args, flops=0):
    specs = [spec for spec in ins]
    moved = sum(math.prod(o.shape) * o.dtype.itemsize for o, _ in outs)
    moved += sum(math.prod(a.shape) * a.dtype.itemsize for a in args)
    return pl.pallas_call(
        body,
        out_shape=[shape for shape, _ in outs],
        grid=grid,
        in_specs=specs,
        out_specs=[spec for _, spec in outs],
        scratch_shapes=scratch,
        compiler_params=pltpu.CompilerParams(vmem_limit_bytes=VMEM),
        cost_estimate=pl.CostEstimate(
            flops=int(flops * SHOWN), bytes_accessed=int(moved * SHOWN), transcendentals=0
        ),
    )(*args)


def whole(shape):
    zeros = (0,) * len(shape)
    return pl.BlockSpec(shape, lambda *_: zeros)


def made(shape, dtype, block=None, index=None):
    spec = whole(shape) if block is None else pl.BlockSpec(block, index)
    return jax.ShapeDtypeStruct(shape, dtype), spec


def slabs(count, first, width, depth):
    return pl.BlockSpec((count, 1, depth, width), lambda h, *_: (first // count, h, 0, 0))


def send_first(rows, x, gb):
    def body(x_ref, gb_ref, out_ref):
        a = norm_rounded(x_ref[...], gb_ref[0:1], gb_ref[3:4])
        out_ref[...] = nn(rows.to_time(), a).astype(BF16)

    d = x.shape[1]
    return call(
        body, (1,), [whole(x.shape), whole(gb.shape)], [made((rows.time_rows, d), BF16)], [], (x, gb)
    )[0]


def time_forward(rows, a, w, head_shares):
    t, d = a.shape
    width = w.shape[3]
    pairs = width // LANES
    rate = LOG2E / math.sqrt(HEAD_DIM)

    def body(a_ref, w_ref, qkv_ref, out_ref, log_ref, bias_ref):
        @pl.when(pl.program_id(0) == 0)
        def _():
            bias_ref[...] = rows.time_bias()

        act = a_ref[...]
        for g in range(3):
            qkv_ref[g] = nn(act, w_ref[g, 0]).astype(BF16)

        @pl.loop(0, pairs)
        def _(i):
            lanes = pl.ds(pl.multiple_of(i * LANES, LANES), LANES)
            mixed, logs = pair_forward(
                qkv_ref[0, :, lanes], qkv_ref[1, :, lanes], qkv_ref[2, :, lanes], bias_ref[...], rate
            )
            out_ref[:, lanes] = mixed
            log_ref[0, i] = jnp.concatenate(logs, axis=0)

    return call(
        body,
        (head_shares,),
        [whole(a.shape), slabs(3, 0, width, d)],
        [
            made((3, t, d), BF16, (3, t, width), lambda h: (0, 0, h)),
            made((t, d), BF16, (t, width), lambda h: (0, h)),
            made((head_shares, pairs, 2, t), F32, (1, pairs, 2, t), lambda h: (h, 0, 0, 0)),
        ],
        [pltpu.VMEM((t, t), F32)],
        (a, w),
        flops=2 * t * d * 3 * d,
    )


def middle_forward(rows, back, x, w, mix, gb):
    t, d = x.shape
    width = w.shape[3]
    shares = w.shape[1]

    def body(back_ref, x_ref, to_ref, sq_ref, mix_ref, gb_ref, o1_ref, y1_ref, x1_ref, qkv_ref):
        o1 = tn(rows.to_time(), back_ref[...]).astype(BF16)
        o1_ref[...] = o1
        y1 = jnp.zeros((t, d), F32)
        for h in range(shares):
            y1 = y1 + nt(o1[:, h * width : (h + 1) * width], to_ref[0, h])
        y1 = y1.astype(BF16)
        y1_ref[...] = y1
        x1 = x_ref[...] + nn(y1, mix_ref[...])
        x1_ref[...] = x1
        a2 = norm_rounded(x1, gb_ref[1:2], gb_ref[4:5])
        for g in range(3):
            for h in range(shares):
                qkv_ref[g, :, h * width : (h + 1) * width] = nn(a2, sq_ref[g, h]).astype(BF16)

    return call(
        body,
        (1,),
        [
            whole(back.shape),
            whole(x.shape),
            pl.BlockSpec((1, shares, d, width), lambda i: (6, 0, 0, 0)),
            pl.BlockSpec((3, shares, d, width), lambda i: (1, 0, 0, 0)),
            whole(mix.shape),
            whole(gb.shape),
        ],
        [made((t, d), BF16), made((t, d), BF16), made((t, d), F32), made((3, t, d), BF16)],
        [],
        (back, x, w, w, mix, gb),
        flops=2 * t * d * 5 * d,
    )


def space_forward(rows, qkv, x1, w):
    t, d = x1.shape
    width = w.shape[3]
    shares = w.shape[1]
    pairs = width // LANES
    rate = LOG2E / math.sqrt(HEAD_DIM)
    n = rows.frame_rows

    def body(qkv_ref, x1_ref, w_ref, o2_ref, x2_ref, log_ref):
        bias = rows.space_bias()

        @pl.loop(0, pairs)
        def _(i):
            lanes = pl.ds(pl.multiple_of(i * LANES, LANES), LANES)
            for f in range(rows.frames):
                at = slice(f * n, (f + 1) * n)
                mixed, logs = pair_forward(
                    qkv_ref[0, at, lanes], qkv_ref[1, at, lanes], qkv_ref[2, at, lanes], bias, rate
                )
                o2_ref[at, lanes] = mixed
                log_ref[0, i, f] = jnp.concatenate(logs, axis=0)

        @pl.when(pl.program_id(0) == 0)
        def _():
            x2_ref[...] = x1_ref[...]

        x2_ref[...] += nt(o2_ref[...], w_ref[0, 0])

    return call(
        body,
        (shares,),
        [
            pl.BlockSpec((3, t, width), lambda h: (0, 0, h)),
            whole(x1.shape),
            slabs(1, 7, width, d),
        ],
        [
            made((t, d), BF16, (t, width), lambda h: (0, h)),
            made((t, d), F32),
            made(
                (shares, pairs, rows.frames, 2, n),
                F32,
                (1, pairs, rows.frames, 2, n),
                lambda h: (h, 0, 0, 0, 0),
            ),
        ],
        [],
        (qkv, x1, w),
        flops=2 * t * d * d,
    )


def ff_slab(first, per_share, depth, width):
    return pl.BlockSpec(
        (1, 1, depth, width), lambda j: (first + j % per_share, j // per_share, 0, 0)
    )


def mlp_forward(rows, x2, w, gb, gb_next):
    t, d = x2.shape
    width = w.shape[3]
    shares = w.shape[1]
    per_share = (w.shape[0] - 9) // 2
    steps = shares * per_share
    last = gb_next is None

    def body(x2_ref, wi_ref, wo_ref, gb_ref, *rest):
        if last:
            x3_ref, a3_ref = rest
        else:
            gn_ref, x3_ref, send_ref, a3_ref = rest
        j = pl.program_id(0)

        @pl.when(j == 0)
        def _():
            a3_ref[...] = norm_rounded(x2_ref[...], gb_ref[2:3], gb_ref[5:6])
            x3_ref[...] = x2_ref[...]

        hid = nn(a3_ref[...], wi_ref[0, 0])
        act = (0.5 * hid * (1.0 + lax.erf(hid * HALF_ROOT))).astype(BF16)
        x3_ref[...] += nt(act, wo_ref[0, 0])

        if not last:

            @pl.when(j == steps - 1)
            def _():
                a = norm_rounded(x3_ref[...], gn_ref[0:1], gn_ref[3:4])
                send_ref[...] = nn(rows.to_time(), a).astype(BF16)

    ins = [
        whole(x2.shape),
        ff_slab(8, per_share, d, width),
        ff_slab(8 + per_share, per_share, d, width),
        whole(gb.shape),
    ]
    outs = [made((t, d), F32)]
    args = [x2, w, w, gb]
    if not last:
        ins.append(whole(gb_next.shape))
        outs.append(made((rows.time_rows, d), BF16))
        args.append(gb_next)
    return call(
        body, (steps,), ins, outs, [pltpu.VMEM((t, d), BF16)], tuple(args), flops=4 * t * d * width * steps
    )


def mlp_backward(rows, grad, x2, w, gb, me, halves):
    t, d = x2.shape
    width = w.shape[3]
    shares = w.shape[1]
    per_share = (w.shape[0] - 9) // 2
    steps = shares * per_share

    def body(me_ref, g_ref, x2_ref, wi_ref, wo_ref, gb_ref, go_ref, keep_ref, send_ref, sums_ref, a3_ref, a3t_ref, e3_ref, e3t_ref, u_ref, room_ref):
        j = pl.program_id(0)

        @pl.when(j == 0)
        def _():
            hat, _ = norm_parts(x2_ref[...])
            a3 = hat * gb_ref[2:3] + gb_ref[5:6]
            a3_ref[...] = a3.astype(BF16)
            a3t_ref[...] = a3.T.astype(BF16)
            g = g_ref[...]
            e3_ref[...] = g.astype(BF16)
            e3t_ref[...] = g.T.astype(BF16)
            u_ref[...] = jnp.zeros((t, d), F32)

        hid = nn(a3_ref[...], wi_ref[0, 0])
        phi = 0.5 * (1.0 + lax.erf(hid * HALF_ROOT))
        act = (hid * phi).astype(BF16)
        slope = phi + hid * jnp.exp(-0.5 * hid * hid) * INV_ROOT_TAU
        dhid = (nn(e3_ref[...], wo_ref[0, 0]) * slope).astype(BF16)
        split_rows(nn(e3t_ref[...], act), keep_ref, send_ref, (1, 0, 0), room_ref, me_ref)
        split_rows(nn(a3t_ref[...], dhid), keep_ref, send_ref, (0, 0, 0), room_ref, me_ref)
        u_ref[...] += nt(dhid, wi_ref[0, 0])

        @pl.when(j == steps - 1)
        def _():
            change, sums = norm_back(u_ref[...], x2_ref[...], gb_ref[2:3])
            go_ref[...] = g_ref[...] + change
            sums_ref[...] = sums

    slab_outs = halves.array(
        (2, per_share, shares), (2, 1, 1), lambda j: (0, j % per_share, j // per_share)
    )
    grad, keep, send, sums = call(
        body,
        (steps,),
        [
            SCALARS,
            whole(grad.shape),
            whole(x2.shape),
            ff_slab(8, per_share, d, width),
            ff_slab(8 + per_share, per_share, d, width),
            whole(gb.shape),
        ],
        [made((t, d), F32), *slab_outs, made((2, d), F32)],
        [
            pltpu.VMEM((t, d), BF16),
            pltpu.VMEM((d, t), BF16),
            pltpu.VMEM((t, d), BF16),
            pltpu.VMEM((d, t), BF16),
            pltpu.VMEM((t, d), F32),
            halves.room(),
        ],
        (me, grad, x2, w, w, gb),
        flops=10 * t * d * width * steps,
    )
    flat = (2 * per_share,) + keep.shape[2:]
    return grad, (keep.reshape(flat), send.reshape(flat)), sums


def space_backward(rows, grad, x1, qkv, o2, logs, w, gb, me, halves):
    t, d = x1.shape
    width = w.shape[3]
    shares = w.shape[1]
    pairs = width // LANES
    scale = 1.0 / math.sqrt(HEAD_DIM)
    rate = LOG2E * scale
    n = rows.frame_rows

    def body(me_ref, g_ref, x1_ref, qkv_ref, o2_ref, log_ref, wo_ref, wq_ref, gb_ref, go_ref, keep_ref, send_ref, sums_ref, e2_ref, e2t_ref, a2t_ref, do_ref, dqkv_ref, u_ref, room_ref):
        h = pl.program_id(0)

        @pl.when(h == 0)
        def _():
            g = g_ref[...]
            e2_ref[...] = g.astype(BF16)
            e2t_ref[...] = g.T.astype(BF16)
            hat, _ = norm_parts(x1_ref[...])
            a2t_ref[...] = (hat * gb_ref[1:2] + gb_ref[4:5]).T.astype(BF16)
            u_ref[...] = jnp.zeros((t, d), F32)

        bias = rows.space_bias()
        split_rows(nn(e2t_ref[...], o2_ref[...]), keep_ref, send_ref, (0, 0), room_ref, me_ref)
        do_ref[...] = nn(e2_ref[...], wo_ref[0, 0]).astype(BF16)

        @pl.loop(0, pairs)
        def _(i):
            lanes = pl.ds(pl.multiple_of(i * LANES, LANES), LANES)
            for f in range(rows.frames):
                at = slice(f * n, (f + 1) * n)
                log = log_ref[0, i, f]
                grads = pair_backward(
                    qkv_ref[0, at, lanes],
                    qkv_ref[1, at, lanes],
                    qkv_ref[2, at, lanes],
                    do_ref[at, lanes],
                    (log[0:1], log[1:2]),
                    bias,
                    rate,
                    scale,
                )
                for part in range(3):
                    dqkv_ref[part, at, lanes] = grads[part]

        for part in range(3):
            split_rows(
                nn(a2t_ref[...], dqkv_ref[part]), keep_ref, send_ref, (part + 1, 0), room_ref, me_ref
            )
            u_ref[...] += nt(dqkv_ref[part], wq_ref[part, 0])

        @pl.when(h == shares - 1)
        def _():
            change, sums = norm_back(u_ref[...], x1_ref[...], gb_ref[1:2])
            go_ref[...] = g_ref[...] + change
            sums_ref[...] = sums

    grad, keep, send, sums = call(
        body,
        (shares,),
        [
            SCALARS,
            whole(grad.shape),
            whole(x1.shape),
            pl.BlockSpec((3, t, width), lambda h: (0, 0, h)),
            pl.BlockSpec((t, width), lambda h: (0, h)),
            pl.BlockSpec((1,) + logs.shape[1:], lambda h: (h, 0, 0, 0, 0)),
            slabs(1, 7, width, d),
            slabs(3, 3, width, d),
            whole(gb.shape),
        ],
        [
            made((t, d), F32),
            *halves.array((4, shares), (4, 1), lambda h: (0, h)),
            made((2, d), F32),
        ],
        [
            pltpu.VMEM((t, d), BF16),
            pltpu.VMEM((d, t), BF16),
            pltpu.VMEM((d, t), BF16),
            pltpu.VMEM((t, width), BF16),
            pltpu.VMEM((3, t, width), BF16),
            pltpu.VMEM((t, d), F32),
            halves.room(),
        ],
        (me, grad, x1, qkv, o2, logs, w, w, gb),
        flops=2 * t * d * d * 8,
    )
    return grad, (keep, send), sums


def mix_fits(depth, shards, shares):
    return depth // (shards * shares) % 8 == 0


def middle_backward(rows, grad, y1, o1, w, mix, me, halves, shards):
    t, d = grad.shape
    width = w.shape[3]
    shares = w.shape[1]
    fits = mix_fits(d, shards, shares)
    part = d // (shards * shares)

    def body(me_ref, g_ref, y1_ref, o1_ref, to_ref, mix_ref, send_ref, gk_ref, gs_ref, *rest):
        if fits:
            room_ref, order_ref = rest
        else:
            gm_ref, room_ref = rest
        e1 = g_ref[...].astype(BF16)
        dy1 = nt(e1, mix_ref[...]).astype(BF16)
        send = rows.to_time()
        for h in range(shares):
            lanes = slice(h * width, (h + 1) * width)
            do1 = nn(dy1, to_ref[0, h]).astype(BF16)
            send_ref[:, lanes] = nn(send, do1).astype(BF16)
            split_rows(tn(dy1, o1_ref[:, lanes]), gk_ref, gs_ref, (0, h), room_ref, me_ref)
        gm = tn(y1_ref[...], e1)
        if fits:
            gm = gm.reshape(shards, shares, part, d)
            for h in range(shares):
                for half in range(shares):
                    order_ref[:, half] = gm[:, h, :, half * width : (half + 1) * width]
                split_rows(order_ref[...], gk_ref, gs_ref, (1, h), room_ref, me_ref)
        else:
            gm_ref[...] = gm.astype(BF16)

    outs = [made((rows.time_rows, d), BF16)]
    outs += halves.array((1 + fits, shares), (1 + fits, shares), lambda i: (0, 0))
    scratch = [halves.room()]
    if fits:
        scratch.append(pltpu.VMEM((shards, shares, part, width), F32))
    else:
        outs.append(made((d, d), BF16))
    got = call(
        body,
        (1,),
        [
            SCALARS,
            whole(grad.shape),
            whole(y1.shape),
            whole(o1.shape),
            pl.BlockSpec((1, shares, d, width), lambda i: (6, 0, 0, 0)),
            whole(mix.shape),
        ],
        outs,
        scratch,
        (me, grad, y1, o1, w, mix),
        flops=8 * t * d * d,
    )
    do1, keep, send = got[:3]
    if not fits:
        gm = mix_slab(got[3], shards, shares).reshape((1, shares, halves.pairs, 2) + keep.shape[3:])
        keep = jnp.concatenate((keep, lax.dynamic_index_in_dim(gm, me[0], 3, keepdims=False)), axis=0)
        send = jnp.concatenate((send, lax.dynamic_index_in_dim(gm, 1 - me[0], 3, keepdims=False)), axis=0)
    return do1, (keep, send)


def time_backward(rows, do1, a, qkv, logs, w, me, halves):
    t, d = a.shape
    width = w.shape[3]
    shares = w.shape[1]
    pairs = width // LANES
    scale = 1.0 / math.sqrt(HEAD_DIM)
    rate = LOG2E * scale

    def body(me_ref, do_ref, a_ref, qkv_ref, log_ref, w_ref, out_ref, keep_ref, send_ref, bias_ref, dqkv_ref, at_ref, u_ref, room_ref):
        h = pl.program_id(0)

        @pl.when(h == 0)
        def _():
            bias_ref[...] = rows.time_bias()
            at_ref[...] = a_ref[...].T
            u_ref[...] = jnp.zeros((t, d), F32)

        @pl.loop(0, pairs)
        def _(i):
            lanes = pl.ds(pl.multiple_of(i * LANES, LANES), LANES)
            log = log_ref[0, i]
            grads = pair_backward(
                qkv_ref[0, :, lanes],
                qkv_ref[1, :, lanes],
                qkv_ref[2, :, lanes],
                do_ref[:, lanes],
                (log[0:1], log[1:2]),
                bias_ref[...],
                rate,
                scale,
            )
            for part in range(3):
                dqkv_ref[part, :, lanes] = grads[part]

        for part in range(3):
            split_rows(
                nn(at_ref[...], dqkv_ref[part]), keep_ref, send_ref, (part, 0), room_ref, me_ref
            )
            u_ref[...] += nt(dqkv_ref[part], w_ref[part, 0])

        @pl.when(h == shares - 1)
        def _():
            out_ref[...] = u_ref[...].astype(BF16)

    da1, keep, send = call(
        body,
        (shares,),
        [
            SCALARS,
            pl.BlockSpec((t, width), lambda h: (0, h)),
            whole(a.shape),
            pl.BlockSpec((3, t, width), lambda h: (0, 0, h)),
            pl.BlockSpec((1,) + logs.shape[1:], lambda h: (h, 0, 0, 0)),
            slabs(3, 0, width, d),
        ],
        [
            made((t, d), BF16),
            *halves.array((3, shares), (3, 1), lambda h: (0, h)),
        ],
        [
            pltpu.VMEM((t, t), F32),
            pltpu.VMEM((3, t, width), BF16),
            pltpu.VMEM((d, t), BF16),
            pltpu.VMEM((t, d), F32),
            halves.room(),
        ],
        (me, do1, a, qkv, logs, w),
        flops=2 * t * d * d * 6,
    )
    return da1, (keep, send)


def first_norm_back(rows, back, x, grad, gb):
    t, d = x.shape

    def body(back_ref, x_ref, g_ref, gb_ref, go_ref, sums_ref):
        u = tn(rows.to_time(), back_ref[...])
        change, sums = norm_back(u, x_ref[...], gb_ref[0:1])
        go_ref[...] = g_ref[...] + change
        sums_ref[...] = sums

    return call(
        body,
        (1,),
        [whole(back.shape), whole(x.shape), whole(grad.shape), whole(gb.shape)],
        [made((t, d), F32), made((2, d), F32)],
        [],
        (back, x, grad, gb),
    )


def swap_places(rows_array):
    return lax.all_to_all(rows_array, "seq", split_axis=0, concat_axis=0, tiled=True)


def pack_layer(time_qkv, time_out, time_mix, space_qkv, space_out, mlp_in, mlp_out):
    width = time_qkv.shape[2]
    r = time_qkv.shape[0]
    halves = time_mix.shape[1] // width

    def columns(a):
        return a.reshape(r, -1, width).transpose(1, 0, 2)

    mix = time_mix.reshape(-1, halves, width).transpose(1, 0, 2).reshape(1, r, width)
    return jnp.concatenate(
        (
            columns(time_qkv),
            columns(space_qkv),
            time_out.T[None],
            space_out.T[None],
            columns(mlp_in),
            columns(mlp_out.T),
            mix,
        ),
        axis=0,
    )


def gather_slabs(pack):
    full = lax.all_gather(pack, ("head", "clip", "seq"), axis=1, tiled=True)
    return full.reshape(pack.shape[0], lax.axis_size("head"), -1, pack.shape[2])


def mix_whole(slab, shards):
    shares, depth, width = slab.shape
    part = slab.reshape(shares, shards, shares, depth // (shards * shares), width)
    return part.transpose(1, 0, 3, 2, 4).reshape(depth, shares * width)


def mix_slab(whole_grad, shards, shares):
    depth, full = whole_grad.shape
    width = full // shares
    part = whole_grad.reshape(shards, shares, depth // (shards * shares), shares, width)
    return part.transpose(1, 0, 3, 2, 4).reshape(1, shares, depth, width)


class Term:
    def __init__(self, array, names, first, count):
        self.array = array
        self.names = names
        self.first = first
        self.count = count

    def cut(self, first, count):
        return Term(self.array, self.names, self.first + first, count)


class Job:
    def __init__(self, pieces, other, ways):
        self.pieces = pieces
        self.other = other
        self.ways = ways
        names = pieces[0][-1].names
        self.lead = () if other is None else tuple(2 for n in names if n != other)
        self.count = sum(piece[0].count for piece in pieces)
        self.rows, self.width = pieces[0][0].array.shape[-2:]

    def shape(self):
        if self.other is None:
            return (self.ways, self.count, self.rows // self.ways, self.width)
        return (self.count,) + self.lead + (self.rows, self.width)


def fold(jobs, me):
    place = {"x": 1, "h": 2}
    terms = [t for job in jobs for piece in job.pieces for t in piece]
    arrays = []
    for t in terms:
        if not any(t.array is a for a in arrays):
            arrays.append(t.array)
    number = [next(i for i, a in enumerate(arrays) if a is t.array) for t in terms]
    rooms = []
    for job in jobs:
        for piece in job.pieces:
            rooms += [(t.count,) + job.lead + (job.rows, job.width) for t in piece]

    def body(me_ref, *refs):
        sources = refs[: len(arrays)]
        outs = refs[len(arrays) : len(arrays) + len(jobs)]
        held = refs[len(arrays) + len(jobs) : -1]
        sems = refs[-1]
        copies = []
        for job in jobs:
            for piece in job.pieces:
                for t in piece:
                    n = len(copies)
                    at = [pl.ds(t.first, t.count)]
                    for name in t.names:
                        if name == job.other:
                            at.append(1 - me_ref[place[name]])
                        elif job.other is not None and name in job.pieces[0][-1].names:
                            at.append(slice(None))
                        else:
                            at.append(me_ref[place[name]])
                    copies.append(
                        pltpu.make_async_copy(sources[number[n]].at[tuple(at)], held[n], sems.at[n])
                    )
        for copy in copies:
            copy.start()
        n = 0
        for job, out in zip(jobs, outs):
            base = 0
            for piece in job.pieces:
                these = held[n : n + len(piece)]
                for k in range(len(piece)):
                    copies[n + k].wait()
                n += len(piece)

                @pl.loop(0, piece[0].count)
                def _(i, these=these, base=base, out=out, job=job):
                    def total(at):
                        value = these[0][at].astype(F32)
                        for one in these[1:]:
                            value = value + one[at].astype(F32)
                        return value.astype(BF16)

                    if job.other is None:
                        value = total((i,))
                        r = job.rows // job.ways
                        for s in range(job.ways):
                            out[s, base + i] = value[s * r : (s + 1) * r]
                    elif job.lead:
                        for k in range(2):
                            out[base + i, k] = total((i, k))
                    else:
                        out[base + i] = total((i,))

                base += piece[0].count

    moved = sum(2 * math.prod(r) for r in rooms) + sum(2 * math.prod(j.shape()) for j in jobs)
    return pl.pallas_call(
        body,
        out_shape=[jax.ShapeDtypeStruct(job.shape(), BF16) for job in jobs],
        in_specs=[SCALARS] + [pl.BlockSpec(memory_space=pl.ANY)] * len(arrays),
        out_specs=[pl.BlockSpec(memory_space=pltpu.VMEM)] * len(jobs),
        scratch_shapes=[pltpu.VMEM(r, BF16) for r in rooms] + [pltpu.SemaphoreType.DMA((len(rooms),))],
        compiler_params=pltpu.CompilerParams(vmem_limit_bytes=VMEM),
        cost_estimate=pl.CostEstimate(flops=0, bytes_accessed=moved, transcendentals=0),
    )(me, *arrays)


def cross(a, name):
    axis, bit = ("head", 0) if name == "h" else ("clip", 1 if name == "x" else 0)
    size = lax.axis_size(axis)
    return lax.ppermute(a, axis, [(i, i ^ (1 << bit)) for i in range(size)])


class Group:
    def __init__(self, halves_of):
        self.pieces = []
        for keep, send in halves_of:
            got = cross(send, "c")
            n = keep.shape[0]
            self.pieces.append([Term(a, ("h", "x"), 0, n) for a in (keep, got)])
        total = sum(p[0].count for p in self.pieces)
        self.parts = ([], [])
        seen = 0
        for piece in self.pieces:
            n = piece[0].count
            first = min(max((total + 1) // 2 - seen, 0), n)
            if first:
                self.parts[0].append([t.cut(0, first) for t in piece])
            if n > first:
                self.parts[1].append([t.cut(first, n - first) for t in piece])
            seen += n
        self.step = 0
        self.result = None

    def jobs(self, ways):
        if self.step == 2:
            return [Job(self.parts[0] + self.parts[1], None, ways)]
        orders = (("x", "h"), ("h", "x"))
        return [Job(part, order[self.step], ways) for part, order in zip(self.parts, orders)]

    def go(self, sums):
        if self.step == 2:
            got = lax.all_to_all(sums[0], "seq", split_axis=0, concat_axis=0, tiled=True)
            self.result = jnp.sum(got.astype(F32), axis=0)
        else:
            orders = (("x", "h"), ("h", "x"))
            left = (orders[0][1 - self.step], orders[1][1 - self.step])
            for part, order, name, one in zip(self.parts, orders, left, sums):
                got = cross(one, order[self.step])
                base = 0
                for piece in part:
                    names = () if self.step else (name,)
                    piece.append(Term(got, names, base, piece[0].count))
                    base += piece[0].count
        self.step += 1


def move(x, groups, me):
    ways = lax.axis_size("seq")
    jobs = [g.jobs(ways) for g in groups]
    sums = fold([j for some in jobs for j in some], me)
    x, sums = lax.optimization_barrier((x, sums))
    for g, some in zip(groups, jobs):
        g.go(sums[: len(some)])
        sums = sums[len(some) :]
    return x


def settle(x, groups):
    terms = {}
    for g in groups:
        for part in g.parts:
            for piece in part:
                terms.setdefault(id(piece[-1].array), []).append(piece[-1])
    x, arrays = lax.optimization_barrier((x, [same[0].array for same in terms.values()]))
    for same, array in zip(terms.values(), arrays):
        for term in same:
            term.array = array
    return x


def reduce_plain(halves_of, core):
    def joined(keep, send):
        low = jnp.where(core == 0, keep, send)
        high = jnp.where(core == 0, send, keep)
        n, shares, pairs, depth, width = keep.shape
        return jnp.stack((low, high), axis=3).reshape(n, shares, 2 * pairs * depth, width)

    g = jnp.concatenate([joined(*pair) for pair in halves_of], axis=0)
    g = lax.psum_scatter(g, "head", scatter_dimension=1, tiled=True)
    g = lax.psum_scatter(g.astype(F32), ("clip", "seq"), scatter_dimension=2, tiled=True)
    return g[:, 0]


def gather_norms(gain, bias):
    layers, norms, part = gain.shape
    both = jnp.concatenate((gain, bias), axis=1).reshape(1, -1)
    count = lax.axis_size("clip") * lax.axis_size("seq") * lax.axis_size("head")
    width = round_up(both.shape[1], 128)
    padded = jnp.pad(both, ((0, 0), (0, width - both.shape[1])))
    every = lax.all_to_all(
        jnp.broadcast_to(padded, (count, width)), ALL, split_axis=0, concat_axis=0, tiled=True
    )[:, : both.shape[1]]
    return every.reshape(count, layers * 2 * norms, part).transpose(1, 0, 2).reshape(layers, 2 * norms, -1)


def reduce_norms(sums):
    count = lax.axis_size("clip") * lax.axis_size("seq") * lax.axis_size("head")
    rows, features = sums.shape
    part = features // count
    a = sums.reshape(rows, count, part).transpose(1, 0, 2).reshape(count, rows * part)
    width = round_up(rows * part, 128)
    a = jnp.pad(a, ((0, 0), (0, width - rows * part)))
    every = lax.all_to_all(a, ALL, split_axis=0, concat_axis=0, tiled=True)
    return jnp.sum(every, axis=0)[: rows * part].reshape(rows, part)


def on_device(
    tokens,
    cotangent,
    time_qkv,
    time_out,
    time_mix,
    space_qkv,
    space_out,
    mlp_in,
    mlp_out,
    norm_gain,
    norm_bias,
):
    layers = time_qkv.shape[0]
    clips, frames, places, d = tokens.shape
    ways = lax.axis_size("seq")
    shards = lax.axis_size("clip") * ways
    rows = Rows(clips * frames, places, ways)
    shares = lax.axis_size("head")

    def as_rows(a):
        a = a.astype(F32).reshape(rows.frames, places, d)
        a = jnp.pad(a, ((0, 0), (0, rows.frame_rows - places), (0, 0)))
        return a.reshape(rows.rows, d)

    def from_rows(a):
        a = a.reshape(rows.frames, rows.frame_rows, d)[:, :places]
        return a.reshape(tokens.shape)

    gbs = gather_norms(norm_gain, norm_bias)
    gb = [gbs[l] for l in range(layers)]
    weights = [
        gather_slabs(
            pack_layer(
                time_qkv[l], time_out[l], time_mix[l], space_qkv[l], space_out[l], mlp_in[l], mlp_out[l]
            )
        )
        for l in range(layers)
    ]
    mixes = [mix_whole(w[-1], shards) for w in weights]

    x = as_rows(tokens)
    send = send_first(rows, x, gb[0])
    kept = []
    for l in range(layers):
        w = weights[l]
        a1 = swap_places(send)
        qkv1, o1_time, log1 = time_forward(rows, a1, w, shares)
        back = swap_places(o1_time)
        o1, y1, x1, qkv2 = middle_forward(rows, back, x, w, mixes[l], gb[l])
        o2, x2, log2 = space_forward(rows, qkv2, x1, w)
        kept.append((x, a1, qkv1, log1, o1, y1, x1, qkv2, o2, log2, x2))
        if l + 1 < layers:
            x, send = mlp_forward(rows, x2, w, gb[l], gb[l + 1])
        else:
            (x,) = mlp_forward(rows, x2, w, gb[l], None)
    output = from_rows(x).astype(BF16)

    grad = as_rows(cotangent)
    halves = Halves(lax.axis_size("clip"), d, time_qkv.shape[3])
    clip = lax.axis_index("clip")
    me = jnp.stack((clip & 1, (clip >> 1) & 1, lax.axis_index("head"))).astype(jnp.int32)
    norm_rows = [None] * layers
    summed = [None] * layers
    late = []
    quick = lax.axis_size("clip") == 4 and shares == 2 and time_qkv.shape[1] % 16 == 0
    for l in reversed(range(layers)):
        w = weights[l]
        x, a1, qkv1, log1, o1, y1, x1, qkv2, o2, log2, x2 = kept[l]
        grad, g_ff, s3 = mlp_backward(rows, grad, x2, w, gb[l], me, halves)
        if quick:
            ff = Group([g_ff])
            if late:
                grad = move(grad, late, me)
        grad, g_space, s2 = space_backward(rows, grad, x1, qkv2, o2, log2, w, gb[l], me, halves)
        if quick:
            space = Group([g_space])
            grad = move(grad, [ff], me)
        do1, g_out = middle_backward(rows, grad, y1, o1, w, mixes[l], me, halves, shards)
        do1 = swap_places(do1)
        if quick:
            do1 = move(do1, [ff, space] + late[1:], me)
        da1, g_time = time_backward(rows, do1, a1, qkv1, log1, w, me, halves)
        if quick:
            da1 = settle(da1, [ff, space])
        da1 = swap_places(da1)
        if quick:
            rest = Group([g_out, g_time])
            da1 = move(da1, [ff, space, rest], me)
            late = [space, rest]
        grad, s1 = first_norm_back(rows, da1, x, grad, gb[l])
        norm_rows[l] = jnp.concatenate((s1[0:1], s2[0:1], s3[0:1], s1[1:2], s2[1:2], s3[1:2]), axis=0)
        if quick:
            summed[l] = [ff, space, rest]
        else:
            summed[l] = [reduce_plain([g_ff, g_space, g_out, g_time], clip & 1)]
    if quick:
        move((), [space, rest], me)
        move((), [rest], me)
        summed = [[g.result for g in some] for some in summed]
    cuts = (g_ff[0].shape[0], g_space[0].shape[0], g_out[0].shape[0], g_time[0].shape[0])
    results = []
    for some in summed:
        slabs_of = jnp.concatenate(some, axis=0)
        ends = [sum(cuts[: i + 1]) for i in range(4)]
        results.append([slabs_of[e - c : e] for c, e in zip(cuts, ends)])
    tokens_grad = from_rows(grad)
    norm_sums = reduce_norms(jnp.concatenate(norm_rows, axis=0)).reshape(layers, 2, 3, -1)

    def stacked(form):
        return jnp.stack([form(*results[l]) for l in range(layers)])

    def rows_of(a):
        return a.transpose(1, 0, 2)

    def flat(a):
        return rows_of(a).reshape(a.shape[1], -1)

    def mix_rows(a):
        r, width = a.shape
        return a.reshape(shares, r // shares, width).transpose(1, 0, 2).reshape(r // shares, -1)

    per_share = mlp_in.shape[2] // time_qkv.shape[3]
    return (
        output,
        tokens_grad,
        stacked(lambda ff, s, t, q: rows_of(q)),
        stacked(lambda ff, s, t, q: t[0].T),
        stacked(lambda ff, s, t, q: mix_rows(t[1])),
        stacked(lambda ff, s, t, q: rows_of(s[1:])),
        stacked(lambda ff, s, t, q: s[0].T),
        stacked(lambda ff, s, t, q: flat(ff[:per_share])),
        stacked(lambda ff, s, t, q: flat(ff[per_share:]).T),
        norm_sums[:, 0],
        norm_sums[:, 1],
    )


def solution(mesh):
    token_spec = P(("clip", "head"), "seq", None, None)
    in_specs = (
        token_spec,
        token_spec,
        P(None, ("clip", "seq"), None, "head"),
        P(None, "head", ("clip", "seq")),
        P(None, ("clip", "seq", "head"), None),
        P(None, ("clip", "seq"), None, "head"),
        P(None, "head", ("clip", "seq")),
        P(None, ("clip", "seq"), "head"),
        P(None, "head", ("clip", "seq")),
        P(None, None, ("clip", "seq", "head")),
        P(None, None, ("clip", "seq", "head")),
    )
    return jax.shard_map(
        on_device, mesh=mesh, in_specs=in_specs, out_specs=in_specs, check_vma=False
    )
```

```python
import functools
import math

import jax
import jax.numpy as jnp
from jax import lax
from jax.experimental import pallas as pl
from jax.experimental.pallas import tpu as pltpu
from jax.sharding import PartitionSpec as P

HEAD_DIM = 64
NORM_EPS = 1e-06
HALF_ROOT = 0.7071067811865476
INV_ROOT_TAU = 0.3989422804014327
LOG2E = 1.4426950408889634
FAR = -1e30
LANES = 128
VMEM = 56 * 1024 * 1024
SHOWN = 1.0
ALL = ("clip", "seq", "head")
BF16 = jnp.bfloat16
F32 = jnp.float32


def round_up(value, step):
    return -(-value // step) * step


def nn(a, b):
    return lax.dot_general(a, b, (((1,), (0,)), ((), ())), preferred_element_type=F32)


def nt(a, b):
    return lax.dot_general(a, b, (((1,), (1,)), ((), ())), preferred_element_type=F32)


def tn(a, b):
    return lax.dot_general(a, b, (((0,), (0,)), ((), ())), preferred_element_type=F32)


def norm_parts(x):
    mean = jnp.mean(x, axis=-1, keepdims=True)
    centred = x - mean
    spread = lax.rsqrt(jnp.mean(centred * centred, axis=-1, keepdims=True) + NORM_EPS)
    return centred * spread, spread


def norm_rounded(x, gain, bias):
    hat, _ = norm_parts(x)
    return (hat * gain + bias).astype(BF16)


def norm_back(u, x, gain):
    hat, spread = norm_parts(x)
    scaled = u * gain
    mean_scaled = jnp.mean(scaled, axis=-1, keepdims=True)
    mean_cross = jnp.mean(scaled * hat, axis=-1, keepdims=True)
    change = spread * (scaled - mean_scaled - hat * mean_cross)
    sums = jnp.concatenate(
        (jnp.sum(u * hat, axis=0, keepdims=True), jnp.sum(u, axis=0, keepdims=True)), axis=0
    )
    return change, sums


class Rows:
    def __init__(self, frames, places, ways):
        self.frames = frames
        self.places = places
        self.ways = ways
        self.frame_rows = round_up(places, 16)
        self.rows = frames * self.frame_rows
        self.block = places // ways
        self.chunk = round_up(frames * self.block, 8)
        self.time_rows = ways * self.chunk

    def split(self, r):
        way = jnp.zeros_like(r)
        for k in range(1, self.ways):
            way = way + (r >= k * self.chunk).astype(jnp.int32)
        rest = r - way * self.chunk
        frame = jnp.zeros_like(r)
        for k in range(1, self.frames):
            frame = frame + (rest >= k * self.block).astype(jnp.int32)
        real = rest < self.frames * self.block
        return way, frame, rest - frame * self.block, real

    def to_time(self):
        r = lax.broadcasted_iota(jnp.int32, (self.time_rows, 1), 0)
        way, frame, place, real = self.split(r)
        source = jnp.where(real, frame * self.frame_rows + way * self.block + place, -1)
        c = lax.broadcasted_iota(jnp.int32, (self.time_rows, self.rows), 1)
        return jnp.where(c == source, 1.0, 0.0).astype(BF16)

    def time_bias(self):
        def label(r):
            _, _, place, real = self.split(r)
            return jnp.where(real, place, -1)

        a = label(lax.broadcasted_iota(jnp.int32, (self.time_rows, 1), 0))
        b = label(lax.broadcasted_iota(jnp.int32, (1, self.time_rows), 1))
        return jnp.where(a == b, 0.0, FAR).astype(F32)

    def space_bias(self):
        a = lax.broadcasted_iota(jnp.int32, (self.frame_rows, 1), 0)
        return jnp.where(a < self.places, 0.0, FAR).astype(F32)


def lane_masks(rows):
    lane = lax.broadcasted_iota(jnp.int32, (rows, LANES), 1)
    return lane < HEAD_DIM


def one_of(value, low, half):
    zero = jnp.zeros_like(value)
    return jnp.where(low, value, zero) if half == 0 else jnp.where(low, zero, value)


def pair_forward(q, k, v, bias, rate):
    low = lane_masks(q.shape[0])
    mixed, logs = [], []
    for half in range(2):
        s = nt(k, one_of(q, low, half)) + bias
        peak = jnp.max(s, axis=0, keepdims=True)
        e = jnp.exp2((s - peak) * rate)
        total = jnp.sum(e, axis=0, keepdims=True)
        soft = (e * (1.0 / total)).astype(BF16)
        mixed.append(tn(soft, v))
        logs.append(peak * rate + jnp.log2(total))
    return jnp.where(low, mixed[0], mixed[1]).astype(BF16), logs


def pair_backward(q, k, v, do, logs, bias, rate, scale):
    low = lane_masks(q.shape[0])
    dq, dk, dv = [], [], []
    for half in range(2):
        s = nt(k, one_of(q, low, half)) + bias
        soft = jnp.exp2(s * rate - logs[half])
        dp = nt(v, one_of(do, low, half))
        ds = (soft * (dp - jnp.sum(soft * dp, axis=0, keepdims=True))).astype(BF16)
        dv.append(nn(soft.astype(BF16), do))
        dk.append(nn(ds, q))
        dq.append(tn(ds, k))
    return (
        (jnp.where(low, dq[0], dq[1]) * scale).astype(BF16),
        (jnp.where(low, dk[0], dk[1]) * scale).astype(BF16),
        jnp.where(low, dv[0], dv[1]).astype(BF16),
    )


def split_rows(value, keep_ref, send_ref, at, room_ref, me_ref):
    mine = me_ref[0]
    room_ref[...] = value.reshape(room_ref.shape)
    keep_ref[at] = room_ref[:, mine].astype(BF16)
    send_ref[at] = room_ref[:, 1 - mine].astype(BF16)


class Halves:
    def __init__(self, clips, depth, width):
        self.pairs = clips // 2
        self.rows = depth // clips
        self.width = width

    def array(self, lead, block, index):
        tail = (self.pairs, self.rows, self.width)
        one = lambda: made(lead + tail, BF16, block + tail, lambda *g: index(*g) + (0, 0, 0))
        return [one(), one()]

    def room(self):
        return pltpu.VMEM((self.pairs, 2, self.rows, self.width), F32)


SCALARS = pl.BlockSpec(memory_space=pltpu.SMEM)


def call(body, grid, ins, outs, scratch, args, flops=0):
    specs = [spec for spec in ins]
    moved = sum(math.prod(o.shape) * o.dtype.itemsize for o, _ in outs)
    moved += sum(math.prod(a.shape) * a.dtype.itemsize for a in args)
    return pl.pallas_call(
        body,
        out_shape=[shape for shape, _ in outs],
        grid=grid,
        in_specs=specs,
        out_specs=[spec for _, spec in outs],
        scratch_shapes=scratch,
        compiler_params=pltpu.CompilerParams(vmem_limit_bytes=VMEM),
        cost_estimate=pl.CostEstimate(
            flops=int(flops * SHOWN), bytes_accessed=int(moved * SHOWN), transcendentals=0
        ),
    )(*args)


def whole(shape):
    zeros = (0,) * len(shape)
    return pl.BlockSpec(shape, lambda *_: zeros)


def made(shape, dtype, block=None, index=None):
    spec = whole(shape) if block is None else pl.BlockSpec(block, index)
    return jax.ShapeDtypeStruct(shape, dtype), spec


def slabs(count, first, width, depth):
    return pl.BlockSpec((count, 1, depth, width), lambda h, *_: (first // count, h, 0, 0))


def send_first(rows, x, gb):
    def body(x_ref, gb_ref, out_ref):
        a = norm_rounded(x_ref[...], gb_ref[0:1], gb_ref[3:4])
        out_ref[...] = nn(rows.to_time(), a).astype(BF16)

    d = x.shape[1]
    return call(
        body, (1,), [whole(x.shape), whole(gb.shape)], [made((rows.time_rows, d), BF16)], [], (x, gb)
    )[0]


def time_forward(rows, a, w, head_shares):
    t, d = a.shape
    width = w.shape[3]
    pairs = width // LANES
    rate = LOG2E / math.sqrt(HEAD_DIM)

    def body(a_ref, w_ref, qkv_ref, out_ref, log_ref, bias_ref):
        @pl.when(pl.program_id(0) == 0)
        def _():
            bias_ref[...] = rows.time_bias()

        act = a_ref[...]
        for g in range(3):
            qkv_ref[g] = nn(act, w_ref[g, 0]).astype(BF16)

        @pl.loop(0, pairs)
        def _(i):
            lanes = pl.ds(pl.multiple_of(i * LANES, LANES), LANES)
            mixed, logs = pair_forward(
                qkv_ref[0, :, lanes], qkv_ref[1, :, lanes], qkv_ref[2, :, lanes], bias_ref[...], rate
            )
            out_ref[:, lanes] = mixed
            log_ref[0, i] = jnp.concatenate(logs, axis=0)

    return call(
        body,
        (head_shares,),
        [whole(a.shape), slabs(3, 0, width, d)],
        [
            made((3, t, d), BF16, (3, t, width), lambda h: (0, 0, h)),
            made((t, d), BF16, (t, width), lambda h: (0, h)),
            made((head_shares, pairs, 2, t), F32, (1, pairs, 2, t), lambda h: (h, 0, 0, 0)),
        ],
        [pltpu.VMEM((t, t), F32)],
        (a, w),
        flops=2 * t * d * 3 * d,
    )


def middle_forward(rows, back, x, w, mix, gb):
    t, d = x.shape
    width = w.shape[3]
    shares = w.shape[1]

    def body(back_ref, x_ref, to_ref, sq_ref, mix_ref, gb_ref, o1_ref, y1_ref, x1_ref, qkv_ref):
        o1 = tn(rows.to_time(), back_ref[...]).astype(BF16)
        o1_ref[...] = o1
        y1 = jnp.zeros((t, d), F32)
        for h in range(shares):
            y1 = y1 + nt(o1[:, h * width : (h + 1) * width], to_ref[0, h])
        y1 = y1.astype(BF16)
        y1_ref[...] = y1
        x1 = x_ref[...] + nn(y1, mix_ref[...])
        x1_ref[...] = x1
        a2 = norm_rounded(x1, gb_ref[1:2], gb_ref[4:5])
        for g in range(3):
            for h in range(shares):
                qkv_ref[g, :, h * width : (h + 1) * width] = nn(a2, sq_ref[g, h]).astype(BF16)

    return call(
        body,
        (1,),
        [
            whole(back.shape),
            whole(x.shape),
            pl.BlockSpec((1, shares, d, width), lambda i: (6, 0, 0, 0)),
            pl.BlockSpec((3, shares, d, width), lambda i: (1, 0, 0, 0)),
            whole(mix.shape),
            whole(gb.shape),
        ],
        [made((t, d), BF16), made((t, d), BF16), made((t, d), F32), made((3, t, d), BF16)],
        [],
        (back, x, w, w, mix, gb),
        flops=2 * t * d * 5 * d,
    )


def space_forward(rows, qkv, x1, w):
    t, d = x1.shape
    width = w.shape[3]
    shares = w.shape[1]
    pairs = width // LANES
    rate = LOG2E / math.sqrt(HEAD_DIM)
    n = rows.frame_rows

    def body(qkv_ref, x1_ref, w_ref, o2_ref, x2_ref, log_ref):
        bias = rows.space_bias()

        @pl.loop(0, pairs)
        def _(i):
            lanes = pl.ds(pl.multiple_of(i * LANES, LANES), LANES)
            for f in range(rows.frames):
                at = slice(f * n, (f + 1) * n)
                mixed, logs = pair_forward(
                    qkv_ref[0, at, lanes], qkv_ref[1, at, lanes], qkv_ref[2, at, lanes], bias, rate
                )
                o2_ref[at, lanes] = mixed
                log_ref[0, i, f] = jnp.concatenate(logs, axis=0)

        @pl.when(pl.program_id(0) == 0)
        def _():
            x2_ref[...] = x1_ref[...]

        x2_ref[...] += nt(o2_ref[...], w_ref[0, 0])

    return call(
        body,
        (shares,),
        [
            pl.BlockSpec((3, t, width), lambda h: (0, 0, h)),
            whole(x1.shape),
            slabs(1, 7, width, d),
        ],
        [
            made((t, d), BF16, (t, width), lambda h: (0, h)),
            made((t, d), F32),
            made(
                (shares, pairs, rows.frames, 2, n),
                F32,
                (1, pairs, rows.frames, 2, n),
                lambda h: (h, 0, 0, 0, 0),
            ),
        ],
        [],
        (qkv, x1, w),
        flops=2 * t * d * d,
    )


def ff_slab(first, per_share, depth, width):
    return pl.BlockSpec(
        (1, 1, depth, width), lambda j: (first + j % per_share, j // per_share, 0, 0)
    )


def mlp_forward(rows, x2, w, gb, gb_next):
    t, d = x2.shape
    width = w.shape[3]
    shares = w.shape[1]
    per_share = (w.shape[0] - 9) // 2
    steps = shares * per_share
    last = gb_next is None

    def body(x2_ref, wi_ref, wo_ref, gb_ref, *rest):
        if last:
            x3_ref, a3_ref = rest
        else:
            gn_ref, x3_ref, send_ref, a3_ref = rest
        j = pl.program_id(0)

        @pl.when(j == 0)
        def _():
            a3_ref[...] = norm_rounded(x2_ref[...], gb_ref[2:3], gb_ref[5:6])
            x3_ref[...] = x2_ref[...]

        hid = nn(a3_ref[...], wi_ref[0, 0])
        act = (0.5 * hid * (1.0 + lax.erf(hid * HALF_ROOT))).astype(BF16)
        x3_ref[...] += nt(act, wo_ref[0, 0])

        if not last:

            @pl.when(j == steps - 1)
            def _():
                a = norm_rounded(x3_ref[...], gn_ref[0:1], gn_ref[3:4])
                send_ref[...] = nn(rows.to_time(), a).astype(BF16)

    ins = [
        whole(x2.shape),
        ff_slab(8, per_share, d, width),
        ff_slab(8 + per_share, per_share, d, width),
        whole(gb.shape),
    ]
    outs = [made((t, d), F32)]
    args = [x2, w, w, gb]
    if not last:
        ins.append(whole(gb_next.shape))
        outs.append(made((rows.time_rows, d), BF16))
        args.append(gb_next)
    return call(
        body, (steps,), ins, outs, [pltpu.VMEM((t, d), BF16)], tuple(args), flops=4 * t * d * width * steps
    )


def mlp_backward(rows, grad, x2, w, gb, me, halves):
    t, d = x2.shape
    width = w.shape[3]
    shares = w.shape[1]
    per_share = (w.shape[0] - 9) // 2
    steps = shares * per_share

    def body(me_ref, g_ref, x2_ref, wi_ref, wo_ref, gb_ref, go_ref, keep_ref, send_ref, sums_ref, a3_ref, a3t_ref, e3_ref, e3t_ref, u_ref, room_ref):
        j = pl.program_id(0)

        @pl.when(j == 0)
        def _():
            hat, _ = norm_parts(x2_ref[...])
            a3 = hat * gb_ref[2:3] + gb_ref[5:6]
            a3_ref[...] = a3.astype(BF16)
            a3t_ref[...] = a3.T.astype(BF16)
            g = g_ref[...]
            e3_ref[...] = g.astype(BF16)
            e3t_ref[...] = g.T.astype(BF16)
            u_ref[...] = jnp.zeros((t, d), F32)

        hid = nn(a3_ref[...], wi_ref[0, 0])
        phi = 0.5 * (1.0 + lax.erf(hid * HALF_ROOT))
        act = (hid * phi).astype(BF16)
        slope = phi + hid * jnp.exp(-0.5 * hid * hid) * INV_ROOT_TAU
        dhid = (nn(e3_ref[...], wo_ref[0, 0]) * slope).astype(BF16)
        split_rows(nn(e3t_ref[...], act), keep_ref, send_ref, (1, 0, 0), room_ref, me_ref)
        split_rows(nn(a3t_ref[...], dhid), keep_ref, send_ref, (0, 0, 0), room_ref, me_ref)
        u_ref[...] += nt(dhid, wi_ref[0, 0])

        @pl.when(j == steps - 1)
        def _():
            change, sums = norm_back(u_ref[...], x2_ref[...], gb_ref[2:3])
            go_ref[...] = g_ref[...] + change
            sums_ref[...] = sums

    slab_outs = halves.array(
        (2, per_share, shares), (2, 1, 1), lambda j: (0, j % per_share, j // per_share)
    )
    grad, keep, send, sums = call(
        body,
        (steps,),
        [
            SCALARS,
            whole(grad.shape),
            whole(x2.shape),
            ff_slab(8, per_share, d, width),
            ff_slab(8 + per_share, per_share, d, width),
            whole(gb.shape),
        ],
        [made((t, d), F32), *slab_outs, made((2, d), F32)],
        [
            pltpu.VMEM((t, d), BF16),
            pltpu.VMEM((d, t), BF16),
            pltpu.VMEM((t, d), BF16),
            pltpu.VMEM((d, t), BF16),
            pltpu.VMEM((t, d), F32),
            halves.room(),
        ],
        (me, grad, x2, w, w, gb),
        flops=10 * t * d * width * steps,
    )
    flat = (2 * per_share,) + keep.shape[2:]
    return grad, (keep.reshape(flat), send.reshape(flat)), sums


def space_backward(rows, grad, x1, qkv, o2, logs, w, gb, me, halves):
    t, d = x1.shape
    width = w.shape[3]
    shares = w.shape[1]
    pairs = width // LANES
    scale = 1.0 / math.sqrt(HEAD_DIM)
    rate = LOG2E * scale
    n = rows.frame_rows

    def body(me_ref, g_ref, x1_ref, qkv_ref, o2_ref, log_ref, wo_ref, wq_ref, gb_ref, go_ref, keep_ref, send_ref, sums_ref, e2_ref, e2t_ref, a2t_ref, do_ref, dqkv_ref, u_ref, room_ref):
        h = pl.program_id(0)

        @pl.when(h == 0)
        def _():
            g = g_ref[...]
            e2_ref[...] = g.astype(BF16)
            e2t_ref[...] = g.T.astype(BF16)
            hat, _ = norm_parts(x1_ref[...])
            a2t_ref[...] = (hat * gb_ref[1:2] + gb_ref[4:5]).T.astype(BF16)
            u_ref[...] = jnp.zeros((t, d), F32)

        bias = rows.space_bias()
        split_rows(nn(e2t_ref[...], o2_ref[...]), keep_ref, send_ref, (0, 0), room_ref, me_ref)
        do_ref[...] = nn(e2_ref[...], wo_ref[0, 0]).astype(BF16)

        @pl.loop(0, pairs)
        def _(i):
            lanes = pl.ds(pl.multiple_of(i * LANES, LANES), LANES)
            for f in range(rows.frames):
                at = slice(f * n, (f + 1) * n)
                log = log_ref[0, i, f]
                grads = pair_backward(
                    qkv_ref[0, at, lanes],
                    qkv_ref[1, at, lanes],
                    qkv_ref[2, at, lanes],
                    do_ref[at, lanes],
                    (log[0:1], log[1:2]),
                    bias,
                    rate,
                    scale,
                )
                for part in range(3):
                    dqkv_ref[part, at, lanes] = grads[part]

        for part in range(3):
            split_rows(
                nn(a2t_ref[...], dqkv_ref[part]), keep_ref, send_ref, (part + 1, 0), room_ref, me_ref
            )
            u_ref[...] += nt(dqkv_ref[part], wq_ref[part, 0])

        @pl.when(h == shares - 1)
        def _():
            change, sums = norm_back(u_ref[...], x1_ref[...], gb_ref[1:2])
            go_ref[...] = g_ref[...] + change
            sums_ref[...] = sums

    grad, keep, send, sums = call(
        body,
        (shares,),
        [
            SCALARS,
            whole(grad.shape),
            whole(x1.shape),
            pl.BlockSpec((3, t, width), lambda h: (0, 0, h)),
            pl.BlockSpec((t, width), lambda h: (0, h)),
            pl.BlockSpec((1,) + logs.shape[1:], lambda h: (h, 0, 0, 0, 0)),
            slabs(1, 7, width, d),
            slabs(3, 3, width, d),
            whole(gb.shape),
        ],
        [
            made((t, d), F32),
            *halves.array((4, shares), (4, 1), lambda h: (0, h)),
            made((2, d), F32),
        ],
        [
            pltpu.VMEM((t, d), BF16),
            pltpu.VMEM((d, t), BF16),
            pltpu.VMEM((d, t), BF16),
            pltpu.VMEM((t, width), BF16),
            pltpu.VMEM((3, t, width), BF16),
            pltpu.VMEM((t, d), F32),
            halves.room(),
        ],
        (me, grad, x1, qkv, o2, logs, w, w, gb),
        flops=2 * t * d * d * 8,
    )
    return grad, (keep, send), sums


def mix_fits(depth, shards, shares):
    return depth // (shards * shares) % 8 == 0


def middle_backward(rows, grad, y1, o1, w, mix, me, halves, shards):
    t, d = grad.shape
    width = w.shape[3]
    shares = w.shape[1]
    fits = mix_fits(d, shards, shares)
    part = d // (shards * shares)

    def body(me_ref, g_ref, y1_ref, o1_ref, to_ref, mix_ref, send_ref, gk_ref, gs_ref, *rest):
        if fits:
            room_ref, order_ref = rest
        else:
            gm_ref, room_ref = rest
        e1 = g_ref[...].astype(BF16)
        dy1 = nt(e1, mix_ref[...]).astype(BF16)
        send = rows.to_time()
        for h in range(shares):
            lanes = slice(h * width, (h + 1) * width)
            do1 = nn(dy1, to_ref[0, h]).astype(BF16)
            send_ref[:, lanes] = nn(send, do1).astype(BF16)
            split_rows(tn(dy1, o1_ref[:, lanes]), gk_ref, gs_ref, (0, h), room_ref, me_ref)
        gm = tn(y1_ref[...], e1)
        if fits:
            gm = gm.reshape(shards, shares, part, d)
            for h in range(shares):
                for half in range(shares):
                    order_ref[:, half] = gm[:, h, :, half * width : (half + 1) * width]
                split_rows(order_ref[...], gk_ref, gs_ref, (1, h), room_ref, me_ref)
        else:
            gm_ref[...] = gm.astype(BF16)

    outs = [made((rows.time_rows, d), BF16)]
    outs += halves.array((1 + fits, shares), (1 + fits, shares), lambda i: (0, 0))
    scratch = [halves.room()]
    if fits:
        scratch.append(pltpu.VMEM((shards, shares, part, width), F32))
    else:
        outs.append(made((d, d), BF16))
    got = call(
        body,
        (1,),
        [
            SCALARS,
            whole(grad.shape),
            whole(y1.shape),
            whole(o1.shape),
            pl.BlockSpec((1, shares, d, width), lambda i: (6, 0, 0, 0)),
            whole(mix.shape),
        ],
        outs,
        scratch,
        (me, grad, y1, o1, w, mix),
        flops=8 * t * d * d,
    )
    do1, keep, send = got[:3]
    if not fits:
        gm = mix_slab(got[3], shards, shares).reshape((1, shares, halves.pairs, 2) + keep.shape[3:])
        keep = jnp.concatenate((keep, lax.dynamic_index_in_dim(gm, me[0], 3, keepdims=False)), axis=0)
        send = jnp.concatenate((send, lax.dynamic_index_in_dim(gm, 1 - me[0], 3, keepdims=False)), axis=0)
    return do1, (keep, send)


def time_backward(rows, do1, a, qkv, logs, w, me, halves):
    t, d = a.shape
    width = w.shape[3]
    shares = w.shape[1]
    pairs = width // LANES
    scale = 1.0 / math.sqrt(HEAD_DIM)
    rate = LOG2E * scale

    def body(me_ref, do_ref, a_ref, qkv_ref, log_ref, w_ref, out_ref, keep_ref, send_ref, bias_ref, dqkv_ref, at_ref, u_ref, room_ref):
        h = pl.program_id(0)

        @pl.when(h == 0)
        def _():
            bias_ref[...] = rows.time_bias()
            at_ref[...] = a_ref[...].T
            u_ref[...] = jnp.zeros((t, d), F32)

        @pl.loop(0, pairs)
        def _(i):
            lanes = pl.ds(pl.multiple_of(i * LANES, LANES), LANES)
            log = log_ref[0, i]
            grads = pair_backward(
                qkv_ref[0, :, lanes],
                qkv_ref[1, :, lanes],
                qkv_ref[2, :, lanes],
                do_ref[:, lanes],
                (log[0:1], log[1:2]),
                bias_ref[...],
                rate,
                scale,
            )
            for part in range(3):
                dqkv_ref[part, :, lanes] = grads[part]

        for part in range(3):
            split_rows(
                nn(at_ref[...], dqkv_ref[part]), keep_ref, send_ref, (part, 0), room_ref, me_ref
            )
            u_ref[...] += nt(dqkv_ref[part], w_ref[part, 0])

        @pl.when(h == shares - 1)
        def _():
            out_ref[...] = u_ref[...].astype(BF16)

    da1, keep, send = call(
        body,
        (shares,),
        [
            SCALARS,
            pl.BlockSpec((t, width), lambda h: (0, h)),
            whole(a.shape),
            pl.BlockSpec((3, t, width), lambda h: (0, 0, h)),
            pl.BlockSpec((1,) + logs.shape[1:], lambda h: (h, 0, 0, 0)),
            slabs(3, 0, width, d),
        ],
        [
            made((t, d), BF16),
            *halves.array((3, shares), (3, 1), lambda h: (0, h)),
        ],
        [
            pltpu.VMEM((t, t), F32),
            pltpu.VMEM((3, t, width), BF16),
            pltpu.VMEM((d, t), BF16),
            pltpu.VMEM((t, d), F32),
            halves.room(),
        ],
        (me, do1, a, qkv, logs, w),
        flops=2 * t * d * d * 6,
    )
    return da1, (keep, send)


def first_norm_back(rows, back, x, grad, gb):
    t, d = x.shape

    def body(back_ref, x_ref, g_ref, gb_ref, go_ref, sums_ref):
        u = tn(rows.to_time(), back_ref[...])
        change, sums = norm_back(u, x_ref[...], gb_ref[0:1])
        go_ref[...] = g_ref[...] + change
        sums_ref[...] = sums

    return call(
        body,
        (1,),
        [whole(back.shape), whole(x.shape), whole(grad.shape), whole(gb.shape)],
        [made((t, d), F32), made((2, d), F32)],
        [],
        (back, x, grad, gb),
    )


def swap_places(rows_array):
    return lax.all_to_all(rows_array, "seq", split_axis=0, concat_axis=0, tiled=True)


def pack_layer(time_qkv, time_out, time_mix, space_qkv, space_out, mlp_in, mlp_out):
    width = time_qkv.shape[2]
    r = time_qkv.shape[0]
    halves = time_mix.shape[1] // width

    def columns(a):
        return a.reshape(r, -1, width).transpose(1, 0, 2)

    mix = time_mix.reshape(-1, halves, width).transpose(1, 0, 2).reshape(1, r, width)
    return jnp.concatenate(
        (
            columns(time_qkv),
            columns(space_qkv),
            time_out.T[None],
            space_out.T[None],
            columns(mlp_in),
            columns(mlp_out.T),
            mix,
        ),
        axis=0,
    )


def gather_slabs(pack):
    full = lax.all_gather(pack, ("head", "clip", "seq"), axis=1, tiled=True)
    return full.reshape(pack.shape[0], lax.axis_size("head"), -1, pack.shape[2])


def mix_whole(slab, shards):
    shares, depth, width = slab.shape
    part = slab.reshape(shares, shards, shares, depth // (shards * shares), width)
    return part.transpose(1, 0, 3, 2, 4).reshape(depth, shares * width)


def mix_slab(whole_grad, shards, shares):
    depth, full = whole_grad.shape
    width = full // shares
    part = whole_grad.reshape(shards, shares, depth // (shards * shares), shares, width)
    return part.transpose(1, 0, 3, 2, 4).reshape(1, shares, depth, width)


class Piece:
    def __init__(self, keep, got, first, n, order):
        self.near = (keep, got)
        self.first = first
        self.n = n
        self.order = order
        self.step = 0
        self.held = []
        self.result = None


PLACE = {"x": 1, "h": 2}


def fold(pieces, me):
    ways = lax.axis_size("seq")
    depth, width = pieces[0].near[0].shape[-2:]
    r = depth // ways
    used = {}
    arrays = []

    def number(a):
        for i, known in enumerate(arrays):
            if known is a:
                return i
        arrays.append(a)
        return len(arrays) - 1

    plans = []
    for p in pieces:
        link = p.order[p.step] if p.step < 2 else "z"
        blocks = p.n * (2 if p.step == 0 else 1)
        base = used.get(link, 0)
        used[link] = base + blocks
        near = [number(a) for a in p.near]
        held = [(number(a), at) for a, at in p.held]
        plans.append((p, link, base, near, held))
    links = sorted(used)
    shapes = [
        (ways, used[k], r, width) if k == "z" else (used[k], depth, width) for k in links
    ]
    rooms, counts = [], []
    for p, link, base, near, held in plans:
        each = 2 if p.step == 0 else 1
        counts.append((each, len(near) + len(held)))
        rooms += [(each * p.n, depth, width)] * (len(near) + len(held))
    copies_needed = sum(each * terms for each, terms in counts)

    def body(me_ref, *refs):
        sources = refs[: len(arrays)]
        outs = dict(zip(links, refs[len(arrays) : len(arrays) + len(links)]))
        held_refs = refs[len(arrays) + len(links) : -1]
        sems = refs[-1]
        mine = {name: me_ref[PLACE[name]] for name in PLACE}
        groups = []
        room = 0
        sem = 0
        for p, link, base, near, held in plans:
            group = []
            if p.step == 0:
                for term in near:
                    for k in range(2):
                        pick = {p.order[0]: 1 - mine[p.order[0]], p.order[1]: k}
                        source = sources[term].at[pl.ds(p.first, p.n), pick["h"], pick["x"]]
                        group.append((source, held_refs[room].at[pl.ds(k * p.n, p.n)]))
                    room += 1
            else:
                last = p.order[1]
                pick = {p.order[0]: mine[p.order[0]]}
                pick[last] = 1 - mine[last] if p.step == 1 else mine[last]
                for term in near:
                    source = sources[term].at[pl.ds(p.first, p.n), pick["h"], pick["x"]]
                    group.append((source, held_refs[room]))
                    room += 1
                for i, (term, at) in enumerate(held):
                    start = at + pick[last] * p.n if i == 0 else at
                    group.append((sources[term].at[pl.ds(start, p.n)], held_refs[room]))
                    room += 1
            made_copies = []
            for source, target in group:
                made_copies.append(pltpu.make_async_copy(source, target, sems.at[sem]))
                sem += 1
            groups.append(made_copies)
        for group in groups:
            for copy in group:
                copy.start()
        room = 0
        for (p, link, base, near, held), (each, terms), group in zip(plans, counts, groups):
            these = held_refs[room : room + terms]
            room += terms
            for copy in group:
                copy.wait()

            @pl.loop(0, each * p.n)
            def _(i, these=these, base=base, out=outs[link], last=p.step == 2):
                value = these[0][i].astype(F32)
                for one in these[1:]:
                    value = value + one[i].astype(F32)
                value = value.astype(BF16)
                if last:
                    for k in range(ways):
                        out[k, base + i] = value[k * r : (k + 1) * r]
                else:
                    out[base + i] = value

    moved = sum(2 * math.prod(room) for room in rooms) + sum(2 * math.prod(shape) for shape in shapes)
    sums = pl.pallas_call(
        body,
        out_shape=[jax.ShapeDtypeStruct(shape, BF16) for shape in shapes],
        in_specs=[SCALARS] + [pl.BlockSpec(memory_space=pl.ANY)] * len(arrays),
        out_specs=[pl.BlockSpec(memory_space=pltpu.VMEM)] * len(links),
        scratch_shapes=[pltpu.VMEM(room, BF16) for room in rooms]
        + [pltpu.SemaphoreType.DMA((copies_needed,))],
        compiler_params=pltpu.CompilerParams(vmem_limit_bytes=VMEM),
        cost_estimate=pl.CostEstimate(flops=0, bytes_accessed=moved, transcendentals=0),
    )(me, *arrays)
    return [(p, link, base) for p, link, base, _, _ in plans], dict(zip(links, sums))


def cross(a, name):
    axis, bit = ("head", 0) if name == "h" else ("clip", 1 if name == "x" else 0)
    size = lax.axis_size(axis)
    return lax.ppermute(a, axis, [(i, i ^ (1 << bit)) for i in range(size)])


def pieces_of(halves_of):
    total = sum(keep.shape[0] for keep, _ in halves_of)
    found = []
    seen = 0
    for keep, send in halves_of:
        got = cross(send, "c")
        n = keep.shape[0]
        first = min(max((total + 1) // 2 - seen, 0), n)
        if first:
            found.append(Piece(keep, got, 0, first, ("x", "h")))
        if n > first:
            found.append(Piece(keep, got, first, n - first, ("h", "x")))
        seen += n
    return found


def move(x, pieces, me):
    plans, sums = fold(pieces, me)
    x, sums = lax.optimization_barrier((x, sums))
    got = {}
    for link, array in sums.items():
        if link == "z":
            every = lax.all_to_all(array, "seq", split_axis=0, concat_axis=0, tiled=True)
            got[link] = jnp.sum(every.astype(F32), axis=0)
        else:
            got[link] = cross(array, link)
    for p, link, base in plans:
        if link == "z":
            p.result = got[link][base : base + p.n]
        else:
            p.held.append((got[link], base))
        p.step += 1
    return x


def settle(x, pieces):
    arrays = []
    for p in pieces:
        if not any(p.held[-1][0] is a for a in arrays):
            arrays.append(p.held[-1][0])
    x, came = lax.optimization_barrier((x, arrays))
    for p in pieces:
        for old, new in zip(arrays, came):
            if p.held[-1][0] is old:
                p.held[-1] = (new, p.held[-1][1])
                break
    return x


def reduce_plain(halves_of, core):
    def joined(keep, send):
        low = jnp.where(core == 0, keep, send)
        high = jnp.where(core == 0, send, keep)
        n, shares, pairs, depth, width = keep.shape
        return jnp.stack((low, high), axis=3).reshape(n, shares, 2 * pairs * depth, width)

    g = jnp.concatenate([joined(*pair) for pair in halves_of], axis=0)
    g = lax.psum_scatter(g, "head", scatter_dimension=1, tiled=True)
    g = lax.psum_scatter(g.astype(F32), ("clip", "seq"), scatter_dimension=2, tiled=True)
    return g[:, 0]


def gather_norms(gain, bias):
    layers, norms, part = gain.shape
    both = jnp.concatenate((gain, bias), axis=1).reshape(1, -1)
    count = lax.axis_size("clip") * lax.axis_size("seq") * lax.axis_size("head")
    width = round_up(both.shape[1], 128)
    padded = jnp.pad(both, ((0, 0), (0, width - both.shape[1])))
    every = lax.all_to_all(
        jnp.broadcast_to(padded, (count, width)), ALL, split_axis=0, concat_axis=0, tiled=True
    )[:, : both.shape[1]]
    return every.reshape(count, layers * 2 * norms, part).transpose(1, 0, 2).reshape(layers, 2 * norms, -1)


def reduce_norms(sums):
    count = lax.axis_size("clip") * lax.axis_size("seq") * lax.axis_size("head")
    rows, features = sums.shape
    part = features // count
    a = sums.reshape(rows, count, part).transpose(1, 0, 2).reshape(count, rows * part)
    width = round_up(rows * part, 128)
    a = jnp.pad(a, ((0, 0), (0, width - rows * part)))
    every = lax.all_to_all(a, ALL, split_axis=0, concat_axis=0, tiled=True)
    return jnp.sum(every, axis=0)[: rows * part].reshape(rows, part)


def on_device(
    tokens,
    cotangent,
    time_qkv,
    time_out,
    time_mix,
    space_qkv,
    space_out,
    mlp_in,
    mlp_out,
    norm_gain,
    norm_bias,
):
    layers = time_qkv.shape[0]
    clips, frames, places, d = tokens.shape
    ways = lax.axis_size("seq")
    shards = lax.axis_size("clip") * ways
    rows = Rows(clips * frames, places, ways)
    shares = lax.axis_size("head")

    def as_rows(a):
        a = a.astype(F32).reshape(rows.frames, places, d)
        a = jnp.pad(a, ((0, 0), (0, rows.frame_rows - places), (0, 0)))
        return a.reshape(rows.rows, d)

    def from_rows(a):
        a = a.reshape(rows.frames, rows.frame_rows, d)[:, :places]
        return a.reshape(tokens.shape)

    gbs = gather_norms(norm_gain, norm_bias)
    gb = [gbs[l] for l in range(layers)]
    weights = [
        gather_slabs(
            pack_layer(
                time_qkv[l], time_out[l], time_mix[l], space_qkv[l], space_out[l], mlp_in[l], mlp_out[l]
            )
        )
        for l in range(layers)
    ]
    mixes = [mix_whole(w[-1], shards) for w in weights]

    x = as_rows(tokens)
    send = send_first(rows, x, gb[0])
    kept = []
    for l in range(layers):
        w = weights[l]
        a1 = swap_places(send)
        qkv1, o1_time, log1 = time_forward(rows, a1, w, shares)
        back = swap_places(o1_time)
        o1, y1, x1, qkv2 = middle_forward(rows, back, x, w, mixes[l], gb[l])
        o2, x2, log2 = space_forward(rows, qkv2, x1, w)
        kept.append((x, a1, qkv1, log1, o1, y1, x1, qkv2, o2, log2, x2))
        if l + 1 < layers:
            x, send = mlp_forward(rows, x2, w, gb[l], gb[l + 1])
        else:
            (x,) = mlp_forward(rows, x2, w, gb[l], None)
    output = from_rows(x).astype(BF16)

    grad = as_rows(cotangent)
    halves = Halves(lax.axis_size("clip"), d, time_qkv.shape[3])
    clip = lax.axis_index("clip")
    me = jnp.stack((clip & 1, (clip >> 1) & 1, lax.axis_index("head"))).astype(jnp.int32)
    norm_rows = [None] * layers
    summed = [None] * layers
    late = []
    quick = lax.axis_size("clip") == 4 and shares == 2 and time_qkv.shape[1] % 16 == 0
    for l in reversed(range(layers)):
        w = weights[l]
        x, a1, qkv1, log1, o1, y1, x1, qkv2, o2, log2, x2 = kept[l]
        grad, g_ff, s3 = mlp_backward(rows, grad, x2, w, gb[l], me, halves)
        if quick:
            ff = pieces_of([g_ff])
            if late:
                grad = settle(grad, late)
                grad = move(grad, late, me)
                late = [p for p in late if p.step < 3]
        grad, g_space, s2 = space_backward(rows, grad, x1, qkv2, o2, log2, w, gb[l], me, halves)
        if quick:
            space = pieces_of([g_space])
            grad = move(grad, ff, me)
        do1, g_out = middle_backward(rows, grad, y1, o1, w, mixes[l], me, halves, shards)
        do1 = swap_places(do1)
        if quick:
            do1 = move(do1, ff + space + late, me)
        da1, g_time = time_backward(rows, do1, a1, qkv1, log1, w, me, halves)
        if quick:
            da1 = settle(da1, ff + space)
        da1 = swap_places(da1)
        if quick:
            rest = pieces_of([g_out, g_time])
            da1 = move(da1, ff + space + rest, me)
            late = space + rest
        grad, s1 = first_norm_back(rows, da1, x, grad, gb[l])
        norm_rows[l] = jnp.concatenate((s1[0:1], s2[0:1], s3[0:1], s1[1:2], s2[1:2], s3[1:2]), axis=0)
        if quick:
            summed[l] = ff + space + rest
        else:
            summed[l] = [reduce_plain([g_ff, g_space, g_out, g_time], clip & 1)]
    if quick:
        move((), late, me)
        move((), rest, me)
        summed = [[p.result for p in some] for some in summed]
    cuts = (g_ff[0].shape[0], g_space[0].shape[0], g_out[0].shape[0], g_time[0].shape[0])
    results = []
    for some in summed:
        slabs_of = jnp.concatenate(some, axis=0)
        ends = [sum(cuts[: i + 1]) for i in range(4)]
        results.append([slabs_of[e - c : e] for c, e in zip(cuts, ends)])
    tokens_grad = from_rows(grad)
    norm_sums = reduce_norms(jnp.concatenate(norm_rows, axis=0)).reshape(layers, 2, 3, -1)

    def stacked(form):
        return jnp.stack([form(*results[l]) for l in range(layers)])

    def rows_of(a):
        return a.transpose(1, 0, 2)

    def flat(a):
        return rows_of(a).reshape(a.shape[1], -1)

    def mix_rows(a):
        r, width = a.shape
        return a.reshape(shares, r // shares, width).transpose(1, 0, 2).reshape(r // shares, -1)

    per_share = mlp_in.shape[2] // time_qkv.shape[3]
    return (
        output,
        tokens_grad,
        stacked(lambda ff, s, t, q: rows_of(q)),
        stacked(lambda ff, s, t, q: t[0].T),
        stacked(lambda ff, s, t, q: mix_rows(t[1])),
        stacked(lambda ff, s, t, q: rows_of(s[1:])),
        stacked(lambda ff, s, t, q: s[0].T),
        stacked(lambda ff, s, t, q: flat(ff[:per_share])),
        stacked(lambda ff, s, t, q: flat(ff[per_share:]).T),
        norm_sums[:, 0],
        norm_sums[:, 1],
    )


def solution(mesh):
    token_spec = P(("clip", "head"), "seq", None, None)
    in_specs = (
        token_spec,
        token_spec,
        P(None, ("clip", "seq"), None, "head"),
        P(None, "head", ("clip", "seq")),
        P(None, ("clip", "seq", "head"), None),
        P(None, ("clip", "seq"), None, "head"),
        P(None, "head", ("clip", "seq")),
        P(None, ("clip", "seq"), "head"),
        P(None, "head", ("clip", "seq")),
        P(None, None, ("clip", "seq", "head")),
        P(None, None, ("clip", "seq", "head")),
    )
    return jax.shard_map(
        on_device, mesh=mesh, in_specs=in_specs, out_specs=in_specs, check_vma=False
    )
```

```python
import functools
import math

import jax
import jax.numpy as jnp
from jax import lax
from jax.experimental import pallas as pl
from jax.experimental.pallas import tpu as pltpu
from jax.sharding import PartitionSpec as P

HEAD_DIM = 64
NORM_EPS = 1e-06
HALF_ROOT = 0.7071067811865476
INV_ROOT_TAU = 0.3989422804014327
LOG2E = 1.4426950408889634
FAR = -1e30
LANES = 128
VMEM = 56 * 1024 * 1024
SHOWN = 1.0
ALL = ("clip", "seq", "head")
BF16 = jnp.bfloat16
F32 = jnp.float32


def round_up(value, step):
    return -(-value // step) * step


def nn(a, b):
    return lax.dot_general(a, b, (((1,), (0,)), ((), ())), preferred_element_type=F32)


def nt(a, b):
    return lax.dot_general(a, b, (((1,), (1,)), ((), ())), preferred_element_type=F32)


def tn(a, b):
    return lax.dot_general(a, b, (((0,), (0,)), ((), ())), preferred_element_type=F32)


def norm_parts(x):
    mean = jnp.mean(x, axis=-1, keepdims=True)
    centred = x - mean
    spread = lax.rsqrt(jnp.mean(centred * centred, axis=-1, keepdims=True) + NORM_EPS)
    return centred * spread, spread


def norm_rounded(x, gain, bias):
    hat, _ = norm_parts(x)
    return (hat * gain + bias).astype(BF16)


def norm_back(u, x, gain):
    hat, spread = norm_parts(x)
    scaled = u * gain
    mean_scaled = jnp.mean(scaled, axis=-1, keepdims=True)
    mean_cross = jnp.mean(scaled * hat, axis=-1, keepdims=True)
    change = spread * (scaled - mean_scaled - hat * mean_cross)
    sums = jnp.concatenate(
        (jnp.sum(u * hat, axis=0, keepdims=True), jnp.sum(u, axis=0, keepdims=True)), axis=0
    )
    return change, sums


class Rows:
    def __init__(self, frames, places, ways):
        self.frames = frames
        self.places = places
        self.ways = ways
        self.frame_rows = round_up(places, 16)
        self.rows = frames * self.frame_rows
        self.block = places // ways
        self.chunk = round_up(frames * self.block, 8)
        self.time_rows = ways * self.chunk

    def split(self, r):
        way = jnp.zeros_like(r)
        for k in range(1, self.ways):
            way = way + (r >= k * self.chunk).astype(jnp.int32)
        rest = r - way * self.chunk
        frame = jnp.zeros_like(r)
        for k in range(1, self.frames):
            frame = frame + (rest >= k * self.block).astype(jnp.int32)
        real = rest < self.frames * self.block
        return way, frame, rest - frame * self.block, real

    def to_time(self):
        r = lax.broadcasted_iota(jnp.int32, (self.time_rows, 1), 0)
        way, frame, place, real = self.split(r)
        source = jnp.where(real, frame * self.frame_rows + way * self.block + place, -1)
        c = lax.broadcasted_iota(jnp.int32, (self.time_rows, self.rows), 1)
        return jnp.where(c == source, 1.0, 0.0).astype(BF16)

    def time_bias(self):
        def label(r):
            _, _, place, real = self.split(r)
            return jnp.where(real, place, -1)

        a = label(lax.broadcasted_iota(jnp.int32, (self.time_rows, 1), 0))
        b = label(lax.broadcasted_iota(jnp.int32, (1, self.time_rows), 1))
        return jnp.where(a == b, 0.0, FAR).astype(F32)

    def space_bias(self):
        a = lax.broadcasted_iota(jnp.int32, (self.frame_rows, 1), 0)
        return jnp.where(a < self.places, 0.0, FAR).astype(F32)


def lane_masks(rows):
    lane = lax.broadcasted_iota(jnp.int32, (rows, LANES), 1)
    return lane < HEAD_DIM


def one_of(value, low, half):
    zero = jnp.zeros_like(value)
    return jnp.where(low, value, zero) if half == 0 else jnp.where(low, zero, value)


def pair_forward(q, k, v, bias, rate):
    low = lane_masks(q.shape[0])
    mixed, logs = [], []
    for half in range(2):
        s = nt(k, one_of(q, low, half)) + bias
        peak = jnp.max(s, axis=0, keepdims=True)
        e = jnp.exp2((s - peak) * rate)
        total = jnp.sum(e, axis=0, keepdims=True)
        soft = (e * (1.0 / total)).astype(BF16)
        mixed.append(tn(soft, v))
        logs.append(peak * rate + jnp.log2(total))
    return jnp.where(low, mixed[0], mixed[1]).astype(BF16), logs


def pair_backward(q, k, v, do, logs, bias, rate, scale):
    low = lane_masks(q.shape[0])
    dq, dk, dv = [], [], []
    for half in range(2):
        s = nt(k, one_of(q, low, half)) + bias
        soft = jnp.exp2(s * rate - logs[half])
        dp = nt(v, one_of(do, low, half))
        ds = (soft * (dp - jnp.sum(soft * dp, axis=0, keepdims=True))).astype(BF16)
        dv.append(nn(soft.astype(BF16), do))
        dk.append(nn(ds, q))
        dq.append(tn(ds, k))
    return (
        (jnp.where(low, dq[0], dq[1]) * scale).astype(BF16),
        (jnp.where(low, dk[0], dk[1]) * scale).astype(BF16),
        jnp.where(low, dv[0], dv[1]).astype(BF16),
    )


def split_rows(value, keep_ref, send_ref, at, room_ref, me_ref):
    mine = me_ref[0]
    room_ref[...] = value.reshape(room_ref.shape)
    keep_ref[at] = room_ref[:, mine].astype(BF16)
    send_ref[at] = room_ref[:, 1 - mine].astype(BF16)


class Halves:
    def __init__(self, clips, depth, width):
        self.pairs = clips // 2
        self.rows = depth // clips
        self.width = width

    def array(self, lead, block, index):
        tail = (self.pairs, self.rows, self.width)
        one = lambda: made(lead + tail, BF16, block + tail, lambda *g: index(*g) + (0, 0, 0))
        return [one(), one()]

    def room(self):
        return pltpu.VMEM((self.pairs, 2, self.rows, self.width), F32)


SCALARS = pl.BlockSpec(memory_space=pltpu.SMEM)


def call(body, grid, ins, outs, scratch, args, flops=0):
    specs = [spec for spec in ins]
    moved = sum(math.prod(o.shape) * o.dtype.itemsize for o, _ in outs)
    moved += sum(math.prod(a.shape) * a.dtype.itemsize for a in args)
    return pl.pallas_call(
        body,
        out_shape=[shape for shape, _ in outs],
        grid=grid,
        in_specs=specs,
        out_specs=[spec for _, spec in outs],
        scratch_shapes=scratch,
        compiler_params=pltpu.CompilerParams(vmem_limit_bytes=VMEM),
        cost_estimate=pl.CostEstimate(
            flops=int(flops * SHOWN), bytes_accessed=int(moved * SHOWN), transcendentals=0
        ),
    )(*args)


def whole(shape):
    zeros = (0,) * len(shape)
    return pl.BlockSpec(shape, lambda *_: zeros)


def made(shape, dtype, block=None, index=None):
    spec = whole(shape) if block is None else pl.BlockSpec(block, index)
    return jax.ShapeDtypeStruct(shape, dtype), spec


def slabs(count, first, width, depth):
    return pl.BlockSpec((count, 1, depth, width), lambda h, *_: (first // count, h, 0, 0))


def send_first(rows, x, gb):
    def body(x_ref, gb_ref, out_ref):
        a = norm_rounded(x_ref[...], gb_ref[0:1], gb_ref[3:4])
        out_ref[...] = nn(rows.to_time(), a).astype(BF16)

    d = x.shape[1]
    return call(
        body, (1,), [whole(x.shape), whole(gb.shape)], [made((rows.time_rows, d), BF16)], [], (x, gb)
    )[0]


def time_forward(rows, a, w, head_shares):
    t, d = a.shape
    width = w.shape[3]
    pairs = width // LANES
    rate = LOG2E / math.sqrt(HEAD_DIM)

    def body(a_ref, w_ref, qkv_ref, out_ref, log_ref, bias_ref):
        @pl.when(pl.program_id(0) == 0)
        def _():
            bias_ref[...] = rows.time_bias()

        act = a_ref[...]
        for g in range(3):
            qkv_ref[g] = nn(act, w_ref[g, 0]).astype(BF16)

        @pl.loop(0, pairs)
        def _(i):
            lanes = pl.ds(pl.multiple_of(i * LANES, LANES), LANES)
            mixed, logs = pair_forward(
                qkv_ref[0, :, lanes], qkv_ref[1, :, lanes], qkv_ref[2, :, lanes], bias_ref[...], rate
            )
            out_ref[:, lanes] = mixed
            log_ref[0, i] = jnp.concatenate(logs, axis=0)

    return call(
        body,
        (head_shares,),
        [whole(a.shape), slabs(3, 0, width, d)],
        [
            made((3, t, d), BF16, (3, t, width), lambda h: (0, 0, h)),
            made((t, d), BF16, (t, width), lambda h: (0, h)),
            made((head_shares, pairs, 2, t), F32, (1, pairs, 2, t), lambda h: (h, 0, 0, 0)),
        ],
        [pltpu.VMEM((t, t), F32)],
        (a, w),
        flops=2 * t * d * 3 * d,
    )


def middle_forward(rows, back, x, w, mix, gb):
    t, d = x.shape
    width = w.shape[3]
    shares = w.shape[1]

    def body(back_ref, x_ref, to_ref, sq_ref, mix_ref, gb_ref, o1_ref, y1_ref, x1_ref, qkv_ref):
        o1 = tn(rows.to_time(), back_ref[...]).astype(BF16)
        o1_ref[...] = o1
        y1 = jnp.zeros((t, d), F32)
        for h in range(shares):
            y1 = y1 + nt(o1[:, h * width : (h + 1) * width], to_ref[0, h])
        y1 = y1.astype(BF16)
        y1_ref[...] = y1
        x1 = x_ref[...] + nn(y1, mix_ref[...])
        x1_ref[...] = x1
        a2 = norm_rounded(x1, gb_ref[1:2], gb_ref[4:5])
        for g in range(3):
            for h in range(shares):
                qkv_ref[g, :, h * width : (h + 1) * width] = nn(a2, sq_ref[g, h]).astype(BF16)

    return call(
        body,
        (1,),
        [
            whole(back.shape),
            whole(x.shape),
            pl.BlockSpec((1, shares, d, width), lambda i: (6, 0, 0, 0)),
            pl.BlockSpec((3, shares, d, width), lambda i: (1, 0, 0, 0)),
            whole(mix.shape),
            whole(gb.shape),
        ],
        [made((t, d), BF16), made((t, d), BF16), made((t, d), F32), made((3, t, d), BF16)],
        [],
        (back, x, w, w, mix, gb),
        flops=2 * t * d * 5 * d,
    )


def space_forward(rows, qkv, x1, w):
    t, d = x1.shape
    width = w.shape[3]
    shares = w.shape[1]
    pairs = width // LANES
    rate = LOG2E / math.sqrt(HEAD_DIM)
    n = rows.frame_rows

    def body(qkv_ref, x1_ref, w_ref, o2_ref, x2_ref, log_ref):
        bias = rows.space_bias()

        @pl.loop(0, pairs)
        def _(i):
            lanes = pl.ds(pl.multiple_of(i * LANES, LANES), LANES)
            for f in range(rows.frames):
                at = slice(f * n, (f + 1) * n)
                mixed, logs = pair_forward(
                    qkv_ref[0, at, lanes], qkv_ref[1, at, lanes], qkv_ref[2, at, lanes], bias, rate
                )
                o2_ref[at, lanes] = mixed
                log_ref[0, i, f] = jnp.concatenate(logs, axis=0)

        @pl.when(pl.program_id(0) == 0)
        def _():
            x2_ref[...] = x1_ref[...]

        x2_ref[...] += nt(o2_ref[...], w_ref[0, 0])

    return call(
        body,
        (shares,),
        [
            pl.BlockSpec((3, t, width), lambda h: (0, 0, h)),
            whole(x1.shape),
            slabs(1, 7, width, d),
        ],
        [
            made((t, d), BF16, (t, width), lambda h: (0, h)),
            made((t, d), F32),
            made(
                (shares, pairs, rows.frames, 2, n),
                F32,
                (1, pairs, rows.frames, 2, n),
                lambda h: (h, 0, 0, 0, 0),
            ),
        ],
        [],
        (qkv, x1, w),
        flops=2 * t * d * d,
    )


def ff_slab(first, per_share, depth, width):
    return pl.BlockSpec(
        (1, 1, depth, width), lambda j: (first + j % per_share, j // per_share, 0, 0)
    )


def mlp_forward(rows, x2, w, gb, gb_next):
    t, d = x2.shape
    width = w.shape[3]
    shares = w.shape[1]
    per_share = (w.shape[0] - 9) // 2
    steps = shares * per_share
    last = gb_next is None

    def body(x2_ref, wi_ref, wo_ref, gb_ref, *rest):
        if last:
            x3_ref, a3_ref = rest
        else:
            gn_ref, x3_ref, send_ref, a3_ref = rest
        j = pl.program_id(0)

        @pl.when(j == 0)
        def _():
            a3_ref[...] = norm_rounded(x2_ref[...], gb_ref[2:3], gb_ref[5:6])
            x3_ref[...] = x2_ref[...]

        hid = nn(a3_ref[...], wi_ref[0, 0])
        act = (0.5 * hid * (1.0 + lax.erf(hid * HALF_ROOT))).astype(BF16)
        x3_ref[...] += nt(act, wo_ref[0, 0])

        if not last:

            @pl.when(j == steps - 1)
            def _():
                a = norm_rounded(x3_ref[...], gn_ref[0:1], gn_ref[3:4])
                send_ref[...] = nn(rows.to_time(), a).astype(BF16)

    ins = [
        whole(x2.shape),
        ff_slab(8, per_share, d, width),
        ff_slab(8 + per_share, per_share, d, width),
        whole(gb.shape),
    ]
    outs = [made((t, d), F32)]
    args = [x2, w, w, gb]
    if not last:
        ins.append(whole(gb_next.shape))
        outs.append(made((rows.time_rows, d), BF16))
        args.append(gb_next)
    return call(
        body, (steps,), ins, outs, [pltpu.VMEM((t, d), BF16)], tuple(args), flops=4 * t * d * width * steps
    )


def mlp_backward(rows, grad, x2, w, gb, me, halves):
    t, d = x2.shape
    width = w.shape[3]
    shares = w.shape[1]
    per_share = (w.shape[0] - 9) // 2
    steps = shares * per_share

    def body(me_ref, g_ref, x2_ref, wi_ref, wo_ref, gb_ref, go_ref, ki_ref, si_ref, ko_ref, so_ref, sums_ref, a3_ref, a3t_ref, e3_ref, e3t_ref, u_ref, room_ref):
        j = pl.program_id(0)

        @pl.when(j == 0)
        def _():
            hat, _ = norm_parts(x2_ref[...])
            a3 = hat * gb_ref[2:3] + gb_ref[5:6]
            a3_ref[...] = a3.astype(BF16)
            a3t_ref[...] = a3.T.astype(BF16)
            g = g_ref[...]
            e3_ref[...] = g.astype(BF16)
            e3t_ref[...] = g.T.astype(BF16)
            u_ref[...] = jnp.zeros((t, d), F32)

        hid = nn(a3_ref[...], wi_ref[0, 0])
        phi = 0.5 * (1.0 + lax.erf(hid * HALF_ROOT))
        act = (hid * phi).astype(BF16)
        slope = phi + hid * jnp.exp(-0.5 * hid * hid) * INV_ROOT_TAU
        dhid = (nn(e3_ref[...], wo_ref[0, 0]) * slope).astype(BF16)
        split_rows(nn(e3t_ref[...], act), ko_ref, so_ref, (0, 0), room_ref, me_ref)
        split_rows(nn(a3t_ref[...], dhid), ki_ref, si_ref, (0, 0), room_ref, me_ref)
        u_ref[...] += nt(dhid, wi_ref[0, 0])

        @pl.when(j == steps - 1)
        def _():
            change, sums = norm_back(u_ref[...], x2_ref[...], gb_ref[2:3])
            go_ref[...] = g_ref[...] + change
            sums_ref[...] = sums

    slab_outs = [
        one
        for _ in range(2)
        for one in halves.array(
            (per_share, shares), (1, 1), lambda j: (j % per_share, j // per_share)
        )
    ]
    grad, ki, si, ko, so, sums = call(
        body,
        (steps,),
        [
            SCALARS,
            whole(grad.shape),
            whole(x2.shape),
            ff_slab(8, per_share, d, width),
            ff_slab(8 + per_share, per_share, d, width),
            whole(gb.shape),
        ],
        [made((t, d), F32), *slab_outs, made((2, d), F32)],
        [
            pltpu.VMEM((t, d), BF16),
            pltpu.VMEM((d, t), BF16),
            pltpu.VMEM((t, d), BF16),
            pltpu.VMEM((d, t), BF16),
            pltpu.VMEM((t, d), F32),
            halves.room(),
        ],
        (me, grad, x2, w, w, gb),
        flops=10 * t * d * width * steps,
    )
    return grad, [(ki, si), (ko, so)], sums


def space_backward(rows, grad, x1, qkv, o2, logs, w, gb, me, halves):
    t, d = x1.shape
    width = w.shape[3]
    shares = w.shape[1]
    pairs = width // LANES
    scale = 1.0 / math.sqrt(HEAD_DIM)
    rate = LOG2E * scale
    n = rows.frame_rows

    def body(me_ref, g_ref, x1_ref, qkv_ref, o2_ref, log_ref, wo_ref, wq_ref, gb_ref, go_ref, keep_ref, send_ref, sums_ref, e2_ref, e2t_ref, a2t_ref, do_ref, dqkv_ref, u_ref, room_ref):
        h = pl.program_id(0)

        @pl.when(h == 0)
        def _():
            g = g_ref[...]
            e2_ref[...] = g.astype(BF16)
            e2t_ref[...] = g.T.astype(BF16)
            hat, _ = norm_parts(x1_ref[...])
            a2t_ref[...] = (hat * gb_ref[1:2] + gb_ref[4:5]).T.astype(BF16)
            u_ref[...] = jnp.zeros((t, d), F32)

        bias = rows.space_bias()
        split_rows(nn(e2t_ref[...], o2_ref[...]), keep_ref, send_ref, (0, 0), room_ref, me_ref)
        do_ref[...] = nn(e2_ref[...], wo_ref[0, 0]).astype(BF16)

        @pl.loop(0, pairs)
        def _(i):
            lanes = pl.ds(pl.multiple_of(i * LANES, LANES), LANES)
            for f in range(rows.frames):
                at = slice(f * n, (f + 1) * n)
                log = log_ref[0, i, f]
                grads = pair_backward(
                    qkv_ref[0, at, lanes],
                    qkv_ref[1, at, lanes],
                    qkv_ref[2, at, lanes],
                    do_ref[at, lanes],
                    (log[0:1], log[1:2]),
                    bias,
                    rate,
                    scale,
                )
                for part in range(3):
                    dqkv_ref[part, at, lanes] = grads[part]

        for part in range(3):
            split_rows(
                nn(a2t_ref[...], dqkv_ref[part]), keep_ref, send_ref, (part + 1, 0), room_ref, me_ref
            )
            u_ref[...] += nt(dqkv_ref[part], wq_ref[part, 0])

        @pl.when(h == shares - 1)
        def _():
            change, sums = norm_back(u_ref[...], x1_ref[...], gb_ref[1:2])
            go_ref[...] = g_ref[...] + change
            sums_ref[...] = sums

    grad, keep, send, sums = call(
        body,
        (shares,),
        [
            SCALARS,
            whole(grad.shape),
            whole(x1.shape),
            pl.BlockSpec((3, t, width), lambda h: (0, 0, h)),
            pl.BlockSpec((t, width), lambda h: (0, h)),
            pl.BlockSpec((1,) + logs.shape[1:], lambda h: (h, 0, 0, 0, 0)),
            slabs(1, 7, width, d),
            slabs(3, 3, width, d),
            whole(gb.shape),
        ],
        [
            made((t, d), F32),
            *halves.array((4, shares), (4, 1), lambda h: (0, h)),
            made((2, d), F32),
        ],
        [
            pltpu.VMEM((t, d), BF16),
            pltpu.VMEM((d, t), BF16),
            pltpu.VMEM((d, t), BF16),
            pltpu.VMEM((t, width), BF16),
            pltpu.VMEM((3, t, width), BF16),
            pltpu.VMEM((t, d), F32),
            halves.room(),
        ],
        (me, grad, x1, qkv, o2, logs, w, w, gb),
        flops=2 * t * d * d * 8,
    )
    return grad, (keep, send), sums


def mix_fits(depth, shards, shares):
    return depth // (shards * shares) % 8 == 0


def middle_backward(rows, grad, y1, o1, w, mix, me, halves, shards):
    t, d = grad.shape
    width = w.shape[3]
    shares = w.shape[1]
    fits = mix_fits(d, shards, shares)
    part = d // (shards * shares)

    def body(me_ref, g_ref, y1_ref, o1_ref, to_ref, mix_ref, send_ref, gk_ref, gs_ref, *rest):
        if fits:
            room_ref, order_ref = rest
        else:
            gm_ref, room_ref = rest
        e1 = g_ref[...].astype(BF16)
        dy1 = nt(e1, mix_ref[...]).astype(BF16)
        send = rows.to_time()
        for h in range(shares):
            lanes = slice(h * width, (h + 1) * width)
            do1 = nn(dy1, to_ref[0, h]).astype(BF16)
            send_ref[:, lanes] = nn(send, do1).astype(BF16)
            split_rows(tn(dy1, o1_ref[:, lanes]), gk_ref, gs_ref, (0, h), room_ref, me_ref)
        gm = tn(y1_ref[...], e1)
        if fits:
            gm = gm.reshape(shards, shares, part, d)
            for h in range(shares):
                for half in range(shares):
                    order_ref[:, half] = gm[:, h, :, half * width : (half + 1) * width]
                split_rows(order_ref[...], gk_ref, gs_ref, (1, h), room_ref, me_ref)
        else:
            gm_ref[...] = gm.astype(BF16)

    outs = [made((rows.time_rows, d), BF16)]
    outs += halves.array((1 + fits, shares), (1 + fits, shares), lambda i: (0, 0))
    scratch = [halves.room()]
    if fits:
        scratch.append(pltpu.VMEM((shards, shares, part, width), F32))
    else:
        outs.append(made((d, d), BF16))
    got = call(
        body,
        (1,),
        [
            SCALARS,
            whole(grad.shape),
            whole(y1.shape),
            whole(o1.shape),
            pl.BlockSpec((1, shares, d, width), lambda i: (6, 0, 0, 0)),
            whole(mix.shape),
        ],
        outs,
        scratch,
        (me, grad, y1, o1, w, mix),
        flops=8 * t * d * d,
    )
    do1, keep, send = got[:3]
    if not fits:
        gm = mix_slab(got[3], shards, shares).reshape((1, shares, halves.pairs, 2) + keep.shape[3:])
        keep = jnp.concatenate((keep, lax.dynamic_index_in_dim(gm, me[0], 3, keepdims=False)), axis=0)
        send = jnp.concatenate((send, lax.dynamic_index_in_dim(gm, 1 - me[0], 3, keepdims=False)), axis=0)
    return do1, (keep, send)


def time_backward(rows, do1, a, qkv, logs, w, me, halves):
    t, d = a.shape
    width = w.shape[3]
    shares = w.shape[1]
    pairs = width // LANES
    scale = 1.0 / math.sqrt(HEAD_DIM)
    rate = LOG2E * scale

    def body(me_ref, do_ref, a_ref, qkv_ref, log_ref, w_ref, out_ref, keep_ref, send_ref, bias_ref, dqkv_ref, at_ref, u_ref, room_ref):
        h = pl.program_id(0)

        @pl.when(h == 0)
        def _():
            bias_ref[...] = rows.time_bias()
            at_ref[...] = a_ref[...].T
            u_ref[...] = jnp.zeros((t, d), F32)

        @pl.loop(0, pairs)
        def _(i):
            lanes = pl.ds(pl.multiple_of(i * LANES, LANES), LANES)
            log = log_ref[0, i]
            grads = pair_backward(
                qkv_ref[0, :, lanes],
                qkv_ref[1, :, lanes],
                qkv_ref[2, :, lanes],
                do_ref[:, lanes],
                (log[0:1], log[1:2]),
                bias_ref[...],
                rate,
                scale,
            )
            for part in range(3):
                dqkv_ref[part, :, lanes] = grads[part]

        for part in range(3):
            split_rows(
                nn(at_ref[...], dqkv_ref[part]), keep_ref, send_ref, (part, 0), room_ref, me_ref
            )
            u_ref[...] += nt(dqkv_ref[part], w_ref[part, 0])

        @pl.when(h == shares - 1)
        def _():
            out_ref[...] = u_ref[...].astype(BF16)

    da1, keep, send = call(
        body,
        (shares,),
        [
            SCALARS,
            pl.BlockSpec((t, width), lambda h: (0, h)),
            whole(a.shape),
            pl.BlockSpec((3, t, width), lambda h: (0, 0, h)),
            pl.BlockSpec((1,) + logs.shape[1:], lambda h: (h, 0, 0, 0)),
            slabs(3, 0, width, d),
        ],
        [
            made((t, d), BF16),
            *halves.array((3, shares), (3, 1), lambda h: (0, h)),
        ],
        [
            pltpu.VMEM((t, t), F32),
            pltpu.VMEM((3, t, width), BF16),
            pltpu.VMEM((d, t), BF16),
            pltpu.VMEM((t, d), F32),
            halves.room(),
        ],
        (me, do1, a, qkv, logs, w),
        flops=2 * t * d * d * 6,
    )
    return da1, (keep, send)


def first_norm_back(rows, back, x, grad, gb):
    t, d = x.shape

    def body(back_ref, x_ref, g_ref, gb_ref, go_ref, sums_ref):
        u = tn(rows.to_time(), back_ref[...])
        change, sums = norm_back(u, x_ref[...], gb_ref[0:1])
        go_ref[...] = g_ref[...] + change
        sums_ref[...] = sums

    return call(
        body,
        (1,),
        [whole(back.shape), whole(x.shape), whole(grad.shape), whole(gb.shape)],
        [made((t, d), F32), made((2, d), F32)],
        [],
        (back, x, grad, gb),
    )


def swap_places(rows_array):
    return lax.all_to_all(rows_array, "seq", split_axis=0, concat_axis=0, tiled=True)


def pack_layer(time_qkv, time_out, time_mix, space_qkv, space_out, mlp_in, mlp_out):
    width = time_qkv.shape[2]
    r = time_qkv.shape[0]
    halves = time_mix.shape[1] // width

    def columns(a):
        return a.reshape(r, -1, width).transpose(1, 0, 2)

    mix = time_mix.reshape(-1, halves, width).transpose(1, 0, 2).reshape(1, r, width)
    return jnp.concatenate(
        (
            columns(time_qkv),
            columns(space_qkv),
            time_out.T[None],
            space_out.T[None],
            columns(mlp_in),
            columns(mlp_out.T),
            mix,
        ),
        axis=0,
    )


def gather_slabs(pack):
    full = lax.all_gather(pack, ("head", "clip", "seq"), axis=1, tiled=True)
    return full.reshape(pack.shape[0], lax.axis_size("head"), -1, pack.shape[2])


def mix_whole(slab, shards):
    shares, depth, width = slab.shape
    part = slab.reshape(shares, shards, shares, depth // (shards * shares), width)
    return part.transpose(1, 0, 3, 2, 4).reshape(depth, shares * width)


def mix_slab(whole_grad, shards, shares):
    depth, full = whole_grad.shape
    width = full // shares
    part = whole_grad.reshape(shards, shares, depth // (shards * shares), shares, width)
    return part.transpose(1, 0, 3, 2, 4).reshape(1, shares, depth, width)


class Piece:
    def __init__(self, keep, got, first, n, order):
        self.near = (keep, got)
        self.first = first
        self.n = n
        self.order = order
        self.step = 0
        self.held = []
        self.result = None


PLACE = {"x": 1, "h": 2}


def fold(pieces, me, last_by_rows):
    ways = lax.axis_size("seq")
    depth, width = pieces[0].near[0].shape[-2:]
    r = depth // ways
    used = {}
    arrays = []

    def number(a):
        for i, known in enumerate(arrays):
            if known is a:
                return i
        arrays.append(a)
        return len(arrays) - 1

    plans = []
    for p in pieces:
        link = p.order[p.step] if p.step < 2 else "z"
        blocks = p.n * (2 if p.step == 0 else 1)
        base = used.get(link, 0)
        used[link] = base + blocks
        near = [number(a) for a in p.near]
        held = [(number(a), at) for a, at in p.held]
        plans.append((p, link, base, near, held))
    links = sorted(used)
    shapes = [
        (ways, used[k], r, width) if k == "z" and last_by_rows else (used[k], depth, width)
        for k in links
    ]
    rooms, counts = [], []
    for p, link, base, near, held in plans:
        each = 2 if p.step == 0 else 1
        counts.append((each, len(near) + len(held)))
        rooms += [(each * p.n, depth, width)] * (len(near) + len(held))
    copies_needed = sum(each * terms for each, terms in counts)

    def body(me_ref, *refs):
        sources = refs[: len(arrays)]
        outs = dict(zip(links, refs[len(arrays) : len(arrays) + len(links)]))
        held_refs = refs[len(arrays) + len(links) : -1]
        sems = refs[-1]
        mine = {name: me_ref[PLACE[name]] for name in PLACE}
        groups = []
        room = 0
        sem = 0
        for p, link, base, near, held in plans:
            group = []
            if p.step == 0:
                for term in near:
                    for k in range(2):
                        pick = {p.order[0]: 1 - mine[p.order[0]], p.order[1]: k}
                        source = sources[term].at[pl.ds(p.first, p.n), pick["h"], pick["x"]]
                        group.append((source, held_refs[room].at[pl.ds(k * p.n, p.n)]))
                    room += 1
            else:
                last = p.order[1]
                pick = {p.order[0]: mine[p.order[0]]}
                pick[last] = 1 - mine[last] if p.step == 1 else mine[last]
                for term in near:
                    source = sources[term].at[pl.ds(p.first, p.n), pick["h"], pick["x"]]
                    group.append((source, held_refs[room]))
                    room += 1
                for i, (term, at) in enumerate(held):
                    start = at + pick[last] * p.n if i == 0 else at
                    group.append((sources[term].at[pl.ds(start, p.n)], held_refs[room]))
                    room += 1
            made_copies = []
            for source, target in group:
                made_copies.append(pltpu.make_async_copy(source, target, sems.at[sem]))
                sem += 1
            groups.append(made_copies)
        for group in groups:
            for copy in group:
                copy.start()
        room = 0
        for (p, link, base, near, held), (each, terms), group in zip(plans, counts, groups):
            these = held_refs[room : room + terms]
            room += terms
            for copy in group:
                copy.wait()

            @pl.loop(0, each * p.n)
            def _(i, these=these, base=base, out=outs[link], last=p.step == 2 and last_by_rows):
                value = these[0][i].astype(F32)
                for one in these[1:]:
                    value = value + one[i].astype(F32)
                value = value.astype(BF16)
                if last:
                    for k in range(ways):
                        out[k, base + i] = value[k * r : (k + 1) * r]
                else:
                    out[base + i] = value

    moved = sum(2 * math.prod(room) for room in rooms) + sum(2 * math.prod(shape) for shape in shapes)
    sums = pl.pallas_call(
        body,
        out_shape=[jax.ShapeDtypeStruct(shape, BF16) for shape in shapes],
        in_specs=[SCALARS] + [pl.BlockSpec(memory_space=pltpu.HBM)] * len(arrays),
        out_specs=[pl.BlockSpec(memory_space=pltpu.VMEM)] * len(links),
        scratch_shapes=[pltpu.VMEM(room, BF16) for room in rooms]
        + [pltpu.SemaphoreType.DMA((copies_needed,))],
        compiler_params=pltpu.CompilerParams(vmem_limit_bytes=VMEM),
        cost_estimate=pl.CostEstimate(flops=0, bytes_accessed=moved, transcendentals=0),
    )(me, *arrays)
    return [(p, link, base) for p, link, base, _, _ in plans], dict(zip(links, sums))


def cross(a, name):
    axis, bit = ("head", 0) if name == "h" else ("clip", 1 if name == "x" else 0)
    size = lax.axis_size(axis)
    return lax.ppermute(a, axis, [(i, i ^ (1 << bit)) for i in range(size)])


def pieces_of(halves_of):
    total = sum(keep.shape[0] for keep, _ in halves_of)
    found = []
    seen = 0
    for keep, send in halves_of:
        got = cross(send, "c")
        n = keep.shape[0]
        first = min(max((total + 1) // 2 - seen, 0), n)
        if first:
            found.append(Piece(keep, got, 0, first, ("x", "h")))
        if n > first:
            found.append(Piece(keep, got, first, n - first, ("h", "x")))
        seen += n
    return found


def move(x, pieces, me, at_end=False):
    plans, sums = fold(pieces, me, at_end)
    x, sums = lax.optimization_barrier((x, sums))
    got = {}
    for link, array in sums.items():
        if link == "z":
            if at_end:
                every = lax.all_to_all(array, "seq", split_axis=0, concat_axis=0, tiled=True)
                got[link] = jnp.sum(every.astype(F32), axis=0)
            else:
                own = lax.psum_scatter(array, "seq", scatter_dimension=1, tiled=True)
                got[link] = own.astype(F32)
        else:
            got[link] = cross(array, link)
    for p, link, base in plans:
        if link == "z":
            p.result = got[link][base : base + p.n]
        else:
            p.held.append((got[link], base))
        p.step += 1
    return x


def settle(x, pieces):
    arrays = []
    for p in pieces:
        if not any(p.held[-1][0] is a for a in arrays):
            arrays.append(p.held[-1][0])
    x, came = lax.optimization_barrier((x, arrays))
    for p in pieces:
        for old, new in zip(arrays, came):
            if p.held[-1][0] is old:
                p.held[-1] = (new, p.held[-1][1])
                break
    return x


def reduce_plain(halves_of, core):
    def joined(keep, send):
        low = jnp.where(core == 0, keep, send)
        high = jnp.where(core == 0, send, keep)
        n, shares, pairs, depth, width = keep.shape
        return jnp.stack((low, high), axis=3).reshape(n, shares, 2 * pairs * depth, width)

    g = jnp.concatenate([joined(*pair) for pair in halves_of], axis=0)
    g = lax.psum_scatter(g, "head", scatter_dimension=1, tiled=True)
    g = lax.psum_scatter(g.astype(F32), ("clip", "seq"), scatter_dimension=2, tiled=True)
    return g[:, 0]


def gather_norms(gain, bias):
    layers, norms, part = gain.shape
    both = jnp.concatenate((gain, bias), axis=1).reshape(1, -1)
    count = lax.axis_size("clip") * lax.axis_size("seq") * lax.axis_size("head")
    width = round_up(both.shape[1], 128)
    padded = jnp.pad(both, ((0, 0), (0, width - both.shape[1])))
    every = lax.all_to_all(
        jnp.broadcast_to(padded, (count, width)), ALL, split_axis=0, concat_axis=0, tiled=True
    )[:, : both.shape[1]]
    return every.reshape(count, layers * 2 * norms, part).transpose(1, 0, 2).reshape(layers, 2 * norms, -1)


def reduce_norms(sums):
    count = lax.axis_size("clip") * lax.axis_size("seq") * lax.axis_size("head")
    rows, features = sums.shape
    part = features // count
    a = sums.reshape(rows, count, part).transpose(1, 0, 2).reshape(count, rows * part)
    width = round_up(rows * part, 128)
    a = jnp.pad(a, ((0, 0), (0, width - rows * part)))
    every = lax.all_to_all(a, ALL, split_axis=0, concat_axis=0, tiled=True)
    return jnp.sum(every, axis=0)[: rows * part].reshape(rows, part)


def on_device(
    tokens,
    cotangent,
    time_qkv,
    time_out,
    time_mix,
    space_qkv,
    space_out,
    mlp_in,
    mlp_out,
    norm_gain,
    norm_bias,
):
    layers = time_qkv.shape[0]
    clips, frames, places, d = tokens.shape
    ways = lax.axis_size("seq")
    shards = lax.axis_size("clip") * ways
    rows = Rows(clips * frames, places, ways)
    shares = lax.axis_size("head")

    def as_rows(a):
        a = a.astype(F32).reshape(rows.frames, places, d)
        a = jnp.pad(a, ((0, 0), (0, rows.frame_rows - places), (0, 0)))
        return a.reshape(rows.rows, d)

    def from_rows(a):
        a = a.reshape(rows.frames, rows.frame_rows, d)[:, :places]
        return a.reshape(tokens.shape)

    gbs = gather_norms(norm_gain, norm_bias)
    gb = [gbs[l] for l in range(layers)]
    weights = [
        gather_slabs(
            pack_layer(
                time_qkv[l], time_out[l], time_mix[l], space_qkv[l], space_out[l], mlp_in[l], mlp_out[l]
            )
        )
        for l in range(layers)
    ]
    mixes = [mix_whole(w[-1], shards) for w in weights]

    x = as_rows(tokens)
    send = send_first(rows, x, gb[0])
    kept = []
    for l in range(layers):
        w = weights[l]
        a1 = swap_places(send)
        qkv1, o1_time, log1 = time_forward(rows, a1, w, shares)
        back = swap_places(o1_time)
        o1, y1, x1, qkv2 = middle_forward(rows, back, x, w, mixes[l], gb[l])
        o2, x2, log2 = space_forward(rows, qkv2, x1, w)
        kept.append((x, a1, qkv1, log1, o1, y1, x1, qkv2, o2, log2, x2))
        if l + 1 < layers:
            x, send = mlp_forward(rows, x2, w, gb[l], gb[l + 1])
        else:
            (x,) = mlp_forward(rows, x2, w, gb[l], None)
    output = from_rows(x).astype(BF16)

    grad = as_rows(cotangent)
    halves = Halves(lax.axis_size("clip"), d, time_qkv.shape[3])
    clip = lax.axis_index("clip")
    me = jnp.stack((clip & 1, (clip >> 1) & 1, lax.axis_index("head"))).astype(jnp.int32)
    norm_rows = [None] * layers
    summed = [None] * layers
    late = []
    quick = lax.axis_size("clip") == 4 and shares == 2 and time_qkv.shape[1] % 16 == 0
    for l in reversed(range(layers)):
        w = weights[l]
        x, a1, qkv1, log1, o1, y1, x1, qkv2, o2, log2, x2 = kept[l]
        grad, g_ff, s3 = mlp_backward(rows, grad, x2, w, gb[l], me, halves)
        if quick:
            ff = pieces_of(g_ff)
            if late:
                grad = settle(grad, late)
                grad = move(grad, late, me)
                late = [p for p in late if p.step < 3]
        grad, g_space, s2 = space_backward(rows, grad, x1, qkv2, o2, log2, w, gb[l], me, halves)
        if quick:
            space = pieces_of([g_space])
            grad = move(grad, ff, me)
        do1, g_out = middle_backward(rows, grad, y1, o1, w, mixes[l], me, halves, shards)
        do1 = swap_places(do1)
        if quick:
            do1 = move(do1, ff + space + late, me)
        da1, g_time = time_backward(rows, do1, a1, qkv1, log1, w, me, halves)
        if quick:
            da1 = settle(da1, ff + space)
        da1 = swap_places(da1)
        if quick:
            rest = pieces_of([g_out, g_time])
            da1 = move(da1, ff + space + rest, me)
            late = space + rest
        grad, s1 = first_norm_back(rows, da1, x, grad, gb[l])
        norm_rows[l] = jnp.concatenate((s1[0:1], s2[0:1], s3[0:1], s1[1:2], s2[1:2], s3[1:2]), axis=0)
        if quick:
            summed[l] = ff + space + rest
        else:
            summed[l] = [reduce_plain(g_ff + [g_space, g_out, g_time], clip & 1)]
    if quick:
        move((), late, me, True)
        move((), rest, me, True)
        summed = [[p.result for p in some] for some in summed]
    cuts = (2 * g_ff[0][0].shape[0], g_space[0].shape[0], g_out[0].shape[0], g_time[0].shape[0])
    results = []
    for some in summed:
        slabs_of = jnp.concatenate(some, axis=0)
        ends = [sum(cuts[: i + 1]) for i in range(4)]
        results.append([slabs_of[e - c : e] for c, e in zip(cuts, ends)])
    tokens_grad = from_rows(grad)
    norm_sums = reduce_norms(jnp.concatenate(norm_rows, axis=0)).reshape(layers, 2, 3, -1)

    def stacked(form):
        return jnp.stack([form(*results[l]) for l in range(layers)])

    def rows_of(a):
        return a.transpose(1, 0, 2)

    def flat(a):
        return rows_of(a).reshape(a.shape[1], -1)

    def mix_rows(a):
        r, width = a.shape
        return a.reshape(shares, r // shares, width).transpose(1, 0, 2).reshape(r // shares, -1)

    per_share = mlp_in.shape[2] // time_qkv.shape[3]
    return (
        output,
        tokens_grad,
        stacked(lambda ff, s, t, q: rows_of(q)),
        stacked(lambda ff, s, t, q: t[0].T),
        stacked(lambda ff, s, t, q: mix_rows(t[1])),
        stacked(lambda ff, s, t, q: rows_of(s[1:])),
        stacked(lambda ff, s, t, q: s[0].T),
        stacked(lambda ff, s, t, q: flat(ff[:per_share])),
        stacked(lambda ff, s, t, q: flat(ff[per_share:]).T),
        norm_sums[:, 0],
        norm_sums[:, 1],
    )


def solution(mesh):
    token_spec = P(("clip", "head"), "seq", None, None)
    in_specs = (
        token_spec,
        token_spec,
        P(None, ("clip", "seq"), None, "head"),
        P(None, "head", ("clip", "seq")),
        P(None, ("clip", "seq", "head"), None),
        P(None, ("clip", "seq"), None, "head"),
        P(None, "head", ("clip", "seq")),
        P(None, ("clip", "seq"), "head"),
        P(None, "head", ("clip", "seq")),
        P(None, None, ("clip", "seq", "head")),
        P(None, None, ("clip", "seq", "head")),
    )
    return jax.shard_map(
        on_device, mesh=mesh, in_specs=in_specs, out_specs=in_specs, check_vma=False
    )
```

```python
import functools
import math

import jax
import jax.numpy as jnp
from jax import lax
from jax.experimental import pallas as pl
from jax.experimental.pallas import tpu as pltpu
from jax.sharding import PartitionSpec as P

HEAD_DIM = 64
NORM_EPS = 1e-06
HALF_ROOT = 0.7071067811865476
INV_ROOT_TAU = 0.3989422804014327
LOG2E = 1.4426950408889634
FAR = -1e30
LANES = 128
VMEM = 56 * 1024 * 1024
SHOWN = 1.0
ALL = ("clip", "seq", "head")
BF16 = jnp.bfloat16
F32 = jnp.float32


def round_up(value, step):
    return -(-value // step) * step


def nn(a, b):
    return lax.dot_general(a, b, (((1,), (0,)), ((), ())), preferred_element_type=F32)


def nt(a, b):
    return lax.dot_general(a, b, (((1,), (1,)), ((), ())), preferred_element_type=F32)


def tn(a, b):
    return lax.dot_general(a, b, (((0,), (0,)), ((), ())), preferred_element_type=F32)


def norm_parts(x):
    mean = jnp.mean(x, axis=-1, keepdims=True)
    centred = x - mean
    spread = lax.rsqrt(jnp.mean(centred * centred, axis=-1, keepdims=True) + NORM_EPS)
    return centred * spread, spread


def norm_rounded(x, gain, bias):
    hat, _ = norm_parts(x)
    return (hat * gain + bias).astype(BF16)


def norm_back(u, x, gain):
    hat, spread = norm_parts(x)
    scaled = u * gain
    mean_scaled = jnp.mean(scaled, axis=-1, keepdims=True)
    mean_cross = jnp.mean(scaled * hat, axis=-1, keepdims=True)
    change = spread * (scaled - mean_scaled - hat * mean_cross)
    sums = jnp.concatenate(
        (jnp.sum(u * hat, axis=0, keepdims=True), jnp.sum(u, axis=0, keepdims=True)), axis=0
    )
    return change, sums


class Rows:
    def __init__(self, frames, places, ways):
        self.frames = frames
        self.places = places
        self.ways = ways
        self.frame_rows = round_up(places, 16)
        self.rows = frames * self.frame_rows
        self.block = places // ways
        self.chunk = round_up(frames * self.block, 8)
        self.time_rows = ways * self.chunk

    def split(self, r):
        way = jnp.zeros_like(r)
        for k in range(1, self.ways):
            way = way + (r >= k * self.chunk).astype(jnp.int32)
        rest = r - way * self.chunk
        frame = jnp.zeros_like(r)
        for k in range(1, self.frames):
            frame = frame + (rest >= k * self.block).astype(jnp.int32)
        real = rest < self.frames * self.block
        return way, frame, rest - frame * self.block, real

    def to_time(self, k, member):
        r = lax.broadcasted_iota(jnp.int32, (self.chunk, 1), 0)
        _, frame, place, real = self.split(r)
        way = jnp.bitwise_xor(member, k)
        source = jnp.where(real, frame * self.frame_rows + way * self.block + place, -1)
        c = lax.broadcasted_iota(jnp.int32, (self.chunk, self.rows), 1)
        return jnp.where(c == source, 1.0, 0.0).astype(BF16)

    def gathered(self, chunk_refs, member):
        total = tn(self.to_time(0, member), chunk_refs[0][...])
        for k in range(1, self.ways):
            total = total + tn(self.to_time(k, member), chunk_refs[k][...])
        return total

    def chunks(self, width, block=None, index=None):
        return [
            made((self.chunk, width), BF16)
            if block is None
            else made((self.chunk, width), BF16, (self.chunk, block), index)
            for _ in range(self.ways)
        ]

    def time_bias(self):
        def label(r):
            _, _, place, real = self.split(r)
            return jnp.where(real, place, -1)

        a = label(lax.broadcasted_iota(jnp.int32, (self.time_rows, 1), 0))
        b = label(lax.broadcasted_iota(jnp.int32, (1, self.time_rows), 1))
        return jnp.where(a == b, 0.0, FAR).astype(F32)

    def space_bias(self):
        a = lax.broadcasted_iota(jnp.int32, (self.frame_rows, 1), 0)
        return jnp.where(a < self.places, 0.0, FAR).astype(F32)


def lane_masks(rows):
    lane = lax.broadcasted_iota(jnp.int32, (rows, LANES), 1)
    return lane < HEAD_DIM


def one_of(value, low, half):
    zero = jnp.zeros_like(value)
    return jnp.where(low, value, zero) if half == 0 else jnp.where(low, zero, value)


def pair_forward(q, k, v, bias, rate):
    low = lane_masks(q.shape[0])
    mixed, logs = [], []
    for half in range(2):
        s = nt(k, one_of(q, low, half)) + bias
        peak = jnp.max(s, axis=0, keepdims=True)
        e = jnp.exp2((s - peak) * rate)
        total = jnp.sum(e, axis=0, keepdims=True)
        soft = (e * (1.0 / total)).astype(BF16)
        mixed.append(tn(soft, v))
        logs.append(peak * rate + jnp.log2(total))
    return jnp.where(low, mixed[0], mixed[1]).astype(BF16), logs


def pair_backward(q, k, v, do, logs, bias, rate, scale):
    low = lane_masks(q.shape[0])
    dq, dk, dv = [], [], []
    for half in range(2):
        s = nt(k, one_of(q, low, half)) + bias
        soft = jnp.exp2(s * rate - logs[half])
        dp = nt(v, one_of(do, low, half))
        ds = (soft * (dp - jnp.sum(soft * dp, axis=0, keepdims=True))).astype(BF16)
        dv.append(nn(soft.astype(BF16), do))
        dk.append(nn(ds, q))
        dq.append(tn(ds, k))
    return (
        (jnp.where(low, dq[0], dq[1]) * scale).astype(BF16),
        (jnp.where(low, dk[0], dk[1]) * scale).astype(BF16),
        jnp.where(low, dv[0], dv[1]).astype(BF16),
    )


def split_rows(value, keep_ref, send_ref, at, room_ref, me_ref):
    mine = me_ref[0]
    room_ref[...] = value.reshape(room_ref.shape)
    keep_ref[at] = room_ref[:, mine].astype(BF16)
    send_ref[at] = room_ref[:, 1 - mine].astype(BF16)


class Halves:
    def __init__(self, clips, depth, width):
        self.pairs = clips // 2
        self.rows = depth // clips
        self.width = width

    def array(self, lead, block, index):
        tail = (self.pairs, self.rows, self.width)
        one = lambda: made(lead + tail, BF16, block + tail, lambda *g: index(*g) + (0, 0, 0))
        return [one(), one()]

    def room(self):
        return pltpu.VMEM((self.pairs, 2, self.rows, self.width), F32)


SCALARS = pl.BlockSpec(memory_space=pltpu.SMEM)


def call(body, grid, ins, outs, scratch, args, flops=0):
    specs = [spec for spec in ins]
    moved = sum(math.prod(o.shape) * o.dtype.itemsize for o, _ in outs)
    moved += sum(math.prod(a.shape) * a.dtype.itemsize for a in args)
    return pl.pallas_call(
        body,
        out_shape=[shape for shape, _ in outs],
        grid=grid,
        in_specs=specs,
        out_specs=[spec for _, spec in outs],
        scratch_shapes=scratch,
        compiler_params=pltpu.CompilerParams(vmem_limit_bytes=VMEM),
        cost_estimate=pl.CostEstimate(
            flops=int(flops * SHOWN), bytes_accessed=int(moved * SHOWN), transcendentals=0
        ),
    )(*args)


def whole(shape):
    zeros = (0,) * len(shape)
    return pl.BlockSpec(shape, lambda *_: zeros)


def made(shape, dtype, block=None, index=None):
    spec = whole(shape) if block is None else pl.BlockSpec(block, index)
    return jax.ShapeDtypeStruct(shape, dtype), spec


def slabs(count, first, width, depth):
    return pl.BlockSpec((count, 1, depth, width), lambda h, *_: (first // count, h, 0, 0))


def send_first(rows, x, gb, me):
    def body(me_ref, x_ref, gb_ref, *out_refs):
        a = norm_rounded(x_ref[...], gb_ref[0:1], gb_ref[3:4])
        for k in range(rows.ways):
            out_refs[k][...] = nn(rows.to_time(k, me_ref[3]), a).astype(BF16)

    d = x.shape[1]
    return call(
        body, (1,), [SCALARS, whole(x.shape), whole(gb.shape)], rows.chunks(d), [], (me, x, gb)
    )


def time_forward(rows, chunks, w):
    t, d = rows.time_rows, chunks[0].shape[1]
    width = w.shape[3]
    shares = w.shape[1]
    pairs = width // LANES
    ways = rows.ways
    rate = LOG2E / math.sqrt(HEAD_DIM)

    def body(*refs):
        chunk_refs = refs[:ways]
        w_ref, a_ref, qkv_ref, log_ref = refs[ways : ways + 4]
        out_refs = refs[ways + 4 : 2 * ways + 4]
        bias_ref, mixed_ref = refs[2 * ways + 4 :]

        @pl.when(pl.program_id(0) == 0)
        def _():
            bias_ref[...] = rows.time_bias()
            for k in range(ways):
                a_ref[k * rows.chunk : (k + 1) * rows.chunk] = chunk_refs[k][...]

        act = a_ref[...]
        for g in range(3):
            qkv_ref[g] = nn(act, w_ref[g, 0]).astype(BF16)

        @pl.loop(0, pairs)
        def _(i):
            lanes = pl.ds(pl.multiple_of(i * LANES, LANES), LANES)
            mixed, logs = pair_forward(
                qkv_ref[0, :, lanes], qkv_ref[1, :, lanes], qkv_ref[2, :, lanes], bias_ref[...], rate
            )
            mixed_ref[:, lanes] = mixed
            log_ref[0, i] = jnp.concatenate(logs, axis=0)

        for k in range(ways):
            out_refs[k][...] = mixed_ref[k * rows.chunk : (k + 1) * rows.chunk]

    got = call(
        body,
        (shares,),
        [whole(c.shape) for c in chunks] + [slabs(3, 0, width, d)],
        [
            made((t, d), BF16),
            made((3, t, d), BF16, (3, t, width), lambda h: (0, 0, h)),
            made((shares, pairs, 2, t), F32, (1, pairs, 2, t), lambda h: (h, 0, 0, 0)),
            *rows.chunks(d, width, lambda h: (0, h)),
        ],
        [pltpu.VMEM((t, t), F32), pltpu.VMEM((t, width), BF16)],
        (*chunks, w),
        flops=2 * t * d * 3 * d,
    )
    return got[0], got[1], got[2], got[3:]


def middle_forward(rows, back, x, w, mix, gb, me):
    t, d = x.shape
    width = w.shape[3]
    shares = w.shape[1]

    def body(me_ref, *refs):
        x_ref, to_ref, sq_ref, mix_ref, gb_ref, o1_ref, y1_ref, x1_ref, qkv_ref = refs[rows.ways :]
        o1 = rows.gathered(refs[: rows.ways], me_ref[3]).astype(BF16)
        o1_ref[...] = o1
        y1 = jnp.zeros((t, d), F32)
        for h in range(shares):
            y1 = y1 + nt(o1[:, h * width : (h + 1) * width], to_ref[0, h])
        y1 = y1.astype(BF16)
        y1_ref[...] = y1
        x1 = x_ref[...] + nn(y1, mix_ref[...])
        x1_ref[...] = x1
        a2 = norm_rounded(x1, gb_ref[1:2], gb_ref[4:5])
        for g in range(3):
            for h in range(shares):
                qkv_ref[g, :, h * width : (h + 1) * width] = nn(a2, sq_ref[g, h]).astype(BF16)

    return call(
        body,
        (1,),
        [
            SCALARS,
            *(whole(c.shape) for c in back),
            whole(x.shape),
            pl.BlockSpec((1, shares, d, width), lambda i: (6, 0, 0, 0)),
            pl.BlockSpec((3, shares, d, width), lambda i: (1, 0, 0, 0)),
            whole(mix.shape),
            whole(gb.shape),
        ],
        [made((t, d), BF16), made((t, d), BF16), made((t, d), F32), made((3, t, d), BF16)],
        [],
        (me, *back, x, w, w, mix, gb),
        flops=2 * t * d * 5 * d,
    )


def space_forward(rows, qkv, x1, w):
    t, d = x1.shape
    width = w.shape[3]
    shares = w.shape[1]
    pairs = width // LANES
    rate = LOG2E / math.sqrt(HEAD_DIM)
    n = rows.frame_rows

    def body(qkv_ref, x1_ref, w_ref, o2_ref, x2_ref, log_ref):
        bias = rows.space_bias()

        @pl.loop(0, pairs)
        def _(i):
            lanes = pl.ds(pl.multiple_of(i * LANES, LANES), LANES)
            for f in range(rows.frames):
                at = slice(f * n, (f + 1) * n)
                mixed, logs = pair_forward(
                    qkv_ref[0, at, lanes], qkv_ref[1, at, lanes], qkv_ref[2, at, lanes], bias, rate
                )
                o2_ref[at, lanes] = mixed
                log_ref[0, i, f] = jnp.concatenate(logs, axis=0)

        @pl.when(pl.program_id(0) == 0)
        def _():
            x2_ref[...] = x1_ref[...]

        x2_ref[...] += nt(o2_ref[...], w_ref[0, 0])

    return call(
        body,
        (shares,),
        [
            pl.BlockSpec((3, t, width), lambda h: (0, 0, h)),
            whole(x1.shape),
            slabs(1, 7, width, d),
        ],
        [
            made((t, d), BF16, (t, width), lambda h: (0, h)),
            made((t, d), F32),
            made(
                (shares, pairs, rows.frames, 2, n),
                F32,
                (1, pairs, rows.frames, 2, n),
                lambda h: (h, 0, 0, 0, 0),
            ),
        ],
        [],
        (qkv, x1, w),
        flops=2 * t * d * d,
    )


def ff_slab(first, per_share, depth, width):
    return pl.BlockSpec(
        (1, 1, depth, width), lambda j: (first + j % per_share, j // per_share, 0, 0)
    )


def mlp_forward(rows, x2, w, gb, gb_next, me):
    t, d = x2.shape
    width = w.shape[3]
    shares = w.shape[1]
    per_share = (w.shape[0] - 9) // 2
    steps = shares * per_share
    last = gb_next is None

    def body(x2_ref, wi_ref, wo_ref, gb_ref, *rest):
        if last:
            x3_ref, a3_ref = rest
        else:
            me_ref, gn_ref, x3_ref = rest[:3]
            send_refs, a3_ref = rest[3:-1], rest[-1]
        j = pl.program_id(0)

        @pl.when(j == 0)
        def _():
            a3_ref[...] = norm_rounded(x2_ref[...], gb_ref[2:3], gb_ref[5:6])
            x3_ref[...] = x2_ref[...]

        hid = nn(a3_ref[...], wi_ref[0, 0])
        act = (0.5 * hid * (1.0 + lax.erf(hid * HALF_ROOT))).astype(BF16)
        x3_ref[...] += nt(act, wo_ref[0, 0])

        if not last:

            @pl.when(j == steps - 1)
            def _():
                a = norm_rounded(x3_ref[...], gn_ref[0:1], gn_ref[3:4])
                for k in range(rows.ways):
                    send_refs[k][...] = nn(rows.to_time(k, me_ref[3]), a).astype(BF16)

    ins = [
        whole(x2.shape),
        ff_slab(8, per_share, d, width),
        ff_slab(8 + per_share, per_share, d, width),
        whole(gb.shape),
    ]
    outs = [made((t, d), F32)]
    args = [x2, w, w, gb]
    if not last:
        ins += [SCALARS, whole(gb_next.shape)]
        outs += rows.chunks(d)
        args += [me, gb_next]
    return call(
        body, (steps,), ins, outs, [pltpu.VMEM((t, d), BF16)], tuple(args), flops=4 * t * d * width * steps
    )


def mlp_backward(rows, grad, x2, w, gb, me, halves):
    t, d = x2.shape
    width = w.shape[3]
    shares = w.shape[1]
    per_share = (w.shape[0] - 9) // 2
    steps = shares * per_share

    def body(me_ref, g_ref, x2_ref, wi_ref, wo_ref, gb_ref, go_ref, ki_ref, si_ref, ko_ref, so_ref, sums_ref, a3_ref, a3t_ref, e3_ref, e3t_ref, u_ref, room_ref):
        j = pl.program_id(0)

        @pl.when(j == 0)
        def _():
            hat, _ = norm_parts(x2_ref[...])
            a3 = hat * gb_ref[2:3] + gb_ref[5:6]
            a3_ref[...] = a3.astype(BF16)
            a3t_ref[...] = a3.T.astype(BF16)
            g = g_ref[...]
            e3_ref[...] = g.astype(BF16)
            e3t_ref[...] = g.T.astype(BF16)
            u_ref[...] = jnp.zeros((t, d), F32)

        hid = nn(a3_ref[...], wi_ref[0, 0])
        phi = 0.5 * (1.0 + lax.erf(hid * HALF_ROOT))
        act = (hid * phi).astype(BF16)
        slope = phi + hid * jnp.exp(-0.5 * hid * hid) * INV_ROOT_TAU
        dhid = (nn(e3_ref[...], wo_ref[0, 0]) * slope).astype(BF16)
        split_rows(nn(e3t_ref[...], act), ko_ref, so_ref, (0, 0), room_ref, me_ref)
        split_rows(nn(a3t_ref[...], dhid), ki_ref, si_ref, (0, 0), room_ref, me_ref)
        u_ref[...] += nt(dhid, wi_ref[0, 0])

        @pl.when(j == steps - 1)
        def _():
            change, sums = norm_back(u_ref[...], x2_ref[...], gb_ref[2:3])
            go_ref[...] = g_ref[...] + change
            sums_ref[...] = sums

    slab_outs = [
        one
        for _ in range(2)
        for one in halves.array(
            (per_share, shares), (1, 1), lambda j: (j % per_share, j // per_share)
        )
    ]
    grad, ki, si, ko, so, sums = call(
        body,
        (steps,),
        [
            SCALARS,
            whole(grad.shape),
            whole(x2.shape),
            ff_slab(8, per_share, d, width),
            ff_slab(8 + per_share, per_share, d, width),
            whole(gb.shape),
        ],
        [made((t, d), F32), *slab_outs, made((2, d), F32)],
        [
            pltpu.VMEM((t, d), BF16),
            pltpu.VMEM((d, t), BF16),
            pltpu.VMEM((t, d), BF16),
            pltpu.VMEM((d, t), BF16),
            pltpu.VMEM((t, d), F32),
            halves.room(),
        ],
        (me, grad, x2, w, w, gb),
        flops=10 * t * d * width * steps,
    )
    return grad, [(ki, si), (ko, so)], sums


def space_backward(rows, grad, x1, qkv, o2, logs, w, gb, me, halves):
    t, d = x1.shape
    width = w.shape[3]
    shares = w.shape[1]
    pairs = width // LANES
    scale = 1.0 / math.sqrt(HEAD_DIM)
    rate = LOG2E * scale
    n = rows.frame_rows

    def body(me_ref, g_ref, x1_ref, qkv_ref, o2_ref, log_ref, wo_ref, wq_ref, gb_ref, go_ref, keep_ref, send_ref, sums_ref, e2_ref, e2t_ref, a2t_ref, do_ref, dqkv_ref, u_ref, room_ref):
        h = pl.program_id(0)

        @pl.when(h == 0)
        def _():
            g = g_ref[...]
            e2_ref[...] = g.astype(BF16)
            e2t_ref[...] = g.T.astype(BF16)
            hat, _ = norm_parts(x1_ref[...])
            a2t_ref[...] = (hat * gb_ref[1:2] + gb_ref[4:5]).T.astype(BF16)
            u_ref[...] = jnp.zeros((t, d), F32)

        bias = rows.space_bias()
        split_rows(nn(e2t_ref[...], o2_ref[...]), keep_ref, send_ref, (0, 0), room_ref, me_ref)
        do_ref[...] = nn(e2_ref[...], wo_ref[0, 0]).astype(BF16)

        @pl.loop(0, pairs)
        def _(i):
            lanes = pl.ds(pl.multiple_of(i * LANES, LANES), LANES)
            for f in range(rows.frames):
                at = slice(f * n, (f + 1) * n)
                log = log_ref[0, i, f]
                grads = pair_backward(
                    qkv_ref[0, at, lanes],
                    qkv_ref[1, at, lanes],
                    qkv_ref[2, at, lanes],
                    do_ref[at, lanes],
                    (log[0:1], log[1:2]),
                    bias,
                    rate,
                    scale,
                )
                for part in range(3):
                    dqkv_ref[part, at, lanes] = grads[part]

        for part in range(3):
            split_rows(
                nn(a2t_ref[...], dqkv_ref[part]), keep_ref, send_ref, (part + 1, 0), room_ref, me_ref
            )
            u_ref[...] += nt(dqkv_ref[part], wq_ref[part, 0])

        @pl.when(h == shares - 1)
        def _():
            change, sums = norm_back(u_ref[...], x1_ref[...], gb_ref[1:2])
            go_ref[...] = g_ref[...] + change
            sums_ref[...] = sums

    grad, keep, send, sums = call(
        body,
        (shares,),
        [
            SCALARS,
            whole(grad.shape),
            whole(x1.shape),
            pl.BlockSpec((3, t, width), lambda h: (0, 0, h)),
            pl.BlockSpec((t, width), lambda h: (0, h)),
            pl.BlockSpec((1,) + logs.shape[1:], lambda h: (h, 0, 0, 0, 0)),
            slabs(1, 7, width, d),
            slabs(3, 3, width, d),
            whole(gb.shape),
        ],
        [
            made((t, d), F32),
            *halves.array((4, shares), (4, 1), lambda h: (0, h)),
            made((2, d), F32),
        ],
        [
            pltpu.VMEM((t, d), BF16),
            pltpu.VMEM((d, t), BF16),
            pltpu.VMEM((d, t), BF16),
            pltpu.VMEM((t, width), BF16),
            pltpu.VMEM((3, t, width), BF16),
            pltpu.VMEM((t, d), F32),
            halves.room(),
        ],
        (me, grad, x1, qkv, o2, logs, w, w, gb),
        flops=2 * t * d * d * 8,
    )
    return grad, (keep, send), sums


def mix_fits(depth, shards, shares):
    return depth // (shards * shares) % 8 == 0


def middle_backward(rows, grad, y1, o1, w, mix, me, halves, shards):
    t, d = grad.shape
    width = w.shape[3]
    shares = w.shape[1]
    fits = mix_fits(d, shards, shares)
    part = d // (shards * shares)

    def body(me_ref, g_ref, y1_ref, o1_ref, to_ref, mix_ref, *rest):
        send_refs, rest = rest[: rows.ways], rest[rows.ways :]
        gk_ref, gs_ref, *rest = rest
        if fits:
            room_ref, order_ref = rest
        else:
            gm_ref, room_ref = rest
        e1 = g_ref[...].astype(BF16)
        dy1 = nt(e1, mix_ref[...]).astype(BF16)
        sends = [rows.to_time(k, me_ref[3]) for k in range(rows.ways)]
        for h in range(shares):
            lanes = slice(h * width, (h + 1) * width)
            do1 = nn(dy1, to_ref[0, h]).astype(BF16)
            for k in range(rows.ways):
                send_refs[k][:, lanes] = nn(sends[k], do1).astype(BF16)
            split_rows(tn(dy1, o1_ref[:, lanes]), gk_ref, gs_ref, (0, h), room_ref, me_ref)
        gm = tn(y1_ref[...], e1)
        if fits:
            gm = gm.reshape(shards, shares, part, d)
            for h in range(shares):
                for half in range(shares):
                    order_ref[:, half] = gm[:, h, :, half * width : (half + 1) * width]
                split_rows(order_ref[...], gk_ref, gs_ref, (1, h), room_ref, me_ref)
        else:
            gm_ref[...] = gm.astype(BF16)

    outs = rows.chunks(d)
    outs += halves.array((1 + fits, shares), (1 + fits, shares), lambda i: (0, 0))
    scratch = [halves.room()]
    if fits:
        scratch.append(pltpu.VMEM((shards, shares, part, width), F32))
    else:
        outs.append(made((d, d), BF16))
    got = call(
        body,
        (1,),
        [
            SCALARS,
            whole(grad.shape),
            whole(y1.shape),
            whole(o1.shape),
            pl.BlockSpec((1, shares, d, width), lambda i: (6, 0, 0, 0)),
            whole(mix.shape),
        ],
        outs,
        scratch,
        (me, grad, y1, o1, w, mix),
        flops=8 * t * d * d,
    )
    do1, (keep, send) = got[: rows.ways], got[rows.ways : rows.ways + 2]
    if not fits:
        gm = mix_slab(got[-1], shards, shares).reshape((1, shares, halves.pairs, 2) + keep.shape[3:])
        keep = jnp.concatenate((keep, lax.dynamic_index_in_dim(gm, me[0], 3, keepdims=False)), axis=0)
        send = jnp.concatenate((send, lax.dynamic_index_in_dim(gm, 1 - me[0], 3, keepdims=False)), axis=0)
    return do1, (keep, send)


def time_backward(rows, do1, a, qkv, logs, w, me, halves):
    t, d = a.shape
    width = w.shape[3]
    shares = w.shape[1]
    pairs = width // LANES
    scale = 1.0 / math.sqrt(HEAD_DIM)
    rate = LOG2E * scale

    def body(me_ref, *refs):
        do_refs, refs = refs[: rows.ways], refs[rows.ways :]
        a_ref, qkv_ref, log_ref, w_ref = refs[:4]
        out_refs, refs = refs[4 : 4 + rows.ways], refs[4 + rows.ways :]
        keep_ref, send_ref, bias_ref, dqkv_ref, at_ref, u_ref, room_ref, do_ref = refs
        h = pl.program_id(0)

        @pl.when(h == 0)
        def _():
            bias_ref[...] = rows.time_bias()
            at_ref[...] = a_ref[...].T
            u_ref[...] = jnp.zeros((t, d), F32)

        for k in range(rows.ways):
            do_ref[k * rows.chunk : (k + 1) * rows.chunk] = do_refs[k][...]

        @pl.loop(0, pairs)
        def _(i):
            lanes = pl.ds(pl.multiple_of(i * LANES, LANES), LANES)
            log = log_ref[0, i]
            grads = pair_backward(
                qkv_ref[0, :, lanes],
                qkv_ref[1, :, lanes],
                qkv_ref[2, :, lanes],
                do_ref[:, lanes],
                (log[0:1], log[1:2]),
                bias_ref[...],
                rate,
                scale,
            )
            for part in range(3):
                dqkv_ref[part, :, lanes] = grads[part]

        for part in range(3):
            split_rows(
                nn(at_ref[...], dqkv_ref[part]), keep_ref, send_ref, (part, 0), room_ref, me_ref
            )
            u_ref[...] += nt(dqkv_ref[part], w_ref[part, 0])

        @pl.when(h == shares - 1)
        def _():
            for k in range(rows.ways):
                out_refs[k][...] = u_ref[k * rows.chunk : (k + 1) * rows.chunk].astype(BF16)

    got = call(
        body,
        (shares,),
        [
            SCALARS,
            *(pl.BlockSpec((rows.chunk, width), lambda h: (0, h)) for _ in do1),
            whole(a.shape),
            pl.BlockSpec((3, t, width), lambda h: (0, 0, h)),
            pl.BlockSpec((1,) + logs.shape[1:], lambda h: (h, 0, 0, 0)),
            slabs(3, 0, width, d),
        ],
        [
            *rows.chunks(d),
            *halves.array((3, shares), (3, 1), lambda h: (0, h)),
        ],
        [
            pltpu.VMEM((t, t), F32),
            pltpu.VMEM((3, t, width), BF16),
            pltpu.VMEM((d, t), BF16),
            pltpu.VMEM((t, d), F32),
            halves.room(),
            pltpu.VMEM((t, width), BF16),
        ],
        (me, *do1, a, qkv, logs, w),
        flops=2 * t * d * d * 6,
    )
    return got[: rows.ways], tuple(got[rows.ways :])


def first_norm_back(rows, back, x, grad, gb, me):
    t, d = x.shape

    def body(me_ref, *refs):
        x_ref, g_ref, gb_ref, go_ref, sums_ref = refs[rows.ways :]
        u = rows.gathered(refs[: rows.ways], me_ref[3])
        change, sums = norm_back(u, x_ref[...], gb_ref[0:1])
        go_ref[...] = g_ref[...] + change
        sums_ref[...] = sums

    return call(
        body,
        (1,),
        [SCALARS, *(whole(c.shape) for c in back), whole(x.shape), whole(grad.shape), whole(gb.shape)],
        [made((t, d), F32), made((2, d), F32)],
        [],
        (me, *back, x, grad, gb),
    )


def homes():
    clips, ways = lax.axis_size("clip"), lax.axis_size("seq")
    pairs = []
    for clip in range(clips):
        for seq in range(ways):
            home_clip = clip - clip % 2 + seq % 2
            home_seq = seq // 2 + (ways // 2) * (clip % 2)
            pairs.append((clip * ways + seq, home_clip * ways + home_seq))
    return pairs


def go_home(a):
    return lax.ppermute(a, ("clip", "seq"), homes())


def go_back(a):
    return lax.ppermute(a, ("clip", "seq"), [(home, device) for device, home in homes()])


def member_of(clip, seq):
    return clip % 2 + 2 * (seq % (lax.axis_size("seq") // 2))


def swap_places(chunks):
    clips, ways = lax.axis_size("clip"), lax.axis_size("seq")
    got = [chunks[0]]
    for k in range(1, ways):
        pairs = []
        for clip in range(clips):
            for seq in range(ways):
                other = member_of(clip, seq) ^ k
                to_clip = clip - clip % 2 + other % 2
                to_seq = seq - seq % (ways // 2) + other // 2
                pairs.append((clip * ways + seq, to_clip * ways + to_seq))
        got.append(lax.ppermute(chunks[k], ("clip", "seq"), pairs))
    return got


def pack_layer(time_qkv, time_out, time_mix, space_qkv, space_out, mlp_in, mlp_out):
    width = time_qkv.shape[2]
    r = time_qkv.shape[0]
    halves = time_mix.shape[1] // width

    def columns(a):
        return a.reshape(r, -1, width).transpose(1, 0, 2)

    mix = time_mix.reshape(-1, halves, width).transpose(1, 0, 2).reshape(1, r, width)
    return jnp.concatenate(
        (
            columns(time_qkv),
            columns(space_qkv),
            time_out.T[None],
            space_out.T[None],
            columns(mlp_in),
            columns(mlp_out.T),
            mix,
        ),
        axis=0,
    )


def gather_slabs(pack):
    full = lax.all_gather(pack, ("head", "clip", "seq"), axis=1, tiled=True)
    return full.reshape(pack.shape[0], lax.axis_size("head"), -1, pack.shape[2])


def mix_whole(slab, shards):
    shares, depth, width = slab.shape
    part = slab.reshape(shares, shards, shares, depth // (shards * shares), width)
    return part.transpose(1, 0, 3, 2, 4).reshape(depth, shares * width)


def mix_slab(whole_grad, shards, shares):
    depth, full = whole_grad.shape
    width = full // shares
    part = whole_grad.reshape(shards, shares, depth // (shards * shares), shares, width)
    return part.transpose(1, 0, 3, 2, 4).reshape(1, shares, depth, width)


class Piece:
    def __init__(self, keep, got, first, n, order):
        self.near = (keep, got)
        self.first = first
        self.n = n
        self.order = order
        self.step = 0
        self.held = []
        self.result = None


PLACE = {"x": 1, "h": 2}


def fold(pieces, me, last_by_rows):
    ways = lax.axis_size("seq")
    depth, width = pieces[0].near[0].shape[-2:]
    r = depth // ways
    used = {}
    arrays = []

    def number(a):
        for i, known in enumerate(arrays):
            if known is a:
                return i
        arrays.append(a)
        return len(arrays) - 1

    plans = []
    for p in pieces:
        link = p.order[p.step] if p.step < 2 else "z"
        blocks = p.n * (2 if p.step == 0 else 1)
        base = used.get(link, 0)
        used[link] = base + blocks
        near = [number(a) for a in p.near]
        held = [(number(a), at) for a, at in p.held]
        plans.append((p, link, base, near, held))
    links = sorted(used)
    shapes = [
        (ways, used[k], r, width) if k == "z" and last_by_rows else (used[k], depth, width)
        for k in links
    ]
    rooms, counts = [], []
    for p, link, base, near, held in plans:
        each = 2 if p.step == 0 else 1
        counts.append((each, len(near) + len(held)))
        rooms += [(each * p.n, depth, width)] * (len(near) + len(held))
    copies_needed = sum(each * terms for each, terms in counts)

    def body(me_ref, *refs):
        sources = refs[: len(arrays)]
        outs = dict(zip(links, refs[len(arrays) : len(arrays) + len(links)]))
        held_refs = refs[len(arrays) + len(links) : -1]
        sems = refs[-1]
        mine = {name: me_ref[PLACE[name]] for name in PLACE}
        groups = []
        room = 0
        sem = 0
        for p, link, base, near, held in plans:
            group = []
            if p.step == 0:
                for term in near:
                    for k in range(2):
                        pick = {p.order[0]: 1 - mine[p.order[0]], p.order[1]: k}
                        source = sources[term].at[pl.ds(p.first, p.n), pick["h"], pick["x"]]
                        group.append((source, held_refs[room].at[pl.ds(k * p.n, p.n)]))
                    room += 1
            else:
                last = p.order[1]
                pick = {p.order[0]: mine[p.order[0]]}
                pick[last] = 1 - mine[last] if p.step == 1 else mine[last]
                for term in near:
                    source = sources[term].at[pl.ds(p.first, p.n), pick["h"], pick["x"]]
                    group.append((source, held_refs[room]))
                    room += 1
                for i, (term, at) in enumerate(held):
                    start = at + pick[last] * p.n if i == 0 else at
                    group.append((sources[term].at[pl.ds(start, p.n)], held_refs[room]))
                    room += 1
            made_copies = []
            for source, target in group:
                made_copies.append(pltpu.make_async_copy(source, target, sems.at[sem]))
                sem += 1
            groups.append(made_copies)
        for group in groups:
            for copy in group:
                copy.start()
        room = 0
        for (p, link, base, near, held), (each, terms), group in zip(plans, counts, groups):
            these = held_refs[room : room + terms]
            room += terms
            for copy in group:
                copy.wait()

            @pl.loop(0, each * p.n)
            def _(i, these=these, base=base, out=outs[link], last=p.step == 2 and last_by_rows):
                value = these[0][i].astype(F32)
                for one in these[1:]:
                    value = value + one[i].astype(F32)
                value = value.astype(BF16)
                if last:
                    for k in range(ways):
                        out[k, base + i] = value[k * r : (k + 1) * r]
                else:
                    out[base + i] = value

    moved = sum(2 * math.prod(room) for room in rooms) + sum(2 * math.prod(shape) for shape in shapes)
    sums = pl.pallas_call(
        body,
        out_shape=[jax.ShapeDtypeStruct(shape, BF16) for shape in shapes],
        in_specs=[SCALARS] + [pl.BlockSpec(memory_space=pltpu.HBM)] * len(arrays),
        out_specs=[pl.BlockSpec(memory_space=pltpu.VMEM)] * len(links),
        scratch_shapes=[pltpu.VMEM(room, BF16) for room in rooms]
        + [pltpu.SemaphoreType.DMA((copies_needed,))],
        compiler_params=pltpu.CompilerParams(vmem_limit_bytes=VMEM),
        cost_estimate=pl.CostEstimate(flops=0, bytes_accessed=moved, transcendentals=0),
    )(me, *arrays)
    return [(p, link, base) for p, link, base, _, _ in plans], dict(zip(links, sums))


def cross(a, name):
    axis, bit = ("head", 0) if name == "h" else ("clip", 1 if name == "x" else 0)
    size = lax.axis_size(axis)
    return lax.ppermute(a, axis, [(i, i ^ (1 << bit)) for i in range(size)])


def pieces_of(halves_of):
    total = sum(keep.shape[0] for keep, _ in halves_of)
    found = []
    seen = 0
    for keep, send in halves_of:
        got = cross(send, "c")
        n = keep.shape[0]
        first = min(max((total + 1) // 2 - seen, 0), n)
        if first:
            found.append(Piece(keep, got, 0, first, ("x", "h")))
        if n > first:
            found.append(Piece(keep, got, first, n - first, ("h", "x")))
        seen += n
    return found


def move(x, pieces, me, at_end=False):
    plans, sums = fold(pieces, me, at_end)
    x, sums = lax.optimization_barrier((x, sums))
    got = {}
    for link, array in sums.items():
        if link == "z":
            if at_end:
                every = lax.all_to_all(array, "seq", split_axis=0, concat_axis=0, tiled=True)
                got[link] = jnp.sum(every.astype(F32), axis=0)
            else:
                own = lax.psum_scatter(array, "seq", scatter_dimension=1, tiled=True)
                got[link] = own.astype(F32)
        else:
            got[link] = cross(array, link)
    for p, link, base in plans:
        if link == "z":
            p.result = got[link][base : base + p.n]
        else:
            p.held.append((got[link], base))
        p.step += 1
    return x


def settle(x, pieces):
    arrays = []
    for p in pieces:
        if not any(p.held[-1][0] is a for a in arrays):
            arrays.append(p.held[-1][0])
    x, came = lax.optimization_barrier((x, arrays))
    for p in pieces:
        for old, new in zip(arrays, came):
            if p.held[-1][0] is old:
                p.held[-1] = (new, p.held[-1][1])
                break
    return x


def reduce_plain(halves_of, core):
    def joined(keep, send):
        low = jnp.where(core == 0, keep, send)
        high = jnp.where(core == 0, send, keep)
        n, shares, pairs, depth, width = keep.shape
        return jnp.stack((low, high), axis=3).reshape(n, shares, 2 * pairs * depth, width)

    g = jnp.concatenate([joined(*pair) for pair in halves_of], axis=0)
    g = lax.psum_scatter(g, "head", scatter_dimension=1, tiled=True)
    g = lax.psum_scatter(g.astype(F32), ("clip", "seq"), scatter_dimension=2, tiled=True)
    return g[:, 0]


def gather_norms(gain, bias):
    layers, norms, part = gain.shape
    both = jnp.concatenate((gain, bias), axis=1).reshape(1, -1)
    count = lax.axis_size("clip") * lax.axis_size("seq") * lax.axis_size("head")
    width = round_up(both.shape[1], 128)
    padded = jnp.pad(both, ((0, 0), (0, width - both.shape[1])))
    every = lax.all_to_all(
        jnp.broadcast_to(padded, (count, width)), ALL, split_axis=0, concat_axis=0, tiled=True
    )[:, : both.shape[1]]
    return every.reshape(count, layers * 2 * norms, part).transpose(1, 0, 2).reshape(layers, 2 * norms, -1)


def reduce_norms(sums):
    count = lax.axis_size("clip") * lax.axis_size("seq") * lax.axis_size("head")
    rows, features = sums.shape
    part = features // count
    a = sums.reshape(rows, count, part).transpose(1, 0, 2).reshape(count, rows * part)
    width = round_up(rows * part, 128)
    a = jnp.pad(a, ((0, 0), (0, width - rows * part)))
    every = lax.all_to_all(a, ALL, split_axis=0, concat_axis=0, tiled=True)
    return jnp.sum(every, axis=0)[: rows * part].reshape(rows, part)


def on_device(
    tokens,
    cotangent,
    time_qkv,
    time_out,
    time_mix,
    space_qkv,
    space_out,
    mlp_in,
    mlp_out,
    norm_gain,
    norm_bias,
):
    layers = time_qkv.shape[0]
    clips, frames, places, d = tokens.shape
    ways = lax.axis_size("seq")
    shards = lax.axis_size("clip") * ways
    rows = Rows(clips * frames, places, ways)
    shares = lax.axis_size("head")

    def as_rows(a):
        a = a.astype(F32).reshape(rows.frames, places, d)
        a = jnp.pad(a, ((0, 0), (0, rows.frame_rows - places), (0, 0)))
        return a.reshape(rows.rows, d)

    def from_rows(a):
        a = a.reshape(rows.frames, rows.frame_rows, d)[:, :places]
        return a.reshape(tokens.shape)

    gbs = gather_norms(norm_gain, norm_bias)
    gb = [gbs[l] for l in range(layers)]
    weights = [
        gather_slabs(
            pack_layer(
                time_qkv[l], time_out[l], time_mix[l], space_qkv[l], space_out[l], mlp_in[l], mlp_out[l]
            )
        )
        for l in range(layers)
    ]
    mixes = [mix_whole(w[-1], shards) for w in weights]

    halves = Halves(lax.axis_size("clip"), d, time_qkv.shape[3])
    clip = lax.axis_index("clip")
    member = member_of(clip, lax.axis_index("seq"))
    me = jnp.stack((clip & 1, (clip >> 1) & 1, lax.axis_index("head"), member)).astype(jnp.int32)

    x = as_rows(go_home(tokens))
    send = send_first(rows, x, gb[0], me)
    kept = []
    for l in range(layers):
        w = weights[l]
        a1, qkv1, log1, o1_time = time_forward(rows, swap_places(send), w)
        back = swap_places(o1_time)
        o1, y1, x1, qkv2 = middle_forward(rows, back, x, w, mixes[l], gb[l], me)
        o2, x2, log2 = space_forward(rows, qkv2, x1, w)
        kept.append((x, a1, qkv1, log1, o1, y1, x1, qkv2, o2, log2, x2))
        if l + 1 < layers:
            x, *send = mlp_forward(rows, x2, w, gb[l], gb[l + 1], me)
        else:
            (x,) = mlp_forward(rows, x2, w, gb[l], None, me)
    output = go_back(from_rows(x.astype(BF16)))

    grad = as_rows(go_home(cotangent))
    norm_rows = [None] * layers
    summed = [None] * layers
    late = []
    quick = lax.axis_size("clip") == 4 and shares == 2 and time_qkv.shape[1] % 16 == 0
    for l in reversed(range(layers)):
        w = weights[l]
        x, a1, qkv1, log1, o1, y1, x1, qkv2, o2, log2, x2 = kept[l]
        grad, g_ff, s3 = mlp_backward(rows, grad, x2, w, gb[l], me, halves)
        if quick:
            ff = pieces_of(g_ff)
            if late:
                grad = settle(grad, late)
                grad = move(grad, late, me)
                late = [p for p in late if p.step < 3]
        grad, g_space, s2 = space_backward(rows, grad, x1, qkv2, o2, log2, w, gb[l], me, halves)
        if quick:
            space = pieces_of([g_space])
            grad = move(grad, ff, me)
        do1, g_out = middle_backward(rows, grad, y1, o1, w, mixes[l], me, halves, shards)
        do1 = swap_places(do1)
        if quick:
            do1 = move(do1, ff + space + late, me)
        da1, g_time = time_backward(rows, do1, a1, qkv1, log1, w, me, halves)
        if quick:
            da1 = settle(da1, ff + space)
        da1 = swap_places(da1)
        if quick:
            rest = pieces_of([g_out, g_time])
            da1 = move(da1, ff + space + rest, me)
            late = space + rest
        grad, s1 = first_norm_back(rows, da1, x, grad, gb[l], me)
        norm_rows[l] = jnp.concatenate((s1[0:1], s2[0:1], s3[0:1], s1[1:2], s2[1:2], s3[1:2]), axis=0)
        if quick:
            summed[l] = ff + space + rest
        else:
            summed[l] = [reduce_plain(g_ff + [g_space, g_out, g_time], clip & 1)]
    if quick:
        move((), late, me, True)
        move((), rest, me, True)
        summed = [[p.result for p in some] for some in summed]
    cuts = (2 * g_ff[0][0].shape[0], g_space[0].shape[0], g_out[0].shape[0], g_time[0].shape[0])
    results = []
    for some in summed:
        slabs_of = jnp.concatenate(some, axis=0)
        ends = [sum(cuts[: i + 1]) for i in range(4)]
        results.append([slabs_of[e - c : e] for c, e in zip(cuts, ends)])
    tokens_grad = go_back(from_rows(grad.astype(BF16))).astype(F32)
    norm_sums = reduce_norms(jnp.concatenate(norm_rows, axis=0)).reshape(layers, 2, 3, -1)

    def stacked(form):
        return jnp.stack([form(*results[l]) for l in range(layers)])

    def rows_of(a):
        return a.transpose(1, 0, 2)

    def flat(a):
        return rows_of(a).reshape(a.shape[1], -1)

    def mix_rows(a):
        r, width = a.shape
        return a.reshape(shares, r // shares, width).transpose(1, 0, 2).reshape(r // shares, -1)

    per_share = mlp_in.shape[2] // time_qkv.shape[3]
    return (
        output,
        tokens_grad,
        stacked(lambda ff, s, t, q: rows_of(q)),
        stacked(lambda ff, s, t, q: t[0].T),
        stacked(lambda ff, s, t, q: mix_rows(t[1])),
        stacked(lambda ff, s, t, q: rows_of(s[1:])),
        stacked(lambda ff, s, t, q: s[0].T),
        stacked(lambda ff, s, t, q: flat(ff[:per_share])),
        stacked(lambda ff, s, t, q: flat(ff[per_share:]).T),
        norm_sums[:, 0],
        norm_sums[:, 1],
    )


def solution(mesh):
    token_spec = P(("clip", "head"), "seq", None, None)
    in_specs = (
        token_spec,
        token_spec,
        P(None, ("clip", "seq"), None, "head"),
        P(None, "head", ("clip", "seq")),
        P(None, ("clip", "seq", "head"), None),
        P(None, ("clip", "seq"), None, "head"),
        P(None, "head", ("clip", "seq")),
        P(None, ("clip", "seq"), "head"),
        P(None, "head", ("clip", "seq")),
        P(None, None, ("clip", "seq", "head")),
        P(None, None, ("clip", "seq", "head")),
    )
    return jax.shard_map(
        on_device, mesh=mesh, in_specs=in_specs, out_specs=in_specs, check_vma=False
    )
```

```python
import functools
import math

import jax
import jax.numpy as jnp
from jax import lax
from jax.experimental import pallas as pl
from jax.experimental.pallas import tpu as pltpu
from jax.sharding import PartitionSpec as P

HEAD_DIM = 64
NORM_EPS = 1e-06
HALF_ROOT = 0.7071067811865476
INV_ROOT_TAU = 0.3989422804014327
LOG2E = 1.4426950408889634
FAR = -1e30
LANES = 128
VMEM = 56 * 1024 * 1024
SHOWN = 1.0
ALL = ("clip", "seq", "head")
BF16 = jnp.bfloat16
F32 = jnp.float32


def round_up(value, step):
    return -(-value // step) * step


def nn(a, b):
    return lax.dot_general(a, b, (((1,), (0,)), ((), ())), preferred_element_type=F32)


def nt(a, b):
    return lax.dot_general(a, b, (((1,), (1,)), ((), ())), preferred_element_type=F32)


def tn(a, b):
    return lax.dot_general(a, b, (((0,), (0,)), ((), ())), preferred_element_type=F32)


def norm_parts(x):
    mean = jnp.mean(x, axis=-1, keepdims=True)
    centred = x - mean
    spread = lax.rsqrt(jnp.mean(centred * centred, axis=-1, keepdims=True) + NORM_EPS)
    return centred * spread, spread


def norm_rounded(x, gain, bias):
    hat, _ = norm_parts(x)
    return (hat * gain + bias).astype(BF16)


def norm_back(u, x, gain):
    hat, spread = norm_parts(x)
    scaled = u * gain
    mean_scaled = jnp.mean(scaled, axis=-1, keepdims=True)
    mean_cross = jnp.mean(scaled * hat, axis=-1, keepdims=True)
    change = spread * (scaled - mean_scaled - hat * mean_cross)
    sums = jnp.concatenate(
        (jnp.sum(u * hat, axis=0, keepdims=True), jnp.sum(u, axis=0, keepdims=True)), axis=0
    )
    return change, sums


class Rows:
    def __init__(self, frames, places, ways):
        self.frames = frames
        self.places = places
        self.ways = ways
        self.frame_rows = round_up(places, 16)
        self.rows = frames * self.frame_rows
        self.block = places // ways
        self.chunk = round_up(frames * self.block, 8)
        self.time_rows = ways * self.chunk

    def split(self, r):
        way = jnp.zeros_like(r)
        for k in range(1, self.ways):
            way = way + (r >= k * self.chunk).astype(jnp.int32)
        rest = r - way * self.chunk
        frame = jnp.zeros_like(r)
        for k in range(1, self.frames):
            frame = frame + (rest >= k * self.block).astype(jnp.int32)
        real = rest < self.frames * self.block
        return way, frame, rest - frame * self.block, real

    def to_time(self, k, member):
        r = lax.broadcasted_iota(jnp.int32, (self.chunk, 1), 0)
        _, frame, place, real = self.split(r)
        way = jnp.bitwise_xor(member, k)
        source = jnp.where(real, frame * self.frame_rows + way * self.block + place, -1)
        c = lax.broadcasted_iota(jnp.int32, (self.chunk, self.rows), 1)
        return jnp.where(c == source, 1.0, 0.0).astype(BF16)

    def gathered(self, chunk_refs, member):
        total = tn(self.to_time(0, member), chunk_refs[0][...])
        for k in range(1, self.ways):
            total = total + tn(self.to_time(k, member), chunk_refs[k][...])
        return total

    def chunks(self, width, block=None, index=None):
        return [
            made((self.chunk, width), BF16)
            if block is None
            else made((self.chunk, width), BF16, (self.chunk, block), index)
            for _ in range(self.ways)
        ]

    def time_bias(self):
        def label(r):
            _, _, place, real = self.split(r)
            return jnp.where(real, place, -1)

        a = label(lax.broadcasted_iota(jnp.int32, (self.time_rows, 1), 0))
        b = label(lax.broadcasted_iota(jnp.int32, (1, self.time_rows), 1))
        return jnp.where(a == b, 0.0, FAR).astype(F32)

    def space_bias(self):
        a = lax.broadcasted_iota(jnp.int32, (self.frame_rows, 1), 0)
        return jnp.where(a < self.places, 0.0, FAR).astype(F32)


def lane_masks(rows):
    lane = lax.broadcasted_iota(jnp.int32, (rows, LANES), 1)
    return lane < HEAD_DIM


def one_of(value, low, half):
    zero = jnp.zeros_like(value)
    return jnp.where(low, value, zero) if half == 0 else jnp.where(low, zero, value)


def pair_forward(q, k, v, bias, rate):
    low = lane_masks(q.shape[0])
    mixed, logs = [], []
    for half in range(2):
        s = nt(k, one_of(q, low, half)) + bias
        peak = jnp.max(s, axis=0, keepdims=True)
        e = jnp.exp2((s - peak) * rate)
        total = jnp.sum(e, axis=0, keepdims=True)
        soft = (e * (1.0 / total)).astype(BF16)
        mixed.append(tn(soft, v))
        logs.append(peak * rate + jnp.log2(total))
    return jnp.where(low, mixed[0], mixed[1]).astype(BF16), logs


def pair_backward(q, k, v, do, logs, bias, rate, scale):
    low = lane_masks(q.shape[0])
    dq, dk, dv = [], [], []
    for half in range(2):
        s = nt(k, one_of(q, low, half)) + bias
        soft = jnp.exp2(s * rate - logs[half])
        dp = nt(v, one_of(do, low, half))
        ds = (soft * (dp - jnp.sum(soft * dp, axis=0, keepdims=True))).astype(BF16)
        dv.append(nn(soft.astype(BF16), do))
        dk.append(nn(ds, q))
        dq.append(tn(ds, k))
    return (
        (jnp.where(low, dq[0], dq[1]) * scale).astype(BF16),
        (jnp.where(low, dk[0], dk[1]) * scale).astype(BF16),
        jnp.where(low, dv[0], dv[1]).astype(BF16),
    )


def split_rows(value, keep_ref, send_ref, at, room_ref, me_ref):
    mine = me_ref[0]
    room_ref[...] = value.reshape(room_ref.shape)
    keep_ref[at] = room_ref[:, mine].astype(BF16)
    send_ref[at] = room_ref[:, 1 - mine].astype(BF16)


class Halves:
    def __init__(self, clips, depth, width):
        self.pairs = clips // 2
        self.rows = depth // clips
        self.width = width

    def array(self, lead, block, index):
        tail = (self.pairs, self.rows, self.width)
        one = lambda: made(lead + tail, BF16, block + tail, lambda *g: index(*g) + (0, 0, 0))
        return [one(), one()]

    def room(self):
        return pltpu.VMEM((self.pairs, 2, self.rows, self.width), F32)


SCALARS = pl.BlockSpec(memory_space=pltpu.SMEM)


def call(body, grid, ins, outs, scratch, args, flops=0):
    specs = [spec for spec in ins]
    moved = sum(math.prod(o.shape) * o.dtype.itemsize for o, _ in outs)
    moved += sum(math.prod(a.shape) * a.dtype.itemsize for a in args)
    return pl.pallas_call(
        body,
        out_shape=[shape for shape, _ in outs],
        grid=grid,
        in_specs=specs,
        out_specs=[spec for _, spec in outs],
        scratch_shapes=scratch,
        compiler_params=pltpu.CompilerParams(vmem_limit_bytes=VMEM),
        cost_estimate=pl.CostEstimate(
            flops=int(flops * SHOWN), bytes_accessed=int(moved * SHOWN), transcendentals=0
        ),
    )(*args)


def whole(shape):
    zeros = (0,) * len(shape)
    return pl.BlockSpec(shape, lambda *_: zeros)


def made(shape, dtype, block=None, index=None):
    spec = whole(shape) if block is None else pl.BlockSpec(block, index)
    return jax.ShapeDtypeStruct(shape, dtype), spec


def slabs(count, first, width, depth):
    return pl.BlockSpec((count, 1, depth, width), lambda h, *_: (first // count, h, 0, 0))


def send_first(rows, x, gb, me):
    def body(me_ref, x_ref, gb_ref, *out_refs):
        a = norm_rounded(x_ref[...], gb_ref[0:1], gb_ref[3:4])
        for k in range(rows.ways):
            out_refs[k][...] = nn(rows.to_time(k, me_ref[3]), a).astype(BF16)

    d = x.shape[1]
    return call(
        body, (1,), [SCALARS, whole(x.shape), whole(gb.shape)], rows.chunks(d), [], (me, x, gb)
    )


def time_forward(rows, chunks, w):
    t, d = rows.time_rows, chunks[0].shape[1]
    width = w.shape[3]
    shares = w.shape[1]
    pairs = width // LANES
    ways = rows.ways
    rate = LOG2E / math.sqrt(HEAD_DIM)

    def body(*refs):
        chunk_refs = refs[:ways]
        w_ref, a_ref, qkv_ref, log_ref = refs[ways : ways + 4]
        out_refs = refs[ways + 4 : 2 * ways + 4]
        bias_ref, mixed_ref = refs[2 * ways + 4 :]

        @pl.when(pl.program_id(0) == 0)
        def _():
            bias_ref[...] = rows.time_bias()
            for k in range(ways):
                a_ref[k * rows.chunk : (k + 1) * rows.chunk] = chunk_refs[k][...]

        act = a_ref[...]
        for g in range(3):
            qkv_ref[g] = nn(act, w_ref[g, 0]).astype(BF16)

        @pl.loop(0, pairs)
        def _(i):
            lanes = pl.ds(pl.multiple_of(i * LANES, LANES), LANES)
            mixed, logs = pair_forward(
                qkv_ref[0, :, lanes], qkv_ref[1, :, lanes], qkv_ref[2, :, lanes], bias_ref[...], rate
            )
            mixed_ref[:, lanes] = mixed
            log_ref[0, i] = jnp.concatenate(logs, axis=0)

        for k in range(ways):
            out_refs[k][...] = mixed_ref[k * rows.chunk : (k + 1) * rows.chunk]

    got = call(
        body,
        (shares,),
        [whole(c.shape) for c in chunks] + [slabs(3, 0, width, d)],
        [
            made((t, d), BF16),
            made((3, t, d), BF16, (3, t, width), lambda h: (0, 0, h)),
            made((shares, pairs, 2, t), F32, (1, pairs, 2, t), lambda h: (h, 0, 0, 0)),
            *rows.chunks(d, width, lambda h: (0, h)),
        ],
        [pltpu.VMEM((t, t), F32), pltpu.VMEM((t, width), BF16)],
        (*chunks, w),
        flops=2 * t * d * 3 * d,
    )
    return got[0], got[1], got[2], got[3:]


def middle_forward(rows, back, x, w, mix, gb, me):
    t, d = x.shape
    width = w.shape[3]
    shares = w.shape[1]

    def body(me_ref, *refs):
        x_ref, to_ref, sq_ref, mix_ref, gb_ref, o1_ref, y1_ref, x1_ref, qkv_ref = refs[rows.ways :]
        o1 = rows.gathered(refs[: rows.ways], me_ref[3]).astype(BF16)
        o1_ref[...] = o1
        y1 = jnp.zeros((t, d), F32)
        for h in range(shares):
            y1 = y1 + nt(o1[:, h * width : (h + 1) * width], to_ref[0, h])
        y1 = y1.astype(BF16)
        y1_ref[...] = y1
        x1 = x_ref[...] + nn(y1, mix_ref[...])
        x1_ref[...] = x1
        a2 = norm_rounded(x1, gb_ref[1:2], gb_ref[4:5])
        for g in range(3):
            for h in range(shares):
                qkv_ref[g, :, h * width : (h + 1) * width] = nn(a2, sq_ref[g, h]).astype(BF16)

    return call(
        body,
        (1,),
        [
            SCALARS,
            *(whole(c.shape) for c in back),
            whole(x.shape),
            pl.BlockSpec((1, shares, d, width), lambda i: (6, 0, 0, 0)),
            pl.BlockSpec((3, shares, d, width), lambda i: (1, 0, 0, 0)),
            whole(mix.shape),
            whole(gb.shape),
        ],
        [made((t, d), BF16), made((t, d), BF16), made((t, d), F32), made((3, t, d), BF16)],
        [],
        (me, *back, x, w, w, mix, gb),
        flops=2 * t * d * 5 * d,
    )


def space_forward(rows, qkv, x1, w):
    t, d = x1.shape
    width = w.shape[3]
    shares = w.shape[1]
    pairs = width // LANES
    rate = LOG2E / math.sqrt(HEAD_DIM)
    n = rows.frame_rows

    def body(qkv_ref, x1_ref, w_ref, o2_ref, x2_ref, log_ref):
        bias = rows.space_bias()

        @pl.loop(0, pairs)
        def _(i):
            lanes = pl.ds(pl.multiple_of(i * LANES, LANES), LANES)
            for f in range(rows.frames):
                at = slice(f * n, (f + 1) * n)
                mixed, logs = pair_forward(
                    qkv_ref[0, at, lanes], qkv_ref[1, at, lanes], qkv_ref[2, at, lanes], bias, rate
                )
                o2_ref[at, lanes] = mixed
                log_ref[0, i, f] = jnp.concatenate(logs, axis=0)

        @pl.when(pl.program_id(0) == 0)
        def _():
            x2_ref[...] = x1_ref[...]

        x2_ref[...] += nt(o2_ref[...], w_ref[0, 0])

    return call(
        body,
        (shares,),
        [
            pl.BlockSpec((3, t, width), lambda h: (0, 0, h)),
            whole(x1.shape),
            slabs(1, 7, width, d),
        ],
        [
            made((t, d), BF16, (t, width), lambda h: (0, h)),
            made((t, d), F32),
            made(
                (shares, pairs, rows.frames, 2, n),
                F32,
                (1, pairs, rows.frames, 2, n),
                lambda h: (h, 0, 0, 0, 0),
            ),
        ],
        [],
        (qkv, x1, w),
        flops=2 * t * d * d,
    )


def ff_slab(first, per_share, depth, width):
    return pl.BlockSpec(
        (1, 1, depth, width), lambda j: (first + j % per_share, j // per_share, 0, 0)
    )


def mlp_forward(rows, x2, w, gb, gb_next, me):
    t, d = x2.shape
    width = w.shape[3]
    shares = w.shape[1]
    per_share = (w.shape[0] - 9) // 2
    steps = shares * per_share

    def body(x2_ref, wi_ref, wo_ref, gb_ref, me_ref, gn_ref, x3_ref, *rest):
        send_refs, a3_ref = rest[:-1], rest[-1]
        j = pl.program_id(0)

        @pl.when(j == 0)
        def _():
            a3_ref[...] = norm_rounded(x2_ref[...], gb_ref[2:3], gb_ref[5:6])
            x3_ref[...] = x2_ref[...]

        hid = nn(a3_ref[...], wi_ref[0, 0])
        act = (0.5 * hid * (1.0 + lax.erf(hid * HALF_ROOT))).astype(BF16)
        x3_ref[...] += nt(act, wo_ref[0, 0])

        @pl.when(j == steps - 1)
        def _():
            a = norm_rounded(x3_ref[...], gn_ref[0:1], gn_ref[3:4])
            for k in range(rows.ways):
                send_refs[k][...] = nn(rows.to_time(k, me_ref[3]), a).astype(BF16)

    ins = [
        whole(x2.shape),
        ff_slab(8, per_share, d, width),
        ff_slab(8 + per_share, per_share, d, width),
        whole(gb.shape),
    ]
    ins += [SCALARS, whole(gb_next.shape)]
    outs = [made((t, d), F32)] + rows.chunks(d)
    args = (x2, w, w, gb, me, gb_next)
    return call(
        body, (steps,), ins, outs, [pltpu.VMEM((t, d), BF16)], args, flops=4 * t * d * width * steps
    )


def mlp_backward(rows, grad, x2, w, gb, me, halves, with_output):
    t, d = x2.shape
    width = w.shape[3]
    shares = w.shape[1]
    per_share = (w.shape[0] - 9) // 2
    steps = shares * per_share

    def body(me_ref, g_ref, x2_ref, wi_ref, wo_ref, gb_ref, go_ref, ki_ref, si_ref, ko_ref, so_ref, sums_ref, *rest):
        if with_output:
            x3_ref, *rest = rest
        a3_ref, a3t_ref, e3_ref, e3t_ref, u_ref, room_ref = rest
        j = pl.program_id(0)

        @pl.when(j == 0)
        def _():
            hat, _ = norm_parts(x2_ref[...])
            a3 = hat * gb_ref[2:3] + gb_ref[5:6]
            a3_ref[...] = a3.astype(BF16)
            a3t_ref[...] = a3.T.astype(BF16)
            g = g_ref[...]
            e3_ref[...] = g.astype(BF16)
            e3t_ref[...] = g.T.astype(BF16)
            u_ref[...] = jnp.zeros((t, d), F32)
            if with_output:
                x3_ref[...] = x2_ref[...]

        hid = nn(a3_ref[...], wi_ref[0, 0])
        phi = 0.5 * (1.0 + lax.erf(hid * HALF_ROOT))
        act = (hid * phi).astype(BF16)
        slope = phi + hid * jnp.exp(-0.5 * hid * hid) * INV_ROOT_TAU
        dhid = (nn(e3_ref[...], wo_ref[0, 0]) * slope).astype(BF16)
        split_rows(nn(e3t_ref[...], act), ko_ref, so_ref, (0, 0), room_ref, me_ref)
        split_rows(nn(a3t_ref[...], dhid), ki_ref, si_ref, (0, 0), room_ref, me_ref)
        u_ref[...] += nt(dhid, wi_ref[0, 0])
        if with_output:
            x3_ref[...] += nt(act, wo_ref[0, 0])

        @pl.when(j == steps - 1)
        def _():
            change, sums = norm_back(u_ref[...], x2_ref[...], gb_ref[2:3])
            go_ref[...] = g_ref[...] + change
            sums_ref[...] = sums

    slab_outs = [
        one
        for _ in range(2)
        for one in halves.array(
            (per_share, shares), (1, 1), lambda j: (j % per_share, j // per_share)
        )
    ]
    grad, ki, si, ko, so, sums, *x3 = call(
        body,
        (steps,),
        [
            SCALARS,
            whole(grad.shape),
            whole(x2.shape),
            ff_slab(8, per_share, d, width),
            ff_slab(8 + per_share, per_share, d, width),
            whole(gb.shape),
        ],
        [made((t, d), F32), *slab_outs, made((2, d), F32)] + [made((t, d), F32)] * with_output,
        [
            pltpu.VMEM((t, d), BF16),
            pltpu.VMEM((d, t), BF16),
            pltpu.VMEM((t, d), BF16),
            pltpu.VMEM((d, t), BF16),
            pltpu.VMEM((t, d), F32),
            halves.room(),
        ],
        (me, grad, x2, w, w, gb),
        flops=10 * t * d * width * steps,
    )
    return grad, [(ki, si), (ko, so)], sums, x3


def space_backward(rows, grad, x1, qkv, o2, logs, w, gb, me, halves):
    t, d = x1.shape
    width = w.shape[3]
    shares = w.shape[1]
    pairs = width // LANES
    scale = 1.0 / math.sqrt(HEAD_DIM)
    rate = LOG2E * scale
    n = rows.frame_rows

    def body(me_ref, g_ref, x1_ref, qkv_ref, o2_ref, log_ref, wo_ref, wq_ref, gb_ref, go_ref, keep_ref, send_ref, sums_ref, e2_ref, e2t_ref, a2t_ref, do_ref, dqkv_ref, u_ref, room_ref):
        h = pl.program_id(0)

        @pl.when(h == 0)
        def _():
            g = g_ref[...]
            e2_ref[...] = g.astype(BF16)
            e2t_ref[...] = g.T.astype(BF16)
            hat, _ = norm_parts(x1_ref[...])
            a2t_ref[...] = (hat * gb_ref[1:2] + gb_ref[4:5]).T.astype(BF16)
            u_ref[...] = jnp.zeros((t, d), F32)

        bias = rows.space_bias()
        split_rows(nn(e2t_ref[...], o2_ref[...]), keep_ref, send_ref, (0, 0), room_ref, me_ref)
        do_ref[...] = nn(e2_ref[...], wo_ref[0, 0]).astype(BF16)

        @pl.loop(0, pairs)
        def _(i):
            lanes = pl.ds(pl.multiple_of(i * LANES, LANES), LANES)
            for f in range(rows.frames):
                at = slice(f * n, (f + 1) * n)
                log = log_ref[0, i, f]
                grads = pair_backward(
                    qkv_ref[0, at, lanes],
                    qkv_ref[1, at, lanes],
                    qkv_ref[2, at, lanes],
                    do_ref[at, lanes],
                    (log[0:1], log[1:2]),
                    bias,
                    rate,
                    scale,
                )
                for part in range(3):
                    dqkv_ref[part, at, lanes] = grads[part]

        for part in range(3):
            split_rows(
                nn(a2t_ref[...], dqkv_ref[part]), keep_ref, send_ref, (part + 1, 0), room_ref, me_ref
            )
            u_ref[...] += nt(dqkv_ref[part], wq_ref[part, 0])

        @pl.when(h == shares - 1)
        def _():
            change, sums = norm_back(u_ref[...], x1_ref[...], gb_ref[1:2])
            go_ref[...] = g_ref[...] + change
            sums_ref[...] = sums

    grad, keep, send, sums = call(
        body,
        (shares,),
        [
            SCALARS,
            whole(grad.shape),
            whole(x1.shape),
            pl.BlockSpec((3, t, width), lambda h: (0, 0, h)),
            pl.BlockSpec((t, width), lambda h: (0, h)),
            pl.BlockSpec((1,) + logs.shape[1:], lambda h: (h, 0, 0, 0, 0)),
            slabs(1, 7, width, d),
            slabs(3, 3, width, d),
            whole(gb.shape),
        ],
        [
            made((t, d), F32),
            *halves.array((4, shares), (4, 1), lambda h: (0, h)),
            made((2, d), F32),
        ],
        [
            pltpu.VMEM((t, d), BF16),
            pltpu.VMEM((d, t), BF16),
            pltpu.VMEM((d, t), BF16),
            pltpu.VMEM((t, width), BF16),
            pltpu.VMEM((3, t, width), BF16),
            pltpu.VMEM((t, d), F32),
            halves.room(),
        ],
        (me, grad, x1, qkv, o2, logs, w, w, gb),
        flops=2 * t * d * d * 8,
    )
    return grad, (keep, send), sums


def mix_fits(depth, shards, shares):
    return depth // (shards * shares) % 8 == 0


def middle_backward(rows, grad, y1, o1, w, mix, me, halves, shards):
    t, d = grad.shape
    width = w.shape[3]
    shares = w.shape[1]
    fits = mix_fits(d, shards, shares)
    part = d // (shards * shares)

    def body(me_ref, g_ref, y1_ref, o1_ref, to_ref, mix_ref, *rest):
        send_refs, rest = rest[: rows.ways], rest[rows.ways :]
        gk_ref, gs_ref, *rest = rest
        if fits:
            room_ref, order_ref = rest
        else:
            gm_ref, room_ref = rest
        e1 = g_ref[...].astype(BF16)
        dy1 = nt(e1, mix_ref[...]).astype(BF16)
        sends = [rows.to_time(k, me_ref[3]) for k in range(rows.ways)]
        for h in range(shares):
            lanes = slice(h * width, (h + 1) * width)
            do1 = nn(dy1, to_ref[0, h]).astype(BF16)
            for k in range(rows.ways):
                send_refs[k][:, lanes] = nn(sends[k], do1).astype(BF16)
            split_rows(tn(dy1, o1_ref[:, lanes]), gk_ref, gs_ref, (0, h), room_ref, me_ref)
        gm = tn(y1_ref[...], e1)
        if fits:
            gm = gm.reshape(shards, shares, part, d)
            for h in range(shares):
                for half in range(shares):
                    order_ref[:, half] = gm[:, h, :, half * width : (half + 1) * width]
                split_rows(order_ref[...], gk_ref, gs_ref, (1, h), room_ref, me_ref)
        else:
            gm_ref[...] = gm.astype(BF16)

    outs = rows.chunks(d)
    outs += halves.array((1 + fits, shares), (1 + fits, shares), lambda i: (0, 0))
    scratch = [halves.room()]
    if fits:
        scratch.append(pltpu.VMEM((shards, shares, part, width), F32))
    else:
        outs.append(made((d, d), BF16))
    got = call(
        body,
        (1,),
        [
            SCALARS,
            whole(grad.shape),
            whole(y1.shape),
            whole(o1.shape),
            pl.BlockSpec((1, shares, d, width), lambda i: (6, 0, 0, 0)),
            whole(mix.shape),
        ],
        outs,
        scratch,
        (me, grad, y1, o1, w, mix),
        flops=8 * t * d * d,
    )
    do1, (keep, send) = got[: rows.ways], got[rows.ways : rows.ways + 2]
    if not fits:
        gm = mix_slab(got[-1], shards, shares).reshape((1, shares, halves.pairs, 2) + keep.shape[3:])
        keep = jnp.concatenate((keep, lax.dynamic_index_in_dim(gm, me[0], 3, keepdims=False)), axis=0)
        send = jnp.concatenate((send, lax.dynamic_index_in_dim(gm, 1 - me[0], 3, keepdims=False)), axis=0)
    return do1, (keep, send)


def time_backward(rows, do1, a, qkv, logs, w, me, halves):
    t, d = a.shape
    width = w.shape[3]
    shares = w.shape[1]
    pairs = width // LANES
    scale = 1.0 / math.sqrt(HEAD_DIM)
    rate = LOG2E * scale

    def body(me_ref, *refs):
        do_refs, refs = refs[: rows.ways], refs[rows.ways :]
        a_ref, qkv_ref, log_ref, w_ref = refs[:4]
        out_refs, refs = refs[4 : 4 + rows.ways], refs[4 + rows.ways :]
        half_refs, refs = refs[:6], refs[6:]
        bias_ref, dqkv_ref, at_ref, u_ref, room_ref, do_ref = refs
        h = pl.program_id(0)

        @pl.when(h == 0)
        def _():
            bias_ref[...] = rows.time_bias()
            at_ref[...] = a_ref[...].T
            u_ref[...] = jnp.zeros((t, d), F32)

        for k in range(rows.ways):
            do_ref[k * rows.chunk : (k + 1) * rows.chunk] = do_refs[k][...]

        @pl.loop(0, pairs)
        def _(i):
            lanes = pl.ds(pl.multiple_of(i * LANES, LANES), LANES)
            log = log_ref[0, i]
            grads = pair_backward(
                qkv_ref[0, :, lanes],
                qkv_ref[1, :, lanes],
                qkv_ref[2, :, lanes],
                do_ref[:, lanes],
                (log[0:1], log[1:2]),
                bias_ref[...],
                rate,
                scale,
            )
            for part in range(3):
                dqkv_ref[part, :, lanes] = grads[part]

        for part in range(3):
            value = nn(at_ref[...], dqkv_ref[part])
            split_rows(value, half_refs[2 * part], half_refs[2 * part + 1], (0, 0), room_ref, me_ref)
            u_ref[...] += nt(dqkv_ref[part], w_ref[part, 0])

        @pl.when(h == shares - 1)
        def _():
            for k in range(rows.ways):
                out_refs[k][...] = u_ref[k * rows.chunk : (k + 1) * rows.chunk].astype(BF16)

    got = call(
        body,
        (shares,),
        [
            SCALARS,
            *(pl.BlockSpec((rows.chunk, width), lambda h: (0, h)) for _ in do1),
            whole(a.shape),
            pl.BlockSpec((3, t, width), lambda h: (0, 0, h)),
            pl.BlockSpec((1,) + logs.shape[1:], lambda h: (h, 0, 0, 0)),
            slabs(3, 0, width, d),
        ],
        [
            *rows.chunks(d),
            *(one for _ in range(3) for one in halves.array((1, shares), (1, 1), lambda h: (0, h))),
        ],
        [
            pltpu.VMEM((t, t), F32),
            pltpu.VMEM((3, t, width), BF16),
            pltpu.VMEM((d, t), BF16),
            pltpu.VMEM((t, d), F32),
            halves.room(),
            pltpu.VMEM((t, width), BF16),
        ],
        (me, *do1, a, qkv, logs, w),
        flops=2 * t * d * d * 6,
    )
    parts = got[rows.ways :]
    return got[: rows.ways], [tuple(parts[i : i + 2]) for i in (0, 2, 4)]


def first_norm_back(rows, back, x, grad, gb, me):
    t, d = x.shape

    def body(me_ref, *refs):
        x_ref, g_ref, gb_ref, go_ref, sums_ref = refs[rows.ways :]
        u = rows.gathered(refs[: rows.ways], me_ref[3])
        change, sums = norm_back(u, x_ref[...], gb_ref[0:1])
        go_ref[...] = g_ref[...] + change
        sums_ref[...] = sums

    return call(
        body,
        (1,),
        [SCALARS, *(whole(c.shape) for c in back), whole(x.shape), whole(grad.shape), whole(gb.shape)],
        [made((t, d), F32), made((2, d), F32)],
        [],
        (me, *back, x, grad, gb),
    )


def homes():
    clips, ways = lax.axis_size("clip"), lax.axis_size("seq")
    pairs = []
    for clip in range(clips):
        for seq in range(ways):
            home_clip = clip - clip % 2 + seq % 2
            home_seq = seq // 2 + (ways // 2) * (clip % 2)
            pairs.append((clip * ways + seq, home_clip * ways + home_seq))
    return pairs


def go_home(a):
    return lax.ppermute(a, ("clip", "seq"), homes())


def go_back(a):
    return lax.ppermute(a, ("clip", "seq"), [(home, device) for device, home in homes()])


def member_of(clip, seq):
    return clip % 2 + 2 * (seq % (lax.axis_size("seq") // 2))


def swap_places(chunks):
    clips, ways = lax.axis_size("clip"), lax.axis_size("seq")
    got = [chunks[0]]
    for k in range(1, ways):
        pairs = []
        for clip in range(clips):
            for seq in range(ways):
                other = member_of(clip, seq) ^ k
                to_clip = clip - clip % 2 + other % 2
                to_seq = seq - seq % (ways // 2) + other // 2
                pairs.append((clip * ways + seq, to_clip * ways + to_seq))
        got.append(lax.ppermute(chunks[k], ("clip", "seq"), pairs))
    return got


def pack_layer(time_qkv, time_out, time_mix, space_qkv, space_out, mlp_in, mlp_out):
    width = time_qkv.shape[2]
    r = time_qkv.shape[0]
    halves = time_mix.shape[1] // width

    def columns(a):
        return a.reshape(r, -1, width).transpose(1, 0, 2)

    mix = time_mix.reshape(-1, halves, width).transpose(1, 0, 2).reshape(1, r, width)
    return jnp.concatenate(
        (
            columns(time_qkv),
            columns(space_qkv),
            time_out.T[None],
            space_out.T[None],
            columns(mlp_in),
            columns(mlp_out.T),
            mix,
        ),
        axis=0,
    )


def gather_slabs(pack):
    full = lax.all_gather(pack, ("head", "clip", "seq"), axis=1, tiled=True)
    return full.reshape(pack.shape[0], lax.axis_size("head"), -1, pack.shape[2])


def mix_whole(slab, shards):
    shares, depth, width = slab.shape
    part = slab.reshape(shares, shards, shares, depth // (shards * shares), width)
    return part.transpose(1, 0, 3, 2, 4).reshape(depth, shares * width)


def mix_slab(whole_grad, shards, shares):
    depth, full = whole_grad.shape
    width = full // shares
    part = whole_grad.reshape(shards, shares, depth // (shards * shares), shares, width)
    return part.transpose(1, 0, 3, 2, 4).reshape(1, shares, depth, width)


class Piece:
    def __init__(self, keep, got, first, n, order):
        self.near = (keep, got)
        self.first = first
        self.n = n
        self.order = order
        self.step = 0
        self.held = []
        self.result = None


PLACE = {"x": 1, "h": 2}


def fold(pieces, me, last_by_rows):
    ways = lax.axis_size("seq")
    depth, width = pieces[0].near[0].shape[-2:]
    r = depth // ways
    used = {}
    arrays = []

    def number(a):
        for i, known in enumerate(arrays):
            if known is a:
                return i
        arrays.append(a)
        return len(arrays) - 1

    plans = []
    for p in pieces:
        link = p.order[p.step] if p.step < 2 else "z"
        blocks = p.n * (2 if p.step == 0 else 1)
        base = used.get(link, 0)
        used[link] = base + blocks
        near = [number(a) for a in p.near]
        held = [(number(a), at) for a, at in p.held]
        plans.append((p, link, base, near, held))
    links = sorted(used)
    shapes = [
        (ways, used[k], r, width) if k == "z" and last_by_rows else (used[k], depth, width)
        for k in links
    ]
    rooms, counts = [], []
    for p, link, base, near, held in plans:
        each = 2 if p.step == 0 else 1
        counts.append((each, len(near) + len(held)))
        rooms += [(each * p.n, depth, width)] * (len(near) + len(held))
    copies_needed = sum(each * terms for each, terms in counts)

    def body(me_ref, *refs):
        sources = refs[: len(arrays)]
        outs = dict(zip(links, refs[len(arrays) : len(arrays) + len(links)]))
        held_refs = refs[len(arrays) + len(links) : -1]
        sems = refs[-1]
        mine = {name: me_ref[PLACE[name]] for name in PLACE}
        groups = []
        room = 0
        sem = 0
        for p, link, base, near, held in plans:
            group = []
            if p.step == 0:
                for term in near:
                    for k in range(2):
                        pick = {p.order[0]: 1 - mine[p.order[0]], p.order[1]: k}
                        source = sources[term].at[pl.ds(p.first, p.n), pick["h"], pick["x"]]
                        group.append((source, held_refs[room].at[pl.ds(k * p.n, p.n)]))
                    room += 1
            else:
                last = p.order[1]
                pick = {p.order[0]: mine[p.order[0]]}
                pick[last] = 1 - mine[last] if p.step == 1 else mine[last]
                for term in near:
                    source = sources[term].at[pl.ds(p.first, p.n), pick["h"], pick["x"]]
                    group.append((source, held_refs[room]))
                    room += 1
                for i, (term, at) in enumerate(held):
                    start = at + pick[last] * p.n if i == 0 else at
                    group.append((sources[term].at[pl.ds(start, p.n)], held_refs[room]))
                    room += 1
            made_copies = []
            for source, target in group:
                made_copies.append(pltpu.make_async_copy(source, target, sems.at[sem]))
                sem += 1
            groups.append(made_copies)
        for group in groups:
            for copy in group:
                copy.start()
        room = 0
        for (p, link, base, near, held), (each, terms), group in zip(plans, counts, groups):
            these = held_refs[room : room + terms]
            room += terms
            for copy in group:
                copy.wait()

            @pl.loop(0, each * p.n)
            def _(i, these=these, base=base, out=outs[link], last=p.step == 2 and last_by_rows):
                value = these[0][i].astype(F32)
                for one in these[1:]:
                    value = value + one[i].astype(F32)
                value = value.astype(BF16)
                if last:
                    for k in range(ways):
                        out[k, base + i] = value[k * r : (k + 1) * r]
                else:
                    out[base + i] = value

    moved = sum(2 * math.prod(room) for room in rooms) + sum(2 * math.prod(shape) for shape in shapes)
    sums = pl.pallas_call(
        body,
        out_shape=[jax.ShapeDtypeStruct(shape, BF16) for shape in shapes],
        in_specs=[SCALARS] + [pl.BlockSpec(memory_space=pltpu.HBM)] * len(arrays),
        out_specs=[pl.BlockSpec(memory_space=pltpu.VMEM)] * len(links),
        scratch_shapes=[pltpu.VMEM(room, BF16) for room in rooms]
        + [pltpu.SemaphoreType.DMA((copies_needed,))],
        compiler_params=pltpu.CompilerParams(vmem_limit_bytes=VMEM),
        cost_estimate=pl.CostEstimate(flops=0, bytes_accessed=moved, transcendentals=0),
    )(me, *arrays)
    return [(p, link, base) for p, link, base, _, _ in plans], dict(zip(links, sums))


def cross(a, name):
    axis, bit = ("head", 0) if name == "h" else ("clip", 1 if name == "x" else 0)
    size = lax.axis_size(axis)
    return lax.ppermute(a, axis, [(i, i ^ (1 << bit)) for i in range(size)])


def pieces_of(halves_of):
    total = sum(keep.shape[0] for keep, _ in halves_of)
    found = []
    seen = 0
    for keep, send in halves_of:
        got = cross(send, "c")
        n = keep.shape[0]
        first = min(max((total + 1) // 2 - seen, 0), n)
        if first:
            found.append(Piece(keep, got, 0, first, ("x", "h")))
        if n > first:
            found.append(Piece(keep, got, first, n - first, ("h", "x")))
        seen += n
    return found


def move(x, pieces, me, at_end=False):
    plans, sums = fold(pieces, me, at_end)
    x, sums = lax.optimization_barrier((x, sums))
    got = {}
    for link, array in sums.items():
        if link == "z":
            if at_end:
                every = lax.all_to_all(array, "seq", split_axis=0, concat_axis=0, tiled=True)
                got[link] = jnp.sum(every.astype(F32), axis=0)
            else:
                own = lax.psum_scatter(array, "seq", scatter_dimension=1, tiled=True)
                got[link] = own.astype(F32)
        else:
            got[link] = cross(array, link)
    for p, link, base in plans:
        if link == "z":
            p.result = got[link][base : base + p.n]
        else:
            p.held.append((got[link], base))
        p.step += 1
    return x


def settle(x, pieces):
    arrays = []
    for p in pieces:
        if not any(p.held[-1][0] is a for a in arrays):
            arrays.append(p.held[-1][0])
    x, came = lax.optimization_barrier((x, arrays))
    for p in pieces:
        for old, new in zip(arrays, came):
            if p.held[-1][0] is old:
                p.held[-1] = (new, p.held[-1][1])
                break
    return x


def reduce_plain(halves_of, core):
    def joined(keep, send):
        low = jnp.where(core == 0, keep, send)
        high = jnp.where(core == 0, send, keep)
        n, shares, pairs, depth, width = keep.shape
        return jnp.stack((low, high), axis=3).reshape(n, shares, 2 * pairs * depth, width)

    g = jnp.concatenate([joined(*pair) for pair in halves_of], axis=0)
    g = lax.psum_scatter(g, "head", scatter_dimension=1, tiled=True)
    g = lax.psum_scatter(g.astype(F32), ("clip", "seq"), scatter_dimension=2, tiled=True)
    return g[:, 0]


def gather_norms(gain, bias):
    layers, norms, part = gain.shape
    both = jnp.concatenate((gain, bias), axis=1).reshape(1, -1)
    count = lax.axis_size("clip") * lax.axis_size("seq") * lax.axis_size("head")
    width = round_up(both.shape[1], 128)
    padded = jnp.pad(both, ((0, 0), (0, width - both.shape[1])))
    every = lax.all_to_all(
        jnp.broadcast_to(padded, (count, width)), ALL, split_axis=0, concat_axis=0, tiled=True
    )[:, : both.shape[1]]
    return every.reshape(count, layers * 2 * norms, part).transpose(1, 0, 2).reshape(layers, 2 * norms, -1)


def reduce_norms(sums):
    count = lax.axis_size("clip") * lax.axis_size("seq") * lax.axis_size("head")
    rows, features = sums.shape
    part = features // count
    a = sums.reshape(rows, count, part).transpose(1, 0, 2).reshape(count, rows * part)
    width = round_up(rows * part, 128)
    a = jnp.pad(a, ((0, 0), (0, width - rows * part)))
    every = lax.all_to_all(a, ALL, split_axis=0, concat_axis=0, tiled=True)
    return jnp.sum(every, axis=0)[: rows * part].reshape(rows, part)


def on_device(
    tokens,
    cotangent,
    time_qkv,
    time_out,
    time_mix,
    space_qkv,
    space_out,
    mlp_in,
    mlp_out,
    norm_gain,
    norm_bias,
):
    layers = time_qkv.shape[0]
    clips, frames, places, d = tokens.shape
    ways = lax.axis_size("seq")
    shards = lax.axis_size("clip") * ways
    rows = Rows(clips * frames, places, ways)
    shares = lax.axis_size("head")

    def as_rows(a):
        a = a.astype(F32).reshape(rows.frames, places, d)
        a = jnp.pad(a, ((0, 0), (0, rows.frame_rows - places), (0, 0)))
        return a.reshape(rows.rows, d)

    def from_rows(a):
        a = a.reshape(rows.frames, rows.frame_rows, d)[:, :places]
        return a.reshape(tokens.shape)

    gbs = gather_norms(norm_gain, norm_bias)
    gb = [gbs[l] for l in range(layers)]
    weights = [
        gather_slabs(
            pack_layer(
                time_qkv[l], time_out[l], time_mix[l], space_qkv[l], space_out[l], mlp_in[l], mlp_out[l]
            )
        )
        for l in range(layers)
    ]
    mixes = [mix_whole(w[-1], shards) for w in weights]

    halves = Halves(lax.axis_size("clip"), d, time_qkv.shape[3])
    clip = lax.axis_index("clip")
    member = member_of(clip, lax.axis_index("seq"))
    me = jnp.stack((clip & 1, (clip >> 1) & 1, lax.axis_index("head"), member)).astype(jnp.int32)

    x = as_rows(go_home(tokens))
    send = send_first(rows, x, gb[0], me)
    kept = []
    for l in range(layers):
        w = weights[l]
        a1, qkv1, log1, o1_time = time_forward(rows, swap_places(send), w)
        back = swap_places(o1_time)
        o1, y1, x1, qkv2 = middle_forward(rows, back, x, w, mixes[l], gb[l], me)
        o2, x2, log2 = space_forward(rows, qkv2, x1, w)
        kept.append((x, a1, qkv1, log1, o1, y1, x1, qkv2, o2, log2, x2))
        if l + 1 < layers:
            x, *send = mlp_forward(rows, x2, w, gb[l], gb[l + 1], me)

    grad = as_rows(go_home(cotangent))
    norm_rows = [None] * layers
    summed = [None] * layers
    late = []
    quick = lax.axis_size("clip") == 4 and shares == 2 and time_qkv.shape[1] % 16 == 0
    for l in reversed(range(layers)):
        w = weights[l]
        x, a1, qkv1, log1, o1, y1, x1, qkv2, o2, log2, x2 = kept[l]
        grad, g_ff, s3, x3 = mlp_backward(rows, grad, x2, w, gb[l], me, halves, l + 1 == layers)
        if x3:
            output = go_back(from_rows(x3[0].astype(BF16)))
        if quick:
            ff = pieces_of(g_ff)
            if late:
                grad = settle(grad, late)
                grad = move(grad, late, me)
                late = [p for p in late if p.step < 3]
        grad, g_space, s2 = space_backward(rows, grad, x1, qkv2, o2, log2, w, gb[l], me, halves)
        if quick:
            space = pieces_of([g_space])
            grad, output = move((grad, output), ff, me)
        do1, g_out = middle_backward(rows, grad, y1, o1, w, mixes[l], me, halves, shards)
        do1 = swap_places(do1)
        if quick:
            do1 = move(do1, ff + space + late, me)
        da1, g_time = time_backward(rows, do1, a1, qkv1, log1, w, me, halves)
        if quick:
            da1 = settle(da1, ff + space)
        da1 = swap_places(da1)
        if quick:
            rest = pieces_of([g_out] + g_time)
            da1 = move(da1, ff + space + rest, me)
            late = space + rest
        grad, s1 = first_norm_back(rows, da1, x, grad, gb[l], me)
        norm_rows[l] = jnp.concatenate((s1[0:1], s2[0:1], s3[0:1], s1[1:2], s2[1:2], s3[1:2]), axis=0)
        if quick:
            summed[l] = ff + space + rest
        else:
            summed[l] = [reduce_plain(g_ff + [g_space, g_out] + g_time, clip & 1)]
    if quick:
        move((), late, me, True)
        move((), rest, me, True)
        summed = [[p.result for p in some] for some in summed]
    cuts = (2 * g_ff[0][0].shape[0], g_space[0].shape[0], g_out[0].shape[0], len(g_time))
    results = []
    for some in summed:
        slabs_of = jnp.concatenate(some, axis=0)
        ends = [sum(cuts[: i + 1]) for i in range(4)]
        results.append([slabs_of[e - c : e] for c, e in zip(cuts, ends)])
    tokens_grad = go_back(from_rows(grad.astype(BF16))).astype(F32)
    norm_sums = reduce_norms(jnp.concatenate(norm_rows, axis=0)).reshape(layers, 2, 3, -1)

    def stacked(form):
        return jnp.stack([form(*results[l]) for l in range(layers)])

    def rows_of(a):
        return a.transpose(1, 0, 2)

    def flat(a):
        return rows_of(a).reshape(a.shape[1], -1)

    def mix_rows(a):
        r, width = a.shape
        return a.reshape(shares, r // shares, width).transpose(1, 0, 2).reshape(r // shares, -1)

    per_share = mlp_in.shape[2] // time_qkv.shape[3]
    return (
        output,
        tokens_grad,
        stacked(lambda ff, s, t, q: rows_of(q)),
        stacked(lambda ff, s, t, q: t[0].T),
        stacked(lambda ff, s, t, q: mix_rows(t[1])),
        stacked(lambda ff, s, t, q: rows_of(s[1:])),
        stacked(lambda ff, s, t, q: s[0].T),
        stacked(lambda ff, s, t, q: flat(ff[:per_share])),
        stacked(lambda ff, s, t, q: flat(ff[per_share:]).T),
        norm_sums[:, 0],
        norm_sums[:, 1],
    )


def solution(mesh):
    token_spec = P(("clip", "head"), "seq", None, None)
    in_specs = (
        token_spec,
        token_spec,
        P(None, ("clip", "seq"), None, "head"),
        P(None, "head", ("clip", "seq")),
        P(None, ("clip", "seq", "head"), None),
        P(None, ("clip", "seq"), None, "head"),
        P(None, "head", ("clip", "seq")),
        P(None, ("clip", "seq"), "head"),
        P(None, "head", ("clip", "seq")),
        P(None, None, ("clip", "seq", "head")),
        P(None, None, ("clip", "seq", "head")),
    )
    return jax.shard_map(
        on_device, mesh=mesh, in_specs=in_specs, out_specs=in_specs, check_vma=False
    )
```

```python
import functools
import math

import jax
import jax.numpy as jnp
from jax import lax
from jax.experimental import pallas as pl
from jax.experimental.pallas import tpu as pltpu
from jax.sharding import PartitionSpec as P

HEAD_DIM = 64
NORM_EPS = 1e-06
HALF_ROOT = 0.7071067811865476
INV_ROOT_TAU = 0.3989422804014327
LOG2E = 1.4426950408889634
FAR = -1e30
LANES = 128
VMEM = 56 * 1024 * 1024
SHOWN = 1.0
ALL = ("clip", "seq", "head")
BF16 = jnp.bfloat16
F32 = jnp.float32


def round_up(value, step):
    return -(-value // step) * step


def nn(a, b):
    return lax.dot_general(a, b, (((1,), (0,)), ((), ())), preferred_element_type=F32)


def nt(a, b):
    return lax.dot_general(a, b, (((1,), (1,)), ((), ())), preferred_element_type=F32)


def tn(a, b):
    return lax.dot_general(a, b, (((0,), (0,)), ((), ())), preferred_element_type=F32)


def norm_parts(x):
    mean = jnp.mean(x, axis=-1, keepdims=True)
    centred = x - mean
    spread = lax.rsqrt(jnp.mean(centred * centred, axis=-1, keepdims=True) + NORM_EPS)
    return centred * spread, spread


def norm_rounded(x, gain, bias):
    hat, _ = norm_parts(x)
    return (hat * gain + bias).astype(BF16)


def norm_back(u, x, gain):
    hat, spread = norm_parts(x)
    scaled = u * gain
    mean_scaled = jnp.mean(scaled, axis=-1, keepdims=True)
    mean_cross = jnp.mean(scaled * hat, axis=-1, keepdims=True)
    change = spread * (scaled - mean_scaled - hat * mean_cross)
    sums = jnp.concatenate(
        (jnp.sum(u * hat, axis=0, keepdims=True), jnp.sum(u, axis=0, keepdims=True)), axis=0
    )
    return change, sums


class Rows:
    def __init__(self, frames, places, ways):
        self.frames = frames
        self.places = places
        self.ways = ways
        self.frame_rows = round_up(places, 16)
        self.rows = frames * self.frame_rows
        self.block = places // ways
        self.chunk = round_up(frames * self.block, 8)
        self.time_rows = ways * self.chunk

    def split(self, r):
        way = jnp.zeros_like(r)
        for k in range(1, self.ways):
            way = way + (r >= k * self.chunk).astype(jnp.int32)
        rest = r - way * self.chunk
        frame = jnp.zeros_like(r)
        for k in range(1, self.frames):
            frame = frame + (rest >= k * self.block).astype(jnp.int32)
        real = rest < self.frames * self.block
        return way, frame, rest - frame * self.block, real

    def to_time(self, k, member):
        r = lax.broadcasted_iota(jnp.int32, (self.chunk, 1), 0)
        _, frame, place, real = self.split(r)
        way = jnp.bitwise_xor(member, k)
        source = jnp.where(real, frame * self.frame_rows + way * self.block + place, -1)
        c = lax.broadcasted_iota(jnp.int32, (self.chunk, self.rows), 1)
        return jnp.where(c == source, 1.0, 0.0).astype(BF16)

    def gathered(self, chunk_refs, member):
        total = tn(self.to_time(0, member), chunk_refs[0][...])
        for k in range(1, self.ways):
            total = total + tn(self.to_time(k, member), chunk_refs[k][...])
        return total

    def chunks(self, width, block=None, index=None):
        return [
            made((self.chunk, width), BF16)
            if block is None
            else made((self.chunk, width), BF16, (self.chunk, block), index)
            for _ in range(self.ways)
        ]

    def time_bias(self):
        def label(r):
            _, _, place, real = self.split(r)
            return jnp.where(real, place, -1)

        a = label(lax.broadcasted_iota(jnp.int32, (self.time_rows, 1), 0))
        b = label(lax.broadcasted_iota(jnp.int32, (1, self.time_rows), 1))
        return jnp.where(a == b, 0.0, FAR).astype(F32)

    def space_bias(self):
        a = lax.broadcasted_iota(jnp.int32, (self.frame_rows, 1), 0)
        return jnp.where(a < self.places, 0.0, FAR).astype(F32)


def lane_masks(rows):
    lane = lax.broadcasted_iota(jnp.int32, (rows, LANES), 1)
    return lane < HEAD_DIM


def one_of(value, low, half):
    zero = jnp.zeros_like(value)
    return jnp.where(low, value, zero) if half == 0 else jnp.where(low, zero, value)


def pair_forward(q, k, v, bias, rate):
    low = lane_masks(q.shape[0])
    mixed, logs = [], []
    for half in range(2):
        s = nt(k, one_of(q, low, half)) + bias
        peak = jnp.max(s, axis=0, keepdims=True)
        e = jnp.exp2((s - peak) * rate)
        total = jnp.sum(e, axis=0, keepdims=True)
        soft = (e * (1.0 / total)).astype(BF16)
        mixed.append(tn(soft, v))
        logs.append(peak * rate + jnp.log2(total))
    return jnp.where(low, mixed[0], mixed[1]).astype(BF16), logs


def pair_backward(q, k, v, do, logs, bias, rate, scale):
    low = lane_masks(q.shape[0])
    dq, dk, dv = [], [], []
    for half in range(2):
        s = nt(k, one_of(q, low, half)) + bias
        soft = jnp.exp2(s * rate - logs[half])
        dp = nt(v, one_of(do, low, half))
        ds = (soft * (dp - jnp.sum(soft * dp, axis=0, keepdims=True))).astype(BF16)
        dv.append(nn(soft.astype(BF16), do))
        dk.append(nn(ds, q))
        dq.append(tn(ds, k))
    return (
        (jnp.where(low, dq[0], dq[1]) * scale).astype(BF16),
        (jnp.where(low, dk[0], dk[1]) * scale).astype(BF16),
        jnp.where(low, dv[0], dv[1]).astype(BF16),
    )


def split_rows(value, keep_ref, send_ref, at, room_ref, me_ref):
    mine = me_ref[0]
    room_ref[...] = value.reshape(room_ref.shape)
    keep_ref[at] = room_ref[:, mine].astype(BF16)
    send_ref[at] = room_ref[:, 1 - mine].astype(BF16)


class Halves:
    def __init__(self, clips, depth, width):
        self.pairs = clips // 2
        self.rows = depth // clips
        self.width = width

    def array(self, lead, block, index):
        tail = (self.pairs, self.rows, self.width)
        one = lambda: made(lead + tail, BF16, block + tail, lambda *g: index(*g) + (0, 0, 0))
        return [one(), one()]

    def room(self):
        return pltpu.VMEM((self.pairs, 2, self.rows, self.width), F32)


SCALARS = pl.BlockSpec(memory_space=pltpu.SMEM)


def call(body, grid, ins, outs, scratch, args, flops=0):
    specs = [spec for spec in ins]
    moved = sum(math.prod(o.shape) * o.dtype.itemsize for o, _ in outs)
    moved += sum(math.prod(a.shape) * a.dtype.itemsize for a in args)
    return pl.pallas_call(
        body,
        out_shape=[shape for shape, _ in outs],
        grid=grid,
        in_specs=specs,
        out_specs=[spec for _, spec in outs],
        scratch_shapes=scratch,
        compiler_params=pltpu.CompilerParams(vmem_limit_bytes=VMEM),
        cost_estimate=pl.CostEstimate(
            flops=int(flops * SHOWN), bytes_accessed=int(moved * SHOWN), transcendentals=0
        ),
    )(*args)


def whole(shape):
    zeros = (0,) * len(shape)
    return pl.BlockSpec(shape, lambda *_: zeros)


def made(shape, dtype, block=None, index=None):
    spec = whole(shape) if block is None else pl.BlockSpec(block, index)
    return jax.ShapeDtypeStruct(shape, dtype), spec


def slabs(count, first, width, depth):
    return pl.BlockSpec((count, 1, depth, width), lambda h, *_: (first // count, h, 0, 0))


def send_first(rows, x, gb, me):
    def body(me_ref, x_ref, gb_ref, *out_refs):
        a = norm_rounded(x_ref[...], gb_ref[0:1], gb_ref[3:4])
        for k in range(rows.ways):
            out_refs[k][...] = nn(rows.to_time(k, me_ref[3]), a).astype(BF16)

    d = x.shape[1]
    return call(
        body, (1,), [SCALARS, whole(x.shape), whole(gb.shape)], rows.chunks(d), [], (me, x, gb)
    )


def time_forward(rows, chunks, w):
    t, d = rows.time_rows, chunks[0].shape[1]
    width = w.shape[3]
    shares = w.shape[1]
    pairs = width // LANES
    ways = rows.ways
    rate = LOG2E / math.sqrt(HEAD_DIM)

    def body(*refs):
        chunk_refs = refs[:ways]
        w_ref, a_ref, qkv_ref, log_ref = refs[ways : ways + 4]
        out_refs = refs[ways + 4 : 2 * ways + 4]
        bias_ref, mixed_ref = refs[2 * ways + 4 :]

        @pl.when(pl.program_id(0) == 0)
        def _():
            bias_ref[...] = rows.time_bias()
            for k in range(ways):
                a_ref[k * rows.chunk : (k + 1) * rows.chunk] = chunk_refs[k][...]

        act = a_ref[...]
        for g in range(3):
            qkv_ref[g] = nn(act, w_ref[g, 0]).astype(BF16)

        @pl.loop(0, pairs)
        def _(i):
            lanes = pl.ds(pl.multiple_of(i * LANES, LANES), LANES)
            mixed, logs = pair_forward(
                qkv_ref[0, :, lanes], qkv_ref[1, :, lanes], qkv_ref[2, :, lanes], bias_ref[...], rate
            )
            mixed_ref[:, lanes] = mixed
            log_ref[0, i] = jnp.concatenate(logs, axis=0)

        for k in range(ways):
            out_refs[k][...] = mixed_ref[k * rows.chunk : (k + 1) * rows.chunk]

    got = call(
        body,
        (shares,),
        [whole(c.shape) for c in chunks] + [slabs(3, 0, width, d)],
        [
            made((t, d), BF16),
            made((3, t, d), BF16, (3, t, width), lambda h: (0, 0, h)),
            made((shares, pairs, 2, t), F32, (1, pairs, 2, t), lambda h: (h, 0, 0, 0)),
            *rows.chunks(d, width, lambda h: (0, h)),
        ],
        [pltpu.VMEM((t, t), F32), pltpu.VMEM((t, width), BF16)],
        (*chunks, w),
        flops=2 * t * d * 3 * d,
    )
    return got[0], got[1], got[2], got[3:]


def middle_forward(rows, back, x, w, mix, gb, me):
    t, d = x.shape
    width = w.shape[3]
    shares = w.shape[1]

    def body(me_ref, *refs):
        x_ref, to_ref, sq_ref, mix_ref, gb_ref, o1_ref, y1_ref, x1_ref, qkv_ref = refs[rows.ways :]
        o1 = rows.gathered(refs[: rows.ways], me_ref[3]).astype(BF16)
        o1_ref[...] = o1
        y1 = jnp.zeros((t, d), F32)
        for h in range(shares):
            y1 = y1 + nt(o1[:, h * width : (h + 1) * width], to_ref[0, h])
        y1 = y1.astype(BF16)
        y1_ref[...] = y1
        x1 = x_ref[...] + nn(y1, mix_ref[...])
        x1_ref[...] = x1
        a2 = norm_rounded(x1, gb_ref[1:2], gb_ref[4:5])
        for g in range(3):
            for h in range(shares):
                qkv_ref[g, :, h * width : (h + 1) * width] = nn(a2, sq_ref[g, h]).astype(BF16)

    return call(
        body,
        (1,),
        [
            SCALARS,
            *(whole(c.shape) for c in back),
            whole(x.shape),
            pl.BlockSpec((1, shares, d, width), lambda i: (6, 0, 0, 0)),
            pl.BlockSpec((3, shares, d, width), lambda i: (1, 0, 0, 0)),
            whole(mix.shape),
            whole(gb.shape),
        ],
        [made((t, d), BF16), made((t, d), BF16), made((t, d), F32), made((3, t, d), BF16)],
        [],
        (me, *back, x, w, w, mix, gb),
        flops=2 * t * d * 5 * d,
    )


def space_forward(rows, qkv, x1, w):
    t, d = x1.shape
    width = w.shape[3]
    shares = w.shape[1]
    pairs = width // LANES
    rate = LOG2E / math.sqrt(HEAD_DIM)
    n = rows.frame_rows

    def body(qkv_ref, x1_ref, w_ref, o2_ref, x2_ref, log_ref):
        bias = rows.space_bias()

        @pl.loop(0, pairs)
        def _(i):
            lanes = pl.ds(pl.multiple_of(i * LANES, LANES), LANES)
            for f in range(rows.frames):
                at = slice(f * n, (f + 1) * n)
                mixed, logs = pair_forward(
                    qkv_ref[0, at, lanes], qkv_ref[1, at, lanes], qkv_ref[2, at, lanes], bias, rate
                )
                o2_ref[at, lanes] = mixed
                log_ref[0, i, f] = jnp.concatenate(logs, axis=0)

        @pl.when(pl.program_id(0) == 0)
        def _():
            x2_ref[...] = x1_ref[...]

        x2_ref[...] += nt(o2_ref[...], w_ref[0, 0])

    return call(
        body,
        (shares,),
        [
            pl.BlockSpec((3, t, width), lambda h: (0, 0, h)),
            whole(x1.shape),
            slabs(1, 7, width, d),
        ],
        [
            made((t, d), BF16, (t, width), lambda h: (0, h)),
            made((t, d), F32),
            made(
                (shares, pairs, rows.frames, 2, n),
                F32,
                (1, pairs, rows.frames, 2, n),
                lambda h: (h, 0, 0, 0, 0),
            ),
        ],
        [],
        (qkv, x1, w),
        flops=2 * t * d * d,
    )


def ff_slab(first, per_share, depth, width):
    return pl.BlockSpec(
        (1, 1, depth, width), lambda j: (first + j % per_share, j // per_share, 0, 0)
    )


def mlp_forward(rows, x2, w, gb, gb_next, me):
    t, d = x2.shape
    width = w.shape[3]
    shares = w.shape[1]
    per_share = w.shape[0] // 2
    steps = shares * per_share

    def body(x2_ref, wi_ref, wo_ref, gb_ref, me_ref, gn_ref, x3_ref, *rest):
        send_refs, a3_ref = rest[:-1], rest[-1]
        j = pl.program_id(0)

        @pl.when(j == 0)
        def _():
            a3_ref[...] = norm_rounded(x2_ref[...], gb_ref[2:3], gb_ref[5:6])
            x3_ref[...] = x2_ref[...]

        hid = nn(a3_ref[...], wi_ref[0, 0])
        act = (0.5 * hid * (1.0 + lax.erf(hid * HALF_ROOT))).astype(BF16)
        x3_ref[...] += nt(act, wo_ref[0, 0])

        @pl.when(j == steps - 1)
        def _():
            a = norm_rounded(x3_ref[...], gn_ref[0:1], gn_ref[3:4])
            for k in range(rows.ways):
                send_refs[k][...] = nn(rows.to_time(k, me_ref[3]), a).astype(BF16)

    ins = [
        whole(x2.shape),
        ff_slab(0, per_share, d, width),
        ff_slab(per_share, per_share, d, width),
        whole(gb.shape),
    ]
    ins += [SCALARS, whole(gb_next.shape)]
    outs = [made((t, d), F32)] + rows.chunks(d)
    args = (x2, w, w, gb, me, gb_next)
    return call(
        body, (steps,), ins, outs, [pltpu.VMEM((t, d), BF16)], args, flops=4 * t * d * width * steps
    )


def mlp_backward(rows, grad, x2, w, gb, me, halves, with_output):
    t, d = x2.shape
    width = w.shape[3]
    shares = w.shape[1]
    per_share = w.shape[0] // 2
    steps = shares * per_share

    def body(me_ref, g_ref, x2_ref, wi_ref, wo_ref, gb_ref, go_ref, ki_ref, si_ref, ko_ref, so_ref, sums_ref, *rest):
        if with_output:
            x3_ref, *rest = rest
        a3_ref, a3t_ref, e3_ref, e3t_ref, u_ref, room_ref = rest
        j = pl.program_id(0)

        @pl.when(j == 0)
        def _():
            hat, _ = norm_parts(x2_ref[...])
            a3 = hat * gb_ref[2:3] + gb_ref[5:6]
            a3_ref[...] = a3.astype(BF16)
            a3t_ref[...] = a3.T.astype(BF16)
            g = g_ref[...]
            e3_ref[...] = g.astype(BF16)
            e3t_ref[...] = g.T.astype(BF16)
            u_ref[...] = jnp.zeros((t, d), F32)
            if with_output:
                x3_ref[...] = x2_ref[...]

        hid = nn(a3_ref[...], wi_ref[0, 0])
        phi = 0.5 * (1.0 + lax.erf(hid * HALF_ROOT))
        act = (hid * phi).astype(BF16)
        slope = phi + hid * jnp.exp(-0.5 * hid * hid) * INV_ROOT_TAU
        dhid = (nn(e3_ref[...], wo_ref[0, 0]) * slope).astype(BF16)
        split_rows(nn(e3t_ref[...], act), ko_ref, so_ref, (0, 0), room_ref, me_ref)
        split_rows(nn(a3t_ref[...], dhid), ki_ref, si_ref, (0, 0), room_ref, me_ref)
        u_ref[...] += nt(dhid, wi_ref[0, 0])
        if with_output:
            x3_ref[...] += nt(act, wo_ref[0, 0])

        @pl.when(j == steps - 1)
        def _():
            change, sums = norm_back(u_ref[...], x2_ref[...], gb_ref[2:3])
            go_ref[...] = g_ref[...] + change
            sums_ref[...] = sums

    slab_outs = [
        one
        for _ in range(2)
        for one in halves.array(
            (per_share, shares), (1, 1), lambda j: (j % per_share, j // per_share)
        )
    ]
    grad, ki, si, ko, so, sums, *x3 = call(
        body,
        (steps,),
        [
            SCALARS,
            whole(grad.shape),
            whole(x2.shape),
            ff_slab(0, per_share, d, width),
            ff_slab(per_share, per_share, d, width),
            whole(gb.shape),
        ],
        [made((t, d), F32), *slab_outs, made((2, d), F32)] + [made((t, d), F32)] * with_output,
        [
            pltpu.VMEM((t, d), BF16),
            pltpu.VMEM((d, t), BF16),
            pltpu.VMEM((t, d), BF16),
            pltpu.VMEM((d, t), BF16),
            pltpu.VMEM((t, d), F32),
            halves.room(),
        ],
        (me, grad, x2, w, w, gb),
        flops=10 * t * d * width * steps,
    )
    return grad, [(ki, si), (ko, so)], sums, x3


def space_backward(rows, grad, x1, qkv, o2, logs, w, gb, me, halves):
    t, d = x1.shape
    width = w.shape[3]
    shares = w.shape[1]
    pairs = width // LANES
    scale = 1.0 / math.sqrt(HEAD_DIM)
    rate = LOG2E * scale
    n = rows.frame_rows

    def body(me_ref, g_ref, x1_ref, qkv_ref, o2_ref, log_ref, wo_ref, wq_ref, gb_ref, go_ref, keep_ref, send_ref, sums_ref, e2_ref, e2t_ref, a2t_ref, do_ref, dqkv_ref, u_ref, room_ref):
        h = pl.program_id(0)

        @pl.when(h == 0)
        def _():
            g = g_ref[...]
            e2_ref[...] = g.astype(BF16)
            e2t_ref[...] = g.T.astype(BF16)
            hat, _ = norm_parts(x1_ref[...])
            a2t_ref[...] = (hat * gb_ref[1:2] + gb_ref[4:5]).T.astype(BF16)
            u_ref[...] = jnp.zeros((t, d), F32)

        bias = rows.space_bias()
        split_rows(nn(e2t_ref[...], o2_ref[...]), keep_ref, send_ref, (0, 0), room_ref, me_ref)
        do_ref[...] = nn(e2_ref[...], wo_ref[0, 0]).astype(BF16)

        @pl.loop(0, pairs)
        def _(i):
            lanes = pl.ds(pl.multiple_of(i * LANES, LANES), LANES)
            for f in range(rows.frames):
                at = slice(f * n, (f + 1) * n)
                log = log_ref[0, i, f]
                grads = pair_backward(
                    qkv_ref[0, at, lanes],
                    qkv_ref[1, at, lanes],
                    qkv_ref[2, at, lanes],
                    do_ref[at, lanes],
                    (log[0:1], log[1:2]),
                    bias,
                    rate,
                    scale,
                )
                for part in range(3):
                    dqkv_ref[part, at, lanes] = grads[part]

        for part in range(3):
            split_rows(
                nn(a2t_ref[...], dqkv_ref[part]), keep_ref, send_ref, (part + 1, 0), room_ref, me_ref
            )
            u_ref[...] += nt(dqkv_ref[part], wq_ref[part, 0])

        @pl.when(h == shares - 1)
        def _():
            change, sums = norm_back(u_ref[...], x1_ref[...], gb_ref[1:2])
            go_ref[...] = g_ref[...] + change
            sums_ref[...] = sums

    grad, keep, send, sums = call(
        body,
        (shares,),
        [
            SCALARS,
            whole(grad.shape),
            whole(x1.shape),
            pl.BlockSpec((3, t, width), lambda h: (0, 0, h)),
            pl.BlockSpec((t, width), lambda h: (0, h)),
            pl.BlockSpec((1,) + logs.shape[1:], lambda h: (h, 0, 0, 0, 0)),
            slabs(1, 7, width, d),
            slabs(3, 3, width, d),
            whole(gb.shape),
        ],
        [
            made((t, d), F32),
            *halves.array((4, shares), (4, 1), lambda h: (0, h)),
            made((2, d), F32),
        ],
        [
            pltpu.VMEM((t, d), BF16),
            pltpu.VMEM((d, t), BF16),
            pltpu.VMEM((d, t), BF16),
            pltpu.VMEM((t, width), BF16),
            pltpu.VMEM((3, t, width), BF16),
            pltpu.VMEM((t, d), F32),
            halves.room(),
        ],
        (me, grad, x1, qkv, o2, logs, w, w, gb),
        flops=2 * t * d * d * 8,
    )
    return grad, (keep, send), sums


def mix_fits(depth, shards, shares):
    return depth // (shards * shares) % 8 == 0


def middle_backward(rows, grad, y1, o1, w, mix, me, halves, shards):
    t, d = grad.shape
    width = w.shape[3]
    shares = w.shape[1]
    fits = mix_fits(d, shards, shares)
    part = d // (shards * shares)

    def body(me_ref, g_ref, y1_ref, o1_ref, to_ref, mix_ref, *rest):
        send_refs, rest = rest[: rows.ways], rest[rows.ways :]
        gk_ref, gs_ref, *rest = rest
        if fits:
            room_ref, order_ref = rest
        else:
            gm_ref, room_ref = rest
        e1 = g_ref[...].astype(BF16)
        dy1 = nt(e1, mix_ref[...]).astype(BF16)
        sends = [rows.to_time(k, me_ref[3]) for k in range(rows.ways)]
        for h in range(shares):
            lanes = slice(h * width, (h + 1) * width)
            do1 = nn(dy1, to_ref[0, h]).astype(BF16)
            for k in range(rows.ways):
                send_refs[k][:, lanes] = nn(sends[k], do1).astype(BF16)
            split_rows(tn(dy1, o1_ref[:, lanes]), gk_ref, gs_ref, (0, h), room_ref, me_ref)
        gm = tn(y1_ref[...], e1)
        if fits:
            gm = gm.reshape(shards, shares, part, d)
            for h in range(shares):
                for half in range(shares):
                    order_ref[:, half] = gm[:, h, :, half * width : (half + 1) * width]
                split_rows(order_ref[...], gk_ref, gs_ref, (1, h), room_ref, me_ref)
        else:
            gm_ref[...] = gm.astype(BF16)

    outs = rows.chunks(d)
    outs += halves.array((1 + fits, shares), (1 + fits, shares), lambda i: (0, 0))
    scratch = [halves.room()]
    if fits:
        scratch.append(pltpu.VMEM((shards, shares, part, width), F32))
    else:
        outs.append(made((d, d), BF16))
    got = call(
        body,
        (1,),
        [
            SCALARS,
            whole(grad.shape),
            whole(y1.shape),
            whole(o1.shape),
            pl.BlockSpec((1, shares, d, width), lambda i: (6, 0, 0, 0)),
            whole(mix.shape),
        ],
        outs,
        scratch,
        (me, grad, y1, o1, w, mix),
        flops=8 * t * d * d,
    )
    do1, (keep, send) = got[: rows.ways], got[rows.ways : rows.ways + 2]
    if not fits:
        gm = mix_slab(got[-1], shards, shares).reshape((1, shares, halves.pairs, 2) + keep.shape[3:])
        keep = jnp.concatenate((keep, lax.dynamic_index_in_dim(gm, me[0], 3, keepdims=False)), axis=0)
        send = jnp.concatenate((send, lax.dynamic_index_in_dim(gm, 1 - me[0], 3, keepdims=False)), axis=0)
    return do1, (keep, send)


def time_backward(rows, do1, a, qkv, logs, w, me, halves):
    t, d = a.shape
    width = w.shape[3]
    shares = w.shape[1]
    pairs = width // LANES
    scale = 1.0 / math.sqrt(HEAD_DIM)
    rate = LOG2E * scale

    def body(me_ref, *refs):
        do_refs, refs = refs[: rows.ways], refs[rows.ways :]
        a_ref, qkv_ref, log_ref, w_ref = refs[:4]
        out_refs, refs = refs[4 : 4 + rows.ways], refs[4 + rows.ways :]
        half_refs, refs = refs[:6], refs[6:]
        bias_ref, dqkv_ref, at_ref, u_ref, room_ref, do_ref = refs
        h = pl.program_id(0)

        @pl.when(h == 0)
        def _():
            bias_ref[...] = rows.time_bias()
            at_ref[...] = a_ref[...].T
            u_ref[...] = jnp.zeros((t, d), F32)

        for k in range(rows.ways):
            do_ref[k * rows.chunk : (k + 1) * rows.chunk] = do_refs[k][...]

        @pl.loop(0, pairs)
        def _(i):
            lanes = pl.ds(pl.multiple_of(i * LANES, LANES), LANES)
            log = log_ref[0, i]
            grads = pair_backward(
                qkv_ref[0, :, lanes],
                qkv_ref[1, :, lanes],
                qkv_ref[2, :, lanes],
                do_ref[:, lanes],
                (log[0:1], log[1:2]),
                bias_ref[...],
                rate,
                scale,
            )
            for part in range(3):
                dqkv_ref[part, :, lanes] = grads[part]

        for part in range(3):
            value = nn(at_ref[...], dqkv_ref[part])
            split_rows(value, half_refs[2 * part], half_refs[2 * part + 1], (0, 0), room_ref, me_ref)
            u_ref[...] += nt(dqkv_ref[part], w_ref[part, 0])

        @pl.when(h == shares - 1)
        def _():
            for k in range(rows.ways):
                out_refs[k][...] = u_ref[k * rows.chunk : (k + 1) * rows.chunk].astype(BF16)

    got = call(
        body,
        (shares,),
        [
            SCALARS,
            *(pl.BlockSpec((rows.chunk, width), lambda h: (0, h)) for _ in do1),
            whole(a.shape),
            pl.BlockSpec((3, t, width), lambda h: (0, 0, h)),
            pl.BlockSpec((1,) + logs.shape[1:], lambda h: (h, 0, 0, 0)),
            slabs(3, 0, width, d),
        ],
        [
            *rows.chunks(d),
            *(one for _ in range(3) for one in halves.array((1, shares), (1, 1), lambda h: (0, h))),
        ],
        [
            pltpu.VMEM((t, t), F32),
            pltpu.VMEM((3, t, width), BF16),
            pltpu.VMEM((d, t), BF16),
            pltpu.VMEM((t, d), F32),
            halves.room(),
            pltpu.VMEM((t, width), BF16),
        ],
        (me, *do1, a, qkv, logs, w),
        flops=2 * t * d * d * 6,
    )
    parts = got[rows.ways :]
    return got[: rows.ways], [tuple(parts[i : i + 2]) for i in (0, 2, 4)]


def first_norm_back(rows, back, x, grad, gb, me):
    t, d = x.shape

    def body(me_ref, *refs):
        x_ref, g_ref, gb_ref, go_ref, sums_ref = refs[rows.ways :]
        u = rows.gathered(refs[: rows.ways], me_ref[3])
        change, sums = norm_back(u, x_ref[...], gb_ref[0:1])
        go_ref[...] = g_ref[...] + change
        sums_ref[...] = sums

    return call(
        body,
        (1,),
        [SCALARS, *(whole(c.shape) for c in back), whole(x.shape), whole(grad.shape), whole(gb.shape)],
        [made((t, d), F32), made((2, d), F32)],
        [],
        (me, *back, x, grad, gb),
    )


def homes():
    clips, ways = lax.axis_size("clip"), lax.axis_size("seq")
    pairs = []
    for clip in range(clips):
        for seq in range(ways):
            home_clip = clip - clip % 2 + seq % 2
            home_seq = seq // 2 + (ways // 2) * (clip % 2)
            pairs.append((clip * ways + seq, home_clip * ways + home_seq))
    return pairs


def go_home(a):
    return lax.ppermute(a, ("clip", "seq"), homes())


def go_back(a):
    return lax.ppermute(a, ("clip", "seq"), [(home, device) for device, home in homes()])


def member_of(clip, seq):
    return clip % 2 + 2 * (seq % (lax.axis_size("seq") // 2))


def swap_places(chunks):
    clips, ways = lax.axis_size("clip"), lax.axis_size("seq")
    got = [chunks[0]]
    for k in range(1, ways):
        pairs = []
        for clip in range(clips):
            for seq in range(ways):
                other = member_of(clip, seq) ^ k
                to_clip = clip - clip % 2 + other % 2
                to_seq = seq - seq % (ways // 2) + other // 2
                pairs.append((clip * ways + seq, to_clip * ways + to_seq))
        got.append(lax.ppermute(chunks[k], ("clip", "seq"), pairs))
    return got


def columns(a, r, width):
    return a.reshape(r, -1, width).transpose(1, 0, 2)


def pack_attention(time_qkv, time_out, time_mix, space_qkv, space_out):
    r, _, width = time_qkv.shape
    mix = time_mix.reshape(-1, time_mix.shape[1] // width, width).transpose(1, 0, 2).reshape(1, r, width)
    return jnp.concatenate(
        (
            columns(time_qkv, r, width),
            columns(space_qkv, r, width),
            time_out.T[None],
            space_out.T[None],
            mix,
        ),
        axis=0,
    )


def pack_feed_forward(mlp_in, mlp_out, width):
    r = mlp_in.shape[0]
    return jnp.concatenate((columns(mlp_in, r, width), columns(mlp_out.T, r, width)), axis=0)


def gather_slabs(pack):
    full = lax.all_gather(pack, ("head", "clip", "seq"), axis=1, tiled=True)
    return full.reshape(pack.shape[0], lax.axis_size("head"), -1, pack.shape[2])


def spread_slabs(pack, me):
    ways, clips = lax.axis_size("seq"), lax.axis_size("clip")
    shares = lax.axis_size("head")
    n, r, width = pack.shape
    turned = [pack] + [
        lax.ppermute(pack, "seq", [(i, (i + k) % ways) for i in range(ways)]) for k in range(1, ways)
    ]
    runs = []
    for steps, first, second in (((0, 1), "x", "h"), ((3, 2), "h", "x")):
        some = jnp.stack([turned[k] for k in steps])
        some = jnp.concatenate((some, cross(some, first)), axis=0)
        where = [(k, {first: f}) for f in (0, 1) for k in steps]
        for g, blocks in enumerate((some, cross(some, second))):
            runs.append((blocks, [(k, {**at, second: g}) for k, at in where], 0))
    runs += [(cross(blocks, "c"), where, 1) for blocks, where, _ in runs]
    count = sum(len(where) for _, where, _ in runs)

    def body(me_ref, *refs):
        sources, out_ref, sems = refs[: len(runs)], refs[-2], refs[-1]
        copies = []
        for source, (_, where, core) in zip(sources, runs):
            for i, (k, at) in enumerate(where):
                share = jnp.bitwise_xor(me_ref[2], at["h"])
                clip = 2 * jnp.bitwise_xor(me_ref[1], at["x"]) + jnp.bitwise_xor(me_ref[0], core)
                seq = lax.rem(me_ref[4] + (ways - k), ways)
                copies.append(
                    pltpu.make_async_copy(
                        source.at[i], out_ref.at[:, share, clip * ways + seq], sems.at[len(copies)]
                    )
                )
        for copy in copies:
            copy.start()
        for copy in copies:
            copy.wait()

    full = pl.pallas_call(
        body,
        out_shape=jax.ShapeDtypeStruct((n, shares, clips * ways, r, width), BF16),
        in_specs=[SCALARS] + [pl.BlockSpec(memory_space=pltpu.HBM)] * len(runs),
        out_specs=pl.BlockSpec(memory_space=pltpu.HBM),
        scratch_shapes=[pltpu.SemaphoreType.DMA((count,))],
        compiler_params=pltpu.CompilerParams(vmem_limit_bytes=VMEM),
        cost_estimate=pl.CostEstimate(
            flops=0, bytes_accessed=4 * n * shares * clips * ways * r * width, transcendentals=0
        ),
    )(me, *(blocks for blocks, _, _ in runs))
    return full.reshape(n, shares, clips * ways * r, width)


def mix_whole(slab, shards):
    shares, depth, width = slab.shape
    part = slab.reshape(shares, shards, shares, depth // (shards * shares), width)
    return part.transpose(1, 0, 3, 2, 4).reshape(depth, shares * width)


def mix_slab(whole_grad, shards, shares):
    depth, full = whole_grad.shape
    width = full // shares
    part = whole_grad.reshape(shards, shares, depth // (shards * shares), shares, width)
    return part.transpose(1, 0, 3, 2, 4).reshape(1, shares, depth, width)


class Piece:
    def __init__(self, keep, got, first, n, order):
        self.near = (keep, got)
        self.first = first
        self.n = n
        self.order = order
        self.step = 0
        self.held = []
        self.result = None


PLACE = {"x": 1, "h": 2}


def fold(pieces, me, last_by_rows):
    ways = lax.axis_size("seq")
    depth, width = pieces[0].near[0].shape[-2:]
    r = depth // ways
    used = {}
    arrays = []

    def number(a):
        for i, known in enumerate(arrays):
            if known is a:
                return i
        arrays.append(a)
        return len(arrays) - 1

    plans = []
    for p in pieces:
        link = p.order[p.step] if p.step < 2 else "z"
        blocks = p.n * (2 if p.step == 0 else 1)
        base = used.get(link, 0)
        used[link] = base + blocks
        near = [number(a) for a in p.near]
        held = [(number(a), at) for a, at in p.held]
        plans.append((p, link, base, near, held))
    links = sorted(used)
    shapes = [
        (ways, used[k], r, width) if k == "z" and last_by_rows else (used[k], depth, width)
        for k in links
    ]
    rooms, counts = [], []
    for p, link, base, near, held in plans:
        each = 2 if p.step == 0 else 1
        counts.append((each, len(near) + len(held)))
        rooms += [(each * p.n, depth, width)] * (len(near) + len(held))
    copies_needed = sum(each * terms for each, terms in counts)

    def body(me_ref, *refs):
        sources = refs[: len(arrays)]
        outs = dict(zip(links, refs[len(arrays) : len(arrays) + len(links)]))
        held_refs = refs[len(arrays) + len(links) : -1]
        sems = refs[-1]
        mine = {name: me_ref[PLACE[name]] for name in PLACE}
        groups = []
        room = 0
        sem = 0
        for p, link, base, near, held in plans:
            group = []
            if p.step == 0:
                for term in near:
                    for k in range(2):
                        pick = {p.order[0]: 1 - mine[p.order[0]], p.order[1]: k}
                        source = sources[term].at[pl.ds(p.first, p.n), pick["h"], pick["x"]]
                        group.append((source, held_refs[room].at[pl.ds(k * p.n, p.n)]))
                    room += 1
            else:
                last = p.order[1]
                pick = {p.order[0]: mine[p.order[0]]}
                pick[last] = 1 - mine[last] if p.step == 1 else mine[last]
                for term in near:
                    source = sources[term].at[pl.ds(p.first, p.n), pick["h"], pick["x"]]
                    group.append((source, held_refs[room]))
                    room += 1
                for i, (term, at) in enumerate(held):
                    start = at + pick[last] * p.n if i == 0 else at
                    group.append((sources[term].at[pl.ds(start, p.n)], held_refs[room]))
                    room += 1
            made_copies = []
            for source, target in group:
                made_copies.append(pltpu.make_async_copy(source, target, sems.at[sem]))
                sem += 1
            groups.append(made_copies)
        for group in groups:
            for copy in group:
                copy.start()
        room = 0
        for (p, link, base, near, held), (each, terms), group in zip(plans, counts, groups):
            these = held_refs[room : room + terms]
            room += terms
            for copy in group:
                copy.wait()

            @pl.loop(0, each * p.n)
            def _(i, these=these, base=base, out=outs[link], last=p.step == 2 and last_by_rows):
                value = these[0][i].astype(F32)
                for one in these[1:]:
                    value = value + one[i].astype(F32)
                value = value.astype(BF16)
                if last:
                    for k in range(ways):
                        out[k, base + i] = value[k * r : (k + 1) * r]
                else:
                    out[base + i] = value

    moved = sum(2 * math.prod(room) for room in rooms) + sum(2 * math.prod(shape) for shape in shapes)
    sums = pl.pallas_call(
        body,
        out_shape=[jax.ShapeDtypeStruct(shape, BF16) for shape in shapes],
        in_specs=[SCALARS] + [pl.BlockSpec(memory_space=pltpu.HBM)] * len(arrays),
        out_specs=[pl.BlockSpec(memory_space=pltpu.VMEM)] * len(links),
        scratch_shapes=[pltpu.VMEM(room, BF16) for room in rooms]
        + [pltpu.SemaphoreType.DMA((copies_needed,))],
        compiler_params=pltpu.CompilerParams(vmem_limit_bytes=VMEM),
        cost_estimate=pl.CostEstimate(flops=0, bytes_accessed=moved, transcendentals=0),
    )(me, *arrays)
    return [(p, link, base) for p, link, base, _, _ in plans], dict(zip(links, sums))


def cross(a, name):
    axis, bit = ("head", 0) if name == "h" else ("clip", 1 if name == "x" else 0)
    size = lax.axis_size(axis)
    return lax.ppermute(a, axis, [(i, i ^ (1 << bit)) for i in range(size)])


def pieces_of(halves_of):
    total = sum(keep.shape[0] for keep, _ in halves_of)
    found = []
    seen = 0
    for keep, send in halves_of:
        got = cross(send, "c")
        n = keep.shape[0]
        first = min(max((total + 1) // 2 - seen, 0), n)
        if first:
            found.append(Piece(keep, got, 0, first, ("x", "h")))
        if n > first:
            found.append(Piece(keep, got, first, n - first, ("h", "x")))
        seen += n
    return found


def move(x, pieces, me, at_end=False):
    plans, sums = fold(pieces, me, at_end)
    x, sums = lax.optimization_barrier((x, sums))
    got = {}
    for link, array in sums.items():
        if link == "z":
            if at_end:
                every = lax.all_to_all(array, "seq", split_axis=0, concat_axis=0, tiled=True)
                got[link] = jnp.sum(every.astype(F32), axis=0)
            else:
                own = lax.psum_scatter(array, "seq", scatter_dimension=1, tiled=True)
                got[link] = own.astype(F32)
        else:
            got[link] = cross(array, link)
    for p, link, base in plans:
        if link == "z":
            p.result = got[link][base : base + p.n]
        else:
            p.held.append((got[link], base))
        p.step += 1
    return x


def settle(x, pieces):
    arrays = []
    for p in pieces:
        if not any(p.held[-1][0] is a for a in arrays):
            arrays.append(p.held[-1][0])
    x, came = lax.optimization_barrier((x, arrays))
    for p in pieces:
        for old, new in zip(arrays, came):
            if p.held[-1][0] is old:
                p.held[-1] = (new, p.held[-1][1])
                break
    return x


def reduce_plain(halves_of, core):
    def joined(keep, send):
        low = jnp.where(core == 0, keep, send)
        high = jnp.where(core == 0, send, keep)
        n, shares, pairs, depth, width = keep.shape
        return jnp.stack((low, high), axis=3).reshape(n, shares, 2 * pairs * depth, width)

    g = jnp.concatenate([joined(*pair) for pair in halves_of], axis=0)
    g = lax.psum_scatter(g, "head", scatter_dimension=1, tiled=True)
    g = lax.psum_scatter(g.astype(F32), ("clip", "seq"), scatter_dimension=2, tiled=True)
    return g[:, 0]


def gather_norms(gain, bias):
    layers, norms, part = gain.shape
    both = jnp.concatenate((gain, bias), axis=1).reshape(1, -1)
    count = lax.axis_size("clip") * lax.axis_size("seq") * lax.axis_size("head")
    width = round_up(both.shape[1], 128)
    padded = jnp.pad(both, ((0, 0), (0, width - both.shape[1])))
    every = lax.all_to_all(
        jnp.broadcast_to(padded, (count, width)), ALL, split_axis=0, concat_axis=0, tiled=True
    )[:, : both.shape[1]]
    return every.reshape(count, layers * 2 * norms, part).transpose(1, 0, 2).reshape(layers, 2 * norms, -1)


def reduce_norms(sums):
    count = lax.axis_size("clip") * lax.axis_size("seq") * lax.axis_size("head")
    rows, features = sums.shape
    part = features // count
    a = sums.reshape(rows, count, part).transpose(1, 0, 2).reshape(count, rows * part)
    width = round_up(rows * part, 128)
    a = jnp.pad(a, ((0, 0), (0, width - rows * part)))
    every = lax.all_to_all(a, ALL, split_axis=0, concat_axis=0, tiled=True)
    return jnp.sum(every, axis=0)[: rows * part].reshape(rows, part)


def on_device(
    tokens,
    cotangent,
    time_qkv,
    time_out,
    time_mix,
    space_qkv,
    space_out,
    mlp_in,
    mlp_out,
    norm_gain,
    norm_bias,
):
    layers = time_qkv.shape[0]
    clips, frames, places, d = tokens.shape
    ways = lax.axis_size("seq")
    shards = lax.axis_size("clip") * ways
    rows = Rows(clips * frames, places, ways)
    shares = lax.axis_size("head")

    def as_rows(a):
        a = a.astype(F32).reshape(rows.frames, places, d)
        a = jnp.pad(a, ((0, 0), (0, rows.frame_rows - places), (0, 0)))
        return a.reshape(rows.rows, d)

    def from_rows(a):
        a = a.reshape(rows.frames, rows.frame_rows, d)[:, :places]
        return a.reshape(tokens.shape)

    gbs = gather_norms(norm_gain, norm_bias)
    gb = [gbs[l] for l in range(layers)]
    packs = [
        pack_attention(time_qkv[l], time_out[l], time_mix[l], space_qkv[l], space_out[l])
        for l in range(layers)
    ]
    packs_ff = [pack_feed_forward(mlp_in[l], mlp_out[l], time_qkv.shape[3]) for l in range(layers)]
    weights = [gather_slabs(pack) for pack in packs]
    mixes = [mix_whole(w[-1], shards) for w in weights]
    quick = lax.axis_size("clip") == 4 and shares == 2 and ways == 4 and time_qkv.shape[1] % 16 == 0

    halves = Halves(lax.axis_size("clip"), d, time_qkv.shape[3])
    clip = lax.axis_index("clip")
    member = member_of(clip, lax.axis_index("seq"))
    me = jnp.stack((clip & 1, (clip >> 1) & 1, lax.axis_index("head"), member, lax.axis_index("seq"))).astype(
        jnp.int32
    )
    if quick:
        weights_ff = [spread_slabs(pack, me) for pack in packs_ff]
    else:
        weights_ff = [gather_slabs(pack) for pack in packs_ff]

    x = as_rows(go_home(tokens))
    send = send_first(rows, x, gb[0], me)
    kept = []
    for l in range(layers):
        w = weights[l]
        send = swap_places(send)
        if quick and l == 0:
            send, weights_ff[l] = lax.optimization_barrier((send, weights_ff[l]))
        a1, qkv1, log1, o1_time = time_forward(rows, send, w)
        back = swap_places(o1_time)
        o1, y1, x1, qkv2 = middle_forward(rows, back, x, w, mixes[l], gb[l], me)
        if quick and l == 0:
            x1, weights_ff[1:] = lax.optimization_barrier((x1, weights_ff[1:]))
        o2, x2, log2 = space_forward(rows, qkv2, x1, w)
        kept.append((x, a1, qkv1, log1, o1, y1, x1, qkv2, o2, log2, x2))
        if l + 1 < layers:
            x, *send = mlp_forward(rows, x2, weights_ff[l], gb[l], gb[l + 1], me)

    grad = as_rows(go_home(cotangent))
    norm_rows = [None] * layers
    summed = [None] * layers
    late = []
    for l in reversed(range(layers)):
        w = weights[l]
        x, a1, qkv1, log1, o1, y1, x1, qkv2, o2, log2, x2 = kept[l]
        grad, g_ff, s3, x3 = mlp_backward(
            rows, grad, x2, weights_ff[l], gb[l], me, halves, l + 1 == layers
        )
        if x3:
            output = go_back(from_rows(x3[0].astype(BF16)))
        if quick:
            ff = pieces_of(g_ff)
            if late:
                grad = settle(grad, late)
                grad = move(grad, late, me)
                late = [p for p in late if p.step < 3]
        grad, g_space, s2 = space_backward(rows, grad, x1, qkv2, o2, log2, w, gb[l], me, halves)
        if quick:
            space = pieces_of([g_space])
            if late:
                grad = settle(grad, late)
            grad, output = move((grad, output), ff, me)
        do1, g_out = middle_backward(rows, grad, y1, o1, w, mixes[l], me, halves, shards)
        do1 = swap_places(do1)
        if quick:
            do1 = move(do1, ff + space + late, me)
        da1, g_time = time_backward(rows, do1, a1, qkv1, log1, w, me, halves)
        if quick:
            da1 = settle(da1, ff + space)
        da1 = swap_places(da1)
        if quick:
            rest = pieces_of([g_out] + g_time)
            da1 = move(da1, ff + space + rest, me)
            late = space + rest
        grad, s1 = first_norm_back(rows, da1, x, grad, gb[l], me)
        norm_rows[l] = jnp.concatenate((s1[0:1], s2[0:1], s3[0:1], s1[1:2], s2[1:2], s3[1:2]), axis=0)
        if quick:
            summed[l] = ff + space + rest
        else:
            summed[l] = [reduce_plain(g_ff + [g_space, g_out] + g_time, clip & 1)]
    if quick:
        tokens_grad = move(go_back(from_rows(grad.astype(BF16))), late, me, True)
        move((), rest, me, True)
        summed = [[p.result for p in some] for some in summed]
    cuts = (2 * g_ff[0][0].shape[0], g_space[0].shape[0], g_out[0].shape[0], len(g_time))
    results = []
    for some in summed:
        slabs_of = jnp.concatenate(some, axis=0)
        ends = [sum(cuts[: i + 1]) for i in range(4)]
        results.append([slabs_of[e - c : e] for c, e in zip(cuts, ends)])
    if not quick:
        tokens_grad = go_back(from_rows(grad.astype(BF16)))
    tokens_grad = tokens_grad.astype(F32)
    norm_sums = reduce_norms(jnp.concatenate(norm_rows, axis=0)).reshape(layers, 2, 3, -1)

    def stacked(form):
        return jnp.stack([form(*results[l]) for l in range(layers)])

    def rows_of(a):
        return a.transpose(1, 0, 2)

    def flat(a):
        return rows_of(a).reshape(a.shape[1], -1)

    def mix_rows(a):
        r, width = a.shape
        return a.reshape(shares, r // shares, width).transpose(1, 0, 2).reshape(r // shares, -1)

    per_share = mlp_in.shape[2] // time_qkv.shape[3]
    return (
        output,
        tokens_grad,
        stacked(lambda ff, s, t, q: rows_of(q)),
        stacked(lambda ff, s, t, q: t[0].T),
        stacked(lambda ff, s, t, q: mix_rows(t[1])),
        stacked(lambda ff, s, t, q: rows_of(s[1:])),
        stacked(lambda ff, s, t, q: s[0].T),
        stacked(lambda ff, s, t, q: flat(ff[:per_share])),
        stacked(lambda ff, s, t, q: flat(ff[per_share:]).T),
        norm_sums[:, 0],
        norm_sums[:, 1],
    )


def solution(mesh):
    token_spec = P(("clip", "head"), "seq", None, None)
    in_specs = (
        token_spec,
        token_spec,
        P(None, ("clip", "seq"), None, "head"),
        P(None, "head", ("clip", "seq")),
        P(None, ("clip", "seq", "head"), None),
        P(None, ("clip", "seq"), None, "head"),
        P(None, "head", ("clip", "seq")),
        P(None, ("clip", "seq"), "head"),
        P(None, "head", ("clip", "seq")),
        P(None, None, ("clip", "seq", "head")),
        P(None, None, ("clip", "seq", "head")),
    )
    return jax.shard_map(
        on_device, mesh=mesh, in_specs=in_specs, out_specs=in_specs, check_vma=False
    )
```

```python
import functools
import math

import jax
import jax.numpy as jnp
from jax import lax
from jax.experimental import pallas as pl
from jax.experimental.pallas import tpu as pltpu
from jax.sharding import PartitionSpec as P

HEAD_DIM = 64
NORM_EPS = 1e-06
HALF_ROOT = 0.7071067811865476
INV_ROOT_TAU = 0.3989422804014327
LOG2E = 1.4426950408889634
FAR = -1e30
LANES = 128
VMEM = 56 * 1024 * 1024
SHOWN = 1.0
ALL = ("clip", "seq", "head")
BF16 = jnp.bfloat16
F32 = jnp.float32


def round_up(value, step):
    return -(-value // step) * step


def nn(a, b):
    return lax.dot_general(a, b, (((1,), (0,)), ((), ())), preferred_element_type=F32)


def nt(a, b):
    return lax.dot_general(a, b, (((1,), (1,)), ((), ())), preferred_element_type=F32)


def tn(a, b):
    return lax.dot_general(a, b, (((0,), (0,)), ((), ())), preferred_element_type=F32)


def norm_parts(x):
    mean = jnp.mean(x, axis=-1, keepdims=True)
    centred = x - mean
    spread = lax.rsqrt(jnp.mean(centred * centred, axis=-1, keepdims=True) + NORM_EPS)
    return centred * spread, spread


def norm_rounded(x, gain, bias):
    hat, _ = norm_parts(x)
    return (hat * gain + bias).astype(BF16)


def norm_back(u, x, gain):
    hat, spread = norm_parts(x)
    scaled = u * gain
    mean_scaled = jnp.mean(scaled, axis=-1, keepdims=True)
    mean_cross = jnp.mean(scaled * hat, axis=-1, keepdims=True)
    change = spread * (scaled - mean_scaled - hat * mean_cross)
    sums = jnp.concatenate(
        (jnp.sum(u * hat, axis=0, keepdims=True), jnp.sum(u, axis=0, keepdims=True)), axis=0
    )
    return change, sums


class Rows:
    def __init__(self, frames, places, ways):
        self.frames = frames
        self.places = places
        self.ways = ways
        self.frame_rows = round_up(places, 16)
        self.rows = frames * self.frame_rows
        self.block = places // ways
        self.chunk = round_up(frames * self.block, 8)
        self.time_rows = ways * self.chunk

    def split(self, r):
        way = jnp.zeros_like(r)
        for k in range(1, self.ways):
            way = way + (r >= k * self.chunk).astype(jnp.int32)
        rest = r - way * self.chunk
        frame = jnp.zeros_like(r)
        for k in range(1, self.frames):
            frame = frame + (rest >= k * self.block).astype(jnp.int32)
        real = rest < self.frames * self.block
        return way, frame, rest - frame * self.block, real

    def to_time(self, k, member):
        r = lax.broadcasted_iota(jnp.int32, (self.chunk, 1), 0)
        _, frame, place, real = self.split(r)
        way = jnp.bitwise_xor(member, k)
        source = jnp.where(real, frame * self.frame_rows + way * self.block + place, -1)
        c = lax.broadcasted_iota(jnp.int32, (self.chunk, self.rows), 1)
        return jnp.where(c == source, 1.0, 0.0).astype(BF16)

    def gathered(self, chunk_refs, member):
        total = tn(self.to_time(0, member), chunk_refs[0][...])
        for k in range(1, self.ways):
            total = total + tn(self.to_time(k, member), chunk_refs[k][...])
        return total

    def chunks(self, width, block=None, index=None):
        return [
            made((self.chunk, width), BF16)
            if block is None
            else made((self.chunk, width), BF16, (self.chunk, block), index)
            for _ in range(self.ways)
        ]

    def time_bias(self):
        def label(r):
            _, _, place, real = self.split(r)
            return jnp.where(real, place, -1)

        a = label(lax.broadcasted_iota(jnp.int32, (self.time_rows, 1), 0))
        b = label(lax.broadcasted_iota(jnp.int32, (1, self.time_rows), 1))
        return jnp.where(a == b, 0.0, FAR).astype(F32)

    def space_bias(self):
        a = lax.broadcasted_iota(jnp.int32, (self.frame_rows, 1), 0)
        return jnp.where(a < self.places, 0.0, FAR).astype(F32)


def lane_masks(rows):
    lane = lax.broadcasted_iota(jnp.int32, (rows, LANES), 1)
    return lane < HEAD_DIM


def one_of(value, low, half):
    zero = jnp.zeros_like(value)
    return jnp.where(low, value, zero) if half == 0 else jnp.where(low, zero, value)


def pair_forward(q, k, v, bias, rate):
    low = lane_masks(q.shape[0])
    mixed, logs = [], []
    for half in range(2):
        s = nt(k, one_of(q, low, half)) + bias
        peak = jnp.max(s, axis=0, keepdims=True)
        e = jnp.exp2((s - peak) * rate)
        total = jnp.sum(e, axis=0, keepdims=True)
        soft = (e * (1.0 / total)).astype(BF16)
        mixed.append(tn(soft, v))
        logs.append(peak * rate + jnp.log2(total))
    return jnp.where(low, mixed[0], mixed[1]).astype(BF16), logs


def pair_backward(q, k, v, do, logs, bias, rate, scale):
    low = lane_masks(q.shape[0])
    dq, dk, dv = [], [], []
    for half in range(2):
        s = nt(k, one_of(q, low, half)) + bias
        soft = jnp.exp2(s * rate - logs[half])
        dp = nt(v, one_of(do, low, half))
        ds = (soft * (dp - jnp.sum(soft * dp, axis=0, keepdims=True))).astype(BF16)
        dv.append(nn(soft.astype(BF16), do))
        dk.append(nn(ds, q))
        dq.append(tn(ds, k))
    return (
        (jnp.where(low, dq[0], dq[1]) * scale).astype(BF16),
        (jnp.where(low, dk[0], dk[1]) * scale).astype(BF16),
        jnp.where(low, dv[0], dv[1]).astype(BF16),
    )


def split_rows(value, keep_ref, send_ref, at, room_ref, me_ref):
    mine = me_ref[0]
    room_ref[...] = value.reshape(room_ref.shape)
    keep_ref[at] = room_ref[:, mine].astype(BF16)
    send_ref[at] = room_ref[:, 1 - mine].astype(BF16)


class Halves:
    def __init__(self, clips, depth, width):
        self.pairs = clips // 2
        self.rows = depth // clips
        self.width = width

    def array(self, lead, block, index):
        tail = (self.pairs, self.rows, self.width)
        one = lambda: made(lead + tail, BF16, block + tail, lambda *g: index(*g) + (0, 0, 0))
        return [one(), one()]

    def room(self):
        return pltpu.VMEM((self.pairs, 2, self.rows, self.width), F32)


SCALARS = pl.BlockSpec(memory_space=pltpu.SMEM)


def call(body, grid, ins, outs, scratch, args, flops=0):
    specs = [spec for spec in ins]
    moved = sum(math.prod(o.shape) * o.dtype.itemsize for o, _ in outs)
    moved += sum(math.prod(a.shape) * a.dtype.itemsize for a in args)
    return pl.pallas_call(
        body,
        out_shape=[shape for shape, _ in outs],
        grid=grid,
        in_specs=specs,
        out_specs=[spec for _, spec in outs],
        scratch_shapes=scratch,
        compiler_params=pltpu.CompilerParams(vmem_limit_bytes=VMEM),
        cost_estimate=pl.CostEstimate(
            flops=int(flops * SHOWN), bytes_accessed=int(moved * SHOWN), transcendentals=0
        ),
    )(*args)


def whole(shape):
    zeros = (0,) * len(shape)
    return pl.BlockSpec(shape, lambda *_: zeros)


def made(shape, dtype, block=None, index=None):
    spec = whole(shape) if block is None else pl.BlockSpec(block, index)
    return jax.ShapeDtypeStruct(shape, dtype), spec


def slabs(count, first, width, depth):
    return pl.BlockSpec((count, 1, depth, width), lambda h, *_: (first // count, h, 0, 0))


def send_first(rows, x, gb, me):
    def body(me_ref, x_ref, gb_ref, *out_refs):
        a = norm_rounded(x_ref[...], gb_ref[0:1], gb_ref[3:4])
        for k in range(rows.ways):
            out_refs[k][...] = nn(rows.to_time(k, me_ref[3]), a).astype(BF16)

    d = x.shape[1]
    return call(
        body, (1,), [SCALARS, whole(x.shape), whole(gb.shape)], rows.chunks(d), [], (me, x, gb)
    )


def time_forward(rows, chunks, w):
    t, d = rows.time_rows, chunks[0].shape[1]
    width = w.shape[3]
    shares = w.shape[1]
    pairs = width // LANES
    ways = rows.ways
    rate = LOG2E / math.sqrt(HEAD_DIM)

    def body(*refs):
        chunk_refs = refs[:ways]
        w_ref, a_ref, qkv_ref, log_ref = refs[ways : ways + 4]
        out_refs = refs[ways + 4 : 2 * ways + 4]
        bias_ref, mixed_ref = refs[2 * ways + 4 :]

        @pl.when(pl.program_id(0) == 0)
        def _():
            bias_ref[...] = rows.time_bias()
            for k in range(ways):
                a_ref[k * rows.chunk : (k + 1) * rows.chunk] = chunk_refs[k][...]

        act = a_ref[...]
        for g in range(3):
            qkv_ref[g] = nn(act, w_ref[g, 0]).astype(BF16)

        @pl.loop(0, pairs)
        def _(i):
            lanes = pl.ds(pl.multiple_of(i * LANES, LANES), LANES)
            mixed, logs = pair_forward(
                qkv_ref[0, :, lanes], qkv_ref[1, :, lanes], qkv_ref[2, :, lanes], bias_ref[...], rate
            )
            mixed_ref[:, lanes] = mixed
            log_ref[0, i] = jnp.concatenate(logs, axis=0)

        for k in range(ways):
            out_refs[k][...] = mixed_ref[k * rows.chunk : (k + 1) * rows.chunk]

    got = call(
        body,
        (shares,),
        [whole(c.shape) for c in chunks] + [slabs(3, 0, width, d)],
        [
            made((t, d), BF16),
            made((3, t, d), BF16, (3, t, width), lambda h: (0, 0, h)),
            made((shares, pairs, 2, t), F32, (1, pairs, 2, t), lambda h: (h, 0, 0, 0)),
            *rows.chunks(d, width, lambda h: (0, h)),
        ],
        [pltpu.VMEM((t, t), F32), pltpu.VMEM((t, width), BF16)],
        (*chunks, w),
        flops=2 * t * d * 3 * d,
    )
    return got[0], got[1], got[2], got[3:]


def middle_forward(rows, back, x, w, mix, gb, me):
    t, d = x.shape
    width = w.shape[3]
    shares = w.shape[1]

    def body(me_ref, *refs):
        x_ref, to_ref, sq_ref, mix_ref, gb_ref, o1_ref, y1_ref, x1_ref, qkv_ref = refs[rows.ways :]
        o1 = rows.gathered(refs[: rows.ways], me_ref[3]).astype(BF16)
        o1_ref[...] = o1
        y1 = jnp.zeros((t, d), F32)
        for h in range(shares):
            y1 = y1 + nt(o1[:, h * width : (h + 1) * width], to_ref[0, h])
        y1 = y1.astype(BF16)
        y1_ref[...] = y1
        x1 = x_ref[...] + nn(y1, mix_ref[...])
        x1_ref[...] = x1
        a2 = norm_rounded(x1, gb_ref[1:2], gb_ref[4:5])
        for g in range(3):
            for h in range(shares):
                qkv_ref[g, :, h * width : (h + 1) * width] = nn(a2, sq_ref[g, h]).astype(BF16)

    return call(
        body,
        (1,),
        [
            SCALARS,
            *(whole(c.shape) for c in back),
            whole(x.shape),
            pl.BlockSpec((1, shares, d, width), lambda i: (6, 0, 0, 0)),
            pl.BlockSpec((3, shares, d, width), lambda i: (1, 0, 0, 0)),
            whole(mix.shape),
            whole(gb.shape),
        ],
        [made((t, d), BF16), made((t, d), BF16), made((t, d), F32), made((3, t, d), BF16)],
        [],
        (me, *back, x, w, w, mix, gb),
        flops=2 * t * d * 5 * d,
    )


def space_forward(rows, qkv, x1, w):
    t, d = x1.shape
    width = w.shape[3]
    shares = w.shape[1]
    pairs = width // LANES
    rate = LOG2E / math.sqrt(HEAD_DIM)
    n = rows.frame_rows

    def body(qkv_ref, x1_ref, w_ref, o2_ref, x2_ref, log_ref):
        bias = rows.space_bias()

        @pl.loop(0, pairs)
        def _(i):
            lanes = pl.ds(pl.multiple_of(i * LANES, LANES), LANES)
            for f in range(rows.frames):
                at = slice(f * n, (f + 1) * n)
                mixed, logs = pair_forward(
                    qkv_ref[0, at, lanes], qkv_ref[1, at, lanes], qkv_ref[2, at, lanes], bias, rate
                )
                o2_ref[at, lanes] = mixed
                log_ref[0, i, f] = jnp.concatenate(logs, axis=0)

        @pl.when(pl.program_id(0) == 0)
        def _():
            x2_ref[...] = x1_ref[...]

        x2_ref[...] += nt(o2_ref[...], w_ref[0, 0])

    return call(
        body,
        (shares,),
        [
            pl.BlockSpec((3, t, width), lambda h: (0, 0, h)),
            whole(x1.shape),
            slabs(1, 7, width, d),
        ],
        [
            made((t, d), BF16, (t, width), lambda h: (0, h)),
            made((t, d), F32),
            made(
                (shares, pairs, rows.frames, 2, n),
                F32,
                (1, pairs, rows.frames, 2, n),
                lambda h: (h, 0, 0, 0, 0),
            ),
        ],
        [],
        (qkv, x1, w),
        flops=2 * t * d * d,
    )


def ff_slab(first, per_share, depth, width):
    return pl.BlockSpec(
        (1, 1, depth, width), lambda j: (first + j % per_share, j // per_share, 0, 0)
    )


def mlp_forward(rows, x2, w, gb, gb_next, me):
    t, d = x2.shape
    width = w.shape[3]
    shares = w.shape[1]
    per_share = w.shape[0] // 2
    steps = shares * per_share

    def body(x2_ref, wi_ref, wo_ref, gb_ref, me_ref, gn_ref, x3_ref, *rest):
        send_refs, a3_ref = rest[:-1], rest[-1]
        j = pl.program_id(0)

        @pl.when(j == 0)
        def _():
            a3_ref[...] = norm_rounded(x2_ref[...], gb_ref[2:3], gb_ref[5:6])
            x3_ref[...] = x2_ref[...]

        hid = nn(a3_ref[...], wi_ref[0, 0])
        act = (0.5 * hid * (1.0 + lax.erf(hid * HALF_ROOT))).astype(BF16)
        x3_ref[...] += nt(act, wo_ref[0, 0])

        @pl.when(j == steps - 1)
        def _():
            a = norm_rounded(x3_ref[...], gn_ref[0:1], gn_ref[3:4])
            for k in range(rows.ways):
                send_refs[k][...] = nn(rows.to_time(k, me_ref[3]), a).astype(BF16)

    ins = [
        whole(x2.shape),
        ff_slab(0, per_share, d, width),
        ff_slab(per_share, per_share, d, width),
        whole(gb.shape),
    ]
    ins += [SCALARS, whole(gb_next.shape)]
    outs = [made((t, d), F32)] + rows.chunks(d)
    args = (x2, w, w, gb, me, gb_next)
    return call(
        body, (steps,), ins, outs, [pltpu.VMEM((t, d), BF16)], args, flops=4 * t * d * width * steps
    )


def mlp_backward(rows, grad, x2, w, gb, me, halves, with_output):
    t, d = x2.shape
    width = w.shape[3]
    shares = w.shape[1]
    per_share = w.shape[0] // 2
    steps = shares * per_share

    def body(me_ref, g_ref, x2_ref, wi_ref, wo_ref, gb_ref, go_ref, ki_ref, si_ref, ko_ref, so_ref, sums_ref, *rest):
        if with_output:
            x3_ref, *rest = rest
        a3_ref, a3t_ref, e3_ref, e3t_ref, u_ref, room_ref = rest
        j = pl.program_id(0)

        @pl.when(j == 0)
        def _():
            hat, _ = norm_parts(x2_ref[...])
            a3 = hat * gb_ref[2:3] + gb_ref[5:6]
            a3_ref[...] = a3.astype(BF16)
            a3t_ref[...] = a3.T.astype(BF16)
            g = g_ref[...]
            e3_ref[...] = g.astype(BF16)
            e3t_ref[...] = g.T.astype(BF16)
            u_ref[...] = jnp.zeros((t, d), F32)
            if with_output:
                x3_ref[...] = x2_ref[...]

        hid = nn(a3_ref[...], wi_ref[0, 0])
        phi = 0.5 * (1.0 + lax.erf(hid * HALF_ROOT))
        act = (hid * phi).astype(BF16)
        slope = phi + hid * jnp.exp(-0.5 * hid * hid) * INV_ROOT_TAU
        dhid = (nn(e3_ref[...], wo_ref[0, 0]) * slope).astype(BF16)
        split_rows(nn(e3t_ref[...], act), ko_ref, so_ref, (0, 0), room_ref, me_ref)
        split_rows(nn(a3t_ref[...], dhid), ki_ref, si_ref, (0, 0), room_ref, me_ref)
        u_ref[...] += nt(dhid, wi_ref[0, 0])
        if with_output:
            x3_ref[...] += nt(act, wo_ref[0, 0])

        @pl.when(j == steps - 1)
        def _():
            change, sums = norm_back(u_ref[...], x2_ref[...], gb_ref[2:3])
            go_ref[...] = g_ref[...] + change
            sums_ref[...] = sums

    slab_outs = [
        one
        for _ in range(2)
        for one in halves.array(
            (per_share, shares), (1, 1), lambda j: (j % per_share, j // per_share)
        )
    ]
    grad, ki, si, ko, so, sums, *x3 = call(
        body,
        (steps,),
        [
            SCALARS,
            whole(grad.shape),
            whole(x2.shape),
            ff_slab(0, per_share, d, width),
            ff_slab(per_share, per_share, d, width),
            whole(gb.shape),
        ],
        [made((t, d), F32), *slab_outs, made((2, d), F32)] + [made((t, d), F32)] * with_output,
        [
            pltpu.VMEM((t, d), BF16),
            pltpu.VMEM((d, t), BF16),
            pltpu.VMEM((t, d), BF16),
            pltpu.VMEM((d, t), BF16),
            pltpu.VMEM((t, d), F32),
            halves.room(),
        ],
        (me, grad, x2, w, w, gb),
        flops=10 * t * d * width * steps,
    )
    return grad, [(ki, si), (ko, so)], sums, x3


def space_backward(rows, grad, x1, qkv, o2, logs, w, gb, me, halves):
    t, d = x1.shape
    width = w.shape[3]
    shares = w.shape[1]
    pairs = width // LANES
    scale = 1.0 / math.sqrt(HEAD_DIM)
    rate = LOG2E * scale
    n = rows.frame_rows

    def body(me_ref, g_ref, x1_ref, qkv_ref, o2_ref, log_ref, wo_ref, wq_ref, gb_ref, go_ref, keep_ref, send_ref, sums_ref, e2_ref, e2t_ref, a2t_ref, do_ref, dqkv_ref, u_ref, room_ref):
        h = pl.program_id(0)

        @pl.when(h == 0)
        def _():
            g = g_ref[...]
            e2_ref[...] = g.astype(BF16)
            e2t_ref[...] = g.T.astype(BF16)
            hat, _ = norm_parts(x1_ref[...])
            a2t_ref[...] = (hat * gb_ref[1:2] + gb_ref[4:5]).T.astype(BF16)
            u_ref[...] = jnp.zeros((t, d), F32)

        bias = rows.space_bias()
        split_rows(nn(e2t_ref[...], o2_ref[...]), keep_ref, send_ref, (0, 0), room_ref, me_ref)
        do_ref[...] = nn(e2_ref[...], wo_ref[0, 0]).astype(BF16)

        @pl.loop(0, pairs)
        def _(i):
            lanes = pl.ds(pl.multiple_of(i * LANES, LANES), LANES)
            for f in range(rows.frames):
                at = slice(f * n, (f + 1) * n)
                log = log_ref[0, i, f]
                grads = pair_backward(
                    qkv_ref[0, at, lanes],
                    qkv_ref[1, at, lanes],
                    qkv_ref[2, at, lanes],
                    do_ref[at, lanes],
                    (log[0:1], log[1:2]),
                    bias,
                    rate,
                    scale,
                )
                for part in range(3):
                    dqkv_ref[part, at, lanes] = grads[part]

        for part in range(3):
            split_rows(
                nn(a2t_ref[...], dqkv_ref[part]), keep_ref, send_ref, (part + 1, 0), room_ref, me_ref
            )
            u_ref[...] += nt(dqkv_ref[part], wq_ref[part, 0])

        @pl.when(h == shares - 1)
        def _():
            change, sums = norm_back(u_ref[...], x1_ref[...], gb_ref[1:2])
            go_ref[...] = g_ref[...] + change
            sums_ref[...] = sums

    grad, keep, send, sums = call(
        body,
        (shares,),
        [
            SCALARS,
            whole(grad.shape),
            whole(x1.shape),
            pl.BlockSpec((3, t, width), lambda h: (0, 0, h)),
            pl.BlockSpec((t, width), lambda h: (0, h)),
            pl.BlockSpec((1,) + logs.shape[1:], lambda h: (h, 0, 0, 0, 0)),
            slabs(1, 7, width, d),
            slabs(3, 3, width, d),
            whole(gb.shape),
        ],
        [
            made((t, d), F32),
            *halves.array((4, shares), (4, 1), lambda h: (0, h)),
            made((2, d), F32),
        ],
        [
            pltpu.VMEM((t, d), BF16),
            pltpu.VMEM((d, t), BF16),
            pltpu.VMEM((d, t), BF16),
            pltpu.VMEM((t, width), BF16),
            pltpu.VMEM((3, t, width), BF16),
            pltpu.VMEM((t, d), F32),
            halves.room(),
        ],
        (me, grad, x1, qkv, o2, logs, w, w, gb),
        flops=2 * t * d * d * 8,
    )
    return grad, (keep, send), sums


def mix_fits(depth, shards, shares):
    return depth // (shards * shares) % 8 == 0


def middle_backward(rows, grad, y1, o1, w, mix, me, halves, shards):
    t, d = grad.shape
    width = w.shape[3]
    shares = w.shape[1]
    fits = mix_fits(d, shards, shares)
    part = d // (shards * shares)

    def body(me_ref, g_ref, y1_ref, o1_ref, to_ref, mix_ref, *rest):
        send_refs, rest = rest[: rows.ways], rest[rows.ways :]
        gk_ref, gs_ref, *rest = rest
        if fits:
            room_ref, order_ref = rest
        else:
            gm_ref, room_ref = rest
        e1 = g_ref[...].astype(BF16)
        dy1 = nt(e1, mix_ref[...]).astype(BF16)
        sends = [rows.to_time(k, me_ref[3]) for k in range(rows.ways)]
        for h in range(shares):
            lanes = slice(h * width, (h + 1) * width)
            do1 = nn(dy1, to_ref[0, h]).astype(BF16)
            for k in range(rows.ways):
                send_refs[k][:, lanes] = nn(sends[k], do1).astype(BF16)
            split_rows(tn(dy1, o1_ref[:, lanes]), gk_ref, gs_ref, (0, h), room_ref, me_ref)
        gm = tn(y1_ref[...], e1)
        if fits:
            gm = gm.reshape(shards, shares, part, d)
            for h in range(shares):
                for half in range(shares):
                    order_ref[:, half] = gm[:, h, :, half * width : (half + 1) * width]
                split_rows(order_ref[...], gk_ref, gs_ref, (1, h), room_ref, me_ref)
        else:
            gm_ref[...] = gm.astype(BF16)

    outs = rows.chunks(d)
    outs += halves.array((1 + fits, shares), (1 + fits, shares), lambda i: (0, 0))
    scratch = [halves.room()]
    if fits:
        scratch.append(pltpu.VMEM((shards, shares, part, width), F32))
    else:
        outs.append(made((d, d), BF16))
    got = call(
        body,
        (1,),
        [
            SCALARS,
            whole(grad.shape),
            whole(y1.shape),
            whole(o1.shape),
            pl.BlockSpec((1, shares, d, width), lambda i: (6, 0, 0, 0)),
            whole(mix.shape),
        ],
        outs,
        scratch,
        (me, grad, y1, o1, w, mix),
        flops=8 * t * d * d,
    )
    do1, (keep, send) = got[: rows.ways], got[rows.ways : rows.ways + 2]
    if not fits:
        gm = mix_slab(got[-1], shards, shares).reshape((1, shares, halves.pairs, 2) + keep.shape[3:])
        keep = jnp.concatenate((keep, lax.dynamic_index_in_dim(gm, me[0], 3, keepdims=False)), axis=0)
        send = jnp.concatenate((send, lax.dynamic_index_in_dim(gm, 1 - me[0], 3, keepdims=False)), axis=0)
    return do1, (keep, send)


def time_backward(rows, do1, a, qkv, logs, w, me, halves):
    t, d = a.shape
    width = w.shape[3]
    shares = w.shape[1]
    pairs = width // LANES
    scale = 1.0 / math.sqrt(HEAD_DIM)
    rate = LOG2E * scale

    def body(me_ref, *refs):
        do_refs, refs = refs[: rows.ways], refs[rows.ways :]
        a_ref, qkv_ref, log_ref, w_ref = refs[:4]
        out_refs, refs = refs[4 : 4 + rows.ways], refs[4 + rows.ways :]
        half_refs, refs = refs[:6], refs[6:]
        bias_ref, dqkv_ref, at_ref, u_ref, room_ref, do_ref = refs
        h = pl.program_id(0)

        @pl.when(h == 0)
        def _():
            bias_ref[...] = rows.time_bias()
            at_ref[...] = a_ref[...].T
            u_ref[...] = jnp.zeros((t, d), F32)

        for k in range(rows.ways):
            do_ref[k * rows.chunk : (k + 1) * rows.chunk] = do_refs[k][...]

        @pl.loop(0, pairs)
        def _(i):
            lanes = pl.ds(pl.multiple_of(i * LANES, LANES), LANES)
            log = log_ref[0, i]
            grads = pair_backward(
                qkv_ref[0, :, lanes],
                qkv_ref[1, :, lanes],
                qkv_ref[2, :, lanes],
                do_ref[:, lanes],
                (log[0:1], log[1:2]),
                bias_ref[...],
                rate,
                scale,
            )
            for part in range(3):
                dqkv_ref[part, :, lanes] = grads[part]

        for part in range(3):
            value = nn(at_ref[...], dqkv_ref[part])
            split_rows(value, half_refs[2 * part], half_refs[2 * part + 1], (0, 0), room_ref, me_ref)
            u_ref[...] += nt(dqkv_ref[part], w_ref[part, 0])

        @pl.when(h == shares - 1)
        def _():
            for k in range(rows.ways):
                out_refs[k][...] = u_ref[k * rows.chunk : (k + 1) * rows.chunk].astype(BF16)

    got = call(
        body,
        (shares,),
        [
            SCALARS,
            *(pl.BlockSpec((rows.chunk, width), lambda h: (0, h)) for _ in do1),
            whole(a.shape),
            pl.BlockSpec((3, t, width), lambda h: (0, 0, h)),
            pl.BlockSpec((1,) + logs.shape[1:], lambda h: (h, 0, 0, 0)),
            slabs(3, 0, width, d),
        ],
        [
            *rows.chunks(d),
            *(one for _ in range(3) for one in halves.array((1, shares), (1, 1), lambda h: (0, h))),
        ],
        [
            pltpu.VMEM((t, t), F32),
            pltpu.VMEM((3, t, width), BF16),
            pltpu.VMEM((d, t), BF16),
            pltpu.VMEM((t, d), F32),
            halves.room(),
            pltpu.VMEM((t, width), BF16),
        ],
        (me, *do1, a, qkv, logs, w),
        flops=2 * t * d * d * 6,
    )
    parts = got[rows.ways :]
    return got[: rows.ways], [tuple(parts[i : i + 2]) for i in (0, 2, 4)]


def first_norm_back(rows, back, x, grad, gb, me):
    t, d = x.shape

    def body(me_ref, *refs):
        x_ref, g_ref, gb_ref, go_ref, sums_ref = refs[rows.ways :]
        u = rows.gathered(refs[: rows.ways], me_ref[3])
        change, sums = norm_back(u, x_ref[...], gb_ref[0:1])
        go_ref[...] = g_ref[...] + change
        sums_ref[...] = sums

    return call(
        body,
        (1,),
        [SCALARS, *(whole(c.shape) for c in back), whole(x.shape), whole(grad.shape), whole(gb.shape)],
        [made((t, d), F32), made((2, d), F32)],
        [],
        (me, *back, x, grad, gb),
    )


def homes():
    clips, ways = lax.axis_size("clip"), lax.axis_size("seq")
    pairs = []
    for clip in range(clips):
        for seq in range(ways):
            home_clip = clip - clip % 2 + seq % 2
            home_seq = seq // 2 + (ways // 2) * (clip % 2)
            pairs.append((clip * ways + seq, home_clip * ways + home_seq))
    return pairs


def go_home(a):
    return lax.ppermute(a, ("clip", "seq"), homes())


def go_back(a):
    return lax.ppermute(a, ("clip", "seq"), [(home, device) for device, home in homes()])


def member_of(clip, seq):
    return clip % 2 + 2 * (seq % (lax.axis_size("seq") // 2))


def swap_places(chunks):
    clips, ways = lax.axis_size("clip"), lax.axis_size("seq")
    got = [chunks[0]]
    for k in range(1, ways):
        pairs = []
        for clip in range(clips):
            for seq in range(ways):
                other = member_of(clip, seq) ^ k
                to_clip = clip - clip % 2 + other % 2
                to_seq = seq - seq % (ways // 2) + other // 2
                pairs.append((clip * ways + seq, to_clip * ways + to_seq))
        got.append(lax.ppermute(chunks[k], ("clip", "seq"), pairs))
    return got


def columns(a, r, width):
    return a.reshape(r, -1, width).transpose(1, 0, 2)


def pack_attention(time_qkv, time_out, time_mix, space_qkv, space_out):
    r, _, width = time_qkv.shape
    mix = time_mix.reshape(-1, time_mix.shape[1] // width, width).transpose(1, 0, 2).reshape(1, r, width)
    return jnp.concatenate(
        (
            columns(time_qkv, r, width),
            columns(space_qkv, r, width),
            time_out.T[None],
            space_out.T[None],
            mix,
        ),
        axis=0,
    )


def pack_feed_forward(mlp_in, mlp_out, width):
    r = mlp_in.shape[0]
    return jnp.concatenate((columns(mlp_in, r, width), columns(mlp_out.T, r, width)), axis=0)


def gather_slabs(pack):
    full = lax.all_gather(pack, ("head", "clip", "seq"), axis=1, tiled=True)
    return full.reshape(pack.shape[0], lax.axis_size("head"), -1, pack.shape[2])


def spread_steps(pack, me):
    ways, clips = lax.axis_size("seq"), lax.axis_size("clip")
    shares = lax.axis_size("head")
    n, r, width = pack.shape
    pack = yield pack
    turned = [pack] + [
        lax.ppermute(pack, "seq", [(i, (i + k) % ways) for i in range(ways)]) for k in range(1, ways)
    ]
    turned = yield turned
    orders = (((0, 1), "x", "h"), ((3, 2), "h", "x"))
    some = [jnp.stack([turned[k] for k in steps]) for steps, _, _ in orders]
    come = yield [cross(a, first) for a, (_, first, _) in zip(some, orders)]
    some = [jnp.concatenate(pair, axis=0) for pair in zip(some, come)]
    come = yield [cross(a, second) for a, (_, _, second) in zip(some, orders)]
    runs = []
    for mine, other, (steps, first, second) in zip(some, come, orders):
        where = [(k, {first: f}) for f in (0, 1) for k in steps]
        for g, blocks in enumerate((mine, other)):
            runs.append((blocks, [(k, {**at, second: g}) for k, at in where], 0))
    come = yield [cross(blocks, "c") for blocks, _, _ in runs]
    runs += [(far, where, 1) for far, (_, where, _) in zip(come, runs)]
    count = sum(len(where) for _, where, _ in runs)

    def body(me_ref, *refs):
        sources, out_ref, sems = refs[: len(runs)], refs[-2], refs[-1]
        copies = []
        for source, (_, where, core) in zip(sources, runs):
            for i, (k, at) in enumerate(where):
                share = jnp.bitwise_xor(me_ref[2], at["h"])
                clip = 2 * jnp.bitwise_xor(me_ref[1], at["x"]) + jnp.bitwise_xor(me_ref[0], core)
                seq = lax.rem(me_ref[4] + (ways - k), ways)
                copies.append(
                    pltpu.make_async_copy(
                        source.at[i], out_ref.at[:, share, clip * ways + seq], sems.at[len(copies)]
                    )
                )
        for copy in copies:
            copy.start()
        for copy in copies:
            copy.wait()

    full = pl.pallas_call(
        body,
        out_shape=jax.ShapeDtypeStruct((n, shares, clips * ways, r, width), BF16),
        in_specs=[SCALARS] + [pl.BlockSpec(memory_space=pltpu.HBM)] * len(runs),
        out_specs=pl.BlockSpec(memory_space=pltpu.VMEM),
        scratch_shapes=[pltpu.SemaphoreType.DMA((count,))],
        compiler_params=pltpu.CompilerParams(vmem_limit_bytes=VMEM),
        cost_estimate=pl.CostEstimate(
            flops=0, bytes_accessed=4 * n * shares * clips * ways * r * width, transcendentals=0
        ),
    )(me, *(blocks for blocks, _, _ in runs))
    yield full.reshape(n, shares, clips * ways * r, width)


def spread_slabs(pack, me):
    way = spread_steps(pack, me)
    come = next(way)
    for _ in range(5):
        come = way.send(come)
    return come


class Spread:
    def __init__(self, pack, me):
        self.way = spread_steps(pack, me)
        self.come = next(self.way)

    def step(self, x):
        x, come = lax.optimization_barrier((x, self.come))
        self.come = self.way.send(come)
        return x


def mix_whole(slab, shards):
    shares, depth, width = slab.shape
    part = slab.reshape(shares, shards, shares, depth // (shards * shares), width)
    return part.transpose(1, 0, 3, 2, 4).reshape(depth, shares * width)


def mix_slab(whole_grad, shards, shares):
    depth, full = whole_grad.shape
    width = full // shares
    part = whole_grad.reshape(shards, shares, depth // (shards * shares), shares, width)
    return part.transpose(1, 0, 3, 2, 4).reshape(1, shares, depth, width)


class Piece:
    def __init__(self, keep, got, first, n, order):
        self.near = (keep, got)
        self.first = first
        self.n = n
        self.order = order
        self.step = 0
        self.held = []
        self.result = None


PLACE = {"x": 1, "h": 2}


def fold(pieces, me, last_by_rows):
    ways = lax.axis_size("seq")
    depth, width = pieces[0].near[0].shape[-2:]
    r = depth // ways
    used = {}
    arrays = []

    def number(a):
        for i, known in enumerate(arrays):
            if known is a:
                return i
        arrays.append(a)
        return len(arrays) - 1

    plans = []
    for p in pieces:
        link = p.order[p.step] if p.step < 2 else "z"
        blocks = p.n * (2 if p.step == 0 else 1)
        base = used.get(link, 0)
        used[link] = base + blocks
        near = [number(a) for a in p.near]
        held = [(number(a), at) for a, at in p.held]
        plans.append((p, link, base, near, held))
    links = sorted(used)
    shapes = [
        (ways, used[k], r, width) if k == "z" and last_by_rows else (used[k], depth, width)
        for k in links
    ]
    rooms, counts = [], []
    for p, link, base, near, held in plans:
        each = 2 if p.step == 0 else 1
        counts.append((each, len(near) + len(held)))
        rooms += [(each * p.n, depth, width)] * (len(near) + len(held))
    copies_needed = sum(each * terms for each, terms in counts)

    def body(me_ref, *refs):
        sources = refs[: len(arrays)]
        outs = dict(zip(links, refs[len(arrays) : len(arrays) + len(links)]))
        held_refs = refs[len(arrays) + len(links) : -1]
        sems = refs[-1]
        mine = {name: me_ref[PLACE[name]] for name in PLACE}
        groups = []
        room = 0
        sem = 0
        for p, link, base, near, held in plans:
            group = []
            if p.step == 0:
                for term in near:
                    for k in range(2):
                        pick = {p.order[0]: 1 - mine[p.order[0]], p.order[1]: k}
                        source = sources[term].at[pl.ds(p.first, p.n), pick["h"], pick["x"]]
                        group.append((source, held_refs[room].at[pl.ds(k * p.n, p.n)]))
                    room += 1
            else:
                last = p.order[1]
                pick = {p.order[0]: mine[p.order[0]]}
                pick[last] = 1 - mine[last] if p.step == 1 else mine[last]
                for term in near:
                    source = sources[term].at[pl.ds(p.first, p.n), pick["h"], pick["x"]]
                    group.append((source, held_refs[room]))
                    room += 1
                for i, (term, at) in enumerate(held):
                    start = at + pick[last] * p.n if i == 0 else at
                    group.append((sources[term].at[pl.ds(start, p.n)], held_refs[room]))
                    room += 1
            made_copies = []
            for source, target in group:
                made_copies.append(pltpu.make_async_copy(source, target, sems.at[sem]))
                sem += 1
            groups.append(made_copies)
        for group in groups:
            for copy in group:
                copy.start()
        room = 0
        for (p, link, base, near, held), (each, terms), group in zip(plans, counts, groups):
            these = held_refs[room : room + terms]
            room += terms
            for copy in group:
                copy.wait()

            @pl.loop(0, each * p.n)
            def _(i, these=these, base=base, out=outs[link], last=p.step == 2 and last_by_rows):
                value = these[0][i].astype(F32)
                for one in these[1:]:
                    value = value + one[i].astype(F32)
                value = value.astype(BF16)
                if last:
                    for k in range(ways):
                        out[k, base + i] = value[k * r : (k + 1) * r]
                else:
                    out[base + i] = value

    moved = sum(2 * math.prod(room) for room in rooms) + sum(2 * math.prod(shape) for shape in shapes)
    sums = pl.pallas_call(
        body,
        out_shape=[jax.ShapeDtypeStruct(shape, BF16) for shape in shapes],
        in_specs=[SCALARS] + [pl.BlockSpec(memory_space=pltpu.HBM)] * len(arrays),
        out_specs=[pl.BlockSpec(memory_space=pltpu.VMEM)] * len(links),
        scratch_shapes=[pltpu.VMEM(room, BF16) for room in rooms]
        + [pltpu.SemaphoreType.DMA((copies_needed,))],
        compiler_params=pltpu.CompilerParams(vmem_limit_bytes=VMEM),
        cost_estimate=pl.CostEstimate(flops=0, bytes_accessed=moved, transcendentals=0),
    )(me, *arrays)
    return [(p, link, base) for p, link, base, _, _ in plans], dict(zip(links, sums))


def cross(a, name):
    axis, bit = ("head", 0) if name == "h" else ("clip", 1 if name == "x" else 0)
    size = lax.axis_size(axis)
    return lax.ppermute(a, axis, [(i, i ^ (1 << bit)) for i in range(size)])


def pieces_of(halves_of):
    total = sum(keep.shape[0] for keep, _ in halves_of)
    found = []
    seen = 0
    for keep, send in halves_of:
        got = cross(send, "c")
        n = keep.shape[0]
        first = min(max((total + 1) // 2 - seen, 0), n)
        if first:
            found.append(Piece(keep, got, 0, first, ("x", "h")))
        if n > first:
            found.append(Piece(keep, got, first, n - first, ("h", "x")))
        seen += n
    return found


def move(x, pieces, me, at_end=False):
    plans, sums = fold(pieces, me, at_end)
    x, sums = lax.optimization_barrier((x, sums))
    got = {}
    for link, array in sums.items():
        if link == "z":
            if at_end:
                every = lax.all_to_all(array, "seq", split_axis=0, concat_axis=0, tiled=True)
                got[link] = jnp.sum(every.astype(F32), axis=0)
            else:
                own = lax.psum_scatter(array, "seq", scatter_dimension=1, tiled=True)
                got[link] = own.astype(F32)
        else:
            got[link] = cross(array, link)
    for p, link, base in plans:
        if link == "z":
            p.result = got[link][base : base + p.n]
        else:
            p.held.append((got[link], base))
        p.step += 1
    return x


def settle(x, pieces):
    arrays = []
    for p in pieces:
        if not any(p.held[-1][0] is a for a in arrays):
            arrays.append(p.held[-1][0])
    x, came = lax.optimization_barrier((x, arrays))
    for p in pieces:
        for old, new in zip(arrays, came):
            if p.held[-1][0] is old:
                p.held[-1] = (new, p.held[-1][1])
                break
    return x


def reduce_plain(halves_of, core):
    def joined(keep, send):
        low = jnp.where(core == 0, keep, send)
        high = jnp.where(core == 0, send, keep)
        n, shares, pairs, depth, width = keep.shape
        return jnp.stack((low, high), axis=3).reshape(n, shares, 2 * pairs * depth, width)

    g = jnp.concatenate([joined(*pair) for pair in halves_of], axis=0)
    g = lax.psum_scatter(g, "head", scatter_dimension=1, tiled=True)
    g = lax.psum_scatter(g.astype(F32), ("clip", "seq"), scatter_dimension=2, tiled=True)
    return g[:, 0]


def gather_norms(gain, bias):
    layers, norms, part = gain.shape
    both = jnp.concatenate((gain, bias), axis=1).reshape(1, -1)
    count = lax.axis_size("clip") * lax.axis_size("seq") * lax.axis_size("head")
    width = round_up(both.shape[1], 128)
    padded = jnp.pad(both, ((0, 0), (0, width - both.shape[1])))
    every = lax.all_to_all(
        jnp.broadcast_to(padded, (count, width)), ALL, split_axis=0, concat_axis=0, tiled=True
    )[:, : both.shape[1]]
    return every.reshape(count, layers * 2 * norms, part).transpose(1, 0, 2).reshape(layers, 2 * norms, -1)


def reduce_norms(sums):
    count = lax.axis_size("clip") * lax.axis_size("seq") * lax.axis_size("head")
    rows, features = sums.shape
    part = features // count
    a = sums.reshape(rows, count, part).transpose(1, 0, 2).reshape(count, rows * part)
    width = round_up(rows * part, 128)
    a = jnp.pad(a, ((0, 0), (0, width - rows * part)))
    every = lax.all_to_all(a, ALL, split_axis=0, concat_axis=0, tiled=True)
    return jnp.sum(every, axis=0)[: rows * part].reshape(rows, part)


def on_device(
    tokens,
    cotangent,
    time_qkv,
    time_out,
    time_mix,
    space_qkv,
    space_out,
    mlp_in,
    mlp_out,
    norm_gain,
    norm_bias,
):
    layers = time_qkv.shape[0]
    clips, frames, places, d = tokens.shape
    ways = lax.axis_size("seq")
    shards = lax.axis_size("clip") * ways
    rows = Rows(clips * frames, places, ways)
    shares = lax.axis_size("head")

    def as_rows(a):
        a = a.astype(F32).reshape(rows.frames, places, d)
        a = jnp.pad(a, ((0, 0), (0, rows.frame_rows - places), (0, 0)))
        return a.reshape(rows.rows, d)

    def from_rows(a):
        a = a.reshape(rows.frames, rows.frame_rows, d)[:, :places]
        return a.reshape(tokens.shape)

    gbs = gather_norms(norm_gain, norm_bias)
    gb = [gbs[l] for l in range(layers)]
    packs = [
        pack_attention(time_qkv[l], time_out[l], time_mix[l], space_qkv[l], space_out[l])
        for l in range(layers)
    ]
    packs_ff = [pack_feed_forward(mlp_in[l], mlp_out[l], time_qkv.shape[3]) for l in range(layers)]
    weights = [gather_slabs(pack) for pack in packs]
    mixes = [mix_whole(w[-1], shards) for w in weights]
    quick = lax.axis_size("clip") == 4 and shares == 2 and ways == 4 and time_qkv.shape[1] % 16 == 0

    halves = Halves(lax.axis_size("clip"), d, time_qkv.shape[3])
    clip = lax.axis_index("clip")
    member = member_of(clip, lax.axis_index("seq"))
    me = jnp.stack((clip & 1, (clip >> 1) & 1, lax.axis_index("head"), member, lax.axis_index("seq"))).astype(
        jnp.int32
    )
    if quick:
        weights_ff = [spread_slabs(packs_ff[0], me)]
    else:
        weights_ff = [gather_slabs(pack) for pack in packs_ff]

    x = as_rows(go_home(tokens))
    send = send_first(rows, x, gb[0], me)
    kept = []
    for l in range(layers):
        w = weights[l]
        send = swap_places(send)
        if quick:
            if l + 1 < layers:
                send, weights_ff[l] = lax.optimization_barrier((send, weights_ff[l]))
                spread = Spread(packs_ff[l + 1], me)
                send, w = spread.step((send, w))
            else:
                send = spread.step(send)
        a1, qkv1, log1, o1_time = time_forward(rows, send, w)
        back = swap_places(o1_time)
        if quick:
            back = spread.step(back)
        o1, y1, x1, qkv2 = middle_forward(rows, back, x, w, mixes[l], gb[l], me)
        o2, x2, log2 = space_forward(rows, qkv2, x1, w)
        if quick:
            if l + 1 == layers:
                weights_ff.append(spread.come)
                x2, weights_ff[l] = lax.optimization_barrier((x2, weights_ff[l]))
            else:
                x2 = spread.step(x2)
        kept.append((x, a1, qkv1, log1, o1, y1, x1, qkv2, o2, log2, x2))
        if l + 1 < layers:
            x, *send = mlp_forward(rows, x2, weights_ff[l], gb[l], gb[l + 1], me)

    grad = as_rows(go_home(cotangent))
    norm_rows = [None] * layers
    summed = [None] * layers
    late = []
    for l in reversed(range(layers)):
        w = weights[l]
        x, a1, qkv1, log1, o1, y1, x1, qkv2, o2, log2, x2 = kept[l]
        grad, g_ff, s3, x3 = mlp_backward(
            rows, grad, x2, weights_ff[l], gb[l], me, halves, l + 1 == layers
        )
        if x3:
            output = go_back(from_rows(x3[0].astype(BF16)))
        if quick:
            ff = pieces_of(g_ff)
            if late:
                grad = settle(grad, late)
                grad = move(grad, late, me)
                late = [p for p in late if p.step < 3]
        grad, g_space, s2 = space_backward(rows, grad, x1, qkv2, o2, log2, w, gb[l], me, halves)
        if quick:
            space = pieces_of([g_space])
            if late:
                grad = settle(grad, late)
            grad, output = move((grad, output), ff, me)
        do1, g_out = middle_backward(rows, grad, y1, o1, w, mixes[l], me, halves, shards)
        do1 = swap_places(do1)
        if quick:
            do1 = move(do1, ff + space + late, me)
        da1, g_time = time_backward(rows, do1, a1, qkv1, log1, w, me, halves)
        if quick:
            da1 = settle(da1, ff + space)
        da1 = swap_places(da1)
        if quick:
            rest = pieces_of([g_out] + g_time)
            da1 = move(da1, ff + space + rest, me)
            late = space + rest
        grad, s1 = first_norm_back(rows, da1, x, grad, gb[l], me)
        norm_rows[l] = jnp.concatenate((s1[0:1], s2[0:1], s3[0:1], s1[1:2], s2[1:2], s3[1:2]), axis=0)
        if quick:
            summed[l] = ff + space + rest
        else:
            summed[l] = [reduce_plain(g_ff + [g_space, g_out] + g_time, clip & 1)]
    if quick:
        tokens_grad = move(go_back(from_rows(grad.astype(BF16))), late, me, True)
        move((), rest, me, True)
        summed = [[p.result for p in some] for some in summed]
    cuts = (2 * g_ff[0][0].shape[0], g_space[0].shape[0], g_out[0].shape[0], len(g_time))
    results = []
    for some in summed:
        slabs_of = jnp.concatenate(some, axis=0)
        ends = [sum(cuts[: i + 1]) for i in range(4)]
        results.append([slabs_of[e - c : e] for c, e in zip(cuts, ends)])
    if not quick:
        tokens_grad = go_back(from_rows(grad.astype(BF16)))
    tokens_grad = tokens_grad.astype(F32)
    norm_sums = reduce_norms(jnp.concatenate(norm_rows, axis=0)).reshape(layers, 2, 3, -1)

    def stacked(form):
        return jnp.stack([form(*results[l]) for l in range(layers)])

    def rows_of(a):
        return a.transpose(1, 0, 2)

    def flat(a):
        return rows_of(a).reshape(a.shape[1], -1)

    def mix_rows(a):
        r, width = a.shape
        return a.reshape(shares, r // shares, width).transpose(1, 0, 2).reshape(r // shares, -1)

    per_share = mlp_in.shape[2] // time_qkv.shape[3]
    return (
        output,
        tokens_grad,
        stacked(lambda ff, s, t, q: rows_of(q)),
        stacked(lambda ff, s, t, q: t[0].T),
        stacked(lambda ff, s, t, q: mix_rows(t[1])),
        stacked(lambda ff, s, t, q: rows_of(s[1:])),
        stacked(lambda ff, s, t, q: s[0].T),
        stacked(lambda ff, s, t, q: flat(ff[:per_share])),
        stacked(lambda ff, s, t, q: flat(ff[per_share:]).T),
        norm_sums[:, 0],
        norm_sums[:, 1],
    )


def solution(mesh):
    token_spec = P(("clip", "head"), "seq", None, None)
    in_specs = (
        token_spec,
        token_spec,
        P(None, ("clip", "seq"), None, "head"),
        P(None, "head", ("clip", "seq")),
        P(None, ("clip", "seq", "head"), None),
        P(None, ("clip", "seq"), None, "head"),
        P(None, "head", ("clip", "seq")),
        P(None, ("clip", "seq"), "head"),
        P(None, "head", ("clip", "seq")),
        P(None, None, ("clip", "seq", "head")),
        P(None, None, ("clip", "seq", "head")),
    )
    return jax.shard_map(
        on_device, mesh=mesh, in_specs=in_specs, out_specs=in_specs, check_vma=False
    )
```

```python
import functools
import math

import jax
import jax.numpy as jnp
from jax import lax
from jax.experimental import pallas as pl
from jax.experimental.pallas import tpu as pltpu
from jax.sharding import PartitionSpec as P

HEAD_DIM = 64
NORM_EPS = 1e-06
HALF_ROOT = 0.7071067811865476
INV_ROOT_TAU = 0.3989422804014327
LOG2E = 1.4426950408889634
FAR = -1e30
LANES = 128
VMEM = 56 * 1024 * 1024
SHOWN = 1.0
ALL = ("clip", "seq", "head")
BF16 = jnp.bfloat16
F32 = jnp.float32


def round_up(value, step):
    return -(-value // step) * step


def nn(a, b):
    return lax.dot_general(a, b, (((1,), (0,)), ((), ())), preferred_element_type=F32)


def nt(a, b):
    return lax.dot_general(a, b, (((1,), (1,)), ((), ())), preferred_element_type=F32)


def tn(a, b):
    return lax.dot_general(a, b, (((0,), (0,)), ((), ())), preferred_element_type=F32)


def norm_parts(x):
    mean = jnp.mean(x, axis=-1, keepdims=True)
    centred = x - mean
    spread = lax.rsqrt(jnp.mean(centred * centred, axis=-1, keepdims=True) + NORM_EPS)
    return centred * spread, spread


def norm_rounded(x, gain, bias):
    hat, _ = norm_parts(x)
    return (hat * gain + bias).astype(BF16)


def norm_back(u, x, gain):
    hat, spread = norm_parts(x)
    scaled = u * gain
    mean_scaled = jnp.mean(scaled, axis=-1, keepdims=True)
    mean_cross = jnp.mean(scaled * hat, axis=-1, keepdims=True)
    change = spread * (scaled - mean_scaled - hat * mean_cross)
    sums = jnp.concatenate(
        (jnp.sum(u * hat, axis=0, keepdims=True), jnp.sum(u, axis=0, keepdims=True)), axis=0
    )
    return change, sums


class Rows:
    def __init__(self, frames, places, ways):
        self.frames = frames
        self.places = places
        self.ways = ways
        self.frame_rows = round_up(places, 16)
        self.rows = frames * self.frame_rows
        self.block = places // ways
        self.chunk = round_up(frames * self.block, 8)
        self.time_rows = ways * self.chunk

    def split(self, r):
        way = jnp.zeros_like(r)
        for k in range(1, self.ways):
            way = way + (r >= k * self.chunk).astype(jnp.int32)
        rest = r - way * self.chunk
        frame = jnp.zeros_like(r)
        for k in range(1, self.frames):
            frame = frame + (rest >= k * self.block).astype(jnp.int32)
        real = rest < self.frames * self.block
        return way, frame, rest - frame * self.block, real

    def to_time(self, k, member):
        r = lax.broadcasted_iota(jnp.int32, (self.chunk, 1), 0)
        _, frame, place, real = self.split(r)
        way = jnp.bitwise_xor(member, k)
        source = jnp.where(real, frame * self.frame_rows + way * self.block + place, -1)
        c = lax.broadcasted_iota(jnp.int32, (self.chunk, self.rows), 1)
        return jnp.where(c == source, 1.0, 0.0).astype(BF16)

    def gathered(self, chunk_refs, member):
        total = tn(self.to_time(0, member), chunk_refs[0][...])
        for k in range(1, self.ways):
            total = total + tn(self.to_time(k, member), chunk_refs[k][...])
        return total

    def chunks(self, width, block=None, index=None):
        return [
            made((self.chunk, width), BF16)
            if block is None
            else made((self.chunk, width), BF16, (self.chunk, block), index)
            for _ in range(self.ways)
        ]

    def time_bias(self):
        def label(r):
            _, _, place, real = self.split(r)
            return jnp.where(real, place, -1)

        a = label(lax.broadcasted_iota(jnp.int32, (self.time_rows, 1), 0))
        b = label(lax.broadcasted_iota(jnp.int32, (1, self.time_rows), 1))
        return jnp.where(a == b, 0.0, FAR).astype(F32)

    def space_bias(self):
        a = lax.broadcasted_iota(jnp.int32, (self.frame_rows, 1), 0)
        return jnp.where(a < self.places, 0.0, FAR).astype(F32)


def lane_masks(rows):
    lane = lax.broadcasted_iota(jnp.int32, (rows, LANES), 1)
    return lane < HEAD_DIM


def one_of(value, low, half):
    zero = jnp.zeros_like(value)
    return jnp.where(low, value, zero) if half == 0 else jnp.where(low, zero, value)


def pair_forward(q, k, v, bias, rate):
    low = lane_masks(q.shape[0])
    mixed, logs = [], []
    for half in range(2):
        s = nt(k, one_of(q, low, half)) + bias
        peak = jnp.max(s, axis=0, keepdims=True)
        e = jnp.exp2((s - peak) * rate)
        total = jnp.sum(e, axis=0, keepdims=True)
        soft = (e * (1.0 / total)).astype(BF16)
        mixed.append(tn(soft, v))
        logs.append(peak * rate + jnp.log2(total))
    return jnp.where(low, mixed[0], mixed[1]).astype(BF16), logs


def pair_backward(q, k, v, do, logs, bias, rate, scale):
    low = lane_masks(q.shape[0])
    dq, dk, dv = [], [], []
    for half in range(2):
        s = nt(k, one_of(q, low, half)) + bias
        soft = jnp.exp2(s * rate - logs[half])
        dp = nt(v, one_of(do, low, half))
        ds = (soft * (dp - jnp.sum(soft * dp, axis=0, keepdims=True))).astype(BF16)
        dv.append(nn(soft.astype(BF16), do))
        dk.append(nn(ds, q))
        dq.append(tn(ds, k))
    return (
        (jnp.where(low, dq[0], dq[1]) * scale).astype(BF16),
        (jnp.where(low, dk[0], dk[1]) * scale).astype(BF16),
        jnp.where(low, dv[0], dv[1]).astype(BF16),
    )


def split_rows(value, keep_ref, send_ref, at, room_ref, me_ref):
    mine = me_ref[0]
    room_ref[...] = value.reshape(room_ref.shape)
    keep_ref[at] = room_ref[:, mine].astype(BF16)
    send_ref[at] = room_ref[:, 1 - mine].astype(BF16)


class Halves:
    def __init__(self, clips, depth, width):
        self.pairs = clips // 2
        self.rows = depth // clips
        self.width = width

    def array(self, lead, block, index):
        tail = (self.pairs, self.rows, self.width)
        one = lambda: made(lead + tail, BF16, block + tail, lambda *g: index(*g) + (0, 0, 0))
        return [one(), one()]

    def room(self):
        return pltpu.VMEM((self.pairs, 2, self.rows, self.width), F32)


SCALARS = pl.BlockSpec(memory_space=pltpu.SMEM)


def call(body, grid, ins, outs, scratch, args, flops=0):
    specs = [spec for spec in ins]
    moved = sum(math.prod(o.shape) * o.dtype.itemsize for o, _ in outs)
    moved += sum(math.prod(a.shape) * a.dtype.itemsize for a in args)
    return pl.pallas_call(
        body,
        out_shape=[shape for shape, _ in outs],
        grid=grid,
        in_specs=specs,
        out_specs=[spec for _, spec in outs],
        scratch_shapes=scratch,
        compiler_params=pltpu.CompilerParams(vmem_limit_bytes=VMEM),
        cost_estimate=pl.CostEstimate(
            flops=int(flops * SHOWN), bytes_accessed=int(moved * SHOWN), transcendentals=0
        ),
    )(*args)


def whole(shape):
    zeros = (0,) * len(shape)
    return pl.BlockSpec(shape, lambda *_: zeros)


def made(shape, dtype, block=None, index=None):
    spec = whole(shape) if block is None else pl.BlockSpec(block, index)
    return jax.ShapeDtypeStruct(shape, dtype), spec


def slabs(count, first, width, depth):
    return pl.BlockSpec((count, 1, depth, width), lambda h, *_: (first // count, h, 0, 0))


def send_first(rows, x, gb, me):
    def body(me_ref, x_ref, gb_ref, *out_refs):
        a = norm_rounded(x_ref[...], gb_ref[0:1], gb_ref[3:4])
        for k in range(rows.ways):
            out_refs[k][...] = nn(rows.to_time(k, me_ref[3]), a).astype(BF16)

    d = x.shape[1]
    return call(
        body, (1,), [SCALARS, whole(x.shape), whole(gb.shape)], rows.chunks(d), [], (me, x, gb)
    )


def time_forward(rows, chunks, w):
    t, d = rows.time_rows, chunks[0].shape[1]
    width = w.shape[3]
    shares = w.shape[1]
    pairs = width // LANES
    ways = rows.ways
    rate = LOG2E / math.sqrt(HEAD_DIM)

    def body(*refs):
        chunk_refs = refs[:ways]
        w_ref, a_ref, qkv_ref, log_ref = refs[ways : ways + 4]
        out_refs = refs[ways + 4 : 2 * ways + 4]
        bias_ref, mixed_ref = refs[2 * ways + 4 :]

        @pl.when(pl.program_id(0) == 0)
        def _():
            bias_ref[...] = rows.time_bias()
            for k in range(ways):
                a_ref[k * rows.chunk : (k + 1) * rows.chunk] = chunk_refs[k][...]

        act = a_ref[...]
        for g in range(3):
            qkv_ref[g] = nn(act, w_ref[g, 0]).astype(BF16)

        @pl.loop(0, pairs)
        def _(i):
            lanes = pl.ds(pl.multiple_of(i * LANES, LANES), LANES)
            mixed, logs = pair_forward(
                qkv_ref[0, :, lanes], qkv_ref[1, :, lanes], qkv_ref[2, :, lanes], bias_ref[...], rate
            )
            mixed_ref[:, lanes] = mixed
            log_ref[0, i] = jnp.concatenate(logs, axis=0)

        for k in range(ways):
            out_refs[k][...] = mixed_ref[k * rows.chunk : (k + 1) * rows.chunk]

    got = call(
        body,
        (shares,),
        [whole(c.shape) for c in chunks] + [slabs(3, 0, width, d)],
        [
            made((t, d), BF16),
            made((3, t, d), BF16, (3, t, width), lambda h: (0, 0, h)),
            made((shares, pairs, 2, t), F32, (1, pairs, 2, t), lambda h: (h, 0, 0, 0)),
            *rows.chunks(d, width, lambda h: (0, h)),
        ],
        [pltpu.VMEM((t, t), F32), pltpu.VMEM((t, width), BF16)],
        (*chunks, w),
        flops=2 * t * d * 3 * d,
    )
    return got[0], got[1], got[2], got[3:]


def middle_forward(rows, back, x, w, mix, gb, me):
    t, d = x.shape
    width = w.shape[3]
    shares = w.shape[1]

    def body(me_ref, *refs):
        x_ref, to_ref, sq_ref, mix_ref, gb_ref, o1_ref, y1_ref, x1_ref, qkv_ref = refs[rows.ways :]
        o1 = rows.gathered(refs[: rows.ways], me_ref[3]).astype(BF16)
        o1_ref[...] = o1
        y1 = jnp.zeros((t, d), F32)
        for h in range(shares):
            y1 = y1 + nt(o1[:, h * width : (h + 1) * width], to_ref[0, h])
        y1 = y1.astype(BF16)
        y1_ref[...] = y1
        x1 = x_ref[...] + nn(y1, mix_ref[...])
        x1_ref[...] = x1
        a2 = norm_rounded(x1, gb_ref[1:2], gb_ref[4:5])
        for g in range(3):
            for h in range(shares):
                qkv_ref[g, :, h * width : (h + 1) * width] = nn(a2, sq_ref[g, h]).astype(BF16)

    return call(
        body,
        (1,),
        [
            SCALARS,
            *(whole(c.shape) for c in back),
            whole(x.shape),
            pl.BlockSpec((1, shares, d, width), lambda i: (6, 0, 0, 0)),
            pl.BlockSpec((3, shares, d, width), lambda i: (1, 0, 0, 0)),
            whole(mix.shape),
            whole(gb.shape),
        ],
        [made((t, d), BF16), made((t, d), BF16), made((t, d), F32), made((3, t, d), BF16)],
        [],
        (me, *back, x, w, w, mix, gb),
        flops=2 * t * d * 5 * d,
    )


def space_forward(rows, qkv, x1, w):
    t, d = x1.shape
    width = w.shape[3]
    shares = w.shape[1]
    pairs = width // LANES
    rate = LOG2E / math.sqrt(HEAD_DIM)
    n = rows.frame_rows

    def body(qkv_ref, x1_ref, w_ref, o2_ref, x2_ref, log_ref):
        bias = rows.space_bias()

        @pl.loop(0, pairs)
        def _(i):
            lanes = pl.ds(pl.multiple_of(i * LANES, LANES), LANES)
            for f in range(rows.frames):
                at = slice(f * n, (f + 1) * n)
                mixed, logs = pair_forward(
                    qkv_ref[0, at, lanes], qkv_ref[1, at, lanes], qkv_ref[2, at, lanes], bias, rate
                )
                o2_ref[at, lanes] = mixed
                log_ref[0, i, f] = jnp.concatenate(logs, axis=0)

        @pl.when(pl.program_id(0) == 0)
        def _():
            x2_ref[...] = x1_ref[...]

        x2_ref[...] += nt(o2_ref[...], w_ref[0, 0])

    return call(
        body,
        (shares,),
        [
            pl.BlockSpec((3, t, width), lambda h: (0, 0, h)),
            whole(x1.shape),
            slabs(1, 7, width, d),
        ],
        [
            made((t, d), BF16, (t, width), lambda h: (0, h)),
            made((t, d), F32),
            made(
                (shares, pairs, rows.frames, 2, n),
                F32,
                (1, pairs, rows.frames, 2, n),
                lambda h: (h, 0, 0, 0, 0),
            ),
        ],
        [],
        (qkv, x1, w),
        flops=2 * t * d * d,
    )


def ff_slab(first, per_share, depth, width):
    return pl.BlockSpec(
        (1, 1, depth, width), lambda j: (first + j % per_share, j // per_share, 0, 0)
    )


def mlp_forward(rows, x2, w, gb, gb_next, me):
    t, d = x2.shape
    width = w.shape[3]
    shares = w.shape[1]
    per_share = w.shape[0] // 2
    steps = shares * per_share

    def body(x2_ref, wi_ref, wo_ref, gb_ref, me_ref, gn_ref, x3_ref, *rest):
        send_refs, a3_ref = rest[:-1], rest[-1]
        j = pl.program_id(0)

        @pl.when(j == 0)
        def _():
            a3_ref[...] = norm_rounded(x2_ref[...], gb_ref[2:3], gb_ref[5:6])
            x3_ref[...] = x2_ref[...]

        hid = nn(a3_ref[...], wi_ref[0, 0])
        act = (0.5 * hid * (1.0 + lax.erf(hid * HALF_ROOT))).astype(BF16)
        x3_ref[...] += nt(act, wo_ref[0, 0])

        @pl.when(j == steps - 1)
        def _():
            a = norm_rounded(x3_ref[...], gn_ref[0:1], gn_ref[3:4])
            for k in range(rows.ways):
                send_refs[k][...] = nn(rows.to_time(k, me_ref[3]), a).astype(BF16)

    ins = [
        whole(x2.shape),
        ff_slab(0, per_share, d, width),
        ff_slab(per_share, per_share, d, width),
        whole(gb.shape),
    ]
    ins += [SCALARS, whole(gb_next.shape)]
    outs = [made((t, d), F32)] + rows.chunks(d)
    args = (x2, w, w, gb, me, gb_next)
    return call(
        body, (steps,), ins, outs, [pltpu.VMEM((t, d), BF16)], args, flops=4 * t * d * width * steps
    )


def mlp_backward(rows, grad, x2, w, gb, me, halves, with_output):
    t, d = x2.shape
    width = w.shape[3]
    shares = w.shape[1]
    per_share = w.shape[0] // 2
    steps = shares * per_share

    def body(me_ref, g_ref, x2_ref, wi_ref, wo_ref, gb_ref, go_ref, ki_ref, si_ref, ko_ref, so_ref, sums_ref, *rest):
        if with_output:
            x3_ref, *rest = rest
        a3_ref, a3t_ref, e3_ref, e3t_ref, u_ref, room_ref = rest
        j = pl.program_id(0)

        @pl.when(j == 0)
        def _():
            hat, _ = norm_parts(x2_ref[...])
            a3 = hat * gb_ref[2:3] + gb_ref[5:6]
            a3_ref[...] = a3.astype(BF16)
            a3t_ref[...] = a3.T.astype(BF16)
            g = g_ref[...]
            e3_ref[...] = g.astype(BF16)
            e3t_ref[...] = g.T.astype(BF16)
            u_ref[...] = jnp.zeros((t, d), F32)
            if with_output:
                x3_ref[...] = x2_ref[...]

        hid = nn(a3_ref[...], wi_ref[0, 0])
        phi = 0.5 * (1.0 + lax.erf(hid * HALF_ROOT))
        act = (hid * phi).astype(BF16)
        slope = phi + hid * jnp.exp(-0.5 * hid * hid) * INV_ROOT_TAU
        dhid = (nn(e3_ref[...], wo_ref[0, 0]) * slope).astype(BF16)
        split_rows(nn(e3t_ref[...], act), ko_ref, so_ref, (0, 0), room_ref, me_ref)
        split_rows(nn(a3t_ref[...], dhid), ki_ref, si_ref, (0, 0), room_ref, me_ref)
        u_ref[...] += nt(dhid, wi_ref[0, 0])
        if with_output:
            x3_ref[...] += nt(act, wo_ref[0, 0])

        @pl.when(j == steps - 1)
        def _():
            change, sums = norm_back(u_ref[...], x2_ref[...], gb_ref[2:3])
            go_ref[...] = g_ref[...] + change
            sums_ref[...] = sums

    slab_outs = [
        one
        for _ in range(2)
        for one in halves.array(
            (per_share, shares), (1, 1), lambda j: (j % per_share, j // per_share)
        )
    ]
    grad, ki, si, ko, so, sums, *x3 = call(
        body,
        (steps,),
        [
            SCALARS,
            whole(grad.shape),
            whole(x2.shape),
            ff_slab(0, per_share, d, width),
            ff_slab(per_share, per_share, d, width),
            whole(gb.shape),
        ],
        [made((t, d), F32), *slab_outs, made((2, d), F32)] + [made((t, d), F32)] * with_output,
        [
            pltpu.VMEM((t, d), BF16),
            pltpu.VMEM((d, t), BF16),
            pltpu.VMEM((t, d), BF16),
            pltpu.VMEM((d, t), BF16),
            pltpu.VMEM((t, d), F32),
            halves.room(),
        ],
        (me, grad, x2, w, w, gb),
        flops=10 * t * d * width * steps,
    )
    return grad, [(ki, si), (ko, so)], sums, x3


def space_backward(rows, grad, x1, qkv, o2, logs, w, gb, me, halves):
    t, d = x1.shape
    width = w.shape[3]
    shares = w.shape[1]
    pairs = width // LANES
    scale = 1.0 / math.sqrt(HEAD_DIM)
    rate = LOG2E * scale
    n = rows.frame_rows

    def body(me_ref, g_ref, x1_ref, qkv_ref, o2_ref, log_ref, wo_ref, wq_ref, gb_ref, go_ref, keep_ref, send_ref, sums_ref, e2_ref, e2t_ref, a2t_ref, do_ref, dqkv_ref, u_ref, room_ref):
        h = pl.program_id(0)

        @pl.when(h == 0)
        def _():
            g = g_ref[...]
            e2_ref[...] = g.astype(BF16)
            e2t_ref[...] = g.T.astype(BF16)
            hat, _ = norm_parts(x1_ref[...])
            a2t_ref[...] = (hat * gb_ref[1:2] + gb_ref[4:5]).T.astype(BF16)
            u_ref[...] = jnp.zeros((t, d), F32)

        bias = rows.space_bias()
        split_rows(nn(e2t_ref[...], o2_ref[...]), keep_ref, send_ref, (0, 0), room_ref, me_ref)
        do_ref[...] = nn(e2_ref[...], wo_ref[0, 0]).astype(BF16)

        @pl.loop(0, pairs)
        def _(i):
            lanes = pl.ds(pl.multiple_of(i * LANES, LANES), LANES)
            for f in range(rows.frames):
                at = slice(f * n, (f + 1) * n)
                log = log_ref[0, i, f]
                grads = pair_backward(
                    qkv_ref[0, at, lanes],
                    qkv_ref[1, at, lanes],
                    qkv_ref[2, at, lanes],
                    do_ref[at, lanes],
                    (log[0:1], log[1:2]),
                    bias,
                    rate,
                    scale,
                )
                for part in range(3):
                    dqkv_ref[part, at, lanes] = grads[part]

        for part in range(3):
            split_rows(
                nn(a2t_ref[...], dqkv_ref[part]), keep_ref, send_ref, (part + 1, 0), room_ref, me_ref
            )
            u_ref[...] += nt(dqkv_ref[part], wq_ref[part, 0])

        @pl.when(h == shares - 1)
        def _():
            change, sums = norm_back(u_ref[...], x1_ref[...], gb_ref[1:2])
            go_ref[...] = g_ref[...] + change
            sums_ref[...] = sums

    grad, keep, send, sums = call(
        body,
        (shares,),
        [
            SCALARS,
            whole(grad.shape),
            whole(x1.shape),
            pl.BlockSpec((3, t, width), lambda h: (0, 0, h)),
            pl.BlockSpec((t, width), lambda h: (0, h)),
            pl.BlockSpec((1,) + logs.shape[1:], lambda h: (h, 0, 0, 0, 0)),
            slabs(1, 7, width, d),
            slabs(3, 3, width, d),
            whole(gb.shape),
        ],
        [
            made((t, d), F32),
            *halves.array((4, shares), (4, 1), lambda h: (0, h)),
            made((2, d), F32),
        ],
        [
            pltpu.VMEM((t, d), BF16),
            pltpu.VMEM((d, t), BF16),
            pltpu.VMEM((d, t), BF16),
            pltpu.VMEM((t, width), BF16),
            pltpu.VMEM((3, t, width), BF16),
            pltpu.VMEM((t, d), F32),
            halves.room(),
        ],
        (me, grad, x1, qkv, o2, logs, w, w, gb),
        flops=2 * t * d * d * 8,
    )
    return grad, (keep, send), sums


def mix_fits(depth, shards, shares):
    return depth // (shards * shares) % 8 == 0


def middle_backward(rows, grad, y1, o1, w, mix, me, halves, shards):
    t, d = grad.shape
    width = w.shape[3]
    shares = w.shape[1]
    fits = mix_fits(d, shards, shares)
    part = d // (shards * shares)

    def body(me_ref, g_ref, y1_ref, o1_ref, to_ref, mix_ref, *rest):
        send_refs, rest = rest[: rows.ways], rest[rows.ways :]
        gk_ref, gs_ref, *rest = rest
        if fits:
            room_ref, order_ref = rest
        else:
            gm_ref, room_ref = rest
        e1 = g_ref[...].astype(BF16)
        dy1 = nt(e1, mix_ref[...]).astype(BF16)
        sends = [rows.to_time(k, me_ref[3]) for k in range(rows.ways)]
        for h in range(shares):
            lanes = slice(h * width, (h + 1) * width)
            do1 = nn(dy1, to_ref[0, h]).astype(BF16)
            for k in range(rows.ways):
                send_refs[k][:, lanes] = nn(sends[k], do1).astype(BF16)
            split_rows(tn(dy1, o1_ref[:, lanes]), gk_ref, gs_ref, (0, h), room_ref, me_ref)
        gm = tn(y1_ref[...], e1)
        if fits:
            gm = gm.reshape(shards, shares, part, d)
            for h in range(shares):
                for half in range(shares):
                    order_ref[:, half] = gm[:, h, :, half * width : (half + 1) * width]
                split_rows(order_ref[...], gk_ref, gs_ref, (1, h), room_ref, me_ref)
        else:
            gm_ref[...] = gm.astype(BF16)

    outs = rows.chunks(d)
    outs += halves.array((1 + fits, shares), (1 + fits, shares), lambda i: (0, 0))
    scratch = [halves.room()]
    if fits:
        scratch.append(pltpu.VMEM((shards, shares, part, width), F32))
    else:
        outs.append(made((d, d), BF16))
    got = call(
        body,
        (1,),
        [
            SCALARS,
            whole(grad.shape),
            whole(y1.shape),
            whole(o1.shape),
            pl.BlockSpec((1, shares, d, width), lambda i: (6, 0, 0, 0)),
            whole(mix.shape),
        ],
        outs,
        scratch,
        (me, grad, y1, o1, w, mix),
        flops=8 * t * d * d,
    )
    do1, (keep, send) = got[: rows.ways], got[rows.ways : rows.ways + 2]
    if not fits:
        gm = mix_slab(got[-1], shards, shares).reshape((1, shares, halves.pairs, 2) + keep.shape[3:])
        keep = jnp.concatenate((keep, lax.dynamic_index_in_dim(gm, me[0], 3, keepdims=False)), axis=0)
        send = jnp.concatenate((send, lax.dynamic_index_in_dim(gm, 1 - me[0], 3, keepdims=False)), axis=0)
    return do1, (keep, send)


def time_backward(rows, do1, a, qkv, logs, w, me, halves):
    t, d = a.shape
    width = w.shape[3]
    shares = w.shape[1]
    pairs = width // LANES
    scale = 1.0 / math.sqrt(HEAD_DIM)
    rate = LOG2E * scale

    def body(me_ref, *refs):
        do_refs, refs = refs[: rows.ways], refs[rows.ways :]
        a_ref, qkv_ref, log_ref, w_ref = refs[:4]
        out_refs, refs = refs[4 : 4 + rows.ways], refs[4 + rows.ways :]
        half_refs, refs = refs[:6], refs[6:]
        bias_ref, dqkv_ref, at_ref, u_ref, room_ref, do_ref = refs
        h = pl.program_id(0)

        @pl.when(h == 0)
        def _():
            bias_ref[...] = rows.time_bias()
            at_ref[...] = a_ref[...].T
            u_ref[...] = jnp.zeros((t, d), F32)

        for k in range(rows.ways):
            do_ref[k * rows.chunk : (k + 1) * rows.chunk] = do_refs[k][...]

        @pl.loop(0, pairs)
        def _(i):
            lanes = pl.ds(pl.multiple_of(i * LANES, LANES), LANES)
            log = log_ref[0, i]
            grads = pair_backward(
                qkv_ref[0, :, lanes],
                qkv_ref[1, :, lanes],
                qkv_ref[2, :, lanes],
                do_ref[:, lanes],
                (log[0:1], log[1:2]),
                bias_ref[...],
                rate,
                scale,
            )
            for part in range(3):
                dqkv_ref[part, :, lanes] = grads[part]

        for part in range(3):
            value = nn(at_ref[...], dqkv_ref[part])
            split_rows(value, half_refs[2 * part], half_refs[2 * part + 1], (0, 0), room_ref, me_ref)
            u_ref[...] += nt(dqkv_ref[part], w_ref[part, 0])

        @pl.when(h == shares - 1)
        def _():
            for k in range(rows.ways):
                out_refs[k][...] = u_ref[k * rows.chunk : (k + 1) * rows.chunk].astype(BF16)

    got = call(
        body,
        (shares,),
        [
            SCALARS,
            *(pl.BlockSpec((rows.chunk, width), lambda h: (0, h)) for _ in do1),
            whole(a.shape),
            pl.BlockSpec((3, t, width), lambda h: (0, 0, h)),
            pl.BlockSpec((1,) + logs.shape[1:], lambda h: (h, 0, 0, 0)),
            slabs(3, 0, width, d),
        ],
        [
            *rows.chunks(d),
            *(one for _ in range(3) for one in halves.array((1, shares), (1, 1), lambda h: (0, h))),
        ],
        [
            pltpu.VMEM((t, t), F32),
            pltpu.VMEM((3, t, width), BF16),
            pltpu.VMEM((d, t), BF16),
            pltpu.VMEM((t, d), F32),
            halves.room(),
            pltpu.VMEM((t, width), BF16),
        ],
        (me, *do1, a, qkv, logs, w),
        flops=2 * t * d * d * 6,
    )
    parts = got[rows.ways :]
    return got[: rows.ways], [tuple(parts[i : i + 2]) for i in (0, 2, 4)]


def first_norm_back(rows, back, x, grad, gb, me):
    t, d = x.shape

    def body(me_ref, *refs):
        x_ref, g_ref, gb_ref, go_ref, sums_ref = refs[rows.ways :]
        u = rows.gathered(refs[: rows.ways], me_ref[3])
        change, sums = norm_back(u, x_ref[...], gb_ref[0:1])
        go_ref[...] = g_ref[...] + change
        sums_ref[...] = sums

    return call(
        body,
        (1,),
        [SCALARS, *(whole(c.shape) for c in back), whole(x.shape), whole(grad.shape), whole(gb.shape)],
        [made((t, d), F32), made((2, d), F32)],
        [],
        (me, *back, x, grad, gb),
    )


def homes():
    clips, ways = lax.axis_size("clip"), lax.axis_size("seq")
    pairs = []
    for clip in range(clips):
        for seq in range(ways):
            home_clip = clip - clip % 2 + seq % 2
            home_seq = seq // 2 + (ways // 2) * (clip % 2)
            pairs.append((clip * ways + seq, home_clip * ways + home_seq))
    return pairs


def go_home(a):
    return lax.ppermute(a, ("clip", "seq"), homes())


def go_back(a):
    return lax.ppermute(a, ("clip", "seq"), [(home, device) for device, home in homes()])


def member_of(clip, seq):
    return clip % 2 + 2 * (seq % (lax.axis_size("seq") // 2))


def swap_places(chunks):
    clips, ways = lax.axis_size("clip"), lax.axis_size("seq")
    got = [chunks[0]]
    for k in range(1, ways):
        pairs = []
        for clip in range(clips):
            for seq in range(ways):
                other = member_of(clip, seq) ^ k
                to_clip = clip - clip % 2 + other % 2
                to_seq = seq - seq % (ways // 2) + other // 2
                pairs.append((clip * ways + seq, to_clip * ways + to_seq))
        got.append(lax.ppermute(chunks[k], ("clip", "seq"), pairs))
    return got


def columns(a, r, width):
    return a.reshape(r, -1, width).transpose(1, 0, 2)


def pack_attention(time_qkv, time_out, time_mix, space_qkv, space_out):
    r, _, width = time_qkv.shape
    mix = time_mix.reshape(-1, time_mix.shape[1] // width, width).transpose(1, 0, 2).reshape(1, r, width)
    return jnp.concatenate(
        (
            columns(time_qkv, r, width),
            columns(space_qkv, r, width),
            time_out.T[None],
            space_out.T[None],
            mix,
        ),
        axis=0,
    )


def pack_feed_forward(mlp_in, mlp_out, width):
    r = mlp_in.shape[0]
    return jnp.concatenate((columns(mlp_in, r, width), columns(mlp_out.T, r, width)), axis=0)


def gather_slabs(pack):
    full = lax.all_gather(pack, ("head", "clip", "seq"), axis=1, tiled=True)
    return full.reshape(pack.shape[0], lax.axis_size("head"), -1, pack.shape[2])


def spread_steps(pack, me):
    ways, clips = lax.axis_size("seq"), lax.axis_size("clip")
    shares = lax.axis_size("head")
    n, r, width = pack.shape
    pack = yield pack
    turned = [pack] + [
        lax.ppermute(pack, "seq", [(i, (i + k) % ways) for i in range(ways)]) for k in range(1, ways)
    ]
    turned = yield turned
    orders = (((0, 1), "x", "h"), ((3, 2), "h", "x"))
    some = [jnp.stack([turned[k] for k in steps]) for steps, _, _ in orders]
    come = yield [cross(a, first) for a, (_, first, _) in zip(some, orders)]
    some = [jnp.concatenate(pair, axis=0) for pair in zip(some, come)]
    come = yield [cross(a, second) for a, (_, _, second) in zip(some, orders)]
    runs = []
    for mine, other, (steps, first, second) in zip(some, come, orders):
        where = [(k, {first: f}) for f in (0, 1) for k in steps]
        for g, blocks in enumerate((mine, other)):
            runs.append((blocks, [(k, {**at, second: g}) for k, at in where], 0))
    come = yield [cross(blocks, "c") for blocks, _, _ in runs]
    runs += [(far, where, 1) for far, (_, where, _) in zip(come, runs)]
    count = sum(len(where) for _, where, _ in runs)

    def body(me_ref, *refs):
        sources, out_ref, sems = refs[: len(runs)], refs[-2], refs[-1]
        copies = []
        for source, (_, where, core) in zip(sources, runs):
            for i, (k, at) in enumerate(where):
                share = jnp.bitwise_xor(me_ref[2], at["h"])
                clip = 2 * jnp.bitwise_xor(me_ref[1], at["x"]) + jnp.bitwise_xor(me_ref[0], core)
                seq = lax.rem(me_ref[4] + (ways - k), ways)
                copies.append(
                    pltpu.make_async_copy(
                        source.at[i], out_ref.at[:, share, clip * ways + seq], sems.at[len(copies)]
                    )
                )
        for copy in copies:
            copy.start()
        for copy in copies:
            copy.wait()

    full = pl.pallas_call(
        body,
        out_shape=jax.ShapeDtypeStruct((n, shares, clips * ways, r, width), BF16),
        in_specs=[SCALARS] + [pl.BlockSpec(memory_space=pltpu.HBM)] * len(runs),
        out_specs=pl.BlockSpec(memory_space=pltpu.VMEM),
        scratch_shapes=[pltpu.SemaphoreType.DMA((count,))],
        compiler_params=pltpu.CompilerParams(vmem_limit_bytes=VMEM),
        cost_estimate=pl.CostEstimate(
            flops=0, bytes_accessed=4 * n * shares * clips * ways * r * width, transcendentals=0
        ),
    )(me, *(blocks for blocks, _, _ in runs))
    yield full.reshape(n, shares, clips * ways * r, width)


class Spread:
    def __init__(self, pack, me):
        self.way = spread_steps(pack, me)
        self.come = next(self.way)

    def step(self, x):
        x, come = lax.optimization_barrier((x, self.come))
        self.come = self.way.send(come)
        return x


def mix_whole(slab, shards):
    shares, depth, width = slab.shape
    part = slab.reshape(shares, shards, shares, depth // (shards * shares), width)
    return part.transpose(1, 0, 3, 2, 4).reshape(depth, shares * width)


def mix_slab(whole_grad, shards, shares):
    depth, full = whole_grad.shape
    width = full // shares
    part = whole_grad.reshape(shards, shares, depth // (shards * shares), shares, width)
    return part.transpose(1, 0, 3, 2, 4).reshape(1, shares, depth, width)


class Piece:
    def __init__(self, keep, got, first, n, order):
        self.near = (keep, got)
        self.first = first
        self.n = n
        self.order = order
        self.step = 0
        self.held = []
        self.result = None


PLACE = {"x": 1, "h": 2}


def fold(pieces, me, last_by_rows):
    ways = lax.axis_size("seq")
    depth, width = pieces[0].near[0].shape[-2:]
    r = depth // ways
    used = {}
    arrays = []

    def number(a):
        for i, known in enumerate(arrays):
            if known is a:
                return i
        arrays.append(a)
        return len(arrays) - 1

    plans = []
    for p in pieces:
        link = p.order[p.step] if p.step < 2 else "z"
        blocks = p.n * (2 if p.step == 0 else 1)
        base = used.get(link, 0)
        used[link] = base + blocks
        near = [number(a) for a in p.near]
        held = [(number(a), at) for a, at in p.held]
        plans.append((p, link, base, near, held))
    links = sorted(used)
    shapes = [
        (ways, used[k], r, width) if k == "z" and last_by_rows else (used[k], depth, width)
        for k in links
    ]
    rooms, counts = [], []
    for p, link, base, near, held in plans:
        each = 2 if p.step == 0 else 1
        counts.append((each, len(near) + len(held)))
        rooms += [(each * p.n, depth, width)] * (len(near) + len(held))
    copies_needed = sum(each * terms for each, terms in counts)

    def body(me_ref, *refs):
        sources = refs[: len(arrays)]
        outs = dict(zip(links, refs[len(arrays) : len(arrays) + len(links)]))
        held_refs = refs[len(arrays) + len(links) : -1]
        sems = refs[-1]
        mine = {name: me_ref[PLACE[name]] for name in PLACE}
        groups = []
        room = 0
        sem = 0
        for p, link, base, near, held in plans:
            group = []
            if p.step == 0:
                for term in near:
                    for k in range(2):
                        pick = {p.order[0]: 1 - mine[p.order[0]], p.order[1]: k}
                        source = sources[term].at[pl.ds(p.first, p.n), pick["h"], pick["x"]]
                        group.append((source, held_refs[room].at[pl.ds(k * p.n, p.n)]))
                    room += 1
            else:
                last = p.order[1]
                pick = {p.order[0]: mine[p.order[0]]}
                pick[last] = 1 - mine[last] if p.step == 1 else mine[last]
                for term in near:
                    source = sources[term].at[pl.ds(p.first, p.n), pick["h"], pick["x"]]
                    group.append((source, held_refs[room]))
                    room += 1
                for i, (term, at) in enumerate(held):
                    start = at + pick[last] * p.n if i == 0 else at
                    group.append((sources[term].at[pl.ds(start, p.n)], held_refs[room]))
                    room += 1
            made_copies = []
            for source, target in group:
                made_copies.append(pltpu.make_async_copy(source, target, sems.at[sem]))
                sem += 1
            groups.append(made_copies)
        for group in groups:
            for copy in group:
                copy.start()
        room = 0
        for (p, link, base, near, held), (each, terms), group in zip(plans, counts, groups):
            these = held_refs[room : room + terms]
            room += terms
            for copy in group:
                copy.wait()

            @pl.loop(0, each * p.n)
            def _(i, these=these, base=base, out=outs[link], last=p.step == 2 and last_by_rows):
                value = these[0][i].astype(F32)
                for one in these[1:]:
                    value = value + one[i].astype(F32)
                value = value.astype(BF16)
                if last:
                    for k in range(ways):
                        out[k, base + i] = value[k * r : (k + 1) * r]
                else:
                    out[base + i] = value

    moved = sum(2 * math.prod(room) for room in rooms) + sum(2 * math.prod(shape) for shape in shapes)
    sums = pl.pallas_call(
        body,
        out_shape=[jax.ShapeDtypeStruct(shape, BF16) for shape in shapes],
        in_specs=[SCALARS] + [pl.BlockSpec(memory_space=pltpu.HBM)] * len(arrays),
        out_specs=[pl.BlockSpec(memory_space=pltpu.VMEM)] * len(links),
        scratch_shapes=[pltpu.VMEM(room, BF16) for room in rooms]
        + [pltpu.SemaphoreType.DMA((copies_needed,))],
        compiler_params=pltpu.CompilerParams(vmem_limit_bytes=VMEM),
        cost_estimate=pl.CostEstimate(flops=0, bytes_accessed=moved, transcendentals=0),
    )(me, *arrays)
    return [(p, link, base) for p, link, base, _, _ in plans], dict(zip(links, sums))


def cross(a, name):
    axis, bit = ("head", 0) if name == "h" else ("clip", 1 if name == "x" else 0)
    size = lax.axis_size(axis)
    return lax.ppermute(a, axis, [(i, i ^ (1 << bit)) for i in range(size)])


def pieces_of(halves_of):
    total = sum(keep.shape[0] for keep, _ in halves_of)
    found = []
    seen = 0
    for keep, send in halves_of:
        got = cross(send, "c")
        n = keep.shape[0]
        first = min(max((total + 1) // 2 - seen, 0), n)
        if first:
            found.append(Piece(keep, got, 0, first, ("x", "h")))
        if n > first:
            found.append(Piece(keep, got, first, n - first, ("h", "x")))
        seen += n
    return found


def move(x, pieces, me, at_end=False):
    plans, sums = fold(pieces, me, at_end)
    x, sums = lax.optimization_barrier((x, sums))
    got = {}
    for link, array in sums.items():
        if link == "z":
            if at_end:
                every = lax.all_to_all(array, "seq", split_axis=0, concat_axis=0, tiled=True)
                got[link] = jnp.sum(every.astype(F32), axis=0)
            else:
                own = lax.psum_scatter(array, "seq", scatter_dimension=1, tiled=True)
                got[link] = own.astype(F32)
        else:
            got[link] = cross(array, link)
    for p, link, base in plans:
        if link == "z":
            p.result = got[link][base : base + p.n]
        else:
            p.held.append((got[link], base))
        p.step += 1
    return x


def settle(x, pieces):
    arrays = []
    for p in pieces:
        if not any(p.held[-1][0] is a for a in arrays):
            arrays.append(p.held[-1][0])
    x, came = lax.optimization_barrier((x, arrays))
    for p in pieces:
        for old, new in zip(arrays, came):
            if p.held[-1][0] is old:
                p.held[-1] = (new, p.held[-1][1])
                break
    return x


def reduce_plain(halves_of, core):
    def joined(keep, send):
        low = jnp.where(core == 0, keep, send)
        high = jnp.where(core == 0, send, keep)
        n, shares, pairs, depth, width = keep.shape
        return jnp.stack((low, high), axis=3).reshape(n, shares, 2 * pairs * depth, width)

    g = jnp.concatenate([joined(*pair) for pair in halves_of], axis=0)
    g = lax.psum_scatter(g, "head", scatter_dimension=1, tiled=True)
    g = lax.psum_scatter(g.astype(F32), ("clip", "seq"), scatter_dimension=2, tiled=True)
    return g[:, 0]


def gather_norms(gain, bias):
    layers, norms, part = gain.shape
    both = jnp.concatenate((gain, bias), axis=1).reshape(1, -1)
    count = lax.axis_size("clip") * lax.axis_size("seq") * lax.axis_size("head")
    width = round_up(both.shape[1], 128)
    padded = jnp.pad(both, ((0, 0), (0, width - both.shape[1])))
    every = lax.all_to_all(
        jnp.broadcast_to(padded, (count, width)), ALL, split_axis=0, concat_axis=0, tiled=True
    )[:, : both.shape[1]]
    return every.reshape(count, layers * 2 * norms, part).transpose(1, 0, 2).reshape(layers, 2 * norms, -1)


def reduce_norms(sums):
    count = lax.axis_size("clip") * lax.axis_size("seq") * lax.axis_size("head")
    rows, features = sums.shape
    part = features // count
    a = sums.reshape(rows, count, part).transpose(1, 0, 2).reshape(count, rows * part)
    width = round_up(rows * part, 128)
    a = jnp.pad(a, ((0, 0), (0, width - rows * part)))
    every = lax.all_to_all(a, ALL, split_axis=0, concat_axis=0, tiled=True)
    return jnp.sum(every, axis=0)[: rows * part].reshape(rows, part)


def on_device(
    tokens,
    cotangent,
    time_qkv,
    time_out,
    time_mix,
    space_qkv,
    space_out,
    mlp_in,
    mlp_out,
    norm_gain,
    norm_bias,
):
    layers = time_qkv.shape[0]
    clips, frames, places, d = tokens.shape
    ways = lax.axis_size("seq")
    shards = lax.axis_size("clip") * ways
    rows = Rows(clips * frames, places, ways)
    shares = lax.axis_size("head")

    def as_rows(a):
        a = a.astype(F32).reshape(rows.frames, places, d)
        a = jnp.pad(a, ((0, 0), (0, rows.frame_rows - places), (0, 0)))
        return a.reshape(rows.rows, d)

    def from_rows(a):
        a = a.reshape(rows.frames, rows.frame_rows, d)[:, :places]
        return a.reshape(tokens.shape)

    gbs = gather_norms(norm_gain, norm_bias)
    gb = [gbs[l] for l in range(layers)]
    packs = [
        pack_attention(time_qkv[l], time_out[l], time_mix[l], space_qkv[l], space_out[l])
        for l in range(layers)
    ]
    packs_ff = [pack_feed_forward(mlp_in[l], mlp_out[l], time_qkv.shape[3]) for l in range(layers)]
    weights = [gather_slabs(pack) for pack in packs]
    mixes = [mix_whole(w[-1], shards) for w in weights]
    quick = lax.axis_size("clip") == 4 and shares == 2 and ways == 4 and time_qkv.shape[1] % 16 == 0

    halves = Halves(lax.axis_size("clip"), d, time_qkv.shape[3])
    clip = lax.axis_index("clip")
    member = member_of(clip, lax.axis_index("seq"))
    me = jnp.stack((clip & 1, (clip >> 1) & 1, lax.axis_index("head"), member, lax.axis_index("seq"))).astype(
        jnp.int32
    )
    if quick:
        spreads = [Spread(pack, me) for pack in packs_ff]
        spreads[0].step(())
        weights_ff = []
    else:
        weights_ff = [gather_slabs(pack) for pack in packs_ff]

    home = go_home(tokens)
    if quick:
        (home, gb, later), first = (home, gb, packs_ff[1:]), spreads[0]
        home, gb, later = first.step((home, gb, later))
        for spread, pack in zip(spreads[1:], later):
            spread.come = pack
            spread.step(())
    x = as_rows(home)
    send = send_first(rows, x, gb[0], me)
    kept = []
    for l in range(layers):
        w = weights[l]
        send = swap_places(send)
        if quick and l == 0:
            for _ in range(3):
                send = first.step(send)
            weights_ff.append(first.come)
            send, weights_ff[0] = lax.optimization_barrier((send, weights_ff[0]))
            for spread in spreads[1:]:
                send = spread.step(send)
        elif quick:
            send = spreads[l].step(send)
            weights_ff.append(spreads[l].come)
        a1, qkv1, log1, o1_time = time_forward(rows, send, w)
        back = swap_places(o1_time)
        if quick and l == 0:
            for spread in spreads[1:]:
                back = spread.step(back)
        o1, y1, x1, qkv2 = middle_forward(rows, back, x, w, mixes[l], gb[l], me)
        o2, x2, log2 = space_forward(rows, qkv2, x1, w)
        if quick and l == 0:
            for spread in spreads[1:]:
                x2 = spread.step(x2)
        kept.append((x, a1, qkv1, log1, o1, y1, x1, qkv2, o2, log2, x2))
        if l + 1 < layers:
            x, *send = mlp_forward(rows, x2, weights_ff[l], gb[l], gb[l + 1], me)

    grad = as_rows(go_home(cotangent))
    norm_rows = [None] * layers
    summed = [None] * layers
    late = []
    for l in reversed(range(layers)):
        w = weights[l]
        x, a1, qkv1, log1, o1, y1, x1, qkv2, o2, log2, x2 = kept[l]
        grad, g_ff, s3, x3 = mlp_backward(
            rows, grad, x2, weights_ff[l], gb[l], me, halves, l + 1 == layers
        )
        if x3:
            output = go_back(from_rows(x3[0].astype(BF16)))
        if quick:
            ff = pieces_of(g_ff)
            if late:
                grad = settle(grad, late)
                grad = move(grad, late, me)
                late = [p for p in late if p.step < 3]
        grad, g_space, s2 = space_backward(rows, grad, x1, qkv2, o2, log2, w, gb[l], me, halves)
        if quick:
            space = pieces_of([g_space])
            if late:
                grad = settle(grad, late)
            grad, output = move((grad, output), ff, me)
        do1, g_out = middle_backward(rows, grad, y1, o1, w, mixes[l], me, halves, shards)
        do1 = swap_places(do1)
        if quick:
            do1 = move(do1, ff + space + late, me)
        da1, g_time = time_backward(rows, do1, a1, qkv1, log1, w, me, halves)
        if quick:
            da1 = settle(da1, ff + space)
        da1 = swap_places(da1)
        if quick:
            rest = pieces_of([g_out] + g_time)
            da1 = move(da1, ff + space + rest, me)
            late = space + rest
        grad, s1 = first_norm_back(rows, da1, x, grad, gb[l], me)
        norm_rows[l] = jnp.concatenate((s1[0:1], s2[0:1], s3[0:1], s1[1:2], s2[1:2], s3[1:2]), axis=0)
        if quick:
            summed[l] = ff + space + rest
        else:
            summed[l] = [reduce_plain(g_ff + [g_space, g_out] + g_time, clip & 1)]
    if quick:
        tokens_grad = move(go_back(from_rows(grad.astype(BF16))), late, me)
        move((), rest, me, True)
        summed = [[p.result for p in some] for some in summed]
    cuts = (2 * g_ff[0][0].shape[0], g_space[0].shape[0], g_out[0].shape[0], len(g_time))
    results = []
    for some in summed:
        slabs_of = jnp.concatenate(some, axis=0)
        ends = [sum(cuts[: i + 1]) for i in range(4)]
        results.append([slabs_of[e - c : e] for c, e in zip(cuts, ends)])
    if not quick:
        tokens_grad = go_back(from_rows(grad.astype(BF16)))
    tokens_grad = tokens_grad.astype(F32)
    norm_sums = reduce_norms(jnp.concatenate(norm_rows, axis=0)).reshape(layers, 2, 3, -1)

    def stacked(form):
        return jnp.stack([form(*results[l]) for l in range(layers)])

    def rows_of(a):
        return a.transpose(1, 0, 2)

    def flat(a):
        return rows_of(a).reshape(a.shape[1], -1)

    def mix_rows(a):
        r, width = a.shape
        return a.reshape(shares, r // shares, width).transpose(1, 0, 2).reshape(r // shares, -1)

    per_share = mlp_in.shape[2] // time_qkv.shape[3]
    return (
        output,
        tokens_grad,
        stacked(lambda ff, s, t, q: rows_of(q)),
        stacked(lambda ff, s, t, q: t[0].T),
        stacked(lambda ff, s, t, q: mix_rows(t[1])),
        stacked(lambda ff, s, t, q: rows_of(s[1:])),
        stacked(lambda ff, s, t, q: s[0].T),
        stacked(lambda ff, s, t, q: flat(ff[:per_share])),
        stacked(lambda ff, s, t, q: flat(ff[per_share:]).T),
        norm_sums[:, 0],
        norm_sums[:, 1],
    )


def solution(mesh):
    token_spec = P(("clip", "head"), "seq", None, None)
    in_specs = (
        token_spec,
        token_spec,
        P(None, ("clip", "seq"), None, "head"),
        P(None, "head", ("clip", "seq")),
        P(None, ("clip", "seq", "head"), None),
        P(None, ("clip", "seq"), None, "head"),
        P(None, "head", ("clip", "seq")),
        P(None, ("clip", "seq"), "head"),
        P(None, "head", ("clip", "seq")),
        P(None, None, ("clip", "seq", "head")),
        P(None, None, ("clip", "seq", "head")),
    )
    return jax.shard_map(
        on_device, mesh=mesh, in_specs=in_specs, out_specs=in_specs, check_vma=False
    )
```

```python
import functools
import math

import jax
import jax.numpy as jnp
from jax import lax
from jax.experimental import pallas as pl
from jax.experimental.pallas import tpu as pltpu
from jax.sharding import PartitionSpec as P

HEAD_DIM = 64
NORM_EPS = 1e-06
HALF_ROOT = 0.7071067811865476
INV_ROOT_TAU = 0.3989422804014327
LOG2E = 1.4426950408889634
FAR = -1e30
LANES = 128
VMEM = 56 * 1024 * 1024
SHOWN = 1.0
ALL = ("clip", "seq", "head")
BF16 = jnp.bfloat16
F32 = jnp.float32


def round_up(value, step):
    return -(-value // step) * step


def nn(a, b):
    return lax.dot_general(a, b, (((1,), (0,)), ((), ())), preferred_element_type=F32)


def nt(a, b):
    return lax.dot_general(a, b, (((1,), (1,)), ((), ())), preferred_element_type=F32)


def tn(a, b):
    return lax.dot_general(a, b, (((0,), (0,)), ((), ())), preferred_element_type=F32)


def norm_parts(x):
    mean = jnp.mean(x, axis=-1, keepdims=True)
    centred = x - mean
    spread = lax.rsqrt(jnp.mean(centred * centred, axis=-1, keepdims=True) + NORM_EPS)
    return centred * spread, spread


def norm_rounded(x, gain, bias):
    hat, _ = norm_parts(x)
    return (hat * gain + bias).astype(BF16)


def norm_back(u, x, gain):
    hat, spread = norm_parts(x)
    scaled = u * gain
    mean_scaled = jnp.mean(scaled, axis=-1, keepdims=True)
    mean_cross = jnp.mean(scaled * hat, axis=-1, keepdims=True)
    change = spread * (scaled - mean_scaled - hat * mean_cross)
    sums = jnp.concatenate(
        (jnp.sum(u * hat, axis=0, keepdims=True), jnp.sum(u, axis=0, keepdims=True)), axis=0
    )
    return change, sums


class Rows:
    def __init__(self, frames, places, ways):
        self.frames = frames
        self.places = places
        self.ways = ways
        self.frame_rows = round_up(places, 16)
        self.rows = frames * self.frame_rows
        self.block = places // ways
        self.chunk = round_up(frames * self.block, 8)
        self.time_rows = ways * self.chunk

    def split(self, r):
        way = jnp.zeros_like(r)
        for k in range(1, self.ways):
            way = way + (r >= k * self.chunk).astype(jnp.int32)
        rest = r - way * self.chunk
        frame = jnp.zeros_like(r)
        for k in range(1, self.frames):
            frame = frame + (rest >= k * self.block).astype(jnp.int32)
        real = rest < self.frames * self.block
        return way, frame, rest - frame * self.block, real

    def to_time(self, k, member):
        r = lax.broadcasted_iota(jnp.int32, (self.chunk, 1), 0)
        _, frame, place, real = self.split(r)
        way = jnp.bitwise_xor(member, k)
        source = jnp.where(real, frame * self.frame_rows + way * self.block + place, -1)
        c = lax.broadcasted_iota(jnp.int32, (self.chunk, self.rows), 1)
        return jnp.where(c == source, 1.0, 0.0).astype(BF16)

    def gathered(self, chunk_refs, member):
        total = tn(self.to_time(0, member), chunk_refs[0][...])
        for k in range(1, self.ways):
            total = total + tn(self.to_time(k, member), chunk_refs[k][...])
        return total

    def chunks(self, width, block=None, index=None):
        return [
            made((self.chunk, width), BF16)
            if block is None
            else made((self.chunk, width), BF16, (self.chunk, block), index)
            for _ in range(self.ways)
        ]

    def time_bias(self):
        def label(r):
            _, _, place, real = self.split(r)
            return jnp.where(real, place, -1)

        a = label(lax.broadcasted_iota(jnp.int32, (self.time_rows, 1), 0))
        b = label(lax.broadcasted_iota(jnp.int32, (1, self.time_rows), 1))
        return jnp.where(a == b, 0.0, FAR).astype(F32)

    def space_bias(self):
        a = lax.broadcasted_iota(jnp.int32, (self.frame_rows, 1), 0)
        return jnp.where(a < self.places, 0.0, FAR).astype(F32)


def lane_masks(rows):
    lane = lax.broadcasted_iota(jnp.int32, (rows, LANES), 1)
    return lane < HEAD_DIM


def one_of(value, low, half):
    zero = jnp.zeros_like(value)
    return jnp.where(low, value, zero) if half == 0 else jnp.where(low, zero, value)


def pair_forward(q, k, v, bias, rate):
    low = lane_masks(q.shape[0])
    mixed, logs = [], []
    for half in range(2):
        s = nt(k, one_of(q, low, half)) + bias
        peak = jnp.max(s, axis=0, keepdims=True)
        e = jnp.exp2((s - peak) * rate)
        total = jnp.sum(e, axis=0, keepdims=True)
        soft = (e * (1.0 / total)).astype(BF16)
        mixed.append(tn(soft, v))
        logs.append(peak * rate + jnp.log2(total))
    return jnp.where(low, mixed[0], mixed[1]).astype(BF16), logs


def pair_backward(q, k, v, do, logs, bias, rate, scale):
    low = lane_masks(q.shape[0])
    dq, dk, dv = [], [], []
    for half in range(2):
        s = nt(k, one_of(q, low, half)) + bias
        soft = jnp.exp2(s * rate - logs[half])
        dp = nt(v, one_of(do, low, half))
        ds = (soft * (dp - jnp.sum(soft * dp, axis=0, keepdims=True))).astype(BF16)
        dv.append(nn(soft.astype(BF16), do))
        dk.append(nn(ds, q))
        dq.append(tn(ds, k))
    return (
        (jnp.where(low, dq[0], dq[1]) * scale).astype(BF16),
        (jnp.where(low, dk[0], dk[1]) * scale).astype(BF16),
        jnp.where(low, dv[0], dv[1]).astype(BF16),
    )


def split_rows(value, keep_ref, send_ref, at, room_ref, me_ref):
    mine = me_ref[0]
    room_ref[...] = value.reshape(room_ref.shape)
    keep_ref[at] = room_ref[:, mine].astype(BF16)
    send_ref[at] = room_ref[:, 1 - mine].astype(BF16)


class Halves:
    def __init__(self, clips, depth, width):
        self.pairs = clips // 2
        self.rows = depth // clips
        self.width = width

    def array(self, lead, block, index):
        tail = (self.pairs, self.rows, self.width)
        one = lambda: made(lead + tail, BF16, block + tail, lambda *g: index(*g) + (0, 0, 0))
        return [one(), one()]

    def room(self):
        return pltpu.VMEM((self.pairs, 2, self.rows, self.width), F32)


SCALARS = pl.BlockSpec(memory_space=pltpu.SMEM)


def call(body, grid, ins, outs, scratch, args, flops=0):
    specs = [spec for spec in ins]
    moved = sum(math.prod(o.shape) * o.dtype.itemsize for o, _ in outs)
    moved += sum(math.prod(a.shape) * a.dtype.itemsize for a in args)
    return pl.pallas_call(
        body,
        out_shape=[shape for shape, _ in outs],
        grid=grid,
        in_specs=specs,
        out_specs=[spec for _, spec in outs],
        scratch_shapes=scratch,
        compiler_params=pltpu.CompilerParams(vmem_limit_bytes=VMEM),
        cost_estimate=pl.CostEstimate(
            flops=int(flops * SHOWN), bytes_accessed=int(moved * SHOWN), transcendentals=0
        ),
    )(*args)


def whole(shape):
    zeros = (0,) * len(shape)
    return pl.BlockSpec(shape, lambda *_: zeros)


def made(shape, dtype, block=None, index=None):
    spec = whole(shape) if block is None else pl.BlockSpec(block, index)
    return jax.ShapeDtypeStruct(shape, dtype), spec


def slabs(count, first, width, depth):
    return pl.BlockSpec((count, 1, depth, width), lambda h, *_: (first // count, h, 0, 0))


def send_first(rows, x, gb, me):
    def body(me_ref, x_ref, gb_ref, *out_refs):
        a = norm_rounded(x_ref[...], gb_ref[0:1], gb_ref[3:4])
        for k in range(rows.ways):
            out_refs[k][...] = nn(rows.to_time(k, me_ref[3]), a).astype(BF16)

    d = x.shape[1]
    return call(
        body, (1,), [SCALARS, whole(x.shape), whole(gb.shape)], rows.chunks(d), [], (me, x, gb)
    )


def time_forward(rows, chunks, w):
    t, d = rows.time_rows, chunks[0].shape[1]
    width = w.shape[3]
    shares = w.shape[1]
    pairs = width // LANES
    ways = rows.ways
    rate = LOG2E / math.sqrt(HEAD_DIM)

    def body(*refs):
        chunk_refs = refs[:ways]
        w_ref, a_ref, qkv_ref, log_ref = refs[ways : ways + 4]
        out_refs = refs[ways + 4 : 2 * ways + 4]
        bias_ref, mixed_ref = refs[2 * ways + 4 :]

        @pl.when(pl.program_id(0) == 0)
        def _():
            bias_ref[...] = rows.time_bias()
            for k in range(ways):
                a_ref[k * rows.chunk : (k + 1) * rows.chunk] = chunk_refs[k][...]

        act = a_ref[...]
        for g in range(3):
            qkv_ref[g] = nn(act, w_ref[g, 0]).astype(BF16)

        @pl.loop(0, pairs)
        def _(i):
            lanes = pl.ds(pl.multiple_of(i * LANES, LANES), LANES)
            mixed, logs = pair_forward(
                qkv_ref[0, :, lanes], qkv_ref[1, :, lanes], qkv_ref[2, :, lanes], bias_ref[...], rate
            )
            mixed_ref[:, lanes] = mixed
            log_ref[0, i] = jnp.concatenate(logs, axis=0)

        for k in range(ways):
            out_refs[k][...] = mixed_ref[k * rows.chunk : (k + 1) * rows.chunk]

    got = call(
        body,
        (shares,),
        [whole(c.shape) for c in chunks] + [slabs(3, 0, width, d)],
        [
            made((t, d), BF16),
            made((3, t, d), BF16, (3, t, width), lambda h: (0, 0, h)),
            made((shares, pairs, 2, t), F32, (1, pairs, 2, t), lambda h: (h, 0, 0, 0)),
            *rows.chunks(d, width, lambda h: (0, h)),
        ],
        [pltpu.VMEM((t, t), F32), pltpu.VMEM((t, width), BF16)],
        (*chunks, w),
        flops=2 * t * d * 3 * d,
    )
    return got[0], got[1], got[2], got[3:]


def middle_forward(rows, back, x, w, ws, mix, gb, me):
    t, d = x.shape
    width = w.shape[3]
    shares = w.shape[1]

    def body(me_ref, *refs):
        x_ref, to_ref, sq_ref, mix_ref, gb_ref, o1_ref, y1_ref, x1_ref, qkv_ref = refs[rows.ways :]
        o1 = rows.gathered(refs[: rows.ways], me_ref[3]).astype(BF16)
        o1_ref[...] = o1
        y1 = jnp.zeros((t, d), F32)
        for h in range(shares):
            y1 = y1 + nt(o1[:, h * width : (h + 1) * width], to_ref[0, h])
        y1 = y1.astype(BF16)
        y1_ref[...] = y1
        x1 = x_ref[...] + nn(y1, mix_ref[...])
        x1_ref[...] = x1
        a2 = norm_rounded(x1, gb_ref[1:2], gb_ref[4:5])
        for g in range(3):
            for h in range(shares):
                qkv_ref[g, :, h * width : (h + 1) * width] = nn(a2, sq_ref[g, h]).astype(BF16)

    return call(
        body,
        (1,),
        [
            SCALARS,
            *(whole(c.shape) for c in back),
            whole(x.shape),
            pl.BlockSpec((1, shares, d, width), lambda i: (3, 0, 0, 0)),
            pl.BlockSpec((3, shares, d, width), lambda i: (0, 0, 0, 0)),
            whole(mix.shape),
            whole(gb.shape),
        ],
        [made((t, d), BF16), made((t, d), BF16), made((t, d), F32), made((3, t, d), BF16)],
        [],
        (me, *back, x, w, ws, mix, gb),
        flops=2 * t * d * 5 * d,
    )


def space_forward(rows, qkv, x1, w):
    t, d = x1.shape
    width = w.shape[3]
    shares = w.shape[1]
    pairs = width // LANES
    rate = LOG2E / math.sqrt(HEAD_DIM)
    n = rows.frame_rows

    def body(qkv_ref, x1_ref, w_ref, o2_ref, x2_ref, log_ref):
        bias = rows.space_bias()

        @pl.loop(0, pairs)
        def _(i):
            lanes = pl.ds(pl.multiple_of(i * LANES, LANES), LANES)
            for f in range(rows.frames):
                at = slice(f * n, (f + 1) * n)
                mixed, logs = pair_forward(
                    qkv_ref[0, at, lanes], qkv_ref[1, at, lanes], qkv_ref[2, at, lanes], bias, rate
                )
                o2_ref[at, lanes] = mixed
                log_ref[0, i, f] = jnp.concatenate(logs, axis=0)

        @pl.when(pl.program_id(0) == 0)
        def _():
            x2_ref[...] = x1_ref[...]

        x2_ref[...] += nt(o2_ref[...], w_ref[0, 0])

    return call(
        body,
        (shares,),
        [
            pl.BlockSpec((3, t, width), lambda h: (0, 0, h)),
            whole(x1.shape),
            slabs(1, 3, width, d),
        ],
        [
            made((t, d), BF16, (t, width), lambda h: (0, h)),
            made((t, d), F32),
            made(
                (shares, pairs, rows.frames, 2, n),
                F32,
                (1, pairs, rows.frames, 2, n),
                lambda h: (h, 0, 0, 0, 0),
            ),
        ],
        [],
        (qkv, x1, w),
        flops=2 * t * d * d,
    )


def ff_slab(first, per_share, depth, width):
    return pl.BlockSpec(
        (1, 1, depth, width), lambda j: (first + j % per_share, j // per_share, 0, 0)
    )


def mlp_forward(rows, x2, w, gb, gb_next, me):
    t, d = x2.shape
    width = w.shape[3]
    shares = w.shape[1]
    per_share = (w.shape[0] - 4) // 2
    steps = shares * per_share

    def body(x2_ref, wi_ref, wo_ref, gb_ref, me_ref, gn_ref, x3_ref, *rest):
        send_refs, a3_ref = rest[:-1], rest[-1]
        j = pl.program_id(0)

        @pl.when(j == 0)
        def _():
            a3_ref[...] = norm_rounded(x2_ref[...], gb_ref[2:3], gb_ref[5:6])
            x3_ref[...] = x2_ref[...]

        hid = nn(a3_ref[...], wi_ref[0, 0])
        act = (0.5 * hid * (1.0 + lax.erf(hid * HALF_ROOT))).astype(BF16)
        x3_ref[...] += nt(act, wo_ref[0, 0])

        @pl.when(j == steps - 1)
        def _():
            a = norm_rounded(x3_ref[...], gn_ref[0:1], gn_ref[3:4])
            for k in range(rows.ways):
                send_refs[k][...] = nn(rows.to_time(k, me_ref[3]), a).astype(BF16)

    ins = [
        whole(x2.shape),
        ff_slab(4, per_share, d, width),
        ff_slab(4 + per_share, per_share, d, width),
        whole(gb.shape),
    ]
    ins += [SCALARS, whole(gb_next.shape)]
    outs = [made((t, d), F32)] + rows.chunks(d)
    args = (x2, w, w, gb, me, gb_next)
    return call(
        body, (steps,), ins, outs, [pltpu.VMEM((t, d), BF16)], args, flops=4 * t * d * width * steps
    )


def mlp_backward(rows, grad, x2, w, gb, me, halves, with_output):
    t, d = x2.shape
    width = w.shape[3]
    shares = w.shape[1]
    per_share = (w.shape[0] - 4) // 2
    steps = shares * per_share

    def body(me_ref, g_ref, x2_ref, wi_ref, wo_ref, gb_ref, go_ref, ki_ref, si_ref, ko_ref, so_ref, sums_ref, *rest):
        if with_output:
            x3_ref, *rest = rest
        a3_ref, a3t_ref, e3_ref, e3t_ref, u_ref, room_ref = rest
        j = pl.program_id(0)

        @pl.when(j == 0)
        def _():
            hat, _ = norm_parts(x2_ref[...])
            a3 = hat * gb_ref[2:3] + gb_ref[5:6]
            a3_ref[...] = a3.astype(BF16)
            a3t_ref[...] = a3.T.astype(BF16)
            g = g_ref[...]
            e3_ref[...] = g.astype(BF16)
            e3t_ref[...] = g.T.astype(BF16)
            u_ref[...] = jnp.zeros((t, d), F32)
            if with_output:
                x3_ref[...] = x2_ref[...]

        hid = nn(a3_ref[...], wi_ref[0, 0])
        phi = 0.5 * (1.0 + lax.erf(hid * HALF_ROOT))
        act = (hid * phi).astype(BF16)
        slope = phi + hid * jnp.exp(-0.5 * hid * hid) * INV_ROOT_TAU
        dhid = (nn(e3_ref[...], wo_ref[0, 0]) * slope).astype(BF16)
        split_rows(nn(e3t_ref[...], act), ko_ref, so_ref, (0, 0), room_ref, me_ref)
        split_rows(nn(a3t_ref[...], dhid), ki_ref, si_ref, (0, 0), room_ref, me_ref)
        u_ref[...] += nt(dhid, wi_ref[0, 0])
        if with_output:
            x3_ref[...] += nt(act, wo_ref[0, 0])

        @pl.when(j == steps - 1)
        def _():
            change, sums = norm_back(u_ref[...], x2_ref[...], gb_ref[2:3])
            go_ref[...] = g_ref[...] + change
            sums_ref[...] = sums

    slab_outs = [
        one
        for _ in range(2)
        for one in halves.array(
            (per_share, shares), (1, 1), lambda j: (j % per_share, j // per_share)
        )
    ]
    grad, ki, si, ko, so, sums, *x3 = call(
        body,
        (steps,),
        [
            SCALARS,
            whole(grad.shape),
            whole(x2.shape),
            ff_slab(4, per_share, d, width),
            ff_slab(4 + per_share, per_share, d, width),
            whole(gb.shape),
        ],
        [made((t, d), F32), *slab_outs, made((2, d), F32)] + [made((t, d), F32)] * with_output,
        [
            pltpu.VMEM((t, d), BF16),
            pltpu.VMEM((d, t), BF16),
            pltpu.VMEM((t, d), BF16),
            pltpu.VMEM((d, t), BF16),
            pltpu.VMEM((t, d), F32),
            halves.room(),
        ],
        (me, grad, x2, w, w, gb),
        flops=10 * t * d * width * steps,
    )
    return grad, [(ki, si), (ko, so)], sums, x3


def space_backward(rows, grad, x1, qkv, o2, logs, w, gb, me, halves):
    t, d = x1.shape
    width = w.shape[3]
    shares = w.shape[1]
    pairs = width // LANES
    scale = 1.0 / math.sqrt(HEAD_DIM)
    rate = LOG2E * scale
    n = rows.frame_rows

    def body(me_ref, g_ref, x1_ref, qkv_ref, o2_ref, log_ref, wo_ref, wq_ref, gb_ref, go_ref, keep_ref, send_ref, sums_ref, e2_ref, e2t_ref, a2t_ref, do_ref, dqkv_ref, u_ref, room_ref):
        h = pl.program_id(0)

        @pl.when(h == 0)
        def _():
            g = g_ref[...]
            e2_ref[...] = g.astype(BF16)
            e2t_ref[...] = g.T.astype(BF16)
            hat, _ = norm_parts(x1_ref[...])
            a2t_ref[...] = (hat * gb_ref[1:2] + gb_ref[4:5]).T.astype(BF16)
            u_ref[...] = jnp.zeros((t, d), F32)

        bias = rows.space_bias()
        split_rows(nn(e2t_ref[...], o2_ref[...]), keep_ref, send_ref, (0, 0), room_ref, me_ref)
        do_ref[...] = nn(e2_ref[...], wo_ref[0, 0]).astype(BF16)

        @pl.loop(0, pairs)
        def _(i):
            lanes = pl.ds(pl.multiple_of(i * LANES, LANES), LANES)
            for f in range(rows.frames):
                at = slice(f * n, (f + 1) * n)
                log = log_ref[0, i, f]
                grads = pair_backward(
                    qkv_ref[0, at, lanes],
                    qkv_ref[1, at, lanes],
                    qkv_ref[2, at, lanes],
                    do_ref[at, lanes],
                    (log[0:1], log[1:2]),
                    bias,
                    rate,
                    scale,
                )
                for part in range(3):
                    dqkv_ref[part, at, lanes] = grads[part]

        for part in range(3):
            split_rows(
                nn(a2t_ref[...], dqkv_ref[part]), keep_ref, send_ref, (part + 1, 0), room_ref, me_ref
            )
            u_ref[...] += nt(dqkv_ref[part], wq_ref[part, 0])

        @pl.when(h == shares - 1)
        def _():
            change, sums = norm_back(u_ref[...], x1_ref[...], gb_ref[1:2])
            go_ref[...] = g_ref[...] + change
            sums_ref[...] = sums

    grad, keep, send, sums = call(
        body,
        (shares,),
        [
            SCALARS,
            whole(grad.shape),
            whole(x1.shape),
            pl.BlockSpec((3, t, width), lambda h: (0, 0, h)),
            pl.BlockSpec((t, width), lambda h: (0, h)),
            pl.BlockSpec((1,) + logs.shape[1:], lambda h: (h, 0, 0, 0, 0)),
            slabs(1, 3, width, d),
            slabs(3, 0, width, d),
            whole(gb.shape),
        ],
        [
            made((t, d), F32),
            *halves.array((4, shares), (4, 1), lambda h: (0, h)),
            made((2, d), F32),
        ],
        [
            pltpu.VMEM((t, d), BF16),
            pltpu.VMEM((d, t), BF16),
            pltpu.VMEM((d, t), BF16),
            pltpu.VMEM((t, width), BF16),
            pltpu.VMEM((3, t, width), BF16),
            pltpu.VMEM((t, d), F32),
            halves.room(),
        ],
        (me, grad, x1, qkv, o2, logs, w, w, gb),
        flops=2 * t * d * d * 8,
    )
    return grad, (keep, send), sums


def mix_fits(depth, shards, shares):
    return depth // (shards * shares) % 8 == 0


def middle_backward(rows, grad, y1, o1, w, mix, me, halves, shards):
    t, d = grad.shape
    width = w.shape[3]
    shares = w.shape[1]
    fits = mix_fits(d, shards, shares)
    part = d // (shards * shares)

    def body(me_ref, g_ref, y1_ref, o1_ref, to_ref, mix_ref, *rest):
        send_refs, rest = rest[: rows.ways], rest[rows.ways :]
        gk_ref, gs_ref, *rest = rest
        if fits:
            room_ref, order_ref = rest
        else:
            gm_ref, room_ref = rest
        e1 = g_ref[...].astype(BF16)
        dy1 = nt(e1, mix_ref[...]).astype(BF16)
        sends = [rows.to_time(k, me_ref[3]) for k in range(rows.ways)]
        for h in range(shares):
            lanes = slice(h * width, (h + 1) * width)
            do1 = nn(dy1, to_ref[0, h]).astype(BF16)
            for k in range(rows.ways):
                send_refs[k][:, lanes] = nn(sends[k], do1).astype(BF16)
            split_rows(tn(dy1, o1_ref[:, lanes]), gk_ref, gs_ref, (0, h), room_ref, me_ref)
        gm = tn(y1_ref[...], e1)
        if fits:
            gm = gm.reshape(shards, shares, part, d)
            for h in range(shares):
                for half in range(shares):
                    order_ref[:, half] = gm[:, h, :, half * width : (half + 1) * width]
                split_rows(order_ref[...], gk_ref, gs_ref, (1, h), room_ref, me_ref)
        else:
            gm_ref[...] = gm.astype(BF16)

    outs = rows.chunks(d)
    outs += halves.array((1 + fits, shares), (1 + fits, shares), lambda i: (0, 0))
    scratch = [halves.room()]
    if fits:
        scratch.append(pltpu.VMEM((shards, shares, part, width), F32))
    else:
        outs.append(made((d, d), BF16))
    got = call(
        body,
        (1,),
        [
            SCALARS,
            whole(grad.shape),
            whole(y1.shape),
            whole(o1.shape),
            pl.BlockSpec((1, shares, d, width), lambda i: (3, 0, 0, 0)),
            whole(mix.shape),
        ],
        outs,
        scratch,
        (me, grad, y1, o1, w, mix),
        flops=8 * t * d * d,
    )
    do1, (keep, send) = got[: rows.ways], got[rows.ways : rows.ways + 2]
    if not fits:
        gm = mix_slab(got[-1], shards, shares).reshape((1, shares, halves.pairs, 2) + keep.shape[3:])
        keep = jnp.concatenate((keep, lax.dynamic_index_in_dim(gm, me[0], 3, keepdims=False)), axis=0)
        send = jnp.concatenate((send, lax.dynamic_index_in_dim(gm, 1 - me[0], 3, keepdims=False)), axis=0)
    return do1, (keep, send)


def time_backward(rows, do1, a, qkv, logs, w, me, halves):
    t, d = a.shape
    width = w.shape[3]
    shares = w.shape[1]
    pairs = width // LANES
    scale = 1.0 / math.sqrt(HEAD_DIM)
    rate = LOG2E * scale

    def body(me_ref, *refs):
        do_refs, refs = refs[: rows.ways], refs[rows.ways :]
        a_ref, qkv_ref, log_ref, w_ref = refs[:4]
        out_refs, refs = refs[4 : 4 + rows.ways], refs[4 + rows.ways :]
        half_refs, refs = refs[:6], refs[6:]
        bias_ref, dqkv_ref, at_ref, u_ref, room_ref, do_ref = refs
        h = pl.program_id(0)

        @pl.when(h == 0)
        def _():
            bias_ref[...] = rows.time_bias()
            at_ref[...] = a_ref[...].T
            u_ref[...] = jnp.zeros((t, d), F32)

        for k in range(rows.ways):
            do_ref[k * rows.chunk : (k + 1) * rows.chunk] = do_refs[k][...]

        @pl.loop(0, pairs)
        def _(i):
            lanes = pl.ds(pl.multiple_of(i * LANES, LANES), LANES)
            log = log_ref[0, i]
            grads = pair_backward(
                qkv_ref[0, :, lanes],
                qkv_ref[1, :, lanes],
                qkv_ref[2, :, lanes],
                do_ref[:, lanes],
                (log[0:1], log[1:2]),
                bias_ref[...],
                rate,
                scale,
            )
            for part in range(3):
                dqkv_ref[part, :, lanes] = grads[part]

        for part in range(3):
            value = nn(at_ref[...], dqkv_ref[part])
            split_rows(value, half_refs[2 * part], half_refs[2 * part + 1], (0, 0), room_ref, me_ref)
            u_ref[...] += nt(dqkv_ref[part], w_ref[part, 0])

        @pl.when(h == shares - 1)
        def _():
            for k in range(rows.ways):
                out_refs[k][...] = u_ref[k * rows.chunk : (k + 1) * rows.chunk].astype(BF16)

    got = call(
        body,
        (shares,),
        [
            SCALARS,
            *(pl.BlockSpec((rows.chunk, width), lambda h: (0, h)) for _ in do1),
            whole(a.shape),
            pl.BlockSpec((3, t, width), lambda h: (0, 0, h)),
            pl.BlockSpec((1,) + logs.shape[1:], lambda h: (h, 0, 0, 0)),
            slabs(3, 0, width, d),
        ],
        [
            *rows.chunks(d),
            *(one for _ in range(3) for one in halves.array((1, shares), (1, 1), lambda h: (0, h))),
        ],
        [
            pltpu.VMEM((t, t), F32),
            pltpu.VMEM((3, t, width), BF16),
            pltpu.VMEM((d, t), BF16),
            pltpu.VMEM((t, d), F32),
            halves.room(),
            pltpu.VMEM((t, width), BF16),
        ],
        (me, *do1, a, qkv, logs, w),
        flops=2 * t * d * d * 6,
    )
    parts = got[rows.ways :]
    return got[: rows.ways], [tuple(parts[i : i + 2]) for i in (0, 2, 4)]


def first_norm_back(rows, back, x, grad, gb, me):
    t, d = x.shape

    def body(me_ref, *refs):
        x_ref, g_ref, gb_ref, go_ref, sums_ref = refs[rows.ways :]
        u = rows.gathered(refs[: rows.ways], me_ref[3])
        change, sums = norm_back(u, x_ref[...], gb_ref[0:1])
        go_ref[...] = g_ref[...] + change
        sums_ref[...] = sums

    return call(
        body,
        (1,),
        [SCALARS, *(whole(c.shape) for c in back), whole(x.shape), whole(grad.shape), whole(gb.shape)],
        [made((t, d), F32), made((2, d), F32)],
        [],
        (me, *back, x, grad, gb),
    )


def homes():
    clips, ways = lax.axis_size("clip"), lax.axis_size("seq")
    pairs = []
    for clip in range(clips):
        for seq in range(ways):
            home_clip = clip - clip % 2 + seq % 2
            home_seq = seq // 2 + (ways // 2) * (clip % 2)
            pairs.append((clip * ways + seq, home_clip * ways + home_seq))
    return pairs


def go_home(a):
    return lax.ppermute(a, ("clip", "seq"), homes())


def go_back(a):
    return lax.ppermute(a, ("clip", "seq"), [(home, device) for device, home in homes()])


def member_of(clip, seq):
    return clip % 2 + 2 * (seq % (lax.axis_size("seq") // 2))


def swap_places(chunks):
    clips, ways = lax.axis_size("clip"), lax.axis_size("seq")
    got = [chunks[0]]
    for k in range(1, ways):
        pairs = []
        for clip in range(clips):
            for seq in range(ways):
                other = member_of(clip, seq) ^ k
                to_clip = clip - clip % 2 + other % 2
                to_seq = seq - seq % (ways // 2) + other // 2
                pairs.append((clip * ways + seq, to_clip * ways + to_seq))
        got.append(lax.ppermute(chunks[k], ("clip", "seq"), pairs))
    return got


def columns(a, r, width):
    return a.reshape(r, -1, width).transpose(1, 0, 2)


def pack_time(time_qkv, time_out, time_mix):
    r, _, width = time_qkv.shape
    mix = time_mix.reshape(-1, time_mix.shape[1] // width, width).transpose(1, 0, 2).reshape(1, r, width)
    return jnp.concatenate((columns(time_qkv, r, width), time_out.T[None], mix), axis=0)


def pack_rest(space_qkv, space_out, mlp_in, mlp_out):
    r, _, width = space_qkv.shape
    return jnp.concatenate(
        (
            columns(space_qkv, r, width),
            space_out.T[None],
            columns(mlp_in, r, width),
            columns(mlp_out.T, r, width),
        ),
        axis=0,
    )


def gather_slabs(pack):
    full = lax.all_gather(pack, ("head", "clip", "seq"), axis=1, tiled=True)
    return full.reshape(pack.shape[0], lax.axis_size("head"), -1, pack.shape[2])


def spread_steps(pack, me):
    ways, clips = lax.axis_size("seq"), lax.axis_size("clip")
    shares = lax.axis_size("head")
    n, r, width = pack.shape
    pack = yield pack
    turned = [pack] + [
        lax.ppermute(pack, "seq", [(i, (i + k) % ways) for i in range(ways)]) for k in range(1, ways)
    ]
    turned = yield turned
    orders = (((0, 1), "x", "h"), ((3, 2), "h", "x"))
    some = [jnp.stack([turned[k] for k in steps]) for steps, _, _ in orders]
    come = yield [cross(a, first) for a, (_, first, _) in zip(some, orders)]
    some = [jnp.concatenate(pair, axis=0) for pair in zip(some, come)]
    come = yield [cross(a, second) for a, (_, _, second) in zip(some, orders)] + [
        cross(a, "c") for a in some
    ]
    far = yield come + [cross(a, "c") for a in come[:2]]
    come, far = far[:2], far[2:]
    runs = []
    for i, (steps, first, second) in enumerate(orders):
        where = [(k, {first: f}) for f in (0, 1) for k in steps]
        near = [(k, {**at, second: 0}) for k, at in where]
        past = [(k, {**at, second: 1}) for k, at in where]
        runs += [(some[i], near, 0), (come[i], past, 0), (far[i], near, 1), (far[2 + i], past, 1)]
    count = sum(len(where) for _, where, _ in runs)

    def body(me_ref, *refs):
        sources, out_ref, sems = refs[: len(runs)], refs[-2], refs[-1]
        copies = []
        for source, (_, where, core) in zip(sources, runs):
            for i, (k, at) in enumerate(where):
                share = jnp.bitwise_xor(me_ref[2], at["h"])
                clip = 2 * jnp.bitwise_xor(me_ref[1], at["x"]) + jnp.bitwise_xor(me_ref[0], core)
                seq = lax.rem(me_ref[4] + (ways - k), ways)
                copies.append(
                    pltpu.make_async_copy(
                        source.at[i], out_ref.at[:, share, clip * ways + seq], sems.at[len(copies)]
                    )
                )
        for copy in copies:
            copy.start()
        for copy in copies:
            copy.wait()

    full = pl.pallas_call(
        body,
        out_shape=jax.ShapeDtypeStruct((n, shares, clips * ways, r, width), BF16),
        in_specs=[SCALARS] + [pl.BlockSpec(memory_space=pltpu.HBM)] * len(runs),
        out_specs=pl.BlockSpec(memory_space=pltpu.VMEM),
        scratch_shapes=[pltpu.SemaphoreType.DMA((count,))],
        compiler_params=pltpu.CompilerParams(vmem_limit_bytes=VMEM),
        cost_estimate=pl.CostEstimate(
            flops=0, bytes_accessed=4 * n * shares * clips * ways * r * width, transcendentals=0
        ),
    )(me, *(blocks for blocks, _, _ in runs))
    yield full.reshape(n, shares, clips * ways * r, width)


class Spread:
    def __init__(self, pack, me):
        self.way = spread_steps(pack, me)
        self.come = next(self.way)

    def hold(self, x):
        x, self.come = lax.optimization_barrier((x, self.come))
        return x

    def step(self, x):
        x = self.hold(x)
        self.come = self.way.send(self.come)
        return x


def mix_whole(slab, shards):
    shares, depth, width = slab.shape
    part = slab.reshape(shares, shards, shares, depth // (shards * shares), width)
    return part.transpose(1, 0, 3, 2, 4).reshape(depth, shares * width)


def mix_slab(whole_grad, shards, shares):
    depth, full = whole_grad.shape
    width = full // shares
    part = whole_grad.reshape(shards, shares, depth // (shards * shares), shares, width)
    return part.transpose(1, 0, 3, 2, 4).reshape(1, shares, depth, width)


class Piece:
    def __init__(self, keep, got, first, n, order):
        self.near = (keep, got)
        self.first = first
        self.n = n
        self.order = order
        self.step = 0
        self.held = []
        self.result = None


PLACE = {"x": 1, "h": 2}


def fold(pieces, me, last_by_rows):
    ways = lax.axis_size("seq")
    depth, width = pieces[0].near[0].shape[-2:]
    r = depth // ways
    used = {}
    arrays = []

    def number(a):
        for i, known in enumerate(arrays):
            if known is a:
                return i
        arrays.append(a)
        return len(arrays) - 1

    plans = []
    for p in pieces:
        link = p.order[p.step] if p.step < 2 else "z"
        blocks = p.n * (2 if p.step == 0 else 1)
        base = used.get(link, 0)
        used[link] = base + blocks
        near = [number(a) for a in p.near]
        held = [(number(a), at) for a, at in p.held]
        plans.append((p, link, base, near, held))
    links = sorted(used)
    shapes = [
        (ways, used[k], r, width) if k == "z" and last_by_rows else (used[k], depth, width)
        for k in links
    ]
    rooms, counts = [], []
    for p, link, base, near, held in plans:
        each = 2 if p.step == 0 else 1
        counts.append((each, len(near) + len(held)))
        rooms += [(each * p.n, depth, width)] * (len(near) + len(held))
    copies_needed = sum(each * terms for each, terms in counts)

    def body(me_ref, *refs):
        sources = refs[: len(arrays)]
        outs = dict(zip(links, refs[len(arrays) : len(arrays) + len(links)]))
        held_refs = refs[len(arrays) + len(links) : -1]
        sems = refs[-1]
        mine = {name: me_ref[PLACE[name]] for name in PLACE}
        groups = []
        room = 0
        sem = 0
        for p, link, base, near, held in plans:
            group = []
            if p.step == 0:
                for term in near:
                    for k in range(2):
                        pick = {p.order[0]: 1 - mine[p.order[0]], p.order[1]: k}
                        source = sources[term].at[pl.ds(p.first, p.n), pick["h"], pick["x"]]
                        group.append((source, held_refs[room].at[pl.ds(k * p.n, p.n)]))
                    room += 1
            else:
                last = p.order[1]
                pick = {p.order[0]: mine[p.order[0]]}
                pick[last] = 1 - mine[last] if p.step == 1 else mine[last]
                for term in near:
                    source = sources[term].at[pl.ds(p.first, p.n), pick["h"], pick["x"]]
                    group.append((source, held_refs[room]))
                    room += 1
                for i, (term, at) in enumerate(held):
                    start = at + pick[last] * p.n if i == 0 else at
                    group.append((sources[term].at[pl.ds(start, p.n)], held_refs[room]))
                    room += 1
            made_copies = []
            for source, target in group:
                made_copies.append(pltpu.make_async_copy(source, target, sems.at[sem]))
                sem += 1
            groups.append(made_copies)
        for group in groups:
            for copy in group:
                copy.start()
        room = 0
        for (p, link, base, near, held), (each, terms), group in zip(plans, counts, groups):
            these = held_refs[room : room + terms]
            room += terms
            for copy in group:
                copy.wait()

            @pl.loop(0, each * p.n)
            def _(i, these=these, base=base, out=outs[link], last=p.step == 2 and last_by_rows):
                value = these[0][i].astype(F32)
                for one in these[1:]:
                    value = value + one[i].astype(F32)
                value = value.astype(BF16)
                if last:
                    for k in range(ways):
                        out[k, base + i] = value[k * r : (k + 1) * r]
                else:
                    out[base + i] = value

    moved = sum(2 * math.prod(room) for room in rooms) + sum(2 * math.prod(shape) for shape in shapes)
    sums = pl.pallas_call(
        body,
        out_shape=[jax.ShapeDtypeStruct(shape, BF16) for shape in shapes],
        in_specs=[SCALARS] + [pl.BlockSpec(memory_space=pltpu.HBM)] * len(arrays),
        out_specs=[pl.BlockSpec(memory_space=pltpu.VMEM)] * len(links),
        scratch_shapes=[pltpu.VMEM(room, BF16) for room in rooms]
        + [pltpu.SemaphoreType.DMA((copies_needed,))],
        compiler_params=pltpu.CompilerParams(vmem_limit_bytes=VMEM),
        cost_estimate=pl.CostEstimate(flops=0, bytes_accessed=moved, transcendentals=0),
    )(me, *arrays)
    return [(p, link, base) for p, link, base, _, _ in plans], dict(zip(links, sums))


def cross(a, name):
    axis, bit = ("head", 0) if name == "h" else ("clip", 1 if name == "x" else 0)
    size = lax.axis_size(axis)
    return lax.ppermute(a, axis, [(i, i ^ (1 << bit)) for i in range(size)])


def pieces_of(halves_of):
    total = sum(keep.shape[0] for keep, _ in halves_of)
    found = []
    seen = 0
    for keep, send in halves_of:
        got = cross(send, "c")
        n = keep.shape[0]
        first = min(max((total + 1) // 2 - seen, 0), n)
        if first:
            found.append(Piece(keep, got, 0, first, ("x", "h")))
        if n > first:
            found.append(Piece(keep, got, first, n - first, ("h", "x")))
        seen += n
    return found


def move(x, pieces, me, at_end=False):
    plans, sums = fold(pieces, me, at_end)
    x, sums = lax.optimization_barrier((x, sums))
    got = {}
    for link, array in sums.items():
        if link == "z":
            if at_end:
                every = lax.all_to_all(array, "seq", split_axis=0, concat_axis=0, tiled=True)
                got[link] = jnp.sum(every.astype(F32), axis=0)
            else:
                own = lax.psum_scatter(array, "seq", scatter_dimension=1, tiled=True)
                got[link] = own.astype(F32)
        else:
            got[link] = cross(array, link)
    for p, link, base in plans:
        if link == "z":
            p.result = got[link][base : base + p.n]
        else:
            p.held.append((got[link], base))
        p.step += 1
    return x


def settle(x, pieces):
    arrays = []
    for p in pieces:
        if not any(p.held[-1][0] is a for a in arrays):
            arrays.append(p.held[-1][0])
    x, came = lax.optimization_barrier((x, arrays))
    for p in pieces:
        for old, new in zip(arrays, came):
            if p.held[-1][0] is old:
                p.held[-1] = (new, p.held[-1][1])
                break
    return x


def reduce_plain(halves_of, core):
    def joined(keep, send):
        low = jnp.where(core == 0, keep, send)
        high = jnp.where(core == 0, send, keep)
        n, shares, pairs, depth, width = keep.shape
        return jnp.stack((low, high), axis=3).reshape(n, shares, 2 * pairs * depth, width)

    g = jnp.concatenate([joined(*pair) for pair in halves_of], axis=0)
    g = lax.psum_scatter(g, "head", scatter_dimension=1, tiled=True)
    g = lax.psum_scatter(g.astype(F32), ("clip", "seq"), scatter_dimension=2, tiled=True)
    return g[:, 0]


def gather_norms(gain, bias):
    layers, norms, part = gain.shape
    both = jnp.concatenate((gain, bias), axis=1).reshape(1, -1)
    count = lax.axis_size("clip") * lax.axis_size("seq") * lax.axis_size("head")
    width = round_up(both.shape[1], 128)
    padded = jnp.pad(both, ((0, 0), (0, width - both.shape[1])))
    every = lax.all_to_all(
        jnp.broadcast_to(padded, (count, width)), ALL, split_axis=0, concat_axis=0, tiled=True
    )[:, : both.shape[1]]
    return every.reshape(count, layers * 2 * norms, part).transpose(1, 0, 2).reshape(layers, 2 * norms, -1)


def reduce_norms(sums):
    count = lax.axis_size("clip") * lax.axis_size("seq") * lax.axis_size("head")
    rows, features = sums.shape
    part = features // count
    a = sums.reshape(rows, count, part).transpose(1, 0, 2).reshape(count, rows * part)
    width = round_up(rows * part, 128)
    a = jnp.pad(a, ((0, 0), (0, width - rows * part)))
    every = lax.all_to_all(a, ALL, split_axis=0, concat_axis=0, tiled=True)
    return jnp.sum(every, axis=0)[: rows * part].reshape(rows, part)


def on_device(
    tokens,
    cotangent,
    time_qkv,
    time_out,
    time_mix,
    space_qkv,
    space_out,
    mlp_in,
    mlp_out,
    norm_gain,
    norm_bias,
):
    layers = time_qkv.shape[0]
    clips, frames, places, d = tokens.shape
    ways = lax.axis_size("seq")
    shards = lax.axis_size("clip") * ways
    rows = Rows(clips * frames, places, ways)
    shares = lax.axis_size("head")

    def as_rows(a):
        a = a.astype(F32).reshape(rows.frames, places, d)
        a = jnp.pad(a, ((0, 0), (0, rows.frame_rows - places), (0, 0)))
        return a.reshape(rows.rows, d)

    def from_rows(a):
        a = a.reshape(rows.frames, rows.frame_rows, d)[:, :places]
        return a.reshape(tokens.shape)

    gbs = gather_norms(norm_gain, norm_bias)
    gb = [gbs[l] for l in range(layers)]
    packs = [
        pack_time(time_qkv[l], time_out[l], time_mix[l])
        for l in range(layers)
    ]
    packs_ff = [pack_rest(space_qkv[l], space_out[l], mlp_in[l], mlp_out[l]) for l in range(layers)]
    weights = [gather_slabs(pack) for pack in packs]
    mixes = [mix_whole(w[-1], shards) for w in weights]
    quick = lax.axis_size("clip") == 4 and shares == 2 and ways == 4 and time_qkv.shape[1] % 16 == 0

    halves = Halves(lax.axis_size("clip"), d, time_qkv.shape[3])
    clip = lax.axis_index("clip")
    member = member_of(clip, lax.axis_index("seq"))
    me = jnp.stack((clip & 1, (clip >> 1) & 1, lax.axis_index("head"), member, lax.axis_index("seq"))).astype(
        jnp.int32
    )
    if quick:
        spreads = [Spread(pack, me) for pack in packs_ff]
        weights_ff = []
    else:
        weights_ff = [gather_slabs(pack) for pack in packs_ff]

    home = go_home(tokens)
    if quick:
        first = spreads[0]
        home, gb = first.step((home, gb))
    x = as_rows(home)
    send = send_first(rows, x, gb[0], me)
    kept = []
    for l in range(layers):
        w = weights[l]
        send = swap_places(send)
        if quick and l == 0:
            send = first.step(send)
            for spread in spreads[1:]:
                send = spread.step(send)
            send = first.step(send)
            for spread in spreads[1:]:
                send = spread.hold(send)
        a1, qkv1, log1, o1_time = time_forward(rows, send, w)
        back = swap_places(o1_time)
        if quick:
            for _ in range(2):
                back = spreads[l].step(back)
            if l == 0:
                for spread in spreads[1:]:
                    back = spread.step(back)
            weights_ff.append(spreads[l].come)
        o1, y1, x1, qkv2 = middle_forward(rows, back, x, w, weights_ff[l], mixes[l], gb[l], me)
        o2, x2, log2 = space_forward(rows, qkv2, x1, weights_ff[l])
        if quick and l == 0:
            for spread in spreads[1:]:
                x2 = spread.step(x2)
        kept.append((x, a1, qkv1, log1, o1, y1, x1, qkv2, o2, log2, x2))
        if l + 1 < layers:
            x, *send = mlp_forward(rows, x2, weights_ff[l], gb[l], gb[l + 1], me)

    grad = as_rows(go_home(cotangent))
    norm_rows = [None] * layers
    summed = [None] * layers
    late = []
    for l in reversed(range(layers)):
        w = weights[l]
        x, a1, qkv1, log1, o1, y1, x1, qkv2, o2, log2, x2 = kept[l]
        grad, g_ff, s3, x3 = mlp_backward(
            rows, grad, x2, weights_ff[l], gb[l], me, halves, l + 1 == layers
        )
        if x3:
            output = go_back(from_rows(x3[0].astype(BF16)))
        if quick:
            ff = pieces_of(g_ff)
            if late:
                grad = settle(grad, late)
                grad = move(grad, late, me)
                late = [p for p in late if p.step < 3]
        grad, g_space, s2 = space_backward(
            rows, grad, x1, qkv2, o2, log2, weights_ff[l], gb[l], me, halves
        )
        if quick:
            space = pieces_of([g_space])
            if late:
                grad = settle(grad, late)
            grad, output = move((grad, output), ff, me)
        do1, g_out = middle_backward(rows, grad, y1, o1, w, mixes[l], me, halves, shards)
        do1 = swap_places(do1)
        if quick:
            do1 = move(do1, ff + space + late, me)
        da1, g_time = time_backward(rows, do1, a1, qkv1, log1, w, me, halves)
        if quick:
            da1 = settle(da1, ff + space)
        da1 = swap_places(da1)
        if quick:
            rest = pieces_of([g_out] + g_time)
            da1 = move(da1, ff + space + rest, me)
            late = space + rest
        grad, s1 = first_norm_back(rows, da1, x, grad, gb[l], me)
        norm_rows[l] = jnp.concatenate((s1[0:1], s2[0:1], s3[0:1], s1[1:2], s2[1:2], s3[1:2]), axis=0)
        if quick:
            summed[l] = ff + space + rest
        else:
            summed[l] = [reduce_plain(g_ff + [g_space, g_out] + g_time, clip & 1)]
    if quick:
        tokens_grad = move(go_back(from_rows(grad.astype(BF16))), late, me)
        move((), rest, me, True)
        summed = [[p.result for p in some] for some in summed]
    cuts = (2 * g_ff[0][0].shape[0], g_space[0].shape[0], g_out[0].shape[0], len(g_time))
    results = []
    for some in summed:
        slabs_of = jnp.concatenate(some, axis=0)
        ends = [sum(cuts[: i + 1]) for i in range(4)]
        results.append([slabs_of[e - c : e] for c, e in zip(cuts, ends)])
    if not quick:
        tokens_grad = go_back(from_rows(grad.astype(BF16)))
    tokens_grad = tokens_grad.astype(F32)
    norm_sums = reduce_norms(jnp.concatenate(norm_rows, axis=0)).reshape(layers, 2, 3, -1)

    def stacked(form):
        return jnp.stack([form(*results[l]) for l in range(layers)])

    def rows_of(a):
        return a.transpose(1, 0, 2)

    def flat(a):
        return rows_of(a).reshape(a.shape[1], -1)

    def mix_rows(a):
        r, width = a.shape
        return a.reshape(shares, r // shares, width).transpose(1, 0, 2).reshape(r // shares, -1)

    per_share = mlp_in.shape[2] // time_qkv.shape[3]
    return (
        output,
        tokens_grad,
        stacked(lambda ff, s, t, q: rows_of(q)),
        stacked(lambda ff, s, t, q: t[0].T),
        stacked(lambda ff, s, t, q: mix_rows(t[1])),
        stacked(lambda ff, s, t, q: rows_of(s[1:])),
        stacked(lambda ff, s, t, q: s[0].T),
        stacked(lambda ff, s, t, q: flat(ff[:per_share])),
        stacked(lambda ff, s, t, q: flat(ff[per_share:]).T),
        norm_sums[:, 0],
        norm_sums[:, 1],
    )


def solution(mesh):
    token_spec = P(("clip", "head"), "seq", None, None)
    in_specs = (
        token_spec,
        token_spec,
        P(None, ("clip", "seq"), None, "head"),
        P(None, "head", ("clip", "seq")),
        P(None, ("clip", "seq", "head"), None),
        P(None, ("clip", "seq"), None, "head"),
        P(None, "head", ("clip", "seq")),
        P(None, ("clip", "seq"), "head"),
        P(None, "head", ("clip", "seq")),
        P(None, None, ("clip", "seq", "head")),
        P(None, None, ("clip", "seq", "head")),
    )
    return jax.shard_map(
        on_device, mesh=mesh, in_specs=in_specs, out_specs=in_specs, check_vma=False
    )
```

```python
import functools
import math

import jax
import jax.numpy as jnp
from jax import lax
from jax.experimental import pallas as pl
from jax.experimental.pallas import tpu as pltpu
from jax.sharding import PartitionSpec as P

HEAD_DIM = 64
NORM_EPS = 1e-06
HALF_ROOT = 0.7071067811865476
INV_ROOT_TAU = 0.3989422804014327
LOG2E = 1.4426950408889634
FAR = -1e30
LANES = 128
VMEM = 56 * 1024 * 1024
SHOWN = 1.0
ALL = ("clip", "seq", "head")
BF16 = jnp.bfloat16
F32 = jnp.float32


def round_up(value, step):
    return -(-value // step) * step


def nn(a, b):
    return lax.dot_general(a, b, (((1,), (0,)), ((), ())), preferred_element_type=F32)


def nt(a, b):
    return lax.dot_general(a, b, (((1,), (1,)), ((), ())), preferred_element_type=F32)


def tn(a, b):
    return lax.dot_general(a, b, (((0,), (0,)), ((), ())), preferred_element_type=F32)


def norm_parts(x):
    mean = jnp.mean(x, axis=-1, keepdims=True)
    centred = x - mean
    spread = lax.rsqrt(jnp.mean(centred * centred, axis=-1, keepdims=True) + NORM_EPS)
    return centred * spread, spread


def norm_rounded(x, gain, bias):
    hat, _ = norm_parts(x)
    return (hat * gain + bias).astype(BF16)


def norm_back(u, x, gain):
    hat, spread = norm_parts(x)
    scaled = u * gain
    mean_scaled = jnp.mean(scaled, axis=-1, keepdims=True)
    mean_cross = jnp.mean(scaled * hat, axis=-1, keepdims=True)
    change = spread * (scaled - mean_scaled - hat * mean_cross)
    sums = jnp.concatenate(
        (jnp.sum(u * hat, axis=0, keepdims=True), jnp.sum(u, axis=0, keepdims=True)), axis=0
    )
    return change, sums


class Rows:
    def __init__(self, frames, places, ways):
        self.frames = frames
        self.places = places
        self.ways = ways
        self.frame_rows = round_up(places, 16)
        self.rows = frames * self.frame_rows
        self.block = places // ways
        self.chunk = round_up(frames * self.block, 8)
        self.time_rows = ways * self.chunk

    def split(self, r):
        way = jnp.zeros_like(r)
        for k in range(1, self.ways):
            way = way + (r >= k * self.chunk).astype(jnp.int32)
        rest = r - way * self.chunk
        frame = jnp.zeros_like(r)
        for k in range(1, self.frames):
            frame = frame + (rest >= k * self.block).astype(jnp.int32)
        real = rest < self.frames * self.block
        return way, frame, rest - frame * self.block, real

    def to_time(self, k, member):
        r = lax.broadcasted_iota(jnp.int32, (self.chunk, 1), 0)
        _, frame, place, real = self.split(r)
        way = jnp.bitwise_xor(member, k)
        source = jnp.where(real, frame * self.frame_rows + way * self.block + place, -1)
        c = lax.broadcasted_iota(jnp.int32, (self.chunk, self.rows), 1)
        return jnp.where(c == source, 1.0, 0.0).astype(BF16)

    def gathered(self, chunk_refs, member):
        total = tn(self.to_time(0, member), chunk_refs[0][...])
        for k in range(1, self.ways):
            total = total + tn(self.to_time(k, member), chunk_refs[k][...])
        return total

    def chunks(self, width, block=None, index=None):
        return [
            made((self.chunk, width), BF16)
            if block is None
            else made((self.chunk, width), BF16, (self.chunk, block), index)
            for _ in range(self.ways)
        ]

    def time_bias(self):
        def label(r):
            _, _, place, real = self.split(r)
            return jnp.where(real, place, -1)

        a = label(lax.broadcasted_iota(jnp.int32, (self.time_rows, 1), 0))
        b = label(lax.broadcasted_iota(jnp.int32, (1, self.time_rows), 1))
        return jnp.where(a == b, 0.0, FAR).astype(F32)

    def space_bias(self):
        a = lax.broadcasted_iota(jnp.int32, (self.frame_rows, 1), 0)
        return jnp.where(a < self.places, 0.0, FAR).astype(F32)


def lane_masks(rows):
    lane = lax.broadcasted_iota(jnp.int32, (rows, LANES), 1)
    return lane < HEAD_DIM


def one_of(value, low, half):
    zero = jnp.zeros_like(value)
    return jnp.where(low, value, zero) if half == 0 else jnp.where(low, zero, value)


def pair_forward(q, k, v, bias, rate):
    low = lane_masks(q.shape[0])
    mixed, logs = [], []
    for half in range(2):
        s = nt(k, one_of(q, low, half)) + bias
        peak = jnp.max(s, axis=0, keepdims=True)
        e = jnp.exp2((s - peak) * rate)
        total = jnp.sum(e, axis=0, keepdims=True)
        soft = (e * (1.0 / total)).astype(BF16)
        mixed.append(tn(soft, v))
        logs.append(peak * rate + jnp.log2(total))
    return jnp.where(low, mixed[0], mixed[1]).astype(BF16), logs


def pair_backward(q, k, v, do, logs, bias, rate, scale):
    low = lane_masks(q.shape[0])
    dq, dk, dv = [], [], []
    for half in range(2):
        s = nt(k, one_of(q, low, half)) + bias
        soft = jnp.exp2(s * rate - logs[half])
        dp = nt(v, one_of(do, low, half))
        ds = (soft * (dp - jnp.sum(soft * dp, axis=0, keepdims=True))).astype(BF16)
        dv.append(nn(soft.astype(BF16), do))
        dk.append(nn(ds, q))
        dq.append(tn(ds, k))
    return (
        (jnp.where(low, dq[0], dq[1]) * scale).astype(BF16),
        (jnp.where(low, dk[0], dk[1]) * scale).astype(BF16),
        jnp.where(low, dv[0], dv[1]).astype(BF16),
    )


def split_rows(value, keep_ref, send_ref, at, room_ref, me_ref):
    mine = me_ref[0]
    room_ref[...] = value.reshape(room_ref.shape)
    keep_ref[at] = room_ref[:, mine].astype(BF16)
    send_ref[at] = room_ref[:, 1 - mine].astype(BF16)


class Halves:
    def __init__(self, clips, depth, width):
        self.pairs = clips // 2
        self.rows = depth // clips
        self.width = width

    def array(self, lead, block, index):
        tail = (self.pairs, self.rows, self.width)
        one = lambda: made(lead + tail, BF16, block + tail, lambda *g: index(*g) + (0, 0, 0))
        return [one(), one()]

    def room(self):
        return pltpu.VMEM((self.pairs, 2, self.rows, self.width), F32)


SCALARS = pl.BlockSpec(memory_space=pltpu.SMEM)


def call(body, grid, ins, outs, scratch, args, flops=0):
    specs = [spec for spec in ins]
    moved = sum(math.prod(o.shape) * o.dtype.itemsize for o, _ in outs)
    moved += sum(math.prod(a.shape) * a.dtype.itemsize for a in args)
    return pl.pallas_call(
        body,
        out_shape=[shape for shape, _ in outs],
        grid=grid,
        in_specs=specs,
        out_specs=[spec for _, spec in outs],
        scratch_shapes=scratch,
        compiler_params=pltpu.CompilerParams(vmem_limit_bytes=VMEM),
        cost_estimate=pl.CostEstimate(
            flops=int(flops * SHOWN), bytes_accessed=int(moved * SHOWN), transcendentals=0
        ),
    )(*args)


def whole(shape):
    zeros = (0,) * len(shape)
    return pl.BlockSpec(shape, lambda *_: zeros)


def made(shape, dtype, block=None, index=None):
    spec = whole(shape) if block is None else pl.BlockSpec(block, index)
    return jax.ShapeDtypeStruct(shape, dtype), spec


def slabs(count, first, width, depth):
    return pl.BlockSpec((count, 1, depth, width), lambda h, *_: (first // count, h, 0, 0))


def send_first(rows, x, gb, me):
    def body(me_ref, x_ref, gb_ref, *out_refs):
        a = norm_rounded(x_ref[...], gb_ref[0:1], gb_ref[3:4])
        for k in range(rows.ways):
            out_refs[k][...] = nn(rows.to_time(k, me_ref[3]), a).astype(BF16)

    d = x.shape[1]
    return call(
        body, (1,), [SCALARS, whole(x.shape), whole(gb.shape)], rows.chunks(d), [], (me, x, gb)
    )


def time_forward(rows, chunks, w):
    t, d = rows.time_rows, chunks[0].shape[1]
    width = w.shape[3]
    shares = w.shape[1]
    pairs = width // LANES
    ways = rows.ways
    rate = LOG2E / math.sqrt(HEAD_DIM)

    def body(*refs):
        chunk_refs = refs[:ways]
        w_ref, a_ref, qkv_ref, log_ref = refs[ways : ways + 4]
        out_refs = refs[ways + 4 : 2 * ways + 4]
        bias_ref, mixed_ref = refs[2 * ways + 4 :]

        @pl.when(pl.program_id(0) == 0)
        def _():
            bias_ref[...] = rows.time_bias()
            for k in range(ways):
                a_ref[k * rows.chunk : (k + 1) * rows.chunk] = chunk_refs[k][...]

        act = a_ref[...]
        for g in range(3):
            qkv_ref[g] = nn(act, w_ref[g, 0]).astype(BF16)

        @pl.loop(0, pairs)
        def _(i):
            lanes = pl.ds(pl.multiple_of(i * LANES, LANES), LANES)
            mixed, logs = pair_forward(
                qkv_ref[0, :, lanes], qkv_ref[1, :, lanes], qkv_ref[2, :, lanes], bias_ref[...], rate
            )
            mixed_ref[:, lanes] = mixed
            log_ref[0, i] = jnp.concatenate(logs, axis=0)

        for k in range(ways):
            out_refs[k][...] = mixed_ref[k * rows.chunk : (k + 1) * rows.chunk]

    got = call(
        body,
        (shares,),
        [whole(c.shape) for c in chunks] + [slabs(3, 0, width, d)],
        [
            made((t, d), BF16),
            made((3, t, d), BF16, (3, t, width), lambda h: (0, 0, h)),
            made((shares, pairs, 2, t), F32, (1, pairs, 2, t), lambda h: (h, 0, 0, 0)),
            *rows.chunks(d, width, lambda h: (0, h)),
        ],
        [pltpu.VMEM((t, t), F32), pltpu.VMEM((t, width), BF16)],
        (*chunks, w),
        flops=2 * t * d * 3 * d,
    )
    return got[0], got[1], got[2], got[3:]


def middle_forward(rows, back, x, w, ws, mix, gb, me):
    t, d = x.shape
    width = w.shape[3]
    shares = w.shape[1]

    def body(me_ref, *refs):
        x_ref, to_ref, sq_ref, mix_ref, gb_ref, o1_ref, y1_ref, x1_ref, qkv_ref = refs[rows.ways :]
        o1 = rows.gathered(refs[: rows.ways], me_ref[3]).astype(BF16)
        o1_ref[...] = o1
        y1 = jnp.zeros((t, d), F32)
        for h in range(shares):
            y1 = y1 + nt(o1[:, h * width : (h + 1) * width], to_ref[0, h])
        y1 = y1.astype(BF16)
        y1_ref[...] = y1
        x1 = x_ref[...] + nn(y1, mix_ref[...])
        x1_ref[...] = x1
        a2 = norm_rounded(x1, gb_ref[1:2], gb_ref[4:5])
        for g in range(3):
            for h in range(shares):
                qkv_ref[g, :, h * width : (h + 1) * width] = nn(a2, sq_ref[g, h]).astype(BF16)

    return call(
        body,
        (1,),
        [
            SCALARS,
            *(whole(c.shape) for c in back),
            whole(x.shape),
            pl.BlockSpec((1, shares, d, width), lambda i: (3, 0, 0, 0)),
            pl.BlockSpec((3, shares, d, width), lambda i: (0, 0, 0, 0)),
            whole(mix.shape),
            whole(gb.shape),
        ],
        [made((t, d), BF16), made((t, d), BF16), made((t, d), F32), made((3, t, d), BF16)],
        [],
        (me, *back, x, w, ws, mix, gb),
        flops=2 * t * d * 5 * d,
    )


def space_forward(rows, qkv, x1, w):
    t, d = x1.shape
    width = w.shape[3]
    shares = w.shape[1]
    pairs = width // LANES
    rate = LOG2E / math.sqrt(HEAD_DIM)
    n = rows.frame_rows

    def body(qkv_ref, x1_ref, w_ref, o2_ref, x2_ref, log_ref):
        bias = rows.space_bias()

        @pl.loop(0, pairs)
        def _(i):
            lanes = pl.ds(pl.multiple_of(i * LANES, LANES), LANES)
            for f in range(rows.frames):
                at = slice(f * n, (f + 1) * n)
                mixed, logs = pair_forward(
                    qkv_ref[0, at, lanes], qkv_ref[1, at, lanes], qkv_ref[2, at, lanes], bias, rate
                )
                o2_ref[at, lanes] = mixed
                log_ref[0, i, f] = jnp.concatenate(logs, axis=0)

        @pl.when(pl.program_id(0) == 0)
        def _():
            x2_ref[...] = x1_ref[...]

        x2_ref[...] += nt(o2_ref[...], w_ref[0, 0])

    return call(
        body,
        (shares,),
        [
            pl.BlockSpec((3, t, width), lambda h: (0, 0, h)),
            whole(x1.shape),
            slabs(1, 3, width, d),
        ],
        [
            made((t, d), BF16, (t, width), lambda h: (0, h)),
            made((t, d), F32),
            made(
                (shares, pairs, rows.frames, 2, n),
                F32,
                (1, pairs, rows.frames, 2, n),
                lambda h: (h, 0, 0, 0, 0),
            ),
        ],
        [],
        (qkv, x1, w),
        flops=2 * t * d * d,
    )


def ff_slab(first, per_share, depth, width):
    return pl.BlockSpec(
        (1, 1, depth, width), lambda j: (first + j % per_share, j // per_share, 0, 0)
    )


def mlp_forward(rows, x2, w, gb, gb_next, me):
    t, d = x2.shape
    width = w.shape[3]
    shares = w.shape[1]
    per_share = (w.shape[0] - 4) // 2
    steps = shares * per_share

    def body(x2_ref, wi_ref, wo_ref, gb_ref, me_ref, gn_ref, x3_ref, *rest):
        send_refs, a3_ref = rest[:-1], rest[-1]
        j = pl.program_id(0)

        @pl.when(j == 0)
        def _():
            a3_ref[...] = norm_rounded(x2_ref[...], gb_ref[2:3], gb_ref[5:6])
            x3_ref[...] = x2_ref[...]

        hid = nn(a3_ref[...], wi_ref[0, 0])
        act = (0.5 * hid * (1.0 + lax.erf(hid * HALF_ROOT))).astype(BF16)
        x3_ref[...] += nt(act, wo_ref[0, 0])

        @pl.when(j == steps - 1)
        def _():
            a = norm_rounded(x3_ref[...], gn_ref[0:1], gn_ref[3:4])
            for k in range(rows.ways):
                send_refs[k][...] = nn(rows.to_time(k, me_ref[3]), a).astype(BF16)

    ins = [
        whole(x2.shape),
        ff_slab(4, per_share, d, width),
        ff_slab(4 + per_share, per_share, d, width),
        whole(gb.shape),
    ]
    ins += [SCALARS, whole(gb_next.shape)]
    outs = [made((t, d), F32)] + rows.chunks(d)
    args = (x2, w, w, gb, me, gb_next)
    return call(
        body, (steps,), ins, outs, [pltpu.VMEM((t, d), BF16)], args, flops=4 * t * d * width * steps
    )


def mlp_backward(rows, grad, x2, w, gb, me, halves, with_output):
    t, d = x2.shape
    width = w.shape[3]
    shares = w.shape[1]
    per_share = (w.shape[0] - 4) // 2
    steps = shares * per_share

    def body(me_ref, g_ref, x2_ref, wi_ref, wo_ref, gb_ref, go_ref, ki_ref, si_ref, ko_ref, so_ref, sums_ref, *rest):
        if with_output:
            x3_ref, *rest = rest
        a3_ref, a3t_ref, e3_ref, e3t_ref, u_ref, room_ref = rest
        j = pl.program_id(0)

        @pl.when(j == 0)
        def _():
            hat, _ = norm_parts(x2_ref[...])
            a3 = hat * gb_ref[2:3] + gb_ref[5:6]
            a3_ref[...] = a3.astype(BF16)
            a3t_ref[...] = a3.T.astype(BF16)
            g = g_ref[...]
            e3_ref[...] = g.astype(BF16)
            e3t_ref[...] = g.T.astype(BF16)
            u_ref[...] = jnp.zeros((t, d), F32)
            if with_output:
                x3_ref[...] = x2_ref[...]

        hid = nn(a3_ref[...], wi_ref[0, 0])
        phi = 0.5 * (1.0 + lax.erf(hid * HALF_ROOT))
        act = (hid * phi).astype(BF16)
        slope = phi + hid * jnp.exp(-0.5 * hid * hid) * INV_ROOT_TAU
        dhid = (nn(e3_ref[...], wo_ref[0, 0]) * slope).astype(BF16)
        split_rows(nn(e3t_ref[...], act), ko_ref, so_ref, (0, 0), room_ref, me_ref)
        split_rows(nn(a3t_ref[...], dhid), ki_ref, si_ref, (0, 0), room_ref, me_ref)
        u_ref[...] += nt(dhid, wi_ref[0, 0])
        if with_output:
            x3_ref[...] += nt(act, wo_ref[0, 0])

        @pl.when(j == steps - 1)
        def _():
            change, sums = norm_back(u_ref[...], x2_ref[...], gb_ref[2:3])
            go_ref[...] = g_ref[...] + change
            sums_ref[...] = sums

    slab_outs = [
        one
        for _ in range(2)
        for one in halves.array(
            (per_share, shares), (1, 1), lambda j: (j % per_share, j // per_share)
        )
    ]
    grad, ki, si, ko, so, sums, *x3 = call(
        body,
        (steps,),
        [
            SCALARS,
            whole(grad.shape),
            whole(x2.shape),
            ff_slab(4, per_share, d, width),
            ff_slab(4 + per_share, per_share, d, width),
            whole(gb.shape),
        ],
        [made((t, d), F32), *slab_outs, made((2, d), F32)] + [made((t, d), F32)] * with_output,
        [
            pltpu.VMEM((t, d), BF16),
            pltpu.VMEM((d, t), BF16),
            pltpu.VMEM((t, d), BF16),
            pltpu.VMEM((d, t), BF16),
            pltpu.VMEM((t, d), F32),
            halves.room(),
        ],
        (me, grad, x2, w, w, gb),
        flops=10 * t * d * width * steps,
    )
    return grad, [(ki, si), (ko, so)], sums, x3


def space_backward(rows, grad, x1, qkv, o2, logs, w, gb, me, halves):
    t, d = x1.shape
    width = w.shape[3]
    shares = w.shape[1]
    pairs = width // LANES
    scale = 1.0 / math.sqrt(HEAD_DIM)
    rate = LOG2E * scale
    n = rows.frame_rows

    def body(me_ref, g_ref, x1_ref, qkv_ref, o2_ref, log_ref, wo_ref, wq_ref, gb_ref, go_ref, keep_ref, send_ref, sums_ref, e2_ref, e2t_ref, a2t_ref, do_ref, dqkv_ref, u_ref, room_ref):
        h = pl.program_id(0)

        @pl.when(h == 0)
        def _():
            g = g_ref[...]
            e2_ref[...] = g.astype(BF16)
            e2t_ref[...] = g.T.astype(BF16)
            hat, _ = norm_parts(x1_ref[...])
            a2t_ref[...] = (hat * gb_ref[1:2] + gb_ref[4:5]).T.astype(BF16)
            u_ref[...] = jnp.zeros((t, d), F32)

        bias = rows.space_bias()
        split_rows(nn(e2t_ref[...], o2_ref[...]), keep_ref, send_ref, (0, 0), room_ref, me_ref)
        do_ref[...] = nn(e2_ref[...], wo_ref[0, 0]).astype(BF16)

        @pl.loop(0, pairs)
        def _(i):
            lanes = pl.ds(pl.multiple_of(i * LANES, LANES), LANES)
            for f in range(rows.frames):
                at = slice(f * n, (f + 1) * n)
                log = log_ref[0, i, f]
                grads = pair_backward(
                    qkv_ref[0, at, lanes],
                    qkv_ref[1, at, lanes],
                    qkv_ref[2, at, lanes],
                    do_ref[at, lanes],
                    (log[0:1], log[1:2]),
                    bias,
                    rate,
                    scale,
                )
                for part in range(3):
                    dqkv_ref[part, at, lanes] = grads[part]

        for part in range(3):
            split_rows(
                nn(a2t_ref[...], dqkv_ref[part]), keep_ref, send_ref, (part + 1, 0), room_ref, me_ref
            )
            u_ref[...] += nt(dqkv_ref[part], wq_ref[part, 0])

        @pl.when(h == shares - 1)
        def _():
            change, sums = norm_back(u_ref[...], x1_ref[...], gb_ref[1:2])
            go_ref[...] = g_ref[...] + change
            sums_ref[...] = sums

    grad, keep, send, sums = call(
        body,
        (shares,),
        [
            SCALARS,
            whole(grad.shape),
            whole(x1.shape),
            pl.BlockSpec((3, t, width), lambda h: (0, 0, h)),
            pl.BlockSpec((t, width), lambda h: (0, h)),
            pl.BlockSpec((1,) + logs.shape[1:], lambda h: (h, 0, 0, 0, 0)),
            slabs(1, 3, width, d),
            slabs(3, 0, width, d),
            whole(gb.shape),
        ],
        [
            made((t, d), F32),
            *halves.array((4, shares), (4, 1), lambda h: (0, h)),
            made((2, d), F32),
        ],
        [
            pltpu.VMEM((t, d), BF16),
            pltpu.VMEM((d, t), BF16),
            pltpu.VMEM((d, t), BF16),
            pltpu.VMEM((t, width), BF16),
            pltpu.VMEM((3, t, width), BF16),
            pltpu.VMEM((t, d), F32),
            halves.room(),
        ],
        (me, grad, x1, qkv, o2, logs, w, w, gb),
        flops=2 * t * d * d * 8,
    )
    return grad, (keep, send), sums


def mix_fits(depth, shards, shares):
    return depth // (shards * shares) % 8 == 0


def middle_backward(rows, grad, y1, o1, w, mix, me, halves, shards):
    t, d = grad.shape
    width = w.shape[3]
    shares = w.shape[1]
    fits = mix_fits(d, shards, shares)
    part = d // (shards * shares)

    def body(me_ref, g_ref, y1_ref, o1_ref, to_ref, mix_ref, *rest):
        send_refs, rest = rest[: rows.ways], rest[rows.ways :]
        gk_ref, gs_ref, *rest = rest
        if fits:
            room_ref, order_ref = rest
        else:
            gm_ref, room_ref = rest
        e1 = g_ref[...].astype(BF16)
        dy1 = nt(e1, mix_ref[...]).astype(BF16)
        sends = [rows.to_time(k, me_ref[3]) for k in range(rows.ways)]
        for h in range(shares):
            lanes = slice(h * width, (h + 1) * width)
            do1 = nn(dy1, to_ref[0, h]).astype(BF16)
            for k in range(rows.ways):
                send_refs[k][:, lanes] = nn(sends[k], do1).astype(BF16)
            split_rows(tn(dy1, o1_ref[:, lanes]), gk_ref, gs_ref, (0, h), room_ref, me_ref)
        gm = tn(y1_ref[...], e1)
        if fits:
            gm = gm.reshape(shards, shares, part, d)
            for h in range(shares):
                for half in range(shares):
                    order_ref[:, half] = gm[:, h, :, half * width : (half + 1) * width]
                split_rows(order_ref[...], gk_ref, gs_ref, (1, h), room_ref, me_ref)
        else:
            gm_ref[...] = gm.astype(BF16)

    outs = rows.chunks(d)
    outs += halves.array((1 + fits, shares), (1 + fits, shares), lambda i: (0, 0))
    scratch = [halves.room()]
    if fits:
        scratch.append(pltpu.VMEM((shards, shares, part, width), F32))
    else:
        outs.append(made((d, d), BF16))
    got = call(
        body,
        (1,),
        [
            SCALARS,
            whole(grad.shape),
            whole(y1.shape),
            whole(o1.shape),
            pl.BlockSpec((1, shares, d, width), lambda i: (3, 0, 0, 0)),
            whole(mix.shape),
        ],
        outs,
        scratch,
        (me, grad, y1, o1, w, mix),
        flops=8 * t * d * d,
    )
    do1, (keep, send) = got[: rows.ways], got[rows.ways : rows.ways + 2]
    if not fits:
        gm = mix_slab(got[-1], shards, shares).reshape((1, shares, halves.pairs, 2) + keep.shape[3:])
        keep = jnp.concatenate((keep, lax.dynamic_index_in_dim(gm, me[0], 3, keepdims=False)), axis=0)
        send = jnp.concatenate((send, lax.dynamic_index_in_dim(gm, 1 - me[0], 3, keepdims=False)), axis=0)
    return do1, (keep, send)


def time_backward(rows, do1, a, qkv, logs, w, me, halves):
    t, d = a.shape
    width = w.shape[3]
    shares = w.shape[1]
    pairs = width // LANES
    scale = 1.0 / math.sqrt(HEAD_DIM)
    rate = LOG2E * scale

    def body(me_ref, *refs):
        do_refs, refs = refs[: rows.ways], refs[rows.ways :]
        a_ref, qkv_ref, log_ref, w_ref = refs[:4]
        out_refs, refs = refs[4 : 4 + rows.ways], refs[4 + rows.ways :]
        half_refs, refs = refs[:6], refs[6:]
        bias_ref, dqkv_ref, at_ref, u_ref, room_ref, do_ref = refs
        h = pl.program_id(0)

        @pl.when(h == 0)
        def _():
            bias_ref[...] = rows.time_bias()
            at_ref[...] = a_ref[...].T
            u_ref[...] = jnp.zeros((t, d), F32)

        for k in range(rows.ways):
            do_ref[k * rows.chunk : (k + 1) * rows.chunk] = do_refs[k][...]

        @pl.loop(0, pairs)
        def _(i):
            lanes = pl.ds(pl.multiple_of(i * LANES, LANES), LANES)
            log = log_ref[0, i]
            grads = pair_backward(
                qkv_ref[0, :, lanes],
                qkv_ref[1, :, lanes],
                qkv_ref[2, :, lanes],
                do_ref[:, lanes],
                (log[0:1], log[1:2]),
                bias_ref[...],
                rate,
                scale,
            )
            for part in range(3):
                dqkv_ref[part, :, lanes] = grads[part]

        for part in range(3):
            value = nn(at_ref[...], dqkv_ref[part])
            split_rows(value, half_refs[2 * part], half_refs[2 * part + 1], (0, 0), room_ref, me_ref)
            u_ref[...] += nt(dqkv_ref[part], w_ref[part, 0])

        @pl.when(h == shares - 1)
        def _():
            for k in range(rows.ways):
                out_refs[k][...] = u_ref[k * rows.chunk : (k + 1) * rows.chunk].astype(BF16)

    got = call(
        body,
        (shares,),
        [
            SCALARS,
            *(pl.BlockSpec((rows.chunk, width), lambda h: (0, h)) for _ in do1),
            whole(a.shape),
            pl.BlockSpec((3, t, width), lambda h: (0, 0, h)),
            pl.BlockSpec((1,) + logs.shape[1:], lambda h: (h, 0, 0, 0)),
            slabs(3, 0, width, d),
        ],
        [
            *rows.chunks(d),
            *(one for _ in range(3) for one in halves.array((1, shares), (1, 1), lambda h: (0, h))),
        ],
        [
            pltpu.VMEM((t, t), F32),
            pltpu.VMEM((3, t, width), BF16),
            pltpu.VMEM((d, t), BF16),
            pltpu.VMEM((t, d), F32),
            halves.room(),
            pltpu.VMEM((t, width), BF16),
        ],
        (me, *do1, a, qkv, logs, w),
        flops=2 * t * d * d * 6,
    )
    parts = got[rows.ways :]
    return got[: rows.ways], [tuple(parts[i : i + 2]) for i in (0, 2, 4)]


def first_norm_back(rows, back, x, grad, gb, me):
    t, d = x.shape

    def body(me_ref, *refs):
        x_ref, g_ref, gb_ref, go_ref, sums_ref = refs[rows.ways :]
        u = rows.gathered(refs[: rows.ways], me_ref[3])
        change, sums = norm_back(u, x_ref[...], gb_ref[0:1])
        go_ref[...] = g_ref[...] + change
        sums_ref[...] = sums

    return call(
        body,
        (1,),
        [SCALARS, *(whole(c.shape) for c in back), whole(x.shape), whole(grad.shape), whole(gb.shape)],
        [made((t, d), F32), made((2, d), F32)],
        [],
        (me, *back, x, grad, gb),
    )


def homes():
    clips, ways = lax.axis_size("clip"), lax.axis_size("seq")
    pairs = []
    for clip in range(clips):
        for seq in range(ways):
            home_clip = clip - clip % 2 + seq % 2
            home_seq = seq // 2 + (ways // 2) * (clip % 2)
            pairs.append((clip * ways + seq, home_clip * ways + home_seq))
    return pairs


def go_home(a):
    return lax.ppermute(a, ("clip", "seq"), homes())


def go_back(a):
    return lax.ppermute(a, ("clip", "seq"), [(home, device) for device, home in homes()])


def member_of(clip, seq):
    return clip % 2 + 2 * (seq % (lax.axis_size("seq") // 2))


def swap_places(chunks):
    clips, ways = lax.axis_size("clip"), lax.axis_size("seq")
    got = [chunks[0]]
    for k in range(1, ways):
        pairs = []
        for clip in range(clips):
            for seq in range(ways):
                other = member_of(clip, seq) ^ k
                to_clip = clip - clip % 2 + other % 2
                to_seq = seq - seq % (ways // 2) + other // 2
                pairs.append((clip * ways + seq, to_clip * ways + to_seq))
        got.append(lax.ppermute(chunks[k], ("clip", "seq"), pairs))
    return got


def columns(a, r, width):
    return a.reshape(r, -1, width).transpose(1, 0, 2)


def pack_time(time_qkv, time_out, time_mix):
    r, _, width = time_qkv.shape
    mix = time_mix.reshape(-1, time_mix.shape[1] // width, width).transpose(1, 0, 2).reshape(1, r, width)
    return jnp.concatenate((columns(time_qkv, r, width), time_out.T[None], mix), axis=0)


def pack_rest(space_qkv, space_out, mlp_in, mlp_out):
    r, _, width = space_qkv.shape
    return jnp.concatenate(
        (
            columns(space_qkv, r, width),
            space_out.T[None],
            columns(mlp_in, r, width),
            columns(mlp_out.T, r, width),
        ),
        axis=0,
    )


def along_seq(pack):
    return lax.all_gather(pack, "seq", axis=1, tiled=True)


def gather_slabs(part):
    full = lax.all_gather(part, ("head", "clip"), axis=1, tiled=True)
    return full.reshape(part.shape[0], lax.axis_size("head"), -1, part.shape[2])


def spread_steps(pack, me):
    ways, clips = lax.axis_size("seq"), lax.axis_size("clip")
    shares = lax.axis_size("head")
    n, r, width = pack.shape
    pack = yield pack
    turned = [pack] + [
        lax.ppermute(pack, "seq", [(i, (i + k) % ways) for i in range(ways)]) for k in range(1, ways)
    ]
    turned = yield turned
    orders = (((0, 1), "x", "h"), ((3, 2), "h", "x"))
    some = [jnp.stack([turned[k] for k in steps]) for steps, _, _ in orders]
    come = yield [cross(a, first) for a, (_, first, _) in zip(some, orders)]
    some = [jnp.concatenate(pair, axis=0) for pair in zip(some, come)]
    come = yield [cross(a, second) for a, (_, _, second) in zip(some, orders)] + [
        cross(a, "c") for a in some
    ]
    far = yield come + [cross(a, "c") for a in come[:2]]
    come, far = far[:2], far[2:]
    runs = []
    for i, (steps, first, second) in enumerate(orders):
        where = [(k, {first: f}) for f in (0, 1) for k in steps]
        near = [(k, {**at, second: 0}) for k, at in where]
        past = [(k, {**at, second: 1}) for k, at in where]
        runs += [(some[i], near, 0), (come[i], past, 0), (far[i], near, 1), (far[2 + i], past, 1)]
    count = sum(len(where) for _, where, _ in runs)

    def body(me_ref, *refs):
        sources, out_ref, sems = refs[: len(runs)], refs[-2], refs[-1]
        copies = []
        for source, (_, where, core) in zip(sources, runs):
            for i, (k, at) in enumerate(where):
                share = jnp.bitwise_xor(me_ref[2], at["h"])
                clip = 2 * jnp.bitwise_xor(me_ref[1], at["x"]) + jnp.bitwise_xor(me_ref[0], core)
                seq = lax.rem(me_ref[4] + (ways - k), ways)
                copies.append(
                    pltpu.make_async_copy(
                        source.at[i], out_ref.at[:, share, clip * ways + seq], sems.at[len(copies)]
                    )
                )
        for copy in copies:
            copy.start()
        for copy in copies:
            copy.wait()

    full = pl.pallas_call(
        body,
        out_shape=jax.ShapeDtypeStruct((n, shares, clips * ways, r, width), BF16),
        in_specs=[SCALARS] + [pl.BlockSpec(memory_space=pltpu.HBM)] * len(runs),
        out_specs=pl.BlockSpec(memory_space=pltpu.VMEM),
        scratch_shapes=[pltpu.SemaphoreType.DMA((count,))],
        compiler_params=pltpu.CompilerParams(vmem_limit_bytes=VMEM),
        cost_estimate=pl.CostEstimate(
            flops=0, bytes_accessed=4 * n * shares * clips * ways * r * width, transcendentals=0
        ),
    )(me, *(blocks for blocks, _, _ in runs))
    yield full.reshape(n, shares, clips * ways * r, width)


class Spread:
    def __init__(self, pack, me):
        self.way = spread_steps(pack, me)
        self.come = next(self.way)

    def hold(self, x):
        x, self.come = lax.optimization_barrier((x, self.come))
        return x

    def step(self, x):
        x = self.hold(x)
        self.come = self.way.send(self.come)
        return x


def mix_whole(slab, shards):
    shares, depth, width = slab.shape
    part = slab.reshape(shares, shards, shares, depth // (shards * shares), width)
    return part.transpose(1, 0, 3, 2, 4).reshape(depth, shares * width)


def mix_slab(whole_grad, shards, shares):
    depth, full = whole_grad.shape
    width = full // shares
    part = whole_grad.reshape(shards, shares, depth // (shards * shares), shares, width)
    return part.transpose(1, 0, 3, 2, 4).reshape(1, shares, depth, width)


class Piece:
    def __init__(self, keep, got, first, n, order):
        self.near = (keep, got)
        self.first = first
        self.n = n
        self.order = order
        self.step = 0
        self.held = []
        self.result = None


PLACE = {"x": 1, "h": 2}


def fold(pieces, me, last_by_rows):
    ways = lax.axis_size("seq")
    depth, width = pieces[0].near[0].shape[-2:]
    r = depth // ways
    used = {}
    arrays = []

    def number(a):
        for i, known in enumerate(arrays):
            if known is a:
                return i
        arrays.append(a)
        return len(arrays) - 1

    plans = []
    for p in pieces:
        link = p.order[p.step] if p.step < 2 else "z"
        blocks = p.n * (2 if p.step == 0 else 1)
        base = used.get(link, 0)
        used[link] = base + blocks
        near = [number(a) for a in p.near]
        held = [(number(a), at) for a, at in p.held]
        plans.append((p, link, base, near, held))
    links = sorted(used)
    shapes = [
        (ways, used[k], r, width) if k == "z" and last_by_rows else (used[k], depth, width)
        for k in links
    ]
    rooms, counts = [], []
    for p, link, base, near, held in plans:
        each = 2 if p.step == 0 else 1
        counts.append((each, len(near) + len(held)))
        rooms += [(each * p.n, depth, width)] * (len(near) + len(held))
    copies_needed = sum(each * terms for each, terms in counts)

    def body(me_ref, *refs):
        sources = refs[: len(arrays)]
        outs = dict(zip(links, refs[len(arrays) : len(arrays) + len(links)]))
        held_refs = refs[len(arrays) + len(links) : -1]
        sems = refs[-1]
        mine = {name: me_ref[PLACE[name]] for name in PLACE}
        groups = []
        room = 0
        sem = 0
        for p, link, base, near, held in plans:
            group = []
            if p.step == 0:
                for term in near:
                    for k in range(2):
                        pick = {p.order[0]: 1 - mine[p.order[0]], p.order[1]: k}
                        source = sources[term].at[pl.ds(p.first, p.n), pick["h"], pick["x"]]
                        group.append((source, held_refs[room].at[pl.ds(k * p.n, p.n)]))
                    room += 1
            else:
                last = p.order[1]
                pick = {p.order[0]: mine[p.order[0]]}
                pick[last] = 1 - mine[last] if p.step == 1 else mine[last]
                for term in near:
                    source = sources[term].at[pl.ds(p.first, p.n), pick["h"], pick["x"]]
                    group.append((source, held_refs[room]))
                    room += 1
                for i, (term, at) in enumerate(held):
                    start = at + pick[last] * p.n if i == 0 else at
                    group.append((sources[term].at[pl.ds(start, p.n)], held_refs[room]))
                    room += 1
            made_copies = []
            for source, target in group:
                made_copies.append(pltpu.make_async_copy(source, target, sems.at[sem]))
                sem += 1
            groups.append(made_copies)
        for group in groups:
            for copy in group:
                copy.start()
        room = 0
        for (p, link, base, near, held), (each, terms), group in zip(plans, counts, groups):
            these = held_refs[room : room + terms]
            room += terms
            for copy in group:
                copy.wait()

            @pl.loop(0, each * p.n)
            def _(i, these=these, base=base, out=outs[link], last=p.step == 2 and last_by_rows):
                value = these[0][i].astype(F32)
                for one in these[1:]:
                    value = value + one[i].astype(F32)
                value = value.astype(BF16)
                if last:
                    for k in range(ways):
                        out[k, base + i] = value[k * r : (k + 1) * r]
                else:
                    out[base + i] = value

    moved = sum(2 * math.prod(room) for room in rooms) + sum(2 * math.prod(shape) for shape in shapes)
    sums = pl.pallas_call(
        body,
        out_shape=[jax.ShapeDtypeStruct(shape, BF16) for shape in shapes],
        in_specs=[SCALARS] + [pl.BlockSpec(memory_space=pltpu.HBM)] * len(arrays),
        out_specs=[pl.BlockSpec(memory_space=pltpu.VMEM)] * len(links),
        scratch_shapes=[pltpu.VMEM(room, BF16) for room in rooms]
        + [pltpu.SemaphoreType.DMA((copies_needed,))],
        compiler_params=pltpu.CompilerParams(vmem_limit_bytes=VMEM),
        cost_estimate=pl.CostEstimate(flops=0, bytes_accessed=moved, transcendentals=0),
    )(me, *arrays)
    return [(p, link, base) for p, link, base, _, _ in plans], dict(zip(links, sums))


def cross(a, name):
    axis, bit = ("head", 0) if name == "h" else ("clip", 1 if name == "x" else 0)
    size = lax.axis_size(axis)
    return lax.ppermute(a, axis, [(i, i ^ (1 << bit)) for i in range(size)])


def pieces_of(halves_of):
    total = sum(keep.shape[0] for keep, _ in halves_of)
    found = []
    seen = 0
    for keep, send in halves_of:
        got = cross(send, "c")
        n = keep.shape[0]
        first = min(max((total + 1) // 2 - seen, 0), n)
        if first:
            found.append(Piece(keep, got, 0, first, ("x", "h")))
        if n > first:
            found.append(Piece(keep, got, first, n - first, ("h", "x")))
        seen += n
    return found


def move(x, pieces, me, at_end=False):
    plans, sums = fold(pieces, me, at_end)
    x, sums = lax.optimization_barrier((x, sums))
    got = {}
    for link, array in sums.items():
        if link == "z":
            if at_end:
                every = lax.all_to_all(array, "seq", split_axis=0, concat_axis=0, tiled=True)
                got[link] = jnp.sum(every.astype(F32), axis=0)
            else:
                own = lax.psum_scatter(array, "seq", scatter_dimension=1, tiled=True)
                got[link] = own.astype(F32)
        else:
            got[link] = cross(array, link)
    for p, link, base in plans:
        if link == "z":
            p.result = got[link][base : base + p.n]
        else:
            p.held.append((got[link], base))
        p.step += 1
    return x


def settle(x, pieces):
    arrays = []
    for p in pieces:
        if not any(p.held[-1][0] is a for a in arrays):
            arrays.append(p.held[-1][0])
    x, came = lax.optimization_barrier((x, arrays))
    for p in pieces:
        for old, new in zip(arrays, came):
            if p.held[-1][0] is old:
                p.held[-1] = (new, p.held[-1][1])
                break
    return x


def reduce_plain(halves_of, core):
    def joined(keep, send):
        low = jnp.where(core == 0, keep, send)
        high = jnp.where(core == 0, send, keep)
        n, shares, pairs, depth, width = keep.shape
        return jnp.stack((low, high), axis=3).reshape(n, shares, 2 * pairs * depth, width)

    g = jnp.concatenate([joined(*pair) for pair in halves_of], axis=0)
    g = lax.psum_scatter(g, "head", scatter_dimension=1, tiled=True)
    g = lax.psum_scatter(g.astype(F32), ("clip", "seq"), scatter_dimension=2, tiled=True)
    return g[:, 0]


def gather_norms(gain, bias):
    layers, norms, part = gain.shape
    both = jnp.concatenate((gain, bias), axis=1).reshape(1, -1)
    count = lax.axis_size("clip") * lax.axis_size("seq") * lax.axis_size("head")
    width = round_up(both.shape[1], 128)
    padded = jnp.pad(both, ((0, 0), (0, width - both.shape[1])))
    every = lax.all_to_all(
        jnp.broadcast_to(padded, (count, width)), ALL, split_axis=0, concat_axis=0, tiled=True
    )[:, : both.shape[1]]
    return every.reshape(count, layers * 2 * norms, part).transpose(1, 0, 2).reshape(layers, 2 * norms, -1)


def reduce_norms(sums):
    count = lax.axis_size("clip") * lax.axis_size("seq") * lax.axis_size("head")
    rows, features = sums.shape
    part = features // count
    a = sums.reshape(rows, count, part).transpose(1, 0, 2).reshape(count, rows * part)
    width = round_up(rows * part, 128)
    a = jnp.pad(a, ((0, 0), (0, width - rows * part)))
    every = lax.all_to_all(a, ALL, split_axis=0, concat_axis=0, tiled=True)
    return jnp.sum(every, axis=0)[: rows * part].reshape(rows, part)


def on_device(
    tokens,
    cotangent,
    time_qkv,
    time_out,
    time_mix,
    space_qkv,
    space_out,
    mlp_in,
    mlp_out,
    norm_gain,
    norm_bias,
):
    layers = time_qkv.shape[0]
    clips, frames, places, d = tokens.shape
    ways = lax.axis_size("seq")
    shards = lax.axis_size("clip") * ways
    rows = Rows(clips * frames, places, ways)
    shares = lax.axis_size("head")

    def as_rows(a):
        a = a.astype(F32).reshape(rows.frames, places, d)
        a = jnp.pad(a, ((0, 0), (0, rows.frame_rows - places), (0, 0)))
        return a.reshape(rows.rows, d)

    def from_rows(a):
        a = a.reshape(rows.frames, rows.frame_rows, d)[:, :places]
        return a.reshape(tokens.shape)

    gbs = gather_norms(norm_gain, norm_bias)
    gb = [gbs[l] for l in range(layers)]
    packs = [
        pack_time(time_qkv[l], time_out[l], time_mix[l])
        for l in range(layers)
    ]
    packs_ff = [pack_rest(space_qkv[l], space_out[l], mlp_in[l], mlp_out[l]) for l in range(layers)]
    quick = lax.axis_size("clip") == 4 and shares == 2 and ways == 4 and time_qkv.shape[1] % 16 == 0

    halves = Halves(lax.axis_size("clip"), d, time_qkv.shape[3])
    clip = lax.axis_index("clip")
    member = member_of(clip, lax.axis_index("seq"))
    me = jnp.stack((clip & 1, (clip >> 1) & 1, lax.axis_index("head"), member, lax.axis_index("seq"))).astype(
        jnp.int32
    )
    if quick:
        spreads = [Spread(pack, me) for pack in packs_ff]
        weights_ff = []
    else:
        weights_ff = [gather_slabs(along_seq(pack)) for pack in packs_ff]

    home = go_home(tokens)
    if quick:
        first = spreads[0]
        gb, home, packs[0] = lax.optimization_barrier((gb, home, packs[0]))
    part = along_seq(packs[0])
    if quick:
        part = first.step(part)
    weights = [gather_slabs(part)]
    x = as_rows(home)
    send = swap_places(send_first(rows, x, gb[0], me))
    if quick:
        send, packs[1:] = lax.optimization_barrier((send, packs[1:]))
    weights += [gather_slabs(along_seq(pack)) for pack in packs[1:]]
    mixes = [mix_whole(w[-1], shards) for w in weights]
    kept = []
    for l in range(layers):
        w = weights[l]
        if l:
            send = swap_places(send)
        if quick and l == 0:
            send = first.step(send)
            for spread in spreads[1:]:
                send = spread.step(send)
            send = first.step(send)
            for spread in spreads[1:]:
                send = spread.hold(send)
        a1, qkv1, log1, o1_time = time_forward(rows, send, w)
        back = swap_places(o1_time)
        if quick:
            for _ in range(2):
                back = spreads[l].step(back)
            if l == 0:
                for spread in spreads[1:]:
                    back = spread.step(back)
            weights_ff.append(spreads[l].come)
        o1, y1, x1, qkv2 = middle_forward(rows, back, x, w, weights_ff[l], mixes[l], gb[l], me)
        o2, x2, log2 = space_forward(rows, qkv2, x1, weights_ff[l])
        if quick and l == 0:
            for spread in spreads[1:]:
                x2 = spread.step(x2)
        kept.append((x, a1, qkv1, log1, o1, y1, x1, qkv2, o2, log2, x2))
        if l + 1 < layers:
            x, *send = mlp_forward(rows, x2, weights_ff[l], gb[l], gb[l + 1], me)

    grad = as_rows(go_home(cotangent))
    norm_rows = [None] * layers
    summed = [None] * layers
    late = []
    for l in reversed(range(layers)):
        w = weights[l]
        x, a1, qkv1, log1, o1, y1, x1, qkv2, o2, log2, x2 = kept[l]
        grad, g_ff, s3, x3 = mlp_backward(
            rows, grad, x2, weights_ff[l], gb[l], me, halves, l + 1 == layers
        )
        if x3:
            output = go_back(from_rows(x3[0].astype(BF16)))
        if quick:
            ff = pieces_of(g_ff)
            if late:
                grad = settle(grad, late)
                grad = move(grad, late, me)
                late = [p for p in late if p.step < 3]
        grad, g_space, s2 = space_backward(
            rows, grad, x1, qkv2, o2, log2, weights_ff[l], gb[l], me, halves
        )
        if quick:
            space = pieces_of([g_space])
            if late:
                grad = settle(grad, late)
            grad, output = move((grad, output), ff, me)
        do1, g_out = middle_backward(rows, grad, y1, o1, w, mixes[l], me, halves, shards)
        do1 = swap_places(do1)
        if quick:
            do1 = move(do1, ff + space + late, me)
        da1, g_time = time_backward(rows, do1, a1, qkv1, log1, w, me, halves)
        if quick:
            da1 = settle(da1, ff + space)
        da1 = swap_places(da1)
        if quick:
            rest = pieces_of([g_out] + g_time)
            da1 = move(da1, ff + space + rest, me)
            late = space + rest
        grad, s1 = first_norm_back(rows, da1, x, grad, gb[l], me)
        norm_rows[l] = jnp.concatenate((s1[0:1], s2[0:1], s3[0:1], s1[1:2], s2[1:2], s3[1:2]), axis=0)
        if quick:
            summed[l] = ff + space + rest
        else:
            summed[l] = [reduce_plain(g_ff + [g_space, g_out] + g_time, clip & 1)]
    if quick:
        tokens_grad = move(go_back(from_rows(grad.astype(BF16))), late, me)
        move((), rest, me, True)
        summed = [[p.result for p in some] for some in summed]
    cuts = (2 * g_ff[0][0].shape[0], g_space[0].shape[0], g_out[0].shape[0], len(g_time))
    results = []
    for some in summed:
        slabs_of = jnp.concatenate(some, axis=0)
        ends = [sum(cuts[: i + 1]) for i in range(4)]
        results.append([slabs_of[e - c : e] for c, e in zip(cuts, ends)])
    if not quick:
        tokens_grad = go_back(from_rows(grad.astype(BF16)))
    tokens_grad = tokens_grad.astype(F32)
    norm_sums = reduce_norms(jnp.concatenate(norm_rows, axis=0)).reshape(layers, 2, 3, -1)

    def stacked(form):
        return jnp.stack([form(*results[l]) for l in range(layers)])

    def rows_of(a):
        return a.transpose(1, 0, 2)

    def flat(a):
        return rows_of(a).reshape(a.shape[1], -1)

    def mix_rows(a):
        r, width = a.shape
        return a.reshape(shares, r // shares, width).transpose(1, 0, 2).reshape(r // shares, -1)

    per_share = mlp_in.shape[2] // time_qkv.shape[3]
    return (
        output,
        tokens_grad,
        stacked(lambda ff, s, t, q: rows_of(q)),
        stacked(lambda ff, s, t, q: t[0].T),
        stacked(lambda ff, s, t, q: mix_rows(t[1])),
        stacked(lambda ff, s, t, q: rows_of(s[1:])),
        stacked(lambda ff, s, t, q: s[0].T),
        stacked(lambda ff, s, t, q: flat(ff[:per_share])),
        stacked(lambda ff, s, t, q: flat(ff[per_share:]).T),
        norm_sums[:, 0],
        norm_sums[:, 1],
    )


def solution(mesh):
    token_spec = P(("clip", "head"), "seq", None, None)
    in_specs = (
        token_spec,
        token_spec,
        P(None, ("clip", "seq"), None, "head"),
        P(None, "head", ("clip", "seq")),
        P(None, ("clip", "seq", "head"), None),
        P(None, ("clip", "seq"), None, "head"),
        P(None, "head", ("clip", "seq")),
        P(None, ("clip", "seq"), "head"),
        P(None, "head", ("clip", "seq")),
        P(None, None, ("clip", "seq", "head")),
        P(None, None, ("clip", "seq", "head")),
    )
    return jax.shard_map(
        on_device, mesh=mesh, in_specs=in_specs, out_specs=in_specs, check_vma=False
    )
```

```python
import functools
import math

import jax
import jax.numpy as jnp
from jax import lax
from jax.experimental import pallas as pl
from jax.experimental.pallas import tpu as pltpu
from jax.sharding import PartitionSpec as P

HEAD_DIM = 64
NORM_EPS = 1e-06
HALF_ROOT = 0.7071067811865476
INV_ROOT_TAU = 0.3989422804014327
LOG2E = 1.4426950408889634
FAR = -1e30
LANES = 128
VMEM = 56 * 1024 * 1024
SHOWN = 1.0
ALL = ("clip", "seq", "head")
BF16 = jnp.bfloat16
F32 = jnp.float32


def round_up(value, step):
    return -(-value // step) * step


def nn(a, b):
    return lax.dot_general(a, b, (((1,), (0,)), ((), ())), preferred_element_type=F32)


def nt(a, b):
    return lax.dot_general(a, b, (((1,), (1,)), ((), ())), preferred_element_type=F32)


def tn(a, b):
    return lax.dot_general(a, b, (((0,), (0,)), ((), ())), preferred_element_type=F32)


def norm_parts(x):
    mean = jnp.mean(x, axis=-1, keepdims=True)
    centred = x - mean
    spread = lax.rsqrt(jnp.mean(centred * centred, axis=-1, keepdims=True) + NORM_EPS)
    return centred * spread, spread


def norm_rounded(x, gain, bias):
    hat, _ = norm_parts(x)
    return (hat * gain + bias).astype(BF16)


def norm_back(u, x, gain):
    hat, spread = norm_parts(x)
    scaled = u * gain
    mean_scaled = jnp.mean(scaled, axis=-1, keepdims=True)
    mean_cross = jnp.mean(scaled * hat, axis=-1, keepdims=True)
    change = spread * (scaled - mean_scaled - hat * mean_cross)
    sums = jnp.concatenate(
        (jnp.sum(u * hat, axis=0, keepdims=True), jnp.sum(u, axis=0, keepdims=True)), axis=0
    )
    return change, sums


class Rows:
    def __init__(self, frames, places, ways):
        self.frames = frames
        self.places = places
        self.ways = ways
        self.frame_rows = round_up(places, 16)
        self.rows = frames * self.frame_rows
        self.block = places // ways
        self.chunk = round_up(frames * self.block, 8)
        self.time_rows = ways * self.chunk

    def split(self, r):
        way = jnp.zeros_like(r)
        for k in range(1, self.ways):
            way = way + (r >= k * self.chunk).astype(jnp.int32)
        rest = r - way * self.chunk
        frame = jnp.zeros_like(r)
        for k in range(1, self.frames):
            frame = frame + (rest >= k * self.block).astype(jnp.int32)
        real = rest < self.frames * self.block
        return way, frame, rest - frame * self.block, real

    def to_time(self, k, member):
        r = lax.broadcasted_iota(jnp.int32, (self.chunk, 1), 0)
        _, frame, place, real = self.split(r)
        way = jnp.bitwise_xor(member, k)
        source = jnp.where(real, frame * self.frame_rows + way * self.block + place, -1)
        c = lax.broadcasted_iota(jnp.int32, (self.chunk, self.rows), 1)
        return jnp.where(c == source, 1.0, 0.0).astype(BF16)

    def gathered(self, chunk_refs, member):
        total = tn(self.to_time(0, member), chunk_refs[0][...])
        for k in range(1, self.ways):
            total = total + tn(self.to_time(k, member), chunk_refs[k][...])
        return total

    def chunks(self, width, block=None, index=None):
        return [
            made((self.chunk, width), BF16)
            if block is None
            else made((self.chunk, width), BF16, (self.chunk, block), index)
            for _ in range(self.ways)
        ]

    def time_bias(self):
        def label(r):
            _, _, place, real = self.split(r)
            return jnp.where(real, place, -1)

        a = label(lax.broadcasted_iota(jnp.int32, (self.time_rows, 1), 0))
        b = label(lax.broadcasted_iota(jnp.int32, (1, self.time_rows), 1))
        return jnp.where(a == b, 0.0, FAR).astype(F32)

    def space_bias(self):
        a = lax.broadcasted_iota(jnp.int32, (self.frame_rows, 1), 0)
        return jnp.where(a < self.places, 0.0, FAR).astype(F32)


def lane_masks(rows):
    lane = lax.broadcasted_iota(jnp.int32, (rows, LANES), 1)
    return lane < HEAD_DIM


def one_of(value, low, half):
    zero = jnp.zeros_like(value)
    return jnp.where(low, value, zero) if half == 0 else jnp.where(low, zero, value)


def pair_forward(q, k, v, bias, rate):
    low = lane_masks(q.shape[0])
    mixed, logs = [], []
    for half in range(2):
        s = nt(k, one_of(q, low, half)) + bias
        peak = jnp.max(s, axis=0, keepdims=True)
        e = jnp.exp2((s - peak) * rate)
        total = jnp.sum(e, axis=0, keepdims=True)
        soft = (e * (1.0 / total)).astype(BF16)
        mixed.append(tn(soft, v))
        logs.append(peak * rate + jnp.log2(total))
    return jnp.where(low, mixed[0], mixed[1]).astype(BF16), logs


def pair_backward(q, k, v, do, logs, bias, rate, scale):
    low = lane_masks(q.shape[0])
    dq, dk, dv = [], [], []
    for half in range(2):
        s = nt(k, one_of(q, low, half)) + bias
        soft = jnp.exp2(s * rate - logs[half])
        dp = nt(v, one_of(do, low, half))
        ds = (soft * (dp - jnp.sum(soft * dp, axis=0, keepdims=True))).astype(BF16)
        dv.append(nn(soft.astype(BF16), do))
        dk.append(nn(ds, q))
        dq.append(tn(ds, k))
    return (
        (jnp.where(low, dq[0], dq[1]) * scale).astype(BF16),
        (jnp.where(low, dk[0], dk[1]) * scale).astype(BF16),
        jnp.where(low, dv[0], dv[1]).astype(BF16),
    )


def split_rows(value, keep_ref, send_ref, at, room_ref, me_ref):
    mine = me_ref[0]
    room_ref[...] = value.reshape(room_ref.shape)
    keep_ref[at] = room_ref[:, mine].astype(BF16)
    send_ref[at] = room_ref[:, 1 - mine].astype(BF16)


class Halves:
    def __init__(self, clips, depth, width):
        self.pairs = clips // 2
        self.rows = depth // clips
        self.width = width

    def array(self, lead, block, index):
        tail = (self.pairs, self.rows, self.width)
        one = lambda: made(lead + tail, BF16, block + tail, lambda *g: index(*g) + (0, 0, 0))
        return [one(), one()]

    def room(self):
        return pltpu.VMEM((self.pairs, 2, self.rows, self.width), F32)


SCALARS = pl.BlockSpec(memory_space=pltpu.SMEM)


def call(body, grid, ins, outs, scratch, args, flops=0):
    specs = [spec for spec in ins]
    moved = sum(math.prod(o.shape) * o.dtype.itemsize for o, _ in outs)
    moved += sum(math.prod(a.shape) * a.dtype.itemsize for a in args)
    return pl.pallas_call(
        body,
        out_shape=[shape for shape, _ in outs],
        grid=grid,
        in_specs=specs,
        out_specs=[spec for _, spec in outs],
        scratch_shapes=scratch,
        compiler_params=pltpu.CompilerParams(vmem_limit_bytes=VMEM),
        cost_estimate=pl.CostEstimate(
            flops=int(flops * SHOWN), bytes_accessed=int(moved * SHOWN), transcendentals=0
        ),
    )(*args)


def whole(shape):
    zeros = (0,) * len(shape)
    return pl.BlockSpec(shape, lambda *_: zeros)


def made(shape, dtype, block=None, index=None):
    spec = whole(shape) if block is None else pl.BlockSpec(block, index)
    return jax.ShapeDtypeStruct(shape, dtype), spec


def slabs(count, first, width, depth):
    return pl.BlockSpec((count, 1, depth, width), lambda h, *_: (first // count, h, 0, 0))


def send_first(rows, x, gb, me):
    def body(me_ref, x_ref, gb_ref, *out_refs):
        a = norm_rounded(x_ref[...], gb_ref[0:1], gb_ref[3:4])
        for k in range(rows.ways):
            out_refs[k][...] = nn(rows.to_time(k, me_ref[3]), a).astype(BF16)

    d = x.shape[1]
    return call(
        body, (1,), [SCALARS, whole(x.shape), whole(gb.shape)], rows.chunks(d), [], (me, x, gb)
    )


def time_forward(rows, chunks, w):
    t, d = rows.time_rows, chunks[0].shape[1]
    width = w.shape[3]
    shares = w.shape[1]
    pairs = width // LANES
    ways = rows.ways
    rate = LOG2E / math.sqrt(HEAD_DIM)

    def body(*refs):
        chunk_refs = refs[:ways]
        w_ref, a_ref, qkv_ref, log_ref = refs[ways : ways + 4]
        out_refs = refs[ways + 4 : 2 * ways + 4]
        bias_ref, mixed_ref = refs[2 * ways + 4 :]

        @pl.when(pl.program_id(0) == 0)
        def _():
            bias_ref[...] = rows.time_bias()
            for k in range(ways):
                a_ref[k * rows.chunk : (k + 1) * rows.chunk] = chunk_refs[k][...]

        act = a_ref[...]
        for g in range(3):
            qkv_ref[g] = nn(act, w_ref[g, 0]).astype(BF16)

        @pl.loop(0, pairs)
        def _(i):
            lanes = pl.ds(pl.multiple_of(i * LANES, LANES), LANES)
            mixed, logs = pair_forward(
                qkv_ref[0, :, lanes], qkv_ref[1, :, lanes], qkv_ref[2, :, lanes], bias_ref[...], rate
            )
            mixed_ref[:, lanes] = mixed
            log_ref[0, i] = jnp.concatenate(logs, axis=0)

        for k in range(ways):
            out_refs[k][...] = mixed_ref[k * rows.chunk : (k + 1) * rows.chunk]

    got = call(
        body,
        (shares,),
        [whole(c.shape) for c in chunks] + [slabs(3, 0, width, d)],
        [
            made((t, d), BF16),
            made((3, t, d), BF16, (3, t, width), lambda h: (0, 0, h)),
            made((shares, pairs, 2, t), F32, (1, pairs, 2, t), lambda h: (h, 0, 0, 0)),
            *rows.chunks(d, width, lambda h: (0, h)),
        ],
        [pltpu.VMEM((t, t), F32), pltpu.VMEM((t, width), BF16)],
        (*chunks, w),
        flops=2 * t * d * 3 * d,
    )
    return got[0], got[1], got[2], got[3:]


def middle_forward(rows, back, x, w, ws, mix, gb, me):
    t, d = x.shape
    width = w.shape[3]
    shares = w.shape[1]

    def body(me_ref, *refs):
        x_ref, to_ref, sq_ref, mix_ref, gb_ref, o1_ref, y1_ref, x1_ref, qkv_ref = refs[rows.ways :]
        o1 = rows.gathered(refs[: rows.ways], me_ref[3]).astype(BF16)
        o1_ref[...] = o1
        y1 = jnp.zeros((t, d), F32)
        for h in range(shares):
            y1 = y1 + nt(o1[:, h * width : (h + 1) * width], to_ref[0, h])
        y1 = y1.astype(BF16)
        y1_ref[...] = y1
        x1 = x_ref[...] + nn(y1, mix_ref[...])
        x1_ref[...] = x1
        a2 = norm_rounded(x1, gb_ref[1:2], gb_ref[4:5])
        for g in range(3):
            for h in range(shares):
                qkv_ref[g, :, h * width : (h + 1) * width] = nn(a2, sq_ref[g, h]).astype(BF16)

    return call(
        body,
        (1,),
        [
            SCALARS,
            *(whole(c.shape) for c in back),
            whole(x.shape),
            pl.BlockSpec((1, shares, d, width), lambda i: (3, 0, 0, 0)),
            pl.BlockSpec((3, shares, d, width), lambda i: (0, 0, 0, 0)),
            whole(mix.shape),
            whole(gb.shape),
        ],
        [made((t, d), BF16), made((t, d), BF16), made((t, d), F32), made((3, t, d), BF16)],
        [],
        (me, *back, x, w, ws, mix, gb),
        flops=2 * t * d * 5 * d,
    )


def space_forward(rows, qkv, x1, w):
    t, d = x1.shape
    width = w.shape[3]
    shares = w.shape[1]
    pairs = width // LANES
    rate = LOG2E / math.sqrt(HEAD_DIM)
    n = rows.frame_rows

    def body(qkv_ref, x1_ref, w_ref, o2_ref, x2_ref, log_ref):
        bias = rows.space_bias()

        @pl.loop(0, pairs)
        def _(i):
            lanes = pl.ds(pl.multiple_of(i * LANES, LANES), LANES)
            for f in range(rows.frames):
                at = slice(f * n, (f + 1) * n)
                mixed, logs = pair_forward(
                    qkv_ref[0, at, lanes], qkv_ref[1, at, lanes], qkv_ref[2, at, lanes], bias, rate
                )
                o2_ref[at, lanes] = mixed
                log_ref[0, i, f] = jnp.concatenate(logs, axis=0)

        @pl.when(pl.program_id(0) == 0)
        def _():
            x2_ref[...] = x1_ref[...]

        x2_ref[...] += nt(o2_ref[...], w_ref[0, 0])

    return call(
        body,
        (shares,),
        [
            pl.BlockSpec((3, t, width), lambda h: (0, 0, h)),
            whole(x1.shape),
            slabs(1, 3, width, d),
        ],
        [
            made((t, d), BF16, (t, width), lambda h: (0, h)),
            made((t, d), F32),
            made(
                (shares, pairs, rows.frames, 2, n),
                F32,
                (1, pairs, rows.frames, 2, n),
                lambda h: (h, 0, 0, 0, 0),
            ),
        ],
        [],
        (qkv, x1, w),
        flops=2 * t * d * d,
    )


def ff_slab(first, per_share, depth, width):
    return pl.BlockSpec(
        (1, 1, depth, width), lambda j: (first + j % per_share, j // per_share, 0, 0)
    )


def mlp_forward(rows, x2, w, gb, gb_next, me):
    t, d = x2.shape
    width = w.shape[3]
    shares = w.shape[1]
    per_share = (w.shape[0] - 4) // 2
    steps = shares * per_share

    def body(x2_ref, wi_ref, wo_ref, gb_ref, me_ref, gn_ref, x3_ref, *rest):
        send_refs, a3_ref = rest[:-1], rest[-1]
        j = pl.program_id(0)

        @pl.when(j == 0)
        def _():
            a3_ref[...] = norm_rounded(x2_ref[...], gb_ref[2:3], gb_ref[5:6])
            x3_ref[...] = x2_ref[...]

        hid = nn(a3_ref[...], wi_ref[0, 0])
        act = (0.5 * hid * (1.0 + lax.erf(hid * HALF_ROOT))).astype(BF16)
        x3_ref[...] += nt(act, wo_ref[0, 0])

        @pl.when(j == steps - 1)
        def _():
            a = norm_rounded(x3_ref[...], gn_ref[0:1], gn_ref[3:4])
            for k in range(rows.ways):
                send_refs[k][...] = nn(rows.to_time(k, me_ref[3]), a).astype(BF16)

    ins = [
        whole(x2.shape),
        ff_slab(4, per_share, d, width),
        ff_slab(4 + per_share, per_share, d, width),
        whole(gb.shape),
    ]
    ins += [SCALARS, whole(gb_next.shape)]
    outs = [made((t, d), F32)] + rows.chunks(d)
    args = (x2, w, w, gb, me, gb_next)
    return call(
        body, (steps,), ins, outs, [pltpu.VMEM((t, d), BF16)], args, flops=4 * t * d * width * steps
    )


def mlp_backward(rows, grad, x2, w, gb, me, halves, with_output):
    t, d = x2.shape
    width = w.shape[3]
    shares = w.shape[1]
    per_share = (w.shape[0] - 4) // 2
    steps = shares * per_share

    def body(me_ref, g_ref, x2_ref, wi_ref, wo_ref, gb_ref, go_ref, ki_ref, si_ref, ko_ref, so_ref, sums_ref, *rest):
        if with_output:
            x3_ref, *rest = rest
        a3_ref, a3t_ref, e3_ref, e3t_ref, u_ref, room_ref = rest
        j = pl.program_id(0)

        @pl.when(j == 0)
        def _():
            hat, _ = norm_parts(x2_ref[...])
            a3 = hat * gb_ref[2:3] + gb_ref[5:6]
            a3_ref[...] = a3.astype(BF16)
            a3t_ref[...] = a3.T.astype(BF16)
            g = g_ref[...]
            e3_ref[...] = g.astype(BF16)
            e3t_ref[...] = g.T.astype(BF16)
            u_ref[...] = jnp.zeros((t, d), F32)
            if with_output:
                x3_ref[...] = x2_ref[...]

        hid = nn(a3_ref[...], wi_ref[0, 0])
        phi = 0.5 * (1.0 + lax.erf(hid * HALF_ROOT))
        act = (hid * phi).astype(BF16)
        slope = phi + hid * jnp.exp(-0.5 * hid * hid) * INV_ROOT_TAU
        dhid = (nn(e3_ref[...], wo_ref[0, 0]) * slope).astype(BF16)
        split_rows(nn(e3t_ref[...], act), ko_ref, so_ref, (0, 0), room_ref, me_ref)
        split_rows(nn(a3t_ref[...], dhid), ki_ref, si_ref, (0, 0), room_ref, me_ref)
        u_ref[...] += nt(dhid, wi_ref[0, 0])
        if with_output:
            x3_ref[...] += nt(act, wo_ref[0, 0])

        @pl.when(j == steps - 1)
        def _():
            change, sums = norm_back(u_ref[...], x2_ref[...], gb_ref[2:3])
            go_ref[...] = g_ref[...] + change
            sums_ref[...] = sums

    slab_outs = [
        one
        for _ in range(2)
        for one in halves.array(
            (per_share, shares), (1, 1), lambda j: (j % per_share, j // per_share)
        )
    ]
    grad, ki, si, ko, so, sums, *x3 = call(
        body,
        (steps,),
        [
            SCALARS,
            whole(grad.shape),
            whole(x2.shape),
            ff_slab(4, per_share, d, width),
            ff_slab(4 + per_share, per_share, d, width),
            whole(gb.shape),
        ],
        [made((t, d), F32), *slab_outs, made((2, d), F32)] + [made((t, d), F32)] * with_output,
        [
            pltpu.VMEM((t, d), BF16),
            pltpu.VMEM((d, t), BF16),
            pltpu.VMEM((t, d), BF16),
            pltpu.VMEM((d, t), BF16),
            pltpu.VMEM((t, d), F32),
            halves.room(),
        ],
        (me, grad, x2, w, w, gb),
        flops=10 * t * d * width * steps,
    )
    return grad, [(ki, si), (ko, so)], sums, x3


def space_backward(rows, grad, x1, qkv, o2, logs, w, gb, me, halves):
    t, d = x1.shape
    width = w.shape[3]
    shares = w.shape[1]
    pairs = width // LANES
    scale = 1.0 / math.sqrt(HEAD_DIM)
    rate = LOG2E * scale
    n = rows.frame_rows

    def body(me_ref, g_ref, x1_ref, qkv_ref, o2_ref, log_ref, wo_ref, wq_ref, gb_ref, go_ref, keep_ref, send_ref, sums_ref, e2_ref, e2t_ref, a2t_ref, do_ref, dqkv_ref, u_ref, room_ref):
        h = pl.program_id(0)

        @pl.when(h == 0)
        def _():
            g = g_ref[...]
            e2_ref[...] = g.astype(BF16)
            e2t_ref[...] = g.T.astype(BF16)
            hat, _ = norm_parts(x1_ref[...])
            a2t_ref[...] = (hat * gb_ref[1:2] + gb_ref[4:5]).T.astype(BF16)
            u_ref[...] = jnp.zeros((t, d), F32)

        bias = rows.space_bias()
        split_rows(nn(e2t_ref[...], o2_ref[...]), keep_ref, send_ref, (0, 0), room_ref, me_ref)
        do_ref[...] = nn(e2_ref[...], wo_ref[0, 0]).astype(BF16)

        @pl.loop(0, pairs)
        def _(i):
            lanes = pl.ds(pl.multiple_of(i * LANES, LANES), LANES)
            for f in range(rows.frames):
                at = slice(f * n, (f + 1) * n)
                log = log_ref[0, i, f]
                grads = pair_backward(
                    qkv_ref[0, at, lanes],
                    qkv_ref[1, at, lanes],
                    qkv_ref[2, at, lanes],
                    do_ref[at, lanes],
                    (log[0:1], log[1:2]),
                    bias,
                    rate,
                    scale,
                )
                for part in range(3):
                    dqkv_ref[part, at, lanes] = grads[part]

        for part in range(3):
            split_rows(
                nn(a2t_ref[...], dqkv_ref[part]), keep_ref, send_ref, (part + 1, 0), room_ref, me_ref
            )
            u_ref[...] += nt(dqkv_ref[part], wq_ref[part, 0])

        @pl.when(h == shares - 1)
        def _():
            change, sums = norm_back(u_ref[...], x1_ref[...], gb_ref[1:2])
            go_ref[...] = g_ref[...] + change
            sums_ref[...] = sums

    grad, keep, send, sums = call(
        body,
        (shares,),
        [
            SCALARS,
            whole(grad.shape),
            whole(x1.shape),
            pl.BlockSpec((3, t, width), lambda h: (0, 0, h)),
            pl.BlockSpec((t, width), lambda h: (0, h)),
            pl.BlockSpec((1,) + logs.shape[1:], lambda h: (h, 0, 0, 0, 0)),
            slabs(1, 3, width, d),
            slabs(3, 0, width, d),
            whole(gb.shape),
        ],
        [
            made((t, d), F32),
            *halves.array((4, shares), (4, 1), lambda h: (0, h)),
            made((2, d), F32),
        ],
        [
            pltpu.VMEM((t, d), BF16),
            pltpu.VMEM((d, t), BF16),
            pltpu.VMEM((d, t), BF16),
            pltpu.VMEM((t, width), BF16),
            pltpu.VMEM((3, t, width), BF16),
            pltpu.VMEM((t, d), F32),
            halves.room(),
        ],
        (me, grad, x1, qkv, o2, logs, w, w, gb),
        flops=2 * t * d * d * 8,
    )
    return grad, (keep, send), sums


def mix_fits(depth, shards, shares):
    return depth // (shards * shares) % 8 == 0


def middle_backward(rows, grad, y1, o1, w, mix, me, halves, shards):
    t, d = grad.shape
    width = w.shape[3]
    shares = w.shape[1]
    fits = mix_fits(d, shards, shares)
    part = d // (shards * shares)

    def body(me_ref, g_ref, y1_ref, o1_ref, to_ref, mix_ref, *rest):
        send_refs, rest = rest[: rows.ways], rest[rows.ways :]
        gk_ref, gs_ref, *rest = rest
        if fits:
            room_ref, order_ref = rest
        else:
            gm_ref, room_ref = rest
        e1 = g_ref[...].astype(BF16)
        dy1 = nt(e1, mix_ref[...]).astype(BF16)
        sends = [rows.to_time(k, me_ref[3]) for k in range(rows.ways)]
        for h in range(shares):
            lanes = slice(h * width, (h + 1) * width)
            do1 = nn(dy1, to_ref[0, h]).astype(BF16)
            for k in range(rows.ways):
                send_refs[k][:, lanes] = nn(sends[k], do1).astype(BF16)
            split_rows(tn(dy1, o1_ref[:, lanes]), gk_ref, gs_ref, (0, h), room_ref, me_ref)
        gm = tn(y1_ref[...], e1)
        if fits:
            gm = gm.reshape(shards, shares, part, d)
            for h in range(shares):
                for half in range(shares):
                    order_ref[:, half] = gm[:, h, :, half * width : (half + 1) * width]
                split_rows(order_ref[...], gk_ref, gs_ref, (1, h), room_ref, me_ref)
        else:
            gm_ref[...] = gm.astype(BF16)

    outs = rows.chunks(d)
    outs += halves.array((1 + fits, shares), (1 + fits, shares), lambda i: (0, 0))
    scratch = [halves.room()]
    if fits:
        scratch.append(pltpu.VMEM((shards, shares, part, width), F32))
    else:
        outs.append(made((d, d), BF16))
    got = call(
        body,
        (1,),
        [
            SCALARS,
            whole(grad.shape),
            whole(y1.shape),
            whole(o1.shape),
            pl.BlockSpec((1, shares, d, width), lambda i: (3, 0, 0, 0)),
            whole(mix.shape),
        ],
        outs,
        scratch,
        (me, grad, y1, o1, w, mix),
        flops=8 * t * d * d,
    )
    do1, (keep, send) = got[: rows.ways], got[rows.ways : rows.ways + 2]
    if not fits:
        gm = mix_slab(got[-1], shards, shares).reshape((1, shares, halves.pairs, 2) + keep.shape[3:])
        keep = jnp.concatenate((keep, lax.dynamic_index_in_dim(gm, me[0], 3, keepdims=False)), axis=0)
        send = jnp.concatenate((send, lax.dynamic_index_in_dim(gm, 1 - me[0], 3, keepdims=False)), axis=0)
    return do1, (keep, send)


def time_backward(rows, do1, a, qkv, logs, w, me, halves):
    t, d = a.shape
    width = w.shape[3]
    shares = w.shape[1]
    pairs = width // LANES
    scale = 1.0 / math.sqrt(HEAD_DIM)
    rate = LOG2E * scale

    def body(me_ref, *refs):
        do_refs, refs = refs[: rows.ways], refs[rows.ways :]
        a_ref, qkv_ref, log_ref, w_ref = refs[:4]
        out_refs, refs = refs[4 : 4 + rows.ways], refs[4 + rows.ways :]
        half_refs, refs = refs[:6], refs[6:]
        bias_ref, dqkv_ref, at_ref, u_ref, room_ref, do_ref = refs
        h = pl.program_id(0)

        @pl.when(h == 0)
        def _():
            bias_ref[...] = rows.time_bias()
            at_ref[...] = a_ref[...].T
            u_ref[...] = jnp.zeros((t, d), F32)

        for k in range(rows.ways):
            do_ref[k * rows.chunk : (k + 1) * rows.chunk] = do_refs[k][...]

        @pl.loop(0, pairs)
        def _(i):
            lanes = pl.ds(pl.multiple_of(i * LANES, LANES), LANES)
            log = log_ref[0, i]
            grads = pair_backward(
                qkv_ref[0, :, lanes],
                qkv_ref[1, :, lanes],
                qkv_ref[2, :, lanes],
                do_ref[:, lanes],
                (log[0:1], log[1:2]),
                bias_ref[...],
                rate,
                scale,
            )
            for part in range(3):
                dqkv_ref[part, :, lanes] = grads[part]

        for part in range(3):
            value = nn(at_ref[...], dqkv_ref[part])
            split_rows(value, half_refs[2 * part], half_refs[2 * part + 1], (0, 0), room_ref, me_ref)
            u_ref[...] += nt(dqkv_ref[part], w_ref[part, 0])

        @pl.when(h == shares - 1)
        def _():
            for k in range(rows.ways):
                out_refs[k][...] = u_ref[k * rows.chunk : (k + 1) * rows.chunk].astype(BF16)

    got = call(
        body,
        (shares,),
        [
            SCALARS,
            *(pl.BlockSpec((rows.chunk, width), lambda h: (0, h)) for _ in do1),
            whole(a.shape),
            pl.BlockSpec((3, t, width), lambda h: (0, 0, h)),
            pl.BlockSpec((1,) + logs.shape[1:], lambda h: (h, 0, 0, 0)),
            slabs(3, 0, width, d),
        ],
        [
            *rows.chunks(d),
            *(one for _ in range(3) for one in halves.array((1, shares), (1, 1), lambda h: (0, h))),
        ],
        [
            pltpu.VMEM((t, t), F32),
            pltpu.VMEM((3, t, width), BF16),
            pltpu.VMEM((d, t), BF16),
            pltpu.VMEM((t, d), F32),
            halves.room(),
            pltpu.VMEM((t, width), BF16),
        ],
        (me, *do1, a, qkv, logs, w),
        flops=2 * t * d * d * 6,
    )
    parts = got[rows.ways :]
    return got[: rows.ways], [tuple(parts[i : i + 2]) for i in (0, 2, 4)]


def first_norm_back(rows, back, x, grad, gb, me):
    t, d = x.shape

    def body(me_ref, *refs):
        x_ref, g_ref, gb_ref, go_ref, sums_ref = refs[rows.ways :]
        u = rows.gathered(refs[: rows.ways], me_ref[3])
        change, sums = norm_back(u, x_ref[...], gb_ref[0:1])
        go_ref[...] = g_ref[...] + change
        sums_ref[...] = sums

    return call(
        body,
        (1,),
        [SCALARS, *(whole(c.shape) for c in back), whole(x.shape), whole(grad.shape), whole(gb.shape)],
        [made((t, d), F32), made((2, d), F32)],
        [],
        (me, *back, x, grad, gb),
    )


def homes():
    clips, ways = lax.axis_size("clip"), lax.axis_size("seq")
    pairs = []
    for clip in range(clips):
        for seq in range(ways):
            home_clip = clip - clip % 2 + seq % 2
            home_seq = seq // 2 + (ways // 2) * (clip % 2)
            pairs.append((clip * ways + seq, home_clip * ways + home_seq))
    return pairs


def go_home(a):
    return lax.ppermute(a, ("clip", "seq"), homes())


def go_back(a):
    return lax.ppermute(a, ("clip", "seq"), [(home, device) for device, home in homes()])


def member_of(clip, seq):
    return clip % 2 + 2 * (seq % (lax.axis_size("seq") // 2))


def swap_places(chunks):
    clips, ways = lax.axis_size("clip"), lax.axis_size("seq")
    got = [chunks[0]]
    for k in range(1, ways):
        pairs = []
        for clip in range(clips):
            for seq in range(ways):
                other = member_of(clip, seq) ^ k
                to_clip = clip - clip % 2 + other % 2
                to_seq = seq - seq % (ways // 2) + other // 2
                pairs.append((clip * ways + seq, to_clip * ways + to_seq))
        got.append(lax.ppermute(chunks[k], ("clip", "seq"), pairs))
    return got


def columns(a, r, width):
    return a.reshape(r, -1, width).transpose(1, 0, 2)


def pack_time(time_qkv, time_out, time_mix):
    r, _, width = time_qkv.shape
    mix = time_mix.reshape(-1, time_mix.shape[1] // width, width).transpose(1, 0, 2).reshape(1, r, width)
    return jnp.concatenate((columns(time_qkv, r, width), time_out.T[None], mix), axis=0)


def pack_rest(space_qkv, space_out, mlp_in, mlp_out):
    r, _, width = space_qkv.shape
    return jnp.concatenate(
        (
            columns(space_qkv, r, width),
            space_out.T[None],
            columns(mlp_in, r, width),
            columns(mlp_out.T, r, width),
        ),
        axis=0,
    )


def along_seq(pack):
    return lax.all_gather(pack, "seq", axis=1, tiled=True)


def gather_slabs(part):
    full = lax.all_gather(part, ("head", "clip"), axis=1, tiled=True)
    return full.reshape(part.shape[0], lax.axis_size("head"), -1, part.shape[2])


def spread_steps(pack, me):
    ways, clips = lax.axis_size("seq"), lax.axis_size("clip")
    shares = lax.axis_size("head")
    n, r, width = pack.shape
    pack = yield pack
    turned = [pack] + [
        lax.ppermute(pack, "seq", [(i, (i + k) % ways) for i in range(ways)]) for k in range(1, ways)
    ]
    turned = yield turned
    orders = (((0, 1), "x", "h"), ((3, 2), "h", "x"))
    some = [jnp.stack([turned[k] for k in steps]) for steps, _, _ in orders]
    come = yield [cross(a, first) for a, (_, first, _) in zip(some, orders)]
    some = [jnp.concatenate(pair, axis=0) for pair in zip(some, come)]
    come = yield [cross(a, second) for a, (_, _, second) in zip(some, orders)] + [
        cross(a, "c") for a in some
    ]
    far = yield come + [cross(a, "c") for a in come[:2]]
    come, far = far[:2], far[2:]
    runs = []
    for i, (steps, first, second) in enumerate(orders):
        where = [(k, {first: f}) for f in (0, 1) for k in steps]
        near = [(k, {**at, second: 0}) for k, at in where]
        past = [(k, {**at, second: 1}) for k, at in where]
        runs += [(some[i], near, 0), (come[i], past, 0), (far[i], near, 1), (far[2 + i], past, 1)]
    count = sum(len(where) for _, where, _ in runs)

    def body(me_ref, *refs):
        sources, out_ref, sems = refs[: len(runs)], refs[-2], refs[-1]
        copies = []
        for source, (_, where, core) in zip(sources, runs):
            for i, (k, at) in enumerate(where):
                share = jnp.bitwise_xor(me_ref[2], at["h"])
                clip = 2 * jnp.bitwise_xor(me_ref[1], at["x"]) + jnp.bitwise_xor(me_ref[0], core)
                seq = lax.rem(me_ref[4] + (ways - k), ways)
                copies.append(
                    pltpu.make_async_copy(
                        source.at[i], out_ref.at[:, share, clip * ways + seq], sems.at[len(copies)]
                    )
                )
        for copy in copies:
            copy.start()
        for copy in copies:
            copy.wait()

    full = pl.pallas_call(
        body,
        out_shape=jax.ShapeDtypeStruct((n, shares, clips * ways, r, width), BF16),
        in_specs=[SCALARS] + [pl.BlockSpec(memory_space=pltpu.HBM)] * len(runs),
        out_specs=pl.BlockSpec(memory_space=pltpu.VMEM),
        scratch_shapes=[pltpu.SemaphoreType.DMA((count,))],
        compiler_params=pltpu.CompilerParams(vmem_limit_bytes=VMEM),
        cost_estimate=pl.CostEstimate(
            flops=0, bytes_accessed=4 * n * shares * clips * ways * r * width, transcendentals=0
        ),
    )(me, *(blocks for blocks, _, _ in runs))
    yield full.reshape(n, shares, clips * ways * r, width)


class Spread:
    def __init__(self, pack, me):
        self.way = spread_steps(pack, me)
        self.come = next(self.way)

    def hold(self, x):
        x, self.come = lax.optimization_barrier((x, self.come))
        return x

    def step(self, x):
        x = self.hold(x)
        self.come = self.way.send(self.come)
        return x


def mix_whole(slab, shards):
    shares, depth, width = slab.shape
    part = slab.reshape(shares, shards, shares, depth // (shards * shares), width)
    return part.transpose(1, 0, 3, 2, 4).reshape(depth, shares * width)


def mix_slab(whole_grad, shards, shares):
    depth, full = whole_grad.shape
    width = full // shares
    part = whole_grad.reshape(shards, shares, depth // (shards * shares), shares, width)
    return part.transpose(1, 0, 3, 2, 4).reshape(1, shares, depth, width)


class Piece:
    def __init__(self, keep, got, first, n, order):
        self.near = (keep, got)
        self.first = first
        self.n = n
        self.order = order
        self.step = 0
        self.held = []
        self.result = None


PLACE = {"x": 1, "h": 2}


def fold(pieces, me, last_by_rows):
    ways = lax.axis_size("seq")
    depth, width = pieces[0].near[0].shape[-2:]
    r = depth // ways
    used = {}
    arrays = []

    def number(a):
        for i, known in enumerate(arrays):
            if known is a:
                return i
        arrays.append(a)
        return len(arrays) - 1

    plans = []
    for p in pieces:
        link = p.order[p.step] if p.step < 2 else "z"
        blocks = p.n * (2 if p.step == 0 else 1)
        base = used.get(link, 0)
        used[link] = base + blocks
        near = [number(a) for a in p.near]
        held = [(number(a), at) for a, at in p.held]
        plans.append((p, link, base, near, held))
    links = sorted(used)
    shapes = [
        (ways, used[k], r, width) if k == "z" and last_by_rows else (used[k], depth, width)
        for k in links
    ]
    rooms, counts = [], []
    for p, link, base, near, held in plans:
        each = 2 if p.step == 0 else 1
        counts.append((each, len(near) + len(held)))
        rooms += [(each * p.n, depth, width)] * (len(near) + len(held))
    copies_needed = sum(each * terms for each, terms in counts)

    def body(me_ref, *refs):
        sources = refs[: len(arrays)]
        outs = dict(zip(links, refs[len(arrays) : len(arrays) + len(links)]))
        held_refs = refs[len(arrays) + len(links) : -1]
        sems = refs[-1]
        mine = {name: me_ref[PLACE[name]] for name in PLACE}
        groups = []
        room = 0
        sem = 0
        for p, link, base, near, held in plans:
            group = []
            if p.step == 0:
                for term in near:
                    for k in range(2):
                        pick = {p.order[0]: 1 - mine[p.order[0]], p.order[1]: k}
                        source = sources[term].at[pl.ds(p.first, p.n), pick["h"], pick["x"]]
                        group.append((source, held_refs[room].at[pl.ds(k * p.n, p.n)]))
                    room += 1
            else:
                last = p.order[1]
                pick = {p.order[0]: mine[p.order[0]]}
                pick[last] = 1 - mine[last] if p.step == 1 else mine[last]
                for term in near:
                    source = sources[term].at[pl.ds(p.first, p.n), pick["h"], pick["x"]]
                    group.append((source, held_refs[room]))
                    room += 1
                for i, (term, at) in enumerate(held):
                    start = at + pick[last] * p.n if i == 0 else at
                    group.append((sources[term].at[pl.ds(start, p.n)], held_refs[room]))
                    room += 1
            made_copies = []
            for source, target in group:
                made_copies.append(pltpu.make_async_copy(source, target, sems.at[sem]))
                sem += 1
            groups.append(made_copies)
        for group in groups:
            for copy in group:
                copy.start()
        room = 0
        for (p, link, base, near, held), (each, terms), group in zip(plans, counts, groups):
            these = held_refs[room : room + terms]
            room += terms
            for copy in group:
                copy.wait()

            @pl.loop(0, each * p.n)
            def _(i, these=these, base=base, out=outs[link], last=p.step == 2 and last_by_rows):
                value = these[0][i].astype(F32)
                for one in these[1:]:
                    value = value + one[i].astype(F32)
                value = value.astype(BF16)
                if last:
                    for k in range(ways):
                        out[k, base + i] = value[k * r : (k + 1) * r]
                else:
                    out[base + i] = value

    moved = sum(2 * math.prod(room) for room in rooms) + sum(2 * math.prod(shape) for shape in shapes)
    sums = pl.pallas_call(
        body,
        out_shape=[jax.ShapeDtypeStruct(shape, BF16) for shape in shapes],
        in_specs=[SCALARS] + [pl.BlockSpec(memory_space=pltpu.HBM)] * len(arrays),
        out_specs=[pl.BlockSpec(memory_space=pltpu.VMEM)] * len(links),
        scratch_shapes=[pltpu.VMEM(room, BF16) for room in rooms]
        + [pltpu.SemaphoreType.DMA((copies_needed,))],
        compiler_params=pltpu.CompilerParams(vmem_limit_bytes=VMEM),
        cost_estimate=pl.CostEstimate(flops=0, bytes_accessed=moved, transcendentals=0),
    )(me, *arrays)
    return [(p, link, base) for p, link, base, _, _ in plans], dict(zip(links, sums))


def cross(a, name):
    axis, bit = ("head", 0) if name == "h" else ("clip", 1 if name == "x" else 0)
    size = lax.axis_size(axis)
    return lax.ppermute(a, axis, [(i, i ^ (1 << bit)) for i in range(size)])


def pieces_of(halves_of):
    total = sum(keep.shape[0] for keep, _ in halves_of)
    found = []
    seen = 0
    for keep, send in halves_of:
        got = cross(send, "c")
        n = keep.shape[0]
        first = min(max((total + 1) // 2 - seen, 0), n)
        if first:
            found.append(Piece(keep, got, 0, first, ("x", "h")))
        if n > first:
            found.append(Piece(keep, got, first, n - first, ("h", "x")))
        seen += n
    return found


def move(x, pieces, me, at_end=False):
    plans, sums = fold(pieces, me, at_end)
    x, sums = lax.optimization_barrier((x, sums))
    got = {}
    for link, array in sums.items():
        if link == "z":
            if at_end:
                every = lax.all_to_all(array, "seq", split_axis=0, concat_axis=0, tiled=True)
                got[link] = jnp.sum(every.astype(F32), axis=0)
            else:
                own = lax.psum_scatter(array, "seq", scatter_dimension=1, tiled=True)
                got[link] = own.astype(F32)
        else:
            got[link] = cross(array, link)
    for p, link, base in plans:
        if link == "z":
            p.result = got[link][base : base + p.n]
        else:
            p.held.append((got[link], base))
        p.step += 1
    return x


def settle(x, pieces):
    arrays = []
    for p in pieces:
        if not any(p.held[-1][0] is a for a in arrays):
            arrays.append(p.held[-1][0])
    x, came = lax.optimization_barrier((x, arrays))
    for p in pieces:
        for old, new in zip(arrays, came):
            if p.held[-1][0] is old:
                p.held[-1] = (new, p.held[-1][1])
                break
    return x


def reduce_plain(halves_of, core):
    def joined(keep, send):
        low = jnp.where(core == 0, keep, send)
        high = jnp.where(core == 0, send, keep)
        n, shares, pairs, depth, width = keep.shape
        return jnp.stack((low, high), axis=3).reshape(n, shares, 2 * pairs * depth, width)

    g = jnp.concatenate([joined(*pair) for pair in halves_of], axis=0)
    g = lax.psum_scatter(g, "head", scatter_dimension=1, tiled=True)
    g = lax.psum_scatter(g.astype(F32), ("clip", "seq"), scatter_dimension=2, tiled=True)
    return g[:, 0]


def gather_norms(gain, bias):
    layers, norms, part = gain.shape
    both = jnp.concatenate((gain, bias), axis=1).reshape(1, -1)
    count = lax.axis_size("clip") * lax.axis_size("seq") * lax.axis_size("head")
    width = round_up(both.shape[1], 128)
    padded = jnp.pad(both, ((0, 0), (0, width - both.shape[1])))
    every = lax.all_to_all(
        jnp.broadcast_to(padded, (count, width)), ALL, split_axis=0, concat_axis=0, tiled=True
    )[:, : both.shape[1]]
    return every.reshape(count, layers * 2 * norms, part).transpose(1, 0, 2).reshape(layers, 2 * norms, -1)


def reduce_norms(sums):
    count = lax.axis_size("clip") * lax.axis_size("seq") * lax.axis_size("head")
    rows, features = sums.shape
    part = features // count
    a = sums.reshape(rows, count, part).transpose(1, 0, 2).reshape(count, rows * part)
    width = round_up(rows * part, 128)
    a = jnp.pad(a, ((0, 0), (0, width - rows * part)))
    every = lax.all_to_all(a, ALL, split_axis=0, concat_axis=0, tiled=True)
    return jnp.sum(every, axis=0)[: rows * part].reshape(rows, part)


def on_device(
    tokens,
    cotangent,
    time_qkv,
    time_out,
    time_mix,
    space_qkv,
    space_out,
    mlp_in,
    mlp_out,
    norm_gain,
    norm_bias,
):
    layers = time_qkv.shape[0]
    clips, frames, places, d = tokens.shape
    ways = lax.axis_size("seq")
    shards = lax.axis_size("clip") * ways
    rows = Rows(clips * frames, places, ways)
    shares = lax.axis_size("head")

    def as_rows(a):
        a = a.astype(F32).reshape(rows.frames, places, d)
        a = jnp.pad(a, ((0, 0), (0, rows.frame_rows - places), (0, 0)))
        return a.reshape(rows.rows, d)

    def from_rows(a):
        a = a.reshape(rows.frames, rows.frame_rows, d)[:, :places]
        return a.reshape(tokens.shape)

    gbs = gather_norms(norm_gain, norm_bias)
    gb = [gbs[l] for l in range(layers)]
    packs = [
        pack_time(time_qkv[l], time_out[l], time_mix[l])
        for l in range(layers)
    ]
    packs_ff = [pack_rest(space_qkv[l], space_out[l], mlp_in[l], mlp_out[l]) for l in range(layers)]
    quick = lax.axis_size("clip") == 4 and shares == 2 and ways == 4 and time_qkv.shape[1] % 16 == 0

    halves = Halves(lax.axis_size("clip"), d, time_qkv.shape[3])
    clip = lax.axis_index("clip")
    member = member_of(clip, lax.axis_index("seq"))
    me = jnp.stack((clip & 1, (clip >> 1) & 1, lax.axis_index("head"), member, lax.axis_index("seq"))).astype(
        jnp.int32
    )
    if quick:
        spreads = [Spread(pack, me) for pack in packs_ff]
        weights_ff = []
    else:
        weights_ff = [gather_slabs(along_seq(pack)) for pack in packs_ff]

    home = go_home(tokens)
    if quick:
        first = spreads[0]
        gb, home, packs = lax.optimization_barrier((gb, home, packs))
    part = along_seq(jnp.concatenate(packs, axis=0))
    if quick:
        part = first.step(part)
    weights = [gather_slabs(a) for a in jnp.split(part, layers, axis=0)]
    x = as_rows(home)
    send = swap_places(send_first(rows, x, gb[0], me))
    mixes = [mix_whole(w[-1], shards) for w in weights]
    kept = []
    for l in range(layers):
        w = weights[l]
        if l:
            send = swap_places(send)
        if quick and l == 0:
            for _ in range(2):
                send = first.step(send)
            for spread in spreads[1:]:
                send = spread.step(send)
            send = first.step(send)
            for spread in spreads[1:]:
                send = spread.hold(send)
        a1, qkv1, log1, o1_time = time_forward(rows, send, w)
        back = swap_places(o1_time)
        if quick:
            for _ in range(2 if l else 1):
                back = spreads[l].step(back)
            if l == 0:
                for spread in spreads[1:]:
                    back = spread.step(back)
            weights_ff.append(spreads[l].come)
        o1, y1, x1, qkv2 = middle_forward(rows, back, x, w, weights_ff[l], mixes[l], gb[l], me)
        o2, x2, log2 = space_forward(rows, qkv2, x1, weights_ff[l])
        if quick and l == 0:
            for spread in spreads[1:]:
                x2 = spread.step(x2)
        kept.append((x, a1, qkv1, log1, o1, y1, x1, qkv2, o2, log2, x2))
        if l + 1 < layers:
            x, *send = mlp_forward(rows, x2, weights_ff[l], gb[l], gb[l + 1], me)

    grad = as_rows(go_home(cotangent))
    norm_rows = [None] * layers
    summed = [None] * layers
    late = []
    for l in reversed(range(layers)):
        w = weights[l]
        x, a1, qkv1, log1, o1, y1, x1, qkv2, o2, log2, x2 = kept[l]
        grad, g_ff, s3, x3 = mlp_backward(
            rows, grad, x2, weights_ff[l], gb[l], me, halves, l + 1 == layers
        )
        if x3:
            output = go_back(from_rows(x3[0].astype(BF16)))
        if quick:
            ff = pieces_of(g_ff)
            if late:
                grad = settle(grad, late)
                grad = move(grad, late, me)
                late = [p for p in late if p.step < 3]
        grad, g_space, s2 = space_backward(
            rows, grad, x1, qkv2, o2, log2, weights_ff[l], gb[l], me, halves
        )
        if quick:
            space = pieces_of([g_space])
            if late:
                grad = settle(grad, late)
            grad, output = move((grad, output), ff, me)
        do1, g_out = middle_backward(rows, grad, y1, o1, w, mixes[l], me, halves, shards)
        do1 = swap_places(do1)
        if quick:
            do1 = move(do1, ff + space + late, me)
        da1, g_time = time_backward(rows, do1, a1, qkv1, log1, w, me, halves)
        if quick:
            da1 = settle(da1, ff + space)
        da1 = swap_places(da1)
        if quick:
            rest = pieces_of([g_out] + g_time)
            da1 = move(da1, ff + space + rest, me)
            late = space + rest
        grad, s1 = first_norm_back(rows, da1, x, grad, gb[l], me)
        norm_rows[l] = jnp.concatenate((s1[0:1], s2[0:1], s3[0:1], s1[1:2], s2[1:2], s3[1:2]), axis=0)
        if quick:
            summed[l] = ff + space + rest
        else:
            summed[l] = [reduce_plain(g_ff + [g_space, g_out] + g_time, clip & 1)]
    if quick:
        tokens_grad = move(go_back(from_rows(grad.astype(BF16))), late, me)
        move((), rest, me, True)
        summed = [[p.result for p in some] for some in summed]
    cuts = (2 * g_ff[0][0].shape[0], g_space[0].shape[0], g_out[0].shape[0], len(g_time))
    results = []
    for some in summed:
        slabs_of = jnp.concatenate(some, axis=0)
        ends = [sum(cuts[: i + 1]) for i in range(4)]
        results.append([slabs_of[e - c : e] for c, e in zip(cuts, ends)])
    if not quick:
        tokens_grad = go_back(from_rows(grad.astype(BF16)))
    tokens_grad = tokens_grad.astype(F32)
    norm_sums = reduce_norms(jnp.concatenate(norm_rows, axis=0)).reshape(layers, 2, 3, -1)

    def stacked(form):
        return jnp.stack([form(*results[l]) for l in range(layers)])

    def rows_of(a):
        return a.transpose(1, 0, 2)

    def flat(a):
        return rows_of(a).reshape(a.shape[1], -1)

    def mix_rows(a):
        r, width = a.shape
        return a.reshape(shares, r // shares, width).transpose(1, 0, 2).reshape(r // shares, -1)

    per_share = mlp_in.shape[2] // time_qkv.shape[3]
    return (
        output,
        tokens_grad,
        stacked(lambda ff, s, t, q: rows_of(q)),
        stacked(lambda ff, s, t, q: t[0].T),
        stacked(lambda ff, s, t, q: mix_rows(t[1])),
        stacked(lambda ff, s, t, q: rows_of(s[1:])),
        stacked(lambda ff, s, t, q: s[0].T),
        stacked(lambda ff, s, t, q: flat(ff[:per_share])),
        stacked(lambda ff, s, t, q: flat(ff[per_share:]).T),
        norm_sums[:, 0],
        norm_sums[:, 1],
    )


def solution(mesh):
    token_spec = P(("clip", "head"), "seq", None, None)
    in_specs = (
        token_spec,
        token_spec,
        P(None, ("clip", "seq"), None, "head"),
        P(None, "head", ("clip", "seq")),
        P(None, ("clip", "seq", "head"), None),
        P(None, ("clip", "seq"), None, "head"),
        P(None, "head", ("clip", "seq")),
        P(None, ("clip", "seq"), "head"),
        P(None, "head", ("clip", "seq")),
        P(None, None, ("clip", "seq", "head")),
        P(None, None, ("clip", "seq", "head")),
    )
    return jax.shard_map(
        on_device, mesh=mesh, in_specs=in_specs, out_specs=in_specs, check_vma=False
    )
```

```python
import functools
import math

import jax
import jax.numpy as jnp
from jax import lax
from jax.experimental import pallas as pl
from jax.experimental.pallas import tpu as pltpu
from jax.sharding import PartitionSpec as P

HEAD_DIM = 64
NORM_EPS = 1e-06
HALF_ROOT = 0.7071067811865476
INV_ROOT_TAU = 0.3989422804014327
LOG2E = 1.4426950408889634
FAR = -1e30
LANES = 128
VMEM = 56 * 1024 * 1024
SHOWN = 1.0
ALL = ("clip", "seq", "head")
BF16 = jnp.bfloat16
F32 = jnp.float32


def round_up(value, step):
    return -(-value // step) * step


def nn(a, b):
    return lax.dot_general(a, b, (((1,), (0,)), ((), ())), preferred_element_type=F32)


def nt(a, b):
    return lax.dot_general(a, b, (((1,), (1,)), ((), ())), preferred_element_type=F32)


def tn(a, b):
    return lax.dot_general(a, b, (((0,), (0,)), ((), ())), preferred_element_type=F32)


def norm_parts(x):
    mean = jnp.mean(x, axis=-1, keepdims=True)
    centred = x - mean
    spread = lax.rsqrt(jnp.mean(centred * centred, axis=-1, keepdims=True) + NORM_EPS)
    return centred * spread, spread


def norm_rounded(x, gain, bias):
    hat, _ = norm_parts(x)
    return (hat * gain + bias).astype(BF16)


def norm_back(u, x, gain):
    hat, spread = norm_parts(x)
    scaled = u * gain
    mean_scaled = jnp.mean(scaled, axis=-1, keepdims=True)
    mean_cross = jnp.mean(scaled * hat, axis=-1, keepdims=True)
    change = spread * (scaled - mean_scaled - hat * mean_cross)
    sums = jnp.concatenate(
        (jnp.sum(u * hat, axis=0, keepdims=True), jnp.sum(u, axis=0, keepdims=True)), axis=0
    )
    return change, sums


class Rows:
    def __init__(self, frames, places, ways):
        self.frames = frames
        self.places = places
        self.ways = ways
        self.frame_rows = round_up(places, 16)
        self.rows = frames * self.frame_rows
        self.block = places // ways
        self.chunk = round_up(frames * self.block, 8)
        self.time_rows = ways * self.chunk

    def split(self, r):
        way = jnp.zeros_like(r)
        for k in range(1, self.ways):
            way = way + (r >= k * self.chunk).astype(jnp.int32)
        rest = r - way * self.chunk
        frame = jnp.zeros_like(r)
        for k in range(1, self.frames):
            frame = frame + (rest >= k * self.block).astype(jnp.int32)
        real = rest < self.frames * self.block
        return way, frame, rest - frame * self.block, real

    def to_time(self, k, member):
        r = lax.broadcasted_iota(jnp.int32, (self.chunk, 1), 0)
        _, frame, place, real = self.split(r)
        way = jnp.bitwise_xor(member, k)
        source = jnp.where(real, frame * self.frame_rows + way * self.block + place, -1)
        c = lax.broadcasted_iota(jnp.int32, (self.chunk, self.rows), 1)
        return jnp.where(c == source, 1.0, 0.0).astype(BF16)

    def gathered(self, chunk_refs, member):
        total = tn(self.to_time(0, member), chunk_refs[0][...])
        for k in range(1, self.ways):
            total = total + tn(self.to_time(k, member), chunk_refs[k][...])
        return total

    def chunks(self, width, block=None, index=None):
        return [
            made((self.chunk, width), BF16)
            if block is None
            else made((self.chunk, width), BF16, (self.chunk, block), index)
            for _ in range(self.ways)
        ]

    def time_bias(self):
        def label(r):
            _, _, place, real = self.split(r)
            return jnp.where(real, place, -1)

        a = label(lax.broadcasted_iota(jnp.int32, (self.time_rows, 1), 0))
        b = label(lax.broadcasted_iota(jnp.int32, (1, self.time_rows), 1))
        return jnp.where(a == b, 0.0, FAR).astype(F32)

    def space_bias(self):
        a = lax.broadcasted_iota(jnp.int32, (self.frame_rows, 1), 0)
        return jnp.where(a < self.places, 0.0, FAR).astype(F32)


def lane_masks(rows):
    lane = lax.broadcasted_iota(jnp.int32, (rows, LANES), 1)
    return lane < HEAD_DIM


def one_of(value, low, half):
    zero = jnp.zeros_like(value)
    return jnp.where(low, value, zero) if half == 0 else jnp.where(low, zero, value)


def pair_forward(q, k, v, bias, rate):
    low = lane_masks(q.shape[0])
    mixed, logs = [], []
    for half in range(2):
        s = nt(k, one_of(q, low, half)) + bias
        peak = jnp.max(s, axis=0, keepdims=True)
        e = jnp.exp2((s - peak) * rate)
        total = jnp.sum(e, axis=0, keepdims=True)
        soft = (e * (1.0 / total)).astype(BF16)
        mixed.append(tn(soft, v))
        logs.append(peak * rate + jnp.log2(total))
    return jnp.where(low, mixed[0], mixed[1]).astype(BF16), logs


def pair_backward(q, k, v, do, logs, bias, rate, scale):
    low = lane_masks(q.shape[0])
    dq, dk, dv = [], [], []
    for half in range(2):
        s = nt(k, one_of(q, low, half)) + bias
        soft = jnp.exp2(s * rate - logs[half])
        dp = nt(v, one_of(do, low, half))
        ds = (soft * (dp - jnp.sum(soft * dp, axis=0, keepdims=True))).astype(BF16)
        dv.append(nn(soft.astype(BF16), do))
        dk.append(nn(ds, q))
        dq.append(tn(ds, k))
    return (
        (jnp.where(low, dq[0], dq[1]) * scale).astype(BF16),
        (jnp.where(low, dk[0], dk[1]) * scale).astype(BF16),
        jnp.where(low, dv[0], dv[1]).astype(BF16),
    )


def split_rows(value, keep_ref, send_ref, at, room_ref, me_ref):
    mine = me_ref[0]
    room_ref[...] = value.reshape(room_ref.shape)
    keep_ref[at] = room_ref[:, mine].astype(BF16)
    send_ref[at] = room_ref[:, 1 - mine].astype(BF16)


class Halves:
    def __init__(self, clips, depth, width):
        self.pairs = clips // 2
        self.rows = depth // clips
        self.width = width

    def array(self, lead, block, index):
        tail = (self.pairs, self.rows, self.width)
        one = lambda: made(lead + tail, BF16, block + tail, lambda *g: index(*g) + (0, 0, 0))
        return [one(), one()]

    def room(self):
        return pltpu.VMEM((self.pairs, 2, self.rows, self.width), F32)


SCALARS = pl.BlockSpec(memory_space=pltpu.SMEM)


def call(body, grid, ins, outs, scratch, args, flops=0):
    specs = [spec for spec in ins]
    moved = sum(math.prod(o.shape) * o.dtype.itemsize for o, _ in outs)
    moved += sum(math.prod(a.shape) * a.dtype.itemsize for a in args)
    return pl.pallas_call(
        body,
        out_shape=[shape for shape, _ in outs],
        grid=grid,
        in_specs=specs,
        out_specs=[spec for _, spec in outs],
        scratch_shapes=scratch,
        compiler_params=pltpu.CompilerParams(vmem_limit_bytes=VMEM),
        cost_estimate=pl.CostEstimate(
            flops=int(flops * SHOWN), bytes_accessed=int(moved * SHOWN), transcendentals=0
        ),
    )(*args)


def whole(shape):
    zeros = (0,) * len(shape)
    return pl.BlockSpec(shape, lambda *_: zeros)


def made(shape, dtype, block=None, index=None):
    spec = whole(shape) if block is None else pl.BlockSpec(block, index)
    return jax.ShapeDtypeStruct(shape, dtype), spec


def slabs(count, first, width, depth):
    return pl.BlockSpec((count, 1, depth, width), lambda h, *_: (first // count, h, 0, 0))


def send_first(rows, x, gb, me):
    def body(me_ref, x_ref, gb_ref, *out_refs):
        a = norm_rounded(x_ref[...], gb_ref[0:1], gb_ref[3:4])
        for k in range(rows.ways):
            out_refs[k][...] = nn(rows.to_time(k, me_ref[3]), a).astype(BF16)

    d = x.shape[1]
    return call(
        body, (1,), [SCALARS, whole(x.shape), whole(gb.shape)], rows.chunks(d), [], (me, x, gb)
    )


def time_forward(rows, chunks, w):
    t, d = rows.time_rows, chunks[0].shape[1]
    width = w.shape[3]
    shares = w.shape[1]
    pairs = width // LANES
    ways = rows.ways
    rate = LOG2E / math.sqrt(HEAD_DIM)

    def body(*refs):
        chunk_refs = refs[:ways]
        w_ref, a_ref, qkv_ref, log_ref = refs[ways : ways + 4]
        out_refs = refs[ways + 4 : 2 * ways + 4]
        bias_ref, mixed_ref = refs[2 * ways + 4 :]

        @pl.when(pl.program_id(0) == 0)
        def _():
            bias_ref[...] = rows.time_bias()
            for k in range(ways):
                a_ref[k * rows.chunk : (k + 1) * rows.chunk] = chunk_refs[k][...]

        act = a_ref[...]
        for g in range(3):
            qkv_ref[g] = nn(act, w_ref[g, 0]).astype(BF16)

        @pl.loop(0, pairs)
        def _(i):
            lanes = pl.ds(pl.multiple_of(i * LANES, LANES), LANES)
            mixed, logs = pair_forward(
                qkv_ref[0, :, lanes], qkv_ref[1, :, lanes], qkv_ref[2, :, lanes], bias_ref[...], rate
            )
            mixed_ref[:, lanes] = mixed
            log_ref[0, i] = jnp.concatenate(logs, axis=0)

        for k in range(ways):
            out_refs[k][...] = mixed_ref[k * rows.chunk : (k + 1) * rows.chunk]

    got = call(
        body,
        (shares,),
        [whole(c.shape) for c in chunks] + [slabs(3, 0, width, d)],
        [
            made((t, d), BF16),
            made((3, t, d), BF16, (3, t, width), lambda h: (0, 0, h)),
            made((shares, pairs, 2, t), F32, (1, pairs, 2, t), lambda h: (h, 0, 0, 0)),
            *rows.chunks(d, width, lambda h: (0, h)),
        ],
        [pltpu.VMEM((t, t), F32), pltpu.VMEM((t, width), BF16)],
        (*chunks, w),
        flops=2 * t * d * 3 * d,
    )
    return got[0], got[1], got[2], got[3:]


def middle_forward(rows, back, x, w, mix, gb, me):
    t, d = x.shape
    width = w.shape[3]
    shares = w.shape[1]

    def body(me_ref, *refs):
        x_ref, to_ref, sq_ref, mix_ref, gb_ref, o1_ref, y1_ref, x1_ref, qkv_ref = refs[rows.ways :]
        o1 = rows.gathered(refs[: rows.ways], me_ref[3]).astype(BF16)
        o1_ref[...] = o1
        y1 = jnp.zeros((t, d), F32)
        for h in range(shares):
            y1 = y1 + nt(o1[:, h * width : (h + 1) * width], to_ref[0, h])
        y1 = y1.astype(BF16)
        y1_ref[...] = y1
        x1 = x_ref[...] + nn(y1, mix_ref[...])
        x1_ref[...] = x1
        a2 = norm_rounded(x1, gb_ref[1:2], gb_ref[4:5])
        for g in range(3):
            for h in range(shares):
                qkv_ref[g, :, h * width : (h + 1) * width] = nn(a2, sq_ref[g, h]).astype(BF16)

    return call(
        body,
        (1,),
        [
            SCALARS,
            *(whole(c.shape) for c in back),
            whole(x.shape),
            pl.BlockSpec((1, shares, d, width), lambda i: (6, 0, 0, 0)),
            pl.BlockSpec((3, shares, d, width), lambda i: (1, 0, 0, 0)),
            whole(mix.shape),
            whole(gb.shape),
        ],
        [made((t, d), BF16), made((t, d), BF16), made((t, d), F32), made((3, t, d), BF16)],
        [],
        (me, *back, x, w, w, mix, gb),
        flops=2 * t * d * 5 * d,
    )


def space_forward(rows, qkv, x1, w):
    t, d = x1.shape
    width = w.shape[3]
    shares = w.shape[1]
    pairs = width // LANES
    rate = LOG2E / math.sqrt(HEAD_DIM)
    n = rows.frame_rows

    def body(qkv_ref, x1_ref, w_ref, o2_ref, x2_ref, log_ref):
        bias = rows.space_bias()

        @pl.loop(0, pairs)
        def _(i):
            lanes = pl.ds(pl.multiple_of(i * LANES, LANES), LANES)
            for f in range(rows.frames):
                at = slice(f * n, (f + 1) * n)
                mixed, logs = pair_forward(
                    qkv_ref[0, at, lanes], qkv_ref[1, at, lanes], qkv_ref[2, at, lanes], bias, rate
                )
                o2_ref[at, lanes] = mixed
                log_ref[0, i, f] = jnp.concatenate(logs, axis=0)

        @pl.when(pl.program_id(0) == 0)
        def _():
            x2_ref[...] = x1_ref[...]

        x2_ref[...] += nt(o2_ref[...], w_ref[0, 0])

    return call(
        body,
        (shares,),
        [
            pl.BlockSpec((3, t, width), lambda h: (0, 0, h)),
            whole(x1.shape),
            slabs(1, 7, width, d),
        ],
        [
            made((t, d), BF16, (t, width), lambda h: (0, h)),
            made((t, d), F32),
            made(
                (shares, pairs, rows.frames, 2, n),
                F32,
                (1, pairs, rows.frames, 2, n),
                lambda h: (h, 0, 0, 0, 0),
            ),
        ],
        [],
        (qkv, x1, w),
        flops=2 * t * d * d,
    )


def ff_slab(first, per_share, depth, width):
    return pl.BlockSpec(
        (1, 1, depth, width), lambda j: (first + j % per_share, j // per_share, 0, 0)
    )


def mlp_forward(rows, x2, w, gb, gb_next, me):
    t, d = x2.shape
    width = w.shape[3]
    shares = w.shape[1]
    per_share = w.shape[0] // 2
    steps = shares * per_share

    def body(x2_ref, wi_ref, wo_ref, gb_ref, me_ref, gn_ref, x3_ref, *rest):
        send_refs, a3_ref = rest[:-1], rest[-1]
        j = pl.program_id(0)

        @pl.when(j == 0)
        def _():
            a3_ref[...] = norm_rounded(x2_ref[...], gb_ref[2:3], gb_ref[5:6])
            x3_ref[...] = x2_ref[...]

        hid = nn(a3_ref[...], wi_ref[0, 0])
        act = (0.5 * hid * (1.0 + lax.erf(hid * HALF_ROOT))).astype(BF16)
        x3_ref[...] += nt(act, wo_ref[0, 0])

        @pl.when(j == steps - 1)
        def _():
            a = norm_rounded(x3_ref[...], gn_ref[0:1], gn_ref[3:4])
            for k in range(rows.ways):
                send_refs[k][...] = nn(rows.to_time(k, me_ref[3]), a).astype(BF16)

    ins = [
        whole(x2.shape),
        ff_slab(0, per_share, d, width),
        ff_slab(per_share, per_share, d, width),
        whole(gb.shape),
    ]
    ins += [SCALARS, whole(gb_next.shape)]
    outs = [made((t, d), F32)] + rows.chunks(d)
    args = (x2, w, w, gb, me, gb_next)
    return call(
        body, (steps,), ins, outs, [pltpu.VMEM((t, d), BF16)], args, flops=4 * t * d * width * steps
    )


def mlp_backward(rows, grad, x2, w, gb, me, halves, with_output):
    t, d = x2.shape
    width = w.shape[3]
    shares = w.shape[1]
    per_share = w.shape[0] // 2
    steps = shares * per_share

    def body(me_ref, g_ref, x2_ref, wi_ref, wo_ref, gb_ref, go_ref, ki_ref, si_ref, ko_ref, so_ref, sums_ref, *rest):
        if with_output:
            x3_ref, *rest = rest
        a3_ref, a3t_ref, e3_ref, e3t_ref, u_ref, room_ref = rest
        j = pl.program_id(0)

        @pl.when(j == 0)
        def _():
            hat, _ = norm_parts(x2_ref[...])
            a3 = hat * gb_ref[2:3] + gb_ref[5:6]
            a3_ref[...] = a3.astype(BF16)
            a3t_ref[...] = a3.T.astype(BF16)
            g = g_ref[...]
            e3_ref[...] = g.astype(BF16)
            e3t_ref[...] = g.T.astype(BF16)
            u_ref[...] = jnp.zeros((t, d), F32)
            if with_output:
                x3_ref[...] = x2_ref[...]

        hid = nn(a3_ref[...], wi_ref[0, 0])
        phi = 0.5 * (1.0 + lax.erf(hid * HALF_ROOT))
        act = (hid * phi).astype(BF16)
        slope = phi + hid * jnp.exp(-0.5 * hid * hid) * INV_ROOT_TAU
        dhid = (nn(e3_ref[...], wo_ref[0, 0]) * slope).astype(BF16)
        split_rows(nn(e3t_ref[...], act), ko_ref, so_ref, (0, 0), room_ref, me_ref)
        split_rows(nn(a3t_ref[...], dhid), ki_ref, si_ref, (0, 0), room_ref, me_ref)
        u_ref[...] += nt(dhid, wi_ref[0, 0])
        if with_output:
            x3_ref[...] += nt(act, wo_ref[0, 0])

        @pl.when(j == steps - 1)
        def _():
            change, sums = norm_back(u_ref[...], x2_ref[...], gb_ref[2:3])
            go_ref[...] = g_ref[...] + change
            sums_ref[...] = sums

    slab_outs = [
        one
        for _ in range(2)
        for one in halves.array(
            (per_share, shares), (1, 1), lambda j: (j % per_share, j // per_share)
        )
    ]
    grad, ki, si, ko, so, sums, *x3 = call(
        body,
        (steps,),
        [
            SCALARS,
            whole(grad.shape),
            whole(x2.shape),
            ff_slab(0, per_share, d, width),
            ff_slab(per_share, per_share, d, width),
            whole(gb.shape),
        ],
        [made((t, d), F32), *slab_outs, made((2, d), F32)] + [made((t, d), F32)] * with_output,
        [
            pltpu.VMEM((t, d), BF16),
            pltpu.VMEM((d, t), BF16),
            pltpu.VMEM((t, d), BF16),
            pltpu.VMEM((d, t), BF16),
            pltpu.VMEM((t, d), F32),
            halves.room(),
        ],
        (me, grad, x2, w, w, gb),
        flops=10 * t * d * width * steps,
    )
    return grad, [(ki, si), (ko, so)], sums, x3


def space_backward(rows, grad, x1, qkv, o2, logs, w, gb, me, halves):
    t, d = x1.shape
    width = w.shape[3]
    shares = w.shape[1]
    pairs = width // LANES
    scale = 1.0 / math.sqrt(HEAD_DIM)
    rate = LOG2E * scale
    n = rows.frame_rows

    def body(me_ref, g_ref, x1_ref, qkv_ref, o2_ref, log_ref, wo_ref, wq_ref, gb_ref, go_ref, keep_ref, send_ref, sums_ref, e2_ref, e2t_ref, a2t_ref, do_ref, dqkv_ref, u_ref, room_ref):
        h = pl.program_id(0)

        @pl.when(h == 0)
        def _():
            g = g_ref[...]
            e2_ref[...] = g.astype(BF16)
            e2t_ref[...] = g.T.astype(BF16)
            hat, _ = norm_parts(x1_ref[...])
            a2t_ref[...] = (hat * gb_ref[1:2] + gb_ref[4:5]).T.astype(BF16)
            u_ref[...] = jnp.zeros((t, d), F32)

        bias = rows.space_bias()
        split_rows(nn(e2t_ref[...], o2_ref[...]), keep_ref, send_ref, (0, 0), room_ref, me_ref)
        do_ref[...] = nn(e2_ref[...], wo_ref[0, 0]).astype(BF16)

        @pl.loop(0, pairs)
        def _(i):
            lanes = pl.ds(pl.multiple_of(i * LANES, LANES), LANES)
            for f in range(rows.frames):
                at = slice(f * n, (f + 1) * n)
                log = log_ref[0, i, f]
                grads = pair_backward(
                    qkv_ref[0, at, lanes],
                    qkv_ref[1, at, lanes],
                    qkv_ref[2, at, lanes],
                    do_ref[at, lanes],
                    (log[0:1], log[1:2]),
                    bias,
                    rate,
                    scale,
                )
                for part in range(3):
                    dqkv_ref[part, at, lanes] = grads[part]

        for part in range(3):
            split_rows(
                nn(a2t_ref[...], dqkv_ref[part]), keep_ref, send_ref, (part + 1, 0), room_ref, me_ref
            )
            u_ref[...] += nt(dqkv_ref[part], wq_ref[part, 0])

        @pl.when(h == shares - 1)
        def _():
            change, sums = norm_back(u_ref[...], x1_ref[...], gb_ref[1:2])
            go_ref[...] = g_ref[...] + change
            sums_ref[...] = sums

    grad, keep, send, sums = call(
        body,
        (shares,),
        [
            SCALARS,
            whole(grad.shape),
            whole(x1.shape),
            pl.BlockSpec((3, t, width), lambda h: (0, 0, h)),
            pl.BlockSpec((t, width), lambda h: (0, h)),
            pl.BlockSpec((1,) + logs.shape[1:], lambda h: (h, 0, 0, 0, 0)),
            slabs(1, 7, width, d),
            slabs(3, 3, width, d),
            whole(gb.shape),
        ],
        [
            made((t, d), F32),
            *halves.array((4, shares), (4, 1), lambda h: (0, h)),
            made((2, d), F32),
        ],
        [
            pltpu.VMEM((t, d), BF16),
            pltpu.VMEM((d, t), BF16),
            pltpu.VMEM((d, t), BF16),
            pltpu.VMEM((t, width), BF16),
            pltpu.VMEM((3, t, width), BF16),
            pltpu.VMEM((t, d), F32),
            halves.room(),
        ],
        (me, grad, x1, qkv, o2, logs, w, w, gb),
        flops=2 * t * d * d * 8,
    )
    return grad, (keep, send), sums


def mix_fits(depth, shards, shares):
    return depth // (shards * shares) % 8 == 0


def middle_backward(rows, grad, y1, o1, w, mix, me, halves, shards):
    t, d = grad.shape
    width = w.shape[3]
    shares = w.shape[1]
    fits = mix_fits(d, shards, shares)
    part = d // (shards * shares)

    def body(me_ref, g_ref, y1_ref, o1_ref, to_ref, mix_ref, *rest):
        send_refs, rest = rest[: rows.ways], rest[rows.ways :]
        gk_ref, gs_ref, *rest = rest
        if fits:
            room_ref, order_ref = rest
        else:
            gm_ref, room_ref = rest
        e1 = g_ref[...].astype(BF16)
        dy1 = nt(e1, mix_ref[...]).astype(BF16)
        sends = [rows.to_time(k, me_ref[3]) for k in range(rows.ways)]
        for h in range(shares):
            lanes = slice(h * width, (h + 1) * width)
            do1 = nn(dy1, to_ref[0, h]).astype(BF16)
            for k in range(rows.ways):
                send_refs[k][:, lanes] = nn(sends[k], do1).astype(BF16)
            split_rows(tn(dy1, o1_ref[:, lanes]), gk_ref, gs_ref, (0, h), room_ref, me_ref)
        gm = tn(y1_ref[...], e1)
        if fits:
            gm = gm.reshape(shards, shares, part, d)
            for h in range(shares):
                for half in range(shares):
                    order_ref[:, half] = gm[:, h, :, half * width : (half + 1) * width]
                split_rows(order_ref[...], gk_ref, gs_ref, (1, h), room_ref, me_ref)
        else:
            gm_ref[...] = gm.astype(BF16)

    outs = rows.chunks(d)
    outs += halves.array((1 + fits, shares), (1 + fits, shares), lambda i: (0, 0))
    scratch = [halves.room()]
    if fits:
        scratch.append(pltpu.VMEM((shards, shares, part, width), F32))
    else:
        outs.append(made((d, d), BF16))
    got = call(
        body,
        (1,),
        [
            SCALARS,
            whole(grad.shape),
            whole(y1.shape),
            whole(o1.shape),
            pl.BlockSpec((1, shares, d, width), lambda i: (6, 0, 0, 0)),
            whole(mix.shape),
        ],
        outs,
        scratch,
        (me, grad, y1, o1, w, mix),
        flops=8 * t * d * d,
    )
    do1, (keep, send) = got[: rows.ways], got[rows.ways : rows.ways + 2]
    if not fits:
        gm = mix_slab(got[-1], shards, shares).reshape((1, shares, halves.pairs, 2) + keep.shape[3:])
        keep = jnp.concatenate((keep, lax.dynamic_index_in_dim(gm, me[0], 3, keepdims=False)), axis=0)
        send = jnp.concatenate((send, lax.dynamic_index_in_dim(gm, 1 - me[0], 3, keepdims=False)), axis=0)
    return do1, (keep, send)


def time_backward(rows, do1, a, qkv, logs, w, me, halves):
    t, d = a.shape
    width = w.shape[3]
    shares = w.shape[1]
    pairs = width // LANES
    scale = 1.0 / math.sqrt(HEAD_DIM)
    rate = LOG2E * scale

    def body(me_ref, *refs):
        do_refs, refs = refs[: rows.ways], refs[rows.ways :]
        a_ref, qkv_ref, log_ref, w_ref = refs[:4]
        out_refs, refs = refs[4 : 4 + rows.ways], refs[4 + rows.ways :]
        half_refs, refs = refs[:6], refs[6:]
        bias_ref, dqkv_ref, at_ref, u_ref, room_ref, do_ref = refs
        h = pl.program_id(0)

        @pl.when(h == 0)
        def _():
            bias_ref[...] = rows.time_bias()
            at_ref[...] = a_ref[...].T
            u_ref[...] = jnp.zeros((t, d), F32)

        for k in range(rows.ways):
            do_ref[k * rows.chunk : (k + 1) * rows.chunk] = do_refs[k][...]

        @pl.loop(0, pairs)
        def _(i):
            lanes = pl.ds(pl.multiple_of(i * LANES, LANES), LANES)
            log = log_ref[0, i]
            grads = pair_backward(
                qkv_ref[0, :, lanes],
                qkv_ref[1, :, lanes],
                qkv_ref[2, :, lanes],
                do_ref[:, lanes],
                (log[0:1], log[1:2]),
                bias_ref[...],
                rate,
                scale,
            )
            for part in range(3):
                dqkv_ref[part, :, lanes] = grads[part]

        for part in range(3):
            value = nn(at_ref[...], dqkv_ref[part])
            split_rows(value, half_refs[2 * part], half_refs[2 * part + 1], (0, 0), room_ref, me_ref)
            u_ref[...] += nt(dqkv_ref[part], w_ref[part, 0])

        @pl.when(h == shares - 1)
        def _():
            for k in range(rows.ways):
                out_refs[k][...] = u_ref[k * rows.chunk : (k + 1) * rows.chunk].astype(BF16)

    got = call(
        body,
        (shares,),
        [
            SCALARS,
            *(pl.BlockSpec((rows.chunk, width), lambda h: (0, h)) for _ in do1),
            whole(a.shape),
            pl.BlockSpec((3, t, width), lambda h: (0, 0, h)),
            pl.BlockSpec((1,) + logs.shape[1:], lambda h: (h, 0, 0, 0)),
            slabs(3, 0, width, d),
        ],
        [
            *rows.chunks(d),
            *(one for _ in range(3) for one in halves.array((1, shares), (1, 1), lambda h: (0, h))),
        ],
        [
            pltpu.VMEM((t, t), F32),
            pltpu.VMEM((3, t, width), BF16),
            pltpu.VMEM((d, t), BF16),
            pltpu.VMEM((t, d), F32),
            halves.room(),
            pltpu.VMEM((t, width), BF16),
        ],
        (me, *do1, a, qkv, logs, w),
        flops=2 * t * d * d * 6,
    )
    parts = got[rows.ways :]
    return got[: rows.ways], [tuple(parts[i : i + 2]) for i in (0, 2, 4)]


def first_norm_back(rows, back, x, grad, gb, me):
    t, d = x.shape

    def body(me_ref, *refs):
        x_ref, g_ref, gb_ref, go_ref, sums_ref = refs[rows.ways :]
        u = rows.gathered(refs[: rows.ways], me_ref[3])
        change, sums = norm_back(u, x_ref[...], gb_ref[0:1])
        go_ref[...] = g_ref[...] + change
        sums_ref[...] = sums

    return call(
        body,
        (1,),
        [SCALARS, *(whole(c.shape) for c in back), whole(x.shape), whole(grad.shape), whole(gb.shape)],
        [made((t, d), F32), made((2, d), F32)],
        [],
        (me, *back, x, grad, gb),
    )


def homes():
    clips, ways = lax.axis_size("clip"), lax.axis_size("seq")
    pairs = []
    for clip in range(clips):
        for seq in range(ways):
            home_clip = clip - clip % 2 + seq % 2
            home_seq = seq // 2 + (ways // 2) * (clip % 2)
            pairs.append((clip * ways + seq, home_clip * ways + home_seq))
    return pairs


def go_home(a):
    return lax.ppermute(a, ("clip", "seq"), homes())


def go_back(a):
    return lax.ppermute(a, ("clip", "seq"), [(home, device) for device, home in homes()])


def member_of(clip, seq):
    return clip % 2 + 2 * (seq % (lax.axis_size("seq") // 2))


def swap_places(chunks):
    clips, ways = lax.axis_size("clip"), lax.axis_size("seq")
    got = [chunks[0]]
    for k in range(1, ways):
        pairs = []
        for clip in range(clips):
            for seq in range(ways):
                other = member_of(clip, seq) ^ k
                to_clip = clip - clip % 2 + other % 2
                to_seq = seq - seq % (ways // 2) + other // 2
                pairs.append((clip * ways + seq, to_clip * ways + to_seq))
        got.append(lax.ppermute(chunks[k], ("clip", "seq"), pairs))
    return got


def columns(a, r, width):
    return a.reshape(r, -1, width).transpose(1, 0, 2)


def pack_attention(time_qkv, time_out, time_mix, space_qkv, space_out):
    r, _, width = time_qkv.shape
    mix = time_mix.reshape(-1, time_mix.shape[1] // width, width).transpose(1, 0, 2).reshape(1, r, width)
    return jnp.concatenate(
        (
            columns(time_qkv, r, width),
            columns(space_qkv, r, width),
            time_out.T[None],
            space_out.T[None],
            mix,
        ),
        axis=0,
    )


def pack_feed_forward(mlp_in, mlp_out, width):
    r = mlp_in.shape[0]
    return jnp.concatenate((columns(mlp_in, r, width), columns(mlp_out.T, r, width)), axis=0)


def gather_slabs(pack):
    full = lax.all_gather(pack, ("head", "clip", "seq"), axis=1, tiled=True)
    return full.reshape(pack.shape[0], lax.axis_size("head"), -1, pack.shape[2])


def spread_steps(pack, me):
    ways, clips = lax.axis_size("seq"), lax.axis_size("clip")
    shares = lax.axis_size("head")
    n, r, width = pack.shape
    pack = yield pack
    turned = [pack] + [
        lax.ppermute(pack, "seq", [(i, (i + k) % ways) for i in range(ways)]) for k in range(1, ways)
    ]
    turned = yield turned
    orders = (((0, 1), "x", "h"), ((3, 2), "h", "x"))
    some = [jnp.stack([turned[k] for k in steps]) for steps, _, _ in orders]
    come = yield [cross(a, first) for a, (_, first, _) in zip(some, orders)]
    some = [jnp.concatenate(pair, axis=0) for pair in zip(some, come)]
    come = yield [cross(a, second) for a, (_, _, second) in zip(some, orders)]
    runs = []
    for mine, other, (steps, first, second) in zip(some, come, orders):
        where = [(k, {first: f}) for f in (0, 1) for k in steps]
        for g, blocks in enumerate((mine, other)):
            runs.append((blocks, [(k, {**at, second: g}) for k, at in where], 0))
    come = yield [cross(blocks, "c") for blocks, _, _ in runs]
    runs += [(far, where, 1) for far, (_, where, _) in zip(come, runs)]
    count = sum(len(where) for _, where, _ in runs)

    def body(me_ref, *refs):
        sources, out_ref, sems = refs[: len(runs)], refs[-2], refs[-1]
        copies = []
        for source, (_, where, core) in zip(sources, runs):
            for i, (k, at) in enumerate(where):
                share = jnp.bitwise_xor(me_ref[2], at["h"])
                clip = 2 * jnp.bitwise_xor(me_ref[1], at["x"]) + jnp.bitwise_xor(me_ref[0], core)
                seq = lax.rem(me_ref[4] + (ways - k), ways)
                copies.append(
                    pltpu.make_async_copy(
                        source.at[i], out_ref.at[:, share, clip * ways + seq], sems.at[len(copies)]
                    )
                )
        for copy in copies:
            copy.start()
        for copy in copies:
            copy.wait()

    full = pl.pallas_call(
        body,
        out_shape=jax.ShapeDtypeStruct((n, shares, clips * ways, r, width), BF16),
        in_specs=[SCALARS] + [pl.BlockSpec(memory_space=pltpu.HBM)] * len(runs),
        out_specs=pl.BlockSpec(memory_space=pltpu.VMEM),
        scratch_shapes=[pltpu.SemaphoreType.DMA((count,))],
        compiler_params=pltpu.CompilerParams(vmem_limit_bytes=VMEM),
        cost_estimate=pl.CostEstimate(
            flops=0, bytes_accessed=4 * n * shares * clips * ways * r * width, transcendentals=0
        ),
    )(me, *(blocks for blocks, _, _ in runs))
    yield full.reshape(n, shares, clips * ways * r, width)


class Spread:
    def __init__(self, pack, me):
        self.way = spread_steps(pack, me)
        self.come = next(self.way)

    def hold(self, x):
        x, self.come = lax.optimization_barrier((x, self.come))
        return x

    def step(self, x):
        x = self.hold(x)
        self.come = self.way.send(self.come)
        return x


def mix_whole(slab, shards):
    shares, depth, width = slab.shape
    part = slab.reshape(shares, shards, shares, depth // (shards * shares), width)
    return part.transpose(1, 0, 3, 2, 4).reshape(depth, shares * width)


def mix_slab(whole_grad, shards, shares):
    depth, full = whole_grad.shape
    width = full // shares
    part = whole_grad.reshape(shards, shares, depth // (shards * shares), shares, width)
    return part.transpose(1, 0, 3, 2, 4).reshape(1, shares, depth, width)


class Piece:
    def __init__(self, keep, got, first, n, order):
        self.near = (keep, got)
        self.first = first
        self.n = n
        self.order = order
        self.step = 0
        self.held = []
        self.result = None


PLACE = {"x": 1, "h": 2}


def fold(pieces, me, last_by_rows):
    ways = lax.axis_size("seq")
    depth, width = pieces[0].near[0].shape[-2:]
    r = depth // ways
    used = {}
    arrays = []

    def number(a):
        for i, known in enumerate(arrays):
            if known is a:
                return i
        arrays.append(a)
        return len(arrays) - 1

    plans = []
    for p in pieces:
        link = p.order[p.step] if p.step < 2 else "z"
        blocks = p.n * (2 if p.step == 0 else 1)
        base = used.get(link, 0)
        used[link] = base + blocks
        near = [number(a) for a in p.near]
        held = [(number(a), at) for a, at in p.held]
        plans.append((p, link, base, near, held))
    links = sorted(used)
    shapes = [
        (ways, used[k], r, width) if k == "z" and last_by_rows else (used[k], depth, width)
        for k in links
    ]
    rooms, counts = [], []
    for p, link, base, near, held in plans:
        each = 2 if p.step == 0 else 1
        counts.append((each, len(near) + len(held)))
        rooms += [(each * p.n, depth, width)] * (len(near) + len(held))
    copies_needed = sum(each * terms for each, terms in counts)

    def body(me_ref, *refs):
        sources = refs[: len(arrays)]
        outs = dict(zip(links, refs[len(arrays) : len(arrays) + len(links)]))
        held_refs = refs[len(arrays) + len(links) : -1]
        sems = refs[-1]
        mine = {name: me_ref[PLACE[name]] for name in PLACE}
        groups = []
        room = 0
        sem = 0
        for p, link, base, near, held in plans:
            group = []
            if p.step == 0:
                for term in near:
                    for k in range(2):
                        pick = {p.order[0]: 1 - mine[p.order[0]], p.order[1]: k}
                        source = sources[term].at[pl.ds(p.first, p.n), pick["h"], pick["x"]]
                        group.append((source, held_refs[room].at[pl.ds(k * p.n, p.n)]))
                    room += 1
            else:
                last = p.order[1]
                pick = {p.order[0]: mine[p.order[0]]}
                pick[last] = 1 - mine[last] if p.step == 1 else mine[last]
                for term in near:
                    source = sources[term].at[pl.ds(p.first, p.n), pick["h"], pick["x"]]
                    group.append((source, held_refs[room]))
                    room += 1
                for i, (term, at) in enumerate(held):
                    start = at + pick[last] * p.n if i == 0 else at
                    group.append((sources[term].at[pl.ds(start, p.n)], held_refs[room]))
                    room += 1
            made_copies = []
            for source, target in group:
                made_copies.append(pltpu.make_async_copy(source, target, sems.at[sem]))
                sem += 1
            groups.append(made_copies)
        for group in groups:
            for copy in group:
                copy.start()
        room = 0
        for (p, link, base, near, held), (each, terms), group in zip(plans, counts, groups):
            these = held_refs[room : room + terms]
            room += terms
            for copy in group:
                copy.wait()

            @pl.loop(0, each * p.n)
            def _(i, these=these, base=base, out=outs[link], last=p.step == 2 and last_by_rows):
                value = these[0][i].astype(F32)
                for one in these[1:]:
                    value = value + one[i].astype(F32)
                value = value.astype(BF16)
                if last:
                    for k in range(ways):
                        out[k, base + i] = value[k * r : (k + 1) * r]
                else:
                    out[base + i] = value

    moved = sum(2 * math.prod(room) for room in rooms) + sum(2 * math.prod(shape) for shape in shapes)
    sums = pl.pallas_call(
        body,
        out_shape=[jax.ShapeDtypeStruct(shape, BF16) for shape in shapes],
        in_specs=[SCALARS] + [pl.BlockSpec(memory_space=pltpu.HBM)] * len(arrays),
        out_specs=[pl.BlockSpec(memory_space=pltpu.VMEM)] * len(links),
        scratch_shapes=[pltpu.VMEM(room, BF16) for room in rooms]
        + [pltpu.SemaphoreType.DMA((copies_needed,))],
        compiler_params=pltpu.CompilerParams(vmem_limit_bytes=VMEM),
        cost_estimate=pl.CostEstimate(flops=0, bytes_accessed=moved, transcendentals=0),
    )(me, *arrays)
    return [(p, link, base) for p, link, base, _, _ in plans], dict(zip(links, sums))


def cross(a, name):
    axis, bit = ("head", 0) if name == "h" else ("clip", 1 if name == "x" else 0)
    size = lax.axis_size(axis)
    return lax.ppermute(a, axis, [(i, i ^ (1 << bit)) for i in range(size)])


def pieces_of(halves_of):
    total = sum(keep.shape[0] for keep, _ in halves_of)
    found = []
    seen = 0
    for keep, send in halves_of:
        got = cross(send, "c")
        n = keep.shape[0]
        first = min(max((total + 1) // 2 - seen, 0), n)
        if first:
            found.append(Piece(keep, got, 0, first, ("x", "h")))
        if n > first:
            found.append(Piece(keep, got, first, n - first, ("h", "x")))
        seen += n
    return found


def move(x, pieces, me, at_end=False):
    plans, sums = fold(pieces, me, at_end)
    x, sums = lax.optimization_barrier((x, sums))
    got = {}
    for link, array in sums.items():
        if link == "z":
            if at_end:
                every = lax.all_to_all(array, "seq", split_axis=0, concat_axis=0, tiled=True)
                got[link] = jnp.sum(every.astype(F32), axis=0)
            else:
                own = lax.psum_scatter(array, "seq", scatter_dimension=1, tiled=True)
                got[link] = own.astype(F32)
        else:
            got[link] = cross(array, link)
    for p, link, base in plans:
        if link == "z":
            p.result = got[link][base : base + p.n]
        else:
            p.held.append((got[link], base))
        p.step += 1
    return x


def settle(x, pieces):
    arrays = []
    for p in pieces:
        if not any(p.held[-1][0] is a for a in arrays):
            arrays.append(p.held[-1][0])
    x, came = lax.optimization_barrier((x, arrays))
    for p in pieces:
        for old, new in zip(arrays, came):
            if p.held[-1][0] is old:
                p.held[-1] = (new, p.held[-1][1])
                break
    return x


def reduce_plain(halves_of, core):
    def joined(keep, send):
        low = jnp.where(core == 0, keep, send)
        high = jnp.where(core == 0, send, keep)
        n, shares, pairs, depth, width = keep.shape
        return jnp.stack((low, high), axis=3).reshape(n, shares, 2 * pairs * depth, width)

    g = jnp.concatenate([joined(*pair) for pair in halves_of], axis=0)
    g = lax.psum_scatter(g, "head", scatter_dimension=1, tiled=True)
    g = lax.psum_scatter(g.astype(F32), ("clip", "seq"), scatter_dimension=2, tiled=True)
    return g[:, 0]


def gather_norms(gain, bias):
    layers, norms, part = gain.shape
    both = jnp.concatenate((gain, bias), axis=1).reshape(1, -1)
    count = lax.axis_size("clip") * lax.axis_size("seq") * lax.axis_size("head")
    width = round_up(both.shape[1], 128)
    padded = jnp.pad(both, ((0, 0), (0, width - both.shape[1])))
    every = lax.all_to_all(
        jnp.broadcast_to(padded, (count, width)), ALL, split_axis=0, concat_axis=0, tiled=True
    )[:, : both.shape[1]]
    return every.reshape(count, layers * 2 * norms, part).transpose(1, 0, 2).reshape(layers, 2 * norms, -1)


def reduce_norms(sums):
    count = lax.axis_size("clip") * lax.axis_size("seq") * lax.axis_size("head")
    rows, features = sums.shape
    part = features // count
    a = sums.reshape(rows, count, part).transpose(1, 0, 2).reshape(count, rows * part)
    width = round_up(rows * part, 128)
    a = jnp.pad(a, ((0, 0), (0, width - rows * part)))
    every = lax.all_to_all(a, ALL, split_axis=0, concat_axis=0, tiled=True)
    return jnp.sum(every, axis=0)[: rows * part].reshape(rows, part)


def on_device(
    tokens,
    cotangent,
    time_qkv,
    time_out,
    time_mix,
    space_qkv,
    space_out,
    mlp_in,
    mlp_out,
    norm_gain,
    norm_bias,
):
    layers = time_qkv.shape[0]
    clips, frames, places, d = tokens.shape
    ways = lax.axis_size("seq")
    shards = lax.axis_size("clip") * ways
    rows = Rows(clips * frames, places, ways)
    shares = lax.axis_size("head")

    def as_rows(a):
        a = a.astype(F32).reshape(rows.frames, places, d)
        a = jnp.pad(a, ((0, 0), (0, rows.frame_rows - places), (0, 0)))
        return a.reshape(rows.rows, d)

    def from_rows(a):
        a = a.reshape(rows.frames, rows.frame_rows, d)[:, :places]
        return a.reshape(tokens.shape)

    gbs = gather_norms(norm_gain, norm_bias)
    gb = [gbs[l] for l in range(layers)]
    packs = [
        pack_attention(time_qkv[l], time_out[l], time_mix[l], space_qkv[l], space_out[l])
        for l in range(layers)
    ]
    packs_ff = [pack_feed_forward(mlp_in[l], mlp_out[l], time_qkv.shape[3]) for l in range(layers)]
    weights = [gather_slabs(pack) for pack in packs]
    mixes = [mix_whole(w[-1], shards) for w in weights]
    quick = lax.axis_size("clip") == 4 and shares == 2 and ways == 4 and time_qkv.shape[1] % 16 == 0

    halves = Halves(lax.axis_size("clip"), d, time_qkv.shape[3])
    clip = lax.axis_index("clip")
    member = member_of(clip, lax.axis_index("seq"))
    me = jnp.stack((clip & 1, (clip >> 1) & 1, lax.axis_index("head"), member, lax.axis_index("seq"))).astype(
        jnp.int32
    )
    if quick:
        spreads = [Spread(pack, me) for pack in packs_ff]
        weights_ff = []
    else:
        weights_ff = [gather_slabs(pack) for pack in packs_ff]

    home = go_home(tokens)
    if quick:
        first = spreads[0]
        home, gb = first.step((home, gb))
    x = as_rows(home)
    send = send_first(rows, x, gb[0], me)
    kept = []
    for l in range(layers):
        w = weights[l]
        send = swap_places(send)
        if quick and l == 0:
            for _ in range(2):
                send = first.step(send)
            for spread in spreads[1:]:
                send = spread.step(send)
                send = spread.hold(send)
            send = first.step(send)
        elif quick:
            send = spreads[l].step(send)
        a1, qkv1, log1, o1_time = time_forward(rows, send, w)
        back = swap_places(o1_time)
        if quick:
            back = spreads[l].step(back)
            weights_ff.append(spreads[l].come)
            if l == 0:
                for spread in spreads[1:]:
                    back = spread.step(back)
        o1, y1, x1, qkv2 = middle_forward(rows, back, x, w, mixes[l], gb[l], me)
        o2, x2, log2 = space_forward(rows, qkv2, x1, w)
        if quick and l == 0:
            for spread in spreads[1:]:
                x2 = spread.step(x2)
        kept.append((x, a1, qkv1, log1, o1, y1, x1, qkv2, o2, log2, x2))
        if l + 1 < layers:
            x, *send = mlp_forward(rows, x2, weights_ff[l], gb[l], gb[l + 1], me)

    grad = as_rows(go_home(cotangent))
    norm_rows = [None] * layers
    summed = [None] * layers
    late = []
    for l in reversed(range(layers)):
        w = weights[l]
        x, a1, qkv1, log1, o1, y1, x1, qkv2, o2, log2, x2 = kept[l]
        grad, g_ff, s3, x3 = mlp_backward(
            rows, grad, x2, weights_ff[l], gb[l], me, halves, l + 1 == layers
        )
        if x3:
            output = go_back(from_rows(x3[0].astype(BF16)))
        if quick:
            ff = pieces_of(g_ff)
            if late:
                grad = settle(grad, late)
                grad = move(grad, late, me)
                late = [p for p in late if p.step < 3]
        grad, g_space, s2 = space_backward(rows, grad, x1, qkv2, o2, log2, w, gb[l], me, halves)
        if quick:
            space = pieces_of([g_space])
            if late:
                grad = settle(grad, late)
            grad, output = move((grad, output), ff, me)
        do1, g_out = middle_backward(rows, grad, y1, o1, w, mixes[l], me, halves, shards)
        do1 = swap_places(do1)
        if quick:
            do1 = move(do1, ff + space + late, me)
        da1, g_time = time_backward(rows, do1, a1, qkv1, log1, w, me, halves)
        if quick:
            da1 = settle(da1, ff + space)
        da1 = swap_places(da1)
        if quick:
            rest = pieces_of([g_out] + g_time)
            da1 = move(da1, ff + space + rest, me)
            late = space + rest
        grad, s1 = first_norm_back(rows, da1, x, grad, gb[l], me)
        norm_rows[l] = jnp.concatenate((s1[0:1], s2[0:1], s3[0:1], s1[1:2], s2[1:2], s3[1:2]), axis=0)
        if quick:
            summed[l] = ff + space + rest
        else:
            summed[l] = [reduce_plain(g_ff + [g_space, g_out] + g_time, clip & 1)]
    norm_sums = reduce_norms(jnp.concatenate(norm_rows, axis=0)).reshape(layers, 2, 3, -1)
    if quick:
        tokens_grad = go_back(from_rows(grad.astype(BF16)))
        tokens_grad, norm_sums = move((tokens_grad, norm_sums), late, me, True)
        move((), rest, me, True)
        summed = [[p.result for p in some] for some in summed]
    cuts = (2 * g_ff[0][0].shape[0], g_space[0].shape[0], g_out[0].shape[0], len(g_time))
    results = []
    for some in summed:
        slabs_of = jnp.concatenate(some, axis=0)
        ends = [sum(cuts[: i + 1]) for i in range(4)]
        results.append([slabs_of[e - c : e] for c, e in zip(cuts, ends)])
    if not quick:
        tokens_grad = go_back(from_rows(grad.astype(BF16)))
    tokens_grad = tokens_grad.astype(F32)

    def stacked(form):
        return jnp.stack([form(*results[l]) for l in range(layers)])

    def rows_of(a):
        return a.transpose(1, 0, 2)

    def flat(a):
        return rows_of(a).reshape(a.shape[1], -1)

    def mix_rows(a):
        r, width = a.shape
        return a.reshape(shares, r // shares, width).transpose(1, 0, 2).reshape(r // shares, -1)

    per_share = mlp_in.shape[2] // time_qkv.shape[3]
    return (
        output,
        tokens_grad,
        stacked(lambda ff, s, t, q: rows_of(q)),
        stacked(lambda ff, s, t, q: t[0].T),
        stacked(lambda ff, s, t, q: mix_rows(t[1])),
        stacked(lambda ff, s, t, q: rows_of(s[1:])),
        stacked(lambda ff, s, t, q: s[0].T),
        stacked(lambda ff, s, t, q: flat(ff[:per_share])),
        stacked(lambda ff, s, t, q: flat(ff[per_share:]).T),
        norm_sums[:, 0],
        norm_sums[:, 1],
    )


def solution(mesh):
    token_spec = P(("clip", "head"), "seq", None, None)
    in_specs = (
        token_spec,
        token_spec,
        P(None, ("clip", "seq"), None, "head"),
        P(None, "head", ("clip", "seq")),
        P(None, ("clip", "seq", "head"), None),
        P(None, ("clip", "seq"), None, "head"),
        P(None, "head", ("clip", "seq")),
        P(None, ("clip", "seq"), "head"),
        P(None, "head", ("clip", "seq")),
        P(None, None, ("clip", "seq", "head")),
        P(None, None, ("clip", "seq", "head")),
    )
    return jax.shard_map(
        on_device, mesh=mesh, in_specs=in_specs, out_specs=in_specs, check_vma=False
    )
```

```python
import functools
import math

import jax
import jax.numpy as jnp
from jax import lax
from jax.experimental import pallas as pl
from jax.experimental.pallas import tpu as pltpu
from jax.sharding import PartitionSpec as P

HEAD_DIM = 64
NORM_EPS = 1e-06
HALF_ROOT = 0.7071067811865476
INV_ROOT_TAU = 0.3989422804014327
LOG2E = 1.4426950408889634
FAR = -1e30
LANES = 128
VMEM = 56 * 1024 * 1024
SHOWN = 1.0
ALL = ("clip", "seq", "head")
BF16 = jnp.bfloat16
F32 = jnp.float32


def round_up(value, step):
    return -(-value // step) * step


def nn(a, b):
    return lax.dot_general(a, b, (((1,), (0,)), ((), ())), preferred_element_type=F32)


def nt(a, b):
    return lax.dot_general(a, b, (((1,), (1,)), ((), ())), preferred_element_type=F32)


def tn(a, b):
    return lax.dot_general(a, b, (((0,), (0,)), ((), ())), preferred_element_type=F32)


def norm_parts(x):
    mean = jnp.mean(x, axis=-1, keepdims=True)
    centred = x - mean
    spread = lax.rsqrt(jnp.mean(centred * centred, axis=-1, keepdims=True) + NORM_EPS)
    return centred * spread, spread


def norm_rounded(x, gain, bias):
    hat, _ = norm_parts(x)
    return (hat * gain + bias).astype(BF16)


def norm_back(u, x, gain):
    hat, spread = norm_parts(x)
    scaled = u * gain
    mean_scaled = jnp.mean(scaled, axis=-1, keepdims=True)
    mean_cross = jnp.mean(scaled * hat, axis=-1, keepdims=True)
    change = spread * (scaled - mean_scaled - hat * mean_cross)
    sums = jnp.concatenate(
        (jnp.sum(u * hat, axis=0, keepdims=True), jnp.sum(u, axis=0, keepdims=True)), axis=0
    )
    return change, sums


class Rows:
    def __init__(self, frames, places, ways):
        self.frames = frames
        self.places = places
        self.ways = ways
        self.frame_rows = round_up(places, 16)
        self.rows = frames * self.frame_rows
        self.block = places // ways
        self.chunk = round_up(frames * self.block, 8)
        self.time_rows = ways * self.chunk

    def split(self, r):
        way = jnp.zeros_like(r)
        for k in range(1, self.ways):
            way = way + (r >= k * self.chunk).astype(jnp.int32)
        rest = r - way * self.chunk
        frame = jnp.zeros_like(r)
        for k in range(1, self.frames):
            frame = frame + (rest >= k * self.block).astype(jnp.int32)
        real = rest < self.frames * self.block
        return way, frame, rest - frame * self.block, real

    def to_time(self, k, member):
        r = lax.broadcasted_iota(jnp.int32, (self.chunk, 1), 0)
        _, frame, place, real = self.split(r)
        way = jnp.bitwise_xor(member, k)
        source = jnp.where(real, frame * self.frame_rows + way * self.block + place, -1)
        c = lax.broadcasted_iota(jnp.int32, (self.chunk, self.rows), 1)
        return jnp.where(c == source, 1.0, 0.0).astype(BF16)

    def gathered(self, chunk_refs, member):
        total = tn(self.to_time(0, member), chunk_refs[0][...])
        for k in range(1, self.ways):
            total = total + tn(self.to_time(k, member), chunk_refs[k][...])
        return total

    def chunks(self, width, block=None, index=None):
        return [
            made((self.chunk, width), BF16)
            if block is None
            else made((self.chunk, width), BF16, (self.chunk, block), index)
            for _ in range(self.ways)
        ]

    def time_bias(self):
        def label(r):
            _, _, place, real = self.split(r)
            return jnp.where(real, place, -1)

        a = label(lax.broadcasted_iota(jnp.int32, (self.time_rows, 1), 0))
        b = label(lax.broadcasted_iota(jnp.int32, (1, self.time_rows), 1))
        return jnp.where(a == b, 0.0, FAR).astype(F32)

    def space_bias(self):
        a = lax.broadcasted_iota(jnp.int32, (self.frame_rows, 1), 0)
        return jnp.where(a < self.places, 0.0, FAR).astype(F32)


def lane_masks(rows):
    lane = lax.broadcasted_iota(jnp.int32, (rows, LANES), 1)
    return lane < HEAD_DIM


def one_of(value, low, half):
    zero = jnp.zeros_like(value)
    return jnp.where(low, value, zero) if half == 0 else jnp.where(low, zero, value)


def pair_forward(q, k, v, bias, rate):
    low = lane_masks(q.shape[0])
    mixed, logs = [], []
    for half in range(2):
        s = nt(k, one_of(q, low, half)) + bias
        peak = jnp.max(s, axis=0, keepdims=True)
        e = jnp.exp2((s - peak) * rate)
        total = jnp.sum(e, axis=0, keepdims=True)
        soft = (e * (1.0 / total)).astype(BF16)
        mixed.append(tn(soft, v))
        logs.append(peak * rate + jnp.log2(total))
    return jnp.where(low, mixed[0], mixed[1]).astype(BF16), logs


def pair_backward(q, k, v, do, logs, bias, rate, scale):
    low = lane_masks(q.shape[0])
    dq, dk, dv = [], [], []
    for half in range(2):
        s = nt(k, one_of(q, low, half)) + bias
        soft = jnp.exp2(s * rate - logs[half])
        dp = nt(v, one_of(do, low, half))
        ds = (soft * (dp - jnp.sum(soft * dp, axis=0, keepdims=True))).astype(BF16)
        dv.append(nn(soft.astype(BF16), do))
        dk.append(nn(ds, q))
        dq.append(tn(ds, k))
    return (
        (jnp.where(low, dq[0], dq[1]) * scale).astype(BF16),
        (jnp.where(low, dk[0], dk[1]) * scale).astype(BF16),
        jnp.where(low, dv[0], dv[1]).astype(BF16),
    )


def split_rows(value, keep_ref, send_ref, at, room_ref, me_ref):
    mine = me_ref[0]
    room_ref[...] = value.reshape(room_ref.shape)
    keep_ref[at] = room_ref[:, mine].astype(BF16)
    send_ref[at] = room_ref[:, 1 - mine].astype(BF16)


def store_by_core(ref, value, halves):
    n = halves.rows
    for core in range(2):
        for pair in range(halves.pairs):
            first = (2 * pair + core) * n
            ref[core, pair * n : (pair + 1) * n] = value[first : first + n]


def split_product(left_ref, right, keep_ref, send_ref, at, me_ref):
    mine = me_ref[0]
    shape = keep_ref.shape[len(at) :]
    keep_ref[at] = nn(left_ref[mine], right).reshape(shape).astype(BF16)
    send_ref[at] = nn(left_ref[1 - mine], right).reshape(shape).astype(BF16)


class Halves:
    def __init__(self, clips, depth, width):
        self.pairs = clips // 2
        self.rows = depth // clips
        self.width = width

    def array(self, lead, block, index):
        tail = (self.pairs, self.rows, self.width)
        one = lambda: made(lead + tail, BF16, block + tail, lambda *g: index(*g) + (0, 0, 0))
        return [one(), one()]

    def turned(self, columns):
        return pltpu.VMEM((2, self.pairs * self.rows, columns), BF16)

    def room(self):
        return pltpu.VMEM((self.pairs, 2, self.rows, self.width), F32)


SCALARS = pl.BlockSpec(memory_space=pltpu.SMEM)


def call(body, grid, ins, outs, scratch, args, flops=0):
    specs = [spec for spec in ins]
    moved = sum(math.prod(o.shape) * o.dtype.itemsize for o, _ in outs)
    moved += sum(math.prod(a.shape) * a.dtype.itemsize for a in args)
    return pl.pallas_call(
        body,
        out_shape=[shape for shape, _ in outs],
        grid=grid,
        in_specs=specs,
        out_specs=[spec for _, spec in outs],
        scratch_shapes=scratch,
        compiler_params=pltpu.CompilerParams(vmem_limit_bytes=VMEM),
        cost_estimate=pl.CostEstimate(
            flops=int(flops * SHOWN), bytes_accessed=int(moved * SHOWN), transcendentals=0
        ),
    )(*args)


def whole(shape):
    zeros = (0,) * len(shape)
    return pl.BlockSpec(shape, lambda *_: zeros)


def made(shape, dtype, block=None, index=None):
    spec = whole(shape) if block is None else pl.BlockSpec(block, index)
    return jax.ShapeDtypeStruct(shape, dtype), spec


def slabs(count, first, width, depth):
    return pl.BlockSpec((count, 1, depth, width), lambda h, *_: (first // count, h, 0, 0))


def send_first(rows, x, gb, me):
    def body(me_ref, x_ref, gb_ref, *out_refs):
        a = norm_rounded(x_ref[...], gb_ref[0:1], gb_ref[3:4])
        for k in range(rows.ways):
            out_refs[k][...] = nn(rows.to_time(k, me_ref[3]), a).astype(BF16)

    d = x.shape[1]
    return call(
        body, (1,), [SCALARS, whole(x.shape), whole(gb.shape)], rows.chunks(d), [], (me, x, gb)
    )


def time_forward(rows, chunks, w):
    t, d = rows.time_rows, chunks[0].shape[1]
    width = w.shape[3]
    shares = w.shape[1]
    pairs = width // LANES
    ways = rows.ways
    rate = LOG2E / math.sqrt(HEAD_DIM)

    def body(*refs):
        chunk_refs = refs[:ways]
        w_ref, a_ref, qkv_ref, log_ref = refs[ways : ways + 4]
        out_refs = refs[ways + 4 : 2 * ways + 4]
        bias_ref, mixed_ref = refs[2 * ways + 4 :]

        @pl.when(pl.program_id(0) == 0)
        def _():
            bias_ref[...] = rows.time_bias()
            for k in range(ways):
                a_ref[k * rows.chunk : (k + 1) * rows.chunk] = chunk_refs[k][...]

        act = a_ref[...]
        for g in range(3):
            qkv_ref[g] = nn(act, w_ref[g, 0]).astype(BF16)

        @pl.loop(0, pairs)
        def _(i):
            lanes = pl.ds(pl.multiple_of(i * LANES, LANES), LANES)
            mixed, logs = pair_forward(
                qkv_ref[0, :, lanes], qkv_ref[1, :, lanes], qkv_ref[2, :, lanes], bias_ref[...], rate
            )
            mixed_ref[:, lanes] = mixed
            log_ref[0, i] = jnp.concatenate(logs, axis=0)

        for k in range(ways):
            out_refs[k][...] = mixed_ref[k * rows.chunk : (k + 1) * rows.chunk]

    got = call(
        body,
        (shares,),
        [whole(c.shape) for c in chunks] + [slabs(3, 0, width, d)],
        [
            made((t, d), BF16),
            made((3, t, d), BF16, (3, t, width), lambda h: (0, 0, h)),
            made((shares, pairs, 2, t), F32, (1, pairs, 2, t), lambda h: (h, 0, 0, 0)),
            *rows.chunks(d, width, lambda h: (0, h)),
        ],
        [pltpu.VMEM((t, t), F32), pltpu.VMEM((t, width), BF16)],
        (*chunks, w),
        flops=2 * t * d * 3 * d,
    )
    return got[0], got[1], got[2], got[3:]


def middle_forward(rows, back, x, w, mix, gb, me):
    t, d = x.shape
    width = w.shape[3]
    shares = w.shape[1]

    def body(me_ref, *refs):
        x_ref, to_ref, sq_ref, mix_ref, gb_ref, o1_ref, y1_ref, x1_ref, qkv_ref = refs[rows.ways :]
        o1 = rows.gathered(refs[: rows.ways], me_ref[3]).astype(BF16)
        o1_ref[...] = o1
        y1 = jnp.zeros((t, d), F32)
        for h in range(shares):
            y1 = y1 + nt(o1[:, h * width : (h + 1) * width], to_ref[0, h])
        y1 = y1.astype(BF16)
        y1_ref[...] = y1
        x1 = x_ref[...] + nn(y1, mix_ref[...])
        x1_ref[...] = x1
        a2 = norm_rounded(x1, gb_ref[1:2], gb_ref[4:5])
        for g in range(3):
            for h in range(shares):
                qkv_ref[g, :, h * width : (h + 1) * width] = nn(a2, sq_ref[g, h]).astype(BF16)

    return call(
        body,
        (1,),
        [
            SCALARS,
            *(whole(c.shape) for c in back),
            whole(x.shape),
            pl.BlockSpec((1, shares, d, width), lambda i: (6, 0, 0, 0)),
            pl.BlockSpec((3, shares, d, width), lambda i: (1, 0, 0, 0)),
            whole(mix.shape),
            whole(gb.shape),
        ],
        [made((t, d), BF16), made((t, d), BF16), made((t, d), F32), made((3, t, d), BF16)],
        [],
        (me, *back, x, w, w, mix, gb),
        flops=2 * t * d * 5 * d,
    )


def space_forward(rows, qkv, x1, w):
    t, d = x1.shape
    width = w.shape[3]
    shares = w.shape[1]
    pairs = width // LANES
    rate = LOG2E / math.sqrt(HEAD_DIM)
    n = rows.frame_rows

    def body(qkv_ref, x1_ref, w_ref, o2_ref, x2_ref, log_ref):
        bias = rows.space_bias()

        @pl.loop(0, pairs)
        def _(i):
            lanes = pl.ds(pl.multiple_of(i * LANES, LANES), LANES)
            for f in range(rows.frames):
                at = slice(f * n, (f + 1) * n)
                mixed, logs = pair_forward(
                    qkv_ref[0, at, lanes], qkv_ref[1, at, lanes], qkv_ref[2, at, lanes], bias, rate
                )
                o2_ref[at, lanes] = mixed
                log_ref[0, i, f] = jnp.concatenate(logs, axis=0)

        @pl.when(pl.program_id(0) == 0)
        def _():
            x2_ref[...] = x1_ref[...]

        x2_ref[...] += nt(o2_ref[...], w_ref[0, 0])

    return call(
        body,
        (shares,),
        [
            pl.BlockSpec((3, t, width), lambda h: (0, 0, h)),
            whole(x1.shape),
            slabs(1, 7, width, d),
        ],
        [
            made((t, d), BF16, (t, width), lambda h: (0, h)),
            made((t, d), F32),
            made(
                (shares, pairs, rows.frames, 2, n),
                F32,
                (1, pairs, rows.frames, 2, n),
                lambda h: (h, 0, 0, 0, 0),
            ),
        ],
        [],
        (qkv, x1, w),
        flops=2 * t * d * d,
    )


def ff_slab(first, per_share, depth, width):
    return pl.BlockSpec(
        (1, 1, depth, width), lambda j: (first + j % per_share, j // per_share, 0, 0)
    )


def mlp_forward(rows, x2, w, gb, gb_next, me):
    t, d = x2.shape
    width = w.shape[3]
    shares = w.shape[1]
    per_share = w.shape[0] // 2
    steps = shares * per_share

    def body(x2_ref, wi_ref, wo_ref, gb_ref, me_ref, gn_ref, x3_ref, *rest):
        send_refs, a3_ref = rest[:-1], rest[-1]
        j = pl.program_id(0)

        @pl.when(j == 0)
        def _():
            a3_ref[...] = norm_rounded(x2_ref[...], gb_ref[2:3], gb_ref[5:6])
            x3_ref[...] = x2_ref[...]

        hid = nn(a3_ref[...], wi_ref[0, 0])
        act = (0.5 * hid * (1.0 + lax.erf(hid * HALF_ROOT))).astype(BF16)
        x3_ref[...] += nt(act, wo_ref[0, 0])

        @pl.when(j == steps - 1)
        def _():
            a = norm_rounded(x3_ref[...], gn_ref[0:1], gn_ref[3:4])
            for k in range(rows.ways):
                send_refs[k][...] = nn(rows.to_time(k, me_ref[3]), a).astype(BF16)

    ins = [
        whole(x2.shape),
        ff_slab(0, per_share, d, width),
        ff_slab(per_share, per_share, d, width),
        whole(gb.shape),
    ]
    ins += [SCALARS, whole(gb_next.shape)]
    outs = [made((t, d), F32)] + rows.chunks(d)
    args = (x2, w, w, gb, me, gb_next)
    return call(
        body, (steps,), ins, outs, [pltpu.VMEM((t, d), BF16)], args, flops=4 * t * d * width * steps
    )


def mlp_backward(rows, grad, x2, w, gb, me, halves, with_output):
    t, d = x2.shape
    width = w.shape[3]
    shares = w.shape[1]
    per_share = w.shape[0] // 2
    steps = shares * per_share

    def body(me_ref, g_ref, x2_ref, wi_ref, wo_ref, gb_ref, go_ref, ki_ref, si_ref, ko_ref, so_ref, sums_ref, *rest):
        if with_output:
            x3_ref, *rest = rest
        a3_ref, a3t_ref, e3_ref, e3t_ref, u_ref = rest
        j = pl.program_id(0)

        @pl.when(j == 0)
        def _():
            hat, _ = norm_parts(x2_ref[...])
            a3 = hat * gb_ref[2:3] + gb_ref[5:6]
            a3_ref[...] = a3.astype(BF16)
            store_by_core(a3t_ref, a3.T.astype(BF16), halves)
            g = g_ref[...]
            e3_ref[...] = g.astype(BF16)
            store_by_core(e3t_ref, g.T.astype(BF16), halves)
            u_ref[...] = jnp.zeros((t, d), F32)
            if with_output:
                x3_ref[...] = x2_ref[...]

        hid = nn(a3_ref[...], wi_ref[0, 0])
        phi = 0.5 * (1.0 + lax.erf(hid * HALF_ROOT))
        act = (hid * phi).astype(BF16)
        slope = phi + hid * jnp.exp(-0.5 * hid * hid) * INV_ROOT_TAU
        dhid = (nn(e3_ref[...], wo_ref[0, 0]) * slope).astype(BF16)
        split_product(e3t_ref, act, ko_ref, so_ref, (0, 0), me_ref)
        split_product(a3t_ref, dhid, ki_ref, si_ref, (0, 0), me_ref)
        u_ref[...] += nt(dhid, wi_ref[0, 0])
        if with_output:
            x3_ref[...] += nt(act, wo_ref[0, 0])

        @pl.when(j == steps - 1)
        def _():
            change, sums = norm_back(u_ref[...], x2_ref[...], gb_ref[2:3])
            go_ref[...] = g_ref[...] + change
            sums_ref[...] = sums

    slab_outs = [
        one
        for _ in range(2)
        for one in halves.array(
            (per_share, shares), (1, 1), lambda j: (j % per_share, j // per_share)
        )
    ]
    grad, ki, si, ko, so, sums, *x3 = call(
        body,
        (steps,),
        [
            SCALARS,
            whole(grad.shape),
            whole(x2.shape),
            ff_slab(0, per_share, d, width),
            ff_slab(per_share, per_share, d, width),
            whole(gb.shape),
        ],
        [made((t, d), F32), *slab_outs, made((2, d), F32)] + [made((t, d), F32)] * with_output,
        [
            pltpu.VMEM((t, d), BF16),
            halves.turned(t),
            pltpu.VMEM((t, d), BF16),
            halves.turned(t),
            pltpu.VMEM((t, d), F32),
        ],
        (me, grad, x2, w, w, gb),
        flops=10 * t * d * width * steps,
    )
    return grad, [(ki, si), (ko, so)], sums, x3


def space_backward(rows, grad, x1, qkv, o2, logs, w, gb, me, halves):
    t, d = x1.shape
    width = w.shape[3]
    shares = w.shape[1]
    pairs = width // LANES
    scale = 1.0 / math.sqrt(HEAD_DIM)
    rate = LOG2E * scale
    n = rows.frame_rows

    def body(me_ref, g_ref, x1_ref, qkv_ref, o2_ref, log_ref, wo_ref, wq_ref, gb_ref, go_ref, keep_ref, send_ref, sums_ref, e2_ref, e2t_ref, a2t_ref, do_ref, dqkv_ref, u_ref):
        h = pl.program_id(0)

        @pl.when(h == 0)
        def _():
            g = g_ref[...]
            e2_ref[...] = g.astype(BF16)
            store_by_core(e2t_ref, g.T.astype(BF16), halves)
            hat, _ = norm_parts(x1_ref[...])
            store_by_core(a2t_ref, (hat * gb_ref[1:2] + gb_ref[4:5]).T.astype(BF16), halves)
            u_ref[...] = jnp.zeros((t, d), F32)

        bias = rows.space_bias()
        split_product(e2t_ref, o2_ref[...], keep_ref, send_ref, (0, 0), me_ref)
        do_ref[...] = nn(e2_ref[...], wo_ref[0, 0]).astype(BF16)

        @pl.loop(0, pairs)
        def _(i):
            lanes = pl.ds(pl.multiple_of(i * LANES, LANES), LANES)
            for f in range(rows.frames):
                at = slice(f * n, (f + 1) * n)
                log = log_ref[0, i, f]
                grads = pair_backward(
                    qkv_ref[0, at, lanes],
                    qkv_ref[1, at, lanes],
                    qkv_ref[2, at, lanes],
                    do_ref[at, lanes],
                    (log[0:1], log[1:2]),
                    bias,
                    rate,
                    scale,
                )
                for part in range(3):
                    dqkv_ref[part, at, lanes] = grads[part]

        for part in range(3):
            split_product(a2t_ref, dqkv_ref[part], keep_ref, send_ref, (part + 1, 0), me_ref)
            u_ref[...] += nt(dqkv_ref[part], wq_ref[part, 0])

        @pl.when(h == shares - 1)
        def _():
            change, sums = norm_back(u_ref[...], x1_ref[...], gb_ref[1:2])
            go_ref[...] = g_ref[...] + change
            sums_ref[...] = sums

    grad, keep, send, sums = call(
        body,
        (shares,),
        [
            SCALARS,
            whole(grad.shape),
            whole(x1.shape),
            pl.BlockSpec((3, t, width), lambda h: (0, 0, h)),
            pl.BlockSpec((t, width), lambda h: (0, h)),
            pl.BlockSpec((1,) + logs.shape[1:], lambda h: (h, 0, 0, 0, 0)),
            slabs(1, 7, width, d),
            slabs(3, 3, width, d),
            whole(gb.shape),
        ],
        [
            made((t, d), F32),
            *halves.array((4, shares), (4, 1), lambda h: (0, h)),
            made((2, d), F32),
        ],
        [
            pltpu.VMEM((t, d), BF16),
            halves.turned(t),
            halves.turned(t),
            pltpu.VMEM((t, width), BF16),
            pltpu.VMEM((3, t, width), BF16),
            pltpu.VMEM((t, d), F32),
        ],
        (me, grad, x1, qkv, o2, logs, w, w, gb),
        flops=2 * t * d * d * 8,
    )
    return grad, (keep, send), sums


def mix_fits(depth, shards, shares):
    return depth // (shards * shares) % 8 == 0


def middle_backward(rows, grad, y1, o1, w, mix, me, halves, shards):
    t, d = grad.shape
    width = w.shape[3]
    shares = w.shape[1]
    fits = mix_fits(d, shards, shares)
    part = d // (shards * shares)

    def body(me_ref, g_ref, y1_ref, o1_ref, to_ref, mix_ref, *rest):
        send_refs, rest = rest[: rows.ways], rest[rows.ways :]
        gk_ref, gs_ref, *rest = rest
        if fits:
            room_ref, order_ref = rest
        else:
            gm_ref, room_ref = rest
        e1 = g_ref[...].astype(BF16)
        dy1 = nt(e1, mix_ref[...]).astype(BF16)
        sends = [rows.to_time(k, me_ref[3]) for k in range(rows.ways)]
        for h in range(shares):
            lanes = slice(h * width, (h + 1) * width)
            do1 = nn(dy1, to_ref[0, h]).astype(BF16)
            for k in range(rows.ways):
                send_refs[k][:, lanes] = nn(sends[k], do1).astype(BF16)
            split_rows(tn(dy1, o1_ref[:, lanes]), gk_ref, gs_ref, (0, h), room_ref, me_ref)
        gm = tn(y1_ref[...], e1)
        if fits:
            gm = gm.reshape(shards, shares, part, d)
            for h in range(shares):
                for half in range(shares):
                    order_ref[:, half] = gm[:, h, :, half * width : (half + 1) * width]
                split_rows(order_ref[...], gk_ref, gs_ref, (1, h), room_ref, me_ref)
        else:
            gm_ref[...] = gm.astype(BF16)

    outs = rows.chunks(d)
    outs += halves.array((1 + fits, shares), (1 + fits, shares), lambda i: (0, 0))
    scratch = [halves.room()]
    if fits:
        scratch.append(pltpu.VMEM((shards, shares, part, width), F32))
    else:
        outs.append(made((d, d), BF16))
    got = call(
        body,
        (1,),
        [
            SCALARS,
            whole(grad.shape),
            whole(y1.shape),
            whole(o1.shape),
            pl.BlockSpec((1, shares, d, width), lambda i: (6, 0, 0, 0)),
            whole(mix.shape),
        ],
        outs,
        scratch,
        (me, grad, y1, o1, w, mix),
        flops=8 * t * d * d,
    )
    do1, (keep, send) = got[: rows.ways], got[rows.ways : rows.ways + 2]
    if not fits:
        gm = mix_slab(got[-1], shards, shares).reshape((1, shares, halves.pairs, 2) + keep.shape[3:])
        keep = jnp.concatenate((keep, lax.dynamic_index_in_dim(gm, me[0], 3, keepdims=False)), axis=0)
        send = jnp.concatenate((send, lax.dynamic_index_in_dim(gm, 1 - me[0], 3, keepdims=False)), axis=0)
    return do1, (keep, send)


def time_backward(rows, do1, a, qkv, logs, w, me, halves):
    t, d = a.shape
    width = w.shape[3]
    shares = w.shape[1]
    pairs = width // LANES
    scale = 1.0 / math.sqrt(HEAD_DIM)
    rate = LOG2E * scale

    def body(me_ref, *refs):
        do_refs, refs = refs[: rows.ways], refs[rows.ways :]
        a_ref, qkv_ref, log_ref, w_ref = refs[:4]
        out_refs, refs = refs[4 : 4 + rows.ways], refs[4 + rows.ways :]
        half_refs, refs = refs[:6], refs[6:]
        bias_ref, dqkv_ref, at_ref, u_ref, do_ref = refs
        h = pl.program_id(0)

        @pl.when(h == 0)
        def _():
            bias_ref[...] = rows.time_bias()
            store_by_core(at_ref, a_ref[...].T, halves)
            u_ref[...] = jnp.zeros((t, d), F32)

        for k in range(rows.ways):
            do_ref[k * rows.chunk : (k + 1) * rows.chunk] = do_refs[k][...]

        @pl.loop(0, pairs)
        def _(i):
            lanes = pl.ds(pl.multiple_of(i * LANES, LANES), LANES)
            log = log_ref[0, i]
            grads = pair_backward(
                qkv_ref[0, :, lanes],
                qkv_ref[1, :, lanes],
                qkv_ref[2, :, lanes],
                do_ref[:, lanes],
                (log[0:1], log[1:2]),
                bias_ref[...],
                rate,
                scale,
            )
            for part in range(3):
                dqkv_ref[part, :, lanes] = grads[part]

        for part in range(3):
            split_product(
                at_ref, dqkv_ref[part], half_refs[2 * part], half_refs[2 * part + 1], (0, 0), me_ref
            )
            u_ref[...] += nt(dqkv_ref[part], w_ref[part, 0])

        @pl.when(h == shares - 1)
        def _():
            for k in range(rows.ways):
                out_refs[k][...] = u_ref[k * rows.chunk : (k + 1) * rows.chunk].astype(BF16)

    got = call(
        body,
        (shares,),
        [
            SCALARS,
            *(pl.BlockSpec((rows.chunk, width), lambda h: (0, h)) for _ in do1),
            whole(a.shape),
            pl.BlockSpec((3, t, width), lambda h: (0, 0, h)),
            pl.BlockSpec((1,) + logs.shape[1:], lambda h: (h, 0, 0, 0)),
            slabs(3, 0, width, d),
        ],
        [
            *rows.chunks(d),
            *(one for _ in range(3) for one in halves.array((1, shares), (1, 1), lambda h: (0, h))),
        ],
        [
            pltpu.VMEM((t, t), F32),
            pltpu.VMEM((3, t, width), BF16),
            halves.turned(t),
            pltpu.VMEM((t, d), F32),
            pltpu.VMEM((t, width), BF16),
        ],
        (me, *do1, a, qkv, logs, w),
        flops=2 * t * d * d * 6,
    )
    parts = got[rows.ways :]
    return got[: rows.ways], [tuple(parts[i : i + 2]) for i in (0, 2, 4)]


def first_norm_back(rows, back, x, grad, gb, me):
    t, d = x.shape

    def body(me_ref, *refs):
        x_ref, g_ref, gb_ref, go_ref, sums_ref = refs[rows.ways :]
        u = rows.gathered(refs[: rows.ways], me_ref[3])
        change, sums = norm_back(u, x_ref[...], gb_ref[0:1])
        go_ref[...] = g_ref[...] + change
        sums_ref[...] = sums

    return call(
        body,
        (1,),
        [SCALARS, *(whole(c.shape) for c in back), whole(x.shape), whole(grad.shape), whole(gb.shape)],
        [made((t, d), F32), made((2, d), F32)],
        [],
        (me, *back, x, grad, gb),
    )


def homes():
    clips, ways = lax.axis_size("clip"), lax.axis_size("seq")
    pairs = []
    for clip in range(clips):
        for seq in range(ways):
            home_clip = clip - clip % 2 + seq % 2
            home_seq = seq // 2 + (ways // 2) * (clip % 2)
            pairs.append((clip * ways + seq, home_clip * ways + home_seq))
    return pairs


def go_home(a):
    return lax.ppermute(a, ("clip", "seq"), homes())


def go_back(a):
    return lax.ppermute(a, ("clip", "seq"), [(home, device) for device, home in homes()])


def member_of(clip, seq):
    return clip % 2 + 2 * (seq % (lax.axis_size("seq") // 2))


def swap_places(chunks):
    clips, ways = lax.axis_size("clip"), lax.axis_size("seq")
    got = [chunks[0]]
    for k in range(1, ways):
        pairs = []
        for clip in range(clips):
            for seq in range(ways):
                other = member_of(clip, seq) ^ k
                to_clip = clip - clip % 2 + other % 2
                to_seq = seq - seq % (ways // 2) + other // 2
                pairs.append((clip * ways + seq, to_clip * ways + to_seq))
        got.append(lax.ppermute(chunks[k], ("clip", "seq"), pairs))
    return got


def columns(a, r, width):
    return a.reshape(r, -1, width).transpose(1, 0, 2)


def pack_attention(time_qkv, time_out, time_mix, space_qkv, space_out):
    r, _, width = time_qkv.shape
    mix = time_mix.reshape(-1, time_mix.shape[1] // width, width).transpose(1, 0, 2).reshape(1, r, width)
    return jnp.concatenate(
        (
            columns(time_qkv, r, width),
            columns(space_qkv, r, width),
            time_out.T[None],
            space_out.T[None],
            mix,
        ),
        axis=0,
    )


def pack_feed_forward(mlp_in, mlp_out, width):
    r = mlp_in.shape[0]
    return jnp.concatenate((columns(mlp_in, r, width), columns(mlp_out.T, r, width)), axis=0)


def gather_slabs(pack):
    full = lax.all_gather(pack, ("head", "clip", "seq"), axis=1, tiled=True)
    return full.reshape(pack.shape[0], lax.axis_size("head"), -1, pack.shape[2])


def spread_steps(pack, me):
    ways, clips = lax.axis_size("seq"), lax.axis_size("clip")
    shares = lax.axis_size("head")
    n, r, width = pack.shape
    pack = yield pack
    turned = [pack] + [
        lax.ppermute(pack, "seq", [(i, (i + k) % ways) for i in range(ways)]) for k in range(1, ways)
    ]
    turned = yield turned
    orders = (((0, 1), "x", "h"), ((3, 2), "h", "x"))
    some = [jnp.stack([turned[k] for k in steps]) for steps, _, _ in orders]
    come = yield [cross(a, first) for a, (_, first, _) in zip(some, orders)]
    some = [jnp.concatenate(pair, axis=0) for pair in zip(some, come)]
    come = yield [cross(a, second) for a, (_, _, second) in zip(some, orders)]
    runs = []
    for mine, other, (steps, first, second) in zip(some, come, orders):
        where = [(k, {first: f}) for f in (0, 1) for k in steps]
        for g, blocks in enumerate((mine, other)):
            runs.append((blocks, [(k, {**at, second: g}) for k, at in where], 0))
    come = yield [cross(blocks, "c") for blocks, _, _ in runs]
    runs += [(far, where, 1) for far, (_, where, _) in zip(come, runs)]
    count = sum(len(where) for _, where, _ in runs)

    def body(me_ref, *refs):
        sources, out_ref, sems = refs[: len(runs)], refs[-2], refs[-1]
        copies = []
        for source, (_, where, core) in zip(sources, runs):
            for i, (k, at) in enumerate(where):
                share = jnp.bitwise_xor(me_ref[2], at["h"])
                clip = 2 * jnp.bitwise_xor(me_ref[1], at["x"]) + jnp.bitwise_xor(me_ref[0], core)
                seq = lax.rem(me_ref[4] + (ways - k), ways)
                copies.append(
                    pltpu.make_async_copy(
                        source.at[i], out_ref.at[:, share, clip * ways + seq], sems.at[len(copies)]
                    )
                )
        for copy in copies:
            copy.start()
        for copy in copies:
            copy.wait()

    full = pl.pallas_call(
        body,
        out_shape=jax.ShapeDtypeStruct((n, shares, clips * ways, r, width), BF16),
        in_specs=[SCALARS] + [pl.BlockSpec(memory_space=pltpu.HBM)] * len(runs),
        out_specs=pl.BlockSpec(memory_space=pltpu.VMEM),
        scratch_shapes=[pltpu.SemaphoreType.DMA((count,))],
        compiler_params=pltpu.CompilerParams(vmem_limit_bytes=VMEM),
        cost_estimate=pl.CostEstimate(
            flops=0, bytes_accessed=4 * n * shares * clips * ways * r * width, transcendentals=0
        ),
    )(me, *(blocks for blocks, _, _ in runs))
    yield full.reshape(n, shares, clips * ways * r, width)


class Spread:
    def __init__(self, pack, me):
        self.way = spread_steps(pack, me)
        self.come = next(self.way)

    def hold(self, x):
        x, self.come = lax.optimization_barrier((x, self.come))
        return x

    def step(self, x):
        x = self.hold(x)
        self.come = self.way.send(self.come)
        return x


def mix_whole(slab, shards):
    shares, depth, width = slab.shape
    part = slab.reshape(shares, shards, shares, depth // (shards * shares), width)
    return part.transpose(1, 0, 3, 2, 4).reshape(depth, shares * width)


def mix_slab(whole_grad, shards, shares):
    depth, full = whole_grad.shape
    width = full // shares
    part = whole_grad.reshape(shards, shares, depth // (shards * shares), shares, width)
    return part.transpose(1, 0, 3, 2, 4).reshape(1, shares, depth, width)


class Piece:
    def __init__(self, keep, got, first, n, order):
        self.near = (keep, got)
        self.first = first
        self.n = n
        self.order = order
        self.step = 0
        self.held = []
        self.result = None


PLACE = {"x": 1, "h": 2}


def fold(pieces, me, last_by_rows):
    ways = lax.axis_size("seq")
    depth, width = pieces[0].near[0].shape[-2:]
    r = depth // ways
    used = {}
    arrays = []

    def number(a):
        for i, known in enumerate(arrays):
            if known is a:
                return i
        arrays.append(a)
        return len(arrays) - 1

    plans = []
    for p in pieces:
        link = p.order[p.step] if p.step < 2 else "z"
        blocks = p.n * (2 if p.step == 0 else 1)
        base = used.get(link, 0)
        used[link] = base + blocks
        near = [number(a) for a in p.near]
        held = [(number(a), at) for a, at in p.held]
        plans.append((p, link, base, near, held))
    links = sorted(used)
    shapes = [
        (ways, used[k], r, width) if k == "z" and last_by_rows else (used[k], depth, width)
        for k in links
    ]
    rooms, counts = [], []
    for p, link, base, near, held in plans:
        each = 2 if p.step == 0 else 1
        counts.append((each, len(near) + len(held)))
        rooms += [(each * p.n, depth, width)] * (len(near) + len(held))
    copies_needed = sum(each * terms for each, terms in counts)

    def body(me_ref, *refs):
        sources = refs[: len(arrays)]
        outs = dict(zip(links, refs[len(arrays) : len(arrays) + len(links)]))
        held_refs = refs[len(arrays) + len(links) : -1]
        sems = refs[-1]
        mine = {name: me_ref[PLACE[name]] for name in PLACE}
        groups = []
        room = 0
        sem = 0
        for p, link, base, near, held in plans:
            group = []
            if p.step == 0:
                for term in near:
                    for k in range(2):
                        pick = {p.order[0]: 1 - mine[p.order[0]], p.order[1]: k}
                        source = sources[term].at[pl.ds(p.first, p.n), pick["h"], pick["x"]]
                        group.append((source, held_refs[room].at[pl.ds(k * p.n, p.n)]))
                    room += 1
            else:
                last = p.order[1]
                pick = {p.order[0]: mine[p.order[0]]}
                pick[last] = 1 - mine[last] if p.step == 1 else mine[last]
                for term in near:
                    source = sources[term].at[pl.ds(p.first, p.n), pick["h"], pick["x"]]
                    group.append((source, held_refs[room]))
                    room += 1
                for i, (term, at) in enumerate(held):
                    start = at + pick[last] * p.n if i == 0 else at
                    group.append((sources[term].at[pl.ds(start, p.n)], held_refs[room]))
                    room += 1
            made_copies = []
            for source, target in group:
                made_copies.append(pltpu.make_async_copy(source, target, sems.at[sem]))
                sem += 1
            groups.append(made_copies)
        for group in groups:
            for copy in group:
                copy.start()
        room = 0
        for (p, link, base, near, held), (each, terms), group in zip(plans, counts, groups):
            these = held_refs[room : room + terms]
            room += terms
            for copy in group:
                copy.wait()

            @pl.loop(0, each * p.n)
            def _(i, these=these, base=base, out=outs[link], last=p.step == 2 and last_by_rows):
                value = these[0][i].astype(F32)
                for one in these[1:]:
                    value = value + one[i].astype(F32)
                value = value.astype(BF16)
                if last:
                    for k in range(ways):
                        out[k, base + i] = value[k * r : (k + 1) * r]
                else:
                    out[base + i] = value

    moved = sum(2 * math.prod(room) for room in rooms) + sum(2 * math.prod(shape) for shape in shapes)
    sums = pl.pallas_call(
        body,
        out_shape=[jax.ShapeDtypeStruct(shape, BF16) for shape in shapes],
        in_specs=[SCALARS] + [pl.BlockSpec(memory_space=pltpu.HBM)] * len(arrays),
        out_specs=[pl.BlockSpec(memory_space=pltpu.VMEM)] * len(links),
        scratch_shapes=[pltpu.VMEM(room, BF16) for room in rooms]
        + [pltpu.SemaphoreType.DMA((copies_needed,))],
        compiler_params=pltpu.CompilerParams(vmem_limit_bytes=VMEM),
        cost_estimate=pl.CostEstimate(flops=0, bytes_accessed=moved, transcendentals=0),
    )(me, *arrays)
    return [(p, link, base) for p, link, base, _, _ in plans], dict(zip(links, sums))


def cross(a, name):
    axis, bit = ("head", 0) if name == "h" else ("clip", 1 if name == "x" else 0)
    size = lax.axis_size(axis)
    return lax.ppermute(a, axis, [(i, i ^ (1 << bit)) for i in range(size)])


def pieces_of(halves_of):
    total = sum(keep.shape[0] for keep, _ in halves_of)
    found = []
    seen = 0
    for keep, send in halves_of:
        got = cross(send, "c")
        n = keep.shape[0]
        first = min(max((total + 1) // 2 - seen, 0), n)
        if first:
            found.append(Piece(keep, got, 0, first, ("x", "h")))
        if n > first:
            found.append(Piece(keep, got, first, n - first, ("h", "x")))
        seen += n
    return found


def move(x, pieces, me, at_end=False):
    plans, sums = fold(pieces, me, at_end)
    x, sums = lax.optimization_barrier((x, sums))
    got = {}
    for link, array in sums.items():
        if link == "z":
            if at_end:
                every = lax.all_to_all(array, "seq", split_axis=0, concat_axis=0, tiled=True)
                got[link] = jnp.sum(every.astype(F32), axis=0)
            else:
                own = lax.psum_scatter(array, "seq", scatter_dimension=1, tiled=True)
                got[link] = own.astype(F32)
        else:
            got[link] = cross(array, link)
    for p, link, base in plans:
        if link == "z":
            p.result = got[link][base : base + p.n]
        else:
            p.held.append((got[link], base))
        p.step += 1
    return x


def settle(x, pieces):
    arrays = []
    for p in pieces:
        if not any(p.held[-1][0] is a for a in arrays):
            arrays.append(p.held[-1][0])
    x, came = lax.optimization_barrier((x, arrays))
    for p in pieces:
        for old, new in zip(arrays, came):
            if p.held[-1][0] is old:
                p.held[-1] = (new, p.held[-1][1])
                break
    return x


def reduce_plain(halves_of, core):
    def joined(keep, send):
        low = jnp.where(core == 0, keep, send)
        high = jnp.where(core == 0, send, keep)
        n, shares, pairs, depth, width = keep.shape
        return jnp.stack((low, high), axis=3).reshape(n, shares, 2 * pairs * depth, width)

    g = jnp.concatenate([joined(*pair) for pair in halves_of], axis=0)
    g = lax.psum_scatter(g, "head", scatter_dimension=1, tiled=True)
    g = lax.psum_scatter(g.astype(F32), ("clip", "seq"), scatter_dimension=2, tiled=True)
    return g[:, 0]


def gather_norms(gain, bias):
    layers, norms, part = gain.shape
    both = jnp.concatenate((gain, bias), axis=1).reshape(1, -1)
    count = lax.axis_size("clip") * lax.axis_size("seq") * lax.axis_size("head")
    width = round_up(both.shape[1], 128)
    padded = jnp.pad(both, ((0, 0), (0, width - both.shape[1])))
    every = lax.all_to_all(
        jnp.broadcast_to(padded, (count, width)), ALL, split_axis=0, concat_axis=0, tiled=True
    )[:, : both.shape[1]]
    return every.reshape(count, layers * 2 * norms, part).transpose(1, 0, 2).reshape(layers, 2 * norms, -1)


def reduce_norms(sums):
    count = lax.axis_size("clip") * lax.axis_size("seq") * lax.axis_size("head")
    rows, features = sums.shape
    part = features // count
    a = sums.reshape(rows, count, part).transpose(1, 0, 2).reshape(count, rows * part)
    width = round_up(rows * part, 128)
    a = jnp.pad(a, ((0, 0), (0, width - rows * part)))
    every = lax.all_to_all(a, ALL, split_axis=0, concat_axis=0, tiled=True)
    return jnp.sum(every, axis=0)[: rows * part].reshape(rows, part)


def on_device(
    tokens,
    cotangent,
    time_qkv,
    time_out,
    time_mix,
    space_qkv,
    space_out,
    mlp_in,
    mlp_out,
    norm_gain,
    norm_bias,
):
    layers = time_qkv.shape[0]
    clips, frames, places, d = tokens.shape
    ways = lax.axis_size("seq")
    shards = lax.axis_size("clip") * ways
    rows = Rows(clips * frames, places, ways)
    shares = lax.axis_size("head")

    def as_rows(a):
        a = a.astype(F32).reshape(rows.frames, places, d)
        a = jnp.pad(a, ((0, 0), (0, rows.frame_rows - places), (0, 0)))
        return a.reshape(rows.rows, d)

    def from_rows(a):
        a = a.reshape(rows.frames, rows.frame_rows, d)[:, :places]
        return a.reshape(tokens.shape)

    gbs = gather_norms(norm_gain, norm_bias)
    gb = [gbs[l] for l in range(layers)]
    packs = [
        pack_attention(time_qkv[l], time_out[l], time_mix[l], space_qkv[l], space_out[l])
        for l in range(layers)
    ]
    packs_ff = [pack_feed_forward(mlp_in[l], mlp_out[l], time_qkv.shape[3]) for l in range(layers)]
    weights = [gather_slabs(pack) for pack in packs]
    mixes = [mix_whole(w[-1], shards) for w in weights]
    quick = lax.axis_size("clip") == 4 and shares == 2 and ways == 4 and time_qkv.shape[1] % 16 == 0

    halves = Halves(lax.axis_size("clip"), d, time_qkv.shape[3])
    clip = lax.axis_index("clip")
    member = member_of(clip, lax.axis_index("seq"))
    me = jnp.stack((clip & 1, (clip >> 1) & 1, lax.axis_index("head"), member, lax.axis_index("seq"))).astype(
        jnp.int32
    )
    if quick:
        spreads = [Spread(pack, me) for pack in packs_ff]
        weights_ff = []
    else:
        weights_ff = [gather_slabs(pack) for pack in packs_ff]

    home = go_home(tokens)
    if quick:
        first = spreads[0]
        home, gb = first.step((home, gb))
    x = as_rows(home)
    send = send_first(rows, x, gb[0], me)
    kept = []
    for l in range(layers):
        w = weights[l]
        send = swap_places(send)
        if quick and l == 0:
            for _ in range(2):
                send = first.step(send)
            for spread in spreads[1:]:
                send = spread.step(send)
                send = spread.hold(send)
            send = first.step(send)
        elif quick:
            send = spreads[l].step(send)
        a1, qkv1, log1, o1_time = time_forward(rows, send, w)
        back = swap_places(o1_time)
        if quick:
            back = spreads[l].step(back)
            weights_ff.append(spreads[l].come)
            if l == 0:
                for spread in spreads[1:]:
                    back = spread.step(back)
        o1, y1, x1, qkv2 = middle_forward(rows, back, x, w, mixes[l], gb[l], me)
        o2, x2, log2 = space_forward(rows, qkv2, x1, w)
        if quick and l == 0:
            for spread in spreads[1:]:
                x2 = spread.step(x2)
        kept.append((x, a1, qkv1, log1, o1, y1, x1, qkv2, o2, log2, x2))
        if l + 1 < layers:
            x, *send = mlp_forward(rows, x2, weights_ff[l], gb[l], gb[l + 1], me)

    grad = as_rows(go_home(cotangent))
    norm_rows = [None] * layers
    summed = [None] * layers
    late = []
    for l in reversed(range(layers)):
        w = weights[l]
        x, a1, qkv1, log1, o1, y1, x1, qkv2, o2, log2, x2 = kept[l]
        grad, g_ff, s3, x3 = mlp_backward(
            rows, grad, x2, weights_ff[l], gb[l], me, halves, l + 1 == layers
        )
        if x3:
            output = go_back(from_rows(x3[0].astype(BF16)))
        if quick:
            ff = pieces_of(g_ff)
            if late:
                grad = settle(grad, late)
                grad = move(grad, late, me)
                late = [p for p in late if p.step < 3]
        grad, g_space, s2 = space_backward(rows, grad, x1, qkv2, o2, log2, w, gb[l], me, halves)
        if quick:
            space = pieces_of([g_space])
            if late:
                grad = settle(grad, late)
            grad, output = move((grad, output), ff, me)
        do1, g_out = middle_backward(rows, grad, y1, o1, w, mixes[l], me, halves, shards)
        do1 = swap_places(do1)
        if quick:
            do1 = move(do1, ff + space + late, me)
        da1, g_time = time_backward(rows, do1, a1, qkv1, log1, w, me, halves)
        if quick:
            da1 = settle(da1, ff + space)
        da1 = swap_places(da1)
        if quick:
            rest = pieces_of([g_out] + g_time)
            da1 = move(da1, ff + space + rest, me)
            late = space + rest
        grad, s1 = first_norm_back(rows, da1, x, grad, gb[l], me)
        norm_rows[l] = jnp.concatenate((s1[0:1], s2[0:1], s3[0:1], s1[1:2], s2[1:2], s3[1:2]), axis=0)
        if quick:
            summed[l] = ff + space + rest
        else:
            summed[l] = [reduce_plain(g_ff + [g_space, g_out] + g_time, clip & 1)]
    norm_sums = reduce_norms(jnp.concatenate(norm_rows, axis=0)).reshape(layers, 2, 3, -1)
    if quick:
        tokens_grad = go_back(from_rows(grad.astype(BF16)))
        tokens_grad, norm_sums = move((tokens_grad, norm_sums), late, me, True)
        move((), rest, me, True)
        summed = [[p.result for p in some] for some in summed]
    cuts = (2 * g_ff[0][0].shape[0], g_space[0].shape[0], g_out[0].shape[0], len(g_time))
    results = []
    for some in summed:
        slabs_of = jnp.concatenate(some, axis=0)
        ends = [sum(cuts[: i + 1]) for i in range(4)]
        results.append([slabs_of[e - c : e] for c, e in zip(cuts, ends)])
    if not quick:
        tokens_grad = go_back(from_rows(grad.astype(BF16)))
    tokens_grad = tokens_grad.astype(F32)

    def stacked(form):
        return jnp.stack([form(*results[l]) for l in range(layers)])

    def rows_of(a):
        return a.transpose(1, 0, 2)

    def flat(a):
        return rows_of(a).reshape(a.shape[1], -1)

    def mix_rows(a):
        r, width = a.shape
        return a.reshape(shares, r // shares, width).transpose(1, 0, 2).reshape(r // shares, -1)

    per_share = mlp_in.shape[2] // time_qkv.shape[3]
    return (
        output,
        tokens_grad,
        stacked(lambda ff, s, t, q: rows_of(q)),
        stacked(lambda ff, s, t, q: t[0].T),
        stacked(lambda ff, s, t, q: mix_rows(t[1])),
        stacked(lambda ff, s, t, q: rows_of(s[1:])),
        stacked(lambda ff, s, t, q: s[0].T),
        stacked(lambda ff, s, t, q: flat(ff[:per_share])),
        stacked(lambda ff, s, t, q: flat(ff[per_share:]).T),
        norm_sums[:, 0],
        norm_sums[:, 1],
    )


def solution(mesh):
    token_spec = P(("clip", "head"), "seq", None, None)
    in_specs = (
        token_spec,
        token_spec,
        P(None, ("clip", "seq"), None, "head"),
        P(None, "head", ("clip", "seq")),
        P(None, ("clip", "seq", "head"), None),
        P(None, ("clip", "seq"), None, "head"),
        P(None, "head", ("clip", "seq")),
        P(None, ("clip", "seq"), "head"),
        P(None, "head", ("clip", "seq")),
        P(None, None, ("clip", "seq", "head")),
        P(None, None, ("clip", "seq", "head")),
    )
    return jax.shard_map(
        on_device, mesh=mesh, in_specs=in_specs, out_specs=in_specs, check_vma=False
    )
```

```python
import functools
import math

import jax
import jax.numpy as jnp
from jax import lax
from jax.experimental import pallas as pl
from jax.experimental.pallas import tpu as pltpu
from jax.sharding import PartitionSpec as P

HEAD_DIM = 64
NORM_EPS = 1e-06
HALF_ROOT = 0.7071067811865476
INV_ROOT_TAU = 0.3989422804014327
LOG2E = 1.4426950408889634
FAR = -1e30
LANES = 128
VMEM = 56 * 1024 * 1024
SHOWN = 1.0
ALL = ("clip", "seq", "head")
BF16 = jnp.bfloat16
F32 = jnp.float32


def round_up(value, step):
    return -(-value // step) * step


def nn(a, b):
    return lax.dot_general(a, b, (((1,), (0,)), ((), ())), preferred_element_type=F32)


def nt(a, b):
    return lax.dot_general(a, b, (((1,), (1,)), ((), ())), preferred_element_type=F32)


def tn(a, b):
    return lax.dot_general(a, b, (((0,), (0,)), ((), ())), preferred_element_type=F32)


def norm_parts(x):
    mean = jnp.mean(x, axis=-1, keepdims=True)
    centred = x - mean
    spread = lax.rsqrt(jnp.mean(centred * centred, axis=-1, keepdims=True) + NORM_EPS)
    return centred * spread, spread


def norm_rounded(x, gain, bias):
    hat, _ = norm_parts(x)
    return (hat * gain + bias).astype(BF16)


def norm_back(u, x, gain):
    hat, spread = norm_parts(x)
    scaled = u * gain
    mean_scaled = jnp.mean(scaled, axis=-1, keepdims=True)
    mean_cross = jnp.mean(scaled * hat, axis=-1, keepdims=True)
    change = spread * (scaled - mean_scaled - hat * mean_cross)
    sums = jnp.concatenate(
        (jnp.sum(u * hat, axis=0, keepdims=True), jnp.sum(u, axis=0, keepdims=True)), axis=0
    )
    return change, sums


class Rows:
    def __init__(self, frames, places, ways):
        self.frames = frames
        self.places = places
        self.ways = ways
        self.frame_rows = round_up(places, 16)
        self.rows = frames * self.frame_rows
        self.block = places // ways
        self.chunk = round_up(frames * self.block, 8)
        self.time_rows = ways * self.chunk

    def split(self, r):
        way = jnp.zeros_like(r)
        for k in range(1, self.ways):
            way = way + (r >= k * self.chunk).astype(jnp.int32)
        rest = r - way * self.chunk
        frame = jnp.zeros_like(r)
        for k in range(1, self.frames):
            frame = frame + (rest >= k * self.block).astype(jnp.int32)
        real = rest < self.frames * self.block
        return way, frame, rest - frame * self.block, real

    def to_time(self, k, member):
        r = lax.broadcasted_iota(jnp.int32, (self.chunk, 1), 0)
        _, frame, place, real = self.split(r)
        way = jnp.bitwise_xor(member, k)
        source = jnp.where(real, frame * self.frame_rows + way * self.block + place, -1)
        c = lax.broadcasted_iota(jnp.int32, (self.chunk, self.rows), 1)
        return jnp.where(c == source, 1.0, 0.0).astype(BF16)

    def gathered(self, chunk_refs, member):
        total = tn(self.to_time(0, member), chunk_refs[0][...])
        for k in range(1, self.ways):
            total = total + tn(self.to_time(k, member), chunk_refs[k][...])
        return total

    def chunks(self, width, block=None, index=None):
        return [
            made((self.chunk, width), BF16)
            if block is None
            else made((self.chunk, width), BF16, (self.chunk, block), index)
            for _ in range(self.ways)
        ]

    def time_bias(self):
        def label(r):
            _, _, place, real = self.split(r)
            return jnp.where(real, place, -1)

        a = label(lax.broadcasted_iota(jnp.int32, (self.time_rows, 1), 0))
        b = label(lax.broadcasted_iota(jnp.int32, (1, self.time_rows), 1))
        return jnp.where(a == b, 0.0, FAR).astype(F32)

    def space_bias(self):
        a = lax.broadcasted_iota(jnp.int32, (self.frame_rows, 1), 0)
        return jnp.where(a < self.places, 0.0, FAR).astype(F32)


def lane_masks(rows):
    lane = lax.broadcasted_iota(jnp.int32, (rows, LANES), 1)
    return lane < HEAD_DIM


def one_of(value, low, half):
    zero = jnp.zeros_like(value)
    return jnp.where(low, value, zero) if half == 0 else jnp.where(low, zero, value)


def pair_forward(q, k, v, bias, rate):
    low = lane_masks(q.shape[0])
    mixed, logs = [], []
    for half in range(2):
        s = nt(k, one_of(q, low, half)) + bias
        peak = jnp.max(s, axis=0, keepdims=True)
        e = jnp.exp2((s - peak) * rate)
        total = jnp.sum(e, axis=0, keepdims=True)
        soft = (e * (1.0 / total)).astype(BF16)
        mixed.append(tn(soft, v))
        logs.append(peak * rate + jnp.log2(total))
    return jnp.where(low, mixed[0], mixed[1]).astype(BF16), logs


def pair_backward(q, k, v, do, logs, bias, rate, scale):
    low = lane_masks(q.shape[0])
    dq, dk, dv = [], [], []
    for half in range(2):
        s = nt(k, one_of(q, low, half)) + bias
        soft = jnp.exp2(s * rate - logs[half])
        dp = nt(v, one_of(do, low, half))
        ds = (soft * (dp - jnp.sum(soft * dp, axis=0, keepdims=True))).astype(BF16)
        dv.append(nn(soft.astype(BF16), do))
        dk.append(nn(ds, q))
        dq.append(tn(ds, k))
    return (
        (jnp.where(low, dq[0], dq[1]) * scale).astype(BF16),
        (jnp.where(low, dk[0], dk[1]) * scale).astype(BF16),
        jnp.where(low, dv[0], dv[1]).astype(BF16),
    )


def split_rows(value, keep_ref, send_ref, at, room_ref, me_ref):
    mine = me_ref[0]
    room_ref[...] = value.reshape(room_ref.shape)
    keep_ref[at] = room_ref[:, mine].astype(BF16)
    send_ref[at] = room_ref[:, 1 - mine].astype(BF16)


def store_by_core(ref, value, halves):
    n = halves.rows
    for core in range(2):
        for pair in range(halves.pairs):
            first = (2 * pair + core) * n
            ref[core, pair * n : (pair + 1) * n] = value[first : first + n]


def split_product(left_ref, right, keep_ref, send_ref, at, me_ref):
    mine = me_ref[0]
    shape = keep_ref.shape[len(at) :]
    keep_ref[at] = nn(left_ref[mine], right).reshape(shape).astype(BF16)
    send_ref[at] = nn(left_ref[1 - mine], right).reshape(shape).astype(BF16)


class Halves:
    def __init__(self, clips, depth, width):
        self.pairs = clips // 2
        self.rows = depth // clips
        self.width = width

    def array(self, lead, block, index):
        tail = (self.pairs, self.rows, self.width)
        one = lambda: made(lead + tail, BF16, block + tail, lambda *g: index(*g) + (0, 0, 0))
        return [one(), one()]

    def turned(self, columns):
        return pltpu.VMEM((2, self.pairs * self.rows, columns), BF16)

    def room(self):
        return pltpu.VMEM((self.pairs, 2, self.rows, self.width), F32)


SCALARS = pl.BlockSpec(memory_space=pltpu.SMEM)


def call(body, grid, ins, outs, scratch, args, flops=0):
    specs = [spec for spec in ins]
    moved = sum(math.prod(o.shape) * o.dtype.itemsize for o, _ in outs)
    moved += sum(math.prod(a.shape) * a.dtype.itemsize for a in args)
    return pl.pallas_call(
        body,
        out_shape=[shape for shape, _ in outs],
        grid=grid,
        in_specs=specs,
        out_specs=[spec for _, spec in outs],
        scratch_shapes=scratch,
        compiler_params=pltpu.CompilerParams(vmem_limit_bytes=VMEM),
        cost_estimate=pl.CostEstimate(
            flops=int(flops * SHOWN), bytes_accessed=int(moved * SHOWN), transcendentals=0
        ),
    )(*args)


def whole(shape):
    zeros = (0,) * len(shape)
    return pl.BlockSpec(shape, lambda *_: zeros)


def made(shape, dtype, block=None, index=None):
    spec = whole(shape) if block is None else pl.BlockSpec(block, index)
    return jax.ShapeDtypeStruct(shape, dtype), spec


def slabs(count, first, width, depth):
    return pl.BlockSpec((count, 1, depth, width), lambda h, *_: (first // count, h, 0, 0))


def send_first(rows, x, gb, me):
    def body(me_ref, x_ref, gb_ref, *out_refs):
        a = norm_rounded(x_ref[...], gb_ref[0:1], gb_ref[3:4])
        for k in range(rows.ways):
            out_refs[k][...] = nn(rows.to_time(k, me_ref[3]), a).astype(BF16)

    d = x.shape[1]
    return call(
        body, (1,), [SCALARS, whole(x.shape), whole(gb.shape)], rows.chunks(d), [], (me, x, gb)
    )


def time_forward(rows, chunks, w):
    t, d = rows.time_rows, chunks[0].shape[1]
    width = w.shape[3]
    shares = w.shape[1]
    pairs = width // LANES
    ways = rows.ways
    rate = LOG2E / math.sqrt(HEAD_DIM)

    def body(*refs):
        chunk_refs = refs[:ways]
        w_ref, a_ref, qkv_ref, log_ref = refs[ways : ways + 4]
        out_refs = refs[ways + 4 : 2 * ways + 4]
        bias_ref, mixed_ref = refs[2 * ways + 4 :]

        @pl.when(pl.program_id(0) == 0)
        def _():
            bias_ref[...] = rows.time_bias()
            for k in range(ways):
                a_ref[k * rows.chunk : (k + 1) * rows.chunk] = chunk_refs[k][...]

        act = a_ref[...]
        for g in range(3):
            qkv_ref[g] = nn(act, w_ref[g, 0]).astype(BF16)

        @pl.loop(0, pairs)
        def _(i):
            lanes = pl.ds(pl.multiple_of(i * LANES, LANES), LANES)
            mixed, logs = pair_forward(
                qkv_ref[0, :, lanes], qkv_ref[1, :, lanes], qkv_ref[2, :, lanes], bias_ref[...], rate
            )
            mixed_ref[:, lanes] = mixed
            log_ref[0, i] = jnp.concatenate(logs, axis=0)

        for k in range(ways):
            out_refs[k][...] = mixed_ref[k * rows.chunk : (k + 1) * rows.chunk]

    got = call(
        body,
        (shares,),
        [whole(c.shape) for c in chunks] + [slabs(3, 0, width, d)],
        [
            made((t, d), BF16),
            made((3, t, d), BF16, (3, t, width), lambda h: (0, 0, h)),
            made((shares, pairs, 2, t), F32, (1, pairs, 2, t), lambda h: (h, 0, 0, 0)),
            *rows.chunks(d, width, lambda h: (0, h)),
        ],
        [pltpu.VMEM((t, t), F32), pltpu.VMEM((t, width), BF16)],
        (*chunks, w),
        flops=2 * t * d * 3 * d,
    )
    return got[0], got[1], got[2], got[3:]


def middle_forward(rows, back, x, w, mix, gb, me):
    t, d = x.shape
    width = w.shape[3]
    shares = w.shape[1]

    def body(me_ref, *refs):
        x_ref, to_ref, sq_ref, mix_ref, gb_ref, o1_ref, y1_ref, x1_ref, qkv_ref = refs[rows.ways :]
        o1 = rows.gathered(refs[: rows.ways], me_ref[3]).astype(BF16)
        o1_ref[...] = o1
        y1 = jnp.zeros((t, d), F32)
        for h in range(shares):
            y1 = y1 + nt(o1[:, h * width : (h + 1) * width], to_ref[0, h])
        y1 = y1.astype(BF16)
        y1_ref[...] = y1
        x1 = x_ref[...] + nn(y1, mix_ref[...])
        x1_ref[...] = x1
        a2 = norm_rounded(x1, gb_ref[1:2], gb_ref[4:5])
        for g in range(3):
            for h in range(shares):
                qkv_ref[g, :, h * width : (h + 1) * width] = nn(a2, sq_ref[g, h]).astype(BF16)

    return call(
        body,
        (1,),
        [
            SCALARS,
            *(whole(c.shape) for c in back),
            whole(x.shape),
            pl.BlockSpec((1, shares, d, width), lambda i: (6, 0, 0, 0)),
            pl.BlockSpec((3, shares, d, width), lambda i: (1, 0, 0, 0)),
            whole(mix.shape),
            whole(gb.shape),
        ],
        [made((t, d), BF16), made((t, d), BF16), made((t, d), F32), made((3, t, d), BF16)],
        [],
        (me, *back, x, w, w, mix, gb),
        flops=2 * t * d * 5 * d,
    )


def space_forward(rows, qkv, x1, w):
    t, d = x1.shape
    width = w.shape[3]
    shares = w.shape[1]
    pairs = width // LANES
    rate = LOG2E / math.sqrt(HEAD_DIM)
    n = rows.frame_rows

    def body(qkv_ref, x1_ref, w_ref, o2_ref, x2_ref, log_ref):
        bias = rows.space_bias()

        @pl.loop(0, pairs)
        def _(i):
            lanes = pl.ds(pl.multiple_of(i * LANES, LANES), LANES)
            for f in range(rows.frames):
                at = slice(f * n, (f + 1) * n)
                mixed, logs = pair_forward(
                    qkv_ref[0, at, lanes], qkv_ref[1, at, lanes], qkv_ref[2, at, lanes], bias, rate
                )
                o2_ref[at, lanes] = mixed
                log_ref[0, i, f] = jnp.concatenate(logs, axis=0)

        @pl.when(pl.program_id(0) == 0)
        def _():
            x2_ref[...] = x1_ref[...]

        x2_ref[...] += nt(o2_ref[...], w_ref[0, 0])

    return call(
        body,
        (shares,),
        [
            pl.BlockSpec((3, t, width), lambda h: (0, 0, h)),
            whole(x1.shape),
            slabs(1, 7, width, d),
        ],
        [
            made((t, d), BF16, (t, width), lambda h: (0, h)),
            made((t, d), F32),
            made(
                (shares, pairs, rows.frames, 2, n),
                F32,
                (1, pairs, rows.frames, 2, n),
                lambda h: (h, 0, 0, 0, 0),
            ),
        ],
        [],
        (qkv, x1, w),
        flops=2 * t * d * d,
    )


def ff_slab(first, per_share, depth, width):
    return pl.BlockSpec(
        (1, 1, depth, width), lambda j: (first + j % per_share, j // per_share, 0, 0)
    )


def mlp_forward(rows, x2, w, per_share, gb, gb_next, me):
    t, d = x2.shape
    width = w.shape[3]
    shares = w.shape[1]
    base = w.shape[0] - 2 * per_share
    steps = shares * per_share

    def body(x2_ref, wi_ref, wo_ref, gb_ref, me_ref, gn_ref, x3_ref, *rest):
        send_refs, a3_ref = rest[:-1], rest[-1]
        j = pl.program_id(0)

        @pl.when(j == 0)
        def _():
            a3_ref[...] = norm_rounded(x2_ref[...], gb_ref[2:3], gb_ref[5:6])
            x3_ref[...] = x2_ref[...]

        hid = nn(a3_ref[...], wi_ref[0, 0])
        act = (0.5 * hid * (1.0 + lax.erf(hid * HALF_ROOT))).astype(BF16)
        x3_ref[...] += nt(act, wo_ref[0, 0])

        @pl.when(j == steps - 1)
        def _():
            a = norm_rounded(x3_ref[...], gn_ref[0:1], gn_ref[3:4])
            for k in range(rows.ways):
                send_refs[k][...] = nn(rows.to_time(k, me_ref[3]), a).astype(BF16)

    ins = [
        whole(x2.shape),
        ff_slab(base, per_share, d, width),
        ff_slab(base + per_share, per_share, d, width),
        whole(gb.shape),
    ]
    ins += [SCALARS, whole(gb_next.shape)]
    outs = [made((t, d), F32)] + rows.chunks(d)
    args = (x2, w, w, gb, me, gb_next)
    return call(
        body, (steps,), ins, outs, [pltpu.VMEM((t, d), BF16)], args, flops=4 * t * d * width * steps
    )


def mlp_backward(rows, grad, x2, w, per_share, gb, me, halves, with_output):
    t, d = x2.shape
    width = w.shape[3]
    shares = w.shape[1]
    base = w.shape[0] - 2 * per_share
    steps = shares * per_share

    def body(me_ref, g_ref, x2_ref, wi_ref, wo_ref, gb_ref, go_ref, ki_ref, si_ref, ko_ref, so_ref, sums_ref, *rest):
        if with_output:
            x3_ref, *rest = rest
        a3_ref, a3t_ref, e3_ref, e3t_ref, u_ref = rest
        j = pl.program_id(0)

        @pl.when(j == 0)
        def _():
            hat, _ = norm_parts(x2_ref[...])
            a3 = hat * gb_ref[2:3] + gb_ref[5:6]
            a3_ref[...] = a3.astype(BF16)
            store_by_core(a3t_ref, a3.T.astype(BF16), halves)
            g = g_ref[...]
            e3_ref[...] = g.astype(BF16)
            store_by_core(e3t_ref, g.T.astype(BF16), halves)
            u_ref[...] = jnp.zeros((t, d), F32)
            if with_output:
                x3_ref[...] = x2_ref[...]

        hid = nn(a3_ref[...], wi_ref[0, 0])
        phi = 0.5 * (1.0 + lax.erf(hid * HALF_ROOT))
        act = (hid * phi).astype(BF16)
        slope = phi + hid * jnp.exp(-0.5 * hid * hid) * INV_ROOT_TAU
        dhid = (nn(e3_ref[...], wo_ref[0, 0]) * slope).astype(BF16)
        split_product(e3t_ref, act, ko_ref, so_ref, (0, 0), me_ref)
        split_product(a3t_ref, dhid, ki_ref, si_ref, (0, 0), me_ref)
        u_ref[...] += nt(dhid, wi_ref[0, 0])
        if with_output:
            x3_ref[...] += nt(act, wo_ref[0, 0])

        @pl.when(j == steps - 1)
        def _():
            change, sums = norm_back(u_ref[...], x2_ref[...], gb_ref[2:3])
            go_ref[...] = g_ref[...] + change
            sums_ref[...] = sums

    slab_outs = [
        one
        for _ in range(2)
        for one in halves.array(
            (per_share, shares), (1, 1), lambda j: (j % per_share, j // per_share)
        )
    ]
    grad, ki, si, ko, so, sums, *x3 = call(
        body,
        (steps,),
        [
            SCALARS,
            whole(grad.shape),
            whole(x2.shape),
            ff_slab(base, per_share, d, width),
            ff_slab(base + per_share, per_share, d, width),
            whole(gb.shape),
        ],
        [made((t, d), F32), *slab_outs, made((2, d), F32)] + [made((t, d), F32)] * with_output,
        [
            pltpu.VMEM((t, d), BF16),
            halves.turned(t),
            pltpu.VMEM((t, d), BF16),
            halves.turned(t),
            pltpu.VMEM((t, d), F32),
        ],
        (me, grad, x2, w, w, gb),
        flops=10 * t * d * width * steps,
    )
    return grad, [(ki, si), (ko, so)], sums, x3


def space_backward(rows, grad, x1, qkv, o2, logs, w, gb, me, halves):
    t, d = x1.shape
    width = w.shape[3]
    shares = w.shape[1]
    pairs = width // LANES
    scale = 1.0 / math.sqrt(HEAD_DIM)
    rate = LOG2E * scale
    n = rows.frame_rows

    def body(me_ref, g_ref, x1_ref, qkv_ref, o2_ref, log_ref, wo_ref, wq_ref, gb_ref, go_ref, keep_ref, send_ref, sums_ref, e2_ref, e2t_ref, a2t_ref, do_ref, dqkv_ref, u_ref):
        h = pl.program_id(0)

        @pl.when(h == 0)
        def _():
            g = g_ref[...]
            e2_ref[...] = g.astype(BF16)
            store_by_core(e2t_ref, g.T.astype(BF16), halves)
            hat, _ = norm_parts(x1_ref[...])
            store_by_core(a2t_ref, (hat * gb_ref[1:2] + gb_ref[4:5]).T.astype(BF16), halves)
            u_ref[...] = jnp.zeros((t, d), F32)

        bias = rows.space_bias()
        split_product(e2t_ref, o2_ref[...], keep_ref, send_ref, (0, 0), me_ref)
        do_ref[...] = nn(e2_ref[...], wo_ref[0, 0]).astype(BF16)

        @pl.loop(0, pairs)
        def _(i):
            lanes = pl.ds(pl.multiple_of(i * LANES, LANES), LANES)
            for f in range(rows.frames):
                at = slice(f * n, (f + 1) * n)
                log = log_ref[0, i, f]
                grads = pair_backward(
                    qkv_ref[0, at, lanes],
                    qkv_ref[1, at, lanes],
                    qkv_ref[2, at, lanes],
                    do_ref[at, lanes],
                    (log[0:1], log[1:2]),
                    bias,
                    rate,
                    scale,
                )
                for part in range(3):
                    dqkv_ref[part, at, lanes] = grads[part]

        for part in range(3):
            split_product(a2t_ref, dqkv_ref[part], keep_ref, send_ref, (part + 1, 0), me_ref)
            u_ref[...] += nt(dqkv_ref[part], wq_ref[part, 0])

        @pl.when(h == shares - 1)
        def _():
            change, sums = norm_back(u_ref[...], x1_ref[...], gb_ref[1:2])
            go_ref[...] = g_ref[...] + change
            sums_ref[...] = sums

    grad, keep, send, sums = call(
        body,
        (shares,),
        [
            SCALARS,
            whole(grad.shape),
            whole(x1.shape),
            pl.BlockSpec((3, t, width), lambda h: (0, 0, h)),
            pl.BlockSpec((t, width), lambda h: (0, h)),
            pl.BlockSpec((1,) + logs.shape[1:], lambda h: (h, 0, 0, 0, 0)),
            slabs(1, 7, width, d),
            slabs(3, 3, width, d),
            whole(gb.shape),
        ],
        [
            made((t, d), F32),
            *halves.array((4, shares), (4, 1), lambda h: (0, h)),
            made((2, d), F32),
        ],
        [
            pltpu.VMEM((t, d), BF16),
            halves.turned(t),
            halves.turned(t),
            pltpu.VMEM((t, width), BF16),
            pltpu.VMEM((3, t, width), BF16),
            pltpu.VMEM((t, d), F32),
        ],
        (me, grad, x1, qkv, o2, logs, w, w, gb),
        flops=2 * t * d * d * 8,
    )
    return grad, (keep, send), sums


def mix_fits(depth, shards, shares):
    return depth // (shards * shares) % 8 == 0


def middle_backward(rows, grad, y1, o1, w, mix, me, halves, shards):
    t, d = grad.shape
    width = w.shape[3]
    shares = w.shape[1]
    fits = mix_fits(d, shards, shares)
    part = d // (shards * shares)

    def body(me_ref, g_ref, y1_ref, o1_ref, to_ref, mix_ref, *rest):
        send_refs, rest = rest[: rows.ways], rest[rows.ways :]
        gk_ref, gs_ref, *rest = rest
        if fits:
            room_ref, order_ref = rest
        else:
            gm_ref, room_ref = rest
        e1 = g_ref[...].astype(BF16)
        dy1 = nt(e1, mix_ref[...]).astype(BF16)
        sends = [rows.to_time(k, me_ref[3]) for k in range(rows.ways)]
        for h in range(shares):
            lanes = slice(h * width, (h + 1) * width)
            do1 = nn(dy1, to_ref[0, h]).astype(BF16)
            for k in range(rows.ways):
                send_refs[k][:, lanes] = nn(sends[k], do1).astype(BF16)
            split_rows(tn(dy1, o1_ref[:, lanes]), gk_ref, gs_ref, (0, h), room_ref, me_ref)
        gm = tn(y1_ref[...], e1)
        if fits:
            gm = gm.reshape(shards, shares, part, d)
            for h in range(shares):
                for half in range(shares):
                    order_ref[:, half] = gm[:, h, :, half * width : (half + 1) * width]
                split_rows(order_ref[...], gk_ref, gs_ref, (1, h), room_ref, me_ref)
        else:
            gm_ref[...] = gm.astype(BF16)

    outs = rows.chunks(d)
    outs += halves.array((1 + fits, shares), (1 + fits, shares), lambda i: (0, 0))
    scratch = [halves.room()]
    if fits:
        scratch.append(pltpu.VMEM((shards, shares, part, width), F32))
    else:
        outs.append(made((d, d), BF16))
    got = call(
        body,
        (1,),
        [
            SCALARS,
            whole(grad.shape),
            whole(y1.shape),
            whole(o1.shape),
            pl.BlockSpec((1, shares, d, width), lambda i: (6, 0, 0, 0)),
            whole(mix.shape),
        ],
        outs,
        scratch,
        (me, grad, y1, o1, w, mix),
        flops=8 * t * d * d,
    )
    do1, (keep, send) = got[: rows.ways], got[rows.ways : rows.ways + 2]
    if not fits:
        gm = mix_slab(got[-1], shards, shares).reshape((1, shares, halves.pairs, 2) + keep.shape[3:])
        keep = jnp.concatenate((keep, lax.dynamic_index_in_dim(gm, me[0], 3, keepdims=False)), axis=0)
        send = jnp.concatenate((send, lax.dynamic_index_in_dim(gm, 1 - me[0], 3, keepdims=False)), axis=0)
    return do1, (keep, send)


def time_backward(rows, do1, a, qkv, logs, w, me, halves):
    t, d = a.shape
    width = w.shape[3]
    shares = w.shape[1]
    pairs = width // LANES
    scale = 1.0 / math.sqrt(HEAD_DIM)
    rate = LOG2E * scale

    def body(me_ref, *refs):
        do_refs, refs = refs[: rows.ways], refs[rows.ways :]
        a_ref, qkv_ref, log_ref, w_ref = refs[:4]
        out_refs, refs = refs[4 : 4 + rows.ways], refs[4 + rows.ways :]
        half_refs, refs = refs[:6], refs[6:]
        bias_ref, dqkv_ref, at_ref, u_ref, do_ref = refs
        h = pl.program_id(0)

        @pl.when(h == 0)
        def _():
            bias_ref[...] = rows.time_bias()
            store_by_core(at_ref, a_ref[...].T, halves)
            u_ref[...] = jnp.zeros((t, d), F32)

        for k in range(rows.ways):
            do_ref[k * rows.chunk : (k + 1) * rows.chunk] = do_refs[k][...]

        @pl.loop(0, pairs)
        def _(i):
            lanes = pl.ds(pl.multiple_of(i * LANES, LANES), LANES)
            log = log_ref[0, i]
            grads = pair_backward(
                qkv_ref[0, :, lanes],
                qkv_ref[1, :, lanes],
                qkv_ref[2, :, lanes],
                do_ref[:, lanes],
                (log[0:1], log[1:2]),
                bias_ref[...],
                rate,
                scale,
            )
            for part in range(3):
                dqkv_ref[part, :, lanes] = grads[part]

        for part in range(3):
            split_product(
                at_ref, dqkv_ref[part], half_refs[2 * part], half_refs[2 * part + 1], (0, 0), me_ref
            )
            u_ref[...] += nt(dqkv_ref[part], w_ref[part, 0])

        @pl.when(h == shares - 1)
        def _():
            for k in range(rows.ways):
                out_refs[k][...] = u_ref[k * rows.chunk : (k + 1) * rows.chunk].astype(BF16)

    got = call(
        body,
        (shares,),
        [
            SCALARS,
            *(pl.BlockSpec((rows.chunk, width), lambda h: (0, h)) for _ in do1),
            whole(a.shape),
            pl.BlockSpec((3, t, width), lambda h: (0, 0, h)),
            pl.BlockSpec((1,) + logs.shape[1:], lambda h: (h, 0, 0, 0)),
            slabs(3, 0, width, d),
        ],
        [
            *rows.chunks(d),
            *(one for _ in range(3) for one in halves.array((1, shares), (1, 1), lambda h: (0, h))),
        ],
        [
            pltpu.VMEM((t, t), F32),
            pltpu.VMEM((3, t, width), BF16),
            halves.turned(t),
            pltpu.VMEM((t, d), F32),
            pltpu.VMEM((t, width), BF16),
        ],
        (me, *do1, a, qkv, logs, w),
        flops=2 * t * d * d * 6,
    )
    parts = got[rows.ways :]
    return got[: rows.ways], [tuple(parts[i : i + 2]) for i in (0, 2, 4)]


def first_norm_back(rows, back, x, grad, gb, me):
    t, d = x.shape

    def body(me_ref, *refs):
        x_ref, g_ref, gb_ref, go_ref, sums_ref = refs[rows.ways :]
        u = rows.gathered(refs[: rows.ways], me_ref[3])
        change, sums = norm_back(u, x_ref[...], gb_ref[0:1])
        go_ref[...] = g_ref[...] + change
        sums_ref[...] = sums

    return call(
        body,
        (1,),
        [SCALARS, *(whole(c.shape) for c in back), whole(x.shape), whole(grad.shape), whole(gb.shape)],
        [made((t, d), F32), made((2, d), F32)],
        [],
        (me, *back, x, grad, gb),
    )


def homes():
    clips, ways = lax.axis_size("clip"), lax.axis_size("seq")
    pairs = []
    for clip in range(clips):
        for seq in range(ways):
            home_clip = clip - clip % 2 + seq % 2
            home_seq = seq // 2 + (ways // 2) * (clip % 2)
            pairs.append((clip * ways + seq, home_clip * ways + home_seq))
    return pairs


def go_home(a):
    return lax.ppermute(a, ("clip", "seq"), homes())


def go_back(a):
    return lax.ppermute(a, ("clip", "seq"), [(home, device) for device, home in homes()])


def member_of(clip, seq):
    return clip % 2 + 2 * (seq % (lax.axis_size("seq") // 2))


def swap_places(chunks):
    clips, ways = lax.axis_size("clip"), lax.axis_size("seq")
    got = [chunks[0]]
    for k in range(1, ways):
        pairs = []
        for clip in range(clips):
            for seq in range(ways):
                other = member_of(clip, seq) ^ k
                to_clip = clip - clip % 2 + other % 2
                to_seq = seq - seq % (ways // 2) + other // 2
                pairs.append((clip * ways + seq, to_clip * ways + to_seq))
        got.append(lax.ppermute(chunks[k], ("clip", "seq"), pairs))
    return got


def columns(a, r, width):
    return a.reshape(r, -1, width).transpose(1, 0, 2)


def pack_attention(time_qkv, time_out, time_mix, space_qkv, space_out):
    r, _, width = time_qkv.shape
    mix = time_mix.reshape(-1, time_mix.shape[1] // width, width).transpose(1, 0, 2).reshape(1, r, width)
    return jnp.concatenate(
        (
            columns(time_qkv, r, width),
            columns(space_qkv, r, width),
            time_out.T[None],
            space_out.T[None],
            mix,
        ),
        axis=0,
    )


def pack_feed_forward(mlp_in, mlp_out, width):
    r = mlp_in.shape[0]
    return jnp.concatenate((columns(mlp_in, r, width), columns(mlp_out.T, r, width)), axis=0)


def gather_slabs(pack):
    full = lax.all_gather(pack, ("head", "clip", "seq"), axis=1, tiled=True)
    return full.reshape(pack.shape[0], lax.axis_size("head"), -1, pack.shape[2])


def spread_steps(pack, me):
    ways, clips = lax.axis_size("seq"), lax.axis_size("clip")
    shares = lax.axis_size("head")
    n, r, width = pack.shape
    pack = yield pack
    turned = [pack] + [
        lax.ppermute(pack, "seq", [(i, (i + k) % ways) for i in range(ways)]) for k in range(1, ways)
    ]
    turned = yield turned
    orders = (((0, 1), "x", "h"), ((3, 2), "h", "x"))
    some = [jnp.stack([turned[k] for k in steps]) for steps, _, _ in orders]
    come = yield [cross(a, first) for a, (_, first, _) in zip(some, orders)]
    some = [jnp.concatenate(pair, axis=0) for pair in zip(some, come)]
    come = yield [cross(a, second) for a, (_, _, second) in zip(some, orders)]
    runs = []
    for mine, other, (steps, first, second) in zip(some, come, orders):
        where = [(k, {first: f}) for f in (0, 1) for k in steps]
        for g, blocks in enumerate((mine, other)):
            runs.append((blocks, [(k, {**at, second: g}) for k, at in where], 0))
    come = yield [cross(blocks, "c") for blocks, _, _ in runs]
    runs += [(far, where, 1) for far, (_, where, _) in zip(come, runs)]
    count = sum(len(where) for _, where, _ in runs)

    def body(me_ref, *refs):
        sources, out_ref, sems = refs[: len(runs)], refs[-2], refs[-1]
        copies = []
        for source, (_, where, core) in zip(sources, runs):
            for i, (k, at) in enumerate(where):
                share = jnp.bitwise_xor(me_ref[2], at["h"])
                clip = 2 * jnp.bitwise_xor(me_ref[1], at["x"]) + jnp.bitwise_xor(me_ref[0], core)
                seq = lax.rem(me_ref[4] + (ways - k), ways)
                copies.append(
                    pltpu.make_async_copy(
                        source.at[i], out_ref.at[:, share, clip * ways + seq], sems.at[len(copies)]
                    )
                )
        for copy in copies:
            copy.start()
        for copy in copies:
            copy.wait()

    full = pl.pallas_call(
        body,
        out_shape=jax.ShapeDtypeStruct((n, shares, clips * ways, r, width), BF16),
        in_specs=[SCALARS] + [pl.BlockSpec(memory_space=pltpu.HBM)] * len(runs),
        out_specs=pl.BlockSpec(memory_space=pltpu.VMEM),
        scratch_shapes=[pltpu.SemaphoreType.DMA((count,))],
        compiler_params=pltpu.CompilerParams(vmem_limit_bytes=VMEM),
        cost_estimate=pl.CostEstimate(
            flops=0, bytes_accessed=4 * n * shares * clips * ways * r * width, transcendentals=0
        ),
    )(me, *(blocks for blocks, _, _ in runs))
    yield full.reshape(n, shares, clips * ways * r, width)


class Spread:
    def __init__(self, pack, me):
        self.way = spread_steps(pack, me)
        self.come = next(self.way)

    def hold(self, x):
        x, self.come = lax.optimization_barrier((x, self.come))
        return x

    def step(self, x):
        x = self.hold(x)
        self.come = self.way.send(self.come)
        return x


def mix_whole(slab, shards):
    shares, depth, width = slab.shape
    part = slab.reshape(shares, shards, shares, depth // (shards * shares), width)
    return part.transpose(1, 0, 3, 2, 4).reshape(depth, shares * width)


def mix_slab(whole_grad, shards, shares):
    depth, full = whole_grad.shape
    width = full // shares
    part = whole_grad.reshape(shards, shares, depth // (shards * shares), shares, width)
    return part.transpose(1, 0, 3, 2, 4).reshape(1, shares, depth, width)


class Piece:
    def __init__(self, keep, got, first, n, order):
        self.near = (keep, got)
        self.first = first
        self.n = n
        self.order = order
        self.step = 0
        self.held = []
        self.result = None


PLACE = {"x": 1, "h": 2}


def fold(pieces, me, last_by_rows):
    ways = lax.axis_size("seq")
    depth, width = pieces[0].near[0].shape[-2:]
    r = depth // ways
    used = {}
    arrays = []

    def number(a):
        for i, known in enumerate(arrays):
            if known is a:
                return i
        arrays.append(a)
        return len(arrays) - 1

    plans = []
    for p in pieces:
        link = p.order[p.step] if p.step < 2 else "z"
        blocks = p.n * (2 if p.step == 0 else 1)
        base = used.get(link, 0)
        used[link] = base + blocks
        near = [number(a) for a in p.near]
        held = [(number(a), at) for a, at in p.held]
        plans.append((p, link, base, near, held))
    links = sorted(used)
    shapes = [
        (ways, used[k], r, width) if k == "z" and last_by_rows else (used[k], depth, width)
        for k in links
    ]
    rooms, counts = [], []
    for p, link, base, near, held in plans:
        each = 2 if p.step == 0 else 1
        counts.append((each, len(near) + len(held)))
        rooms += [(each * p.n, depth, width)] * (len(near) + len(held))
    copies_needed = sum(each * terms for each, terms in counts)

    def body(me_ref, *refs):
        sources = refs[: len(arrays)]
        outs = dict(zip(links, refs[len(arrays) : len(arrays) + len(links)]))
        held_refs = refs[len(arrays) + len(links) : -1]
        sems = refs[-1]
        mine = {name: me_ref[PLACE[name]] for name in PLACE}
        groups = []
        room = 0
        sem = 0
        for p, link, base, near, held in plans:
            group = []
            if p.step == 0:
                for term in near:
                    for k in range(2):
                        pick = {p.order[0]: 1 - mine[p.order[0]], p.order[1]: k}
                        source = sources[term].at[pl.ds(p.first, p.n), pick["h"], pick["x"]]
                        group.append((source, held_refs[room].at[pl.ds(k * p.n, p.n)]))
                    room += 1
            else:
                last = p.order[1]
                pick = {p.order[0]: mine[p.order[0]]}
                pick[last] = 1 - mine[last] if p.step == 1 else mine[last]
                for term in near:
                    source = sources[term].at[pl.ds(p.first, p.n), pick["h"], pick["x"]]
                    group.append((source, held_refs[room]))
                    room += 1
                for i, (term, at) in enumerate(held):
                    start = at + pick[last] * p.n if i == 0 else at
                    group.append((sources[term].at[pl.ds(start, p.n)], held_refs[room]))
                    room += 1
            made_copies = []
            for source, target in group:
                made_copies.append(pltpu.make_async_copy(source, target, sems.at[sem]))
                sem += 1
            groups.append(made_copies)
        for group in groups:
            for copy in group:
                copy.start()
        room = 0
        for (p, link, base, near, held), (each, terms), group in zip(plans, counts, groups):
            these = held_refs[room : room + terms]
            room += terms
            for copy in group:
                copy.wait()

            @pl.loop(0, each * p.n)
            def _(i, these=these, base=base, out=outs[link], last=p.step == 2 and last_by_rows):
                value = these[0][i].astype(F32)
                for one in these[1:]:
                    value = value + one[i].astype(F32)
                value = value.astype(BF16)
                if last:
                    for k in range(ways):
                        out[k, base + i] = value[k * r : (k + 1) * r]
                else:
                    out[base + i] = value

    moved = sum(2 * math.prod(room) for room in rooms) + sum(2 * math.prod(shape) for shape in shapes)
    sums = pl.pallas_call(
        body,
        out_shape=[jax.ShapeDtypeStruct(shape, BF16) for shape in shapes],
        in_specs=[SCALARS] + [pl.BlockSpec(memory_space=pltpu.HBM)] * len(arrays),
        out_specs=[pl.BlockSpec(memory_space=pltpu.VMEM)] * len(links),
        scratch_shapes=[pltpu.VMEM(room, BF16) for room in rooms]
        + [pltpu.SemaphoreType.DMA((copies_needed,))],
        compiler_params=pltpu.CompilerParams(vmem_limit_bytes=VMEM),
        cost_estimate=pl.CostEstimate(flops=0, bytes_accessed=moved, transcendentals=0),
    )(me, *arrays)
    return [(p, link, base) for p, link, base, _, _ in plans], dict(zip(links, sums))


def cross(a, name):
    axis, bit = ("head", 0) if name == "h" else ("clip", 1 if name == "x" else 0)
    size = lax.axis_size(axis)
    return lax.ppermute(a, axis, [(i, i ^ (1 << bit)) for i in range(size)])


def pieces_of(halves_of):
    total = sum(keep.shape[0] for keep, _ in halves_of)
    found = []
    seen = 0
    for keep, send in halves_of:
        got = cross(send, "c")
        n = keep.shape[0]
        first = min(max((total + 1) // 2 - seen, 0), n)
        if first:
            found.append(Piece(keep, got, 0, first, ("x", "h")))
        if n > first:
            found.append(Piece(keep, got, first, n - first, ("h", "x")))
        seen += n
    return found


def move(x, pieces, me, at_end=False):
    plans, sums = fold(pieces, me, at_end)
    x, sums = lax.optimization_barrier((x, sums))
    got = {}
    for link, array in sums.items():
        if link == "z":
            if at_end:
                every = lax.all_to_all(array, "seq", split_axis=0, concat_axis=0, tiled=True)
                got[link] = jnp.sum(every.astype(F32), axis=0)
            else:
                own = lax.psum_scatter(array, "seq", scatter_dimension=1, tiled=True)
                got[link] = own.astype(F32)
        else:
            got[link] = cross(array, link)
    for p, link, base in plans:
        if link == "z":
            p.result = got[link][base : base + p.n]
        else:
            p.held.append((got[link], base))
        p.step += 1
    return x


def settle(x, pieces):
    arrays = []
    for p in pieces:
        if not any(p.held[-1][0] is a for a in arrays):
            arrays.append(p.held[-1][0])
    x, came = lax.optimization_barrier((x, arrays))
    for p in pieces:
        for old, new in zip(arrays, came):
            if p.held[-1][0] is old:
                p.held[-1] = (new, p.held[-1][1])
                break
    return x


def reduce_plain(halves_of, core):
    def joined(keep, send):
        low = jnp.where(core == 0, keep, send)
        high = jnp.where(core == 0, send, keep)
        n, shares, pairs, depth, width = keep.shape
        return jnp.stack((low, high), axis=3).reshape(n, shares, 2 * pairs * depth, width)

    g = jnp.concatenate([joined(*pair) for pair in halves_of], axis=0)
    g = lax.psum_scatter(g, "head", scatter_dimension=1, tiled=True)
    g = lax.psum_scatter(g.astype(F32), ("clip", "seq"), scatter_dimension=2, tiled=True)
    return g[:, 0]


def gather_norms(gain, bias):
    layers, norms, part = gain.shape
    both = jnp.concatenate((gain, bias), axis=1).reshape(1, -1)
    count = lax.axis_size("clip") * lax.axis_size("seq") * lax.axis_size("head")
    width = round_up(both.shape[1], 128)
    padded = jnp.pad(both, ((0, 0), (0, width - both.shape[1])))
    every = lax.all_to_all(
        jnp.broadcast_to(padded, (count, width)), ALL, split_axis=0, concat_axis=0, tiled=True
    )[:, : both.shape[1]]
    return every.reshape(count, layers * 2 * norms, part).transpose(1, 0, 2).reshape(layers, 2 * norms, -1)


def reduce_norms(sums):
    count = lax.axis_size("clip") * lax.axis_size("seq") * lax.axis_size("head")
    rows, features = sums.shape
    part = features // count
    a = sums.reshape(rows, count, part).transpose(1, 0, 2).reshape(count, rows * part)
    width = round_up(rows * part, 128)
    a = jnp.pad(a, ((0, 0), (0, width - rows * part)))
    every = lax.all_to_all(a, ALL, split_axis=0, concat_axis=0, tiled=True)
    return jnp.sum(every, axis=0)[: rows * part].reshape(rows, part)


def on_device(
    tokens,
    cotangent,
    time_qkv,
    time_out,
    time_mix,
    space_qkv,
    space_out,
    mlp_in,
    mlp_out,
    norm_gain,
    norm_bias,
):
    layers = time_qkv.shape[0]
    per_share = mlp_in.shape[2] // time_qkv.shape[3]
    clips, frames, places, d = tokens.shape
    ways = lax.axis_size("seq")
    shards = lax.axis_size("clip") * ways
    rows = Rows(clips * frames, places, ways)
    shares = lax.axis_size("head")

    def as_rows(a):
        a = a.astype(F32).reshape(rows.frames, places, d)
        a = jnp.pad(a, ((0, 0), (0, rows.frame_rows - places), (0, 0)))
        return a.reshape(rows.rows, d)

    def from_rows(a):
        a = a.reshape(rows.frames, rows.frame_rows, d)[:, :places]
        return a.reshape(tokens.shape)

    gbs = gather_norms(norm_gain, norm_bias)
    gb = [gbs[l] for l in range(layers)]
    packs = [
        pack_attention(time_qkv[l], time_out[l], time_mix[l], space_qkv[l], space_out[l])
        for l in range(layers)
    ]
    packs_ff = [pack_feed_forward(mlp_in[l], mlp_out[l], time_qkv.shape[3]) for l in range(layers)]
    packs[0] = jnp.concatenate((packs[0], packs_ff[0]), axis=0)
    weights = [gather_slabs(pack) for pack in packs]
    mixes = [mix_whole(w[8], shards) for w in weights]
    quick = lax.axis_size("clip") == 4 and shares == 2 and ways == 4 and time_qkv.shape[1] % 16 == 0

    halves = Halves(lax.axis_size("clip"), d, time_qkv.shape[3])
    clip = lax.axis_index("clip")
    member = member_of(clip, lax.axis_index("seq"))
    me = jnp.stack((clip & 1, (clip >> 1) & 1, lax.axis_index("head"), member, lax.axis_index("seq"))).astype(
        jnp.int32
    )
    weights_ff = [weights[0]]
    if quick:
        spreads = [None] + [Spread(pack, me) for pack in packs_ff[1:]]
    else:
        weights_ff += [gather_slabs(pack) for pack in packs_ff[1:]]

    home = go_home(tokens)
    x = as_rows(home)
    send = send_first(rows, x, gb[0], me)
    kept = []
    for l in range(layers):
        w = weights[l]
        send = swap_places(send)
        if quick and l == 0:
            for spread in spreads[1:]:
                send = spread.hold(spread.step(send))
        elif quick:
            send = spreads[l].step(send)
        a1, qkv1, log1, o1_time = time_forward(rows, send, w)
        back = swap_places(o1_time)
        if quick and l == 0:
            for spread in spreads[1:]:
                back = spread.step(back)
        elif quick:
            back = spreads[l].step(back)
            weights_ff.append(spreads[l].come)
        o1, y1, x1, qkv2 = middle_forward(rows, back, x, w, mixes[l], gb[l], me)
        o2, x2, log2 = space_forward(rows, qkv2, x1, w)
        if quick and l == 0:
            for spread in spreads[1:]:
                x2 = spread.step(x2)
        kept.append((x, a1, qkv1, log1, o1, y1, x1, qkv2, o2, log2, x2))
        if l + 1 < layers:
            x, *send = mlp_forward(rows, x2, weights_ff[l], per_share, gb[l], gb[l + 1], me)

    grad = as_rows(go_home(cotangent))
    norm_rows = [None] * layers
    summed = [None] * layers
    late = []
    for l in reversed(range(layers)):
        w = weights[l]
        x, a1, qkv1, log1, o1, y1, x1, qkv2, o2, log2, x2 = kept[l]
        grad, g_ff, s3, x3 = mlp_backward(
            rows, grad, x2, weights_ff[l], per_share, gb[l], me, halves, l + 1 == layers
        )
        if x3:
            output = go_back(from_rows(x3[0].astype(BF16)))
        if quick:
            ff = pieces_of(g_ff)
            if late:
                grad = settle(grad, late)
                grad = move(grad, late, me)
                late = [p for p in late if p.step < 3]
        grad, g_space, s2 = space_backward(rows, grad, x1, qkv2, o2, log2, w, gb[l], me, halves)
        if quick:
            space = pieces_of([g_space])
            if late:
                grad = settle(grad, late)
            grad, output = move((grad, output), ff, me)
        do1, g_out = middle_backward(rows, grad, y1, o1, w, mixes[l], me, halves, shards)
        do1 = swap_places(do1)
        if quick:
            do1 = move(do1, ff + space + late, me)
        da1, g_time = time_backward(rows, do1, a1, qkv1, log1, w, me, halves)
        if quick:
            da1 = settle(da1, ff + space)
        da1 = swap_places(da1)
        if quick:
            rest = pieces_of([g_out] + g_time)
            da1 = move(da1, ff + space + rest, me)
            late = space + rest
        grad, s1 = first_norm_back(rows, da1, x, grad, gb[l], me)
        norm_rows[l] = jnp.concatenate((s1[0:1], s2[0:1], s3[0:1], s1[1:2], s2[1:2], s3[1:2]), axis=0)
        if quick:
            summed[l] = ff + space + rest
        else:
            summed[l] = [reduce_plain(g_ff + [g_space, g_out] + g_time, clip & 1)]
    norm_sums = reduce_norms(jnp.concatenate(norm_rows, axis=0)).reshape(layers, 2, 3, -1)
    if quick:
        tokens_grad = go_back(from_rows(grad.astype(BF16)))
        tokens_grad, norm_sums = move((tokens_grad, norm_sums), late, me, True)
        move((), rest, me, True)
        summed = [[p.result for p in some] for some in summed]
    cuts = (2 * g_ff[0][0].shape[0], g_space[0].shape[0], g_out[0].shape[0], len(g_time))
    results = []
    for some in summed:
        slabs_of = jnp.concatenate(some, axis=0)
        ends = [sum(cuts[: i + 1]) for i in range(4)]
        results.append([slabs_of[e - c : e] for c, e in zip(cuts, ends)])
    if not quick:
        tokens_grad = go_back(from_rows(grad.astype(BF16)))
    tokens_grad = tokens_grad.astype(F32)

    def stacked(form):
        return jnp.stack([form(*results[l]) for l in range(layers)])

    def rows_of(a):
        return a.transpose(1, 0, 2)

    def flat(a):
        return rows_of(a).reshape(a.shape[1], -1)

    def mix_rows(a):
        r, width = a.shape
        return a.reshape(shares, r // shares, width).transpose(1, 0, 2).reshape(r // shares, -1)

    return (
        output,
        tokens_grad,
        stacked(lambda ff, s, t, q: rows_of(q)),
        stacked(lambda ff, s, t, q: t[0].T),
        stacked(lambda ff, s, t, q: mix_rows(t[1])),
        stacked(lambda ff, s, t, q: rows_of(s[1:])),
        stacked(lambda ff, s, t, q: s[0].T),
        stacked(lambda ff, s, t, q: flat(ff[:per_share])),
        stacked(lambda ff, s, t, q: flat(ff[per_share:]).T),
        norm_sums[:, 0],
        norm_sums[:, 1],
    )


def solution(mesh):
    token_spec = P(("clip", "head"), "seq", None, None)
    in_specs = (
        token_spec,
        token_spec,
        P(None, ("clip", "seq"), None, "head"),
        P(None, "head", ("clip", "seq")),
        P(None, ("clip", "seq", "head"), None),
        P(None, ("clip", "seq"), None, "head"),
        P(None, "head", ("clip", "seq")),
        P(None, ("clip", "seq"), "head"),
        P(None, "head", ("clip", "seq")),
        P(None, None, ("clip", "seq", "head")),
        P(None, None, ("clip", "seq", "head")),
    )
    return jax.shard_map(
        on_device, mesh=mesh, in_specs=in_specs, out_specs=in_specs, check_vma=False
    )
```

```python
import functools
import math

import jax
import jax.numpy as jnp
from jax import lax
from jax.experimental import pallas as pl
from jax.experimental.pallas import tpu as pltpu
from jax.sharding import PartitionSpec as P

HEAD_DIM = 64
NORM_EPS = 1e-06
HALF_ROOT = 0.7071067811865476
INV_ROOT_TAU = 0.3989422804014327
LOG2E = 1.4426950408889634
FAR = -1e30
LANES = 128
VMEM = 56 * 1024 * 1024
SHOWN = 1.0
ALL = ("clip", "seq", "head")
BF16 = jnp.bfloat16
F32 = jnp.float32


def round_up(value, step):
    return -(-value // step) * step


def nn(a, b):
    return lax.dot_general(a, b, (((1,), (0,)), ((), ())), preferred_element_type=F32)


def nt(a, b):
    return lax.dot_general(a, b, (((1,), (1,)), ((), ())), preferred_element_type=F32)


def tn(a, b):
    return lax.dot_general(a, b, (((0,), (0,)), ((), ())), preferred_element_type=F32)


def norm_parts(x):
    mean = jnp.mean(x, axis=-1, keepdims=True)
    centred = x - mean
    spread = lax.rsqrt(jnp.mean(centred * centred, axis=-1, keepdims=True) + NORM_EPS)
    return centred * spread, spread


def norm_rounded(x, gain, bias):
    hat, _ = norm_parts(x)
    return (hat * gain + bias).astype(BF16)


def norm_back(u, x, gain):
    hat, spread = norm_parts(x)
    scaled = u * gain
    mean_scaled = jnp.mean(scaled, axis=-1, keepdims=True)
    mean_cross = jnp.mean(scaled * hat, axis=-1, keepdims=True)
    change = spread * (scaled - mean_scaled - hat * mean_cross)
    sums = jnp.concatenate(
        (jnp.sum(u * hat, axis=0, keepdims=True), jnp.sum(u, axis=0, keepdims=True)), axis=0
    )
    return change, sums


class Rows:
    def __init__(self, frames, places, ways):
        self.frames = frames
        self.places = places
        self.ways = ways
        self.frame_rows = round_up(places, 16)
        self.rows = frames * self.frame_rows
        self.block = places // ways
        self.chunk = round_up(frames * self.block, 8)
        self.time_rows = ways * self.chunk

    def split(self, r):
        way = jnp.zeros_like(r)
        for k in range(1, self.ways):
            way = way + (r >= k * self.chunk).astype(jnp.int32)
        rest = r - way * self.chunk
        frame = jnp.zeros_like(r)
        for k in range(1, self.frames):
            frame = frame + (rest >= k * self.block).astype(jnp.int32)
        real = rest < self.frames * self.block
        return way, frame, rest - frame * self.block, real

    def to_time(self, k, member):
        r = lax.broadcasted_iota(jnp.int32, (self.chunk, 1), 0)
        _, frame, place, real = self.split(r)
        way = jnp.bitwise_xor(member, k)
        source = jnp.where(real, frame * self.frame_rows + way * self.block + place, -1)
        c = lax.broadcasted_iota(jnp.int32, (self.chunk, self.rows), 1)
        return jnp.where(c == source, 1.0, 0.0).astype(BF16)

    def gathered(self, chunk_refs, member):
        total = tn(self.to_time(0, member), chunk_refs[0][...])
        for k in range(1, self.ways):
            total = total + tn(self.to_time(k, member), chunk_refs[k][...])
        return total

    def chunks(self, width, block=None, index=None):
        return [
            made((self.chunk, width), BF16)
            if block is None
            else made((self.chunk, width), BF16, (self.chunk, block), index)
            for _ in range(self.ways)
        ]

    def time_bias(self):
        def label(r):
            _, _, place, real = self.split(r)
            return jnp.where(real, place, -1)

        a = label(lax.broadcasted_iota(jnp.int32, (self.time_rows, 1), 0))
        b = label(lax.broadcasted_iota(jnp.int32, (1, self.time_rows), 1))
        return jnp.where(a == b, 0.0, FAR).astype(F32)

    def space_bias(self):
        a = lax.broadcasted_iota(jnp.int32, (self.frame_rows, 1), 0)
        return jnp.where(a < self.places, 0.0, FAR).astype(F32)


def lane_masks(rows):
    lane = lax.broadcasted_iota(jnp.int32, (rows, LANES), 1)
    return lane < HEAD_DIM


def one_of(value, low, half):
    zero = jnp.zeros_like(value)
    return jnp.where(low, value, zero) if half == 0 else jnp.where(low, zero, value)


def pair_forward(q, k, v, bias, rate):
    low = lane_masks(q.shape[0])
    mixed, logs = [], []
    for half in range(2):
        s = nt(k, one_of(q, low, half)) + bias
        peak = jnp.max(s, axis=0, keepdims=True)
        e = jnp.exp2((s - peak) * rate)
        total = jnp.sum(e, axis=0, keepdims=True)
        soft = (e * (1.0 / total)).astype(BF16)
        mixed.append(tn(soft, v))
        logs.append(peak * rate + jnp.log2(total))
    return jnp.where(low, mixed[0], mixed[1]).astype(BF16), logs


def pair_backward(q, k, v, do, logs, bias, rate, scale):
    low = lane_masks(q.shape[0])
    dq, dk, dv = [], [], []
    for half in range(2):
        s = nt(k, one_of(q, low, half)) + bias
        soft = jnp.exp2(s * rate - logs[half])
        dp = nt(v, one_of(do, low, half))
        ds = (soft * (dp - jnp.sum(soft * dp, axis=0, keepdims=True))).astype(BF16)
        dv.append(nn(soft.astype(BF16), do))
        dk.append(nn(ds, q))
        dq.append(tn(ds, k))
    return (
        (jnp.where(low, dq[0], dq[1]) * scale).astype(BF16),
        (jnp.where(low, dk[0], dk[1]) * scale).astype(BF16),
        jnp.where(low, dv[0], dv[1]).astype(BF16),
    )


def split_rows(value, keep_ref, send_ref, at, room_ref, me_ref):
    mine = me_ref[0]
    room_ref[...] = value.reshape(room_ref.shape)
    keep_ref[at] = room_ref[:, mine].astype(BF16)
    send_ref[at] = room_ref[:, 1 - mine].astype(BF16)


def store_by_core(ref, value, halves):
    n = halves.rows
    for core in range(2):
        for pair in range(halves.pairs):
            first = (2 * pair + core) * n
            ref[core, pair * n : (pair + 1) * n] = value[first : first + n]


def split_product(left_ref, right, keep_ref, send_ref, at, me_ref):
    mine = me_ref[0]
    shape = keep_ref.shape[len(at) :]
    keep_ref[at] = nn(left_ref[mine], right).reshape(shape).astype(BF16)
    send_ref[at] = nn(left_ref[1 - mine], right).reshape(shape).astype(BF16)


class Halves:
    def __init__(self, clips, depth, width):
        self.pairs = clips // 2
        self.rows = depth // clips
        self.width = width

    def array(self, lead, block, index):
        tail = (self.pairs, self.rows, self.width)
        one = lambda: made(lead + tail, BF16, block + tail, lambda *g: index(*g) + (0, 0, 0))
        return [one(), one()]

    def turned(self, columns):
        return pltpu.VMEM((2, self.pairs * self.rows, columns), BF16)

    def room(self):
        return pltpu.VMEM((self.pairs, 2, self.rows, self.width), F32)


SCALARS = pl.BlockSpec(memory_space=pltpu.SMEM)


def call(body, grid, ins, outs, scratch, args, flops=0):
    specs = [spec for spec in ins]
    moved = sum(math.prod(o.shape) * o.dtype.itemsize for o, _ in outs)
    moved += sum(math.prod(a.shape) * a.dtype.itemsize for a in args)
    return pl.pallas_call(
        body,
        out_shape=[shape for shape, _ in outs],
        grid=grid,
        in_specs=specs,
        out_specs=[spec for _, spec in outs],
        scratch_shapes=scratch,
        compiler_params=pltpu.CompilerParams(vmem_limit_bytes=VMEM),
        cost_estimate=pl.CostEstimate(
            flops=int(flops * SHOWN), bytes_accessed=int(moved * SHOWN), transcendentals=0
        ),
    )(*args)


def whole(shape):
    zeros = (0,) * len(shape)
    return pl.BlockSpec(shape, lambda *_: zeros)


def made(shape, dtype, block=None, index=None):
    spec = whole(shape) if block is None else pl.BlockSpec(block, index)
    return jax.ShapeDtypeStruct(shape, dtype), spec


def slabs(count, first, width, depth):
    return pl.BlockSpec((count, 1, depth, width), lambda h, *_: (first // count, h, 0, 0))


def send_first(rows, x, gb, me):
    def body(me_ref, x_ref, gb_ref, *out_refs):
        a = norm_rounded(x_ref[...], gb_ref[0:1], gb_ref[3:4])
        for k in range(rows.ways):
            out_refs[k][...] = nn(rows.to_time(k, me_ref[3]), a).astype(BF16)

    d = x.shape[1]
    return call(
        body, (1,), [SCALARS, whole(x.shape), whole(gb.shape)], rows.chunks(d), [], (me, x, gb)
    )


def time_forward(rows, chunks, w):
    t, d = rows.time_rows, chunks[0].shape[1]
    width = w.shape[3]
    shares = w.shape[1]
    pairs = width // LANES
    ways = rows.ways
    rate = LOG2E / math.sqrt(HEAD_DIM)

    def body(*refs):
        chunk_refs = refs[:ways]
        w_ref, a_ref, qkv_ref, log_ref = refs[ways : ways + 4]
        out_refs = refs[ways + 4 : 2 * ways + 4]
        bias_ref, mixed_ref = refs[2 * ways + 4 :]

        @pl.when(pl.program_id(0) == 0)
        def _():
            bias_ref[...] = rows.time_bias()
            for k in range(ways):
                a_ref[k * rows.chunk : (k + 1) * rows.chunk] = chunk_refs[k][...]

        act = a_ref[...]
        for g in range(3):
            qkv_ref[g] = nn(act, w_ref[g, 0]).astype(BF16)

        @pl.loop(0, pairs)
        def _(i):
            lanes = pl.ds(pl.multiple_of(i * LANES, LANES), LANES)
            mixed, logs = pair_forward(
                qkv_ref[0, :, lanes], qkv_ref[1, :, lanes], qkv_ref[2, :, lanes], bias_ref[...], rate
            )
            mixed_ref[:, lanes] = mixed
            log_ref[0, i] = jnp.concatenate(logs, axis=0)

        for k in range(ways):
            out_refs[k][...] = mixed_ref[k * rows.chunk : (k + 1) * rows.chunk]

    got = call(
        body,
        (shares,),
        [whole(c.shape) for c in chunks] + [slabs(3, 0, width, d)],
        [
            made((t, d), BF16),
            made((3, t, d), BF16, (3, t, width), lambda h: (0, 0, h)),
            made((shares, pairs, 2, t), F32, (1, pairs, 2, t), lambda h: (h, 0, 0, 0)),
            *rows.chunks(d, width, lambda h: (0, h)),
        ],
        [pltpu.VMEM((t, t), F32), pltpu.VMEM((t, width), BF16)],
        (*chunks, w),
        flops=2 * t * d * 3 * d,
    )
    return got[0], got[1], got[2], got[3:]


def middle_forward(rows, back, x, w, mix, gb, me):
    t, d = x.shape
    width = w.shape[3]
    shares = w.shape[1]

    def body(me_ref, *refs):
        x_ref, to_ref, sq_ref, mix_ref, gb_ref, o1_ref, y1_ref, x1_ref, qkv_ref = refs[rows.ways :]
        o1 = rows.gathered(refs[: rows.ways], me_ref[3]).astype(BF16)
        o1_ref[...] = o1
        y1 = jnp.zeros((t, d), F32)
        for h in range(shares):
            y1 = y1 + nt(o1[:, h * width : (h + 1) * width], to_ref[0, h])
        y1 = y1.astype(BF16)
        y1_ref[...] = y1
        x1 = x_ref[...] + nn(y1, mix_ref[...])
        x1_ref[...] = x1
        a2 = norm_rounded(x1, gb_ref[1:2], gb_ref[4:5])
        for g in range(3):
            for h in range(shares):
                qkv_ref[g, :, h * width : (h + 1) * width] = nn(a2, sq_ref[g, h]).astype(BF16)

    return call(
        body,
        (1,),
        [
            SCALARS,
            *(whole(c.shape) for c in back),
            whole(x.shape),
            pl.BlockSpec((1, shares, d, width), lambda i: (6, 0, 0, 0)),
            pl.BlockSpec((3, shares, d, width), lambda i: (1, 0, 0, 0)),
            whole(mix.shape),
            whole(gb.shape),
        ],
        [made((t, d), BF16), made((t, d), BF16), made((t, d), F32), made((3, t, d), BF16)],
        [],
        (me, *back, x, w, w, mix, gb),
        flops=2 * t * d * 5 * d,
    )


def space_forward(rows, qkv, x1, w):
    t, d = x1.shape
    width = w.shape[3]
    shares = w.shape[1]
    pairs = width // LANES
    rate = LOG2E / math.sqrt(HEAD_DIM)
    n = rows.frame_rows

    def body(qkv_ref, x1_ref, w_ref, o2_ref, x2_ref, log_ref):
        bias = rows.space_bias()

        @pl.loop(0, pairs)
        def _(i):
            lanes = pl.ds(pl.multiple_of(i * LANES, LANES), LANES)
            for f in range(rows.frames):
                at = slice(f * n, (f + 1) * n)
                mixed, logs = pair_forward(
                    qkv_ref[0, at, lanes], qkv_ref[1, at, lanes], qkv_ref[2, at, lanes], bias, rate
                )
                o2_ref[at, lanes] = mixed
                log_ref[0, i, f] = jnp.concatenate(logs, axis=0)

        @pl.when(pl.program_id(0) == 0)
        def _():
            x2_ref[...] = x1_ref[...]

        x2_ref[...] += nt(o2_ref[...], w_ref[0, 0])

    return call(
        body,
        (shares,),
        [
            pl.BlockSpec((3, t, width), lambda h: (0, 0, h)),
            whole(x1.shape),
            slabs(1, 7, width, d),
        ],
        [
            made((t, d), BF16, (t, width), lambda h: (0, h)),
            made((t, d), F32),
            made(
                (shares, pairs, rows.frames, 2, n),
                F32,
                (1, pairs, rows.frames, 2, n),
                lambda h: (h, 0, 0, 0, 0),
            ),
        ],
        [],
        (qkv, x1, w),
        flops=2 * t * d * d,
    )


def ff_slab(first, per_share, depth, width):
    return pl.BlockSpec(
        (1, 1, depth, width), lambda j: (first + j % per_share, j // per_share, 0, 0)
    )


def mlp_forward(rows, x2, w, gb, gb_next, me):
    t, d = x2.shape
    width = w.shape[3]
    shares = w.shape[1]
    per_share = w.shape[0] // 2
    steps = shares * per_share

    def body(x2_ref, wi_ref, wo_ref, gb_ref, me_ref, gn_ref, x3_ref, *rest):
        send_refs, a3_ref = rest[:-1], rest[-1]
        j = pl.program_id(0)

        @pl.when(j == 0)
        def _():
            a3_ref[...] = norm_rounded(x2_ref[...], gb_ref[2:3], gb_ref[5:6])
            x3_ref[...] = x2_ref[...]

        hid = nn(a3_ref[...], wi_ref[0, 0])
        act = (0.5 * hid * (1.0 + lax.erf(hid * HALF_ROOT))).astype(BF16)
        x3_ref[...] += nt(act, wo_ref[0, 0])

        @pl.when(j == steps - 1)
        def _():
            a = norm_rounded(x3_ref[...], gn_ref[0:1], gn_ref[3:4])
            for k in range(rows.ways):
                send_refs[k][...] = nn(rows.to_time(k, me_ref[3]), a).astype(BF16)

    ins = [
        whole(x2.shape),
        ff_slab(0, per_share, d, width),
        ff_slab(per_share, per_share, d, width),
        whole(gb.shape),
    ]
    ins += [SCALARS, whole(gb_next.shape)]
    outs = [made((t, d), F32)] + rows.chunks(d)
    args = (x2, w, w, gb, me, gb_next)
    return call(
        body, (steps,), ins, outs, [pltpu.VMEM((t, d), BF16)], args, flops=4 * t * d * width * steps
    )


def mlp_backward(rows, grad, x2, w, gb, me, halves, with_output):
    t, d = x2.shape
    width = w.shape[3]
    shares = w.shape[1]
    per_share = w.shape[0] // 2
    steps = shares * per_share

    def body(me_ref, g_ref, x2_ref, wi_ref, wo_ref, gb_ref, go_ref, ki_ref, si_ref, ko_ref, so_ref, sums_ref, *rest):
        if with_output:
            x3_ref, *rest = rest
        a3_ref, a3t_ref, e3_ref, e3t_ref, u_ref = rest
        j = pl.program_id(0)

        @pl.when(j == 0)
        def _():
            hat, _ = norm_parts(x2_ref[...])
            a3 = hat * gb_ref[2:3] + gb_ref[5:6]
            a3_ref[...] = a3.astype(BF16)
            store_by_core(a3t_ref, a3.T.astype(BF16), halves)
            g = g_ref[...]
            e3_ref[...] = g.astype(BF16)
            store_by_core(e3t_ref, g.T.astype(BF16), halves)
            u_ref[...] = jnp.zeros((t, d), F32)
            if with_output:
                x3_ref[...] = x2_ref[...]

        hid = nn(a3_ref[...], wi_ref[0, 0])
        phi = 0.5 * (1.0 + lax.erf(hid * HALF_ROOT))
        act = (hid * phi).astype(BF16)
        slope = phi + hid * jnp.exp(-0.5 * hid * hid) * INV_ROOT_TAU
        dhid = (nn(e3_ref[...], wo_ref[0, 0]) * slope).astype(BF16)
        split_product(e3t_ref, act, ko_ref, so_ref, (0, 0), me_ref)
        split_product(a3t_ref, dhid, ki_ref, si_ref, (0, 0), me_ref)
        u_ref[...] += nt(dhid, wi_ref[0, 0])
        if with_output:
            x3_ref[...] += nt(act, wo_ref[0, 0])

        @pl.when(j == steps - 1)
        def _():
            change, sums = norm_back(u_ref[...], x2_ref[...], gb_ref[2:3])
            go_ref[...] = g_ref[...] + change
            sums_ref[...] = sums

    slab_outs = [
        one
        for _ in range(2)
        for one in halves.array(
            (per_share, shares), (1, 1), lambda j: (j % per_share, j // per_share)
        )
    ]
    grad, ki, si, ko, so, sums, *x3 = call(
        body,
        (steps,),
        [
            SCALARS,
            whole(grad.shape),
            whole(x2.shape),
            ff_slab(0, per_share, d, width),
            ff_slab(per_share, per_share, d, width),
            whole(gb.shape),
        ],
        [made((t, d), F32), *slab_outs, made((2, d), F32)] + [made((t, d), F32)] * with_output,
        [
            pltpu.VMEM((t, d), BF16),
            halves.turned(t),
            pltpu.VMEM((t, d), BF16),
            halves.turned(t),
            pltpu.VMEM((t, d), F32),
        ],
        (me, grad, x2, w, w, gb),
        flops=10 * t * d * width * steps,
    )
    return grad, [(ki, si), (ko, so)], sums, x3


def space_backward(rows, grad, x1, qkv, o2, logs, w, gb, me, halves):
    t, d = x1.shape
    width = w.shape[3]
    shares = w.shape[1]
    pairs = width // LANES
    scale = 1.0 / math.sqrt(HEAD_DIM)
    rate = LOG2E * scale
    n = rows.frame_rows

    def body(me_ref, g_ref, x1_ref, qkv_ref, o2_ref, log_ref, wo_ref, wq_ref, gb_ref, go_ref, keep_ref, send_ref, sums_ref, e2_ref, e2t_ref, a2t_ref, do_ref, dqkv_ref, u_ref):
        h = pl.program_id(0)

        @pl.when(h == 0)
        def _():
            g = g_ref[...]
            e2_ref[...] = g.astype(BF16)
            store_by_core(e2t_ref, g.T.astype(BF16), halves)
            hat, _ = norm_parts(x1_ref[...])
            store_by_core(a2t_ref, (hat * gb_ref[1:2] + gb_ref[4:5]).T.astype(BF16), halves)
            u_ref[...] = jnp.zeros((t, d), F32)

        bias = rows.space_bias()
        split_product(e2t_ref, o2_ref[...], keep_ref, send_ref, (0, 0), me_ref)
        do_ref[...] = nn(e2_ref[...], wo_ref[0, 0]).astype(BF16)

        @pl.loop(0, pairs)
        def _(i):
            lanes = pl.ds(pl.multiple_of(i * LANES, LANES), LANES)
            for f in range(rows.frames):
                at = slice(f * n, (f + 1) * n)
                log = log_ref[0, i, f]
                grads = pair_backward(
                    qkv_ref[0, at, lanes],
                    qkv_ref[1, at, lanes],
                    qkv_ref[2, at, lanes],
                    do_ref[at, lanes],
                    (log[0:1], log[1:2]),
                    bias,
                    rate,
                    scale,
                )
                for part in range(3):
                    dqkv_ref[part, at, lanes] = grads[part]

        for part in range(3):
            split_product(a2t_ref, dqkv_ref[part], keep_ref, send_ref, (part + 1, 0), me_ref)
            u_ref[...] += nt(dqkv_ref[part], wq_ref[part, 0])

        @pl.when(h == shares - 1)
        def _():
            change, sums = norm_back(u_ref[...], x1_ref[...], gb_ref[1:2])
            go_ref[...] = g_ref[...] + change
            sums_ref[...] = sums

    grad, keep, send, sums = call(
        body,
        (shares,),
        [
            SCALARS,
            whole(grad.shape),
            whole(x1.shape),
            pl.BlockSpec((3, t, width), lambda h: (0, 0, h)),
            pl.BlockSpec((t, width), lambda h: (0, h)),
            pl.BlockSpec((1,) + logs.shape[1:], lambda h: (h, 0, 0, 0, 0)),
            slabs(1, 7, width, d),
            slabs(3, 3, width, d),
            whole(gb.shape),
        ],
        [
            made((t, d), F32),
            *halves.array((4, shares), (4, 1), lambda h: (0, h)),
            made((2, d), F32),
        ],
        [
            pltpu.VMEM((t, d), BF16),
            halves.turned(t),
            halves.turned(t),
            pltpu.VMEM((t, width), BF16),
            pltpu.VMEM((3, t, width), BF16),
            pltpu.VMEM((t, d), F32),
        ],
        (me, grad, x1, qkv, o2, logs, w, w, gb),
        flops=2 * t * d * d * 8,
    )
    return grad, (keep, send), sums


def mix_fits(depth, shards, shares):
    return depth // (shards * shares) % 8 == 0


def middle_backward(rows, grad, y1, o1, w, mix, me, halves, shards):
    t, d = grad.shape
    width = w.shape[3]
    shares = w.shape[1]
    fits = mix_fits(d, shards, shares)
    part = d // (shards * shares)

    def body(me_ref, g_ref, y1_ref, o1_ref, to_ref, mix_ref, *rest):
        send_refs, rest = rest[: rows.ways], rest[rows.ways :]
        gk_ref, gs_ref, *rest = rest
        if fits:
            room_ref, order_ref = rest
        else:
            gm_ref, room_ref = rest
        e1 = g_ref[...].astype(BF16)
        dy1 = nt(e1, mix_ref[...]).astype(BF16)
        sends = [rows.to_time(k, me_ref[3]) for k in range(rows.ways)]
        for h in range(shares):
            lanes = slice(h * width, (h + 1) * width)
            do1 = nn(dy1, to_ref[0, h]).astype(BF16)
            for k in range(rows.ways):
                send_refs[k][:, lanes] = nn(sends[k], do1).astype(BF16)
            split_rows(tn(dy1, o1_ref[:, lanes]), gk_ref, gs_ref, (0, h), room_ref, me_ref)
        gm = tn(y1_ref[...], e1)
        if fits:
            gm = gm.reshape(shards, shares, part, d)
            for h in range(shares):
                for half in range(shares):
                    order_ref[:, half] = gm[:, h, :, half * width : (half + 1) * width]
                split_rows(order_ref[...], gk_ref, gs_ref, (1, h), room_ref, me_ref)
        else:
            gm_ref[...] = gm.astype(BF16)

    outs = rows.chunks(d)
    outs += halves.array((1 + fits, shares), (1 + fits, shares), lambda i: (0, 0))
    scratch = [halves.room()]
    if fits:
        scratch.append(pltpu.VMEM((shards, shares, part, width), F32))
    else:
        outs.append(made((d, d), BF16))
    got = call(
        body,
        (1,),
        [
            SCALARS,
            whole(grad.shape),
            whole(y1.shape),
            whole(o1.shape),
            pl.BlockSpec((1, shares, d, width), lambda i: (6, 0, 0, 0)),
            whole(mix.shape),
        ],
        outs,
        scratch,
        (me, grad, y1, o1, w, mix),
        flops=8 * t * d * d,
    )
    do1, (keep, send) = got[: rows.ways], got[rows.ways : rows.ways + 2]
    if not fits:
        gm = mix_slab(got[-1], shards, shares).reshape((1, shares, halves.pairs, 2) + keep.shape[3:])
        keep = jnp.concatenate((keep, lax.dynamic_index_in_dim(gm, me[0], 3, keepdims=False)), axis=0)
        send = jnp.concatenate((send, lax.dynamic_index_in_dim(gm, 1 - me[0], 3, keepdims=False)), axis=0)
    return do1, (keep, send)


def time_backward(rows, do1, a, qkv, logs, w, me, halves):
    t, d = a.shape
    width = w.shape[3]
    shares = w.shape[1]
    pairs = width // LANES
    scale = 1.0 / math.sqrt(HEAD_DIM)
    rate = LOG2E * scale

    def body(me_ref, *refs):
        do_refs, refs = refs[: rows.ways], refs[rows.ways :]
        a_ref, qkv_ref, log_ref, w_ref = refs[:4]
        out_refs, refs = refs[4 : 4 + rows.ways], refs[4 + rows.ways :]
        half_refs, refs = refs[:6], refs[6:]
        bias_ref, dqkv_ref, at_ref, u_ref, do_ref = refs
        h = pl.program_id(0)

        @pl.when(h == 0)
        def _():
            bias_ref[...] = rows.time_bias()
            store_by_core(at_ref, a_ref[...].T, halves)
            u_ref[...] = jnp.zeros((t, d), F32)

        for k in range(rows.ways):
            do_ref[k * rows.chunk : (k + 1) * rows.chunk] = do_refs[k][...]

        @pl.loop(0, pairs)
        def _(i):
            lanes = pl.ds(pl.multiple_of(i * LANES, LANES), LANES)
            log = log_ref[0, i]
            grads = pair_backward(
                qkv_ref[0, :, lanes],
                qkv_ref[1, :, lanes],
                qkv_ref[2, :, lanes],
                do_ref[:, lanes],
                (log[0:1], log[1:2]),
                bias_ref[...],
                rate,
                scale,
            )
            for part in range(3):
                dqkv_ref[part, :, lanes] = grads[part]

        for part in range(3):
            split_product(
                at_ref, dqkv_ref[part], half_refs[2 * part], half_refs[2 * part + 1], (0, 0), me_ref
            )
            u_ref[...] += nt(dqkv_ref[part], w_ref[part, 0])

        @pl.when(h == shares - 1)
        def _():
            for k in range(rows.ways):
                out_refs[k][...] = u_ref[k * rows.chunk : (k + 1) * rows.chunk].astype(BF16)

    got = call(
        body,
        (shares,),
        [
            SCALARS,
            *(pl.BlockSpec((rows.chunk, width), lambda h: (0, h)) for _ in do1),
            whole(a.shape),
            pl.BlockSpec((3, t, width), lambda h: (0, 0, h)),
            pl.BlockSpec((1,) + logs.shape[1:], lambda h: (h, 0, 0, 0)),
            slabs(3, 0, width, d),
        ],
        [
            *rows.chunks(d),
            *(one for _ in range(3) for one in halves.array((1, shares), (1, 1), lambda h: (0, h))),
        ],
        [
            pltpu.VMEM((t, t), F32),
            pltpu.VMEM((3, t, width), BF16),
            halves.turned(t),
            pltpu.VMEM((t, d), F32),
            pltpu.VMEM((t, width), BF16),
        ],
        (me, *do1, a, qkv, logs, w),
        flops=2 * t * d * d * 6,
    )
    parts = got[rows.ways :]
    return got[: rows.ways], [tuple(parts[i : i + 2]) for i in (0, 2, 4)]


def first_norm_back(rows, back, x, grad, gb, me):
    t, d = x.shape

    def body(me_ref, *refs):
        x_ref, g_ref, gb_ref, go_ref, sums_ref = refs[rows.ways :]
        u = rows.gathered(refs[: rows.ways], me_ref[3])
        change, sums = norm_back(u, x_ref[...], gb_ref[0:1])
        go_ref[...] = g_ref[...] + change
        sums_ref[...] = sums

    return call(
        body,
        (1,),
        [SCALARS, *(whole(c.shape) for c in back), whole(x.shape), whole(grad.shape), whole(gb.shape)],
        [made((t, d), F32), made((2, d), F32)],
        [],
        (me, *back, x, grad, gb),
    )


def homes():
    clips, ways = lax.axis_size("clip"), lax.axis_size("seq")
    pairs = []
    for clip in range(clips):
        for seq in range(ways):
            home_clip = clip - clip % 2 + seq % 2
            home_seq = seq // 2 + (ways // 2) * (clip % 2)
            pairs.append((clip * ways + seq, home_clip * ways + home_seq))
    return pairs


def go_home(a):
    return lax.ppermute(a, ("clip", "seq"), homes())


def go_back(a):
    return lax.ppermute(a, ("clip", "seq"), [(home, device) for device, home in homes()])


def member_of(clip, seq):
    return clip % 2 + 2 * (seq % (lax.axis_size("seq") // 2))


def swap_places(chunks):
    clips, ways = lax.axis_size("clip"), lax.axis_size("seq")
    got = [chunks[0]]
    for k in range(1, ways):
        pairs = []
        for clip in range(clips):
            for seq in range(ways):
                other = member_of(clip, seq) ^ k
                to_clip = clip - clip % 2 + other % 2
                to_seq = seq - seq % (ways // 2) + other // 2
                pairs.append((clip * ways + seq, to_clip * ways + to_seq))
        got.append(lax.ppermute(chunks[k], ("clip", "seq"), pairs))
    return got


def columns(a, r, width):
    return a.reshape(r, -1, width).transpose(1, 0, 2)


def pack_attention(time_qkv, time_out, time_mix, space_qkv, space_out):
    r, _, width = time_qkv.shape
    mix = time_mix.reshape(-1, time_mix.shape[1] // width, width).transpose(1, 0, 2).reshape(1, r, width)
    return jnp.concatenate(
        (
            columns(time_qkv, r, width),
            columns(space_qkv, r, width),
            time_out.T[None],
            space_out.T[None],
            mix,
        ),
        axis=0,
    )


def pack_feed_forward(mlp_in, mlp_out, width):
    r = mlp_in.shape[0]
    return jnp.concatenate((columns(mlp_in, r, width), columns(mlp_out.T, r, width)), axis=0)


def gather_slabs(pack):
    full = lax.all_gather(pack, ("head", "clip", "seq"), axis=1, tiled=True)
    return full.reshape(pack.shape[0], lax.axis_size("head"), -1, pack.shape[2])


def gather_slabs_later(pack):
    parts = [lax.all_gather(a, "seq", axis=1, tiled=True) for a in jnp.split(pack, [5], axis=0)]
    full = lax.all_gather(jnp.concatenate(parts, axis=0), ("head", "clip"), axis=1, tiled=True)
    return full.reshape(pack.shape[0], lax.axis_size("head"), -1, pack.shape[2])


def spread_steps(pack, me):
    ways, clips = lax.axis_size("seq"), lax.axis_size("clip")
    shares = lax.axis_size("head")
    n, r, width = pack.shape
    pack = yield pack
    turned = [pack] + [
        lax.ppermute(pack, "seq", [(i, (i + k) % ways) for i in range(ways)]) for k in range(1, ways)
    ]
    turned = yield turned
    orders = (((0, 1), "x", "h"), ((3, 2), "h", "x"))
    some = [jnp.stack([turned[k] for k in steps]) for steps, _, _ in orders]
    come = yield [cross(a, first) for a, (_, first, _) in zip(some, orders)]
    some = [jnp.concatenate(pair, axis=0) for pair in zip(some, come)]
    come = yield [cross(a, second) for a, (_, _, second) in zip(some, orders)]
    runs = []
    for mine, other, (steps, first, second) in zip(some, come, orders):
        where = [(k, {first: f}) for f in (0, 1) for k in steps]
        for g, blocks in enumerate((mine, other)):
            runs.append((blocks, [(k, {**at, second: g}) for k, at in where], 0))
    come = yield [cross(blocks, "c") for blocks, _, _ in runs]
    runs += [(far, where, 1) for far, (_, where, _) in zip(come, runs)]
    count = sum(len(where) for _, where, _ in runs)

    def body(me_ref, *refs):
        sources, out_ref, sems = refs[: len(runs)], refs[-2], refs[-1]
        copies = []
        for source, (_, where, core) in zip(sources, runs):
            for i, (k, at) in enumerate(where):
                share = jnp.bitwise_xor(me_ref[2], at["h"])
                clip = 2 * jnp.bitwise_xor(me_ref[1], at["x"]) + jnp.bitwise_xor(me_ref[0], core)
                seq = lax.rem(me_ref[4] + (ways - k), ways)
                copies.append(
                    pltpu.make_async_copy(
                        source.at[i], out_ref.at[:, share, clip * ways + seq], sems.at[len(copies)]
                    )
                )
        for copy in copies:
            copy.start()
        for copy in copies:
            copy.wait()

    full = pl.pallas_call(
        body,
        out_shape=jax.ShapeDtypeStruct((n, shares, clips * ways, r, width), BF16),
        in_specs=[SCALARS] + [pl.BlockSpec(memory_space=pltpu.HBM)] * len(runs),
        out_specs=pl.BlockSpec(memory_space=pltpu.VMEM),
        scratch_shapes=[pltpu.SemaphoreType.DMA((count,))],
        compiler_params=pltpu.CompilerParams(vmem_limit_bytes=VMEM),
        cost_estimate=pl.CostEstimate(
            flops=0, bytes_accessed=4 * n * shares * clips * ways * r * width, transcendentals=0
        ),
    )(me, *(blocks for blocks, _, _ in runs))
    yield full.reshape(n, shares, clips * ways * r, width)


class Spread:
    def __init__(self, pack, me):
        self.way = spread_steps(pack, me)
        self.come = next(self.way)

    def hold(self, x):
        x, self.come = lax.optimization_barrier((x, self.come))
        return x

    def step(self, x):
        x = self.hold(x)
        self.come = self.way.send(self.come)
        return x


def mix_whole(slab, shards):
    shares, depth, width = slab.shape
    part = slab.reshape(shares, shards, shares, depth // (shards * shares), width)
    return part.transpose(1, 0, 3, 2, 4).reshape(depth, shares * width)


def mix_slab(whole_grad, shards, shares):
    depth, full = whole_grad.shape
    width = full // shares
    part = whole_grad.reshape(shards, shares, depth // (shards * shares), shares, width)
    return part.transpose(1, 0, 3, 2, 4).reshape(1, shares, depth, width)


class Piece:
    def __init__(self, keep, got, first, n, order):
        self.near = (keep, got)
        self.first = first
        self.n = n
        self.order = order
        self.step = 0
        self.held = []
        self.result = None


PLACE = {"x": 1, "h": 2}


def fold(pieces, me, last_by_rows):
    ways = lax.axis_size("seq")
    depth, width = pieces[0].near[0].shape[-2:]
    r = depth // ways
    used = {}
    arrays = []

    def number(a):
        for i, known in enumerate(arrays):
            if known is a:
                return i
        arrays.append(a)
        return len(arrays) - 1

    plans = []
    for p in pieces:
        link = p.order[p.step] if p.step < 2 else "z"
        blocks = p.n * (2 if p.step == 0 else 1)
        base = used.get(link, 0)
        used[link] = base + blocks
        near = [number(a) for a in p.near]
        held = [(number(a), at) for a, at in p.held]
        plans.append((p, link, base, near, held))
    links = sorted(used)
    shapes = [
        (ways, used[k], r, width) if k == "z" and last_by_rows else (used[k], depth, width)
        for k in links
    ]
    rooms, counts = [], []
    for p, link, base, near, held in plans:
        each = 2 if p.step == 0 else 1
        counts.append((each, len(near) + len(held)))
        rooms += [(each * p.n, depth, width)] * (len(near) + len(held))
    copies_needed = sum(each * terms for each, terms in counts)

    def body(me_ref, *refs):
        sources = refs[: len(arrays)]
        outs = dict(zip(links, refs[len(arrays) : len(arrays) + len(links)]))
        held_refs = refs[len(arrays) + len(links) : -1]
        sems = refs[-1]
        mine = {name: me_ref[PLACE[name]] for name in PLACE}
        groups = []
        room = 0
        sem = 0
        for p, link, base, near, held in plans:
            group = []
            if p.step == 0:
                for term in near:
                    for k in range(2):
                        pick = {p.order[0]: 1 - mine[p.order[0]], p.order[1]: k}
                        source = sources[term].at[pl.ds(p.first, p.n), pick["h"], pick["x"]]
                        group.append((source, held_refs[room].at[pl.ds(k * p.n, p.n)]))
                    room += 1
            else:
                last = p.order[1]
                pick = {p.order[0]: mine[p.order[0]]}
                pick[last] = 1 - mine[last] if p.step == 1 else mine[last]
                for term in near:
                    source = sources[term].at[pl.ds(p.first, p.n), pick["h"], pick["x"]]
                    group.append((source, held_refs[room]))
                    room += 1
                for i, (term, at) in enumerate(held):
                    start = at + pick[last] * p.n if i == 0 else at
                    group.append((sources[term].at[pl.ds(start, p.n)], held_refs[room]))
                    room += 1
            made_copies = []
            for source, target in group:
                made_copies.append(pltpu.make_async_copy(source, target, sems.at[sem]))
                sem += 1
            groups.append(made_copies)
        for group in groups:
            for copy in group:
                copy.start()
        room = 0
        for (p, link, base, near, held), (each, terms), group in zip(plans, counts, groups):
            these = held_refs[room : room + terms]
            room += terms
            for copy in group:
                copy.wait()

            @pl.loop(0, each * p.n)
            def _(i, these=these, base=base, out=outs[link], last=p.step == 2 and last_by_rows):
                value = these[0][i].astype(F32)
                for one in these[1:]:
                    value = value + one[i].astype(F32)
                value = value.astype(BF16)
                if last:
                    for k in range(ways):
                        out[k, base + i] = value[k * r : (k + 1) * r]
                else:
                    out[base + i] = value

    moved = sum(2 * math.prod(room) for room in rooms) + sum(2 * math.prod(shape) for shape in shapes)
    sums = pl.pallas_call(
        body,
        out_shape=[jax.ShapeDtypeStruct(shape, BF16) for shape in shapes],
        in_specs=[SCALARS] + [pl.BlockSpec(memory_space=pltpu.HBM)] * len(arrays),
        out_specs=[pl.BlockSpec(memory_space=pltpu.VMEM)] * len(links),
        scratch_shapes=[pltpu.VMEM(room, BF16) for room in rooms]
        + [pltpu.SemaphoreType.DMA((copies_needed,))],
        compiler_params=pltpu.CompilerParams(vmem_limit_bytes=VMEM),
        cost_estimate=pl.CostEstimate(flops=0, bytes_accessed=moved, transcendentals=0),
    )(me, *arrays)
    return [(p, link, base) for p, link, base, _, _ in plans], dict(zip(links, sums))


def cross(a, name):
    axis, bit = ("head", 0) if name == "h" else ("clip", 1 if name == "x" else 0)
    size = lax.axis_size(axis)
    return lax.ppermute(a, axis, [(i, i ^ (1 << bit)) for i in range(size)])


def pieces_of(halves_of):
    total = sum(keep.shape[0] for keep, _ in halves_of)
    found = []
    seen = 0
    for keep, send in halves_of:
        got = cross(send, "c")
        n = keep.shape[0]
        first = min(max((total + 1) // 2 - seen, 0), n)
        if first:
            found.append(Piece(keep, got, 0, first, ("x", "h")))
        if n > first:
            found.append(Piece(keep, got, first, n - first, ("h", "x")))
        seen += n
    return found


def move(x, pieces, me, at_end=False):
    plans, sums = fold(pieces, me, at_end)
    x, sums = lax.optimization_barrier((x, sums))
    got = {}
    for link, array in sums.items():
        if link == "z":
            if at_end:
                every = lax.all_to_all(array, "seq", split_axis=0, concat_axis=0, tiled=True)
                got[link] = jnp.sum(every.astype(F32), axis=0)
            else:
                own = lax.psum_scatter(array, "seq", scatter_dimension=1, tiled=True)
                got[link] = own.astype(F32)
        else:
            got[link] = cross(array, link)
    for p, link, base in plans:
        if link == "z":
            p.result = got[link][base : base + p.n]
        else:
            p.held.append((got[link], base))
        p.step += 1
    return x


def settle(x, pieces):
    arrays = []
    for p in pieces:
        if not any(p.held[-1][0] is a for a in arrays):
            arrays.append(p.held[-1][0])
    x, came = lax.optimization_barrier((x, arrays))
    for p in pieces:
        for old, new in zip(arrays, came):
            if p.held[-1][0] is old:
                p.held[-1] = (new, p.held[-1][1])
                break
    return x


def reduce_plain(halves_of, core):
    def joined(keep, send):
        low = jnp.where(core == 0, keep, send)
        high = jnp.where(core == 0, send, keep)
        n, shares, pairs, depth, width = keep.shape
        return jnp.stack((low, high), axis=3).reshape(n, shares, 2 * pairs * depth, width)

    g = jnp.concatenate([joined(*pair) for pair in halves_of], axis=0)
    g = lax.psum_scatter(g, "head", scatter_dimension=1, tiled=True)
    g = lax.psum_scatter(g.astype(F32), ("clip", "seq"), scatter_dimension=2, tiled=True)
    return g[:, 0]


def gather_norms(gain, bias):
    layers, norms, part = gain.shape
    both = jnp.concatenate((gain, bias), axis=1).reshape(1, -1)
    count = lax.axis_size("clip") * lax.axis_size("seq") * lax.axis_size("head")
    width = round_up(both.shape[1], 128)
    padded = jnp.pad(both, ((0, 0), (0, width - both.shape[1])))
    every = lax.all_to_all(
        jnp.broadcast_to(padded, (count, width)), ALL, split_axis=0, concat_axis=0, tiled=True
    )[:, : both.shape[1]]
    return every.reshape(count, layers * 2 * norms, part).transpose(1, 0, 2).reshape(layers, 2 * norms, -1)


def reduce_norms(sums):
    count = lax.axis_size("clip") * lax.axis_size("seq") * lax.axis_size("head")
    rows, features = sums.shape
    part = features // count
    a = sums.reshape(rows, count, part).transpose(1, 0, 2).reshape(count, rows * part)
    width = round_up(rows * part, 128)
    a = jnp.pad(a, ((0, 0), (0, width - rows * part)))
    every = lax.all_to_all(a, ALL, split_axis=0, concat_axis=0, tiled=True)
    return jnp.sum(every, axis=0)[: rows * part].reshape(rows, part)


def on_device(
    tokens,
    cotangent,
    time_qkv,
    time_out,
    time_mix,
    space_qkv,
    space_out,
    mlp_in,
    mlp_out,
    norm_gain,
    norm_bias,
):
    layers = time_qkv.shape[0]
    clips, frames, places, d = tokens.shape
    ways = lax.axis_size("seq")
    shards = lax.axis_size("clip") * ways
    rows = Rows(clips * frames, places, ways)
    shares = lax.axis_size("head")

    def as_rows(a):
        a = a.astype(F32).reshape(rows.frames, places, d)
        a = jnp.pad(a, ((0, 0), (0, rows.frame_rows - places), (0, 0)))
        return a.reshape(rows.rows, d)

    def from_rows(a):
        a = a.reshape(rows.frames, rows.frame_rows, d)[:, :places]
        return a.reshape(tokens.shape)

    gbs = gather_norms(norm_gain, norm_bias)
    gb = [gbs[l] for l in range(layers)]
    packs = [
        pack_attention(time_qkv[l], time_out[l], time_mix[l], space_qkv[l], space_out[l])
        for l in range(layers)
    ]
    packs_ff = [pack_feed_forward(mlp_in[l], mlp_out[l], time_qkv.shape[3]) for l in range(layers)]
    home = go_home(tokens)
    gb, home, packs[1:] = lax.optimization_barrier((gb, home, packs[1:]))
    weights = [gather_slabs(packs[0])] + [gather_slabs_later(pack) for pack in packs[1:]]
    mixes = [mix_whole(w[-1], shards) for w in weights]
    quick = lax.axis_size("clip") == 4 and shares == 2 and ways == 4 and time_qkv.shape[1] % 16 == 0

    halves = Halves(lax.axis_size("clip"), d, time_qkv.shape[3])
    clip = lax.axis_index("clip")
    member = member_of(clip, lax.axis_index("seq"))
    me = jnp.stack((clip & 1, (clip >> 1) & 1, lax.axis_index("head"), member, lax.axis_index("seq"))).astype(
        jnp.int32
    )
    if quick:
        spreads = [Spread(pack, me) for pack in packs_ff]
        weights_ff = []
    else:
        weights_ff = [gather_slabs(pack) for pack in packs_ff]

    if quick:
        first = spreads[0]
        home, gb = first.step((home, gb))
    x = as_rows(home)
    send = send_first(rows, x, gb[0], me)
    kept = []
    for l in range(layers):
        w = weights[l]
        send = swap_places(send)
        if quick and l == 0:
            for _ in range(2):
                send = first.step(send)
            for spread in spreads[1:]:
                send = spread.step(send)
                send = spread.hold(send)
            send = first.step(send)
        elif quick:
            send = spreads[l].step(send)
        a1, qkv1, log1, o1_time = time_forward(rows, send, w)
        back = swap_places(o1_time)
        if quick:
            back = spreads[l].step(back)
            weights_ff.append(spreads[l].come)
            if l == 0:
                for spread in spreads[1:]:
                    back = spread.step(back)
        o1, y1, x1, qkv2 = middle_forward(rows, back, x, w, mixes[l], gb[l], me)
        o2, x2, log2 = space_forward(rows, qkv2, x1, w)
        if quick and l == 0:
            for spread in spreads[1:]:
                x2 = spread.step(x2)
        kept.append((x, a1, qkv1, log1, o1, y1, x1, qkv2, o2, log2, x2))
        if l + 1 < layers:
            x, *send = mlp_forward(rows, x2, weights_ff[l], gb[l], gb[l + 1], me)

    grad = as_rows(go_home(cotangent))
    norm_rows = [None] * layers
    summed = [None] * layers
    late = []
    for l in reversed(range(layers)):
        w = weights[l]
        x, a1, qkv1, log1, o1, y1, x1, qkv2, o2, log2, x2 = kept[l]
        grad, g_ff, s3, x3 = mlp_backward(
            rows, grad, x2, weights_ff[l], gb[l], me, halves, l + 1 == layers
        )
        if x3:
            output = go_back(from_rows(x3[0].astype(BF16)))
        if quick:
            ff = pieces_of(g_ff)
            if late:
                grad = settle(grad, late)
                grad = move(grad, late, me)
                late = [p for p in late if p.step < 3]
        grad, g_space, s2 = space_backward(rows, grad, x1, qkv2, o2, log2, w, gb[l], me, halves)
        if quick:
            space = pieces_of([g_space])
            if late:
                grad = settle(grad, late)
            grad, output = move((grad, output), ff, me)
        do1, g_out = middle_backward(rows, grad, y1, o1, w, mixes[l], me, halves, shards)
        do1 = swap_places(do1)
        if quick:
            do1 = move(do1, ff + space + late, me)
        da1, g_time = time_backward(rows, do1, a1, qkv1, log1, w, me, halves)
        if quick:
            da1 = settle(da1, ff + space)
        da1 = swap_places(da1)
        if quick:
            rest = pieces_of([g_out] + g_time)
            da1 = move(da1, ff + space + rest, me)
            late = space + rest
        grad, s1 = first_norm_back(rows, da1, x, grad, gb[l], me)
        norm_rows[l] = jnp.concatenate((s1[0:1], s2[0:1], s3[0:1], s1[1:2], s2[1:2], s3[1:2]), axis=0)
        if quick:
            summed[l] = ff + space + rest
        else:
            summed[l] = [reduce_plain(g_ff + [g_space, g_out] + g_time, clip & 1)]
    norm_sums = reduce_norms(jnp.concatenate(norm_rows, axis=0)).reshape(layers, 2, 3, -1)
    if quick:
        tokens_grad = go_back(from_rows(grad.astype(BF16)))
        tokens_grad, norm_sums = move((tokens_grad, norm_sums), late, me, True)
        move((), rest, me, True)
        summed = [[p.result for p in some] for some in summed]
    cuts = (2 * g_ff[0][0].shape[0], g_space[0].shape[0], g_out[0].shape[0], len(g_time))
    results = []
    for some in summed:
        slabs_of = jnp.concatenate(some, axis=0)
        ends = [sum(cuts[: i + 1]) for i in range(4)]
        results.append([slabs_of[e - c : e] for c, e in zip(cuts, ends)])
    if not quick:
        tokens_grad = go_back(from_rows(grad.astype(BF16)))
    tokens_grad = tokens_grad.astype(F32)

    def stacked(form):
        return jnp.stack([form(*results[l]) for l in range(layers)])

    def rows_of(a):
        return a.transpose(1, 0, 2)

    def flat(a):
        return rows_of(a).reshape(a.shape[1], -1)

    def mix_rows(a):
        r, width = a.shape
        return a.reshape(shares, r // shares, width).transpose(1, 0, 2).reshape(r // shares, -1)

    per_share = mlp_in.shape[2] // time_qkv.shape[3]
    return (
        output,
        tokens_grad,
        stacked(lambda ff, s, t, q: rows_of(q)),
        stacked(lambda ff, s, t, q: t[0].T),
        stacked(lambda ff, s, t, q: mix_rows(t[1])),
        stacked(lambda ff, s, t, q: rows_of(s[1:])),
        stacked(lambda ff, s, t, q: s[0].T),
        stacked(lambda ff, s, t, q: flat(ff[:per_share])),
        stacked(lambda ff, s, t, q: flat(ff[per_share:]).T),
        norm_sums[:, 0],
        norm_sums[:, 1],
    )


def solution(mesh):
    token_spec = P(("clip", "head"), "seq", None, None)
    in_specs = (
        token_spec,
        token_spec,
        P(None, ("clip", "seq"), None, "head"),
        P(None, "head", ("clip", "seq")),
        P(None, ("clip", "seq", "head"), None),
        P(None, ("clip", "seq"), None, "head"),
        P(None, "head", ("clip", "seq")),
        P(None, ("clip", "seq"), "head"),
        P(None, "head", ("clip", "seq")),
        P(None, None, ("clip", "seq", "head")),
        P(None, None, ("clip", "seq", "head")),
    )
    return jax.shard_map(
        on_device, mesh=mesh, in_specs=in_specs, out_specs=in_specs, check_vma=False
    )
```

```python
import functools
import math

import jax
import jax.numpy as jnp
from jax import lax
from jax.experimental import pallas as pl
from jax.experimental.pallas import tpu as pltpu
from jax.sharding import PartitionSpec as P

HEAD_DIM = 64
NORM_EPS = 1e-06
HALF_ROOT = 0.7071067811865476
INV_ROOT_TAU = 0.3989422804014327
LOG2E = 1.4426950408889634
FAR = -1e30
LANES = 128
VMEM = 56 * 1024 * 1024
SHOWN = 1.0
ALL = ("clip", "seq", "head")
BF16 = jnp.bfloat16
F32 = jnp.float32


def round_up(value, step):
    return -(-value // step) * step


def nn(a, b):
    return lax.dot_general(a, b, (((1,), (0,)), ((), ())), preferred_element_type=F32)


def nt(a, b):
    return lax.dot_general(a, b, (((1,), (1,)), ((), ())), preferred_element_type=F32)


def tn(a, b):
    return lax.dot_general(a, b, (((0,), (0,)), ((), ())), preferred_element_type=F32)


def norm_parts(x):
    mean = jnp.mean(x, axis=-1, keepdims=True)
    centred = x - mean
    spread = lax.rsqrt(jnp.mean(centred * centred, axis=-1, keepdims=True) + NORM_EPS)
    return centred * spread, spread


def norm_rounded(x, gain, bias):
    hat, _ = norm_parts(x)
    return (hat * gain + bias).astype(BF16)


def norm_back(u, x, gain):
    hat, spread = norm_parts(x)
    scaled = u * gain
    mean_scaled = jnp.mean(scaled, axis=-1, keepdims=True)
    mean_cross = jnp.mean(scaled * hat, axis=-1, keepdims=True)
    change = spread * (scaled - mean_scaled - hat * mean_cross)
    sums = jnp.concatenate(
        (jnp.sum(u * hat, axis=0, keepdims=True), jnp.sum(u, axis=0, keepdims=True)), axis=0
    )
    return change, sums


class Rows:
    def __init__(self, frames, places, ways):
        self.frames = frames
        self.places = places
        self.ways = ways
        self.frame_rows = round_up(places, 16)
        self.rows = frames * self.frame_rows
        self.block = places // ways
        self.chunk = round_up(frames * self.block, 8)
        self.time_rows = ways * self.chunk

    def split(self, r):
        way = jnp.zeros_like(r)
        for k in range(1, self.ways):
            way = way + (r >= k * self.chunk).astype(jnp.int32)
        rest = r - way * self.chunk
        frame = jnp.zeros_like(r)
        for k in range(1, self.frames):
            frame = frame + (rest >= k * self.block).astype(jnp.int32)
        real = rest < self.frames * self.block
        return way, frame, rest - frame * self.block, real

    def to_time(self, k, member):
        r = lax.broadcasted_iota(jnp.int32, (self.chunk, 1), 0)
        _, frame, place, real = self.split(r)
        way = jnp.bitwise_xor(member, k)
        source = jnp.where(real, frame * self.frame_rows + way * self.block + place, -1)
        c = lax.broadcasted_iota(jnp.int32, (self.chunk, self.rows), 1)
        return jnp.where(c == source, 1.0, 0.0).astype(BF16)

    def gathered(self, chunk_refs, member):
        total = tn(self.to_time(0, member), chunk_refs[0][...])
        for k in range(1, self.ways):
            total = total + tn(self.to_time(k, member), chunk_refs[k][...])
        return total

    def chunks(self, width, block=None, index=None):
        return [
            made((self.chunk, width), BF16)
            if block is None
            else made((self.chunk, width), BF16, (self.chunk, block), index)
            for _ in range(self.ways)
        ]

    def time_bias(self):
        def label(r):
            _, _, place, real = self.split(r)
            return jnp.where(real, place, -1)

        a = label(lax.broadcasted_iota(jnp.int32, (self.time_rows, 1), 0))
        b = label(lax.broadcasted_iota(jnp.int32, (1, self.time_rows), 1))
        return jnp.where(a == b, 0.0, FAR).astype(F32)

    def space_bias(self):
        a = lax.broadcasted_iota(jnp.int32, (self.frame_rows, 1), 0)
        return jnp.where(a < self.places, 0.0, FAR).astype(F32)


def lane_masks(rows):
    lane = lax.broadcasted_iota(jnp.int32, (rows, LANES), 1)
    return lane < HEAD_DIM


def one_of(value, low, half):
    zero = jnp.zeros_like(value)
    return jnp.where(low, value, zero) if half == 0 else jnp.where(low, zero, value)


def pair_forward(q, k, v, bias, rate):
    low = lane_masks(q.shape[0])
    mixed, logs = [], []
    for half in range(2):
        s = nt(k, one_of(q, low, half)) + bias
        peak = jnp.max(s, axis=0, keepdims=True)
        e = jnp.exp2((s - peak) * rate)
        total = jnp.sum(e, axis=0, keepdims=True)
        soft = (e * (1.0 / total)).astype(BF16)
        mixed.append(tn(soft, v))
        logs.append(peak * rate + jnp.log2(total))
    return jnp.where(low, mixed[0], mixed[1]).astype(BF16), logs


def pair_backward(q, k, v, do, logs, bias, rate, scale):
    low = lane_masks(q.shape[0])
    dq, dk, dv = [], [], []
    for half in range(2):
        s = nt(k, one_of(q, low, half)) + bias
        soft = jnp.exp2(s * rate - logs[half])
        dp = nt(v, one_of(do, low, half))
        ds = (soft * (dp - jnp.sum(soft * dp, axis=0, keepdims=True))).astype(BF16)
        dv.append(nn(soft.astype(BF16), do))
        dk.append(nn(ds, q))
        dq.append(tn(ds, k))
    return (
        (jnp.where(low, dq[0], dq[1]) * scale).astype(BF16),
        (jnp.where(low, dk[0], dk[1]) * scale).astype(BF16),
        jnp.where(low, dv[0], dv[1]).astype(BF16),
    )


def split_rows(value, keep_ref, send_ref, at, room_ref, me_ref):
    mine = me_ref[0]
    room_ref[...] = value.reshape(room_ref.shape)
    keep_ref[at] = room_ref[:, mine].astype(BF16)
    send_ref[at] = room_ref[:, 1 - mine].astype(BF16)


def store_by_core(ref, value, halves):
    n = halves.rows
    for core in range(2):
        for pair in range(halves.pairs):
            first = (2 * pair + core) * n
            ref[core, pair * n : (pair + 1) * n] = value[first : first + n]


def split_product(left_ref, right, keep_ref, send_ref, at, me_ref):
    mine = me_ref[0]
    shape = keep_ref.shape[len(at) :]
    keep_ref[at] = nn(left_ref[mine], right).reshape(shape).astype(BF16)
    send_ref[at] = nn(left_ref[1 - mine], right).reshape(shape).astype(BF16)


class Halves:
    def __init__(self, clips, depth, width):
        self.pairs = clips // 2
        self.rows = depth // clips
        self.width = width

    def array(self, lead, block, index):
        tail = (self.pairs, self.rows, self.width)
        one = lambda: made(lead + tail, BF16, block + tail, lambda *g: index(*g) + (0, 0, 0))
        return [one(), one()]

    def turned(self, columns):
        return pltpu.VMEM((2, self.pairs * self.rows, columns), BF16)

    def room(self):
        return pltpu.VMEM((self.pairs, 2, self.rows, self.width), F32)


SCALARS = pl.BlockSpec(memory_space=pltpu.SMEM)


def call(body, grid, ins, outs, scratch, args, flops=0):
    specs = [spec for spec in ins]
    moved = sum(math.prod(o.shape) * o.dtype.itemsize for o, _ in outs)
    moved += sum(math.prod(a.shape) * a.dtype.itemsize for a in args)
    return pl.pallas_call(
        body,
        out_shape=[shape for shape, _ in outs],
        grid=grid,
        in_specs=specs,
        out_specs=[spec for _, spec in outs],
        scratch_shapes=scratch,
        compiler_params=pltpu.CompilerParams(vmem_limit_bytes=VMEM),
        cost_estimate=pl.CostEstimate(
            flops=int(flops * SHOWN), bytes_accessed=int(moved * SHOWN), transcendentals=0
        ),
    )(*args)


def whole(shape):
    zeros = (0,) * len(shape)
    return pl.BlockSpec(shape, lambda *_: zeros)


def made(shape, dtype, block=None, index=None):
    spec = whole(shape) if block is None else pl.BlockSpec(block, index)
    return jax.ShapeDtypeStruct(shape, dtype), spec


def slabs(count, first, width, depth):
    return pl.BlockSpec((count, 1, depth, width), lambda h, *_: (first // count, h, 0, 0))


def send_first(rows, x, gb, me):
    def body(me_ref, x_ref, gb_ref, *out_refs):
        a = norm_rounded(x_ref[...], gb_ref[0:1], gb_ref[3:4])
        for k in range(rows.ways):
            out_refs[k][...] = nn(rows.to_time(k, me_ref[3]), a).astype(BF16)

    d = x.shape[1]
    return call(
        body, (1,), [SCALARS, whole(x.shape), whole(gb.shape)], rows.chunks(d), [], (me, x, gb)
    )


def time_forward(rows, chunks, w):
    t, d = rows.time_rows, chunks[0].shape[1]
    width = w.shape[3]
    shares = w.shape[1]
    pairs = width // LANES
    ways = rows.ways
    rate = LOG2E / math.sqrt(HEAD_DIM)

    def body(*refs):
        chunk_refs = refs[:ways]
        w_ref, a_ref, qkv_ref, log_ref = refs[ways : ways + 4]
        out_refs = refs[ways + 4 : 2 * ways + 4]
        bias_ref, mixed_ref = refs[2 * ways + 4 :]

        @pl.when(pl.program_id(0) == 0)
        def _():
            bias_ref[...] = rows.time_bias()
            for k in range(ways):
                a_ref[k * rows.chunk : (k + 1) * rows.chunk] = chunk_refs[k][...]

        act = a_ref[...]
        for g in range(3):
            qkv_ref[g] = nn(act, w_ref[g, 0]).astype(BF16)

        @pl.loop(0, pairs)
        def _(i):
            lanes = pl.ds(pl.multiple_of(i * LANES, LANES), LANES)
            mixed, logs = pair_forward(
                qkv_ref[0, :, lanes], qkv_ref[1, :, lanes], qkv_ref[2, :, lanes], bias_ref[...], rate
            )
            mixed_ref[:, lanes] = mixed
            log_ref[0, i] = jnp.concatenate(logs, axis=0)

        for k in range(ways):
            out_refs[k][...] = mixed_ref[k * rows.chunk : (k + 1) * rows.chunk]

    got = call(
        body,
        (shares,),
        [whole(c.shape) for c in chunks] + [slabs(3, 0, width, d)],
        [
            made((t, d), BF16),
            made((3, t, d), BF16, (3, t, width), lambda h: (0, 0, h)),
            made((shares, pairs, 2, t), F32, (1, pairs, 2, t), lambda h: (h, 0, 0, 0)),
            *rows.chunks(d, width, lambda h: (0, h)),
        ],
        [pltpu.VMEM((t, t), F32), pltpu.VMEM((t, width), BF16)],
        (*chunks, w),
        flops=2 * t * d * 3 * d,
    )
    return got[0], got[1], got[2], got[3:]


def middle_forward(rows, back, x, w, mix, gb, me):
    t, d = x.shape
    width = w.shape[3]
    shares = w.shape[1]

    def body(me_ref, *refs):
        x_ref, to_ref, sq_ref, mix_ref, gb_ref, o1_ref, y1_ref, x1_ref, qkv_ref = refs[rows.ways :]
        o1 = rows.gathered(refs[: rows.ways], me_ref[3]).astype(BF16)
        o1_ref[...] = o1
        y1 = jnp.zeros((t, d), F32)
        for h in range(shares):
            y1 = y1 + nt(o1[:, h * width : (h + 1) * width], to_ref[0, h])
        y1 = y1.astype(BF16)
        y1_ref[...] = y1
        x1 = x_ref[...] + nn(y1, mix_ref[...])
        x1_ref[...] = x1
        a2 = norm_rounded(x1, gb_ref[1:2], gb_ref[4:5])
        for g in range(3):
            for h in range(shares):
                qkv_ref[g, :, h * width : (h + 1) * width] = nn(a2, sq_ref[g, h]).astype(BF16)

    return call(
        body,
        (1,),
        [
            SCALARS,
            *(whole(c.shape) for c in back),
            whole(x.shape),
            pl.BlockSpec((1, shares, d, width), lambda i: (6, 0, 0, 0)),
            pl.BlockSpec((3, shares, d, width), lambda i: (1, 0, 0, 0)),
            whole(mix.shape),
            whole(gb.shape),
        ],
        [made((t, d), BF16), made((t, d), BF16), made((t, d), F32), made((3, t, d), BF16)],
        [],
        (me, *back, x, w, w, mix, gb),
        flops=2 * t * d * 5 * d,
    )


def space_forward(rows, qkv, x1, w):
    t, d = x1.shape
    width = w.shape[3]
    shares = w.shape[1]
    pairs = width // LANES
    rate = LOG2E / math.sqrt(HEAD_DIM)
    n = rows.frame_rows

    def body(qkv_ref, x1_ref, w_ref, o2_ref, x2_ref, log_ref):
        bias = rows.space_bias()

        @pl.loop(0, pairs)
        def _(i):
            lanes = pl.ds(pl.multiple_of(i * LANES, LANES), LANES)
            for f in range(rows.frames):
                at = slice(f * n, (f + 1) * n)
                mixed, logs = pair_forward(
                    qkv_ref[0, at, lanes], qkv_ref[1, at, lanes], qkv_ref[2, at, lanes], bias, rate
                )
                o2_ref[at, lanes] = mixed
                log_ref[0, i, f] = jnp.concatenate(logs, axis=0)

        @pl.when(pl.program_id(0) == 0)
        def _():
            x2_ref[...] = x1_ref[...]

        x2_ref[...] += nt(o2_ref[...], w_ref[0, 0])

    return call(
        body,
        (shares,),
        [
            pl.BlockSpec((3, t, width), lambda h: (0, 0, h)),
            whole(x1.shape),
            slabs(1, 7, width, d),
        ],
        [
            made((t, d), BF16, (t, width), lambda h: (0, h)),
            made((t, d), F32),
            made(
                (shares, pairs, rows.frames, 2, n),
                F32,
                (1, pairs, rows.frames, 2, n),
                lambda h: (h, 0, 0, 0, 0),
            ),
        ],
        [],
        (qkv, x1, w),
        flops=2 * t * d * d,
    )


def ff_slab(first, per_share, depth, width):
    return pl.BlockSpec(
        (1, 1, depth, width), lambda j: (first + j % per_share, j // per_share, 0, 0)
    )


def mlp_forward(rows, x2, w, gb, gb_next, me):
    t, d = x2.shape
    width = w.shape[3]
    shares = w.shape[1]
    per_share = w.shape[0] // 2
    steps = shares * per_share

    def body(x2_ref, wi_ref, wo_ref, gb_ref, me_ref, gn_ref, x3_ref, *rest):
        send_refs, a3_ref = rest[:-1], rest[-1]
        j = pl.program_id(0)

        @pl.when(j == 0)
        def _():
            a3_ref[...] = norm_rounded(x2_ref[...], gb_ref[2:3], gb_ref[5:6])
            x3_ref[...] = x2_ref[...]

        hid = nn(a3_ref[...], wi_ref[0, 0])
        act = (0.5 * hid * (1.0 + lax.erf(hid * HALF_ROOT))).astype(BF16)
        x3_ref[...] += nt(act, wo_ref[0, 0])

        @pl.when(j == steps - 1)
        def _():
            a = norm_rounded(x3_ref[...], gn_ref[0:1], gn_ref[3:4])
            for k in range(rows.ways):
                send_refs[k][...] = nn(rows.to_time(k, me_ref[3]), a).astype(BF16)

    ins = [
        whole(x2.shape),
        ff_slab(0, per_share, d, width),
        ff_slab(per_share, per_share, d, width),
        whole(gb.shape),
    ]
    ins += [SCALARS, whole(gb_next.shape)]
    outs = [made((t, d), F32)] + rows.chunks(d)
    args = (x2, w, w, gb, me, gb_next)
    return call(
        body, (steps,), ins, outs, [pltpu.VMEM((t, d), BF16)], args, flops=4 * t * d * width * steps
    )


def mlp_backward(rows, grad, x2, w, gb, me, halves, with_output):
    t, d = x2.shape
    width = w.shape[3]
    shares = w.shape[1]
    per_share = w.shape[0] // 2
    steps = shares * per_share

    def body(me_ref, g_ref, x2_ref, wi_ref, wo_ref, gb_ref, go_ref, ki_ref, si_ref, ko_ref, so_ref, sums_ref, *rest):
        if with_output:
            x3_ref, *rest = rest
        a3_ref, a3t_ref, e3_ref, e3t_ref, u_ref = rest
        j = pl.program_id(0)

        @pl.when(j == 0)
        def _():
            hat, _ = norm_parts(x2_ref[...])
            a3 = hat * gb_ref[2:3] + gb_ref[5:6]
            a3_ref[...] = a3.astype(BF16)
            store_by_core(a3t_ref, a3.T.astype(BF16), halves)
            g = g_ref[...]
            e3_ref[...] = g.astype(BF16)
            store_by_core(e3t_ref, g.T.astype(BF16), halves)
            u_ref[...] = jnp.zeros((t, d), F32)
            if with_output:
                x3_ref[...] = x2_ref[...]

        hid = nn(a3_ref[...], wi_ref[0, 0])
        phi = 0.5 * (1.0 + lax.erf(hid * HALF_ROOT))
        act = (hid * phi).astype(BF16)
        slope = phi + hid * jnp.exp(-0.5 * hid * hid) * INV_ROOT_TAU
        dhid = (nn(e3_ref[...], wo_ref[0, 0]) * slope).astype(BF16)
        split_product(e3t_ref, act, ko_ref, so_ref, (0, 0), me_ref)
        split_product(a3t_ref, dhid, ki_ref, si_ref, (0, 0), me_ref)
        u_ref[...] += nt(dhid, wi_ref[0, 0])
        if with_output:
            x3_ref[...] += nt(act, wo_ref[0, 0])

        @pl.when(j == steps - 1)
        def _():
            change, sums = norm_back(u_ref[...], x2_ref[...], gb_ref[2:3])
            go_ref[...] = g_ref[...] + change
            sums_ref[...] = sums

    slab_outs = [
        one
        for _ in range(2)
        for one in halves.array(
            (per_share, shares), (1, 1), lambda j: (j % per_share, j // per_share)
        )
    ]
    grad, ki, si, ko, so, sums, *x3 = call(
        body,
        (steps,),
        [
            SCALARS,
            whole(grad.shape),
            whole(x2.shape),
            ff_slab(0, per_share, d, width),
            ff_slab(per_share, per_share, d, width),
            whole(gb.shape),
        ],
        [made((t, d), F32), *slab_outs, made((2, d), F32)] + [made((t, d), F32)] * with_output,
        [
            pltpu.VMEM((t, d), BF16),
            halves.turned(t),
            pltpu.VMEM((t, d), BF16),
            halves.turned(t),
            pltpu.VMEM((t, d), F32),
        ],
        (me, grad, x2, w, w, gb),
        flops=10 * t * d * width * steps,
    )
    return grad, [(ki, si), (ko, so)], sums, x3


def space_backward(rows, grad, x1, qkv, o2, logs, w, gb, me, halves):
    t, d = x1.shape
    width = w.shape[3]
    shares = w.shape[1]
    pairs = width // LANES
    scale = 1.0 / math.sqrt(HEAD_DIM)
    rate = LOG2E * scale
    n = rows.frame_rows

    def body(me_ref, g_ref, x1_ref, qkv_ref, o2_ref, log_ref, wo_ref, wq_ref, gb_ref, go_ref, keep_ref, send_ref, sums_ref, e2_ref, e2t_ref, a2t_ref, do_ref, dqkv_ref, u_ref):
        h = pl.program_id(0)

        @pl.when(h == 0)
        def _():
            g = g_ref[...]
            e2_ref[...] = g.astype(BF16)
            store_by_core(e2t_ref, g.T.astype(BF16), halves)
            hat, _ = norm_parts(x1_ref[...])
            store_by_core(a2t_ref, (hat * gb_ref[1:2] + gb_ref[4:5]).T.astype(BF16), halves)
            u_ref[...] = jnp.zeros((t, d), F32)

        bias = rows.space_bias()
        split_product(e2t_ref, o2_ref[...], keep_ref, send_ref, (0, 0), me_ref)
        do_ref[...] = nn(e2_ref[...], wo_ref[0, 0]).astype(BF16)

        @pl.loop(0, pairs)
        def _(i):
            lanes = pl.ds(pl.multiple_of(i * LANES, LANES), LANES)
            for f in range(rows.frames):
                at = slice(f * n, (f + 1) * n)
                log = log_ref[0, i, f]
                grads = pair_backward(
                    qkv_ref[0, at, lanes],
                    qkv_ref[1, at, lanes],
                    qkv_ref[2, at, lanes],
                    do_ref[at, lanes],
                    (log[0:1], log[1:2]),
                    bias,
                    rate,
                    scale,
                )
                for part in range(3):
                    dqkv_ref[part, at, lanes] = grads[part]

        for part in range(3):
            split_product(a2t_ref, dqkv_ref[part], keep_ref, send_ref, (part + 1, 0), me_ref)
            u_ref[...] += nt(dqkv_ref[part], wq_ref[part, 0])

        @pl.when(h == shares - 1)
        def _():
            change, sums = norm_back(u_ref[...], x1_ref[...], gb_ref[1:2])
            go_ref[...] = g_ref[...] + change
            sums_ref[...] = sums

    grad, keep, send, sums = call(
        body,
        (shares,),
        [
            SCALARS,
            whole(grad.shape),
            whole(x1.shape),
            pl.BlockSpec((3, t, width), lambda h: (0, 0, h)),
            pl.BlockSpec((t, width), lambda h: (0, h)),
            pl.BlockSpec((1,) + logs.shape[1:], lambda h: (h, 0, 0, 0, 0)),
            slabs(1, 7, width, d),
            slabs(3, 3, width, d),
            whole(gb.shape),
        ],
        [
            made((t, d), F32),
            *halves.array((4, shares), (4, 1), lambda h: (0, h)),
            made((2, d), F32),
        ],
        [
            pltpu.VMEM((t, d), BF16),
            halves.turned(t),
            halves.turned(t),
            pltpu.VMEM((t, width), BF16),
            pltpu.VMEM((3, t, width), BF16),
            pltpu.VMEM((t, d), F32),
        ],
        (me, grad, x1, qkv, o2, logs, w, w, gb),
        flops=2 * t * d * d * 8,
    )
    return grad, (keep, send), sums


def mix_fits(depth, shards, shares):
    return depth // (shards * shares) % 8 == 0


def middle_backward(rows, grad, y1, o1, w, mix, me, halves, shards):
    t, d = grad.shape
    width = w.shape[3]
    shares = w.shape[1]
    fits = mix_fits(d, shards, shares)
    part = d // (shards * shares)

    def body(me_ref, g_ref, y1_ref, o1_ref, to_ref, mix_ref, *rest):
        send_refs, rest = rest[: rows.ways], rest[rows.ways :]
        gk_ref, gs_ref, *rest = rest
        if fits:
            room_ref, order_ref = rest
        else:
            gm_ref, room_ref = rest
        e1 = g_ref[...].astype(BF16)
        dy1 = nt(e1, mix_ref[...]).astype(BF16)
        sends = [rows.to_time(k, me_ref[3]) for k in range(rows.ways)]
        for h in range(shares):
            lanes = slice(h * width, (h + 1) * width)
            do1 = nn(dy1, to_ref[0, h]).astype(BF16)
            for k in range(rows.ways):
                send_refs[k][:, lanes] = nn(sends[k], do1).astype(BF16)
            split_rows(tn(dy1, o1_ref[:, lanes]), gk_ref, gs_ref, (0, h), room_ref, me_ref)
        gm = tn(y1_ref[...], e1)
        if fits:
            gm = gm.reshape(shards, shares, part, d)
            for h in range(shares):
                for half in range(shares):
                    order_ref[:, half] = gm[:, h, :, half * width : (half + 1) * width]
                split_rows(order_ref[...], gk_ref, gs_ref, (1, h), room_ref, me_ref)
        else:
            gm_ref[...] = gm.astype(BF16)

    outs = rows.chunks(d)
    outs += halves.array((1 + fits, shares), (1 + fits, shares), lambda i: (0, 0))
    scratch = [halves.room()]
    if fits:
        scratch.append(pltpu.VMEM((shards, shares, part, width), F32))
    else:
        outs.append(made((d, d), BF16))
    got = call(
        body,
        (1,),
        [
            SCALARS,
            whole(grad.shape),
            whole(y1.shape),
            whole(o1.shape),
            pl.BlockSpec((1, shares, d, width), lambda i: (6, 0, 0, 0)),
            whole(mix.shape),
        ],
        outs,
        scratch,
        (me, grad, y1, o1, w, mix),
        flops=8 * t * d * d,
    )
    do1, (keep, send) = got[: rows.ways], got[rows.ways : rows.ways + 2]
    if not fits:
        gm = mix_slab(got[-1], shards, shares).reshape((1, shares, halves.pairs, 2) + keep.shape[3:])
        keep = jnp.concatenate((keep, lax.dynamic_index_in_dim(gm, me[0], 3, keepdims=False)), axis=0)
        send = jnp.concatenate((send, lax.dynamic_index_in_dim(gm, 1 - me[0], 3, keepdims=False)), axis=0)
    return do1, (keep, send)


def time_backward(rows, do1, a, qkv, logs, w, me, halves):
    t, d = a.shape
    width = w.shape[3]
    shares = w.shape[1]
    pairs = width // LANES
    scale = 1.0 / math.sqrt(HEAD_DIM)
    rate = LOG2E * scale

    def body(me_ref, *refs):
        do_refs, refs = refs[: rows.ways], refs[rows.ways :]
        a_ref, qkv_ref, log_ref, w_ref = refs[:4]
        out_refs, refs = refs[4 : 4 + rows.ways], refs[4 + rows.ways :]
        half_refs, refs = refs[:6], refs[6:]
        bias_ref, dqkv_ref, at_ref, u_ref, do_ref = refs
        h = pl.program_id(0)

        @pl.when(h == 0)
        def _():
            bias_ref[...] = rows.time_bias()
            store_by_core(at_ref, a_ref[...].T, halves)
            u_ref[...] = jnp.zeros((t, d), F32)

        for k in range(rows.ways):
            do_ref[k * rows.chunk : (k + 1) * rows.chunk] = do_refs[k][...]

        @pl.loop(0, pairs)
        def _(i):
            lanes = pl.ds(pl.multiple_of(i * LANES, LANES), LANES)
            log = log_ref[0, i]
            grads = pair_backward(
                qkv_ref[0, :, lanes],
                qkv_ref[1, :, lanes],
                qkv_ref[2, :, lanes],
                do_ref[:, lanes],
                (log[0:1], log[1:2]),
                bias_ref[...],
                rate,
                scale,
            )
            for part in range(3):
                dqkv_ref[part, :, lanes] = grads[part]

        for part in range(3):
            split_product(
                at_ref, dqkv_ref[part], half_refs[2 * part], half_refs[2 * part + 1], (0, 0), me_ref
            )
            u_ref[...] += nt(dqkv_ref[part], w_ref[part, 0])

        @pl.when(h == shares - 1)
        def _():
            for k in range(rows.ways):
                out_refs[k][...] = u_ref[k * rows.chunk : (k + 1) * rows.chunk].astype(BF16)

    got = call(
        body,
        (shares,),
        [
            SCALARS,
            *(pl.BlockSpec((rows.chunk, width), lambda h: (0, h)) for _ in do1),
            whole(a.shape),
            pl.BlockSpec((3, t, width), lambda h: (0, 0, h)),
            pl.BlockSpec((1,) + logs.shape[1:], lambda h: (h, 0, 0, 0)),
            slabs(3, 0, width, d),
        ],
        [
            *rows.chunks(d),
            *(one for _ in range(3) for one in halves.array((1, shares), (1, 1), lambda h: (0, h))),
        ],
        [
            pltpu.VMEM((t, t), F32),
            pltpu.VMEM((3, t, width), BF16),
            halves.turned(t),
            pltpu.VMEM((t, d), F32),
            pltpu.VMEM((t, width), BF16),
        ],
        (me, *do1, a, qkv, logs, w),
        flops=2 * t * d * d * 6,
    )
    parts = got[rows.ways :]
    return got[: rows.ways], [tuple(parts[i : i + 2]) for i in (0, 2, 4)]


def first_norm_back(rows, back, x, grad, gb, me):
    t, d = x.shape

    def body(me_ref, *refs):
        x_ref, g_ref, gb_ref, go_ref, sums_ref = refs[rows.ways :]
        u = rows.gathered(refs[: rows.ways], me_ref[3])
        change, sums = norm_back(u, x_ref[...], gb_ref[0:1])
        go_ref[...] = g_ref[...] + change
        sums_ref[...] = sums

    return call(
        body,
        (1,),
        [SCALARS, *(whole(c.shape) for c in back), whole(x.shape), whole(grad.shape), whole(gb.shape)],
        [made((t, d), F32), made((2, d), F32)],
        [],
        (me, *back, x, grad, gb),
    )


def homes():
    clips, ways = lax.axis_size("clip"), lax.axis_size("seq")
    pairs = []
    for clip in range(clips):
        for seq in range(ways):
            home_clip = clip - clip % 2 + seq % 2
            home_seq = seq // 2 + (ways // 2) * (clip % 2)
            pairs.append((clip * ways + seq, home_clip * ways + home_seq))
    return pairs


def go_home(a):
    return lax.ppermute(a, ("clip", "seq"), homes())


def go_back(a):
    return lax.ppermute(a, ("clip", "seq"), [(home, device) for device, home in homes()])


def member_of(clip, seq):
    return clip % 2 + 2 * (seq % (lax.axis_size("seq") // 2))


def swap_places(chunks):
    clips, ways = lax.axis_size("clip"), lax.axis_size("seq")
    got = [chunks[0]]
    for k in range(1, ways):
        pairs = []
        for clip in range(clips):
            for seq in range(ways):
                other = member_of(clip, seq) ^ k
                to_clip = clip - clip % 2 + other % 2
                to_seq = seq - seq % (ways // 2) + other // 2
                pairs.append((clip * ways + seq, to_clip * ways + to_seq))
        got.append(lax.ppermute(chunks[k], ("clip", "seq"), pairs))
    return got


def columns(a, r, width):
    return a.reshape(r, -1, width).transpose(1, 0, 2)


def pack_attention(time_qkv, time_out, time_mix, space_qkv, space_out):
    r, _, width = time_qkv.shape
    mix = time_mix.reshape(-1, time_mix.shape[1] // width, width).transpose(1, 0, 2).reshape(1, r, width)
    return jnp.concatenate(
        (
            columns(time_qkv, r, width),
            columns(space_qkv, r, width),
            time_out.T[None],
            space_out.T[None],
            mix,
        ),
        axis=0,
    )


def pack_feed_forward(mlp_in, mlp_out, width):
    r = mlp_in.shape[0]
    return jnp.concatenate((columns(mlp_in, r, width), columns(mlp_out.T, r, width)), axis=0)


def gather_slabs(pack):
    full = lax.all_gather(pack, ("head", "clip", "seq"), axis=1, tiled=True)
    return full.reshape(pack.shape[0], lax.axis_size("head"), -1, pack.shape[2])


def gather_slabs_later(pack):
    parts = [lax.all_gather(a, "seq", axis=1, tiled=True) for a in jnp.split(pack, [5], axis=0)]
    full = lax.all_gather(jnp.concatenate(parts, axis=0), ("head", "clip"), axis=1, tiled=True)
    return full.reshape(pack.shape[0], lax.axis_size("head"), -1, pack.shape[2])


def spread_steps(pack, me):
    ways, clips = lax.axis_size("seq"), lax.axis_size("clip")
    shares = lax.axis_size("head")
    n, r, width = pack.shape
    pack = yield pack
    turned = [pack] + [
        lax.ppermute(pack, "seq", [(i, (i + k) % ways) for i in range(ways)]) for k in range(1, ways)
    ]
    turned = yield turned
    orders = (((0, 1), "x", "h"), ((3, 2), "h", "x"))
    some = [jnp.stack([turned[k] for k in steps]) for steps, _, _ in orders]
    come = yield [cross(a, first) for a, (_, first, _) in zip(some, orders)]
    some = [jnp.concatenate(pair, axis=0) for pair in zip(some, come)]
    come = yield [cross(a, second) for a, (_, _, second) in zip(some, orders)]
    runs = []
    for mine, other, (steps, first, second) in zip(some, come, orders):
        where = [(k, {first: f}) for f in (0, 1) for k in steps]
        for g, blocks in enumerate((mine, other)):
            runs.append((blocks, [(k, {**at, second: g}) for k, at in where], 0))
    come = yield [cross(blocks, "c") for blocks, _, _ in runs]
    runs += [(far, where, 1) for far, (_, where, _) in zip(come, runs)]
    count = sum(len(where) for _, where, _ in runs)

    def body(me_ref, *refs):
        sources, out_ref, sems = refs[: len(runs)], refs[-2], refs[-1]
        copies = []
        for source, (_, where, core) in zip(sources, runs):
            for i, (k, at) in enumerate(where):
                share = jnp.bitwise_xor(me_ref[2], at["h"])
                clip = 2 * jnp.bitwise_xor(me_ref[1], at["x"]) + jnp.bitwise_xor(me_ref[0], core)
                seq = lax.rem(me_ref[4] + (ways - k), ways)
                copies.append(
                    pltpu.make_async_copy(
                        source.at[i], out_ref.at[:, share, clip * ways + seq], sems.at[len(copies)]
                    )
                )
        for copy in copies:
            copy.start()
        for copy in copies:
            copy.wait()

    full = pl.pallas_call(
        body,
        out_shape=jax.ShapeDtypeStruct((n, shares, clips * ways, r, width), BF16),
        in_specs=[SCALARS] + [pl.BlockSpec(memory_space=pltpu.HBM)] * len(runs),
        out_specs=pl.BlockSpec(memory_space=pltpu.VMEM),
        scratch_shapes=[pltpu.SemaphoreType.DMA((count,))],
        compiler_params=pltpu.CompilerParams(vmem_limit_bytes=VMEM),
        cost_estimate=pl.CostEstimate(
            flops=0, bytes_accessed=4 * n * shares * clips * ways * r * width, transcendentals=0
        ),
    )(me, *(blocks for blocks, _, _ in runs))
    yield full.reshape(n, shares, clips * ways * r, width)


class Spread:
    def __init__(self, pack, me):
        self.way = spread_steps(pack, me)
        self.come = next(self.way)

    def hold(self, x):
        x, self.come = lax.optimization_barrier((x, self.come))
        return x

    def step(self, x):
        x = self.hold(x)
        self.come = self.way.send(self.come)
        return x


def mix_whole(slab, shards):
    shares, depth, width = slab.shape
    part = slab.reshape(shares, shards, shares, depth // (shards * shares), width)
    return part.transpose(1, 0, 3, 2, 4).reshape(depth, shares * width)


def mix_slab(whole_grad, shards, shares):
    depth, full = whole_grad.shape
    width = full // shares
    part = whole_grad.reshape(shards, shares, depth // (shards * shares), shares, width)
    return part.transpose(1, 0, 3, 2, 4).reshape(1, shares, depth, width)


class Piece:
    def __init__(self, keep, got, first, n, order):
        self.near = (keep, got)
        self.first = first
        self.n = n
        self.order = order
        self.step = 0
        self.held = []
        self.result = None


PLACE = {"x": 1, "h": 2}


def fold(pieces, me, last_by_rows):
    ways = lax.axis_size("seq")
    depth, width = pieces[0].near[0].shape[-2:]
    r = depth // ways
    used = {}
    arrays = []

    def number(a):
        for i, known in enumerate(arrays):
            if known is a:
                return i
        arrays.append(a)
        return len(arrays) - 1

    plans = []
    for p in pieces:
        link = p.order[p.step] if p.step < 2 else "z"
        blocks = p.n * (2 if p.step == 0 else 1)
        base = used.get(link, 0)
        used[link] = base + blocks
        near = [number(a) for a in p.near]
        held = [(number(a), at) for a, at in p.held]
        plans.append((p, link, base, near, held))
    links = sorted(used)
    shapes = [
        (ways, used[k], r, width) if k == "z" and last_by_rows else (used[k], depth, width)
        for k in links
    ]
    rooms, counts = [], []
    for p, link, base, near, held in plans:
        each = 2 if p.step == 0 else 1
        counts.append((each, len(near) + len(held)))
        rooms += [(each * p.n, depth, width)] * (len(near) + len(held))
    copies_needed = sum(each * terms for each, terms in counts)

    def body(me_ref, *refs):
        sources = refs[: len(arrays)]
        outs = dict(zip(links, refs[len(arrays) : len(arrays) + len(links)]))
        held_refs = refs[len(arrays) + len(links) : -1]
        sems = refs[-1]
        mine = {name: me_ref[PLACE[name]] for name in PLACE}
        groups = []
        room = 0
        sem = 0
        for p, link, base, near, held in plans:
            group = []
            if p.step == 0:
                for term in near:
                    for k in range(2):
                        pick = {p.order[0]: 1 - mine[p.order[0]], p.order[1]: k}
                        source = sources[term].at[pl.ds(p.first, p.n), pick["h"], pick["x"]]
                        group.append((source, held_refs[room].at[pl.ds(k * p.n, p.n)]))
                    room += 1
            else:
                last = p.order[1]
                pick = {p.order[0]: mine[p.order[0]]}
                pick[last] = 1 - mine[last] if p.step == 1 else mine[last]
                for term in near:
                    source = sources[term].at[pl.ds(p.first, p.n), pick["h"], pick["x"]]
                    group.append((source, held_refs[room]))
                    room += 1
                for i, (term, at) in enumerate(held):
                    start = at + pick[last] * p.n if i == 0 else at
                    group.append((sources[term].at[pl.ds(start, p.n)], held_refs[room]))
                    room += 1
            made_copies = []
            for source, target in group:
                made_copies.append(pltpu.make_async_copy(source, target, sems.at[sem]))
                sem += 1
            groups.append(made_copies)
        for group in groups:
            for copy in group:
                copy.start()
        room = 0
        for (p, link, base, near, held), (each, terms), group in zip(plans, counts, groups):
            these = held_refs[room : room + terms]
            room += terms
            for copy in group:
                copy.wait()

            @pl.loop(0, each * p.n)
            def _(i, these=these, base=base, out=outs[link], last=p.step == 2 and last_by_rows):
                value = these[0][i].astype(F32)
                for one in these[1:]:
                    value = value + one[i].astype(F32)
                value = value.astype(BF16)
                if last:
                    for k in range(ways):
                        out[k, base + i] = value[k * r : (k + 1) * r]
                else:
                    out[base + i] = value

    moved = sum(2 * math.prod(room) for room in rooms) + sum(2 * math.prod(shape) for shape in shapes)
    sums = pl.pallas_call(
        body,
        out_shape=[jax.ShapeDtypeStruct(shape, BF16) for shape in shapes],
        in_specs=[SCALARS] + [pl.BlockSpec(memory_space=pltpu.HBM)] * len(arrays),
        out_specs=[pl.BlockSpec(memory_space=pltpu.VMEM)] * len(links),
        scratch_shapes=[pltpu.VMEM(room, BF16) for room in rooms]
        + [pltpu.SemaphoreType.DMA((copies_needed,))],
        compiler_params=pltpu.CompilerParams(vmem_limit_bytes=VMEM),
        cost_estimate=pl.CostEstimate(flops=0, bytes_accessed=moved, transcendentals=0),
    )(me, *arrays)
    return [(p, link, base) for p, link, base, _, _ in plans], dict(zip(links, sums))


def cross(a, name):
    axis, bit = ("head", 0) if name == "h" else ("clip", 1 if name == "x" else 0)
    size = lax.axis_size(axis)
    return lax.ppermute(a, axis, [(i, i ^ (1 << bit)) for i in range(size)])


def pieces_of(halves_of):
    total = sum(keep.shape[0] for keep, _ in halves_of)
    found = []
    seen = 0
    for keep, send in halves_of:
        got = cross(send, "c")
        n = keep.shape[0]
        first = min(max((total + 1) // 2 - seen, 0), n)
        if first:
            found.append(Piece(keep, got, 0, first, ("x", "h")))
        if n > first:
            found.append(Piece(keep, got, first, n - first, ("h", "x")))
        seen += n
    return found


def move(x, pieces, me, at_end=False):
    plans, sums = fold(pieces, me, at_end)
    x, sums = lax.optimization_barrier((x, sums))
    got = {}
    for link, array in sums.items():
        if link == "z":
            if at_end:
                every = lax.all_to_all(array, "seq", split_axis=0, concat_axis=0, tiled=True)
                got[link] = jnp.sum(every.astype(F32), axis=0)
            else:
                own = lax.psum_scatter(array, "seq", scatter_dimension=1, tiled=True)
                got[link] = own.astype(F32)
        else:
            got[link] = cross(array, link)
    for p, link, base in plans:
        if link == "z":
            p.result = got[link][base : base + p.n]
        else:
            p.held.append((got[link], base))
        p.step += 1
    return x


def settle(x, pieces):
    arrays = []
    for p in pieces:
        if not any(p.held[-1][0] is a for a in arrays):
            arrays.append(p.held[-1][0])
    x, came = lax.optimization_barrier((x, arrays))
    for p in pieces:
        for old, new in zip(arrays, came):
            if p.held[-1][0] is old:
                p.held[-1] = (new, p.held[-1][1])
                break
    return x


def reduce_plain(halves_of, core):
    def joined(keep, send):
        low = jnp.where(core == 0, keep, send)
        high = jnp.where(core == 0, send, keep)
        n, shares, pairs, depth, width = keep.shape
        return jnp.stack((low, high), axis=3).reshape(n, shares, 2 * pairs * depth, width)

    g = jnp.concatenate([joined(*pair) for pair in halves_of], axis=0)
    g = lax.psum_scatter(g, "head", scatter_dimension=1, tiled=True)
    g = lax.psum_scatter(g.astype(F32), ("clip", "seq"), scatter_dimension=2, tiled=True)
    return g[:, 0]


def gather_norms(gain, bias):
    layers, norms, part = gain.shape
    both = jnp.concatenate((gain, bias), axis=1).reshape(1, -1)
    count = lax.axis_size("clip") * lax.axis_size("seq") * lax.axis_size("head")
    width = round_up(both.shape[1], 128)
    padded = jnp.pad(both, ((0, 0), (0, width - both.shape[1])))
    every = lax.all_to_all(
        jnp.broadcast_to(padded, (count, width)), ALL, split_axis=0, concat_axis=0, tiled=True
    )[:, : both.shape[1]]
    return every.reshape(count, layers * 2 * norms, part).transpose(1, 0, 2).reshape(layers, 2 * norms, -1)


def reduce_norms(sums):
    count = lax.axis_size("clip") * lax.axis_size("seq") * lax.axis_size("head")
    rows, features = sums.shape
    part = features // count
    a = sums.reshape(rows, count, part).transpose(1, 0, 2).reshape(count, rows * part)
    width = round_up(rows * part, 128)
    a = jnp.pad(a, ((0, 0), (0, width - rows * part)))
    every = lax.all_to_all(a, ALL, split_axis=0, concat_axis=0, tiled=True)
    return jnp.sum(every, axis=0)[: rows * part].reshape(rows, part)


def on_device(
    tokens,
    cotangent,
    time_qkv,
    time_out,
    time_mix,
    space_qkv,
    space_out,
    mlp_in,
    mlp_out,
    norm_gain,
    norm_bias,
):
    layers = time_qkv.shape[0]
    clips, frames, places, d = tokens.shape
    ways = lax.axis_size("seq")
    shards = lax.axis_size("clip") * ways
    rows = Rows(clips * frames, places, ways)
    shares = lax.axis_size("head")

    def as_rows(a):
        a = a.astype(F32).reshape(rows.frames, places, d)
        a = jnp.pad(a, ((0, 0), (0, rows.frame_rows - places), (0, 0)))
        return a.reshape(rows.rows, d)

    def from_rows(a):
        a = a.reshape(rows.frames, rows.frame_rows, d)[:, :places]
        return a.reshape(tokens.shape)

    gbs = gather_norms(norm_gain, norm_bias)
    gb = [gbs[l] for l in range(layers)]
    packs = [
        pack_attention(time_qkv[l], time_out[l], time_mix[l], space_qkv[l], space_out[l])
        for l in range(layers)
    ]
    packs_ff = [pack_feed_forward(mlp_in[l], mlp_out[l], time_qkv.shape[3]) for l in range(layers)]
    weights = [gather_slabs(packs[0])]
    home = go_home(tokens)
    quick = lax.axis_size("clip") == 4 and shares == 2 and ways == 4 and time_qkv.shape[1] % 16 == 0

    halves = Halves(lax.axis_size("clip"), d, time_qkv.shape[3])
    clip = lax.axis_index("clip")
    member = member_of(clip, lax.axis_index("seq"))
    me = jnp.stack((clip & 1, (clip >> 1) & 1, lax.axis_index("head"), member, lax.axis_index("seq"))).astype(
        jnp.int32
    )
    if quick:
        spreads = [Spread(pack, me) for pack in packs_ff]
        weights_ff = []
    else:
        weights_ff = [gather_slabs(pack) for pack in packs_ff]

    if quick:
        first = spreads[0]
        home, gb = first.step((home, gb))
    x = as_rows(home)
    send = swap_places(send_first(rows, x, gb[0], me))
    if quick:
        send, packs[1:] = first.step((send, packs[1:]))
    weights += [gather_slabs_later(pack) for pack in packs[1:]]
    mixes = [mix_whole(w[-1], shards) for w in weights]
    kept = []
    for l in range(layers):
        w = weights[l]
        if l:
            send = swap_places(send)
        if quick and l == 0:
            for spread in spreads[1:]:
                send = spread.step(send)
            send = first.step(send)
            for spread in spreads[1:]:
                send = spread.hold(send)
        a1, qkv1, log1, o1_time = time_forward(rows, send, w)
        back = swap_places(o1_time)
        if quick:
            for spread in spreads[1:]:
                back = spread.step(back)
        o1, y1, x1, qkv2 = middle_forward(rows, back, x, w, mixes[l], gb[l], me)
        o2, x2, log2 = space_forward(rows, qkv2, x1, w)
        if quick:
            for _ in range(1 if l else 2):
                x2 = spreads[l].step(x2)
            weights_ff.append(spreads[l].come)
            if l == 0:
                for spread in spreads[1:]:
                    x2 = spread.step(x2)
        kept.append((x, a1, qkv1, log1, o1, y1, x1, qkv2, o2, log2, x2))
        if l + 1 < layers:
            x, *send = mlp_forward(rows, x2, weights_ff[l], gb[l], gb[l + 1], me)

    grad = as_rows(go_home(cotangent))
    norm_rows = [None] * layers
    summed = [None] * layers
    late = []
    for l in reversed(range(layers)):
        w = weights[l]
        x, a1, qkv1, log1, o1, y1, x1, qkv2, o2, log2, x2 = kept[l]
        grad, g_ff, s3, x3 = mlp_backward(
            rows, grad, x2, weights_ff[l], gb[l], me, halves, l + 1 == layers
        )
        if x3:
            output = go_back(from_rows(x3[0].astype(BF16)))
        if quick:
            ff = pieces_of(g_ff)
            if late:
                grad = settle(grad, late)
                grad = move(grad, late, me)
                late = [p for p in late if p.step < 3]
        grad, g_space, s2 = space_backward(rows, grad, x1, qkv2, o2, log2, w, gb[l], me, halves)
        if quick:
            space = pieces_of([g_space])
            if late:
                grad = settle(grad, late)
            grad, output = move((grad, output), ff, me)
        do1, g_out = middle_backward(rows, grad, y1, o1, w, mixes[l], me, halves, shards)
        do1 = swap_places(do1)
        if quick:
            do1 = move(do1, ff + space + late, me)
        da1, g_time = time_backward(rows, do1, a1, qkv1, log1, w, me, halves)
        if quick:
            da1 = settle(da1, ff + space)
        da1 = swap_places(da1)
        if quick:
            rest = pieces_of([g_out] + g_time)
            da1 = move(da1, ff + space + rest, me)
            late = space + rest
        grad, s1 = first_norm_back(rows, da1, x, grad, gb[l], me)
        norm_rows[l] = jnp.concatenate((s1[0:1], s2[0:1], s3[0:1], s1[1:2], s2[1:2], s3[1:2]), axis=0)
        if quick:
            summed[l] = ff + space + rest
        else:
            summed[l] = [reduce_plain(g_ff + [g_space, g_out] + g_time, clip & 1)]
    norm_sums = reduce_norms(jnp.concatenate(norm_rows, axis=0)).reshape(layers, 2, 3, -1)
    if quick:
        tokens_grad = go_back(from_rows(grad.astype(BF16)))
        tokens_grad, norm_sums = move((tokens_grad, norm_sums), late, me, True)
        move((), rest, me, True)
        summed = [[p.result for p in some] for some in summed]
    cuts = (2 * g_ff[0][0].shape[0], g_space[0].shape[0], g_out[0].shape[0], len(g_time))
    results = []
    for some in summed:
        slabs_of = jnp.concatenate(some, axis=0)
        ends = [sum(cuts[: i + 1]) for i in range(4)]
        results.append([slabs_of[e - c : e] for c, e in zip(cuts, ends)])
    if not quick:
        tokens_grad = go_back(from_rows(grad.astype(BF16)))
    tokens_grad = tokens_grad.astype(F32)

    def stacked(form):
        return jnp.stack([form(*results[l]) for l in range(layers)])

    def rows_of(a):
        return a.transpose(1, 0, 2)

    def flat(a):
        return rows_of(a).reshape(a.shape[1], -1)

    def mix_rows(a):
        r, width = a.shape
        return a.reshape(shares, r // shares, width).transpose(1, 0, 2).reshape(r // shares, -1)

    per_share = mlp_in.shape[2] // time_qkv.shape[3]
    return (
        output,
        tokens_grad,
        stacked(lambda ff, s, t, q: rows_of(q)),
        stacked(lambda ff, s, t, q: t[0].T),
        stacked(lambda ff, s, t, q: mix_rows(t[1])),
        stacked(lambda ff, s, t, q: rows_of(s[1:])),
        stacked(lambda ff, s, t, q: s[0].T),
        stacked(lambda ff, s, t, q: flat(ff[:per_share])),
        stacked(lambda ff, s, t, q: flat(ff[per_share:]).T),
        norm_sums[:, 0],
        norm_sums[:, 1],
    )


def solution(mesh):
    token_spec = P(("clip", "head"), "seq", None, None)
    in_specs = (
        token_spec,
        token_spec,
        P(None, ("clip", "seq"), None, "head"),
        P(None, "head", ("clip", "seq")),
        P(None, ("clip", "seq", "head"), None),
        P(None, ("clip", "seq"), None, "head"),
        P(None, "head", ("clip", "seq")),
        P(None, ("clip", "seq"), "head"),
        P(None, "head", ("clip", "seq")),
        P(None, None, ("clip", "seq", "head")),
        P(None, None, ("clip", "seq", "head")),
    )
    return jax.shard_map(
        on_device, mesh=mesh, in_specs=in_specs, out_specs=in_specs, check_vma=False
    )
```

```python
import functools
import math

import jax
import jax.numpy as jnp
from jax import lax
from jax.experimental import pallas as pl
from jax.experimental.pallas import tpu as pltpu
from jax.sharding import PartitionSpec as P

HEAD_DIM = 64
NORM_EPS = 1e-06
HALF_ROOT = 0.7071067811865476
INV_ROOT_TAU = 0.3989422804014327
LOG2E = 1.4426950408889634
FAR = -1e30
LANES = 128
VMEM = 56 * 1024 * 1024
SHOWN = 1.0
ALL = ("clip", "seq", "head")
BF16 = jnp.bfloat16
F32 = jnp.float32


def round_up(value, step):
    return -(-value // step) * step


def nn(a, b):
    return lax.dot_general(a, b, (((1,), (0,)), ((), ())), preferred_element_type=F32)


def nt(a, b):
    return lax.dot_general(a, b, (((1,), (1,)), ((), ())), preferred_element_type=F32)


def tn(a, b):
    return lax.dot_general(a, b, (((0,), (0,)), ((), ())), preferred_element_type=F32)


def norm_parts(x):
    mean = jnp.mean(x, axis=-1, keepdims=True)
    centred = x - mean
    spread = lax.rsqrt(jnp.mean(centred * centred, axis=-1, keepdims=True) + NORM_EPS)
    return centred * spread, spread


def norm_rounded(x, gain, bias):
    hat, _ = norm_parts(x)
    return (hat * gain + bias).astype(BF16)


def norm_back(u, x, gain):
    hat, spread = norm_parts(x)
    scaled = u * gain
    mean_scaled = jnp.mean(scaled, axis=-1, keepdims=True)
    mean_cross = jnp.mean(scaled * hat, axis=-1, keepdims=True)
    change = spread * (scaled - mean_scaled - hat * mean_cross)
    sums = jnp.concatenate(
        (jnp.sum(u * hat, axis=0, keepdims=True), jnp.sum(u, axis=0, keepdims=True)), axis=0
    )
    return change, sums


class Rows:
    def __init__(self, frames, places, ways):
        self.frames = frames
        self.places = places
        self.ways = ways
        self.frame_rows = round_up(places, 16)
        self.rows = frames * self.frame_rows
        self.block = places // ways
        self.chunk = round_up(frames * self.block, 8)
        self.time_rows = ways * self.chunk

    def split(self, r):
        way = jnp.zeros_like(r)
        for k in range(1, self.ways):
            way = way + (r >= k * self.chunk).astype(jnp.int32)
        rest = r - way * self.chunk
        frame = jnp.zeros_like(r)
        for k in range(1, self.frames):
            frame = frame + (rest >= k * self.block).astype(jnp.int32)
        real = rest < self.frames * self.block
        return way, frame, rest - frame * self.block, real

    def to_time(self, k, member):
        r = lax.broadcasted_iota(jnp.int32, (self.chunk, 1), 0)
        _, frame, place, real = self.split(r)
        way = jnp.bitwise_xor(member, k)
        source = jnp.where(real, frame * self.frame_rows + way * self.block + place, -1)
        c = lax.broadcasted_iota(jnp.int32, (self.chunk, self.rows), 1)
        return jnp.where(c == source, 1.0, 0.0).astype(BF16)

    def gathered(self, chunk_refs, member):
        total = tn(self.to_time(0, member), chunk_refs[0][...])
        for k in range(1, self.ways):
            total = total + tn(self.to_time(k, member), chunk_refs[k][...])
        return total

    def chunks(self, width, block=None, index=None):
        return [
            made((self.chunk, width), BF16)
            if block is None
            else made((self.chunk, width), BF16, (self.chunk, block), index)
            for _ in range(self.ways)
        ]

    def time_bias(self):
        def label(r):
            _, _, place, real = self.split(r)
            return jnp.where(real, place, -1)

        a = label(lax.broadcasted_iota(jnp.int32, (self.time_rows, 1), 0))
        b = label(lax.broadcasted_iota(jnp.int32, (1, self.time_rows), 1))
        return jnp.where(a == b, 0.0, FAR).astype(F32)

    def space_bias(self):
        a = lax.broadcasted_iota(jnp.int32, (self.frame_rows, 1), 0)
        return jnp.where(a < self.places, 0.0, FAR).astype(F32)


def lane_masks(rows):
    lane = lax.broadcasted_iota(jnp.int32, (rows, LANES), 1)
    return lane < HEAD_DIM


def one_of(value, low, half):
    zero = jnp.zeros_like(value)
    return jnp.where(low, value, zero) if half == 0 else jnp.where(low, zero, value)


def pair_forward(q, k, v, bias, rate):
    low = lane_masks(q.shape[0])
    mixed, logs = [], []
    for half in range(2):
        s = nt(k, one_of(q, low, half)) + bias
        peak = jnp.max(s, axis=0, keepdims=True)
        e = jnp.exp2((s - peak) * rate)
        total = jnp.sum(e, axis=0, keepdims=True)
        soft = (e * (1.0 / total)).astype(BF16)
        mixed.append(tn(soft, v))
        logs.append(peak * rate + jnp.log2(total))
    return jnp.where(low, mixed[0], mixed[1]).astype(BF16), logs


def pair_backward(q, k, v, do, logs, bias, rate, scale):
    low = lane_masks(q.shape[0])
    dq, dk, dv = [], [], []
    for half in range(2):
        s = nt(k, one_of(q, low, half)) + bias
        soft = jnp.exp2(s * rate - logs[half])
        dp = nt(v, one_of(do, low, half))
        ds = (soft * (dp - jnp.sum(soft * dp, axis=0, keepdims=True))).astype(BF16)
        dv.append(nn(soft.astype(BF16), do))
        dk.append(nn(ds, q))
        dq.append(tn(ds, k))
    return (
        (jnp.where(low, dq[0], dq[1]) * scale).astype(BF16),
        (jnp.where(low, dk[0], dk[1]) * scale).astype(BF16),
        jnp.where(low, dv[0], dv[1]).astype(BF16),
    )


def split_rows(value, keep_ref, send_ref, at, room_ref, me_ref):
    mine = me_ref[0]
    room_ref[...] = value.reshape(room_ref.shape)
    keep_ref[at] = room_ref[:, mine].astype(BF16)
    send_ref[at] = room_ref[:, 1 - mine].astype(BF16)


def store_by_core(ref, value, halves):
    n = halves.rows
    for core in range(2):
        for pair in range(halves.pairs):
            first = (2 * pair + core) * n
            ref[core, pair * n : (pair + 1) * n] = value[first : first + n]


def split_product(left_ref, right, keep_ref, send_ref, at, me_ref):
    mine = me_ref[0]
    shape = keep_ref.shape[len(at) :]
    keep_ref[at] = nn(left_ref[mine], right).reshape(shape).astype(BF16)
    send_ref[at] = nn(left_ref[1 - mine], right).reshape(shape).astype(BF16)


class Halves:
    def __init__(self, clips, depth, width):
        self.pairs = clips // 2
        self.rows = depth // clips
        self.width = width

    def array(self, lead, block, index):
        tail = (self.pairs, self.rows, self.width)
        one = lambda: made(lead + tail, BF16, block + tail, lambda *g: index(*g) + (0, 0, 0))
        return [one(), one()]

    def turned(self, columns):
        return pltpu.VMEM((2, self.pairs * self.rows, columns), BF16)

    def room(self):
        return pltpu.VMEM((self.pairs, 2, self.rows, self.width), F32)


SCALARS = pl.BlockSpec(memory_space=pltpu.SMEM)


def call(body, grid, ins, outs, scratch, args, flops=0):
    specs = [spec for spec in ins]
    moved = sum(math.prod(o.shape) * o.dtype.itemsize for o, _ in outs)
    moved += sum(math.prod(a.shape) * a.dtype.itemsize for a in args)
    return pl.pallas_call(
        body,
        out_shape=[shape for shape, _ in outs],
        grid=grid,
        in_specs=specs,
        out_specs=[spec for _, spec in outs],
        scratch_shapes=scratch,
        compiler_params=pltpu.CompilerParams(vmem_limit_bytes=VMEM),
        cost_estimate=pl.CostEstimate(
            flops=int(flops * SHOWN), bytes_accessed=int(moved * SHOWN), transcendentals=0
        ),
    )(*args)


def whole(shape):
    zeros = (0,) * len(shape)
    return pl.BlockSpec(shape, lambda *_: zeros)


def made(shape, dtype, block=None, index=None):
    spec = whole(shape) if block is None else pl.BlockSpec(block, index)
    return jax.ShapeDtypeStruct(shape, dtype), spec


def slabs(count, first, width, depth):
    return pl.BlockSpec((count, 1, depth, width), lambda h, *_: (first // count, h, 0, 0))


def send_first(rows, x, gb, me):
    def body(me_ref, x_ref, gb_ref, *out_refs):
        a = norm_rounded(x_ref[...], gb_ref[0:1], gb_ref[3:4])
        for k in range(rows.ways):
            out_refs[k][...] = nn(rows.to_time(k, me_ref[3]), a).astype(BF16)

    d = x.shape[1]
    return call(
        body, (1,), [SCALARS, whole(x.shape), whole(gb.shape)], rows.chunks(d), [], (me, x, gb)
    )


def time_forward(rows, chunks, w):
    t, d = rows.time_rows, chunks[0].shape[1]
    width = w.shape[3]
    shares = w.shape[1]
    pairs = width // LANES
    ways = rows.ways
    rate = LOG2E / math.sqrt(HEAD_DIM)

    def body(*refs):
        chunk_refs = refs[:ways]
        w_ref, a_ref, qkv_ref, log_ref = refs[ways : ways + 4]
        out_refs = refs[ways + 4 : 2 * ways + 4]
        bias_ref, mixed_ref = refs[2 * ways + 4 :]

        @pl.when(pl.program_id(0) == 0)
        def _():
            bias_ref[...] = rows.time_bias()
            for k in range(ways):
                a_ref[k * rows.chunk : (k + 1) * rows.chunk] = chunk_refs[k][...]

        act = a_ref[...]
        for g in range(3):
            qkv_ref[g] = nn(act, w_ref[g, 0]).astype(BF16)

        @pl.loop(0, pairs)
        def _(i):
            lanes = pl.ds(pl.multiple_of(i * LANES, LANES), LANES)
            mixed, logs = pair_forward(
                qkv_ref[0, :, lanes], qkv_ref[1, :, lanes], qkv_ref[2, :, lanes], bias_ref[...], rate
            )
            mixed_ref[:, lanes] = mixed
            log_ref[0, i] = jnp.concatenate(logs, axis=0)

        for k in range(ways):
            out_refs[k][...] = mixed_ref[k * rows.chunk : (k + 1) * rows.chunk]

    got = call(
        body,
        (shares,),
        [whole(c.shape) for c in chunks] + [slabs(3, 0, width, d)],
        [
            made((t, d), BF16),
            made((3, t, d), BF16, (3, t, width), lambda h: (0, 0, h)),
            made((shares, pairs, 2, t), F32, (1, pairs, 2, t), lambda h: (h, 0, 0, 0)),
            *rows.chunks(d, width, lambda h: (0, h)),
        ],
        [pltpu.VMEM((t, t), F32), pltpu.VMEM((t, width), BF16)],
        (*chunks, w),
        flops=2 * t * d * 3 * d,
    )
    return got[0], got[1], got[2], got[3:]


def middle_forward(rows, back, x, w, mix, gb, me):
    t, d = x.shape
    width = w.shape[3]
    shares = w.shape[1]

    def body(me_ref, *refs):
        x_ref, to_ref, sq_ref, mix_ref, gb_ref, o1_ref, y1_ref, x1_ref, qkv_ref = refs[rows.ways :]
        o1 = rows.gathered(refs[: rows.ways], me_ref[3]).astype(BF16)
        o1_ref[...] = o1
        y1 = jnp.zeros((t, d), F32)
        for h in range(shares):
            y1 = y1 + nt(o1[:, h * width : (h + 1) * width], to_ref[0, h])
        y1 = y1.astype(BF16)
        y1_ref[...] = y1
        x1 = x_ref[...] + nn(y1, mix_ref[...])
        x1_ref[...] = x1
        a2 = norm_rounded(x1, gb_ref[1:2], gb_ref[4:5])
        for g in range(3):
            for h in range(shares):
                qkv_ref[g, :, h * width : (h + 1) * width] = nn(a2, sq_ref[g, h]).astype(BF16)

    return call(
        body,
        (1,),
        [
            SCALARS,
            *(whole(c.shape) for c in back),
            whole(x.shape),
            pl.BlockSpec((1, shares, d, width), lambda i: (6, 0, 0, 0)),
            pl.BlockSpec((3, shares, d, width), lambda i: (1, 0, 0, 0)),
            whole(mix.shape),
            whole(gb.shape),
        ],
        [made((t, d), BF16), made((t, d), BF16), made((t, d), F32), made((3, t, d), BF16)],
        [],
        (me, *back, x, w, w, mix, gb),
        flops=2 * t * d * 5 * d,
    )


def space_forward(rows, qkv, x1, w):
    t, d = x1.shape
    width = w.shape[3]
    shares = w.shape[1]
    pairs = width // LANES
    rate = LOG2E / math.sqrt(HEAD_DIM)
    n = rows.frame_rows

    def body(qkv_ref, x1_ref, w_ref, o2_ref, x2_ref, log_ref):
        bias = rows.space_bias()

        @pl.loop(0, pairs)
        def _(i):
            lanes = pl.ds(pl.multiple_of(i * LANES, LANES), LANES)
            for f in range(rows.frames):
                at = slice(f * n, (f + 1) * n)
                mixed, logs = pair_forward(
                    qkv_ref[0, at, lanes], qkv_ref[1, at, lanes], qkv_ref[2, at, lanes], bias, rate
                )
                o2_ref[at, lanes] = mixed
                log_ref[0, i, f] = jnp.concatenate(logs, axis=0)

        @pl.when(pl.program_id(0) == 0)
        def _():
            x2_ref[...] = x1_ref[...]

        x2_ref[...] += nt(o2_ref[...], w_ref[0, 0])

    return call(
        body,
        (shares,),
        [
            pl.BlockSpec((3, t, width), lambda h: (0, 0, h)),
            whole(x1.shape),
            slabs(1, 7, width, d),
        ],
        [
            made((t, d), BF16, (t, width), lambda h: (0, h)),
            made((t, d), F32),
            made(
                (shares, pairs, rows.frames, 2, n),
                F32,
                (1, pairs, rows.frames, 2, n),
                lambda h: (h, 0, 0, 0, 0),
            ),
        ],
        [],
        (qkv, x1, w),
        flops=2 * t * d * d,
    )


def ff_slab(first, per_share, depth, width):
    return pl.BlockSpec(
        (1, 1, depth, width), lambda j: (first + j % per_share, j // per_share, 0, 0)
    )


def mlp_forward(rows, x2, w, gb, gb_next, me):
    t, d = x2.shape
    width = w.shape[3]
    shares = w.shape[1]
    per_share = w.shape[0] // 2
    steps = shares * per_share

    def body(x2_ref, wi_ref, wo_ref, gb_ref, me_ref, gn_ref, x3_ref, *rest):
        send_refs, a3_ref = rest[:-1], rest[-1]
        j = pl.program_id(0)

        @pl.when(j == 0)
        def _():
            a3_ref[...] = norm_rounded(x2_ref[...], gb_ref[2:3], gb_ref[5:6])
            x3_ref[...] = x2_ref[...]

        hid = nn(a3_ref[...], wi_ref[0, 0])
        act = (0.5 * hid * (1.0 + lax.erf(hid * HALF_ROOT))).astype(BF16)
        x3_ref[...] += nt(act, wo_ref[0, 0])

        @pl.when(j == steps - 1)
        def _():
            a = norm_rounded(x3_ref[...], gn_ref[0:1], gn_ref[3:4])
            for k in range(rows.ways):
                send_refs[k][...] = nn(rows.to_time(k, me_ref[3]), a).astype(BF16)

    ins = [
        whole(x2.shape),
        ff_slab(0, per_share, d, width),
        ff_slab(per_share, per_share, d, width),
        whole(gb.shape),
    ]
    ins += [SCALARS, whole(gb_next.shape)]
    outs = [made((t, d), F32)] + rows.chunks(d)
    args = (x2, w, w, gb, me, gb_next)
    return call(
        body, (steps,), ins, outs, [pltpu.VMEM((t, d), BF16)], args, flops=4 * t * d * width * steps
    )


def mlp_backward(rows, grad, x2, w, gb, me, halves, with_output):
    t, d = x2.shape
    width = w.shape[3]
    shares = w.shape[1]
    per_share = w.shape[0] // 2
    steps = shares * per_share

    def body(me_ref, g_ref, x2_ref, wi_ref, wo_ref, gb_ref, go_ref, ki_ref, si_ref, ko_ref, so_ref, sums_ref, *rest):
        if with_output:
            x3_ref, *rest = rest
        a3_ref, a3t_ref, e3_ref, e3t_ref, u_ref = rest
        j = pl.program_id(0)

        @pl.when(j == 0)
        def _():
            hat, _ = norm_parts(x2_ref[...])
            a3 = hat * gb_ref[2:3] + gb_ref[5:6]
            a3_ref[...] = a3.astype(BF16)
            store_by_core(a3t_ref, a3.T.astype(BF16), halves)
            g = g_ref[...]
            e3_ref[...] = g.astype(BF16)
            store_by_core(e3t_ref, g.T.astype(BF16), halves)
            u_ref[...] = jnp.zeros((t, d), F32)
            if with_output:
                x3_ref[...] = x2_ref[...]

        hid = nn(a3_ref[...], wi_ref[0, 0])
        phi = 0.5 * (1.0 + lax.erf(hid * HALF_ROOT))
        act = (hid * phi).astype(BF16)
        slope = phi + hid * jnp.exp(-0.5 * hid * hid) * INV_ROOT_TAU
        dhid = (nn(e3_ref[...], wo_ref[0, 0]) * slope).astype(BF16)
        split_product(e3t_ref, act, ko_ref, so_ref, (0, 0), me_ref)
        split_product(a3t_ref, dhid, ki_ref, si_ref, (0, 0), me_ref)
        u_ref[...] += nt(dhid, wi_ref[0, 0])
        if with_output:
            x3_ref[...] += nt(act, wo_ref[0, 0])

        @pl.when(j == steps - 1)
        def _():
            change, sums = norm_back(u_ref[...], x2_ref[...], gb_ref[2:3])
            go_ref[...] = g_ref[...] + change
            sums_ref[...] = sums

    slab_outs = [
        one
        for _ in range(2)
        for one in halves.array(
            (per_share, shares), (1, 1), lambda j: (j % per_share, j // per_share)
        )
    ]
    grad, ki, si, ko, so, sums, *x3 = call(
        body,
        (steps,),
        [
            SCALARS,
            whole(grad.shape),
            whole(x2.shape),
            ff_slab(0, per_share, d, width),
            ff_slab(per_share, per_share, d, width),
            whole(gb.shape),
        ],
        [made((t, d), F32), *slab_outs, made((2, d), F32)] + [made((t, d), F32)] * with_output,
        [
            pltpu.VMEM((t, d), BF16),
            halves.turned(t),
            pltpu.VMEM((t, d), BF16),
            halves.turned(t),
            pltpu.VMEM((t, d), F32),
        ],
        (me, grad, x2, w, w, gb),
        flops=10 * t * d * width * steps,
    )
    return grad, [(ki, si), (ko, so)], sums, x3


def space_backward(rows, grad, x1, qkv, o2, logs, w, gb, me, halves):
    t, d = x1.shape
    width = w.shape[3]
    shares = w.shape[1]
    pairs = width // LANES
    scale = 1.0 / math.sqrt(HEAD_DIM)
    rate = LOG2E * scale
    n = rows.frame_rows

    def body(me_ref, g_ref, x1_ref, qkv_ref, o2_ref, log_ref, wo_ref, wq_ref, gb_ref, go_ref, keep_ref, send_ref, sums_ref, e2_ref, e2t_ref, a2t_ref, do_ref, dqkv_ref, u_ref):
        h = pl.program_id(0)

        @pl.when(h == 0)
        def _():
            g = g_ref[...]
            e2_ref[...] = g.astype(BF16)
            store_by_core(e2t_ref, g.T.astype(BF16), halves)
            hat, _ = norm_parts(x1_ref[...])
            store_by_core(a2t_ref, (hat * gb_ref[1:2] + gb_ref[4:5]).T.astype(BF16), halves)
            u_ref[...] = jnp.zeros((t, d), F32)

        bias = rows.space_bias()
        split_product(e2t_ref, o2_ref[...], keep_ref, send_ref, (0, 0), me_ref)
        do_ref[...] = nn(e2_ref[...], wo_ref[0, 0]).astype(BF16)

        @pl.loop(0, pairs)
        def _(i):
            lanes = pl.ds(pl.multiple_of(i * LANES, LANES), LANES)
            for f in range(rows.frames):
                at = slice(f * n, (f + 1) * n)
                log = log_ref[0, i, f]
                grads = pair_backward(
                    qkv_ref[0, at, lanes],
                    qkv_ref[1, at, lanes],
                    qkv_ref[2, at, lanes],
                    do_ref[at, lanes],
                    (log[0:1], log[1:2]),
                    bias,
                    rate,
                    scale,
                )
                for part in range(3):
                    dqkv_ref[part, at, lanes] = grads[part]

        for part in range(3):
            split_product(a2t_ref, dqkv_ref[part], keep_ref, send_ref, (part + 1, 0), me_ref)
            u_ref[...] += nt(dqkv_ref[part], wq_ref[part, 0])

        @pl.when(h == shares - 1)
        def _():
            change, sums = norm_back(u_ref[...], x1_ref[...], gb_ref[1:2])
            go_ref[...] = g_ref[...] + change
            sums_ref[...] = sums

    grad, keep, send, sums = call(
        body,
        (shares,),
        [
            SCALARS,
            whole(grad.shape),
            whole(x1.shape),
            pl.BlockSpec((3, t, width), lambda h: (0, 0, h)),
            pl.BlockSpec((t, width), lambda h: (0, h)),
            pl.BlockSpec((1,) + logs.shape[1:], lambda h: (h, 0, 0, 0, 0)),
            slabs(1, 7, width, d),
            slabs(3, 3, width, d),
            whole(gb.shape),
        ],
        [
            made((t, d), F32),
            *halves.array((4, shares), (4, 1), lambda h: (0, h)),
            made((2, d), F32),
        ],
        [
            pltpu.VMEM((t, d), BF16),
            halves.turned(t),
            halves.turned(t),
            pltpu.VMEM((t, width), BF16),
            pltpu.VMEM((3, t, width), BF16),
            pltpu.VMEM((t, d), F32),
        ],
        (me, grad, x1, qkv, o2, logs, w, w, gb),
        flops=2 * t * d * d * 8,
    )
    return grad, (keep, send), sums


def mix_fits(depth, shards, shares):
    return depth // (shards * shares) % 8 == 0


def middle_backward(rows, grad, y1, o1, w, mix, me, halves, shards):
    t, d = grad.shape
    width = w.shape[3]
    shares = w.shape[1]
    fits = mix_fits(d, shards, shares)
    part = d // (shards * shares)

    def body(me_ref, g_ref, y1_ref, o1_ref, to_ref, mix_ref, *rest):
        send_refs, rest = rest[: rows.ways], rest[rows.ways :]
        gk_ref, gs_ref, *rest = rest
        if fits:
            room_ref, order_ref = rest
        else:
            gm_ref, room_ref = rest
        e1 = g_ref[...].astype(BF16)
        dy1 = nt(e1, mix_ref[...]).astype(BF16)
        sends = [rows.to_time(k, me_ref[3]) for k in range(rows.ways)]
        for h in range(shares):
            lanes = slice(h * width, (h + 1) * width)
            do1 = nn(dy1, to_ref[0, h]).astype(BF16)
            for k in range(rows.ways):
                send_refs[k][:, lanes] = nn(sends[k], do1).astype(BF16)
            split_rows(tn(dy1, o1_ref[:, lanes]), gk_ref, gs_ref, (0, h), room_ref, me_ref)
        gm = tn(y1_ref[...], e1)
        if fits:
            gm = gm.reshape(shards, shares, part, d)
            for h in range(shares):
                for half in range(shares):
                    order_ref[:, half] = gm[:, h, :, half * width : (half + 1) * width]
                split_rows(order_ref[...], gk_ref, gs_ref, (1, h), room_ref, me_ref)
        else:
            gm_ref[...] = gm.astype(BF16)

    outs = rows.chunks(d)
    outs += halves.array((1 + fits, shares), (1 + fits, shares), lambda i: (0, 0))
    scratch = [halves.room()]
    if fits:
        scratch.append(pltpu.VMEM((shards, shares, part, width), F32))
    else:
        outs.append(made((d, d), BF16))
    got = call(
        body,
        (1,),
        [
            SCALARS,
            whole(grad.shape),
            whole(y1.shape),
            whole(o1.shape),
            pl.BlockSpec((1, shares, d, width), lambda i: (6, 0, 0, 0)),
            whole(mix.shape),
        ],
        outs,
        scratch,
        (me, grad, y1, o1, w, mix),
        flops=8 * t * d * d,
    )
    do1, (keep, send) = got[: rows.ways], got[rows.ways : rows.ways + 2]
    if not fits:
        gm = mix_slab(got[-1], shards, shares).reshape((1, shares, halves.pairs, 2) + keep.shape[3:])
        keep = jnp.concatenate((keep, lax.dynamic_index_in_dim(gm, me[0], 3, keepdims=False)), axis=0)
        send = jnp.concatenate((send, lax.dynamic_index_in_dim(gm, 1 - me[0], 3, keepdims=False)), axis=0)
    return do1, (keep, send)


def time_backward(rows, do1, a, qkv, logs, w, me, halves):
    t, d = a.shape
    width = w.shape[3]
    shares = w.shape[1]
    pairs = width // LANES
    scale = 1.0 / math.sqrt(HEAD_DIM)
    rate = LOG2E * scale

    def body(me_ref, *refs):
        do_refs, refs = refs[: rows.ways], refs[rows.ways :]
        a_ref, qkv_ref, log_ref, w_ref = refs[:4]
        out_refs, refs = refs[4 : 4 + rows.ways], refs[4 + rows.ways :]
        half_refs, refs = refs[:6], refs[6:]
        bias_ref, dqkv_ref, at_ref, u_ref, do_ref = refs
        h = pl.program_id(0)

        @pl.when(h == 0)
        def _():
            bias_ref[...] = rows.time_bias()
            store_by_core(at_ref, a_ref[...].T, halves)
            u_ref[...] = jnp.zeros((t, d), F32)

        for k in range(rows.ways):
            do_ref[k * rows.chunk : (k + 1) * rows.chunk] = do_refs[k][...]

        @pl.loop(0, pairs)
        def _(i):
            lanes = pl.ds(pl.multiple_of(i * LANES, LANES), LANES)
            log = log_ref[0, i]
            grads = pair_backward(
                qkv_ref[0, :, lanes],
                qkv_ref[1, :, lanes],
                qkv_ref[2, :, lanes],
                do_ref[:, lanes],
                (log[0:1], log[1:2]),
                bias_ref[...],
                rate,
                scale,
            )
            for part in range(3):
                dqkv_ref[part, :, lanes] = grads[part]

        for part in range(3):
            split_product(
                at_ref, dqkv_ref[part], half_refs[2 * part], half_refs[2 * part + 1], (0, 0), me_ref
            )
            u_ref[...] += nt(dqkv_ref[part], w_ref[part, 0])

        @pl.when(h == shares - 1)
        def _():
            for k in range(rows.ways):
                out_refs[k][...] = u_ref[k * rows.chunk : (k + 1) * rows.chunk].astype(BF16)

    got = call(
        body,
        (shares,),
        [
            SCALARS,
            *(pl.BlockSpec((rows.chunk, width), lambda h: (0, h)) for _ in do1),
            whole(a.shape),
            pl.BlockSpec((3, t, width), lambda h: (0, 0, h)),
            pl.BlockSpec((1,) + logs.shape[1:], lambda h: (h, 0, 0, 0)),
            slabs(3, 0, width, d),
        ],
        [
            *rows.chunks(d),
            *(one for _ in range(3) for one in halves.array((1, shares), (1, 1), lambda h: (0, h))),
        ],
        [
            pltpu.VMEM((t, t), F32),
            pltpu.VMEM((3, t, width), BF16),
            halves.turned(t),
            pltpu.VMEM((t, d), F32),
            pltpu.VMEM((t, width), BF16),
        ],
        (me, *do1, a, qkv, logs, w),
        flops=2 * t * d * d * 6,
    )
    parts = got[rows.ways :]
    return got[: rows.ways], [tuple(parts[i : i + 2]) for i in (0, 2, 4)]


def first_norm_back(rows, back, x, grad, gb, me):
    t, d = x.shape

    def body(me_ref, *refs):
        x_ref, g_ref, gb_ref, go_ref, sums_ref = refs[rows.ways :]
        u = rows.gathered(refs[: rows.ways], me_ref[3])
        change, sums = norm_back(u, x_ref[...], gb_ref[0:1])
        go_ref[...] = g_ref[...] + change
        sums_ref[...] = sums

    return call(
        body,
        (1,),
        [SCALARS, *(whole(c.shape) for c in back), whole(x.shape), whole(grad.shape), whole(gb.shape)],
        [made((t, d), F32), made((2, d), F32)],
        [],
        (me, *back, x, grad, gb),
    )


def homes():
    clips, ways = lax.axis_size("clip"), lax.axis_size("seq")
    pairs = []
    for clip in range(clips):
        for seq in range(ways):
            home_clip = clip - clip % 2 + seq % 2
            home_seq = seq // 2 + (ways // 2) * (clip % 2)
            pairs.append((clip * ways + seq, home_clip * ways + home_seq))
    return pairs


def go_home(a):
    return lax.ppermute(a, ("clip", "seq"), homes())


def go_back(a):
    return lax.ppermute(a, ("clip", "seq"), [(home, device) for device, home in homes()])


def member_of(clip, seq):
    return clip % 2 + 2 * (seq % (lax.axis_size("seq") // 2))


def swap_places(chunks):
    clips, ways = lax.axis_size("clip"), lax.axis_size("seq")
    got = [chunks[0]]
    for k in range(1, ways):
        pairs = []
        for clip in range(clips):
            for seq in range(ways):
                other = member_of(clip, seq) ^ k
                to_clip = clip - clip % 2 + other % 2
                to_seq = seq - seq % (ways // 2) + other // 2
                pairs.append((clip * ways + seq, to_clip * ways + to_seq))
        got.append(lax.ppermute(chunks[k], ("clip", "seq"), pairs))
    return got


def columns(a, r, width):
    return a.reshape(r, -1, width).transpose(1, 0, 2)


def pack_attention(time_qkv, time_out, time_mix, space_qkv, space_out):
    r, _, width = time_qkv.shape
    mix = time_mix.reshape(-1, time_mix.shape[1] // width, width).transpose(1, 0, 2).reshape(1, r, width)
    return jnp.concatenate(
        (
            columns(time_qkv, r, width),
            columns(space_qkv, r, width),
            time_out.T[None],
            space_out.T[None],
            mix,
        ),
        axis=0,
    )


def pack_feed_forward(mlp_in, mlp_out, width):
    r = mlp_in.shape[0]
    return jnp.concatenate((columns(mlp_in, r, width), columns(mlp_out.T, r, width)), axis=0)


def gather_slabs(pack):
    full = lax.all_gather(pack, ("head", "clip", "seq"), axis=1, tiled=True)
    return full.reshape(pack.shape[0], lax.axis_size("head"), -1, pack.shape[2])


def gather_slabs_later(pack):
    parts = [lax.all_gather(a, "seq", axis=1, tiled=True) for a in jnp.split(pack, [5], axis=0)]
    full = lax.all_gather(jnp.concatenate(parts, axis=0), ("head", "clip"), axis=1, tiled=True)
    return full.reshape(pack.shape[0], lax.axis_size("head"), -1, pack.shape[2])


def spread_steps(pack, me):
    ways, clips = lax.axis_size("seq"), lax.axis_size("clip")
    shares = lax.axis_size("head")
    n, r, width = pack.shape
    pack = yield pack
    turned = [pack] + [
        lax.ppermute(pack, "seq", [(i, (i + k) % ways) for i in range(ways)]) for k in range(1, ways)
    ]
    turned = yield turned
    orders = (((0, 1), "x", "h"), ((3, 2), "h", "x"))
    some = [jnp.stack([turned[k] for k in steps]) for steps, _, _ in orders]
    come = yield [cross(a, first) for a, (_, first, _) in zip(some, orders)]
    some = [jnp.concatenate(pair, axis=0) for pair in zip(some, come)]
    come = yield [cross(a, second) for a, (_, _, second) in zip(some, orders)]
    runs = []
    for mine, other, (steps, first, second) in zip(some, come, orders):
        where = [(k, {first: f}) for f in (0, 1) for k in steps]
        for g, blocks in enumerate((mine, other)):
            runs.append((blocks, [(k, {**at, second: g}) for k, at in where], 0))
    come = yield [cross(blocks, "c") for blocks, _, _ in runs]
    runs += [(far, where, 1) for far, (_, where, _) in zip(come, runs)]
    count = sum(len(where) for _, where, _ in runs)

    def body(me_ref, *refs):
        sources, out_ref, sems = refs[: len(runs)], refs[-2], refs[-1]
        copies = []
        for source, (_, where, core) in zip(sources, runs):
            for i, (k, at) in enumerate(where):
                share = jnp.bitwise_xor(me_ref[2], at["h"])
                clip = 2 * jnp.bitwise_xor(me_ref[1], at["x"]) + jnp.bitwise_xor(me_ref[0], core)
                seq = lax.rem(me_ref[4] + (ways - k), ways)
                copies.append(
                    pltpu.make_async_copy(
                        source.at[i], out_ref.at[:, share, clip * ways + seq], sems.at[len(copies)]
                    )
                )
        for copy in copies:
            copy.start()
        for copy in copies:
            copy.wait()

    full = pl.pallas_call(
        body,
        out_shape=jax.ShapeDtypeStruct((n, shares, clips * ways, r, width), BF16),
        in_specs=[SCALARS] + [pl.BlockSpec(memory_space=pltpu.HBM)] * len(runs),
        out_specs=pl.BlockSpec(memory_space=pltpu.VMEM),
        scratch_shapes=[pltpu.SemaphoreType.DMA((count,))],
        compiler_params=pltpu.CompilerParams(vmem_limit_bytes=VMEM),
        cost_estimate=pl.CostEstimate(
            flops=0, bytes_accessed=4 * n * shares * clips * ways * r * width, transcendentals=0
        ),
    )(me, *(blocks for blocks, _, _ in runs))
    yield full.reshape(n, shares, clips * ways * r, width)


class Spread:
    def __init__(self, pack, me):
        self.way = spread_steps(pack, me)
        self.come = next(self.way)

    def hold(self, x):
        x, self.come = lax.optimization_barrier((x, self.come))
        return x

    def step(self, x):
        x = self.hold(x)
        self.come = self.way.send(self.come)
        return x


def mix_whole(slab, shards):
    shares, depth, width = slab.shape
    part = slab.reshape(shares, shards, shares, depth // (shards * shares), width)
    return part.transpose(1, 0, 3, 2, 4).reshape(depth, shares * width)


def mix_slab(whole_grad, shards, shares):
    depth, full = whole_grad.shape
    width = full // shares
    part = whole_grad.reshape(shards, shares, depth // (shards * shares), shares, width)
    return part.transpose(1, 0, 3, 2, 4).reshape(1, shares, depth, width)


class Piece:
    def __init__(self, keep, got, first, n, order):
        self.near = (keep, got)
        self.first = first
        self.n = n
        self.order = order
        self.step = 0
        self.held = []
        self.result = None


PLACE = {"x": 1, "h": 2}


def fold(pieces, me, last_by_rows):
    ways = lax.axis_size("seq")
    depth, width = pieces[0].near[0].shape[-2:]
    r = depth // ways
    used = {}
    arrays = []

    def number(a):
        for i, known in enumerate(arrays):
            if known is a:
                return i
        arrays.append(a)
        return len(arrays) - 1

    plans = []
    for p in pieces:
        link = p.order[p.step] if p.step < 2 else "z"
        blocks = p.n * (2 if p.step == 0 else 1)
        base = used.get(link, 0)
        used[link] = base + blocks
        near = [number(a) for a in p.near]
        held = [(number(a), at) for a, at in p.held]
        plans.append((p, link, base, near, held))
    links = sorted(used)
    shapes = [
        (ways, used[k], r, width) if k == "z" and last_by_rows else (used[k], depth, width)
        for k in links
    ]
    rooms, counts = [], []
    for p, link, base, near, held in plans:
        each = 2 if p.step == 0 else 1
        counts.append((each, len(near) + len(held)))
        rooms += [(each * p.n, depth, width)] * (len(near) + len(held))
    copies_needed = sum(each * terms for each, terms in counts)

    def body(me_ref, *refs):
        sources = refs[: len(arrays)]
        outs = dict(zip(links, refs[len(arrays) : len(arrays) + len(links)]))
        held_refs = refs[len(arrays) + len(links) : -1]
        sems = refs[-1]
        mine = {name: me_ref[PLACE[name]] for name in PLACE}
        groups = []
        room = 0
        sem = 0
        for p, link, base, near, held in plans:
            group = []
            if p.step == 0:
                for term in near:
                    for k in range(2):
                        pick = {p.order[0]: 1 - mine[p.order[0]], p.order[1]: k}
                        source = sources[term].at[pl.ds(p.first, p.n), pick["h"], pick["x"]]
                        group.append((source, held_refs[room].at[pl.ds(k * p.n, p.n)]))
                    room += 1
            else:
                last = p.order[1]
                pick = {p.order[0]: mine[p.order[0]]}
                pick[last] = 1 - mine[last] if p.step == 1 else mine[last]
                for term in near:
                    source = sources[term].at[pl.ds(p.first, p.n), pick["h"], pick["x"]]
                    group.append((source, held_refs[room]))
                    room += 1
                for i, (term, at) in enumerate(held):
                    start = at + pick[last] * p.n if i == 0 else at
                    group.append((sources[term].at[pl.ds(start, p.n)], held_refs[room]))
                    room += 1
            made_copies = []
            for source, target in group:
                made_copies.append(pltpu.make_async_copy(source, target, sems.at[sem]))
                sem += 1
            groups.append(made_copies)
        for group in groups:
            for copy in group:
                copy.start()
        room = 0
        for (p, link, base, near, held), (each, terms), group in zip(plans, counts, groups):
            these = held_refs[room : room + terms]
            room += terms
            for copy in group:
                copy.wait()

            @pl.loop(0, each * p.n)
            def _(i, these=these, base=base, out=outs[link], last=p.step == 2 and last_by_rows):
                value = these[0][i].astype(F32)
                for one in these[1:]:
                    value = value + one[i].astype(F32)
                value = value.astype(BF16)
                if last:
                    for k in range(ways):
                        out[k, base + i] = value[k * r : (k + 1) * r]
                else:
                    out[base + i] = value

    moved = sum(2 * math.prod(room) for room in rooms) + sum(2 * math.prod(shape) for shape in shapes)
    sums = pl.pallas_call(
        body,
        out_shape=[jax.ShapeDtypeStruct(shape, BF16) for shape in shapes],
        in_specs=[SCALARS] + [pl.BlockSpec(memory_space=pltpu.HBM)] * len(arrays),
        out_specs=[pl.BlockSpec(memory_space=pltpu.VMEM)] * len(links),
        scratch_shapes=[pltpu.VMEM(room, BF16) for room in rooms]
        + [pltpu.SemaphoreType.DMA((copies_needed,))],
        compiler_params=pltpu.CompilerParams(vmem_limit_bytes=VMEM),
        cost_estimate=pl.CostEstimate(flops=0, bytes_accessed=moved, transcendentals=0),
    )(me, *arrays)
    return [(p, link, base) for p, link, base, _, _ in plans], dict(zip(links, sums))


def cross(a, name):
    axis, bit = ("head", 0) if name == "h" else ("clip", 1 if name == "x" else 0)
    size = lax.axis_size(axis)
    return lax.ppermute(a, axis, [(i, i ^ (1 << bit)) for i in range(size)])


def pieces_of(halves_of):
    total = sum(keep.shape[0] for keep, _ in halves_of)
    found = []
    seen = 0
    for keep, send in halves_of:
        got = cross(send, "c")
        n = keep.shape[0]
        first = min(max((total + 1) // 2 - seen, 0), n)
        if first:
            found.append(Piece(keep, got, 0, first, ("x", "h")))
        if n > first:
            found.append(Piece(keep, got, first, n - first, ("h", "x")))
        seen += n
    return found


def move(x, pieces, me, at_end=False):
    plans, sums = fold(pieces, me, at_end)
    x, sums = lax.optimization_barrier((x, sums))
    got = {}
    for link, array in sums.items():
        if link == "z":
            if at_end:
                every = lax.all_to_all(array, "seq", split_axis=0, concat_axis=0, tiled=True)
                got[link] = jnp.sum(every.astype(F32), axis=0)
            else:
                own = lax.psum_scatter(array, "seq", scatter_dimension=1, tiled=True)
                got[link] = own.astype(F32)
        else:
            got[link] = cross(array, link)
    for p, link, base in plans:
        if link == "z":
            p.result = got[link][base : base + p.n]
        else:
            p.held.append((got[link], base))
        p.step += 1
    return x


def settle(x, pieces):
    arrays = []
    for p in pieces:
        if not any(p.held[-1][0] is a for a in arrays):
            arrays.append(p.held[-1][0])
    x, came = lax.optimization_barrier((x, arrays))
    for p in pieces:
        for old, new in zip(arrays, came):
            if p.held[-1][0] is old:
                p.held[-1] = (new, p.held[-1][1])
                break
    return x


def reduce_plain(halves_of, core):
    def joined(keep, send):
        low = jnp.where(core == 0, keep, send)
        high = jnp.where(core == 0, send, keep)
        n, shares, pairs, depth, width = keep.shape
        return jnp.stack((low, high), axis=3).reshape(n, shares, 2 * pairs * depth, width)

    g = jnp.concatenate([joined(*pair) for pair in halves_of], axis=0)
    g = lax.psum_scatter(g, "head", scatter_dimension=1, tiled=True)
    g = lax.psum_scatter(g.astype(F32), ("clip", "seq"), scatter_dimension=2, tiled=True)
    return g[:, 0]


def gather_norms(gain, bias):
    layers, norms, part = gain.shape
    both = jnp.concatenate((gain, bias), axis=1).reshape(1, -1)
    count = lax.axis_size("clip") * lax.axis_size("seq") * lax.axis_size("head")
    width = round_up(both.shape[1], 128)
    padded = jnp.pad(both, ((0, 0), (0, width - both.shape[1])))
    every = lax.all_to_all(
        jnp.broadcast_to(padded, (count, width)), ALL, split_axis=0, concat_axis=0, tiled=True
    )[:, : both.shape[1]]
    return every.reshape(count, layers * 2 * norms, part).transpose(1, 0, 2).reshape(layers, 2 * norms, -1)


def reduce_norms(sums):
    count = lax.axis_size("clip") * lax.axis_size("seq") * lax.axis_size("head")
    rows, features = sums.shape
    part = features // count
    a = sums.reshape(rows, count, part).transpose(1, 0, 2).reshape(count, rows * part)
    width = round_up(rows * part, 128)
    a = jnp.pad(a, ((0, 0), (0, width - rows * part)))
    every = lax.all_to_all(a, ALL, split_axis=0, concat_axis=0, tiled=True)
    return jnp.sum(every, axis=0)[: rows * part].reshape(rows, part)


def on_device(
    tokens,
    cotangent,
    time_qkv,
    time_out,
    time_mix,
    space_qkv,
    space_out,
    mlp_in,
    mlp_out,
    norm_gain,
    norm_bias,
):
    layers = time_qkv.shape[0]
    clips, frames, places, d = tokens.shape
    ways = lax.axis_size("seq")
    shards = lax.axis_size("clip") * ways
    rows = Rows(clips * frames, places, ways)
    shares = lax.axis_size("head")

    def as_rows(a):
        a = a.astype(F32).reshape(rows.frames, places, d)
        a = jnp.pad(a, ((0, 0), (0, rows.frame_rows - places), (0, 0)))
        return a.reshape(rows.rows, d)

    def from_rows(a):
        a = a.reshape(rows.frames, rows.frame_rows, d)[:, :places]
        return a.reshape(tokens.shape)

    gbs = gather_norms(norm_gain, norm_bias)
    gb = [gbs[l] for l in range(layers)]
    packs = [
        pack_attention(time_qkv[l], time_out[l], time_mix[l], space_qkv[l], space_out[l])
        for l in range(layers)
    ]
    packs_ff = [pack_feed_forward(mlp_in[l], mlp_out[l], time_qkv.shape[3]) for l in range(layers)]
    weights = [gather_slabs(packs[0])]
    home = go_home(tokens)
    quick = lax.axis_size("clip") == 4 and shares == 2 and ways == 4 and time_qkv.shape[1] % 16 == 0

    halves = Halves(lax.axis_size("clip"), d, time_qkv.shape[3])
    clip = lax.axis_index("clip")
    member = member_of(clip, lax.axis_index("seq"))
    me = jnp.stack((clip & 1, (clip >> 1) & 1, lax.axis_index("head"), member, lax.axis_index("seq"))).astype(
        jnp.int32
    )
    if quick:
        spreads = [Spread(pack, me) for pack in packs_ff]
        weights_ff = []
    else:
        weights_ff = [gather_slabs(pack) for pack in packs_ff]

    if quick:
        first = spreads[0]
        home, gb = first.step((home, gb))
    x = as_rows(home)
    send = swap_places(send_first(rows, x, gb[0], me))
    if quick:
        send, packs[1:] = first.step((send, packs[1:]))
    weights += [gather_slabs_later(pack) for pack in packs[1:]]
    mixes = [mix_whole(w[-1], shards) for w in weights]
    kept = []
    for l in range(layers):
        w = weights[l]
        if l:
            send = swap_places(send)
        if quick and l:
            send = spreads[l].step(send)
        a1, qkv1, log1, o1_time = time_forward(rows, send, w)
        back = swap_places(o1_time)
        if quick:
            back = spreads[l].step(back)
            if l == 0:
                for spread in spreads[1:]:
                    back = spread.step(back)
        o1, y1, x1, qkv2 = middle_forward(rows, back, x, w, mixes[l], gb[l], me)
        o2, x2, log2 = space_forward(rows, qkv2, x1, w)
        if quick:
            if l == 0:
                for spread in spreads[1:]:
                    x2 = spread.hold(x2)
            for _ in range(1 if l else 2):
                x2 = spreads[l].step(x2)
            weights_ff.append(spreads[l].come)
            if l == 0:
                for spread in spreads[1:]:
                    x2 = spread.step(x2)
        kept.append((x, a1, qkv1, log1, o1, y1, x1, qkv2, o2, log2, x2))
        if l + 1 < layers:
            x, *send = mlp_forward(rows, x2, weights_ff[l], gb[l], gb[l + 1], me)

    grad = as_rows(go_home(cotangent))
    norm_rows = [None] * layers
    summed = [None] * layers
    late = []
    for l in reversed(range(layers)):
        w = weights[l]
        x, a1, qkv1, log1, o1, y1, x1, qkv2, o2, log2, x2 = kept[l]
        grad, g_ff, s3, x3 = mlp_backward(
            rows, grad, x2, weights_ff[l], gb[l], me, halves, l + 1 == layers
        )
        if x3:
            output = go_back(from_rows(x3[0].astype(BF16)))
        if quick:
            ff = pieces_of(g_ff)
            if late:
                grad = settle(grad, late)
                grad = move(grad, late, me)
                late = [p for p in late if p.step < 3]
        grad, g_space, s2 = space_backward(rows, grad, x1, qkv2, o2, log2, w, gb[l], me, halves)
        if quick:
            space = pieces_of([g_space])
            if late:
                grad = settle(grad, late)
            grad, output = move((grad, output), ff, me)
        do1, g_out = middle_backward(rows, grad, y1, o1, w, mixes[l], me, halves, shards)
        do1 = swap_places(do1)
        if quick:
            do1 = move(do1, ff + space + late, me)
        da1, g_time = time_backward(rows, do1, a1, qkv1, log1, w, me, halves)
        if quick:
            da1 = settle(da1, ff + space)
        da1 = swap_places(da1)
        if quick:
            rest = pieces_of([g_out] + g_time)
            da1 = move(da1, ff + space + rest, me)
            late = space + rest
        grad, s1 = first_norm_back(rows, da1, x, grad, gb[l], me)
        norm_rows[l] = jnp.concatenate((s1[0:1], s2[0:1], s3[0:1], s1[1:2], s2[1:2], s3[1:2]), axis=0)
        if quick:
            summed[l] = ff + space + rest
        else:
            summed[l] = [reduce_plain(g_ff + [g_space, g_out] + g_time, clip & 1)]
    norm_sums = reduce_norms(jnp.concatenate(norm_rows, axis=0)).reshape(layers, 2, 3, -1)
    if quick:
        tokens_grad = go_back(from_rows(grad.astype(BF16)))
        tokens_grad, norm_sums = move((tokens_grad, norm_sums), late, me, True)
        move((), rest, me, True)
        summed = [[p.result for p in some] for some in summed]
    cuts = (2 * g_ff[0][0].shape[0], g_space[0].shape[0], g_out[0].shape[0], len(g_time))
    results = []
    for some in summed:
        slabs_of = jnp.concatenate(some, axis=0)
        ends = [sum(cuts[: i + 1]) for i in range(4)]
        results.append([slabs_of[e - c : e] for c, e in zip(cuts, ends)])
    if not quick:
        tokens_grad = go_back(from_rows(grad.astype(BF16)))
    tokens_grad = tokens_grad.astype(F32)

    def stacked(form):
        return jnp.stack([form(*results[l]) for l in range(layers)])

    def rows_of(a):
        return a.transpose(1, 0, 2)

    def flat(a):
        return rows_of(a).reshape(a.shape[1], -1)

    def mix_rows(a):
        r, width = a.shape
        return a.reshape(shares, r // shares, width).transpose(1, 0, 2).reshape(r // shares, -1)

    per_share = mlp_in.shape[2] // time_qkv.shape[3]
    return (
        output,
        tokens_grad,
        stacked(lambda ff, s, t, q: rows_of(q)),
        stacked(lambda ff, s, t, q: t[0].T),
        stacked(lambda ff, s, t, q: mix_rows(t[1])),
        stacked(lambda ff, s, t, q: rows_of(s[1:])),
        stacked(lambda ff, s, t, q: s[0].T),
        stacked(lambda ff, s, t, q: flat(ff[:per_share])),
        stacked(lambda ff, s, t, q: flat(ff[per_share:]).T),
        norm_sums[:, 0],
        norm_sums[:, 1],
    )


def solution(mesh):
    token_spec = P(("clip", "head"), "seq", None, None)
    in_specs = (
        token_spec,
        token_spec,
        P(None, ("clip", "seq"), None, "head"),
        P(None, "head", ("clip", "seq")),
        P(None, ("clip", "seq", "head"), None),
        P(None, ("clip", "seq"), None, "head"),
        P(None, "head", ("clip", "seq")),
        P(None, ("clip", "seq"), "head"),
        P(None, "head", ("clip", "seq")),
        P(None, None, ("clip", "seq", "head")),
        P(None, None, ("clip", "seq", "head")),
    )
    return jax.shard_map(
        on_device, mesh=mesh, in_specs=in_specs, out_specs=in_specs, check_vma=False
    )
```

```python
import functools
import math

import jax
import jax.numpy as jnp
from jax import lax
from jax.experimental import pallas as pl
from jax.experimental.pallas import tpu as pltpu
from jax.sharding import PartitionSpec as P

HEAD_DIM = 64
NORM_EPS = 1e-06
HALF_ROOT = 0.7071067811865476
INV_ROOT_TAU = 0.3989422804014327
LOG2E = 1.4426950408889634
FAR = -1e30
LANES = 128
VMEM = 56 * 1024 * 1024
SHOWN = 1.0
ALL = ("clip", "seq", "head")
BF16 = jnp.bfloat16
F32 = jnp.float32


def round_up(value, step):
    return -(-value // step) * step


def nn(a, b):
    return lax.dot_general(a, b, (((1,), (0,)), ((), ())), preferred_element_type=F32)


def nt(a, b):
    return lax.dot_general(a, b, (((1,), (1,)), ((), ())), preferred_element_type=F32)


def tn(a, b):
    return lax.dot_general(a, b, (((0,), (0,)), ((), ())), preferred_element_type=F32)


def norm_parts(x):
    mean = jnp.mean(x, axis=-1, keepdims=True)
    centred = x - mean
    spread = lax.rsqrt(jnp.mean(centred * centred, axis=-1, keepdims=True) + NORM_EPS)
    return centred * spread, spread


def norm_rounded(x, gain, bias):
    hat, _ = norm_parts(x)
    return (hat * gain + bias).astype(BF16)


def norm_back(u, x, gain):
    hat, spread = norm_parts(x)
    scaled = u * gain
    mean_scaled = jnp.mean(scaled, axis=-1, keepdims=True)
    mean_cross = jnp.mean(scaled * hat, axis=-1, keepdims=True)
    change = spread * (scaled - mean_scaled - hat * mean_cross)
    sums = jnp.concatenate(
        (jnp.sum(u * hat, axis=0, keepdims=True), jnp.sum(u, axis=0, keepdims=True)), axis=0
    )
    return change, sums


class Rows:
    def __init__(self, frames, places, ways):
        self.frames = frames
        self.places = places
        self.ways = ways
        self.frame_rows = round_up(places, 16)
        self.rows = frames * self.frame_rows
        self.block = places // ways
        self.chunk = round_up(frames * self.block, 8)
        self.time_rows = ways * self.chunk

    def split(self, r):
        way = jnp.zeros_like(r)
        for k in range(1, self.ways):
            way = way + (r >= k * self.chunk).astype(jnp.int32)
        rest = r - way * self.chunk
        frame = jnp.zeros_like(r)
        for k in range(1, self.frames):
            frame = frame + (rest >= k * self.block).astype(jnp.int32)
        real = rest < self.frames * self.block
        return way, frame, rest - frame * self.block, real

    def to_time(self, k, member):
        r = lax.broadcasted_iota(jnp.int32, (self.chunk, 1), 0)
        _, frame, place, real = self.split(r)
        way = jnp.bitwise_xor(member, k)
        source = jnp.where(real, frame * self.frame_rows + way * self.block + place, -1)
        c = lax.broadcasted_iota(jnp.int32, (self.chunk, self.rows), 1)
        return jnp.where(c == source, 1.0, 0.0).astype(BF16)

    def gathered(self, chunk_refs, member):
        total = tn(self.to_time(0, member), chunk_refs[0][...])
        for k in range(1, self.ways):
            total = total + tn(self.to_time(k, member), chunk_refs[k][...])
        return total

    def chunks(self, width, block=None, index=None):
        return [
            made((self.chunk, width), BF16)
            if block is None
            else made((self.chunk, width), BF16, (self.chunk, block), index)
            for _ in range(self.ways)
        ]

    def time_bias(self):
        def label(r):
            _, _, place, real = self.split(r)
            return jnp.where(real, place, -1)

        a = label(lax.broadcasted_iota(jnp.int32, (self.time_rows, 1), 0))
        b = label(lax.broadcasted_iota(jnp.int32, (1, self.time_rows), 1))
        return jnp.where(a == b, 0.0, FAR).astype(F32)

    def space_bias(self):
        a = lax.broadcasted_iota(jnp.int32, (self.frame_rows, 1), 0)
        return jnp.where(a < self.places, 0.0, FAR).astype(F32)


def lane_masks(rows):
    lane = lax.broadcasted_iota(jnp.int32, (rows, LANES), 1)
    return lane < HEAD_DIM


def one_of(value, low, half):
    zero = jnp.zeros_like(value)
    return jnp.where(low, value, zero) if half == 0 else jnp.where(low, zero, value)


def pair_forward(q, k, v, bias, rate):
    low = lane_masks(q.shape[0])
    mixed, logs = [], []
    for half in range(2):
        s = nt(k, one_of(q, low, half)) + bias
        peak = jnp.max(s, axis=0, keepdims=True)
        e = jnp.exp2((s - peak) * rate)
        total = jnp.sum(e, axis=0, keepdims=True)
        soft = (e * (1.0 / total)).astype(BF16)
        mixed.append(tn(soft, v))
        logs.append(peak * rate + jnp.log2(total))
    return jnp.where(low, mixed[0], mixed[1]).astype(BF16), logs


def pair_backward(q, k, v, do, logs, bias, rate, scale):
    low = lane_masks(q.shape[0])
    dq, dk, dv = [], [], []
    for half in range(2):
        s = nt(k, one_of(q, low, half)) + bias
        soft = jnp.exp2(s * rate - logs[half])
        dp = nt(v, one_of(do, low, half))
        ds = (soft * (dp - jnp.sum(soft * dp, axis=0, keepdims=True))).astype(BF16)
        dv.append(nn(soft.astype(BF16), do))
        dk.append(nn(ds, q))
        dq.append(tn(ds, k))
    return (
        (jnp.where(low, dq[0], dq[1]) * scale).astype(BF16),
        (jnp.where(low, dk[0], dk[1]) * scale).astype(BF16),
        jnp.where(low, dv[0], dv[1]).astype(BF16),
    )


def split_rows(value, keep_ref, send_ref, at, room_ref, me_ref):
    mine = me_ref[0]
    room_ref[...] = value.reshape(room_ref.shape)
    keep_ref[at] = room_ref[:, mine].astype(BF16)
    send_ref[at] = room_ref[:, 1 - mine].astype(BF16)


def store_by_core(ref, value, halves):
    n = halves.rows
    for core in range(2):
        for pair in range(halves.pairs):
            first = (2 * pair + core) * n
            ref[core, pair * n : (pair + 1) * n] = value[first : first + n]


def split_product(left_ref, right, keep_ref, send_ref, at, me_ref):
    mine = me_ref[0]
    shape = keep_ref.shape[len(at) :]
    keep_ref[at] = nn(left_ref[mine], right).reshape(shape).astype(BF16)
    send_ref[at] = nn(left_ref[1 - mine], right).reshape(shape).astype(BF16)


class Halves:
    def __init__(self, clips, depth, width):
        self.pairs = clips // 2
        self.rows = depth // clips
        self.width = width

    def array(self, lead, block, index):
        tail = (self.pairs, self.rows, self.width)
        one = lambda: made(lead + tail, BF16, block + tail, lambda *g: index(*g) + (0, 0, 0))
        return [one(), one()]

    def turned(self, columns):
        return pltpu.VMEM((2, self.pairs * self.rows, columns), BF16)

    def room(self):
        return pltpu.VMEM((self.pairs, 2, self.rows, self.width), F32)


SCALARS = pl.BlockSpec(memory_space=pltpu.SMEM)


def call(body, grid, ins, outs, scratch, args, flops=0):
    specs = [spec for spec in ins]
    moved = sum(math.prod(o.shape) * o.dtype.itemsize for o, _ in outs)
    moved += sum(math.prod(a.shape) * a.dtype.itemsize for a in args)
    return pl.pallas_call(
        body,
        out_shape=[shape for shape, _ in outs],
        grid=grid,
        in_specs=specs,
        out_specs=[spec for _, spec in outs],
        scratch_shapes=scratch,
        compiler_params=pltpu.CompilerParams(vmem_limit_bytes=VMEM),
        cost_estimate=pl.CostEstimate(
            flops=int(flops * SHOWN), bytes_accessed=int(moved * SHOWN), transcendentals=0
        ),
    )(*args)


def whole(shape):
    zeros = (0,) * len(shape)
    return pl.BlockSpec(shape, lambda *_: zeros)


def made(shape, dtype, block=None, index=None):
    spec = whole(shape) if block is None else pl.BlockSpec(block, index)
    return jax.ShapeDtypeStruct(shape, dtype), spec


def slabs(count, first, width, depth):
    return pl.BlockSpec((count, 1, depth, width), lambda h, *_: (first // count, h, 0, 0))


def send_first(rows, x, gb, me):
    def body(me_ref, x_ref, gb_ref, *out_refs):
        a = norm_rounded(x_ref[...], gb_ref[0:1], gb_ref[3:4])
        for k in range(rows.ways):
            out_refs[k][...] = nn(rows.to_time(k, me_ref[3]), a).astype(BF16)

    d = x.shape[1]
    return call(
        body, (1,), [SCALARS, whole(x.shape), whole(gb.shape)], rows.chunks(d), [], (me, x, gb)
    )


def time_forward(rows, chunks, w):
    t, d = rows.time_rows, chunks[0].shape[1]
    width = w.shape[3]
    shares = w.shape[1]
    pairs = width // LANES
    ways = rows.ways
    rate = LOG2E / math.sqrt(HEAD_DIM)

    def body(*refs):
        chunk_refs = refs[:ways]
        w_ref, a_ref, qkv_ref, log_ref = refs[ways : ways + 4]
        out_refs = refs[ways + 4 : 2 * ways + 4]
        bias_ref, mixed_ref = refs[2 * ways + 4 :]

        @pl.when(pl.program_id(0) == 0)
        def _():
            bias_ref[...] = rows.time_bias()
            for k in range(ways):
                a_ref[k * rows.chunk : (k + 1) * rows.chunk] = chunk_refs[k][...]

        act = a_ref[...]
        for g in range(3):
            qkv_ref[g] = nn(act, w_ref[g, 0]).astype(BF16)

        @pl.loop(0, pairs)
        def _(i):
            lanes = pl.ds(pl.multiple_of(i * LANES, LANES), LANES)
            mixed, logs = pair_forward(
                qkv_ref[0, :, lanes], qkv_ref[1, :, lanes], qkv_ref[2, :, lanes], bias_ref[...], rate
            )
            mixed_ref[:, lanes] = mixed
            log_ref[0, i] = jnp.concatenate(logs, axis=0)

        for k in range(ways):
            out_refs[k][...] = mixed_ref[k * rows.chunk : (k + 1) * rows.chunk]

    got = call(
        body,
        (shares,),
        [whole(c.shape) for c in chunks] + [slabs(3, 0, width, d)],
        [
            made((t, d), BF16),
            made((3, t, d), BF16, (3, t, width), lambda h: (0, 0, h)),
            made((shares, pairs, 2, t), F32, (1, pairs, 2, t), lambda h: (h, 0, 0, 0)),
            *rows.chunks(d, width, lambda h: (0, h)),
        ],
        [pltpu.VMEM((t, t), F32), pltpu.VMEM((t, width), BF16)],
        (*chunks, w),
        flops=2 * t * d * 3 * d,
    )
    return got[0], got[1], got[2], got[3:]


def middle_forward(rows, back, x, w, mix, gb, me):
    t, d = x.shape
    width = w.shape[3]
    shares = w.shape[1]

    def body(me_ref, *refs):
        x_ref, to_ref, sq_ref, mix_ref, gb_ref, o1_ref, y1_ref, x1_ref, qkv_ref = refs[rows.ways :]
        o1 = rows.gathered(refs[: rows.ways], me_ref[3]).astype(BF16)
        o1_ref[...] = o1
        y1 = jnp.zeros((t, d), F32)
        for h in range(shares):
            y1 = y1 + nt(o1[:, h * width : (h + 1) * width], to_ref[0, h])
        y1 = y1.astype(BF16)
        y1_ref[...] = y1
        x1 = x_ref[...] + nn(y1, mix_ref[...])
        x1_ref[...] = x1
        a2 = norm_rounded(x1, gb_ref[1:2], gb_ref[4:5])
        for g in range(3):
            for h in range(shares):
                qkv_ref[g, :, h * width : (h + 1) * width] = nn(a2, sq_ref[g, h]).astype(BF16)

    return call(
        body,
        (1,),
        [
            SCALARS,
            *(whole(c.shape) for c in back),
            whole(x.shape),
            pl.BlockSpec((1, shares, d, width), lambda i: (6, 0, 0, 0)),
            pl.BlockSpec((3, shares, d, width), lambda i: (1, 0, 0, 0)),
            whole(mix.shape),
            whole(gb.shape),
        ],
        [made((t, d), BF16), made((t, d), BF16), made((t, d), F32), made((3, t, d), BF16)],
        [],
        (me, *back, x, w, w, mix, gb),
        flops=2 * t * d * 5 * d,
    )


def space_forward(rows, qkv, x1, w):
    t, d = x1.shape
    width = w.shape[3]
    shares = w.shape[1]
    pairs = width // LANES
    rate = LOG2E / math.sqrt(HEAD_DIM)
    n = rows.frame_rows

    def body(qkv_ref, x1_ref, w_ref, o2_ref, x2_ref, log_ref):
        bias = rows.space_bias()

        @pl.loop(0, pairs)
        def _(i):
            lanes = pl.ds(pl.multiple_of(i * LANES, LANES), LANES)
            for f in range(rows.frames):
                at = slice(f * n, (f + 1) * n)
                mixed, logs = pair_forward(
                    qkv_ref[0, at, lanes], qkv_ref[1, at, lanes], qkv_ref[2, at, lanes], bias, rate
                )
                o2_ref[at, lanes] = mixed
                log_ref[0, i, f] = jnp.concatenate(logs, axis=0)

        @pl.when(pl.program_id(0) == 0)
        def _():
            x2_ref[...] = x1_ref[...]

        x2_ref[...] += nt(o2_ref[...], w_ref[0, 0])

    return call(
        body,
        (shares,),
        [
            pl.BlockSpec((3, t, width), lambda h: (0, 0, h)),
            whole(x1.shape),
            slabs(1, 7, width, d),
        ],
        [
            made((t, d), BF16, (t, width), lambda h: (0, h)),
            made((t, d), F32),
            made(
                (shares, pairs, rows.frames, 2, n),
                F32,
                (1, pairs, rows.frames, 2, n),
                lambda h: (h, 0, 0, 0, 0),
            ),
        ],
        [],
        (qkv, x1, w),
        flops=2 * t * d * d,
    )


def ff_slab(first, per_share, depth, width):
    return pl.BlockSpec(
        (1, 1, depth, width), lambda j: (first + j % per_share, j // per_share, 0, 0)
    )


def mlp_forward(rows, x2, w, gb, gb_next, me):
    t, d = x2.shape
    width = w.shape[3]
    shares = w.shape[1]
    per_share = w.shape[0] // 2
    steps = shares * per_share

    def body(x2_ref, wi_ref, wo_ref, gb_ref, me_ref, gn_ref, x3_ref, *rest):
        send_refs, a3_ref = rest[:-1], rest[-1]
        j = pl.program_id(0)

        @pl.when(j == 0)
        def _():
            a3_ref[...] = norm_rounded(x2_ref[...], gb_ref[2:3], gb_ref[5:6])
            x3_ref[...] = x2_ref[...]

        hid = nn(a3_ref[...], wi_ref[0, 0])
        act = (0.5 * hid * (1.0 + lax.erf(hid * HALF_ROOT))).astype(BF16)
        x3_ref[...] += nt(act, wo_ref[0, 0])

        @pl.when(j == steps - 1)
        def _():
            a = norm_rounded(x3_ref[...], gn_ref[0:1], gn_ref[3:4])
            for k in range(rows.ways):
                send_refs[k][...] = nn(rows.to_time(k, me_ref[3]), a).astype(BF16)

    ins = [
        whole(x2.shape),
        ff_slab(0, per_share, d, width),
        ff_slab(per_share, per_share, d, width),
        whole(gb.shape),
    ]
    ins += [SCALARS, whole(gb_next.shape)]
    outs = [made((t, d), F32)] + rows.chunks(d)
    args = (x2, w, w, gb, me, gb_next)
    return call(
        body, (steps,), ins, outs, [pltpu.VMEM((t, d), BF16)], args, flops=4 * t * d * width * steps
    )


def mlp_backward(rows, grad, x2, w, gb, me, halves, with_output):
    t, d = x2.shape
    width = w.shape[3]
    shares = w.shape[1]
    per_share = w.shape[0] // 2
    steps = shares * per_share

    def body(me_ref, g_ref, x2_ref, wi_ref, wo_ref, gb_ref, go_ref, ki_ref, si_ref, ko_ref, so_ref, sums_ref, *rest):
        if with_output:
            x3_ref, *rest = rest
        a3_ref, a3t_ref, e3_ref, e3t_ref, u_ref = rest
        j = pl.program_id(0)

        @pl.when(j == 0)
        def _():
            hat, _ = norm_parts(x2_ref[...])
            a3 = hat * gb_ref[2:3] + gb_ref[5:6]
            a3_ref[...] = a3.astype(BF16)
            store_by_core(a3t_ref, a3.T.astype(BF16), halves)
            g = g_ref[...]
            e3_ref[...] = g.astype(BF16)
            store_by_core(e3t_ref, g.T.astype(BF16), halves)
            u_ref[...] = jnp.zeros((t, d), F32)
            if with_output:
                x3_ref[...] = x2_ref[...]

        hid = nn(a3_ref[...], wi_ref[0, 0])
        phi = 0.5 * (1.0 + lax.erf(hid * HALF_ROOT))
        act = (hid * phi).astype(BF16)
        slope = phi + hid * jnp.exp(-0.5 * hid * hid) * INV_ROOT_TAU
        dhid = (nn(e3_ref[...], wo_ref[0, 0]) * slope).astype(BF16)
        split_product(e3t_ref, act, ko_ref, so_ref, (0, 0), me_ref)
        split_product(a3t_ref, dhid, ki_ref, si_ref, (0, 0), me_ref)
        u_ref[...] += nt(dhid, wi_ref[0, 0])
        if with_output:
            x3_ref[...] += nt(act, wo_ref[0, 0])

        @pl.when(j == steps - 1)
        def _():
            change, sums = norm_back(u_ref[...], x2_ref[...], gb_ref[2:3])
            go_ref[...] = g_ref[...] + change
            sums_ref[...] = sums

    slab_outs = [
        one
        for _ in range(2)
        for one in halves.array(
            (per_share, shares), (1, 1), lambda j: (j % per_share, j // per_share)
        )
    ]
    grad, ki, si, ko, so, sums, *x3 = call(
        body,
        (steps,),
        [
            SCALARS,
            whole(grad.shape),
            whole(x2.shape),
            ff_slab(0, per_share, d, width),
            ff_slab(per_share, per_share, d, width),
            whole(gb.shape),
        ],
        [made((t, d), F32), *slab_outs, made((2, d), F32)] + [made((t, d), F32)] * with_output,
        [
            pltpu.VMEM((t, d), BF16),
            halves.turned(t),
            pltpu.VMEM((t, d), BF16),
            halves.turned(t),
            pltpu.VMEM((t, d), F32),
        ],
        (me, grad, x2, w, w, gb),
        flops=10 * t * d * width * steps,
    )
    return grad, [(ki, si), (ko, so)], sums, x3


def space_backward(rows, grad, x1, qkv, o2, logs, w, gb, me, halves):
    t, d = x1.shape
    width = w.shape[3]
    shares = w.shape[1]
    pairs = width // LANES
    scale = 1.0 / math.sqrt(HEAD_DIM)
    rate = LOG2E * scale
    n = rows.frame_rows

    def body(me_ref, g_ref, x1_ref, qkv_ref, o2_ref, log_ref, wo_ref, wq_ref, gb_ref, go_ref, keep_ref, send_ref, sums_ref, e2_ref, e2t_ref, a2t_ref, do_ref, dqkv_ref, u_ref):
        h = pl.program_id(0)

        @pl.when(h == 0)
        def _():
            g = g_ref[...]
            e2_ref[...] = g.astype(BF16)
            store_by_core(e2t_ref, g.T.astype(BF16), halves)
            hat, _ = norm_parts(x1_ref[...])
            store_by_core(a2t_ref, (hat * gb_ref[1:2] + gb_ref[4:5]).T.astype(BF16), halves)
            u_ref[...] = jnp.zeros((t, d), F32)

        bias = rows.space_bias()
        split_product(e2t_ref, o2_ref[...], keep_ref, send_ref, (0, 0), me_ref)
        do_ref[...] = nn(e2_ref[...], wo_ref[0, 0]).astype(BF16)

        @pl.loop(0, pairs)
        def _(i):
            lanes = pl.ds(pl.multiple_of(i * LANES, LANES), LANES)
            for f in range(rows.frames):
                at = slice(f * n, (f + 1) * n)
                log = log_ref[0, i, f]
                grads = pair_backward(
                    qkv_ref[0, at, lanes],
                    qkv_ref[1, at, lanes],
                    qkv_ref[2, at, lanes],
                    do_ref[at, lanes],
                    (log[0:1], log[1:2]),
                    bias,
                    rate,
                    scale,
                )
                for part in range(3):
                    dqkv_ref[part, at, lanes] = grads[part]

        for part in range(3):
            split_product(a2t_ref, dqkv_ref[part], keep_ref, send_ref, (part + 1, 0), me_ref)
            u_ref[...] += nt(dqkv_ref[part], wq_ref[part, 0])

        @pl.when(h == shares - 1)
        def _():
            change, sums = norm_back(u_ref[...], x1_ref[...], gb_ref[1:2])
            go_ref[...] = g_ref[...] + change
            sums_ref[...] = sums

    grad, keep, send, sums = call(
        body,
        (shares,),
        [
            SCALARS,
            whole(grad.shape),
            whole(x1.shape),
            pl.BlockSpec((3, t, width), lambda h: (0, 0, h)),
            pl.BlockSpec((t, width), lambda h: (0, h)),
            pl.BlockSpec((1,) + logs.shape[1:], lambda h: (h, 0, 0, 0, 0)),
            slabs(1, 7, width, d),
            slabs(3, 3, width, d),
            whole(gb.shape),
        ],
        [
            made((t, d), F32),
            *halves.array((4, shares), (4, 1), lambda h: (0, h)),
            made((2, d), F32),
        ],
        [
            pltpu.VMEM((t, d), BF16),
            halves.turned(t),
            halves.turned(t),
            pltpu.VMEM((t, width), BF16),
            pltpu.VMEM((3, t, width), BF16),
            pltpu.VMEM((t, d), F32),
        ],
        (me, grad, x1, qkv, o2, logs, w, w, gb),
        flops=2 * t * d * d * 8,
    )
    return grad, (keep, send), sums


def mix_fits(depth, shards, shares):
    return depth // (shards * shares) % 8 == 0


def middle_backward(rows, grad, y1, o1, w, mix, me, halves, shards):
    t, d = grad.shape
    width = w.shape[3]
    shares = w.shape[1]
    fits = mix_fits(d, shards, shares)
    part = d // (shards * shares)

    def body(me_ref, g_ref, y1_ref, o1_ref, to_ref, mix_ref, *rest):
        send_refs, rest = rest[: rows.ways], rest[rows.ways :]
        gk_ref, gs_ref, *rest = rest
        if fits:
            room_ref, order_ref = rest
        else:
            gm_ref, room_ref = rest
        e1 = g_ref[...].astype(BF16)
        dy1 = nt(e1, mix_ref[...]).astype(BF16)
        sends = [rows.to_time(k, me_ref[3]) for k in range(rows.ways)]
        for h in range(shares):
            lanes = slice(h * width, (h + 1) * width)
            do1 = nn(dy1, to_ref[0, h]).astype(BF16)
            for k in range(rows.ways):
                send_refs[k][:, lanes] = nn(sends[k], do1).astype(BF16)
            split_rows(tn(dy1, o1_ref[:, lanes]), gk_ref, gs_ref, (0, h), room_ref, me_ref)
        gm = tn(y1_ref[...], e1)
        if fits:
            gm = gm.reshape(shards, shares, part, d)
            for h in range(shares):
                for half in range(shares):
                    order_ref[:, half] = gm[:, h, :, half * width : (half + 1) * width]
                split_rows(order_ref[...], gk_ref, gs_ref, (1, h), room_ref, me_ref)
        else:
            gm_ref[...] = gm.astype(BF16)

    outs = rows.chunks(d)
    outs += halves.array((1 + fits, shares), (1 + fits, shares), lambda i: (0, 0))
    scratch = [halves.room()]
    if fits:
        scratch.append(pltpu.VMEM((shards, shares, part, width), F32))
    else:
        outs.append(made((d, d), BF16))
    got = call(
        body,
        (1,),
        [
            SCALARS,
            whole(grad.shape),
            whole(y1.shape),
            whole(o1.shape),
            pl.BlockSpec((1, shares, d, width), lambda i: (6, 0, 0, 0)),
            whole(mix.shape),
        ],
        outs,
        scratch,
        (me, grad, y1, o1, w, mix),
        flops=8 * t * d * d,
    )
    do1, (keep, send) = got[: rows.ways], got[rows.ways : rows.ways + 2]
    if not fits:
        gm = mix_slab(got[-1], shards, shares).reshape((1, shares, halves.pairs, 2) + keep.shape[3:])
        keep = jnp.concatenate((keep, lax.dynamic_index_in_dim(gm, me[0], 3, keepdims=False)), axis=0)
        send = jnp.concatenate((send, lax.dynamic_index_in_dim(gm, 1 - me[0], 3, keepdims=False)), axis=0)
    return do1, (keep, send)


def time_backward(rows, do1, a, qkv, logs, w, me, halves):
    t, d = a.shape
    width = w.shape[3]
    shares = w.shape[1]
    pairs = width // LANES
    scale = 1.0 / math.sqrt(HEAD_DIM)
    rate = LOG2E * scale

    def body(me_ref, *refs):
        do_refs, refs = refs[: rows.ways], refs[rows.ways :]
        a_ref, qkv_ref, log_ref, w_ref = refs[:4]
        out_refs, refs = refs[4 : 4 + rows.ways], refs[4 + rows.ways :]
        half_refs, refs = refs[:6], refs[6:]
        bias_ref, dqkv_ref, at_ref, u_ref, do_ref = refs
        h = pl.program_id(0)

        @pl.when(h == 0)
        def _():
            bias_ref[...] = rows.time_bias()
            store_by_core(at_ref, a_ref[...].T, halves)
            u_ref[...] = jnp.zeros((t, d), F32)

        for k in range(rows.ways):
            do_ref[k * rows.chunk : (k + 1) * rows.chunk] = do_refs[k][...]

        @pl.loop(0, pairs)
        def _(i):
            lanes = pl.ds(pl.multiple_of(i * LANES, LANES), LANES)
            log = log_ref[0, i]
            grads = pair_backward(
                qkv_ref[0, :, lanes],
                qkv_ref[1, :, lanes],
                qkv_ref[2, :, lanes],
                do_ref[:, lanes],
                (log[0:1], log[1:2]),
                bias_ref[...],
                rate,
                scale,
            )
            for part in range(3):
                dqkv_ref[part, :, lanes] = grads[part]

        for part in range(3):
            split_product(
                at_ref, dqkv_ref[part], half_refs[2 * part], half_refs[2 * part + 1], (0, 0), me_ref
            )
            u_ref[...] += nt(dqkv_ref[part], w_ref[part, 0])

        @pl.when(h == shares - 1)
        def _():
            for k in range(rows.ways):
                out_refs[k][...] = u_ref[k * rows.chunk : (k + 1) * rows.chunk].astype(BF16)

    got = call(
        body,
        (shares,),
        [
            SCALARS,
            *(pl.BlockSpec((rows.chunk, width), lambda h: (0, h)) for _ in do1),
            whole(a.shape),
            pl.BlockSpec((3, t, width), lambda h: (0, 0, h)),
            pl.BlockSpec((1,) + logs.shape[1:], lambda h: (h, 0, 0, 0)),
            slabs(3, 0, width, d),
        ],
        [
            *rows.chunks(d),
            *(one for _ in range(3) for one in halves.array((1, shares), (1, 1), lambda h: (0, h))),
        ],
        [
            pltpu.VMEM((t, t), F32),
            pltpu.VMEM((3, t, width), BF16),
            halves.turned(t),
            pltpu.VMEM((t, d), F32),
            pltpu.VMEM((t, width), BF16),
        ],
        (me, *do1, a, qkv, logs, w),
        flops=2 * t * d * d * 6,
    )
    parts = got[rows.ways :]
    return got[: rows.ways], [tuple(parts[i : i + 2]) for i in (0, 2, 4)]


def first_norm_back(rows, back, x, grad, gb, me):
    t, d = x.shape

    def body(me_ref, *refs):
        x_ref, g_ref, gb_ref, go_ref, sums_ref = refs[rows.ways :]
        u = rows.gathered(refs[: rows.ways], me_ref[3])
        change, sums = norm_back(u, x_ref[...], gb_ref[0:1])
        go_ref[...] = g_ref[...] + change
        sums_ref[...] = sums

    return call(
        body,
        (1,),
        [SCALARS, *(whole(c.shape) for c in back), whole(x.shape), whole(grad.shape), whole(gb.shape)],
        [made((t, d), F32), made((2, d), F32)],
        [],
        (me, *back, x, grad, gb),
    )


def homes():
    clips, ways = lax.axis_size("clip"), lax.axis_size("seq")
    pairs = []
    for clip in range(clips):
        for seq in range(ways):
            home_clip = clip - clip % 2 + seq % 2
            home_seq = seq // 2 + (ways // 2) * (clip % 2)
            pairs.append((clip * ways + seq, home_clip * ways + home_seq))
    return pairs


def go_home(a):
    return lax.ppermute(a, ("clip", "seq"), homes())


def go_back(a):
    return lax.ppermute(a, ("clip", "seq"), [(home, device) for device, home in homes()])


def member_of(clip, seq):
    return clip % 2 + 2 * (seq % (lax.axis_size("seq") // 2))


def swap_places(chunks):
    clips, ways = lax.axis_size("clip"), lax.axis_size("seq")
    got = [chunks[0]]
    for k in range(1, ways):
        pairs = []
        for clip in range(clips):
            for seq in range(ways):
                other = member_of(clip, seq) ^ k
                to_clip = clip - clip % 2 + other % 2
                to_seq = seq - seq % (ways // 2) + other // 2
                pairs.append((clip * ways + seq, to_clip * ways + to_seq))
        got.append(lax.ppermute(chunks[k], ("clip", "seq"), pairs))
    return got


def columns(a, r, width):
    return a.reshape(r, -1, width).transpose(1, 0, 2)


def pack_attention(time_qkv, time_out, time_mix, space_qkv, space_out):
    r, _, width = time_qkv.shape
    mix = time_mix.reshape(-1, time_mix.shape[1] // width, width).transpose(1, 0, 2).reshape(1, r, width)
    return jnp.concatenate(
        (
            columns(time_qkv, r, width),
            columns(space_qkv, r, width),
            time_out.T[None],
            space_out.T[None],
            mix,
        ),
        axis=0,
    )


def pack_feed_forward(mlp_in, mlp_out, width):
    r = mlp_in.shape[0]
    return jnp.concatenate((columns(mlp_in, r, width), columns(mlp_out.T, r, width)), axis=0)


def gather_slabs(pack):
    full = lax.all_gather(pack, ("head", "clip", "seq"), axis=1, tiled=True)
    return full.reshape(pack.shape[0], lax.axis_size("head"), -1, pack.shape[2])


def spread_steps(pack, me):
    ways, clips = lax.axis_size("seq"), lax.axis_size("clip")
    shares = lax.axis_size("head")
    n, r, width = pack.shape
    pack = yield pack
    turned = [pack] + [
        lax.ppermute(pack, "seq", [(i, (i + k) % ways) for i in range(ways)]) for k in range(1, ways)
    ]
    turned = yield turned
    orders = (((0, 1), "x", "h"), ((3, 2), "h", "x"))
    some = [jnp.stack([turned[k] for k in steps]) for steps, _, _ in orders]
    come = yield [cross(a, first) for a, (_, first, _) in zip(some, orders)]
    some = [jnp.concatenate(pair, axis=0) for pair in zip(some, come)]
    come = yield [cross(a, second) for a, (_, _, second) in zip(some, orders)]
    runs = []
    for mine, other, (steps, first, second) in zip(some, come, orders):
        where = [(k, {first: f}) for f in (0, 1) for k in steps]
        for g, blocks in enumerate((mine, other)):
            runs.append((blocks, [(k, {**at, second: g}) for k, at in where], 0))
    come = yield [cross(blocks, "c") for blocks, _, _ in runs]
    runs += [(far, where, 1) for far, (_, where, _) in zip(come, runs)]
    count = sum(len(where) for _, where, _ in runs)

    def body(me_ref, *refs):
        sources, out_ref, sems = refs[: len(runs)], refs[-2], refs[-1]
        copies = []
        for source, (_, where, core) in zip(sources, runs):
            for i, (k, at) in enumerate(where):
                share = jnp.bitwise_xor(me_ref[2], at["h"])
                clip = 2 * jnp.bitwise_xor(me_ref[1], at["x"]) + jnp.bitwise_xor(me_ref[0], core)
                seq = lax.rem(me_ref[4] + (ways - k), ways)
                copies.append(
                    pltpu.make_async_copy(
                        source.at[i], out_ref.at[:, share, clip * ways + seq], sems.at[len(copies)]
                    )
                )
        for copy in copies:
            copy.start()
        for copy in copies:
            copy.wait()

    full = pl.pallas_call(
        body,
        out_shape=jax.ShapeDtypeStruct((n, shares, clips * ways, r, width), BF16),
        in_specs=[SCALARS] + [pl.BlockSpec(memory_space=pltpu.HBM)] * len(runs),
        out_specs=pl.BlockSpec(memory_space=pltpu.VMEM),
        scratch_shapes=[pltpu.SemaphoreType.DMA((count,))],
        compiler_params=pltpu.CompilerParams(vmem_limit_bytes=VMEM),
        cost_estimate=pl.CostEstimate(
            flops=0, bytes_accessed=4 * n * shares * clips * ways * r * width, transcendentals=0
        ),
    )(me, *(blocks for blocks, _, _ in runs))
    yield full.reshape(n, shares, clips * ways * r, width)


class Spread:
    def __init__(self, pack, me):
        self.way = spread_steps(pack, me)
        self.come = next(self.way)

    def hold(self, x):
        x, self.come = lax.optimization_barrier((x, self.come))
        return x

    def step(self, x):
        x = self.hold(x)
        self.come = self.way.send(self.come)
        return x


def mix_whole(slab, shards):
    shares, depth, width = slab.shape
    part = slab.reshape(shares, shards, shares, depth // (shards * shares), width)
    return part.transpose(1, 0, 3, 2, 4).reshape(depth, shares * width)


def mix_slab(whole_grad, shards, shares):
    depth, full = whole_grad.shape
    width = full // shares
    part = whole_grad.reshape(shards, shares, depth // (shards * shares), shares, width)
    return part.transpose(1, 0, 3, 2, 4).reshape(1, shares, depth, width)


class Piece:
    def __init__(self, keep, got, first, n, order):
        self.near = (keep, got)
        self.first = first
        self.n = n
        self.order = order
        self.step = 0
        self.held = []
        self.result = None


PLACE = {"x": 1, "h": 2}


def fold(pieces, me, last_by_rows):
    ways = lax.axis_size("seq")
    depth, width = pieces[0].near[0].shape[-2:]
    r = depth // ways
    used = {}
    arrays = []

    def number(a):
        for i, known in enumerate(arrays):
            if known is a:
                return i
        arrays.append(a)
        return len(arrays) - 1

    plans = []
    for p in pieces:
        link = p.order[p.step] if p.step < 2 else "z"
        blocks = p.n * (2 if p.step == 0 else 1)
        base = used.get(link, 0)
        used[link] = base + blocks
        near = [number(a) for a in p.near]
        held = [(number(a), at) for a, at in p.held]
        plans.append((p, link, base, near, held))
    links = sorted(used)
    shapes = [
        (ways, used[k], r, width) if k == "z" and last_by_rows else (used[k], depth, width)
        for k in links
    ]
    rooms, counts = [], []
    for p, link, base, near, held in plans:
        each = 2 if p.step == 0 else 1
        counts.append((each, len(near) + len(held)))
        rooms += [(each * p.n, depth, width)] * (len(near) + len(held))
    copies_needed = sum(each * terms for each, terms in counts)

    def body(me_ref, *refs):
        sources = refs[: len(arrays)]
        outs = dict(zip(links, refs[len(arrays) : len(arrays) + len(links)]))
        held_refs = refs[len(arrays) + len(links) : -1]
        sems = refs[-1]
        mine = {name: me_ref[PLACE[name]] for name in PLACE}
        groups = []
        room = 0
        sem = 0
        for p, link, base, near, held in plans:
            group = []
            if p.step == 0:
                for term in near:
                    for k in range(2):
                        pick = {p.order[0]: 1 - mine[p.order[0]], p.order[1]: k}
                        source = sources[term].at[pl.ds(p.first, p.n), pick["h"], pick["x"]]
                        group.append((source, held_refs[room].at[pl.ds(k * p.n, p.n)]))
                    room += 1
            else:
                last = p.order[1]
                pick = {p.order[0]: mine[p.order[0]]}
                pick[last] = 1 - mine[last] if p.step == 1 else mine[last]
                for term in near:
                    source = sources[term].at[pl.ds(p.first, p.n), pick["h"], pick["x"]]
                    group.append((source, held_refs[room]))
                    room += 1
                for i, (term, at) in enumerate(held):
                    start = at + pick[last] * p.n if i == 0 else at
                    group.append((sources[term].at[pl.ds(start, p.n)], held_refs[room]))
                    room += 1
            made_copies = []
            for source, target in group:
                made_copies.append(pltpu.make_async_copy(source, target, sems.at[sem]))
                sem += 1
            groups.append(made_copies)
        for group in groups:
            for copy in group:
                copy.start()
        room = 0
        for (p, link, base, near, held), (each, terms), group in zip(plans, counts, groups):
            these = held_refs[room : room + terms]
            room += terms
            for copy in group:
                copy.wait()

            @pl.loop(0, each * p.n)
            def _(i, these=these, base=base, out=outs[link], last=p.step == 2 and last_by_rows):
                value = these[0][i].astype(F32)
                for one in these[1:]:
                    value = value + one[i].astype(F32)
                value = value.astype(BF16)
                if last:
                    for k in range(ways):
                        out[k, base + i] = value[k * r : (k + 1) * r]
                else:
                    out[base + i] = value

    moved = sum(2 * math.prod(room) for room in rooms) + sum(2 * math.prod(shape) for shape in shapes)
    sums = pl.pallas_call(
        body,
        out_shape=[jax.ShapeDtypeStruct(shape, BF16) for shape in shapes],
        in_specs=[SCALARS] + [pl.BlockSpec(memory_space=pltpu.HBM)] * len(arrays),
        out_specs=[pl.BlockSpec(memory_space=pltpu.VMEM)] * len(links),
        scratch_shapes=[pltpu.VMEM(room, BF16) for room in rooms]
        + [pltpu.SemaphoreType.DMA((copies_needed,))],
        compiler_params=pltpu.CompilerParams(vmem_limit_bytes=VMEM),
        cost_estimate=pl.CostEstimate(flops=0, bytes_accessed=moved, transcendentals=0),
    )(me, *arrays)
    return [(p, link, base) for p, link, base, _, _ in plans], dict(zip(links, sums))


def cross(a, name):
    axis, bit = ("head", 0) if name == "h" else ("clip", 1 if name == "x" else 0)
    size = lax.axis_size(axis)
    return lax.ppermute(a, axis, [(i, i ^ (1 << bit)) for i in range(size)])


def pieces_of(halves_of):
    total = sum(keep.shape[0] for keep, _ in halves_of)
    found = []
    seen = 0
    for keep, send in halves_of:
        got = cross(send, "c")
        n = keep.shape[0]
        first = min(max((total + 1) // 2 - seen, 0), n)
        if first:
            found.append(Piece(keep, got, 0, first, ("x", "h")))
        if n > first:
            found.append(Piece(keep, got, first, n - first, ("h", "x")))
        seen += n
    return found


def move(x, pieces, me, at_end=False):
    plans, sums = fold(pieces, me, at_end)
    x, sums = lax.optimization_barrier((x, sums))
    got = {}
    for link, array in sums.items():
        if link == "z":
            if at_end:
                every = lax.all_to_all(array, "seq", split_axis=0, concat_axis=0, tiled=True)
                got[link] = jnp.sum(every.astype(F32), axis=0)
            else:
                own = lax.psum_scatter(array, "seq", scatter_dimension=1, tiled=True)
                got[link] = own.astype(F32)
        else:
            got[link] = cross(array, link)
    for p, link, base in plans:
        if link == "z":
            p.result = got[link][base : base + p.n]
        else:
            p.held.append((got[link], base))
        p.step += 1
    return x


def settle(x, pieces):
    arrays = []
    for p in pieces:
        if not any(p.held[-1][0] is a for a in arrays):
            arrays.append(p.held[-1][0])
    x, came = lax.optimization_barrier((x, arrays))
    for p in pieces:
        for old, new in zip(arrays, came):
            if p.held[-1][0] is old:
                p.held[-1] = (new, p.held[-1][1])
                break
    return x


def reduce_plain(halves_of, core):
    def joined(keep, send):
        low = jnp.where(core == 0, keep, send)
        high = jnp.where(core == 0, send, keep)
        n, shares, pairs, depth, width = keep.shape
        return jnp.stack((low, high), axis=3).reshape(n, shares, 2 * pairs * depth, width)

    g = jnp.concatenate([joined(*pair) for pair in halves_of], axis=0)
    g = lax.psum_scatter(g, "head", scatter_dimension=1, tiled=True)
    g = lax.psum_scatter(g.astype(F32), ("clip", "seq"), scatter_dimension=2, tiled=True)
    return g[:, 0]


def gather_norms(gain, bias):
    layers, norms, part = gain.shape
    both = jnp.concatenate((gain, bias), axis=1).reshape(1, -1)
    count = lax.axis_size("clip") * lax.axis_size("seq") * lax.axis_size("head")
    width = round_up(both.shape[1], 128)
    padded = jnp.pad(both, ((0, 0), (0, width - both.shape[1])))
    every = lax.all_to_all(
        jnp.broadcast_to(padded, (count, width)), ALL, split_axis=0, concat_axis=0, tiled=True
    )[:, : both.shape[1]]
    return every.reshape(count, layers * 2 * norms, part).transpose(1, 0, 2).reshape(layers, 2 * norms, -1)


def reduce_norms(sums):
    count = lax.axis_size("clip") * lax.axis_size("seq") * lax.axis_size("head")
    rows, features = sums.shape
    part = features // count
    a = sums.reshape(rows, count, part).transpose(1, 0, 2).reshape(count, rows * part)
    width = round_up(rows * part, 128)
    a = jnp.pad(a, ((0, 0), (0, width - rows * part)))
    every = lax.all_to_all(a, ALL, split_axis=0, concat_axis=0, tiled=True)
    return jnp.sum(every, axis=0)[: rows * part].reshape(rows, part)


def on_device(
    tokens,
    cotangent,
    time_qkv,
    time_out,
    time_mix,
    space_qkv,
    space_out,
    mlp_in,
    mlp_out,
    norm_gain,
    norm_bias,
):
    layers = time_qkv.shape[0]
    clips, frames, places, d = tokens.shape
    ways = lax.axis_size("seq")
    shards = lax.axis_size("clip") * ways
    rows = Rows(clips * frames, places, ways)
    shares = lax.axis_size("head")

    def as_rows(a):
        a = a.astype(F32).reshape(rows.frames, places, d)
        a = jnp.pad(a, ((0, 0), (0, rows.frame_rows - places), (0, 0)))
        return a.reshape(rows.rows, d)

    def from_rows(a):
        a = a.reshape(rows.frames, rows.frame_rows, d)[:, :places]
        return a.reshape(tokens.shape)

    gbs = gather_norms(norm_gain, norm_bias)
    gb = [gbs[l] for l in range(layers)]
    packs = [
        pack_attention(time_qkv[l], time_out[l], time_mix[l], space_qkv[l], space_out[l])
        for l in range(layers)
    ]
    packs_ff = [pack_feed_forward(mlp_in[l], mlp_out[l], time_qkv.shape[3]) for l in range(layers)]
    weights = [gather_slabs(pack) for pack in packs]
    mixes = [mix_whole(w[-1], shards) for w in weights]
    quick = lax.axis_size("clip") == 4 and shares == 2 and ways == 4 and time_qkv.shape[1] % 16 == 0

    halves = Halves(lax.axis_size("clip"), d, time_qkv.shape[3])
    clip = lax.axis_index("clip")
    member = member_of(clip, lax.axis_index("seq"))
    me = jnp.stack((clip & 1, (clip >> 1) & 1, lax.axis_index("head"), member, lax.axis_index("seq"))).astype(
        jnp.int32
    )
    if quick:
        spreads = [Spread(pack, me) for pack in packs_ff]
        weights_ff = []
    else:
        weights_ff = [gather_slabs(pack) for pack in packs_ff]

    home = go_home(tokens)
    if quick:
        first = spreads[0]
        home, gb = first.step((home, gb))
    x = as_rows(home)
    send = send_first(rows, x, gb[0], me)
    kept = []
    for l in range(layers):
        w = weights[l]
        send = swap_places(send)
        if quick and l == 0:
            for _ in range(2):
                send = first.step(send)
            for spread in spreads[1:]:
                send = spread.step(send)
                send = spread.hold(send)
            send = first.step(send)
        elif quick:
            send = spreads[l].step(send)
        a1, qkv1, log1, o1_time = time_forward(rows, send, w)
        back = swap_places(o1_time)
        if quick:
            back = spreads[l].step(back)
            weights_ff.append(spreads[l].come)
            if l == 0:
                for spread in spreads[1:]:
                    back = spread.step(back)
        o1, y1, x1, qkv2 = middle_forward(rows, back, x, w, mixes[l], gb[l], me)
        o2, x2, log2 = space_forward(rows, qkv2, x1, w)
        if quick and l == 0:
            for spread in spreads[1:]:
                x2 = spread.step(x2)
        kept.append((x, a1, qkv1, log1, o1, y1, x1, qkv2, o2, log2, x2))
        if l + 1 < layers:
            x, *send = mlp_forward(rows, x2, weights_ff[l], gb[l], gb[l + 1], me)

    grad = as_rows(go_home(cotangent))
    norm_rows = [None] * layers
    summed = [None] * layers
    late = []
    for l in reversed(range(layers)):
        w = weights[l]
        x, a1, qkv1, log1, o1, y1, x1, qkv2, o2, log2, x2 = kept[l]
        grad, g_ff, s3, x3 = mlp_backward(
            rows, grad, x2, weights_ff[l], gb[l], me, halves, l + 1 == layers
        )
        if x3:
            output = go_back(from_rows(x3[0].astype(BF16)))
        if quick:
            ff = pieces_of(g_ff)
            if late:
                grad = settle(grad, late)
                grad = move(grad, late, me)
                late = [p for p in late if p.step < 3]
        grad, g_space, s2 = space_backward(rows, grad, x1, qkv2, o2, log2, w, gb[l], me, halves)
        if quick:
            space = pieces_of([g_space])
            if late:
                grad = settle(grad, late)
            grad, output = move((grad, output), ff, me)
        do1, g_out = middle_backward(rows, grad, y1, o1, w, mixes[l], me, halves, shards)
        do1 = swap_places(do1)
        if quick:
            do1 = move(do1, ff + space + late, me)
        da1, g_time = time_backward(rows, do1, a1, qkv1, log1, w, me, halves)
        if quick:
            da1 = settle(da1, ff + space)
        da1 = swap_places(da1)
        if quick:
            rest = pieces_of([g_out] + g_time)
            da1 = move(da1, ff + space + rest, me)
            late = space + rest
        grad, s1 = first_norm_back(rows, da1, x, grad, gb[l], me)
        norm_rows[l] = jnp.concatenate((s1[0:1], s2[0:1], s3[0:1], s1[1:2], s2[1:2], s3[1:2]), axis=0)
        if quick:
            summed[l] = ff + space + rest
        else:
            summed[l] = [reduce_plain(g_ff + [g_space, g_out] + g_time, clip & 1)]
    norm_sums = reduce_norms(jnp.concatenate(norm_rows, axis=0)).reshape(layers, 2, 3, -1)
    if quick:
        tokens_grad = go_back(from_rows(grad.astype(BF16)))
        tokens_grad = move(tokens_grad, late, me)
        norm_sums = move(norm_sums, rest, me, True)
        summed = [[p.result for p in some] for some in summed]
    cuts = (2 * g_ff[0][0].shape[0], g_space[0].shape[0], g_out[0].shape[0], len(g_time))
    results = []
    for some in summed:
        slabs_of = jnp.concatenate(some, axis=0)
        ends = [sum(cuts[: i + 1]) for i in range(4)]
        results.append([slabs_of[e - c : e] for c, e in zip(cuts, ends)])
    if not quick:
        tokens_grad = go_back(from_rows(grad.astype(BF16)))
    tokens_grad = tokens_grad.astype(F32)

    def stacked(form):
        return jnp.stack([form(*results[l]) for l in range(layers)])

    def rows_of(a):
        return a.transpose(1, 0, 2)

    def flat(a):
        return rows_of(a).reshape(a.shape[1], -1)

    def mix_rows(a):
        r, width = a.shape
        return a.reshape(shares, r // shares, width).transpose(1, 0, 2).reshape(r // shares, -1)

    per_share = mlp_in.shape[2] // time_qkv.shape[3]
    return (
        output,
        tokens_grad,
        stacked(lambda ff, s, t, q: rows_of(q)),
        stacked(lambda ff, s, t, q: t[0].T),
        stacked(lambda ff, s, t, q: mix_rows(t[1])),
        stacked(lambda ff, s, t, q: rows_of(s[1:])),
        stacked(lambda ff, s, t, q: s[0].T),
        stacked(lambda ff, s, t, q: flat(ff[:per_share])),
        stacked(lambda ff, s, t, q: flat(ff[per_share:]).T),
        norm_sums[:, 0],
        norm_sums[:, 1],
    )


def solution(mesh):
    token_spec = P(("clip", "head"), "seq", None, None)
    in_specs = (
        token_spec,
        token_spec,
        P(None, ("clip", "seq"), None, "head"),
        P(None, "head", ("clip", "seq")),
        P(None, ("clip", "seq", "head"), None),
        P(None, ("clip", "seq"), None, "head"),
        P(None, "head", ("clip", "seq")),
        P(None, ("clip", "seq"), "head"),
        P(None, "head", ("clip", "seq")),
        P(None, None, ("clip", "seq", "head")),
        P(None, None, ("clip", "seq", "head")),
    )
    return jax.shard_map(
        on_device, mesh=mesh, in_specs=in_specs, out_specs=in_specs, check_vma=False
    )
```

```python
import functools
import math

import jax
import jax.numpy as jnp
from jax import lax
from jax.experimental import pallas as pl
from jax.experimental.pallas import tpu as pltpu
from jax.sharding import PartitionSpec as P

HEAD_DIM = 64
NORM_EPS = 1e-06
HALF_ROOT = 0.7071067811865476
INV_ROOT_TAU = 0.3989422804014327
LOG2E = 1.4426950408889634
FAR = -1e30
LANES = 128
VMEM = 56 * 1024 * 1024
SHOWN = 1.0
ALL = ("clip", "seq", "head")
BF16 = jnp.bfloat16
F32 = jnp.float32


def round_up(value, step):
    return -(-value // step) * step


def nn(a, b):
    return lax.dot_general(a, b, (((1,), (0,)), ((), ())), preferred_element_type=F32)


def nt(a, b):
    return lax.dot_general(a, b, (((1,), (1,)), ((), ())), preferred_element_type=F32)


def tn(a, b):
    return lax.dot_general(a, b, (((0,), (0,)), ((), ())), preferred_element_type=F32)


def norm_parts(x):
    mean = jnp.mean(x, axis=-1, keepdims=True)
    centred = x - mean
    spread = lax.rsqrt(jnp.mean(centred * centred, axis=-1, keepdims=True) + NORM_EPS)
    return centred * spread, spread


def norm_rounded(x, gain, bias):
    hat, _ = norm_parts(x)
    return (hat * gain + bias).astype(BF16)


def norm_back(u, x, gain):
    hat, spread = norm_parts(x)
    scaled = u * gain
    mean_scaled = jnp.mean(scaled, axis=-1, keepdims=True)
    mean_cross = jnp.mean(scaled * hat, axis=-1, keepdims=True)
    change = spread * (scaled - mean_scaled - hat * mean_cross)
    sums = jnp.concatenate(
        (jnp.sum(u * hat, axis=0, keepdims=True), jnp.sum(u, axis=0, keepdims=True)), axis=0
    )
    return change, sums


class Rows:
    def __init__(self, frames, places, ways):
        self.frames = frames
        self.places = places
        self.ways = ways
        self.frame_rows = round_up(places, 16)
        self.rows = frames * self.frame_rows
        self.block = places // ways
        self.chunk = round_up(frames * self.block, 8)
        self.time_rows = ways * self.chunk

    def split(self, r):
        way = jnp.zeros_like(r)
        for k in range(1, self.ways):
            way = way + (r >= k * self.chunk).astype(jnp.int32)
        rest = r - way * self.chunk
        frame = jnp.zeros_like(r)
        for k in range(1, self.frames):
            frame = frame + (rest >= k * self.block).astype(jnp.int32)
        real = rest < self.frames * self.block
        return way, frame, rest - frame * self.block, real

    def to_time(self, k, member):
        r = lax.broadcasted_iota(jnp.int32, (self.chunk, 1), 0)
        _, frame, place, real = self.split(r)
        way = jnp.bitwise_xor(member, k)
        source = jnp.where(real, frame * self.frame_rows + way * self.block + place, -1)
        c = lax.broadcasted_iota(jnp.int32, (self.chunk, self.rows), 1)
        return jnp.where(c == source, 1.0, 0.0).astype(BF16)

    def gathered(self, chunk_refs, member):
        total = tn(self.to_time(0, member), chunk_refs[0][...])
        for k in range(1, self.ways):
            total = total + tn(self.to_time(k, member), chunk_refs[k][...])
        return total

    def chunks(self, width, block=None, index=None):
        return [
            made((self.chunk, width), BF16)
            if block is None
            else made((self.chunk, width), BF16, (self.chunk, block), index)
            for _ in range(self.ways)
        ]

    def time_bias(self):
        def label(r):
            _, _, place, real = self.split(r)
            return jnp.where(real, place, -1)

        a = label(lax.broadcasted_iota(jnp.int32, (self.time_rows, 1), 0))
        b = label(lax.broadcasted_iota(jnp.int32, (1, self.time_rows), 1))
        return jnp.where(a == b, 0.0, FAR).astype(F32)

    def space_bias(self):
        a = lax.broadcasted_iota(jnp.int32, (self.frame_rows, 1), 0)
        return jnp.where(a < self.places, 0.0, FAR).astype(F32)


def lane_masks(rows):
    lane = lax.broadcasted_iota(jnp.int32, (rows, LANES), 1)
    return lane < HEAD_DIM


def one_of(value, low, half):
    zero = jnp.zeros_like(value)
    return jnp.where(low, value, zero) if half == 0 else jnp.where(low, zero, value)


def pair_forward(q, k, v, bias, rate):
    low = lane_masks(q.shape[0])
    mixed, logs = [], []
    for half in range(2):
        s = nt(k, one_of(q, low, half)) + bias
        peak = jnp.max(s, axis=0, keepdims=True)
        e = jnp.exp2((s - peak) * rate)
        total = jnp.sum(e, axis=0, keepdims=True)
        soft = (e * (1.0 / total)).astype(BF16)
        mixed.append(tn(soft, v))
        logs.append(peak * rate + jnp.log2(total))
    return jnp.where(low, mixed[0], mixed[1]).astype(BF16), logs


def pair_backward(q, k, v, do, logs, bias, rate, scale):
    low = lane_masks(q.shape[0])
    dq, dk, dv = [], [], []
    for half in range(2):
        s = nt(k, one_of(q, low, half)) + bias
        soft = jnp.exp2(s * rate - logs[half])
        dp = nt(v, one_of(do, low, half))
        ds = (soft * (dp - jnp.sum(soft * dp, axis=0, keepdims=True))).astype(BF16)
        dv.append(nn(soft.astype(BF16), do))
        dk.append(nn(ds, q))
        dq.append(tn(ds, k))
    return (
        (jnp.where(low, dq[0], dq[1]) * scale).astype(BF16),
        (jnp.where(low, dk[0], dk[1]) * scale).astype(BF16),
        jnp.where(low, dv[0], dv[1]).astype(BF16),
    )


def split_rows(value, keep_ref, send_ref, at, room_ref, me_ref):
    mine = me_ref[0]
    room_ref[...] = value.reshape(room_ref.shape)
    keep_ref[at] = room_ref[:, mine].astype(BF16)
    send_ref[at] = room_ref[:, 1 - mine].astype(BF16)


def store_by_core(ref, value, halves):
    n = halves.rows
    for core in range(2):
        for pair in range(halves.pairs):
            first = (2 * pair + core) * n
            ref[core, pair * n : (pair + 1) * n] = value[first : first + n]


def split_product(left_ref, right, keep_ref, send_ref, at, me_ref):
    mine = me_ref[0]
    shape = keep_ref.shape[len(at) :]
    keep_ref[at] = nn(left_ref[mine], right).reshape(shape).astype(BF16)
    send_ref[at] = nn(left_ref[1 - mine], right).reshape(shape).astype(BF16)


class Halves:
    def __init__(self, clips, depth, width):
        self.pairs = clips // 2
        self.rows = depth // clips
        self.width = width

    def array(self, lead, block, index):
        tail = (self.pairs, self.rows, self.width)
        one = lambda: made(lead + tail, BF16, block + tail, lambda *g: index(*g) + (0, 0, 0))
        return [one(), one()]

    def turned(self, columns):
        return pltpu.VMEM((2, self.pairs * self.rows, columns), BF16)

    def room(self):
        return pltpu.VMEM((self.pairs, 2, self.rows, self.width), F32)


SCALARS = pl.BlockSpec(memory_space=pltpu.SMEM)


def call(body, grid, ins, outs, scratch, args, flops=0):
    specs = [spec for spec in ins]
    moved = sum(math.prod(o.shape) * o.dtype.itemsize for o, _ in outs)
    moved += sum(math.prod(a.shape) * a.dtype.itemsize for a in args)
    return pl.pallas_call(
        body,
        out_shape=[shape for shape, _ in outs],
        grid=grid,
        in_specs=specs,
        out_specs=[spec for _, spec in outs],
        scratch_shapes=scratch,
        compiler_params=pltpu.CompilerParams(vmem_limit_bytes=VMEM),
        cost_estimate=pl.CostEstimate(
            flops=int(flops * SHOWN), bytes_accessed=int(moved * SHOWN), transcendentals=0
        ),
    )(*args)


def whole(shape):
    zeros = (0,) * len(shape)
    return pl.BlockSpec(shape, lambda *_: zeros)


def made(shape, dtype, block=None, index=None):
    spec = whole(shape) if block is None else pl.BlockSpec(block, index)
    return jax.ShapeDtypeStruct(shape, dtype), spec


def slabs(count, first, width, depth):
    return pl.BlockSpec((count, 1, depth, width), lambda h, *_: (first // count, h, 0, 0))


def send_first(rows, x, gb, me):
    def body(me_ref, x_ref, gb_ref, *out_refs):
        a = norm_rounded(x_ref[...], gb_ref[0:1], gb_ref[3:4])
        for k in range(rows.ways):
            out_refs[k][...] = nn(rows.to_time(k, me_ref[3]), a).astype(BF16)

    d = x.shape[1]
    return call(
        body, (1,), [SCALARS, whole(x.shape), whole(gb.shape)], rows.chunks(d), [], (me, x, gb)
    )


def time_forward(rows, chunks, w):
    t, d = rows.time_rows, chunks[0].shape[1]
    width = w.shape[3]
    shares = w.shape[1]
    pairs = width // LANES
    ways = rows.ways
    rate = LOG2E / math.sqrt(HEAD_DIM)

    def body(*refs):
        chunk_refs = refs[:ways]
        w_ref, a_ref, qkv_ref, log_ref = refs[ways : ways + 4]
        out_refs = refs[ways + 4 : 2 * ways + 4]
        bias_ref, mixed_ref = refs[2 * ways + 4 :]

        @pl.when(pl.program_id(0) == 0)
        def _():
            bias_ref[...] = rows.time_bias()
            for k in range(ways):
                a_ref[k * rows.chunk : (k + 1) * rows.chunk] = chunk_refs[k][...]

        act = a_ref[...]
        for g in range(3):
            qkv_ref[g] = nn(act, w_ref[g, 0]).astype(BF16)

        @pl.loop(0, pairs)
        def _(i):
            lanes = pl.ds(pl.multiple_of(i * LANES, LANES), LANES)
            mixed, logs = pair_forward(
                qkv_ref[0, :, lanes], qkv_ref[1, :, lanes], qkv_ref[2, :, lanes], bias_ref[...], rate
            )
            mixed_ref[:, lanes] = mixed
            log_ref[0, i] = jnp.concatenate(logs, axis=0)

        for k in range(ways):
            out_refs[k][...] = mixed_ref[k * rows.chunk : (k + 1) * rows.chunk]

    got = call(
        body,
        (shares,),
        [whole(c.shape) for c in chunks] + [slabs(3, 0, width, d)],
        [
            made((t, d), BF16),
            made((3, t, d), BF16, (3, t, width), lambda h: (0, 0, h)),
            made((shares, pairs, 2, t), F32, (1, pairs, 2, t), lambda h: (h, 0, 0, 0)),
            *rows.chunks(d, width, lambda h: (0, h)),
        ],
        [pltpu.VMEM((t, t), F32), pltpu.VMEM((t, width), BF16)],
        (*chunks, w),
        flops=2 * t * d * 3 * d,
    )
    return got[0], got[1], got[2], got[3:]


def middle_forward(rows, back, x, w, mix, gb, me):
    t, d = x.shape
    width = w.shape[3]
    shares = w.shape[1]

    def body(me_ref, *refs):
        x_ref, to_ref, sq_ref, mix_ref, gb_ref, o1_ref, y1_ref, x1_ref, qkv_ref = refs[rows.ways :]
        o1 = rows.gathered(refs[: rows.ways], me_ref[3]).astype(BF16)
        o1_ref[...] = o1
        y1 = jnp.zeros((t, d), F32)
        for h in range(shares):
            y1 = y1 + nt(o1[:, h * width : (h + 1) * width], to_ref[0, h])
        y1 = y1.astype(BF16)
        y1_ref[...] = y1
        x1 = x_ref[...] + nn(y1, mix_ref[...])
        x1_ref[...] = x1
        a2 = norm_rounded(x1, gb_ref[1:2], gb_ref[4:5])
        for g in range(3):
            for h in range(shares):
                qkv_ref[g, :, h * width : (h + 1) * width] = nn(a2, sq_ref[g, h]).astype(BF16)

    return call(
        body,
        (1,),
        [
            SCALARS,
            *(whole(c.shape) for c in back),
            whole(x.shape),
            pl.BlockSpec((1, shares, d, width), lambda i: (6, 0, 0, 0)),
            pl.BlockSpec((3, shares, d, width), lambda i: (1, 0, 0, 0)),
            whole(mix.shape),
            whole(gb.shape),
        ],
        [made((t, d), BF16), made((t, d), BF16), made((t, d), F32), made((3, t, d), BF16)],
        [],
        (me, *back, x, w, w, mix, gb),
        flops=2 * t * d * 5 * d,
    )


def space_forward(rows, qkv, x1, w):
    t, d = x1.shape
    width = w.shape[3]
    shares = w.shape[1]
    pairs = width // LANES
    rate = LOG2E / math.sqrt(HEAD_DIM)
    n = rows.frame_rows

    def body(qkv_ref, x1_ref, w_ref, o2_ref, x2_ref, log_ref):
        bias = rows.space_bias()

        @pl.loop(0, pairs)
        def _(i):
            lanes = pl.ds(pl.multiple_of(i * LANES, LANES), LANES)
            for f in range(rows.frames):
                at = slice(f * n, (f + 1) * n)
                mixed, logs = pair_forward(
                    qkv_ref[0, at, lanes], qkv_ref[1, at, lanes], qkv_ref[2, at, lanes], bias, rate
                )
                o2_ref[at, lanes] = mixed
                log_ref[0, i, f] = jnp.concatenate(logs, axis=0)

        @pl.when(pl.program_id(0) == 0)
        def _():
            x2_ref[...] = x1_ref[...]

        x2_ref[...] += nt(o2_ref[...], w_ref[0, 0])

    return call(
        body,
        (shares,),
        [
            pl.BlockSpec((3, t, width), lambda h: (0, 0, h)),
            whole(x1.shape),
            slabs(1, 7, width, d),
        ],
        [
            made((t, d), BF16, (t, width), lambda h: (0, h)),
            made((t, d), F32),
            made(
                (shares, pairs, rows.frames, 2, n),
                F32,
                (1, pairs, rows.frames, 2, n),
                lambda h: (h, 0, 0, 0, 0),
            ),
        ],
        [],
        (qkv, x1, w),
        flops=2 * t * d * d,
    )


def ff_slab(first, per_share, depth, width):
    return pl.BlockSpec(
        (1, 1, depth, width), lambda j: (first + j % per_share, j // per_share, 0, 0)
    )


def mlp_forward(rows, x2, w, gb, gb_next, me):
    t, d = x2.shape
    width = w.shape[3]
    shares = w.shape[1]
    per_share = w.shape[0] // 2
    steps = shares * per_share

    def body(x2_ref, wi_ref, wo_ref, gb_ref, me_ref, gn_ref, x3_ref, *rest):
        send_refs, a3_ref = rest[:-1], rest[-1]
        j = pl.program_id(0)

        @pl.when(j == 0)
        def _():
            a3_ref[...] = norm_rounded(x2_ref[...], gb_ref[2:3], gb_ref[5:6])
            x3_ref[...] = x2_ref[...]

        hid = nn(a3_ref[...], wi_ref[0, 0])
        act = (0.5 * hid * (1.0 + lax.erf(hid * HALF_ROOT))).astype(BF16)
        x3_ref[...] += nt(act, wo_ref[0, 0])

        @pl.when(j == steps - 1)
        def _():
            a = norm_rounded(x3_ref[...], gn_ref[0:1], gn_ref[3:4])
            for k in range(rows.ways):
                send_refs[k][...] = nn(rows.to_time(k, me_ref[3]), a).astype(BF16)

    ins = [
        whole(x2.shape),
        ff_slab(0, per_share, d, width),
        ff_slab(per_share, per_share, d, width),
        whole(gb.shape),
    ]
    ins += [SCALARS, whole(gb_next.shape)]
    outs = [made((t, d), F32)] + rows.chunks(d)
    args = (x2, w, w, gb, me, gb_next)
    return call(
        body, (steps,), ins, outs, [pltpu.VMEM((t, d), BF16)], args, flops=4 * t * d * width * steps
    )


def mlp_backward(rows, grad, x2, w, gb, me, halves, with_output):
    t, d = x2.shape
    width = w.shape[3]
    shares = w.shape[1]
    per_share = w.shape[0] // 2
    steps = shares * per_share

    def body(me_ref, g_ref, x2_ref, wi_ref, wo_ref, gb_ref, go_ref, ki_ref, si_ref, ko_ref, so_ref, sums_ref, *rest):
        if with_output:
            x3_ref, *rest = rest
        a3_ref, a3t_ref, e3_ref, e3t_ref, u_ref = rest
        j = pl.program_id(0)

        @pl.when(j == 0)
        def _():
            hat, _ = norm_parts(x2_ref[...])
            a3 = hat * gb_ref[2:3] + gb_ref[5:6]
            a3_ref[...] = a3.astype(BF16)
            store_by_core(a3t_ref, a3.T.astype(BF16), halves)
            g = g_ref[...]
            e3_ref[...] = g.astype(BF16)
            store_by_core(e3t_ref, g.T.astype(BF16), halves)
            u_ref[...] = jnp.zeros((t, d), F32)
            if with_output:
                x3_ref[...] = x2_ref[...]

        hid = nn(a3_ref[...], wi_ref[0, 0])
        phi = 0.5 * (1.0 + lax.erf(hid * HALF_ROOT))
        act = (hid * phi).astype(BF16)
        slope = phi + hid * jnp.exp(-0.5 * hid * hid) * INV_ROOT_TAU
        dhid = (nn(e3_ref[...], wo_ref[0, 0]) * slope).astype(BF16)
        split_product(e3t_ref, act, ko_ref, so_ref, (0, 0), me_ref)
        split_product(a3t_ref, dhid, ki_ref, si_ref, (0, 0), me_ref)
        u_ref[...] += nt(dhid, wi_ref[0, 0])
        if with_output:
            x3_ref[...] += nt(act, wo_ref[0, 0])

        @pl.when(j == steps - 1)
        def _():
            change, sums = norm_back(u_ref[...], x2_ref[...], gb_ref[2:3])
            go_ref[...] = g_ref[...] + change
            sums_ref[...] = sums

    slab_outs = [
        one
        for _ in range(2)
        for one in halves.array(
            (per_share, shares), (1, 1), lambda j: (j % per_share, j // per_share)
        )
    ]
    grad, ki, si, ko, so, sums, *x3 = call(
        body,
        (steps,),
        [
            SCALARS,
            whole(grad.shape),
            whole(x2.shape),
            ff_slab(0, per_share, d, width),
            ff_slab(per_share, per_share, d, width),
            whole(gb.shape),
        ],
        [made((t, d), F32), *slab_outs, made((2, d), F32)] + [made((t, d), F32)] * with_output,
        [
            pltpu.VMEM((t, d), BF16),
            halves.turned(t),
            pltpu.VMEM((t, d), BF16),
            halves.turned(t),
            pltpu.VMEM((t, d), F32),
        ],
        (me, grad, x2, w, w, gb),
        flops=10 * t * d * width * steps,
    )
    return grad, [(ki, si), (ko, so)], sums, x3


def space_backward(rows, grad, x1, qkv, o2, logs, w, gb, me, halves):
    t, d = x1.shape
    width = w.shape[3]
    shares = w.shape[1]
    pairs = width // LANES
    scale = 1.0 / math.sqrt(HEAD_DIM)
    rate = LOG2E * scale
    n = rows.frame_rows

    def body(me_ref, g_ref, x1_ref, qkv_ref, o2_ref, log_ref, wo_ref, wq_ref, gb_ref, go_ref, keep_ref, send_ref, sums_ref, e2_ref, e2t_ref, a2t_ref, do_ref, dqkv_ref, u_ref):
        h = pl.program_id(0)

        @pl.when(h == 0)
        def _():
            g = g_ref[...]
            e2_ref[...] = g.astype(BF16)
            store_by_core(e2t_ref, g.T.astype(BF16), halves)
            hat, _ = norm_parts(x1_ref[...])
            store_by_core(a2t_ref, (hat * gb_ref[1:2] + gb_ref[4:5]).T.astype(BF16), halves)
            u_ref[...] = jnp.zeros((t, d), F32)

        bias = rows.space_bias()
        split_product(e2t_ref, o2_ref[...], keep_ref, send_ref, (0, 0), me_ref)
        do_ref[...] = nn(e2_ref[...], wo_ref[0, 0]).astype(BF16)

        @pl.loop(0, pairs)
        def _(i):
            lanes = pl.ds(pl.multiple_of(i * LANES, LANES), LANES)
            for f in range(rows.frames):
                at = slice(f * n, (f + 1) * n)
                log = log_ref[0, i, f]
                grads = pair_backward(
                    qkv_ref[0, at, lanes],
                    qkv_ref[1, at, lanes],
                    qkv_ref[2, at, lanes],
                    do_ref[at, lanes],
                    (log[0:1], log[1:2]),
                    bias,
                    rate,
                    scale,
                )
                for part in range(3):
                    dqkv_ref[part, at, lanes] = grads[part]

        for part in range(3):
            split_product(a2t_ref, dqkv_ref[part], keep_ref, send_ref, (part + 1, 0), me_ref)
            u_ref[...] += nt(dqkv_ref[part], wq_ref[part, 0])

        @pl.when(h == shares - 1)
        def _():
            change, sums = norm_back(u_ref[...], x1_ref[...], gb_ref[1:2])
            go_ref[...] = g_ref[...] + change
            sums_ref[...] = sums

    grad, keep, send, sums = call(
        body,
        (shares,),
        [
            SCALARS,
            whole(grad.shape),
            whole(x1.shape),
            pl.BlockSpec((3, t, width), lambda h: (0, 0, h)),
            pl.BlockSpec((t, width), lambda h: (0, h)),
            pl.BlockSpec((1,) + logs.shape[1:], lambda h: (h, 0, 0, 0, 0)),
            slabs(1, 7, width, d),
            slabs(3, 3, width, d),
            whole(gb.shape),
        ],
        [
            made((t, d), F32),
            *halves.array((4, shares), (4, 1), lambda h: (0, h)),
            made((2, d), F32),
        ],
        [
            pltpu.VMEM((t, d), BF16),
            halves.turned(t),
            halves.turned(t),
            pltpu.VMEM((t, width), BF16),
            pltpu.VMEM((3, t, width), BF16),
            pltpu.VMEM((t, d), F32),
        ],
        (me, grad, x1, qkv, o2, logs, w, w, gb),
        flops=2 * t * d * d * 8,
    )
    return grad, (keep, send), sums


def mix_fits(depth, shards, shares):
    return depth // (shards * shares) % 8 == 0


def middle_backward(rows, grad, y1, o1, w, mix, me, halves, shards):
    t, d = grad.shape
    width = w.shape[3]
    shares = w.shape[1]
    fits = mix_fits(d, shards, shares)
    part = d // (shards * shares)

    def body(me_ref, g_ref, y1_ref, o1_ref, to_ref, mix_ref, *rest):
        send_refs, rest = rest[: rows.ways], rest[rows.ways :]
        gk_ref, gs_ref, *rest = rest
        if fits:
            room_ref, order_ref = rest
        else:
            gm_ref, room_ref = rest
        e1 = g_ref[...].astype(BF16)
        dy1 = nt(e1, mix_ref[...]).astype(BF16)
        sends = [rows.to_time(k, me_ref[3]) for k in range(rows.ways)]
        for h in range(shares):
            lanes = slice(h * width, (h + 1) * width)
            do1 = nn(dy1, to_ref[0, h]).astype(BF16)
            for k in range(rows.ways):
                send_refs[k][:, lanes] = nn(sends[k], do1).astype(BF16)
            split_rows(tn(dy1, o1_ref[:, lanes]), gk_ref, gs_ref, (0, h), room_ref, me_ref)
        gm = tn(y1_ref[...], e1)
        if fits:
            gm = gm.reshape(shards, shares, part, d)
            for h in range(shares):
                for half in range(shares):
                    order_ref[:, half] = gm[:, h, :, half * width : (half + 1) * width]
                split_rows(order_ref[...], gk_ref, gs_ref, (1, h), room_ref, me_ref)
        else:
            gm_ref[...] = gm.astype(BF16)

    outs = rows.chunks(d)
    outs += halves.array((1 + fits, shares), (1 + fits, shares), lambda i: (0, 0))
    scratch = [halves.room()]
    if fits:
        scratch.append(pltpu.VMEM((shards, shares, part, width), F32))
    else:
        outs.append(made((d, d), BF16))
    got = call(
        body,
        (1,),
        [
            SCALARS,
            whole(grad.shape),
            whole(y1.shape),
            whole(o1.shape),
            pl.BlockSpec((1, shares, d, width), lambda i: (6, 0, 0, 0)),
            whole(mix.shape),
        ],
        outs,
        scratch,
        (me, grad, y1, o1, w, mix),
        flops=8 * t * d * d,
    )
    do1, (keep, send) = got[: rows.ways], got[rows.ways : rows.ways + 2]
    if not fits:
        gm = mix_slab(got[-1], shards, shares).reshape((1, shares, halves.pairs, 2) + keep.shape[3:])
        keep = jnp.concatenate((keep, lax.dynamic_index_in_dim(gm, me[0], 3, keepdims=False)), axis=0)
        send = jnp.concatenate((send, lax.dynamic_index_in_dim(gm, 1 - me[0], 3, keepdims=False)), axis=0)
    return do1, (keep, send)


def time_backward(rows, do1, a, qkv, logs, w, me, halves):
    t, d = a.shape
    width = w.shape[3]
    shares = w.shape[1]
    pairs = width // LANES
    scale = 1.0 / math.sqrt(HEAD_DIM)
    rate = LOG2E * scale

    def body(me_ref, *refs):
        do_refs, refs = refs[: rows.ways], refs[rows.ways :]
        a_ref, qkv_ref, log_ref, w_ref = refs[:4]
        out_refs, refs = refs[4 : 4 + rows.ways], refs[4 + rows.ways :]
        half_refs, refs = refs[:6], refs[6:]
        bias_ref, dqkv_ref, at_ref, u_ref, do_ref = refs
        h = pl.program_id(0)

        @pl.when(h == 0)
        def _():
            bias_ref[...] = rows.time_bias()
            store_by_core(at_ref, a_ref[...].T, halves)
            u_ref[...] = jnp.zeros((t, d), F32)

        for k in range(rows.ways):
            do_ref[k * rows.chunk : (k + 1) * rows.chunk] = do_refs[k][...]

        @pl.loop(0, pairs)
        def _(i):
            lanes = pl.ds(pl.multiple_of(i * LANES, LANES), LANES)
            log = log_ref[0, i]
            grads = pair_backward(
                qkv_ref[0, :, lanes],
                qkv_ref[1, :, lanes],
                qkv_ref[2, :, lanes],
                do_ref[:, lanes],
                (log[0:1], log[1:2]),
                bias_ref[...],
                rate,
                scale,
            )
            for part in range(3):
                dqkv_ref[part, :, lanes] = grads[part]

        for part in range(3):
            split_product(
                at_ref, dqkv_ref[part], half_refs[2 * part], half_refs[2 * part + 1], (0, 0), me_ref
            )
            u_ref[...] += nt(dqkv_ref[part], w_ref[part, 0])

        @pl.when(h == shares - 1)
        def _():
            for k in range(rows.ways):
                out_refs[k][...] = u_ref[k * rows.chunk : (k + 1) * rows.chunk].astype(BF16)

    got = call(
        body,
        (shares,),
        [
            SCALARS,
            *(pl.BlockSpec((rows.chunk, width), lambda h: (0, h)) for _ in do1),
            whole(a.shape),
            pl.BlockSpec((3, t, width), lambda h: (0, 0, h)),
            pl.BlockSpec((1,) + logs.shape[1:], lambda h: (h, 0, 0, 0)),
            slabs(3, 0, width, d),
        ],
        [
            *rows.chunks(d),
            *(one for _ in range(3) for one in halves.array((1, shares), (1, 1), lambda h: (0, h))),
        ],
        [
            pltpu.VMEM((t, t), F32),
            pltpu.VMEM((3, t, width), BF16),
            halves.turned(t),
            pltpu.VMEM((t, d), F32),
            pltpu.VMEM((t, width), BF16),
        ],
        (me, *do1, a, qkv, logs, w),
        flops=2 * t * d * d * 6,
    )
    parts = got[rows.ways :]
    return got[: rows.ways], [tuple(parts[i : i + 2]) for i in (0, 2, 4)]


def first_norm_back(rows, back, x, grad, gb, me):
    t, d = x.shape

    def body(me_ref, *refs):
        x_ref, g_ref, gb_ref, go_ref, sums_ref = refs[rows.ways :]
        u = rows.gathered(refs[: rows.ways], me_ref[3])
        change, sums = norm_back(u, x_ref[...], gb_ref[0:1])
        go_ref[...] = g_ref[...] + change
        sums_ref[...] = sums

    return call(
        body,
        (1,),
        [SCALARS, *(whole(c.shape) for c in back), whole(x.shape), whole(grad.shape), whole(gb.shape)],
        [made((t, d), F32), made((2, d), F32)],
        [],
        (me, *back, x, grad, gb),
    )


def homes():
    clips, ways = lax.axis_size("clip"), lax.axis_size("seq")
    pairs = []
    for clip in range(clips):
        for seq in range(ways):
            home_clip = clip - clip % 2 + seq % 2
            home_seq = seq // 2 + (ways // 2) * (clip % 2)
            pairs.append((clip * ways + seq, home_clip * ways + home_seq))
    return pairs


def go_home(a):
    return lax.ppermute(a, ("clip", "seq"), homes())


def go_back(a):
    return lax.ppermute(a, ("clip", "seq"), [(home, device) for device, home in homes()])


def member_of(clip, seq):
    return clip % 2 + 2 * (seq % (lax.axis_size("seq") // 2))


def swap_places(chunks):
    clips, ways = lax.axis_size("clip"), lax.axis_size("seq")
    got = [chunks[0]]
    for k in range(1, ways):
        pairs = []
        for clip in range(clips):
            for seq in range(ways):
                other = member_of(clip, seq) ^ k
                to_clip = clip - clip % 2 + other % 2
                to_seq = seq - seq % (ways // 2) + other // 2
                pairs.append((clip * ways + seq, to_clip * ways + to_seq))
        got.append(lax.ppermute(chunks[k], ("clip", "seq"), pairs))
    return got


def columns(a, r, width):
    return a.reshape(r, -1, width).transpose(1, 0, 2)


def pack_attention(time_qkv, time_out, time_mix, space_qkv, space_out):
    r, _, width = time_qkv.shape
    mix = time_mix.reshape(-1, time_mix.shape[1] // width, width).transpose(1, 0, 2).reshape(1, r, width)
    return jnp.concatenate(
        (
            columns(time_qkv, r, width),
            columns(space_qkv, r, width),
            time_out.T[None],
            space_out.T[None],
            mix,
        ),
        axis=0,
    )


def pack_feed_forward(mlp_in, mlp_out, width):
    r = mlp_in.shape[0]
    return jnp.concatenate((columns(mlp_in, r, width), columns(mlp_out.T, r, width)), axis=0)


def gather_slabs(pack):
    full = lax.all_gather(pack, ("head", "clip", "seq"), axis=1, tiled=True)
    return full.reshape(pack.shape[0], lax.axis_size("head"), -1, pack.shape[2])


def spread_steps(pack, me):
    ways, clips = lax.axis_size("seq"), lax.axis_size("clip")
    shares = lax.axis_size("head")
    n, r, width = pack.shape
    pack = yield pack
    turned = [pack] + [
        lax.ppermute(pack, "seq", [(i, (i + k) % ways) for i in range(ways)]) for k in range(1, ways)
    ]
    turned = yield turned
    orders = (((0, 1), "x", "h"), ((3, 2), "h", "x"))
    some = [jnp.stack([turned[k] for k in steps]) for steps, _, _ in orders]
    come = yield [cross(a, first) for a, (_, first, _) in zip(some, orders)]
    some = [jnp.concatenate(pair, axis=0) for pair in zip(some, come)]
    come = yield [cross(a, second) for a, (_, _, second) in zip(some, orders)]
    runs = []
    for mine, other, (steps, first, second) in zip(some, come, orders):
        where = [(k, {first: f}) for f in (0, 1) for k in steps]
        for g, blocks in enumerate((mine, other)):
            runs.append((blocks, [(k, {**at, second: g}) for k, at in where], 0))
    come = yield [cross(blocks, "c") for blocks, _, _ in runs]
    runs += [(far, where, 1) for far, (_, where, _) in zip(come, runs)]
    count = sum(len(where) for _, where, _ in runs)

    def body(me_ref, *refs):
        sources, out_ref, sems = refs[: len(runs)], refs[-2], refs[-1]
        copies = []
        for source, (_, where, core) in zip(sources, runs):
            for i, (k, at) in enumerate(where):
                share = jnp.bitwise_xor(me_ref[2], at["h"])
                clip = 2 * jnp.bitwise_xor(me_ref[1], at["x"]) + jnp.bitwise_xor(me_ref[0], core)
                seq = lax.rem(me_ref[4] + (ways - k), ways)
                copies.append(
                    pltpu.make_async_copy(
                        source.at[i], out_ref.at[:, share, clip * ways + seq], sems.at[len(copies)]
                    )
                )
        for copy in copies:
            copy.start()
        for copy in copies:
            copy.wait()

    full = pl.pallas_call(
        body,
        out_shape=jax.ShapeDtypeStruct((n, shares, clips * ways, r, width), BF16),
        in_specs=[SCALARS] + [pl.BlockSpec(memory_space=pltpu.HBM)] * len(runs),
        out_specs=pl.BlockSpec(memory_space=pltpu.VMEM),
        scratch_shapes=[pltpu.SemaphoreType.DMA((count,))],
        compiler_params=pltpu.CompilerParams(vmem_limit_bytes=VMEM),
        cost_estimate=pl.CostEstimate(
            flops=0, bytes_accessed=4 * n * shares * clips * ways * r * width, transcendentals=0
        ),
    )(me, *(blocks for blocks, _, _ in runs))
    yield full.reshape(n, shares, clips * ways * r, width)


class Spread:
    def __init__(self, pack, me):
        self.way = spread_steps(pack, me)
        self.come = next(self.way)

    def hold(self, x):
        x, self.come = lax.optimization_barrier((x, self.come))
        return x

    def step(self, x):
        x = self.hold(x)
        self.come = self.way.send(self.come)
        return x


def mix_whole(slab, shards):
    shares, depth, width = slab.shape
    part = slab.reshape(shares, shards, shares, depth // (shards * shares), width)
    return part.transpose(1, 0, 3, 2, 4).reshape(depth, shares * width)


def mix_slab(whole_grad, shards, shares):
    depth, full = whole_grad.shape
    width = full // shares
    part = whole_grad.reshape(shards, shares, depth // (shards * shares), shares, width)
    return part.transpose(1, 0, 3, 2, 4).reshape(1, shares, depth, width)


class Piece:
    def __init__(self, keep, got, first, n, order):
        self.near = (keep, got)
        self.first = first
        self.n = n
        self.order = order
        self.step = 0
        self.held = []
        self.result = None


PLACE = {"x": 1, "h": 2}


def fold(pieces, me, last_by_rows):
    ways = lax.axis_size("seq")
    depth, width = pieces[0].near[0].shape[-2:]
    r = depth // ways
    used = {}
    arrays = []

    def number(a):
        for i, known in enumerate(arrays):
            if known is a:
                return i
        arrays.append(a)
        return len(arrays) - 1

    plans = []
    for p in pieces:
        link = p.order[p.step] if p.step < 2 else "z"
        blocks = p.n * (2 if p.step == 0 else 1)
        base = used.get(link, 0)
        used[link] = base + blocks
        near = [number(a) for a in p.near]
        held = [(number(a), at) for a, at in p.held]
        plans.append((p, link, base, near, held))
    links = sorted(used)
    shapes = [
        (ways, used[k], r, width) if k == "z" and last_by_rows else (used[k], depth, width)
        for k in links
    ]
    rooms, counts = [], []
    for p, link, base, near, held in plans:
        each = 2 if p.step == 0 else 1
        counts.append((each, len(near) + len(held)))
        rooms += [(each * p.n, depth, width)] * (len(near) + len(held))
    copies_needed = sum(each * terms for each, terms in counts)

    def body(me_ref, *refs):
        sources = refs[: len(arrays)]
        outs = dict(zip(links, refs[len(arrays) : len(arrays) + len(links)]))
        held_refs = refs[len(arrays) + len(links) : -1]
        sems = refs[-1]
        mine = {name: me_ref[PLACE[name]] for name in PLACE}
        groups = []
        room = 0
        sem = 0
        for p, link, base, near, held in plans:
            group = []
            if p.step == 0:
                for term in near:
                    for k in range(2):
                        pick = {p.order[0]: 1 - mine[p.order[0]], p.order[1]: k}
                        source = sources[term].at[pl.ds(p.first, p.n), pick["h"], pick["x"]]
                        group.append((source, held_refs[room].at[pl.ds(k * p.n, p.n)]))
                    room += 1
            else:
                last = p.order[1]
                pick = {p.order[0]: mine[p.order[0]]}
                pick[last] = 1 - mine[last] if p.step == 1 else mine[last]
                for term in near:
                    source = sources[term].at[pl.ds(p.first, p.n), pick["h"], pick["x"]]
                    group.append((source, held_refs[room]))
                    room += 1
                for i, (term, at) in enumerate(held):
                    start = at + pick[last] * p.n if i == 0 else at
                    group.append((sources[term].at[pl.ds(start, p.n)], held_refs[room]))
                    room += 1
            made_copies = []
            for source, target in group:
                made_copies.append(pltpu.make_async_copy(source, target, sems.at[sem]))
                sem += 1
            groups.append(made_copies)
        for group in groups:
            for copy in group:
                copy.start()
        room = 0
        for (p, link, base, near, held), (each, terms), group in zip(plans, counts, groups):
            these = held_refs[room : room + terms]
            room += terms
            for copy in group:
                copy.wait()

            @pl.loop(0, each * p.n)
            def _(i, these=these, base=base, out=outs[link], last=p.step == 2 and last_by_rows):
                value = these[0][i].astype(F32)
                for one in these[1:]:
                    value = value + one[i].astype(F32)
                value = value.astype(BF16)
                if last:
                    for k in range(ways):
                        out[k, base + i] = value[k * r : (k + 1) * r]
                else:
                    out[base + i] = value

    moved = sum(2 * math.prod(room) for room in rooms) + sum(2 * math.prod(shape) for shape in shapes)
    sums = pl.pallas_call(
        body,
        out_shape=[jax.ShapeDtypeStruct(shape, BF16) for shape in shapes],
        in_specs=[SCALARS] + [pl.BlockSpec(memory_space=pltpu.HBM)] * len(arrays),
        out_specs=[pl.BlockSpec(memory_space=pltpu.VMEM)] * len(links),
        scratch_shapes=[pltpu.VMEM(room, BF16) for room in rooms]
        + [pltpu.SemaphoreType.DMA((copies_needed,))],
        compiler_params=pltpu.CompilerParams(vmem_limit_bytes=VMEM),
        cost_estimate=pl.CostEstimate(flops=0, bytes_accessed=moved, transcendentals=0),
    )(me, *arrays)
    return [(p, link, base) for p, link, base, _, _ in plans], dict(zip(links, sums))


def cross(a, name):
    axis, bit = ("head", 0) if name == "h" else ("clip", 1 if name == "x" else 0)
    size = lax.axis_size(axis)
    return lax.ppermute(a, axis, [(i, i ^ (1 << bit)) for i in range(size)])


def pieces_of(halves_of):
    total = sum(keep.shape[0] for keep, _ in halves_of)
    found = []
    seen = 0
    for keep, send in halves_of:
        got = cross(send, "c")
        n = keep.shape[0]
        first = min(max((total + 1) // 2 - seen, 0), n)
        if first:
            found.append(Piece(keep, got, 0, first, ("x", "h")))
        if n > first:
            found.append(Piece(keep, got, first, n - first, ("h", "x")))
        seen += n
    return found


def move(x, pieces, me, at_end=False):
    plans, sums = fold(pieces, me, at_end)
    x, sums = lax.optimization_barrier((x, sums))
    got = {}
    for link, array in sums.items():
        if link == "z":
            if at_end:
                every = lax.all_to_all(array, "seq", split_axis=0, concat_axis=0, tiled=True)
                got[link] = jnp.sum(every.astype(F32), axis=0)
            else:
                own = lax.psum_scatter(array, "seq", scatter_dimension=1, tiled=True)
                got[link] = own.astype(F32)
        else:
            got[link] = cross(array, link)
    for p, link, base in plans:
        if link == "z":
            p.result = got[link][base : base + p.n]
        else:
            p.held.append((got[link], base))
        p.step += 1
    return x


def settle(x, pieces):
    arrays = []
    for p in pieces:
        if not any(p.held[-1][0] is a for a in arrays):
            arrays.append(p.held[-1][0])
    x, came = lax.optimization_barrier((x, arrays))
    for p in pieces:
        for old, new in zip(arrays, came):
            if p.held[-1][0] is old:
                p.held[-1] = (new, p.held[-1][1])
                break
    return x


def reduce_plain(halves_of, core):
    def joined(keep, send):
        low = jnp.where(core == 0, keep, send)
        high = jnp.where(core == 0, send, keep)
        n, shares, pairs, depth, width = keep.shape
        return jnp.stack((low, high), axis=3).reshape(n, shares, 2 * pairs * depth, width)

    g = jnp.concatenate([joined(*pair) for pair in halves_of], axis=0)
    g = lax.psum_scatter(g, "head", scatter_dimension=1, tiled=True)
    g = lax.psum_scatter(g.astype(F32), ("clip", "seq"), scatter_dimension=2, tiled=True)
    return g[:, 0]


def gather_norms(gain, bias):
    layers, norms, part = gain.shape
    both = jnp.concatenate((gain, bias), axis=1).reshape(1, -1)
    count = lax.axis_size("clip") * lax.axis_size("seq") * lax.axis_size("head")
    width = round_up(both.shape[1], 128)
    padded = jnp.pad(both, ((0, 0), (0, width - both.shape[1])))
    every = lax.all_to_all(
        jnp.broadcast_to(padded, (count, width)), ALL, split_axis=0, concat_axis=0, tiled=True
    )[:, : both.shape[1]]
    return every.reshape(count, layers * 2 * norms, part).transpose(1, 0, 2).reshape(layers, 2 * norms, -1)


def reduce_norms(sums):
    count = lax.axis_size("clip") * lax.axis_size("seq") * lax.axis_size("head")
    rows, features = sums.shape
    part = features // count
    a = sums.reshape(rows, count, part).transpose(1, 0, 2).reshape(count, rows * part)
    width = round_up(rows * part, 128)
    a = jnp.pad(a, ((0, 0), (0, width - rows * part)))
    every = lax.all_to_all(a, ALL, split_axis=0, concat_axis=0, tiled=True)
    return jnp.sum(every, axis=0)[: rows * part].reshape(rows, part)


def on_device(
    tokens,
    cotangent,
    time_qkv,
    time_out,
    time_mix,
    space_qkv,
    space_out,
    mlp_in,
    mlp_out,
    norm_gain,
    norm_bias,
):
    layers = time_qkv.shape[0]
    clips, frames, places, d = tokens.shape
    ways = lax.axis_size("seq")
    shards = lax.axis_size("clip") * ways
    rows = Rows(clips * frames, places, ways)
    shares = lax.axis_size("head")

    def as_rows(a):
        a = a.astype(F32).reshape(rows.frames, places, d)
        a = jnp.pad(a, ((0, 0), (0, rows.frame_rows - places), (0, 0)))
        return a.reshape(rows.rows, d)

    def from_rows(a):
        a = a.reshape(rows.frames, rows.frame_rows, d)[:, :places]
        return a.reshape(tokens.shape)

    gbs = gather_norms(norm_gain, norm_bias)
    gb = [gbs[l] for l in range(layers)]
    packs = [
        pack_attention(time_qkv[l], time_out[l], time_mix[l], space_qkv[l], space_out[l])
        for l in range(layers)
    ]
    packs_ff = [pack_feed_forward(mlp_in[l], mlp_out[l], time_qkv.shape[3]) for l in range(layers)]
    weights = [gather_slabs(pack) for pack in packs]
    mixes = [mix_whole(w[-1], shards) for w in weights]
    quick = lax.axis_size("clip") == 4 and shares == 2 and ways == 4 and time_qkv.shape[1] % 16 == 0

    halves = Halves(lax.axis_size("clip"), d, time_qkv.shape[3])
    clip = lax.axis_index("clip")
    member = member_of(clip, lax.axis_index("seq"))
    me = jnp.stack((clip & 1, (clip >> 1) & 1, lax.axis_index("head"), member, lax.axis_index("seq"))).astype(
        jnp.int32
    )
    if quick:
        spreads = [Spread(pack, me) for pack in packs_ff]
        weights_ff = []
    else:
        weights_ff = [gather_slabs(pack) for pack in packs_ff]

    home = go_home(tokens)
    if quick:
        first = spreads[0]
        home, gb = first.step((home, gb))
    x = as_rows(home)
    send = send_first(rows, x, gb[0], me)
    kept = []
    for l in range(layers):
        w = weights[l]
        send = swap_places(send)
        if quick and l == 0:
            for _ in range(2):
                send = first.step(send)
            for spread in spreads[1:]:
                send = spread.step(send)
                send = spread.hold(send)
            send = first.step(send)
        elif quick:
            send = spreads[l].step(send)
        a1, qkv1, log1, o1_time = time_forward(rows, send, w)
        back = swap_places(o1_time)
        if quick:
            back = spreads[l].step(back)
            weights_ff.append(spreads[l].come)
            if l == 0:
                for spread in spreads[1:]:
                    back = spread.step(back)
        o1, y1, x1, qkv2 = middle_forward(rows, back, x, w, mixes[l], gb[l], me)
        o2, x2, log2 = space_forward(rows, qkv2, x1, w)
        if quick and l == 0:
            for spread in spreads[1:]:
                x2 = spread.step(x2)
        kept.append((x, a1, qkv1, log1, o1, y1, x1, qkv2, o2, log2, x2))
        if l + 1 < layers:
            x, *send = mlp_forward(rows, x2, weights_ff[l], gb[l], gb[l + 1], me)

    grad = as_rows(go_home(cotangent))
    norm_rows = [None] * layers
    summed = [None] * layers
    late = []
    for l in reversed(range(layers)):
        w = weights[l]
        x, a1, qkv1, log1, o1, y1, x1, qkv2, o2, log2, x2 = kept[l]
        grad, g_ff, s3, x3 = mlp_backward(
            rows, grad, x2, weights_ff[l], gb[l], me, halves, l + 1 == layers
        )
        if x3:
            output = go_back(from_rows(x3[0].astype(BF16)))
        if quick:
            ff = pieces_of(g_ff)
            if late:
                grad = settle(grad, late)
                grad = move(grad, late, me)
                late = [p for p in late if p.step < 3]
        grad, g_space, s2 = space_backward(rows, grad, x1, qkv2, o2, log2, w, gb[l], me, halves)
        if quick:
            space = pieces_of([g_space])
            if late:
                grad = settle(grad, late)
            grad, output = move((grad, output), ff, me)
        do1, g_out = middle_backward(rows, grad, y1, o1, w, mixes[l], me, halves, shards)
        do1 = swap_places(do1)
        if quick:
            do1 = move(do1, ff + space + late, me)
        da1, g_time = time_backward(rows, do1, a1, qkv1, log1, w, me, halves)
        if quick:
            da1 = settle(da1, ff + space)
        da1 = swap_places(da1)
        if quick:
            rest = pieces_of([g_out] + g_time)
            da1 = move(da1, ff + space + rest, me)
            late = space + rest
        grad, s1 = first_norm_back(rows, da1, x, grad, gb[l], me)
        norm_rows[l] = jnp.concatenate((s1[0:1], s2[0:1], s3[0:1], s1[1:2], s2[1:2], s3[1:2]), axis=0)
        if quick:
            summed[l] = ff + space + rest
        else:
            summed[l] = [reduce_plain(g_ff + [g_space, g_out] + g_time, clip & 1)]
    norm_sums = reduce_norms(jnp.concatenate(norm_rows, axis=0)).reshape(layers, 2, 3, -1)
    if quick:
        tokens_grad = go_back(from_rows(grad.astype(BF16)))
        tokens_grad = move(tokens_grad, late, me, True)
        norm_sums = move(norm_sums, rest, me, True)
        summed = [[p.result for p in some] for some in summed]
    cuts = (2 * g_ff[0][0].shape[0], g_space[0].shape[0], g_out[0].shape[0], len(g_time))
    results = []
    for some in summed:
        slabs_of = jnp.concatenate(some, axis=0)
        ends = [sum(cuts[: i + 1]) for i in range(4)]
        results.append([slabs_of[e - c : e] for c, e in zip(cuts, ends)])
    if not quick:
        tokens_grad = go_back(from_rows(grad.astype(BF16)))
    tokens_grad = tokens_grad.astype(F32)

    def stacked(form):
        return jnp.stack([form(*results[l]) for l in range(layers)])

    def rows_of(a):
        return a.transpose(1, 0, 2)

    def flat(a):
        return rows_of(a).reshape(a.shape[1], -1)

    def mix_rows(a):
        r, width = a.shape
        return a.reshape(shares, r // shares, width).transpose(1, 0, 2).reshape(r // shares, -1)

    per_share = mlp_in.shape[2] // time_qkv.shape[3]
    return (
        output,
        tokens_grad,
        stacked(lambda ff, s, t, q: rows_of(q)),
        stacked(lambda ff, s, t, q: t[0].T),
        stacked(lambda ff, s, t, q: mix_rows(t[1])),
        stacked(lambda ff, s, t, q: rows_of(s[1:])),
        stacked(lambda ff, s, t, q: s[0].T),
        stacked(lambda ff, s, t, q: flat(ff[:per_share])),
        stacked(lambda ff, s, t, q: flat(ff[per_share:]).T),
        norm_sums[:, 0],
        norm_sums[:, 1],
    )


def solution(mesh):
    token_spec = P(("clip", "head"), "seq", None, None)
    in_specs = (
        token_spec,
        token_spec,
        P(None, ("clip", "seq"), None, "head"),
        P(None, "head", ("clip", "seq")),
        P(None, ("clip", "seq", "head"), None),
        P(None, ("clip", "seq"), None, "head"),
        P(None, "head", ("clip", "seq")),
        P(None, ("clip", "seq"), "head"),
        P(None, "head", ("clip", "seq")),
        P(None, None, ("clip", "seq", "head")),
        P(None, None, ("clip", "seq", "head")),
    )
    return jax.shard_map(
        on_device, mesh=mesh, in_specs=in_specs, out_specs=in_specs, check_vma=False
    )
```

```python
import functools
import math

import jax
import jax.numpy as jnp
from jax import lax
from jax.experimental import pallas as pl
from jax.experimental.pallas import tpu as pltpu
from jax.sharding import PartitionSpec as P

HEAD_DIM = 64
NORM_EPS = 1e-06
HALF_ROOT = 0.7071067811865476
INV_ROOT_TAU = 0.3989422804014327
LOG2E = 1.4426950408889634
FAR = -1e30
LANES = 128
VMEM = 56 * 1024 * 1024
SHOWN = 1.0
ALL = ("clip", "seq", "head")
BF16 = jnp.bfloat16
F32 = jnp.float32


def round_up(value, step):
    return -(-value // step) * step


def nn(a, b):
    return lax.dot_general(a, b, (((1,), (0,)), ((), ())), preferred_element_type=F32)


def nt(a, b):
    return lax.dot_general(a, b, (((1,), (1,)), ((), ())), preferred_element_type=F32)


def tn(a, b):
    return lax.dot_general(a, b, (((0,), (0,)), ((), ())), preferred_element_type=F32)


def norm_parts(x):
    mean = jnp.mean(x, axis=-1, keepdims=True)
    centred = x - mean
    spread = lax.rsqrt(jnp.mean(centred * centred, axis=-1, keepdims=True) + NORM_EPS)
    return centred * spread, spread


def norm_rounded(x, gain, bias):
    hat, _ = norm_parts(x)
    return (hat * gain + bias).astype(BF16)


def norm_back(u, x, gain):
    hat, spread = norm_parts(x)
    scaled = u * gain
    mean_scaled = jnp.mean(scaled, axis=-1, keepdims=True)
    mean_cross = jnp.mean(scaled * hat, axis=-1, keepdims=True)
    change = spread * (scaled - mean_scaled - hat * mean_cross)
    sums = jnp.concatenate(
        (jnp.sum(u * hat, axis=0, keepdims=True), jnp.sum(u, axis=0, keepdims=True)), axis=0
    )
    return change, sums


class Rows:
    def __init__(self, frames, places, ways):
        self.frames = frames
        self.places = places
        self.ways = ways
        self.frame_rows = round_up(places, 16)
        self.rows = frames * self.frame_rows
        self.block = places // ways
        self.chunk = round_up(frames * self.block, 8)
        self.time_rows = ways * self.chunk

    def split(self, r):
        way = jnp.zeros_like(r)
        for k in range(1, self.ways):
            way = way + (r >= k * self.chunk).astype(jnp.int32)
        rest = r - way * self.chunk
        frame = jnp.zeros_like(r)
        for k in range(1, self.frames):
            frame = frame + (rest >= k * self.block).astype(jnp.int32)
        real = rest < self.frames * self.block
        return way, frame, rest - frame * self.block, real

    def to_time(self, k, member):
        r = lax.broadcasted_iota(jnp.int32, (self.chunk, 1), 0)
        _, frame, place, real = self.split(r)
        way = jnp.bitwise_xor(member, k)
        source = jnp.where(real, frame * self.frame_rows + way * self.block + place, -1)
        c = lax.broadcasted_iota(jnp.int32, (self.chunk, self.rows), 1)
        return jnp.where(c == source, 1.0, 0.0).astype(BF16)

    def gathered(self, chunk_refs, member):
        total = tn(self.to_time(0, member), chunk_refs[0][...])
        for k in range(1, self.ways):
            total = total + tn(self.to_time(k, member), chunk_refs[k][...])
        return total

    def chunks(self, width, block=None, index=None):
        return [
            made((self.chunk, width), BF16)
            if block is None
            else made((self.chunk, width), BF16, (self.chunk, block), index)
            for _ in range(self.ways)
        ]

    def time_bias(self):
        def label(r):
            _, _, place, real = self.split(r)
            return jnp.where(real, place, -1)

        a = label(lax.broadcasted_iota(jnp.int32, (self.time_rows, 1), 0))
        b = label(lax.broadcasted_iota(jnp.int32, (1, self.time_rows), 1))
        return jnp.where(a == b, 0.0, FAR).astype(F32)

    def space_bias(self):
        a = lax.broadcasted_iota(jnp.int32, (self.frame_rows, 1), 0)
        return jnp.where(a < self.places, 0.0, FAR).astype(F32)


def lane_masks(rows):
    lane = lax.broadcasted_iota(jnp.int32, (rows, LANES), 1)
    return lane < HEAD_DIM


def one_of(value, low, half):
    zero = jnp.zeros_like(value)
    return jnp.where(low, value, zero) if half == 0 else jnp.where(low, zero, value)


def pair_forward(q, k, v, bias, rate):
    low = lane_masks(q.shape[0])
    mixed, logs = [], []
    for half in range(2):
        s = nt(k, one_of(q, low, half)) + bias
        peak = jnp.max(s, axis=0, keepdims=True)
        e = jnp.exp2((s - peak) * rate)
        total = jnp.sum(e, axis=0, keepdims=True)
        soft = (e * (1.0 / total)).astype(BF16)
        mixed.append(tn(soft, v))
        logs.append(peak * rate + jnp.log2(total))
    return jnp.where(low, mixed[0], mixed[1]).astype(BF16), logs


def pair_backward(q, k, v, do, logs, bias, rate, scale):
    low = lane_masks(q.shape[0])
    dq, dk, dv = [], [], []
    for half in range(2):
        s = nt(k, one_of(q, low, half)) + bias
        soft = jnp.exp2(s * rate - logs[half])
        dp = nt(v, one_of(do, low, half))
        ds = (soft * (dp - jnp.sum(soft * dp, axis=0, keepdims=True))).astype(BF16)
        dv.append(nn(soft.astype(BF16), do))
        dk.append(nn(ds, q))
        dq.append(tn(ds, k))
    return (
        (jnp.where(low, dq[0], dq[1]) * scale).astype(BF16),
        (jnp.where(low, dk[0], dk[1]) * scale).astype(BF16),
        jnp.where(low, dv[0], dv[1]).astype(BF16),
    )


def split_rows(value, keep_ref, send_ref, at, room_ref, me_ref):
    mine = me_ref[0]
    room_ref[...] = value.reshape(room_ref.shape)
    keep_ref[at] = room_ref[:, mine].astype(BF16)
    send_ref[at] = room_ref[:, 1 - mine].astype(BF16)


def store_by_core(ref, value, halves):
    n = halves.rows
    for core in range(2):
        for pair in range(halves.pairs):
            first = (2 * pair + core) * n
            ref[core, pair * n : (pair + 1) * n] = value[first : first + n]


def split_product(left_ref, right, keep_ref, send_ref, at, me_ref):
    mine = me_ref[0]
    shape = keep_ref.shape[len(at) :]
    keep_ref[at] = nn(left_ref[mine], right).reshape(shape).astype(BF16)
    send_ref[at] = nn(left_ref[1 - mine], right).reshape(shape).astype(BF16)


class Halves:
    def __init__(self, clips, depth, width):
        self.pairs = clips // 2
        self.rows = depth // clips
        self.width = width

    def array(self, lead, block, index):
        tail = (self.pairs, self.rows, self.width)
        one = lambda: made(lead + tail, BF16, block + tail, lambda *g: index(*g) + (0, 0, 0))
        return [one(), one()]

    def turned(self, columns):
        return pltpu.VMEM((2, self.pairs * self.rows, columns), BF16)

    def room(self):
        return pltpu.VMEM((self.pairs, 2, self.rows, self.width), F32)


SCALARS = pl.BlockSpec(memory_space=pltpu.SMEM)


def call(body, grid, ins, outs, scratch, args, flops=0):
    specs = [spec for spec in ins]
    moved = sum(math.prod(o.shape) * o.dtype.itemsize for o, _ in outs)
    moved += sum(math.prod(a.shape) * a.dtype.itemsize for a in args)
    return pl.pallas_call(
        body,
        out_shape=[shape for shape, _ in outs],
        grid=grid,
        in_specs=specs,
        out_specs=[spec for _, spec in outs],
        scratch_shapes=scratch,
        compiler_params=pltpu.CompilerParams(vmem_limit_bytes=VMEM),
        cost_estimate=pl.CostEstimate(
            flops=int(flops * SHOWN), bytes_accessed=int(moved * SHOWN), transcendentals=0
        ),
    )(*args)


def whole(shape):
    zeros = (0,) * len(shape)
    return pl.BlockSpec(shape, lambda *_: zeros)


def made(shape, dtype, block=None, index=None):
    spec = whole(shape) if block is None else pl.BlockSpec(block, index)
    return jax.ShapeDtypeStruct(shape, dtype), spec


def slabs(count, first, width, depth):
    return pl.BlockSpec((count, 1, depth, width), lambda h, *_: (first // count, h, 0, 0))


def send_first(rows, x, gb, me):
    def body(me_ref, x_ref, gb_ref, *out_refs):
        a = norm_rounded(x_ref[...], gb_ref[0:1], gb_ref[3:4])
        for k in range(rows.ways):
            out_refs[k][...] = nn(rows.to_time(k, me_ref[3]), a).astype(BF16)

    d = x.shape[1]
    return call(
        body, (1,), [SCALARS, whole(x.shape), whole(gb.shape)], rows.chunks(d), [], (me, x, gb)
    )


def time_forward(rows, chunks, w):
    t, d = rows.time_rows, chunks[0].shape[1]
    width = w.shape[3]
    shares = w.shape[1]
    pairs = width // LANES
    ways = rows.ways
    rate = LOG2E / math.sqrt(HEAD_DIM)

    def body(*refs):
        chunk_refs = refs[:ways]
        w_ref, a_ref, qkv_ref, log_ref = refs[ways : ways + 4]
        out_refs = refs[ways + 4 : 2 * ways + 4]
        bias_ref, mixed_ref = refs[2 * ways + 4 :]

        @pl.when(pl.program_id(0) == 0)
        def _():
            bias_ref[...] = rows.time_bias()
            for k in range(ways):
                a_ref[k * rows.chunk : (k + 1) * rows.chunk] = chunk_refs[k][...]

        act = a_ref[...]
        for g in range(3):
            qkv_ref[g] = nn(act, w_ref[g, 0]).astype(BF16)

        @pl.loop(0, pairs)
        def _(i):
            lanes = pl.ds(pl.multiple_of(i * LANES, LANES), LANES)
            mixed, logs = pair_forward(
                qkv_ref[0, :, lanes], qkv_ref[1, :, lanes], qkv_ref[2, :, lanes], bias_ref[...], rate
            )
            mixed_ref[:, lanes] = mixed
            log_ref[0, i] = jnp.concatenate(logs, axis=0)

        for k in range(ways):
            out_refs[k][...] = mixed_ref[k * rows.chunk : (k + 1) * rows.chunk]

    got = call(
        body,
        (shares,),
        [whole(c.shape) for c in chunks] + [slabs(3, 0, width, d)],
        [
            made((t, d), BF16),
            made((3, t, d), BF16, (3, t, width), lambda h: (0, 0, h)),
            made((shares, pairs, 2, t), F32, (1, pairs, 2, t), lambda h: (h, 0, 0, 0)),
            *rows.chunks(d, width, lambda h: (0, h)),
        ],
        [pltpu.VMEM((t, t), F32), pltpu.VMEM((t, width), BF16)],
        (*chunks, w),
        flops=2 * t * d * 3 * d,
    )
    return got[0], got[1], got[2], got[3:]


def middle_forward(rows, back, x, w, mix, gb, me):
    t, d = x.shape
    width = w.shape[3]
    shares = w.shape[1]

    def body(me_ref, *refs):
        x_ref, to_ref, sq_ref, mix_ref, gb_ref, o1_ref, y1_ref, x1_ref, qkv_ref = refs[rows.ways :]
        o1 = rows.gathered(refs[: rows.ways], me_ref[3]).astype(BF16)
        o1_ref[...] = o1
        y1 = jnp.zeros((t, d), F32)
        for h in range(shares):
            y1 = y1 + nt(o1[:, h * width : (h + 1) * width], to_ref[0, h])
        y1 = y1.astype(BF16)
        y1_ref[...] = y1
        x1 = x_ref[...] + nn(y1, mix_ref[...])
        x1_ref[...] = x1
        a2 = norm_rounded(x1, gb_ref[1:2], gb_ref[4:5])
        for g in range(3):
            for h in range(shares):
                qkv_ref[g, :, h * width : (h + 1) * width] = nn(a2, sq_ref[g, h]).astype(BF16)

    return call(
        body,
        (1,),
        [
            SCALARS,
            *(whole(c.shape) for c in back),
            whole(x.shape),
            pl.BlockSpec((1, shares, d, width), lambda i: (6, 0, 0, 0)),
            pl.BlockSpec((3, shares, d, width), lambda i: (1, 0, 0, 0)),
            whole(mix.shape),
            whole(gb.shape),
        ],
        [made((t, d), BF16), made((t, d), BF16), made((t, d), F32), made((3, t, d), BF16)],
        [],
        (me, *back, x, w, w, mix, gb),
        flops=2 * t * d * 5 * d,
    )


def space_forward(rows, qkv, x1, w):
    t, d = x1.shape
    width = w.shape[3]
    shares = w.shape[1]
    pairs = width // LANES
    rate = LOG2E / math.sqrt(HEAD_DIM)
    n = rows.frame_rows

    def body(qkv_ref, x1_ref, w_ref, o2_ref, x2_ref, log_ref):
        bias = rows.space_bias()

        @pl.loop(0, pairs)
        def _(i):
            lanes = pl.ds(pl.multiple_of(i * LANES, LANES), LANES)
            for f in range(rows.frames):
                at = slice(f * n, (f + 1) * n)
                mixed, logs = pair_forward(
                    qkv_ref[0, at, lanes], qkv_ref[1, at, lanes], qkv_ref[2, at, lanes], bias, rate
                )
                o2_ref[at, lanes] = mixed
                log_ref[0, i, f] = jnp.concatenate(logs, axis=0)

        @pl.when(pl.program_id(0) == 0)
        def _():
            x2_ref[...] = x1_ref[...]

        x2_ref[...] += nt(o2_ref[...], w_ref[0, 0])

    return call(
        body,
        (shares,),
        [
            pl.BlockSpec((3, t, width), lambda h: (0, 0, h)),
            whole(x1.shape),
            slabs(1, 7, width, d),
        ],
        [
            made((t, d), BF16, (t, width), lambda h: (0, h)),
            made((t, d), F32),
            made(
                (shares, pairs, rows.frames, 2, n),
                F32,
                (1, pairs, rows.frames, 2, n),
                lambda h: (h, 0, 0, 0, 0),
            ),
        ],
        [],
        (qkv, x1, w),
        flops=2 * t * d * d,
    )


def ff_slab(first, per_share, depth, width):
    return pl.BlockSpec(
        (1, 1, depth, width), lambda j: (first + j % per_share, j // per_share, 0, 0)
    )


def mlp_forward(rows, x2, w, gb, gb_next, me):
    t, d = x2.shape
    width = w.shape[3]
    shares = w.shape[1]
    per_share = w.shape[0] // 2
    steps = shares * per_share

    def body(x2_ref, wi_ref, wo_ref, gb_ref, me_ref, gn_ref, x3_ref, *rest):
        send_refs, a3_ref = rest[:-1], rest[-1]
        j = pl.program_id(0)

        @pl.when(j == 0)
        def _():
            a3_ref[...] = norm_rounded(x2_ref[...], gb_ref[2:3], gb_ref[5:6])
            x3_ref[...] = x2_ref[...]

        hid = nn(a3_ref[...], wi_ref[0, 0])
        act = (0.5 * hid * (1.0 + lax.erf(hid * HALF_ROOT))).astype(BF16)
        x3_ref[...] += nt(act, wo_ref[0, 0])

        @pl.when(j == steps - 1)
        def _():
            a = norm_rounded(x3_ref[...], gn_ref[0:1], gn_ref[3:4])
            for k in range(rows.ways):
                send_refs[k][...] = nn(rows.to_time(k, me_ref[3]), a).astype(BF16)

    ins = [
        whole(x2.shape),
        ff_slab(0, per_share, d, width),
        ff_slab(per_share, per_share, d, width),
        whole(gb.shape),
    ]
    ins += [SCALARS, whole(gb_next.shape)]
    outs = [made((t, d), F32)] + rows.chunks(d)
    args = (x2, w, w, gb, me, gb_next)
    return call(
        body, (steps,), ins, outs, [pltpu.VMEM((t, d), BF16)], args, flops=4 * t * d * width * steps
    )


def mlp_backward(rows, grad, x2, w, gb, me, halves, with_output):
    t, d = x2.shape
    width = w.shape[3]
    shares = w.shape[1]
    per_share = w.shape[0] // 2
    steps = shares * per_share

    def body(me_ref, g_ref, x2_ref, wi_ref, wo_ref, gb_ref, go_ref, ki_ref, si_ref, ko_ref, so_ref, sums_ref, *rest):
        if with_output:
            x3_ref, *rest = rest
        a3_ref, a3t_ref, e3_ref, e3t_ref, u_ref = rest
        j = pl.program_id(0)

        @pl.when(j == 0)
        def _():
            hat, _ = norm_parts(x2_ref[...])
            a3 = hat * gb_ref[2:3] + gb_ref[5:6]
            a3_ref[...] = a3.astype(BF16)
            store_by_core(a3t_ref, a3.T.astype(BF16), halves)
            g = g_ref[...]
            e3_ref[...] = g.astype(BF16)
            store_by_core(e3t_ref, g.T.astype(BF16), halves)
            u_ref[...] = jnp.zeros((t, d), F32)
            if with_output:
                x3_ref[...] = x2_ref[...]

        hid = nn(a3_ref[...], wi_ref[0, 0])
        phi = 0.5 * (1.0 + lax.erf(hid * HALF_ROOT))
        act = (hid * phi).astype(BF16)
        slope = phi + hid * jnp.exp(-0.5 * hid * hid) * INV_ROOT_TAU
        dhid = (nn(e3_ref[...], wo_ref[0, 0]) * slope).astype(BF16)
        split_product(e3t_ref, act, ko_ref, so_ref, (0, 0), me_ref)
        split_product(a3t_ref, dhid, ki_ref, si_ref, (0, 0), me_ref)
        u_ref[...] += nt(dhid, wi_ref[0, 0])
        if with_output:
            x3_ref[...] += nt(act, wo_ref[0, 0])

        @pl.when(j == steps - 1)
        def _():
            change, sums = norm_back(u_ref[...], x2_ref[...], gb_ref[2:3])
            go_ref[...] = g_ref[...] + change
            sums_ref[...] = sums

    slab_outs = [
        one
        for _ in range(2)
        for one in halves.array(
            (per_share, shares), (1, 1), lambda j: (j % per_share, j // per_share)
        )
    ]
    grad, ki, si, ko, so, sums, *x3 = call(
        body,
        (steps,),
        [
            SCALARS,
            whole(grad.shape),
            whole(x2.shape),
            ff_slab(0, per_share, d, width),
            ff_slab(per_share, per_share, d, width),
            whole(gb.shape),
        ],
        [made((t, d), F32), *slab_outs, made((2, d), F32)] + [made((t, d), F32)] * with_output,
        [
            pltpu.VMEM((t, d), BF16),
            halves.turned(t),
            pltpu.VMEM((t, d), BF16),
            halves.turned(t),
            pltpu.VMEM((t, d), F32),
        ],
        (me, grad, x2, w, w, gb),
        flops=10 * t * d * width * steps,
    )
    return grad, [(ki, si), (ko, so)], sums, x3


def space_backward(rows, grad, x1, qkv, o2, logs, w, gb, me, halves):
    t, d = x1.shape
    width = w.shape[3]
    shares = w.shape[1]
    pairs = width // LANES
    scale = 1.0 / math.sqrt(HEAD_DIM)
    rate = LOG2E * scale
    n = rows.frame_rows

    def body(me_ref, g_ref, x1_ref, qkv_ref, o2_ref, log_ref, wo_ref, wq_ref, gb_ref, go_ref, keep_ref, send_ref, sums_ref, e2_ref, e2t_ref, a2t_ref, do_ref, dqkv_ref, u_ref):
        h = pl.program_id(0)

        @pl.when(h == 0)
        def _():
            g = g_ref[...]
            e2_ref[...] = g.astype(BF16)
            store_by_core(e2t_ref, g.T.astype(BF16), halves)
            hat, _ = norm_parts(x1_ref[...])
            store_by_core(a2t_ref, (hat * gb_ref[1:2] + gb_ref[4:5]).T.astype(BF16), halves)
            u_ref[...] = jnp.zeros((t, d), F32)

        bias = rows.space_bias()
        split_product(e2t_ref, o2_ref[...], keep_ref, send_ref, (0, 0), me_ref)
        do_ref[...] = nn(e2_ref[...], wo_ref[0, 0]).astype(BF16)

        @pl.loop(0, pairs)
        def _(i):
            lanes = pl.ds(pl.multiple_of(i * LANES, LANES), LANES)
            for f in range(rows.frames):
                at = slice(f * n, (f + 1) * n)
                log = log_ref[0, i, f]
                grads = pair_backward(
                    qkv_ref[0, at, lanes],
                    qkv_ref[1, at, lanes],
                    qkv_ref[2, at, lanes],
                    do_ref[at, lanes],
                    (log[0:1], log[1:2]),
                    bias,
                    rate,
                    scale,
                )
                for part in range(3):
                    dqkv_ref[part, at, lanes] = grads[part]

        for part in range(3):
            split_product(a2t_ref, dqkv_ref[part], keep_ref, send_ref, (part + 1, 0), me_ref)
            u_ref[...] += nt(dqkv_ref[part], wq_ref[part, 0])

        @pl.when(h == shares - 1)
        def _():
            change, sums = norm_back(u_ref[...], x1_ref[...], gb_ref[1:2])
            go_ref[...] = g_ref[...] + change
            sums_ref[...] = sums

    grad, keep, send, sums = call(
        body,
        (shares,),
        [
            SCALARS,
            whole(grad.shape),
            whole(x1.shape),
            pl.BlockSpec((3, t, width), lambda h: (0, 0, h)),
            pl.BlockSpec((t, width), lambda h: (0, h)),
            pl.BlockSpec((1,) + logs.shape[1:], lambda h: (h, 0, 0, 0, 0)),
            slabs(1, 7, width, d),
            slabs(3, 3, width, d),
            whole(gb.shape),
        ],
        [
            made((t, d), F32),
            *halves.array((4, shares), (4, 1), lambda h: (0, h)),
            made((2, d), F32),
        ],
        [
            pltpu.VMEM((t, d), BF16),
            halves.turned(t),
            halves.turned(t),
            pltpu.VMEM((t, width), BF16),
            pltpu.VMEM((3, t, width), BF16),
            pltpu.VMEM((t, d), F32),
        ],
        (me, grad, x1, qkv, o2, logs, w, w, gb),
        flops=2 * t * d * d * 8,
    )
    return grad, (keep, send), sums


def mix_fits(depth, shards, shares):
    return depth // (shards * shares) % 8 == 0


def middle_backward(rows, grad, y1, o1, w, mix, me, halves, shards):
    t, d = grad.shape
    width = w.shape[3]
    shares = w.shape[1]
    fits = mix_fits(d, shards, shares)
    part = d // (shards * shares)

    def body(me_ref, g_ref, y1_ref, o1_ref, to_ref, mix_ref, *rest):
        send_refs, rest = rest[: rows.ways], rest[rows.ways :]
        gk_ref, gs_ref, *rest = rest
        if fits:
            room_ref, order_ref = rest
        else:
            gm_ref, room_ref = rest
        e1 = g_ref[...].astype(BF16)
        dy1 = nt(e1, mix_ref[...]).astype(BF16)
        sends = [rows.to_time(k, me_ref[3]) for k in range(rows.ways)]
        for h in range(shares):
            lanes = slice(h * width, (h + 1) * width)
            do1 = nn(dy1, to_ref[0, h]).astype(BF16)
            for k in range(rows.ways):
                send_refs[k][:, lanes] = nn(sends[k], do1).astype(BF16)
            split_rows(tn(dy1, o1_ref[:, lanes]), gk_ref, gs_ref, (0, h), room_ref, me_ref)
        gm = tn(y1_ref[...], e1)
        if fits:
            gm = gm.reshape(shards, shares, part, d)
            for h in range(shares):
                for half in range(shares):
                    order_ref[:, half] = gm[:, h, :, half * width : (half + 1) * width]
                split_rows(order_ref[...], gk_ref, gs_ref, (1, h), room_ref, me_ref)
        else:
            gm_ref[...] = gm.astype(BF16)

    outs = rows.chunks(d)
    outs += halves.array((1 + fits, shares), (1 + fits, shares), lambda i: (0, 0))
    scratch = [halves.room()]
    if fits:
        scratch.append(pltpu.VMEM((shards, shares, part, width), F32))
    else:
        outs.append(made((d, d), BF16))
    got = call(
        body,
        (1,),
        [
            SCALARS,
            whole(grad.shape),
            whole(y1.shape),
            whole(o1.shape),
            pl.BlockSpec((1, shares, d, width), lambda i: (6, 0, 0, 0)),
            whole(mix.shape),
        ],
        outs,
        scratch,
        (me, grad, y1, o1, w, mix),
        flops=8 * t * d * d,
    )
    do1, (keep, send) = got[: rows.ways], got[rows.ways : rows.ways + 2]
    if not fits:
        gm = mix_slab(got[-1], shards, shares).reshape((1, shares, halves.pairs, 2) + keep.shape[3:])
        keep = jnp.concatenate((keep, lax.dynamic_index_in_dim(gm, me[0], 3, keepdims=False)), axis=0)
        send = jnp.concatenate((send, lax.dynamic_index_in_dim(gm, 1 - me[0], 3, keepdims=False)), axis=0)
    return do1, (keep, send)


def time_backward(rows, do1, a, qkv, logs, w, me, halves):
    t, d = a.shape
    width = w.shape[3]
    shares = w.shape[1]
    pairs = width // LANES
    scale = 1.0 / math.sqrt(HEAD_DIM)
    rate = LOG2E * scale

    def body(me_ref, *refs):
        do_refs, refs = refs[: rows.ways], refs[rows.ways :]
        a_ref, qkv_ref, log_ref, w_ref = refs[:4]
        out_refs, refs = refs[4 : 4 + rows.ways], refs[4 + rows.ways :]
        half_refs, refs = refs[:6], refs[6:]
        bias_ref, dqkv_ref, at_ref, u_ref, do_ref = refs
        h = pl.program_id(0)

        @pl.when(h == 0)
        def _():
            bias_ref[...] = rows.time_bias()
            store_by_core(at_ref, a_ref[...].T, halves)
            u_ref[...] = jnp.zeros((t, d), F32)

        for k in range(rows.ways):
            do_ref[k * rows.chunk : (k + 1) * rows.chunk] = do_refs[k][...]

        @pl.loop(0, pairs)
        def _(i):
            lanes = pl.ds(pl.multiple_of(i * LANES, LANES), LANES)
            log = log_ref[0, i]
            grads = pair_backward(
                qkv_ref[0, :, lanes],
                qkv_ref[1, :, lanes],
                qkv_ref[2, :, lanes],
                do_ref[:, lanes],
                (log[0:1], log[1:2]),
                bias_ref[...],
                rate,
                scale,
            )
            for part in range(3):
                dqkv_ref[part, :, lanes] = grads[part]

        for part in range(3):
            split_product(
                at_ref, dqkv_ref[part], half_refs[2 * part], half_refs[2 * part + 1], (0, 0), me_ref
            )
            u_ref[...] += nt(dqkv_ref[part], w_ref[part, 0])

        @pl.when(h == shares - 1)
        def _():
            for k in range(rows.ways):
                out_refs[k][...] = u_ref[k * rows.chunk : (k + 1) * rows.chunk].astype(BF16)

    got = call(
        body,
        (shares,),
        [
            SCALARS,
            *(pl.BlockSpec((rows.chunk, width), lambda h: (0, h)) for _ in do1),
            whole(a.shape),
            pl.BlockSpec((3, t, width), lambda h: (0, 0, h)),
            pl.BlockSpec((1,) + logs.shape[1:], lambda h: (h, 0, 0, 0)),
            slabs(3, 0, width, d),
        ],
        [
            *rows.chunks(d),
            *(one for _ in range(3) for one in halves.array((1, shares), (1, 1), lambda h: (0, h))),
        ],
        [
            pltpu.VMEM((t, t), F32),
            pltpu.VMEM((3, t, width), BF16),
            halves.turned(t),
            pltpu.VMEM((t, d), F32),
            pltpu.VMEM((t, width), BF16),
        ],
        (me, *do1, a, qkv, logs, w),
        flops=2 * t * d * d * 6,
    )
    parts = got[rows.ways :]
    return got[: rows.ways], [tuple(parts[i : i + 2]) for i in (0, 2, 4)]


def first_norm_back(rows, back, x, grad, gb, me):
    t, d = x.shape

    def body(me_ref, *refs):
        x_ref, g_ref, gb_ref, go_ref, sums_ref = refs[rows.ways :]
        u = rows.gathered(refs[: rows.ways], me_ref[3])
        change, sums = norm_back(u, x_ref[...], gb_ref[0:1])
        go_ref[...] = g_ref[...] + change
        sums_ref[...] = sums

    return call(
        body,
        (1,),
        [SCALARS, *(whole(c.shape) for c in back), whole(x.shape), whole(grad.shape), whole(gb.shape)],
        [made((t, d), F32), made((2, d), F32)],
        [],
        (me, *back, x, grad, gb),
    )


def homes():
    clips, ways = lax.axis_size("clip"), lax.axis_size("seq")
    pairs = []
    for clip in range(clips):
        for seq in range(ways):
            home_clip = clip - clip % 2 + seq % 2
            home_seq = seq // 2 + (ways // 2) * (clip % 2)
            pairs.append((clip * ways + seq, home_clip * ways + home_seq))
    return pairs


def go_home(a):
    return lax.ppermute(a, ("clip", "seq"), homes())


def go_back(a):
    return lax.ppermute(a, ("clip", "seq"), [(home, device) for device, home in homes()])


def member_of(clip, seq):
    return clip % 2 + 2 * (seq % (lax.axis_size("seq") // 2))


def swap_places(chunks):
    clips, ways = lax.axis_size("clip"), lax.axis_size("seq")
    got = [chunks[0]]
    for k in range(1, ways):
        pairs = []
        for clip in range(clips):
            for seq in range(ways):
                other = member_of(clip, seq) ^ k
                to_clip = clip - clip % 2 + other % 2
                to_seq = seq - seq % (ways // 2) + other // 2
                pairs.append((clip * ways + seq, to_clip * ways + to_seq))
        got.append(lax.ppermute(chunks[k], ("clip", "seq"), pairs))
    return got


def columns(a, r, width):
    return a.reshape(r, -1, width).transpose(1, 0, 2)


def pack_attention(time_qkv, time_out, time_mix, space_qkv, space_out):
    r, _, width = time_qkv.shape
    mix = time_mix.reshape(-1, time_mix.shape[1] // width, width).transpose(1, 0, 2).reshape(1, r, width)
    return jnp.concatenate(
        (
            columns(time_qkv, r, width),
            columns(space_qkv, r, width),
            time_out.T[None],
            space_out.T[None],
            mix,
        ),
        axis=0,
    )


def pack_feed_forward(mlp_in, mlp_out, width):
    r = mlp_in.shape[0]
    return jnp.concatenate((columns(mlp_in, r, width), columns(mlp_out.T, r, width)), axis=0)


def gather_slabs(pack):
    full = lax.all_gather(pack, ("head", "clip", "seq"), axis=1, tiled=True)
    return full.reshape(pack.shape[0], lax.axis_size("head"), -1, pack.shape[2])


def spread_steps(pack, me):
    ways, clips = lax.axis_size("seq"), lax.axis_size("clip")
    shares = lax.axis_size("head")
    n, r, width = pack.shape
    pack = yield pack
    turned = [pack] + [
        lax.ppermute(pack, "seq", [(i, (i + k) % ways) for i in range(ways)]) for k in range(1, ways)
    ]
    turned = yield turned
    orders = (((0, 1), "x", "h"), ((3, 2), "h", "x"))
    some = [jnp.stack([turned[k] for k in steps]) for steps, _, _ in orders]
    come = yield [cross(a, first) for a, (_, first, _) in zip(some, orders)]
    some = [jnp.concatenate(pair, axis=0) for pair in zip(some, come)]
    come = yield [cross(a, second) for a, (_, _, second) in zip(some, orders)]
    runs = []
    for mine, other, (steps, first, second) in zip(some, come, orders):
        where = [(k, {first: f}) for f in (0, 1) for k in steps]
        for g, blocks in enumerate((mine, other)):
            runs.append((blocks, [(k, {**at, second: g}) for k, at in where], 0))
    come = yield [cross(blocks, "c") for blocks, _, _ in runs]
    runs += [(far, where, 1) for far, (_, where, _) in zip(come, runs)]
    count = sum(len(where) for _, where, _ in runs)

    def body(me_ref, *refs):
        sources, out_ref, sems = refs[: len(runs)], refs[-2], refs[-1]
        copies = []
        for source, (_, where, core) in zip(sources, runs):
            for i, (k, at) in enumerate(where):
                share = jnp.bitwise_xor(me_ref[2], at["h"])
                clip = 2 * jnp.bitwise_xor(me_ref[1], at["x"]) + jnp.bitwise_xor(me_ref[0], core)
                seq = lax.rem(me_ref[4] + (ways - k), ways)
                copies.append(
                    pltpu.make_async_copy(
                        source.at[i], out_ref.at[:, share, clip * ways + seq], sems.at[len(copies)]
                    )
                )
        for copy in copies:
            copy.start()
        for copy in copies:
            copy.wait()

    full = pl.pallas_call(
        body,
        out_shape=jax.ShapeDtypeStruct((n, shares, clips * ways, r, width), BF16),
        in_specs=[SCALARS] + [pl.BlockSpec(memory_space=pltpu.HBM)] * len(runs),
        out_specs=pl.BlockSpec(memory_space=pltpu.VMEM),
        scratch_shapes=[pltpu.SemaphoreType.DMA((count,))],
        compiler_params=pltpu.CompilerParams(vmem_limit_bytes=VMEM),
        cost_estimate=pl.CostEstimate(
            flops=0, bytes_accessed=4 * n * shares * clips * ways * r * width, transcendentals=0
        ),
    )(me, *(blocks for blocks, _, _ in runs))
    yield full.reshape(n, shares, clips * ways * r, width)


class Spread:
    def __init__(self, pack, me):
        self.way = spread_steps(pack, me)
        self.come = next(self.way)

    def hold(self, x):
        x, self.come = lax.optimization_barrier((x, self.come))
        return x

    def step(self, x):
        x = self.hold(x)
        self.come = self.way.send(self.come)
        return x


def mix_whole(slab, shards):
    shares, depth, width = slab.shape
    part = slab.reshape(shares, shards, shares, depth // (shards * shares), width)
    return part.transpose(1, 0, 3, 2, 4).reshape(depth, shares * width)


def mix_slab(whole_grad, shards, shares):
    depth, full = whole_grad.shape
    width = full // shares
    part = whole_grad.reshape(shards, shares, depth // (shards * shares), shares, width)
    return part.transpose(1, 0, 3, 2, 4).reshape(1, shares, depth, width)


class Piece:
    def __init__(self, keep, got, first, n, order):
        self.near = (keep, got)
        self.first = first
        self.n = n
        self.order = order
        self.step = 0
        self.held = []
        self.result = None


PLACE = {"x": 1, "h": 2}


def fold(pieces, me, last_by_rows):
    ways = lax.axis_size("seq")
    depth, width = pieces[0].near[0].shape[-2:]
    r = depth // ways
    used = {}
    arrays = []

    def number(a):
        for i, known in enumerate(arrays):
            if known is a:
                return i
        arrays.append(a)
        return len(arrays) - 1

    plans = []
    for p in pieces:
        link = p.order[p.step] if p.step < 2 else "z"
        blocks = p.n * (2 if p.step == 0 else 1)
        base = used.get(link, 0)
        used[link] = base + blocks
        near = [number(a) for a in p.near]
        held = [(number(a), at) for a, at in p.held]
        plans.append((p, link, base, near, held))
    links = sorted(used)
    shapes = [
        (ways, used[k], r, width) if k == "z" and last_by_rows else (used[k], depth, width)
        for k in links
    ]
    rooms, counts = [], []
    for p, link, base, near, held in plans:
        each = 2 if p.step == 0 else 1
        counts.append((each, len(near) + len(held)))
        rooms += [(each * p.n, depth, width)] * (len(near) + len(held))
    copies_needed = sum(each * terms for each, terms in counts)

    def body(me_ref, *refs):
        sources = refs[: len(arrays)]
        outs = dict(zip(links, refs[len(arrays) : len(arrays) + len(links)]))
        held_refs = refs[len(arrays) + len(links) : -1]
        sems = refs[-1]
        mine = {name: me_ref[PLACE[name]] for name in PLACE}
        groups = []
        room = 0
        sem = 0
        for p, link, base, near, held in plans:
            group = []
            if p.step == 0:
                for term in near:
                    for k in range(2):
                        pick = {p.order[0]: 1 - mine[p.order[0]], p.order[1]: k}
                        source = sources[term].at[pl.ds(p.first, p.n), pick["h"], pick["x"]]
                        group.append((source, held_refs[room].at[pl.ds(k * p.n, p.n)]))
                    room += 1
            else:
                last = p.order[1]
                pick = {p.order[0]: mine[p.order[0]]}
                pick[last] = 1 - mine[last] if p.step == 1 else mine[last]
                for term in near:
                    source = sources[term].at[pl.ds(p.first, p.n), pick["h"], pick["x"]]
                    group.append((source, held_refs[room]))
                    room += 1
                for i, (term, at) in enumerate(held):
                    start = at + pick[last] * p.n if i == 0 else at
                    group.append((sources[term].at[pl.ds(start, p.n)], held_refs[room]))
                    room += 1
            made_copies = []
            for source, target in group:
                made_copies.append(pltpu.make_async_copy(source, target, sems.at[sem]))
                sem += 1
            groups.append(made_copies)
        for group in groups:
            for copy in group:
                copy.start()
        room = 0
        for (p, link, base, near, held), (each, terms), group in zip(plans, counts, groups):
            these = held_refs[room : room + terms]
            room += terms
            for copy in group:
                copy.wait()

            @pl.loop(0, each * p.n)
            def _(i, these=these, base=base, out=outs[link], last=p.step == 2 and last_by_rows):
                value = these[0][i].astype(F32)
                for one in these[1:]:
                    value = value + one[i].astype(F32)
                value = value.astype(BF16)
                if last:
                    for k in range(ways):
                        out[k, base + i] = value[k * r : (k + 1) * r]
                else:
                    out[base + i] = value

    moved = sum(2 * math.prod(room) for room in rooms) + sum(2 * math.prod(shape) for shape in shapes)
    sums = pl.pallas_call(
        body,
        out_shape=[jax.ShapeDtypeStruct(shape, BF16) for shape in shapes],
        in_specs=[SCALARS] + [pl.BlockSpec(memory_space=pltpu.HBM)] * len(arrays),
        out_specs=[pl.BlockSpec(memory_space=pltpu.VMEM)] * len(links),
        scratch_shapes=[pltpu.VMEM(room, BF16) for room in rooms]
        + [pltpu.SemaphoreType.DMA((copies_needed,))],
        compiler_params=pltpu.CompilerParams(vmem_limit_bytes=VMEM),
        cost_estimate=pl.CostEstimate(flops=0, bytes_accessed=moved, transcendentals=0),
    )(me, *arrays)
    return [(p, link, base) for p, link, base, _, _ in plans], dict(zip(links, sums))


def cross(a, name):
    axis, bit = ("head", 0) if name == "h" else ("clip", 1 if name == "x" else 0)
    size = lax.axis_size(axis)
    return lax.ppermute(a, axis, [(i, i ^ (1 << bit)) for i in range(size)])


def pieces_of(halves_of):
    total = sum(keep.shape[0] for keep, _ in halves_of)
    found = []
    seen = 0
    for keep, send in halves_of:
        got = cross(send, "c")
        n = keep.shape[0]
        first = min(max((total + 1) // 2 - seen, 0), n)
        if first:
            found.append(Piece(keep, got, 0, first, ("x", "h")))
        if n > first:
            found.append(Piece(keep, got, first, n - first, ("h", "x")))
        seen += n
    return found


def move(x, pieces, me, at_end=False):
    plans, sums = fold(pieces, me, at_end)
    x, sums = lax.optimization_barrier((x, sums))
    got = {}
    for link, array in sums.items():
        if link == "z":
            if at_end:
                every = lax.all_to_all(array, "seq", split_axis=0, concat_axis=0, tiled=True)
                got[link] = jnp.sum(every.astype(F32), axis=0)
            else:
                own = lax.psum_scatter(array, "seq", scatter_dimension=1, tiled=True)
                got[link] = own.astype(F32)
        else:
            got[link] = cross(array, link)
    for p, link, base in plans:
        if link == "z":
            p.result = got[link][base : base + p.n]
        else:
            p.held.append((got[link], base))
        p.step += 1
    return x


def settle(x, pieces):
    arrays = []
    for p in pieces:
        if not any(p.held[-1][0] is a for a in arrays):
            arrays.append(p.held[-1][0])
    x, came = lax.optimization_barrier((x, arrays))
    for p in pieces:
        for old, new in zip(arrays, came):
            if p.held[-1][0] is old:
                p.held[-1] = (new, p.held[-1][1])
                break
    return x


def reduce_plain(halves_of, core):
    def joined(keep, send):
        low = jnp.where(core == 0, keep, send)
        high = jnp.where(core == 0, send, keep)
        n, shares, pairs, depth, width = keep.shape
        return jnp.stack((low, high), axis=3).reshape(n, shares, 2 * pairs * depth, width)

    g = jnp.concatenate([joined(*pair) for pair in halves_of], axis=0)
    g = lax.psum_scatter(g, "head", scatter_dimension=1, tiled=True)
    g = lax.psum_scatter(g.astype(F32), ("clip", "seq"), scatter_dimension=2, tiled=True)
    return g[:, 0]


def gather_norms(gain, bias):
    layers, norms, part = gain.shape
    both = jnp.concatenate((gain, bias), axis=1).reshape(1, -1)
    count = lax.axis_size("clip") * lax.axis_size("seq") * lax.axis_size("head")
    width = round_up(both.shape[1], 128)
    padded = jnp.pad(both, ((0, 0), (0, width - both.shape[1])))
    every = lax.all_to_all(
        jnp.broadcast_to(padded, (count, width)), ALL, split_axis=0, concat_axis=0, tiled=True
    )[:, : both.shape[1]]
    return every.reshape(count, layers * 2 * norms, part).transpose(1, 0, 2).reshape(layers, 2 * norms, -1)


def reduce_norms(sums):
    count = lax.axis_size("clip") * lax.axis_size("seq") * lax.axis_size("head")
    rows, features = sums.shape
    part = features // count
    a = sums.reshape(rows, count, part).transpose(1, 0, 2).reshape(count, rows * part)
    width = round_up(rows * part, 128)
    a = jnp.pad(a, ((0, 0), (0, width - rows * part)))
    every = lax.all_to_all(a, ALL, split_axis=0, concat_axis=0, tiled=True)
    return jnp.sum(every, axis=0)[: rows * part].reshape(rows, part)


def on_device(
    tokens,
    cotangent,
    time_qkv,
    time_out,
    time_mix,
    space_qkv,
    space_out,
    mlp_in,
    mlp_out,
    norm_gain,
    norm_bias,
):
    layers = time_qkv.shape[0]
    clips, frames, places, d = tokens.shape
    ways = lax.axis_size("seq")
    shards = lax.axis_size("clip") * ways
    rows = Rows(clips * frames, places, ways)
    shares = lax.axis_size("head")

    def as_rows(a):
        a = a.astype(F32).reshape(rows.frames, places, d)
        a = jnp.pad(a, ((0, 0), (0, rows.frame_rows - places), (0, 0)))
        return a.reshape(rows.rows, d)

    def from_rows(a):
        a = a.reshape(rows.frames, rows.frame_rows, d)[:, :places]
        return a.reshape(tokens.shape)

    gbs = gather_norms(norm_gain, norm_bias)
    gb = [gbs[l] for l in range(layers)]
    packs = [
        pack_attention(time_qkv[l], time_out[l], time_mix[l], space_qkv[l], space_out[l])
        for l in range(layers)
    ]
    packs_ff = [pack_feed_forward(mlp_in[l], mlp_out[l], time_qkv.shape[3]) for l in range(layers)]
    weights = [gather_slabs(pack) for pack in packs]
    mixes = [mix_whole(w[-1], shards) for w in weights]
    quick = lax.axis_size("clip") == 4 and shares == 2 and ways == 4 and time_qkv.shape[1] % 16 == 0

    halves = Halves(lax.axis_size("clip"), d, time_qkv.shape[3])
    clip = lax.axis_index("clip")
    member = member_of(clip, lax.axis_index("seq"))
    me = jnp.stack((clip & 1, (clip >> 1) & 1, lax.axis_index("head"), member, lax.axis_index("seq"))).astype(
        jnp.int32
    )
    if quick:
        spreads = [Spread(pack, me) for pack in packs_ff]
        weights_ff = []
    else:
        weights_ff = [gather_slabs(pack) for pack in packs_ff]

    home = go_home(tokens)
    if quick:
        first = spreads[0]
        home, gb = first.step((home, gb))
    x = as_rows(home)
    send = send_first(rows, x, gb[0], me)
    kept = []
    for l in range(layers):
        w = weights[l]
        send = swap_places(send)
        if quick and l == 0:
            for _ in range(2):
                send = first.step(send)
            for spread in spreads[1:]:
                send = spread.step(send)
                send = spread.hold(send)
            send = first.step(send)
        elif quick:
            send = spreads[l].step(send)
        a1, qkv1, log1, o1_time = time_forward(rows, send, w)
        back = swap_places(o1_time)
        if quick:
            back = spreads[l].step(back)
            weights_ff.append(spreads[l].come)
            if l == 0:
                for spread in spreads[1:]:
                    back = spread.step(back)
        o1, y1, x1, qkv2 = middle_forward(rows, back, x, w, mixes[l], gb[l], me)
        o2, x2, log2 = space_forward(rows, qkv2, x1, w)
        if quick and l == 0:
            for spread in spreads[1:]:
                x2 = spread.step(x2)
        kept.append((x, a1, qkv1, log1, o1, y1, x1, qkv2, o2, log2, x2))
        if l + 1 < layers:
            x, *send = mlp_forward(rows, x2, weights_ff[l], gb[l], gb[l + 1], me)

    grad = as_rows(go_home(cotangent))
    norm_rows = [None] * layers
    summed = [None] * layers
    late = []
    for l in reversed(range(layers)):
        w = weights[l]
        x, a1, qkv1, log1, o1, y1, x1, qkv2, o2, log2, x2 = kept[l]
        grad, g_ff, s3, x3 = mlp_backward(
            rows, grad, x2, weights_ff[l], gb[l], me, halves, l + 1 == layers
        )
        if x3:
            output = go_back(from_rows(x3[0].astype(BF16)))
        if quick:
            ff = pieces_of(g_ff)
            if late:
                grad = settle(grad, late)
                grad = move(grad, late, me)
                late = [p for p in late if p.step < 3]
        grad, g_space, s2 = space_backward(rows, grad, x1, qkv2, o2, log2, w, gb[l], me, halves)
        if quick:
            space = pieces_of([g_space])
            if late:
                grad = settle(grad, late)
            grad, output = move((grad, output), ff, me)
        do1, g_out = middle_backward(rows, grad, y1, o1, w, mixes[l], me, halves, shards)
        do1 = swap_places(do1)
        if quick:
            do1 = move(do1, ff + space + late, me)
        da1, g_time = time_backward(rows, do1, a1, qkv1, log1, w, me, halves)
        if quick:
            da1 = settle(da1, ff + space)
        da1 = swap_places(da1)
        if quick:
            rest = pieces_of([g_out] + g_time)
            da1 = move(da1, ff + space + rest, me)
            late = space + rest
        grad, s1 = first_norm_back(rows, da1, x, grad, gb[l], me)
        norm_rows[l] = jnp.concatenate((s1[0:1], s2[0:1], s3[0:1], s1[1:2], s2[1:2], s3[1:2]), axis=0)
        if quick:
            summed[l] = ff + space + rest
        else:
            summed[l] = [reduce_plain(g_ff + [g_space, g_out] + g_time, clip & 1)]
    norm_sums = reduce_norms(jnp.concatenate(norm_rows, axis=0)).reshape(layers, 2, 3, -1)
    if quick:
        tokens_grad = go_back(from_rows(grad.astype(BF16)))
        tokens_grad = move(tokens_grad, rest, me, True)
        norm_sums = move(norm_sums, space + rest, me, True)
        summed = [[p.result for p in some] for some in summed]
    cuts = (2 * g_ff[0][0].shape[0], g_space[0].shape[0], g_out[0].shape[0], len(g_time))
    results = []
    for some in summed:
        slabs_of = jnp.concatenate(some, axis=0)
        ends = [sum(cuts[: i + 1]) for i in range(4)]
        results.append([slabs_of[e - c : e] for c, e in zip(cuts, ends)])
    if not quick:
        tokens_grad = go_back(from_rows(grad.astype(BF16)))
    tokens_grad = tokens_grad.astype(F32)

    def stacked(form):
        return jnp.stack([form(*results[l]) for l in range(layers)])

    def rows_of(a):
        return a.transpose(1, 0, 2)

    def flat(a):
        return rows_of(a).reshape(a.shape[1], -1)

    def mix_rows(a):
        r, width = a.shape
        return a.reshape(shares, r // shares, width).transpose(1, 0, 2).reshape(r // shares, -1)

    per_share = mlp_in.shape[2] // time_qkv.shape[3]
    return (
        output,
        tokens_grad,
        stacked(lambda ff, s, t, q: rows_of(q)),
        stacked(lambda ff, s, t, q: t[0].T),
        stacked(lambda ff, s, t, q: mix_rows(t[1])),
        stacked(lambda ff, s, t, q: rows_of(s[1:])),
        stacked(lambda ff, s, t, q: s[0].T),
        stacked(lambda ff, s, t, q: flat(ff[:per_share])),
        stacked(lambda ff, s, t, q: flat(ff[per_share:]).T),
        norm_sums[:, 0],
        norm_sums[:, 1],
    )


def solution(mesh):
    token_spec = P(("clip", "head"), "seq", None, None)
    in_specs = (
        token_spec,
        token_spec,
        P(None, ("clip", "seq"), None, "head"),
        P(None, "head", ("clip", "seq")),
        P(None, ("clip", "seq", "head"), None),
        P(None, ("clip", "seq"), None, "head"),
        P(None, "head", ("clip", "seq")),
        P(None, ("clip", "seq"), "head"),
        P(None, "head", ("clip", "seq")),
        P(None, None, ("clip", "seq", "head")),
        P(None, None, ("clip", "seq", "head")),
    )
    return jax.shard_map(
        on_device, mesh=mesh, in_specs=in_specs, out_specs=in_specs, check_vma=False
    )
```
